32 devices in a mesh: dp: 4 (over y, x), expert: 8 (over z, core).
Axes of the slice: x: 2, y: 2, z: 4, core: 2. Of those that a mesh axis runs over, the one named last changes fastest.
Arguments:
- tokens: bfloat16 [8704, 2048], P(('dp', 'expert')), may hold values from -6 to 6
- teacher: bfloat16 [8704, 2048], P(('dp', 'expert')), may hold values from -6 to 6
- att_routes: int32 [8704, 2], P(('dp', 'expert')), may hold values from 0 to 7, all different within a row; in each aligned block of 272 rows (0 to 271, 272 to 543, ...) at most 88 rows name the same one
- ffn_routes: int32 [8704, 2], P(('dp', 'expert')), may hold values from 0 to 3, all different within a row; in each aligned block of 272 rows (0 to 271, 272 to 543, ...) at most 176 rows name the same one
- parent: int32 [4, 13], P('dp'), may hold values from 0 to 4, as said below
- valid: int32 [4], replicated, may hold values from 1632 to 2176
- gain_one: float32 [2048], replicated, may hold values from 0.5 to 1.5
- kv_weight: bfloat16 [2048, 4096], P('expert'), may hold values from -0.125 to 0.125
- att_router: float32 [2048, 8], replicated, may hold values from -0.125 to 0.125
- q_weight: bfloat16 [2048, 16384], P(None, 'expert'), may hold values from -0.125 to 0.125
- o_weight: bfloat16 [2048, 16384], P(None, 'expert'), may hold values from -1 to 1
- gain_two: float32 [2048], replicated, may hold values from 0.5 to 1.5
- ffn_router: float32 [2048, 4], replicated, may hold values from -0.125 to 0.125
- gate_weight: bfloat16 [2048, 22528], P(None, 'expert'), may hold values from -0.125 to 0.125
- up_weight: bfloat16 [2048, 22528], P(None, 'expert'), may hold values from -0.125 to 0.125
- down_weight: bfloat16 [2048, 22528], P(None, 'expert'), may hold values from -0.078125 to 0.078125
Outputs:
- output: bfloat16 [8704, 2048], P(('dp', 'expert'))
- grad_input: bfloat16 [8704, 2048], P(('dp', 'expert'))
- grad_gain_one: float32 [2048], P(('dp', 'expert'))
- grad_kv_weight: float32 [2048, 4096], P(('dp', 'expert'))
- grad_att_router: float32 [2048, 8], P(('dp', 'expert'))
- grad_q_weight: float32 [2048, 16384], P('dp', 'expert')
- grad_o_weight: float32 [2048, 16384], P('dp', 'expert')
- grad_gain_two: float32 [2048], P(('dp', 'expert'))
- grad_ffn_router: float32 [2048, 4], P(('dp', 'expert'))
- grad_gate_weight: float32 [2048, 22528], P('dp', 'expert')
- grad_up_weight: float32 [2048, 22528], P('dp', 'expert')
- grad_down_weight: float32 [2048, 22528], P('dp', 'expert')
The draws below stay inside these ranges and needn't reach their ends.
Inputs may be any that keep to these rules, and one draw needn't show every extreme that they name: `att_routes`: in the rows of one device no attention expert is named by more than 88 rows; a row's two experts differ. `ffn_routes`: in the rows of one device no feed-forward expert is named by more than 176 rows; a row's two experts differ. segment 0 is the trunk, 1 to 4 the branches, 5 to 12 the leaves; trunk and branches have parent 0; each branch is the parent of exactly two leaves. `valid`: tokens of a tree at places below its count enter the loss.
All inputs are finite; a program needn't handle non-finite values.
Results may differ from the reference program's by a relative error of at most 0.015.
Values may be sent and summed in bfloat16 or wider, within the bound.
A program may use at most 384 MiB of HBM per device.

```python
import math
import jax
import jax.numpy as jnp
import numpy as np
from jax import lax

D = 2048
HEADS = 16
HEAD = 128
FF = 5632
ATT_EXPERTS = 8
FFN_EXPERTS = 4
TRUNK = 1024
SEG = 96
TREE_LEN = 2176
ROWS = 272
TOKENS = 8704
TREES_ALL = 4
CAP_ATT = 88
CAP_FFN = 176


def draw_parent(key, part):
    keys = jax.random.split(key, TREES_ALL)

    def one_tree(one_key):
        return jax.random.permutation(one_key, 8)
    order = jax.vmap(one_tree)(keys)
    leaves = (order // 2 + 1).astype(jnp.int32)
    return jnp.concatenate([jnp.zeros((TREES_ALL, 5), jnp.int32), leaves], axis=1)


def place_ends(drawn, rng, smallest, top_value):
    shape = drawn.shape
    index_at = [jax.random.randint(jax.random.fold_in(rng, axis), (), 0, shape[axis]) for axis in range(len(shape))]
    drawn = drawn.at[tuple(index_at)].set(smallest)
    longest = shape.index(max(shape))
    index_at[longest] = (index_at[longest] + 1) % shape[longest]
    return drawn.at[tuple(index_at)].set(top_value)


def levels(stream_key, extent, shards, smallest, high):
    level = 1.0
    for position, blocks in shards:
        draws = jax.random.uniform(jax.random.fold_in(jax.random.fold_in(stream_key, 6), position), (blocks,), jnp.float32, smallest / len(shards), high / len(shards))
        level = level * jnp.repeat(jnp.exp(draws), extent[position] // blocks).reshape((-1,) + (1,) * (len(extent) - 1 - position))
    return level


def assign_block(rng, own, number, rows, amount, top, bound, skew):
    sequence = jax.random.permutation(rng, amount)
    packed, common = load_shares(amount, rows * top, bound, skew, True), load_shares(amount, rows * top, bound, skew, False)
    places = jnp.arange(amount)

    def named(tallies, turn):
        used = int((tallies > 0).sum())
        fixed = max(1, used // 4)
        shifted = fixed + (places - fixed + turn * (used - fixed)) % max(1, amount - fixed)
        return jnp.zeros((amount,), jnp.int32).at[sequence[jnp.where(places < fixed, places, shifted)]].set(jnp.asarray(tallies, jnp.int32))

    tallies = jnp.where(number % 4 == 0, named(packed, number // 4), named(common, number - number // 4 - 1))
    mixed = jax.random.permutation(jax.random.fold_in(own, 3), amount)
    donor, receiver = mixed[0:amount // 2 * 2:2], mixed[1:amount // 2 * 2:2]
    margin = jnp.minimum(tallies[donor] - 1, bound - tallies[receiver]) // 2
    margin = jnp.where((donor == sequence[0]) | (receiver == sequence[0]) | (tallies[receiver] == 0), 0, jnp.maximum(margin, 0))
    shifted = jax.random.randint(jax.random.fold_in(own, 4), (amount // 2,), 0, 1 << 20) % (margin + 1)
    tallies = tallies.at[donor].add(-shifted).at[receiver].add(shifted)
    labels = jnp.searchsorted(jnp.cumsum(tallies), jnp.arange(rows * top), side="right").astype(jnp.int32)
    table = labels.reshape(top, rows).T
    table = table[jax.random.permutation(jax.random.fold_in(own, 1), rows)]
    turn = jax.random.randint(jax.random.fold_in(own, 2), (rows, 1), 0, top)
    return jnp.take_along_axis(table, (jnp.arange(top)[None, :] + turn) % top, axis=1)


def load_shares(number_of, total, reach, lean, full):
    portions = [(1 << 20) // math.isqrt(standing ** lean) + 1 for standing in range(1, number_of + 1)]
    largest = reach if full else min(reach, max(-(-total // number_of), total * portions[0] // sum(portions)))
    least = 1 if total - largest >= number_of - 1 else 0
    given, surplus = [largest] + [least] * (number_of - 1), total - largest - least * (number_of - 1)
    while surplus > 0:
        candidates = [i for i in range(1, number_of) if given[i] < largest] or [i for i in range(1, number_of) if given[i] < reach]
        pool, left = sum([portions[i] for i in candidates]), surplus
        for i in candidates:
            addition = min(reach - given[i], max(1, left * portions[i] // pool), surplus)
            given[i] = given[i] + addition
            surplus = surplus - addition
    return np.array(given)


def normal_values(key, dims, deviation, bound, shards=(), held_as=jnp.bfloat16):
    array = jax.random.normal(key, dims, jnp.float32) * deviation
    if len(shards) > 0:
        array = levels(key, dims, shards, -0.22, 0.18) * array
    return jnp.clip(array, min=-bound, max=bound).astype(held_as)


def setup_inputs(seed: int = 0) -> dict:
    key_list = jax.random.split(jax.random.key(seed), 17)
    tokens = normal_values(key_list[0], (TOKENS, D), 1.0, 6.0, ((0, 32),))
    teacher = normal_values(key_list[1], (TOKENS, D), 1.0, 6.0, ((0, 32),))
    att_routes_keys = jax.random.split(jax.random.fold_in(key_list[2], 1), TOKENS // ROWS)
    att_routes_turns = jax.random.permutation(jax.random.fold_in(key_list[2], 3), TOKENS // ROWS)
    att_routes = jax.vmap(lambda own, number: assign_block(jax.random.fold_in(key_list[2], 2), own, number, ROWS, ATT_EXPERTS, 2, CAP_ATT, 1))(att_routes_keys, att_routes_turns).reshape((TOKENS, 2))
    ffn_routes_keys = jax.random.split(jax.random.fold_in(key_list[3], 1), TOKENS // ROWS)
    ffn_routes_turns = jax.random.permutation(jax.random.fold_in(key_list[3], 3), TOKENS // ROWS)
    ffn_routes = jax.vmap(lambda own, number: assign_block(jax.random.fold_in(key_list[3], 2), own, number, ROWS, FFN_EXPERTS, 2, CAP_FFN, 1))(ffn_routes_keys, ffn_routes_turns).reshape((TOKENS, 2))
    parent = draw_parent(jax.random.fold_in(key_list[16], 71), 0)
    valid = place_ends(jax.random.randint(key_list[5], (TREES_ALL,), TREE_LEN * 3 // 4, TREE_LEN + 1), jax.random.fold_in(key_list[5], 1), TREE_LEN * 3 // 4, TREE_LEN).astype(jnp.int32)
    gain_one = jnp.clip(1.0 + 0.1 * jax.random.normal(key_list[6], (D,), jnp.float32), 0.5, 1.5)
    kv_weight = normal_values(key_list[7], (D, 2 * HEADS * HEAD), D ** -0.5, 0.125, ((0, 8),))
    att_router = normal_values(key_list[8], (D, ATT_EXPERTS), D ** -0.5, 0.125, (), jnp.float32)
    q_weight = normal_values(key_list[9], (D, ATT_EXPERTS * HEADS * HEAD), D ** -0.5, 0.125, ((1, 8),))
    o_weight = normal_values(key_list[10], (D, ATT_EXPERTS * HEADS * HEAD), (HEADS * HEAD // 64) ** -0.5, 1.0, ((1, 8),))
    gain_two = jnp.clip(1.0 + 0.1 * jax.random.normal(key_list[11], (D,), jnp.float32), 0.5, 1.5)
    ffn_router = normal_values(key_list[12], (D, FFN_EXPERTS), D ** -0.5, 0.125, (), jnp.float32)
    gate_weight = normal_values(key_list[13], (D, FFN_EXPERTS * FF), D ** -0.5, 0.125, ((1, 8),))
    up_weight = normal_values(key_list[14], (D, FFN_EXPERTS * FF), D ** -0.5, 0.125, ((1, 8),))
    down_weight = normal_values(key_list[15], (D, FFN_EXPERTS * FF), FF ** -0.5, 0.078125, ((1, 8),))
    return dict(tokens=tokens, teacher=teacher, att_routes=att_routes, ffn_routes=ffn_routes, parent=parent, valid=valid, gain_one=gain_one, kv_weight=kv_weight, att_router=att_router, q_weight=q_weight, o_weight=o_weight, gain_two=gain_two, ffn_router=ffn_router, gate_weight=gate_weight, up_weight=up_weight, down_weight=down_weight)


@jax.custom_vjp
def low(v):
    return lax.optimization_barrier(v.astype(jnp.bfloat16)).astype(jnp.float32)

@jax.custom_vjp
def low_back(v):
    return v

def low_keep(v):
    return (low(v), None)

def low_pass(kept, grad):
    return (grad,)

def back_keep(v):
    return (v, None)

def back_low(kept, grad):
    return (low(grad),)
low.defvjp(low_keep, low_pass)
low_back.defvjp(back_keep, back_low)
epsilon = 1e-06

def matmul(left, right):
    return jnp.dot(left, right, precision=lax.Precision.HIGHEST)

def tree_layout(places):
    after_trunk = places - TRUNK
    after_branch = after_trunk - 4 * SEG
    segments = jnp.where(places < TRUNK, 0, jnp.where(after_branch < 0, 1 + after_trunk // SEG, 5 + after_branch // SEG))
    depths = jnp.where(places < TRUNK, places, jnp.where(after_branch < 0, TRUNK + after_trunk % SEG, TRUNK + SEG + after_branch % SEG))
    return (segments.astype(jnp.int32), depths.astype(jnp.int32))

def ancestors(parent):
    nodes = jnp.arange(13, dtype=jnp.int32)
    grand = lax.optimization_barrier(jnp.sum(jnp.where(parent[:, :, None] == nodes[None, None, :], parent[:, None, :], 0), axis=2))
    return (nodes[None, None, :] == nodes[None, :, None]) | (nodes[None, None, :] == parent[:, :, None]) | (nodes[None, None, :] == grand[:, :, None])

def rotate(values, depths):
    half_size = values.shape[-1] // 2
    frequency = 10000.0 ** (-jnp.arange(half_size, dtype=jnp.float32) * 2.0 / values.shape[-1])
    angles = depths.astype(jnp.float32)[:, None] * frequency[None, :]
    cosine = jnp.cos(angles)[:, None, :]
    sine = jnp.sin(angles)[:, None, :]
    first = values[..., :half_size]
    second = values[..., half_size:]
    return jnp.concatenate([first * cosine - second * sine, second * cosine + first * sine], axis=-1)

def rms_norm(values, gain):
    inverse = lax.rsqrt(lax.optimization_barrier(jnp.mean(values * values, axis=-1, keepdims=True)) + epsilon)
    return values * inverse * gain

def gate_mix(hidden, router, hot):
    logits = matmul(hidden, router)
    picked = lax.optimization_barrier(jnp.sum(hot * logits[:, None, :], axis=2))
    gates = jax.nn.softmax(picked, axis=1)
    return lax.optimization_barrier(jnp.sum(hot * gates[:, :, None], axis=1))

def reference(tokens, teacher, att_routes, ffn_routes, parent, valid, gain_one, kv_weight, att_router, q_weight, o_weight, gain_two, ffn_router, gate_weight, up_weight, down_weight):
    token_count = tokens.shape[0]
    tree_total = token_count // TREE_LEN
    places = jnp.arange(token_count, dtype=jnp.int32) % TREE_LEN
    tree_ids = jnp.arange(token_count, dtype=jnp.int32) // TREE_LEN
    segments, depths = tree_layout(places)
    related = ancestors(parent)
    att_hot = (att_routes[:, :, None] == jnp.arange(ATT_EXPERTS, dtype=jnp.int32)[None, None, :]).astype(jnp.float32)
    ffn_hot = (ffn_routes[:, :, None] == jnp.arange(FFN_EXPERTS, dtype=jnp.int32)[None, None, :]).astype(jnp.float32)
    counted = places < valid[tree_ids]
    width = HEADS * HEAD
    score_scale = HEAD ** (-0.5)
    target = teacher.astype(jnp.float32)
    tree_places = jnp.arange(TREE_LEN, dtype=jnp.int32)
    tree_segments, unused_depth = tree_layout(tree_places)
    block_size = TREE_LEN // 4

    def tree_attention(item):
        q_tree, k_tree, v_tree, related_tree = item

        def one_block(start):
            q_block = lax.dynamic_slice_in_dim(q_tree, start, block_size, 0)
            q_places = start + jnp.arange(block_size, dtype=jnp.int32)
            q_segments = lax.dynamic_slice_in_dim(tree_segments, start, block_size, 0)
            allowed = related_tree[q_segments][:, tree_segments] & (tree_places[None, :] <= q_places[:, None])
            scores = low_back(jnp.einsum('bkhd,jhd->khbj', q_block, k_tree, precision=lax.Precision.HIGHEST) * score_scale)
            probs = low(jax.nn.softmax(jnp.where(allowed[None, None], scores, -1e+30), axis=-1))
            return jnp.einsum('khbj,jhd->bkhd', probs, v_tree, precision=lax.Precision.HIGHEST)
        starts = jnp.arange(4, dtype=jnp.int32) * block_size
        return lax.map(jax.checkpoint(one_block), starts).reshape(TREE_LEN, 2, HEADS, HEAD)

    def forward(x_in, gain_a, kv_w, router_a, q_w, o_w, gain_b, router_b, gate_w, up_w, down_w):
        hidden = low(rms_norm(x_in, gain_a))
        att_mix = gate_mix(hidden, router_a, att_hot)
        kv_all = matmul(hidden, kv_w)
        keys = low(rotate(low_back(kv_all[:, :width]).reshape(token_count, HEADS, HEAD), depths))
        values = low(low_back(kv_all[:, width:])).reshape(token_count, HEADS, HEAD)
        q_stack = q_w.reshape(D, ATT_EXPERTS, width).transpose(1, 0, 2)

        def query_step(carry, item):
            weight, picks = item
            q_pre = low_back(matmul(hidden, weight))
            q_all = low(rotate(q_pre.reshape(token_count, HEADS, HEAD), depths))
            return (carry + picks[:, :, None, None] * q_all[:, None], None)
        q_init = jnp.zeros((token_count, 2, HEADS, HEAD), jnp.float32)
        chosen, unused = lax.scan(jax.checkpoint(query_step), q_init, (q_stack, att_hot.transpose(2, 0, 1)))
        attended = lax.map(tree_attention, (chosen.reshape(tree_total, TREE_LEN, 2, HEADS, HEAD), keys.reshape(tree_total, TREE_LEN, HEADS, HEAD), values.reshape(tree_total, TREE_LEN, HEADS, HEAD), related))
        attended = low_back(low(attended.reshape(token_count, 2, width)))
        o_stack = o_w.reshape(D, ATT_EXPERTS, width).transpose(1, 0, 2)

        def out_step(carry, item):
            weight, picks, mix = item
            rows_in = lax.optimization_barrier(jnp.sum(picks[:, :, None] * attended, axis=1))
            branch = low_back(matmul(rows_in, weight.T))
            return (carry + mix[:, None] * branch, None)
        att_out, unused = lax.scan(jax.checkpoint(out_step), jnp.zeros((token_count, D), jnp.float32), (o_stack, att_hot.transpose(2, 0, 1), att_mix.T))
        x_mid = x_in + att_out
        hidden_two = low(rms_norm(x_mid, gain_b))
        ffn_mix = gate_mix(hidden_two, router_b, ffn_hot)
        gate_stack = gate_w.reshape(D, FFN_EXPERTS, FF).transpose(1, 0, 2)
        up_stack = up_w.reshape(D, FFN_EXPERTS, FF).transpose(1, 0, 2)
        down_stack = down_w.reshape(D, FFN_EXPERTS, FF).transpose(1, 0, 2)

        def ffn_step(carry, item):
            gate_e, up_e, down_e, mix = item
            gate_pre = low_back(matmul(hidden_two, gate_e))
            up_pre = low_back(matmul(hidden_two, up_e))
            acted = low(jax.nn.silu(gate_pre) * up_pre)
            branch = low_back(matmul(acted, down_e.T))
            return (carry + mix[:, None] * branch, None)
        ffn_out, unused = lax.scan(jax.checkpoint(ffn_step), jnp.zeros((token_count, D), jnp.float32), (gate_stack, up_stack, down_stack, ffn_mix.T))
        result = x_mid + ffn_out
        total_valid = jnp.sum(valid).astype(jnp.float32)
        loss = jnp.sum(jnp.where(counted[:, None], (result - target) ** 2, 0.0)) * (token_count / (2.0 * total_valid))
        return (result, loss)
    inputs = (tokens.astype(jnp.float32), gain_one.astype(jnp.float32), kv_weight.astype(jnp.float32), att_router.astype(jnp.float32), q_weight.astype(jnp.float32), o_weight.astype(jnp.float32), gain_two.astype(jnp.float32), ffn_router.astype(jnp.float32), gate_weight.astype(jnp.float32), up_weight.astype(jnp.float32), down_weight.astype(jnp.float32))
    (result, loss), pullback = jax.vjp(forward, *inputs)
    grads = pullback((jnp.zeros_like(result), jnp.ones_like(loss)))
    return (result.astype(jnp.bfloat16), grads[0].astype(jnp.bfloat16), grads[1], grads[2], grads[3], grads[4], grads[5], grads[6], grads[7], grads[8], grads[9], grads[10])
```

```python
import functools
import jax
import jax.numpy as jnp
from jax import lax
from jax.experimental import pallas as pl
from jax.experimental.pallas import tpu as pltpu
from jax.sharding import PartitionSpec as P

HEAD = 128
GROUPS = 4
LOG2E = 1.4426950408889634
VMEM_BYTES = 60 * 1024 * 1024


def dot_nt(left, right):
    return lax.dot_general(left, right, (((1,), (1,)), ((), ())), preferred_element_type=jnp.float32)


def dot_nn(left, right):
    return jnp.dot(left, right, preferred_element_type=jnp.float32)


def spin(values, cosine, sine):
    return values * cosine + pltpu.roll(values, HEAD // 2, 1) * sine


def fill_bias(bias_ref, key_ref, query_ref, keys):
    for group in range(GROUPS):
        place = query_ref[group, 0:1, :]
        own, parent, grand = (query_ref[group, 1 + n : 2 + n, :] for n in range(3))

        def one(block, carry, group=group, place=place, own=own, parent=parent, grand=grand):
            at = pl.multiple_of(block * keys, 16)
            key_place = key_ref[pl.ds(at, keys), 0:1]
            key_segment = key_ref[pl.ds(at, keys), 1:2]
            related = (key_segment == own) | (key_segment == parent) | (key_segment == grand)
            allowed = related & (key_place <= place)
            bias_ref[group * (group + 1) // 2 + block] = jnp.where(allowed, 0.0, -1e30)
            return carry

        lax.fori_loop(0, group + 1, one, 0)


def group_rows(refs, group, rows, lanes):
    parts = [ref[pl.ds(group * rows, rows), lanes] for ref in refs]
    return parts[0] if len(parts) == 1 else jnp.concatenate(parts, axis=0)


def attention_forward_body(sets, step_heads, rows, keys, scale, first_ref, *refs):
    query_refs = refs[:sets]
    key_ref, value_ref, key_info, query_info = refs[sets : sets + 4]
    out_refs = refs[sets + 4 : 2 * sets + 4]
    lse_ref, bias_ref, flipped_ref = refs[2 * sets + 4 :]
    wide = sets * rows

    @pl.when(pl.program_id(0) == 0)
    def _():
        fill_bias(bias_ref, key_info, query_info, keys)

    for head in range(step_heads):
        lanes = pl.ds(head * HEAD, HEAD)
        for block in range(GROUPS):
            values = value_ref[pl.ds(block * keys, keys), lanes].astype(jnp.float32)
            flipped_ref[head, block] = values.T.astype(jnp.bfloat16)
    for group in range(GROUPS):
        queries = [
            group_rows(query_refs, group, rows, pl.ds(head * HEAD, HEAD)) for head in range(step_heads)
        ]

        def one(block, carry, group=group, queries=queries):
            at = pl.multiple_of(block * keys, 16)
            bias = bias_ref[group * (group + 1) // 2 + block]
            result = []
            for head in range(step_heads):
                top, total, mixed = carry[3 * head : 3 * head + 3]
                scores = dot_nt(key_ref[pl.ds(at, keys), pl.ds(head * HEAD, HEAD)], queries[head])
                scores = scores * scale + bias
                new_top = jnp.maximum(top, jnp.max(scores, axis=0, keepdims=True))
                fade = jnp.exp2(top - new_top)
                parts = jnp.exp2(scores - new_top)
                total = total * fade + jnp.sum(parts, axis=0, keepdims=True)
                mixed = mixed * fade + dot_nn(flipped_ref[head, block], parts.astype(jnp.bfloat16))
                result += [new_top, total, mixed]
            return tuple(result)

        start = (
            jnp.full((1, wide), -1e30, jnp.float32),
            jnp.zeros((1, wide), jnp.float32),
            jnp.zeros((HEAD, wide), jnp.float32),
        ) * step_heads
        final = lax.fori_loop(0, group + 1, one, start)
        for head in range(step_heads):
            top, total, mixed = final[3 * head : 3 * head + 3]
            lse_ref[head, group : group + 1, :] = top + jnp.log2(total)
            rows_out = (mixed / total).T.astype(jnp.bfloat16)
            for n, ref in enumerate(out_refs):
                ref[pl.ds(group * rows, rows), pl.ds(head * HEAD, HEAD)] = rows_out[
                    n * rows : (n + 1) * rows
                ]


def attention_backward_body(sets, step_heads, rows, keys, scale, first_ref, *refs):
    query_refs, grad_refs, out_refs = (refs[n * sets : (n + 1) * sets] for n in range(3))
    key_ref, value_ref, lse_ref, key_info, query_info = refs[3 * sets : 3 * sets + 5]
    key_cos, key_sin = refs[3 * sets + 5 : 3 * sets + 7]
    table_refs = refs[3 * sets + 7 : 5 * sets + 7]
    rest = refs[5 * sets + 7 :]
    dq_refs = rest[:sets]
    dk_ref, dv_ref, bias_ref, flipped_ref, dk_acc, dv_acc = rest[sets:]
    softmax_scale = scale / LOG2E

    @pl.when(pl.program_id(0) == 0)
    def _():
        fill_bias(bias_ref, key_info, query_info, keys)

    dk_acc[...] = jnp.zeros_like(dk_acc)
    dv_acc[...] = jnp.zeros_like(dv_acc)
    for head in range(step_heads):
        lanes = pl.ds(head * HEAD, HEAD)
        for block in range(GROUPS):
            values = key_ref[pl.ds(block * keys, keys), lanes].astype(jnp.float32)
            flipped_ref[head, block] = values.T.astype(jnp.bfloat16)
    for group in range(GROUPS):
        queries, grads, centres, tops = [], [], [], []
        for head in range(step_heads):
            lanes = pl.ds(head * HEAD, HEAD)
            queries.append(group_rows(query_refs, group, rows, lanes))
            grad = group_rows(grad_refs, group, rows, lanes)
            out = group_rows(out_refs, group, rows, lanes)
            product = grad.astype(jnp.float32) * out.astype(jnp.float32)
            centres.append(jnp.sum(product.T, axis=0, keepdims=True))
            grads.append(grad)
            tops.append(lse_ref[head, group : group + 1, :])

        def one(block, carry, group=group, queries=queries, grads=grads, centres=centres, tops=tops):
            at = pl.multiple_of(block * keys, 16)
            bias = bias_ref[group * (group + 1) // 2 + block]
            result = []
            for head in range(step_heads):
                lanes = pl.ds(head * HEAD, HEAD)
                key_rows = key_ref[pl.ds(at, keys), lanes]
                scores = dot_nt(key_rows, queries[head])
                probs = jnp.exp2(scores * scale + (bias - tops[head]))
                grad_probs = dot_nt(value_ref[pl.ds(at, keys), lanes], grads[head])
                grad_scores = (probs * (grad_probs - centres[head])).astype(jnp.bfloat16)
                dv_acc[pl.ds(at, keys), lanes] += dot_nn(probs.astype(jnp.bfloat16), grads[head])
                dk_acc[pl.ds(at, keys), lanes] += dot_nn(grad_scores, queries[head])
                result.append(carry[head] + dot_nn(flipped_ref[head, block], grad_scores))
            return tuple(result)

        start = (jnp.zeros((HEAD, sets * rows), jnp.float32),) * step_heads
        final = lax.fori_loop(0, group + 1, one, start)
        for head in range(step_heads):
            dq = final[head].T * softmax_scale
            for n, ref in enumerate(dq_refs):
                span = pl.ds(group * rows, rows)
                turned = spin(
                    dq[n * rows : (n + 1) * rows], table_refs[2 * n][span, :], table_refs[2 * n + 1][span, :]
                )
                ref[span, pl.ds(head * HEAD, HEAD)] = turned.astype(jnp.bfloat16)
    for head in range(step_heads):
        lanes = pl.ds(head * HEAD, HEAD)
        for block in range(GROUPS):
            span = pl.ds(block * keys, keys)
            turned = spin(dk_acc[span, lanes] * softmax_scale, key_cos[span, :], key_sin[span, :])
            dk_ref[span, lanes] = turned.astype(jnp.bfloat16)
            dv_ref[span, lanes] = dv_acc[span, lanes].astype(jnp.bfloat16)


def whole_block(shape):
    return pl.BlockSpec(shape, lambda h, first: (0,) * len(shape))


def attention_forward(queries, starts, keys_all, values_all, key_info, query_info, heads):
    sets, total_rows, tokens = len(queries), queries[0].shape[0], keys_all.shape[0]
    rows, keys = total_rows // GROUPS, tokens // GROUPS
    step_heads = 2
    wide = step_heads * HEAD
    scale = HEAD ** (-0.5) * LOG2E
    query_specs = [
        pl.BlockSpec((total_rows, wide), lambda h, first, n=n: (0, first[n] + h)) for n in range(sets)
    ]
    plain = pl.BlockSpec((total_rows, wide), lambda h, first: (0, h))
    side = pl.BlockSpec((tokens, wide), lambda h, first: (0, h))
    return pl.pallas_call(
        functools.partial(attention_forward_body, sets, step_heads, rows, keys, scale),
        grid_spec=pltpu.PrefetchScalarGridSpec(
            num_scalar_prefetch=1,
            grid=(heads // step_heads,),
            in_specs=query_specs
            + [side, side, whole_block(key_info.shape), whole_block(query_info.shape)],
            out_specs=[plain] * sets
            + [pl.BlockSpec((step_heads, GROUPS, sets * rows), lambda h, first: (h, 0, 0))],
            scratch_shapes=[
                pltpu.VMEM((GROUPS * (GROUPS + 1) // 2, keys, sets * rows), jnp.float32),
                pltpu.VMEM((step_heads, GROUPS, HEAD, keys), jnp.bfloat16),
            ],
        ),
        out_shape=[jax.ShapeDtypeStruct((total_rows, heads * HEAD), jnp.bfloat16)] * sets
        + [jax.ShapeDtypeStruct((heads, GROUPS, sets * rows), jnp.float32)],
        compiler_params=pltpu.CompilerParams(vmem_limit_bytes=VMEM_BYTES),
        name="attention_forward",
    )(starts, *queries, keys_all, values_all, key_info, query_info)


def attention_backward(
    queries, starts, grads, outs, keys_all, values_all, lse, key_info, query_info, key_tables, row_tables, heads
):
    sets, total_rows, tokens = len(queries), queries[0].shape[0], keys_all.shape[0]
    rows, keys = total_rows // GROUPS, tokens // GROUPS
    step_heads = 1
    wide = step_heads * HEAD
    scale = HEAD ** (-0.5) * LOG2E
    shifted = [
        pl.BlockSpec((total_rows, wide), lambda h, first, n=n: (0, first[n] + h)) for n in range(sets)
    ]
    plain = pl.BlockSpec((total_rows, wide), lambda h, first: (0, h))
    side = pl.BlockSpec((tokens, wide), lambda h, first: (0, h))
    return pl.pallas_call(
        functools.partial(attention_backward_body, sets, step_heads, rows, keys, scale),
        grid_spec=pltpu.PrefetchScalarGridSpec(
            num_scalar_prefetch=1,
            grid=(heads // step_heads,),
            in_specs=shifted
            + shifted
            + [plain] * sets
            + [
                side,
                side,
                pl.BlockSpec((step_heads, GROUPS, sets * rows), lambda h, first: (h, 0, 0)),
                whole_block(key_info.shape),
                whole_block(query_info.shape),
                whole_block((tokens, HEAD)),
                whole_block((tokens, HEAD)),
            ]
            + [whole_block((total_rows, HEAD))] * (2 * sets),
            out_specs=[plain] * sets + [side, side],
            scratch_shapes=[
                pltpu.VMEM((GROUPS * (GROUPS + 1) // 2, keys, sets * rows), jnp.float32),
                pltpu.VMEM((step_heads, GROUPS, HEAD, keys), jnp.bfloat16),
                pltpu.VMEM((tokens, wide), jnp.float32),
                pltpu.VMEM((tokens, wide), jnp.float32),
            ],
        ),
        out_shape=[jax.ShapeDtypeStruct((total_rows, heads * HEAD), jnp.bfloat16)] * sets
        + [jax.ShapeDtypeStruct((tokens, heads * HEAD), jnp.bfloat16)] * 2,
        compiler_params=pltpu.CompilerParams(vmem_limit_bytes=VMEM_BYTES),
        name="attention_backward",
    )(
        starts,
        *queries,
        *grads,
        *outs,
        keys_all,
        values_all,
        lse,
        key_info,
        query_info,
        *key_tables,
        *[table for pair in row_tables for table in pair],
    )


def project_body(tile, x_ref, weight_ref, cos_ref, sin_ref, out_ref):
    for at in range(0, x_ref.shape[0], tile):
        span = pl.ds(at, tile)
        product = dot_nn(x_ref[span, :], weight_ref[...])
        for lane in range(0, out_ref.shape[1], HEAD):
            turned = spin(product[:, lane : lane + HEAD], cos_ref[span, :], sin_ref[span, :])
            out_ref[span, lane : lane + HEAD] = turned.astype(jnp.bfloat16)


def project_queries(rows_in, weight, tables):
    rows, depth = rows_in.shape
    columns = weight.shape[1]
    block = 512
    return pl.pallas_call(
        functools.partial(project_body, rows // GROUPS),
        grid=(columns // block,),
        in_specs=[
            pl.BlockSpec((rows, depth), lambda j: (0, 0)),
            pl.BlockSpec((depth, block), lambda j: (0, j)),
            pl.BlockSpec((rows, HEAD), lambda j: (0, 0)),
            pl.BlockSpec((rows, HEAD), lambda j: (0, 0)),
        ],
        out_specs=pl.BlockSpec((rows, block), lambda j: (0, j)),
        out_shape=jax.ShapeDtypeStruct((rows, columns), jnp.bfloat16),
        compiler_params=pltpu.CompilerParams(vmem_limit_bytes=VMEM_BYTES),
        name="project_queries",
    )(rows_in, weight, *tables)


def keys_values_body(half, x_ref, weight_ref, cos_ref, sin_ref, key_ref, value_ref):
    rows = x_ref.shape[1]
    for source in range(x_ref.shape[0]):
        span = pl.ds(source * rows, rows)
        product = dot_nn(x_ref[source], weight_ref[0])
        for lane in range(0, half, HEAD):
            turned = spin(product[:, lane : lane + HEAD], cos_ref[span, :], sin_ref[span, :])
            key_ref[span, lane : lane + HEAD] = turned.astype(jnp.bfloat16)
        value_ref[span, :] = product[:, half:].astype(jnp.bfloat16)


def project_keys_values(gathered, weights, tables):
    sources, rows, unused = gathered.shape
    parts, depth, columns = weights.shape
    half, tokens = columns // 2, sources * rows
    return pl.pallas_call(
        functools.partial(keys_values_body, half),
        grid=(parts,),
        in_specs=[
            pl.BlockSpec((sources, rows, depth), lambda j: (0, 0, 0)),
            pl.BlockSpec((1, depth, columns), lambda j: (j, 0, 0)),
            pl.BlockSpec((tokens, HEAD), lambda j: (0, 0)),
            pl.BlockSpec((tokens, HEAD), lambda j: (0, 0)),
        ],
        out_specs=[pl.BlockSpec((tokens, half), lambda j: (0, j))] * 2,
        out_shape=[jax.ShapeDtypeStruct((tokens, parts * half), jnp.bfloat16)] * 2,
        compiler_params=pltpu.CompilerParams(vmem_limit_bytes=VMEM_BYTES),
        name="project_keys_values",
    )(gathered, weights, *tables)


def merge_body(tile, plan_ref, slots_ref, dk_ref, dv_ref, weight_ref, out_ref, acc_ref):
    part = pl.program_id(1)
    sources, rows = plan_ref.shape[0], plan_ref.shape[1]
    ck = dk_ref.shape[1]

    @pl.when(part == 0)
    def _():
        for source in range(sources):
            acc_ref[pl.ds(source * rows, rows), :] = dot_nn(plan_ref[source], slots_ref[source])

    last = part == pl.num_programs(1) - 1
    for at in range(0, acc_ref.shape[0], tile):
        span = pl.ds(at, tile)
        acc_ref[span, :] += dot_nt(dk_ref[span, :], weight_ref[0, :, :ck]) + dot_nt(
            dv_ref[span, :], weight_ref[0, :, ck:]
        )

    @pl.when(last)
    def _():
        out_ref[...] = acc_ref[...].astype(jnp.bfloat16)


def merge_hidden_grads(plan, slots, grad_keys, grad_values, weights):
    sources, rows, capacity = plan.shape
    parts, depth, columns = weights.shape
    ck, tokens = columns // 2, sources * rows
    wide = depth // 2
    return pl.pallas_call(
        functools.partial(merge_body, tokens // GROUPS),
        grid=(2, parts),
        in_specs=[
            pl.BlockSpec((sources, rows, capacity), lambda i, j: (0, 0, 0)),
            pl.BlockSpec((sources, capacity, wide), lambda i, j: (0, 0, i)),
            pl.BlockSpec((tokens, ck), lambda i, j: (0, j)),
            pl.BlockSpec((tokens, ck), lambda i, j: (0, j)),
            pl.BlockSpec((1, wide, columns), lambda i, j: (j, i, 0)),
        ],
        out_specs=pl.BlockSpec((tokens, wide), lambda i, j: (0, i)),
        out_shape=jax.ShapeDtypeStruct((tokens, depth), jnp.bfloat16),
        scratch_shapes=[pltpu.VMEM((tokens, wide), jnp.float32)],
        compiler_params=pltpu.CompilerParams(vmem_limit_bytes=VMEM_BYTES),
        name="merge_hidden_grads",
    )(plan, slots, grad_keys, grad_values, weights)


D = 2048
HEADS = 16
ATT_EXPERTS = 8
FFN_EXPERTS = 4
TRUNK = 1024
SEG = 96
TREE_LEN = 2176
NODES = 13

epsilon = 1e-06
highest = lax.Precision.HIGHEST
bf16 = jnp.bfloat16
f32 = jnp.float32


def tree_layout(places):
    after_trunk = places - TRUNK
    after_branch = after_trunk - 4 * SEG
    segments = jnp.where(
        places < TRUNK,
        0,
        jnp.where(after_branch < 0, 1 + after_trunk // SEG, 5 + after_branch // SEG),
    )
    depths = jnp.where(
        places < TRUNK,
        places,
        jnp.where(after_branch < 0, TRUNK + after_trunk % SEG, TRUNK + SEG + after_branch % SEG),
    )
    return (segments.astype(jnp.int32), depths.astype(jnp.int32))


def rotation_tables(depths):
    half_size = HEAD // 2
    frequency = 10000.0 ** (-jnp.arange(half_size, dtype=f32) * 2.0 / HEAD)
    angles = depths.astype(f32)[:, None] * frequency[None, :]
    cosine, sine = jnp.cos(angles), jnp.sin(angles)
    cosines = jnp.concatenate([cosine, cosine], axis=1)
    forward = jnp.concatenate([-sine, sine], axis=1)
    return (cosines, forward), (cosines, -forward)


def lookup(table, indices):
    nodes = jnp.arange(NODES, dtype=jnp.int32)
    return jnp.sum(jnp.where(indices[:, None] == nodes[None, :], table[None, :], 0), axis=1)


def running_count(chosen):
    rows = chosen.shape[-1]
    index = jnp.arange(rows, dtype=jnp.int32)
    upto = (index[:, None] <= index[None, :]).astype(bf16)
    return jnp.dot(chosen.astype(bf16), upto, preferred_element_type=f32).astype(jnp.int32) - 1


def source_plan(routes, expert, capacity):
    chosen = jnp.any(routes == expert, axis=2)
    ranking = running_count(chosen)
    slots = jnp.arange(capacity, dtype=jnp.int32)
    return chosen[:, None, :] & (ranking[:, None, :] == slots[None, :, None])


def token_picks(routes, experts, capacity):
    labels = jnp.arange(experts, dtype=jnp.int32)
    hits = routes.T[:, None, :] == labels[None, :, None]
    ranking = running_count(hits[0] | hits[1])
    slots = jnp.arange(capacity, dtype=jnp.int32)
    picks = hits[:, :, None, :] & (ranking[None, :, None, :] == slots[None, None, :, None])
    return picks.astype(bf16), hits[0].T.astype(f32), hits[1].T.astype(f32)


def fill_slots(picks, pair):
    return jnp.einsum("kecr,krd->ecd", picks, pair, preferred_element_type=f32).astype(bf16)


def read_slots(picks, slots):
    return jnp.einsum("kecr,ecd->krd", picks, slots, preferred_element_type=f32)


def gate_values(hidden, router, first, second):
    logits = jnp.dot(hidden.astype(f32), router, precision=highest)
    picked = jnp.stack([jnp.sum(logits * first, axis=1), jnp.sum(logits * second, axis=1)], axis=1)
    return jax.nn.softmax(picked, axis=1)


def router_grads(hidden, router, gates, first, second, picked_grad):
    logit_pick = gates * (picked_grad - jnp.sum(gates * picked_grad, axis=1, keepdims=True))
    logit_grad = logit_pick[:, 0:1] * first + logit_pick[:, 1:2] * second
    router_grad = jnp.dot(hidden.astype(f32).T, logit_grad, precision=highest)
    hidden_grad = jnp.dot(logit_grad, router.T, precision=highest)
    return (router_grad, hidden_grad)


def rms_parts(values):
    inverse = lax.rsqrt(jnp.mean(values * values, axis=-1, keepdims=True) + epsilon)
    return (values * inverse, inverse)


def norm_back(grad_normed, normed, inverse):
    return inverse * (grad_normed - normed * jnp.mean(grad_normed * normed, axis=-1, keepdims=True))


def pair_grads(gates, branches, upstream):
    gate_grad = jnp.stack([jnp.sum(upstream * branches[k], axis=1) for k in range(2)], axis=1)
    scaled = jnp.stack([gates[:, k : k + 1] * upstream for k in range(2)]).astype(bf16)
    return gate_grad, scaled


def exchange(slots):
    return lax.all_to_all(slots, "expert", split_axis=0, concat_axis=0, tiled=True)


def shift(values, step, size, devices):
    moves = [(i, i // size * size + (i % size + step) % size) for i in range(devices)]
    return lax.ppermute(values, "expert", moves)


def group_gather(rows, size, devices):
    return jnp.concatenate([rows] + [shift(rows, step, size, devices) for step in range(1, size)])


def group_reduce(partial, size, devices):
    parts = partial.reshape(size, -1, partial.shape[1])
    total = parts[0].astype(f32)
    for step in range(1, size):
        total = total + shift(parts[step], -step, size, devices).astype(f32)
    return total.astype(bf16)


def dot_tn(left, right):
    return lax.dot_general(left, right, (((0,), (0,)), ((), ())), preferred_element_type=f32)


def body(
    tokens,
    teacher,
    att_routes,
    ffn_routes,
    parent,
    valid,
    gain_one,
    kv_weight,
    att_router,
    q_weight,
    o_weight,
    gain_two,
    ffn_router,
    gate_weight,
    up_weight,
    down_weight,
):
    row_count = tokens.shape[0]
    devices, replicas = lax.axis_size("expert"), lax.axis_size("dp")
    my_index, my_replica = lax.axis_index("expert"), lax.axis_index("dp")
    core = my_index % 2
    att_copies, ffn_copies = devices // ATT_EXPERTS, devices // FFN_EXPERTS
    att_capacity, ffn_capacity = row_count * 13 // 40, row_count * 13 // 20
    token_count = row_count * devices
    half = HEADS * HEAD // 2
    assert token_count == TREE_LEN * parent.shape[0] and parent.shape[0] == 1
    pair = [(i, i ^ 1) for i in range(devices)]
    own_places = my_index * row_count + jnp.arange(row_count, dtype=jnp.int32)

    x_in = tokens.astype(f32)
    normed_one, inverse_one = rms_parts(x_in)
    hidden = (normed_one * gain_one).astype(bf16)
    weight_rows = kv_weight.shape[0]
    piece = half // replicas
    kv_share = lax.dynamic_slice_in_dim(
        kv_weight.reshape(weight_rows, 4, replicas, piece), my_replica, 1, 2
    )
    kv_share = (
        kv_share.reshape(weight_rows, 2, 2, piece).transpose(0, 2, 1, 3).reshape(weight_rows, 4 * piece)
    )
    route_row = jnp.pad(att_routes.astype(bf16).reshape(1, -1), ((0, row_count - weight_rows - 1), (0, 4 * piece - 2 * row_count)))
    sending = jnp.concatenate([hidden, jnp.concatenate([kv_share, route_row])], axis=1)
    gathered = lax.all_gather(sending, "expert", axis=0)
    kv_half = lax.dynamic_slice_in_dim(gathered[:, :weight_rows], D + core * 2 * piece, 2 * piece, 2)
    kv_blocks = lax.all_gather(kv_half.reshape(D, 2 * piece), "dp", axis=0)
    all_routes = (
        gathered[:, weight_rows, D : D + 2 * row_count].astype(jnp.int32).reshape(devices, row_count, 2)
    )

    tree_places = jnp.arange(token_count, dtype=jnp.int32)
    tree_segments, tree_depths = tree_layout(tree_places)
    key_forward, key_backward = rotation_tables(tree_depths)
    key_info = jnp.pad(jnp.stack([tree_places, tree_segments], axis=1), ((0, 0), (0, 6)))
    experts_here = [my_index // att_copies]
    if att_copies == 1:
        experts_here.append(my_index ^ 1)
    plans = [source_plan(all_routes, expert, att_capacity) for expert in experts_here]
    slot_tables, query_parts = [], []
    for plan in plans:
        places = jnp.sum(
            jnp.where(plan, tree_places.reshape(devices, 1, row_count), 0), axis=2
        ).reshape(-1)
        segments, depths = tree_layout(places)
        parents = lookup(parent[0], segments)
        grands = lookup(parent[0], parents)
        query_parts.append(jnp.stack([places, segments, parents, grands]).reshape(4, GROUPS, -1))
        slot_tables.append(rotation_tables(depths))
    query_info = jnp.concatenate(query_parts, axis=2).transpose(1, 0, 2)
    own_plan = plans[0].astype(bf16)
    query_inputs = jnp.einsum(
        "scr,srd->scd", own_plan, gathered[:, :, :D], preferred_element_type=f32
    ).astype(bf16).reshape(-1, D)

    queries = project_queries(query_inputs, q_weight, slot_tables[0][0])
    keys_all, values_all = project_keys_values(gathered, kv_blocks, key_forward)

    def far_half(values):
        return lax.ppermute(
            lax.dynamic_slice_in_dim(values, (1 - core) * half, half, 1), "expert", pair
        )

    def join_halves(mine, sibling):
        other = lax.ppermute(sibling, "expert", pair)
        return jnp.where(
            core == 0,
            jnp.concatenate([mine, other], axis=1),
            jnp.concatenate([other, mine], axis=1),
        )

    heads = half // HEAD
    query_sets = [queries]
    starts = jnp.zeros((2,), jnp.int32)
    if att_copies == 1:
        query_sets.append(far_half(queries))
        starts = jnp.stack([core * heads, 0]).astype(jnp.int32)
    *att_outs, lse = attention_forward(
        query_sets, starts // 2, keys_all, values_all, key_info, query_info, heads
    )
    att_rows = join_halves(*att_outs) if att_copies == 1 else att_outs[0]
    att_partial = lax.dot_general(
        att_rows, o_weight, (((1,), (1,)), ((), ())), preferred_element_type=f32
    ).astype(bf16)
    att_back = exchange(att_partial.reshape(devices, att_capacity, D))
    att_picks, att_first, att_second = token_picks(att_routes, ATT_EXPERTS, att_capacity)
    att_gates = gate_values(hidden, att_router, att_first, att_second)
    if att_copies > 1:
        att_back = (
            att_back.astype(f32).reshape(ATT_EXPERTS, att_copies, att_capacity, D).sum(axis=1).astype(bf16)
        )
    att_branches = read_slots(att_picks, att_back)
    x_mid = x_in + att_gates[:, 0:1] * att_branches[0] + att_gates[:, 1:2] * att_branches[1]

    normed_two, inverse_two = rms_parts(x_mid)
    hidden_two = (normed_two * gain_two).astype(bf16)
    ffn_picks, ffn_first, ffn_second = token_picks(ffn_routes, FFN_EXPERTS, ffn_capacity)
    ffn_gates = gate_values(hidden_two, ffn_router, ffn_first, ffn_second)

    def to_experts(slots):
        rows = exchange(slots.reshape(devices, ffn_capacity // ffn_copies, D))
        return group_gather(rows.reshape(-1, D), ffn_copies, devices)

    def to_tokens(partial):
        rows = group_reduce(partial.astype(bf16), ffn_copies, devices)
        back = exchange(rows.reshape(devices, ffn_capacity // ffn_copies, D))
        return read_slots(ffn_picks, back.reshape(FFN_EXPERTS, ffn_capacity, D))

    ffn_inputs = to_experts(
        jnp.einsum(
            "ecr,rd->ecd", ffn_picks[0] + ffn_picks[1], hidden_two, preferred_element_type=f32
        ).astype(bf16)
    )
    gate_pre = jnp.dot(ffn_inputs, gate_weight, preferred_element_type=f32)
    up_pre = jnp.dot(ffn_inputs, up_weight, preferred_element_type=f32)
    sigmoid_gate = jax.nn.sigmoid(gate_pre)
    silu_gate = gate_pre * sigmoid_gate
    activated = (silu_gate * up_pre).astype(bf16)
    ffn_branches = to_tokens(
        lax.dot_general(activated, down_weight, (((1,), (1,)), ((), ())), preferred_element_type=f32)
    )
    result = x_mid + ffn_gates[:, 0:1] * ffn_branches[0] + ffn_gates[:, 1:2] * ffn_branches[1]

    tree_global = my_replica * parent.shape[0] + own_places // TREE_LEN
    tree_labels = jnp.arange(valid.shape[0], dtype=jnp.int32)
    limits = jnp.sum(
        jnp.where(tree_global[:, None] == tree_labels[None, :], valid[None, :], 0), axis=1
    )
    counted = own_places % TREE_LEN < limits
    loss_factor = valid.shape[0] * TREE_LEN / jnp.sum(valid).astype(f32)
    grad_result = jnp.where(counted[:, None], (result - teacher.astype(f32)) * loss_factor, 0.0)

    ffn_gate_grad, ffn_scaled = pair_grads(ffn_gates, ffn_branches, grad_result)
    grad_ffn_out = to_experts(fill_slots(ffn_picks, ffn_scaled))
    grad_down = dot_tn(grad_ffn_out, activated).astype(bf16)
    grad_ffn_out, grad_down = lax.optimization_barrier((grad_ffn_out, grad_down))
    summed_down = lax.psum_scatter(grad_down, "dp", scatter_dimension=0, tiled=True)
    grad_activated = jnp.dot(grad_ffn_out, down_weight, preferred_element_type=f32)
    grad_gate_pre = (
        grad_activated * up_pre * sigmoid_gate * (1.0 + gate_pre * (1.0 - sigmoid_gate))
    ).astype(bf16)
    grad_up_pre = (grad_activated * silu_gate).astype(bf16)
    grad_ffn_in = lax.dot_general(
        grad_gate_pre, gate_weight, (((1,), (1,)), ((), ())), preferred_element_type=f32
    ) + lax.dot_general(
        grad_up_pre, up_weight, (((1,), (1,)), ((), ())), preferred_element_type=f32
    )
    grad_gate = dot_tn(ffn_inputs, grad_gate_pre).astype(bf16)
    grad_up = dot_tn(ffn_inputs, grad_up_pre).astype(bf16)
    summed_gate = lax.psum_scatter(grad_gate, "dp", scatter_dimension=0, tiled=True)
    summed_up = lax.psum_scatter(grad_up, "dp", scatter_dimension=0, tiled=True)
    ffn_grad_pair = to_tokens(grad_ffn_in)
    grad_ffn_router, hidden_two_extra = router_grads(
        hidden_two, ffn_router, ffn_gates, ffn_first, ffn_second, ffn_gate_grad
    )
    grad_hidden_two = ffn_grad_pair[0] + ffn_grad_pair[1] + hidden_two_extra
    grad_gain_two = jnp.sum(grad_hidden_two * normed_two, axis=0)
    grad_mid = grad_result + norm_back(grad_hidden_two * gain_two, normed_two, inverse_two)

    att_gate_grad, att_scaled = pair_grads(att_gates, att_branches, grad_mid)
    att_slots = fill_slots(att_picks, att_scaled)
    if att_copies > 1:
        att_slots = jnp.repeat(att_slots, att_copies, axis=0)
    grad_att_out = exchange(att_slots).reshape(-1, D)
    grad_o = dot_tn(grad_att_out, att_rows).astype(bf16)
    grad_att_out, grad_o, grad_gate, grad_up = lax.optimization_barrier(
        (grad_att_out, grad_o, grad_gate, grad_up)
    )
    summed_o = lax.psum_scatter(grad_o, "dp", scatter_dimension=0, tiled=True)
    grad_heads = jnp.dot(grad_att_out, o_weight, preferred_element_type=f32).astype(bf16)
    grad_sets = [grad_heads]
    if att_copies == 1:
        grad_sets.append(far_half(grad_heads))
    *grad_queries, grad_keys, grad_values = attention_backward(
        query_sets,
        starts,
        grad_sets,
        att_outs,
        keys_all,
        values_all,
        lse,
        key_info,
        query_info,
        key_backward,
        [tables[1] for tables in slot_tables],
        heads,
    )
    grad_query_pre = join_halves(*grad_queries) if att_copies == 1 else grad_queries[0]
    grad_query_in = lax.dot_general(
        grad_query_pre, q_weight, (((1,), (1,)), ((), ())), preferred_element_type=f32
    ).astype(bf16)
    grad_q = dot_tn(query_inputs, grad_query_pre).astype(bf16)
    hidden_rows = gathered[:, :, :D].reshape(token_count, D)
    grad_kv = jnp.concatenate(
        [dot_tn(hidden_rows, grad_keys).astype(bf16), dot_tn(hidden_rows, grad_values).astype(bf16)], axis=1
    )
    summed_kv = lax.psum_scatter(grad_kv, "dp", scatter_dimension=0, tiled=True)
    summed_q = lax.psum_scatter(grad_q, "dp", scatter_dimension=0, tiled=True)

    merged = merge_hidden_grads(
        own_plan.transpose(0, 2, 1),
        grad_query_in.reshape(devices, att_capacity, D),
        grad_keys,
        grad_values,
        kv_blocks,
    ).reshape(devices // 2, 2, row_count, D)
    kept = lax.dynamic_index_in_dim(merged, core, 1, keepdims=False)
    passed = lax.ppermute(
        lax.dynamic_index_in_dim(merged, 1 - core, 1, keepdims=False), "expert", pair
    )
    chip_sum = (kept.astype(f32) + passed.astype(f32)).astype(bf16)
    same_core = [[2 * i + c for i in range(devices // 2)] for c in range(2)]
    arrived = lax.all_to_all(
        chip_sum, "expert", split_axis=0, concat_axis=0, axis_index_groups=same_core, tiled=True
    )
    grad_att_router, hidden_one_extra = router_grads(
        hidden, att_router, att_gates, att_first, att_second, att_gate_grad
    )
    grad_hidden_one = jnp.sum(arrived.astype(f32), axis=0) + hidden_one_extra
    grad_gain_one = jnp.sum(grad_hidden_one * normed_one, axis=0)
    grad_input = grad_mid + norm_back(grad_hidden_one * gain_one, normed_one, inverse_one)

    everyone = devices * replicas
    smalls = [grad_gain_one, grad_gain_two, grad_att_router, grad_ffn_router]
    packed = jnp.concatenate([small.reshape(everyone, -1) for small in smalls], axis=1)
    own_smalls = jnp.sum(
        lax.all_to_all(packed, ("dp", "expert"), split_axis=0, concat_axis=0, tiled=True), axis=0
    )
    share = D // everyone
    shared_gain_one = own_smalls[:share]
    shared_gain_two = own_smalls[share : 2 * share]
    shared_att_router = own_smalls[2 * share : (2 + ATT_EXPERTS) * share].reshape(share, ATT_EXPERTS)
    shared_ffn_router = own_smalls[(2 + ATT_EXPERTS) * share :].reshape(share, FFN_EXPERTS)

    kv_rows = exchange(summed_kv.reshape(devices, -1, 2 * half))
    kv_sum = jnp.sum(kv_rows.astype(f32).reshape(devices // 2, 2, -1, 2, half), axis=0)
    shared_kv = kv_sum.transpose(1, 2, 0, 3).reshape(-1, 4 * half)

    return (
        result.astype(bf16),
        grad_input.astype(bf16),
        shared_gain_one,
        shared_kv,
        shared_att_router,
        summed_q.astype(f32),
        summed_o.astype(f32),
        shared_gain_two,
        shared_ffn_router,
        summed_gate.astype(f32),
        summed_up.astype(f32),
        summed_down.astype(f32),
    )


def solution(mesh):
    in_specs = (
        P(("dp", "expert"), None),
        P(("dp", "expert"), None),
        P(("dp", "expert"), None),
        P(("dp", "expert"), None),
        P("dp", None),
        P(),
        P(),
        P("expert", None),
        P(),
        P(None, "expert"),
        P(None, "expert"),
        P(),
        P(),
        P(None, "expert"),
        P(None, "expert"),
        P(None, "expert"),
    )
    out_specs = (
        P(("dp", "expert"), None),
        P(("dp", "expert"), None),
        P(("dp", "expert")),
        P(("dp", "expert"), None),
        P(("dp", "expert"), None),
        P("dp", "expert"),
        P("dp", "expert"),
        P(("dp", "expert")),
        P(("dp", "expert"), None),
        P("dp", "expert"),
        P("dp", "expert"),
        P("dp", "expert"),
    )
    return jax.shard_map(body, mesh=mesh, in_specs=in_specs, out_specs=out_specs, check_vma=False)
```

```python
import functools
import jax
import jax.numpy as jnp
from jax import lax
from jax.experimental import pallas as pl
from jax.experimental.pallas import tpu as pltpu
from jax.sharding import PartitionSpec as P

HEAD = 128
GROUPS = 4
LOG2E = 1.4426950408889634
VMEM_BYTES = 60 * 1024 * 1024


def dot_nt(left, right):
    return lax.dot_general(left, right, (((1,), (1,)), ((), ())), preferred_element_type=jnp.float32)


def dot_nn(left, right):
    return jnp.dot(left, right, preferred_element_type=jnp.float32)


def spin(values, cosine, sine):
    return values * cosine + pltpu.roll(values, HEAD // 2, 1) * sine


def fill_bias(bias_ref, key_ref, query_ref, keys):
    for group in range(GROUPS):
        place = query_ref[group, 0:1, :]
        own, parent, grand = (query_ref[group, 1 + n : 2 + n, :] for n in range(3))

        def one(block, carry, group=group, place=place, own=own, parent=parent, grand=grand):
            at = pl.multiple_of(block * keys, 16)
            key_place = key_ref[pl.ds(at, keys), 0:1]
            key_segment = key_ref[pl.ds(at, keys), 1:2]
            related = (key_segment == own) | (key_segment == parent) | (key_segment == grand)
            allowed = related & (key_place <= place)
            bias_ref[group * (group + 1) // 2 + block] = jnp.where(allowed, 0.0, -1e30)
            return carry

        lax.fori_loop(0, group + 1, one, 0)


def group_rows(refs, group, rows, lanes):
    parts = [ref[pl.ds(group * rows, rows), lanes] for ref in refs]
    return parts[0] if len(parts) == 1 else jnp.concatenate(parts, axis=0)


def attention_forward_body(sets, step_heads, rows, keys, scale, first_ref, *refs):
    query_refs = refs[:sets]
    key_ref, value_ref, key_info, query_info = refs[sets : sets + 4]
    out_refs = refs[sets + 4 : 2 * sets + 4]
    lse_ref, bias_ref, flipped_ref = refs[2 * sets + 4 :]
    wide = sets * rows

    @pl.when(pl.program_id(0) == 0)
    def _():
        fill_bias(bias_ref, key_info, query_info, keys)

    for head in range(step_heads):
        lanes = pl.ds(head * HEAD, HEAD)
        for block in range(GROUPS):
            values = value_ref[pl.ds(block * keys, keys), lanes].astype(jnp.float32)
            flipped_ref[head, block] = values.T.astype(jnp.bfloat16)
    for group in range(GROUPS):
        queries = [
            group_rows(query_refs, group, rows, pl.ds(head * HEAD, HEAD)) for head in range(step_heads)
        ]

        def one(block, carry, group=group, queries=queries):
            at = pl.multiple_of(block * keys, 16)
            bias = bias_ref[group * (group + 1) // 2 + block]
            result = []
            for head in range(step_heads):
                top, total, mixed = carry[3 * head : 3 * head + 3]
                scores = dot_nt(key_ref[pl.ds(at, keys), pl.ds(head * HEAD, HEAD)], queries[head])
                scores = scores * scale + bias
                new_top = jnp.maximum(top, jnp.max(scores, axis=0, keepdims=True))
                fade = jnp.exp2(top - new_top)
                parts = jnp.exp2(scores - new_top)
                total = total * fade + jnp.sum(parts, axis=0, keepdims=True)
                mixed = mixed * fade + dot_nn(flipped_ref[head, block], parts.astype(jnp.bfloat16))
                result += [new_top, total, mixed]
            return tuple(result)

        start = (
            jnp.full((1, wide), -1e30, jnp.float32),
            jnp.zeros((1, wide), jnp.float32),
            jnp.zeros((HEAD, wide), jnp.float32),
        ) * step_heads
        final = lax.fori_loop(0, group + 1, one, start)
        for head in range(step_heads):
            top, total, mixed = final[3 * head : 3 * head + 3]
            lse_ref[head, group : group + 1, :] = top + jnp.log2(total)
            rows_out = (mixed / total).T.astype(jnp.bfloat16)
            for n, ref in enumerate(out_refs):
                ref[pl.ds(group * rows, rows), pl.ds(head * HEAD, HEAD)] = rows_out[
                    n * rows : (n + 1) * rows
                ]


def attention_backward_body(sets, step_heads, rows, keys, scale, first_ref, *refs):
    query_refs, grad_refs, out_refs = (refs[n * sets : (n + 1) * sets] for n in range(3))
    key_ref, value_ref, lse_ref, key_info, query_info = refs[3 * sets : 3 * sets + 5]
    key_cos, key_sin = refs[3 * sets + 5 : 3 * sets + 7]
    table_refs = refs[3 * sets + 7 : 5 * sets + 7]
    rest = refs[5 * sets + 7 :]
    dq_refs = rest[:sets]
    dk_ref, dv_ref, bias_ref, flipped_ref, dk_acc, dv_acc = rest[sets:]
    softmax_scale = scale / LOG2E

    @pl.when(pl.program_id(0) == 0)
    def _():
        fill_bias(bias_ref, key_info, query_info, keys)

    dk_acc[...] = jnp.zeros_like(dk_acc)
    dv_acc[...] = jnp.zeros_like(dv_acc)
    for head in range(step_heads):
        lanes = pl.ds(head * HEAD, HEAD)
        for block in range(GROUPS):
            values = key_ref[pl.ds(block * keys, keys), lanes].astype(jnp.float32)
            flipped_ref[head, block] = values.T.astype(jnp.bfloat16)
    for group in range(GROUPS):
        queries, grads, centres, tops = [], [], [], []
        for head in range(step_heads):
            lanes = pl.ds(head * HEAD, HEAD)
            queries.append(group_rows(query_refs, group, rows, lanes))
            grad = group_rows(grad_refs, group, rows, lanes)
            out = group_rows(out_refs, group, rows, lanes)
            product = grad.astype(jnp.float32) * out.astype(jnp.float32)
            centres.append(jnp.sum(product.T, axis=0, keepdims=True))
            grads.append(grad)
            tops.append(lse_ref[head, group : group + 1, :])

        def one(block, carry, group=group, queries=queries, grads=grads, centres=centres, tops=tops):
            at = pl.multiple_of(block * keys, 16)
            bias = bias_ref[group * (group + 1) // 2 + block]
            result = []
            for head in range(step_heads):
                lanes = pl.ds(head * HEAD, HEAD)
                key_rows = key_ref[pl.ds(at, keys), lanes]
                scores = dot_nt(key_rows, queries[head])
                probs = jnp.exp2(scores * scale + (bias - tops[head]))
                grad_probs = dot_nt(value_ref[pl.ds(at, keys), lanes], grads[head])
                grad_scores = (probs * (grad_probs - centres[head])).astype(jnp.bfloat16)
                dv_acc[pl.ds(at, keys), lanes] += dot_nn(probs.astype(jnp.bfloat16), grads[head])
                dk_acc[pl.ds(at, keys), lanes] += dot_nn(grad_scores, queries[head])
                result.append(carry[head] + dot_nn(flipped_ref[head, block], grad_scores))
            return tuple(result)

        start = (jnp.zeros((HEAD, sets * rows), jnp.float32),) * step_heads
        final = lax.fori_loop(0, group + 1, one, start)
        for head in range(step_heads):
            dq = final[head].T * softmax_scale
            for n, ref in enumerate(dq_refs):
                span = pl.ds(group * rows, rows)
                turned = spin(
                    dq[n * rows : (n + 1) * rows], table_refs[2 * n][span, :], table_refs[2 * n + 1][span, :]
                )
                ref[span, pl.ds(head * HEAD, HEAD)] = turned.astype(jnp.bfloat16)
    for head in range(step_heads):
        lanes = pl.ds(head * HEAD, HEAD)
        for block in range(GROUPS):
            span = pl.ds(block * keys, keys)
            turned = spin(dk_acc[span, lanes] * softmax_scale, key_cos[span, :], key_sin[span, :])
            dk_ref[span, lanes] = turned.astype(jnp.bfloat16)
            dv_ref[span, lanes] = dv_acc[span, lanes].astype(jnp.bfloat16)


def whole_block(shape):
    return pl.BlockSpec(shape, lambda h, first: (0,) * len(shape))


def attention_forward(queries, starts, keys_all, values_all, key_info, query_info, heads):
    sets, total_rows, tokens = len(queries), queries[0].shape[0], keys_all.shape[0]
    rows, keys = total_rows // GROUPS, tokens // GROUPS
    step_heads = 2
    wide = step_heads * HEAD
    scale = HEAD ** (-0.5) * LOG2E
    query_specs = [
        pl.BlockSpec((total_rows, wide), lambda h, first, n=n: (0, first[n] + h)) for n in range(sets)
    ]
    plain = pl.BlockSpec((total_rows, wide), lambda h, first: (0, h))
    side = pl.BlockSpec((tokens, wide), lambda h, first: (0, h))
    return pl.pallas_call(
        functools.partial(attention_forward_body, sets, step_heads, rows, keys, scale),
        grid_spec=pltpu.PrefetchScalarGridSpec(
            num_scalar_prefetch=1,
            grid=(heads // step_heads,),
            in_specs=query_specs
            + [side, side, whole_block(key_info.shape), whole_block(query_info.shape)],
            out_specs=[plain] * sets
            + [pl.BlockSpec((step_heads, GROUPS, sets * rows), lambda h, first: (h, 0, 0))],
            scratch_shapes=[
                pltpu.VMEM((GROUPS * (GROUPS + 1) // 2, keys, sets * rows), jnp.float32),
                pltpu.VMEM((step_heads, GROUPS, HEAD, keys), jnp.bfloat16),
            ],
        ),
        out_shape=[jax.ShapeDtypeStruct((total_rows, heads * HEAD), jnp.bfloat16)] * sets
        + [jax.ShapeDtypeStruct((heads, GROUPS, sets * rows), jnp.float32)],
        compiler_params=pltpu.CompilerParams(vmem_limit_bytes=VMEM_BYTES),
        name="attention_forward",
    )(starts, *queries, keys_all, values_all, key_info, query_info)


def attention_backward(
    queries, starts, grads, outs, keys_all, values_all, lse, key_info, query_info, key_tables, row_tables, heads
):
    sets, total_rows, tokens = len(queries), queries[0].shape[0], keys_all.shape[0]
    rows, keys = total_rows // GROUPS, tokens // GROUPS
    step_heads = 1
    wide = step_heads * HEAD
    scale = HEAD ** (-0.5) * LOG2E
    shifted = [
        pl.BlockSpec((total_rows, wide), lambda h, first, n=n: (0, first[n] + h)) for n in range(sets)
    ]
    plain = pl.BlockSpec((total_rows, wide), lambda h, first: (0, h))
    side = pl.BlockSpec((tokens, wide), lambda h, first: (0, h))
    return pl.pallas_call(
        functools.partial(attention_backward_body, sets, step_heads, rows, keys, scale),
        grid_spec=pltpu.PrefetchScalarGridSpec(
            num_scalar_prefetch=1,
            grid=(heads // step_heads,),
            in_specs=shifted
            + shifted
            + [plain] * sets
            + [
                side,
                side,
                pl.BlockSpec((step_heads, GROUPS, sets * rows), lambda h, first: (h, 0, 0)),
                whole_block(key_info.shape),
                whole_block(query_info.shape),
                whole_block((tokens, HEAD)),
                whole_block((tokens, HEAD)),
            ]
            + [whole_block((total_rows, HEAD))] * (2 * sets),
            out_specs=[plain] * sets + [side, side],
            scratch_shapes=[
                pltpu.VMEM((GROUPS * (GROUPS + 1) // 2, keys, sets * rows), jnp.float32),
                pltpu.VMEM((step_heads, GROUPS, HEAD, keys), jnp.bfloat16),
                pltpu.VMEM((tokens, wide), jnp.float32),
                pltpu.VMEM((tokens, wide), jnp.float32),
            ],
        ),
        out_shape=[jax.ShapeDtypeStruct((total_rows, heads * HEAD), jnp.bfloat16)] * sets
        + [jax.ShapeDtypeStruct((tokens, heads * HEAD), jnp.bfloat16)] * 2,
        compiler_params=pltpu.CompilerParams(vmem_limit_bytes=VMEM_BYTES),
        name="attention_backward",
    )(
        starts,
        *queries,
        *grads,
        *outs,
        keys_all,
        values_all,
        lse,
        key_info,
        query_info,
        *key_tables,
        *[table for pair in row_tables for table in pair],
    )


def project_body(tile, x_ref, weight_ref, cos_ref, sin_ref, out_ref):
    for at in range(0, x_ref.shape[0], tile):
        span = pl.ds(at, tile)
        product = dot_nn(x_ref[span, :], weight_ref[...])
        for lane in range(0, out_ref.shape[1], HEAD):
            turned = spin(product[:, lane : lane + HEAD], cos_ref[span, :], sin_ref[span, :])
            out_ref[span, lane : lane + HEAD] = turned.astype(jnp.bfloat16)


def project_queries(rows_in, weight, tables):
    rows, depth = rows_in.shape
    columns = weight.shape[1]
    block = 512
    return pl.pallas_call(
        functools.partial(project_body, rows // GROUPS),
        grid=(columns // block,),
        in_specs=[
            pl.BlockSpec((rows, depth), lambda j: (0, 0)),
            pl.BlockSpec((depth, block), lambda j: (0, j)),
            pl.BlockSpec((rows, HEAD), lambda j: (0, 0)),
            pl.BlockSpec((rows, HEAD), lambda j: (0, 0)),
        ],
        out_specs=pl.BlockSpec((rows, block), lambda j: (0, j)),
        out_shape=jax.ShapeDtypeStruct((rows, columns), jnp.bfloat16),
        compiler_params=pltpu.CompilerParams(vmem_limit_bytes=VMEM_BYTES),
        name="project_queries",
    )(rows_in, weight, *tables)


def keys_values_body(half, x_ref, weight_ref, cos_ref, sin_ref, key_ref, value_ref):
    rows = x_ref.shape[1]
    for source in range(x_ref.shape[0]):
        span = pl.ds(source * rows, rows)
        product = dot_nn(x_ref[source], weight_ref[0])
        for lane in range(0, half, HEAD):
            turned = spin(product[:, lane : lane + HEAD], cos_ref[span, :], sin_ref[span, :])
            key_ref[span, lane : lane + HEAD] = turned.astype(jnp.bfloat16)
        value_ref[span, :] = product[:, half:].astype(jnp.bfloat16)


def project_keys_values(gathered, weights, tables):
    sources, rows, unused = gathered.shape
    parts, depth, columns = weights.shape
    half, tokens = columns // 2, sources * rows
    return pl.pallas_call(
        functools.partial(keys_values_body, half),
        grid=(parts,),
        in_specs=[
            pl.BlockSpec((sources, rows, depth), lambda j: (0, 0, 0)),
            pl.BlockSpec((1, depth, columns), lambda j: (j, 0, 0)),
            pl.BlockSpec((tokens, HEAD), lambda j: (0, 0)),
            pl.BlockSpec((tokens, HEAD), lambda j: (0, 0)),
        ],
        out_specs=[pl.BlockSpec((tokens, half), lambda j: (0, j))] * 2,
        out_shape=[jax.ShapeDtypeStruct((tokens, parts * half), jnp.bfloat16)] * 2,
        compiler_params=pltpu.CompilerParams(vmem_limit_bytes=VMEM_BYTES),
        name="project_keys_values",
    )(gathered, weights, *tables)


def merge_body(tile, plan_ref, slots_ref, dk_ref, dv_ref, weight_ref, out_ref, acc_ref):
    part = pl.program_id(1)
    sources, rows = plan_ref.shape[0], plan_ref.shape[1]
    ck = dk_ref.shape[1]

    @pl.when(part == 0)
    def _():
        for source in range(sources):
            acc_ref[pl.ds(source * rows, rows), :] = dot_nn(plan_ref[source], slots_ref[source])

    last = part == pl.num_programs(1) - 1
    for at in range(0, acc_ref.shape[0], tile):
        span = pl.ds(at, tile)
        acc_ref[span, :] += dot_nt(dk_ref[span, :], weight_ref[0, :, :ck]) + dot_nt(
            dv_ref[span, :], weight_ref[0, :, ck:]
        )

    @pl.when(last)
    def _():
        out_ref[...] = acc_ref[...].astype(jnp.bfloat16)


def merge_hidden_grads(plan, slots, grad_keys, grad_values, weights):
    sources, rows, capacity = plan.shape
    parts, depth, columns = weights.shape
    ck, tokens = columns // 2, sources * rows
    wide = depth // 2
    return pl.pallas_call(
        functools.partial(merge_body, tokens // GROUPS),
        grid=(2, parts),
        in_specs=[
            pl.BlockSpec((sources, rows, capacity), lambda i, j: (0, 0, 0)),
            pl.BlockSpec((sources, capacity, wide), lambda i, j: (0, 0, i)),
            pl.BlockSpec((tokens, ck), lambda i, j: (0, j)),
            pl.BlockSpec((tokens, ck), lambda i, j: (0, j)),
            pl.BlockSpec((1, wide, columns), lambda i, j: (j, i, 0)),
        ],
        out_specs=pl.BlockSpec((tokens, wide), lambda i, j: (0, i)),
        out_shape=jax.ShapeDtypeStruct((tokens, depth), jnp.bfloat16),
        scratch_shapes=[pltpu.VMEM((tokens, wide), jnp.float32)],
        compiler_params=pltpu.CompilerParams(vmem_limit_bytes=VMEM_BYTES),
        name="merge_hidden_grads",
    )(plan, slots, grad_keys, grad_values, weights)


D = 2048
HEADS = 16
ATT_EXPERTS = 8
FFN_EXPERTS = 4
TRUNK = 1024
SEG = 96
TREE_LEN = 2176
NODES = 13

epsilon = 1e-06
highest = lax.Precision.HIGHEST
bf16 = jnp.bfloat16
f32 = jnp.float32


def tree_layout(places):
    after_trunk = places - TRUNK
    after_branch = after_trunk - 4 * SEG
    segments = jnp.where(
        places < TRUNK,
        0,
        jnp.where(after_branch < 0, 1 + after_trunk // SEG, 5 + after_branch // SEG),
    )
    depths = jnp.where(
        places < TRUNK,
        places,
        jnp.where(after_branch < 0, TRUNK + after_trunk % SEG, TRUNK + SEG + after_branch % SEG),
    )
    return (segments.astype(jnp.int32), depths.astype(jnp.int32))


def rotation_tables(depths):
    half_size = HEAD // 2
    frequency = 10000.0 ** (-jnp.arange(half_size, dtype=f32) * 2.0 / HEAD)
    angles = depths.astype(f32)[:, None] * frequency[None, :]
    cosine, sine = jnp.cos(angles), jnp.sin(angles)
    cosines = jnp.concatenate([cosine, cosine], axis=1)
    forward = jnp.concatenate([-sine, sine], axis=1)
    return (cosines, forward), (cosines, -forward)


def lookup(table, indices):
    nodes = jnp.arange(NODES, dtype=jnp.int32)
    return jnp.sum(jnp.where(indices[:, None] == nodes[None, :], table[None, :], 0), axis=1)


def running_count(chosen):
    rows = chosen.shape[-1]
    index = jnp.arange(rows, dtype=jnp.int32)
    upto = (index[:, None] <= index[None, :]).astype(bf16)
    return jnp.dot(chosen.astype(bf16), upto, preferred_element_type=f32).astype(jnp.int32) - 1


def source_plan(routes, expert, capacity):
    chosen = jnp.any(routes == expert, axis=2)
    ranking = running_count(chosen)
    slots = jnp.arange(capacity, dtype=jnp.int32)
    return chosen[:, None, :] & (ranking[:, None, :] == slots[None, :, None])


def token_picks(routes, experts, capacity):
    labels = jnp.arange(experts, dtype=jnp.int32)
    hits = routes.T[:, None, :] == labels[None, :, None]
    ranking = running_count(hits[0] | hits[1])
    slots = jnp.arange(capacity, dtype=jnp.int32)
    picks = hits[:, :, None, :] & (ranking[None, :, None, :] == slots[None, None, :, None])
    return picks.astype(bf16), hits[0].T.astype(f32), hits[1].T.astype(f32)


def fill_slots(picks, pair):
    return jnp.einsum("kecr,krd->ecd", picks, pair, preferred_element_type=f32).astype(bf16)


def read_slots(picks, slots):
    return jnp.einsum("kecr,ecd->krd", picks, slots, preferred_element_type=f32)


def gate_values(hidden, router, first, second):
    logits = jnp.dot(hidden.astype(f32), router, precision=highest)
    picked = jnp.stack([jnp.sum(logits * first, axis=1), jnp.sum(logits * second, axis=1)], axis=1)
    return jax.nn.softmax(picked, axis=1)


def router_grads(hidden, router, gates, first, second, picked_grad):
    logit_pick = gates * (picked_grad - jnp.sum(gates * picked_grad, axis=1, keepdims=True))
    logit_grad = logit_pick[:, 0:1] * first + logit_pick[:, 1:2] * second
    router_grad = jnp.dot(hidden.astype(f32).T, logit_grad, precision=highest)
    hidden_grad = jnp.dot(logit_grad, router.T, precision=highest)
    return (router_grad, hidden_grad)


def rms_parts(values):
    inverse = lax.rsqrt(jnp.mean(values * values, axis=-1, keepdims=True) + epsilon)
    return (values * inverse, inverse)


def norm_back(grad_normed, normed, inverse):
    return inverse * (grad_normed - normed * jnp.mean(grad_normed * normed, axis=-1, keepdims=True))


def pair_grads(gates, branches, upstream):
    gate_grad = jnp.stack([jnp.sum(upstream * branches[k], axis=1) for k in range(2)], axis=1)
    scaled = jnp.stack([gates[:, k : k + 1] * upstream for k in range(2)]).astype(bf16)
    return gate_grad, scaled


def exchange(slots):
    return lax.all_to_all(slots, "expert", split_axis=0, concat_axis=0, tiled=True)


def shift(values, step, size, devices):
    moves = [(i, i // size * size + (i % size + step) % size) for i in range(devices)]
    return lax.ppermute(values, "expert", moves)


def group_gather(rows, size, devices):
    return jnp.concatenate([rows] + [shift(rows, step, size, devices) for step in range(1, size)])


def group_reduce(partial, size, devices):
    parts = partial.reshape(size, -1, partial.shape[1])
    total = parts[0].astype(f32)
    for step in range(1, size):
        total = total + shift(parts[step], -step, size, devices).astype(f32)
    return total.astype(bf16)


def dot_tn(left, right):
    return lax.dot_general(left, right, (((0,), (0,)), ((), ())), preferred_element_type=f32)


def body(
    tokens,
    teacher,
    att_routes,
    ffn_routes,
    parent,
    valid,
    gain_one,
    kv_weight,
    att_router,
    q_weight,
    o_weight,
    gain_two,
    ffn_router,
    gate_weight,
    up_weight,
    down_weight,
):
    row_count = tokens.shape[0]
    devices, replicas = lax.axis_size("expert"), lax.axis_size("dp")
    my_index, my_replica = lax.axis_index("expert"), lax.axis_index("dp")
    core = my_index % 2
    att_copies, ffn_copies = devices // ATT_EXPERTS, devices // FFN_EXPERTS
    att_capacity, ffn_capacity = row_count * 13 // 40, row_count * 13 // 20
    token_count = row_count * devices
    half = HEADS * HEAD // 2
    assert token_count == TREE_LEN * parent.shape[0] and parent.shape[0] == 1
    pair = [(i, i ^ 1) for i in range(devices)]
    own_places = my_index * row_count + jnp.arange(row_count, dtype=jnp.int32)

    x_in = tokens.astype(f32)
    normed_one, inverse_one = rms_parts(x_in)
    hidden = (normed_one * gain_one).astype(bf16)
    weight_rows = kv_weight.shape[0]
    piece = half // replicas
    kv_share = lax.dynamic_slice_in_dim(
        kv_weight.reshape(weight_rows, 4, replicas, piece), my_replica, 1, 2
    )
    kv_share = (
        kv_share.reshape(weight_rows, 2, 2, piece).transpose(0, 2, 1, 3).reshape(weight_rows, 4 * piece)
    )
    route_row = jnp.pad(att_routes.astype(bf16).reshape(1, -1), ((0, row_count - weight_rows - 1), (0, 4 * piece - 2 * row_count)))
    sending = jnp.concatenate([hidden, jnp.concatenate([kv_share, route_row])], axis=1)
    gathered = lax.all_gather(sending, "expert", axis=0)
    kv_half = lax.dynamic_slice_in_dim(gathered[:, :weight_rows], D + core * 2 * piece, 2 * piece, 2)
    kv_blocks = lax.all_gather(kv_half.reshape(D, 2 * piece), "dp", axis=0)
    all_routes = (
        gathered[:, weight_rows, D : D + 2 * row_count].astype(jnp.int32).reshape(devices, row_count, 2)
    )

    tree_places = jnp.arange(token_count, dtype=jnp.int32)
    tree_segments, tree_depths = tree_layout(tree_places)
    key_forward, key_backward = rotation_tables(tree_depths)
    key_info = jnp.pad(jnp.stack([tree_places, tree_segments], axis=1), ((0, 0), (0, 6)))
    experts_here = [my_index // att_copies]
    if att_copies == 1:
        experts_here.append(my_index ^ 1)
    plans = [source_plan(all_routes, expert, att_capacity) for expert in experts_here]
    slot_tables, query_parts = [], []
    for plan in plans:
        places = jnp.sum(
            jnp.where(plan, tree_places.reshape(devices, 1, row_count), 0), axis=2
        ).reshape(-1)
        segments, depths = tree_layout(places)
        parents = lookup(parent[0], segments)
        grands = lookup(parent[0], parents)
        query_parts.append(jnp.stack([places, segments, parents, grands]).reshape(4, GROUPS, -1))
        slot_tables.append(rotation_tables(depths))
    query_info = jnp.concatenate(query_parts, axis=2).transpose(1, 0, 2)
    own_plan = plans[0].astype(bf16)
    query_inputs = jnp.einsum(
        "scr,srd->scd", own_plan, gathered[:, :, :D], preferred_element_type=f32
    ).astype(bf16).reshape(-1, D)

    queries = project_queries(query_inputs, q_weight, slot_tables[0][0])
    keys_all, values_all = project_keys_values(gathered, kv_blocks, key_forward)

    def far_half(values):
        return lax.ppermute(
            lax.dynamic_slice_in_dim(values, (1 - core) * half, half, 1), "expert", pair
        )

    def join_halves(mine, sibling):
        other = lax.ppermute(sibling, "expert", pair)
        return jnp.where(
            core == 0,
            jnp.concatenate([mine, other], axis=1),
            jnp.concatenate([other, mine], axis=1),
        )

    heads = half // HEAD
    query_sets = [queries]
    starts = jnp.zeros((2,), jnp.int32)
    if att_copies == 1:
        query_sets.append(far_half(queries))
        starts = jnp.stack([core * heads, 0]).astype(jnp.int32)
    *att_outs, lse = attention_forward(
        query_sets, starts // 2, keys_all, values_all, key_info, query_info, heads
    )
    att_rows = join_halves(*att_outs) if att_copies == 1 else att_outs[0]
    att_partial = lax.dot_general(
        att_rows, o_weight, (((1,), (1,)), ((), ())), preferred_element_type=f32
    ).astype(bf16)
    att_back = exchange(att_partial.reshape(devices, att_capacity, D))
    att_picks, att_first, att_second = token_picks(att_routes, ATT_EXPERTS, att_capacity)
    att_gates = gate_values(hidden, att_router, att_first, att_second)
    if att_copies > 1:
        att_back = (
            att_back.astype(f32).reshape(ATT_EXPERTS, att_copies, att_capacity, D).sum(axis=1).astype(bf16)
        )
    att_branches = read_slots(att_picks, att_back)
    x_mid = x_in + att_gates[:, 0:1] * att_branches[0] + att_gates[:, 1:2] * att_branches[1]

    normed_two, inverse_two = rms_parts(x_mid)
    hidden_two = (normed_two * gain_two).astype(bf16)
    ffn_picks, ffn_first, ffn_second = token_picks(ffn_routes, FFN_EXPERTS, ffn_capacity)
    ffn_gates = gate_values(hidden_two, ffn_router, ffn_first, ffn_second)

    def to_experts(slots):
        rows = exchange(slots.reshape(devices, ffn_capacity // ffn_copies, D))
        return group_gather(rows.reshape(-1, D), ffn_copies, devices)

    def to_tokens(partial):
        rows = group_reduce(partial.astype(bf16), ffn_copies, devices)
        back = exchange(rows.reshape(devices, ffn_capacity // ffn_copies, D))
        return read_slots(ffn_picks, back.reshape(FFN_EXPERTS, ffn_capacity, D))

    ffn_inputs = to_experts(
        jnp.einsum(
            "ecr,rd->ecd", ffn_picks[0] + ffn_picks[1], hidden_two, preferred_element_type=f32
        ).astype(bf16)
    )
    gate_pre = jnp.dot(ffn_inputs, gate_weight, preferred_element_type=f32)
    up_pre = jnp.dot(ffn_inputs, up_weight, preferred_element_type=f32)
    sigmoid_gate = jax.nn.sigmoid(gate_pre)
    silu_gate = gate_pre * sigmoid_gate
    activated = (silu_gate * up_pre).astype(bf16)
    ffn_branches = to_tokens(
        lax.dot_general(activated, down_weight, (((1,), (1,)), ((), ())), preferred_element_type=f32)
    )
    result = x_mid + ffn_gates[:, 0:1] * ffn_branches[0] + ffn_gates[:, 1:2] * ffn_branches[1]

    tree_global = my_replica * parent.shape[0] + own_places // TREE_LEN
    tree_labels = jnp.arange(valid.shape[0], dtype=jnp.int32)
    limits = jnp.sum(
        jnp.where(tree_global[:, None] == tree_labels[None, :], valid[None, :], 0), axis=1
    )
    counted = own_places % TREE_LEN < limits
    loss_factor = valid.shape[0] * TREE_LEN / jnp.sum(valid).astype(f32)
    grad_result = jnp.where(counted[:, None], (result - teacher.astype(f32)) * loss_factor, 0.0)

    ffn_gate_grad, ffn_scaled = pair_grads(ffn_gates, ffn_branches, grad_result)
    grad_ffn_out = to_experts(fill_slots(ffn_picks, ffn_scaled))
    grad_down = dot_tn(grad_ffn_out, activated).astype(bf16)
    grad_ffn_out, grad_down = lax.optimization_barrier((grad_ffn_out, grad_down))
    summed_down = lax.psum_scatter(grad_down, "dp", scatter_dimension=0, tiled=True)
    grad_activated = jnp.dot(grad_ffn_out, down_weight, preferred_element_type=f32)
    grad_gate_pre = (
        grad_activated * up_pre * sigmoid_gate * (1.0 + gate_pre * (1.0 - sigmoid_gate))
    ).astype(bf16)
    grad_up_pre = (grad_activated * silu_gate).astype(bf16)
    grad_ffn_in = lax.dot_general(
        grad_gate_pre, gate_weight, (((1,), (1,)), ((), ())), preferred_element_type=f32
    ) + lax.dot_general(
        grad_up_pre, up_weight, (((1,), (1,)), ((), ())), preferred_element_type=f32
    )
    grad_gate = dot_tn(ffn_inputs, grad_gate_pre).astype(bf16)
    grad_up = dot_tn(ffn_inputs, grad_up_pre).astype(bf16)
    summed_gate = lax.psum_scatter(grad_gate, "dp", scatter_dimension=0, tiled=True)
    summed_up = lax.psum_scatter(grad_up, "dp", scatter_dimension=0, tiled=True)
    ffn_grad_pair = to_tokens(grad_ffn_in)
    ffn_grad_pair, grad_gate, grad_up = lax.optimization_barrier((ffn_grad_pair, grad_gate, grad_up))
    grad_ffn_router, hidden_two_extra = router_grads(
        hidden_two, ffn_router, ffn_gates, ffn_first, ffn_second, ffn_gate_grad
    )
    grad_hidden_two = ffn_grad_pair[0] + ffn_grad_pair[1] + hidden_two_extra
    grad_gain_two = jnp.sum(grad_hidden_two * normed_two, axis=0)
    grad_mid = grad_result + norm_back(grad_hidden_two * gain_two, normed_two, inverse_two)

    att_gate_grad, att_scaled = pair_grads(att_gates, att_branches, grad_mid)
    att_slots = fill_slots(att_picks, att_scaled)
    att_slots, summed_down = lax.optimization_barrier((att_slots, summed_down))
    if att_copies > 1:
        att_slots = jnp.repeat(att_slots, att_copies, axis=0)
    grad_att_out = exchange(att_slots).reshape(-1, D)
    grad_o = dot_tn(grad_att_out, att_rows).astype(bf16)
    grad_att_out, grad_o = lax.optimization_barrier((grad_att_out, grad_o))
    summed_o = lax.psum_scatter(grad_o, "dp", scatter_dimension=0, tiled=True)
    grad_heads = jnp.dot(grad_att_out, o_weight, preferred_element_type=f32).astype(bf16)
    grad_sets = [grad_heads]
    if att_copies == 1:
        grad_sets.append(far_half(grad_heads))
    grad_sets[-1], summed_gate = lax.optimization_barrier((grad_sets[-1], summed_gate))
    *grad_queries, grad_keys, grad_values = attention_backward(
        query_sets,
        starts,
        grad_sets,
        att_outs,
        keys_all,
        values_all,
        lse,
        key_info,
        query_info,
        key_backward,
        [tables[1] for tables in slot_tables],
        heads,
    )
    grad_query_pre = join_halves(*grad_queries) if att_copies == 1 else grad_queries[0]
    grad_query_in = lax.dot_general(
        grad_query_pre, q_weight, (((1,), (1,)), ((), ())), preferred_element_type=f32
    ).astype(bf16)
    grad_q = dot_tn(query_inputs, grad_query_pre).astype(bf16)
    grad_query_in, summed_up = lax.optimization_barrier((grad_query_in, summed_up))
    hidden_rows = gathered[:, :, :D].reshape(token_count, D)
    grad_kv = jnp.concatenate(
        [dot_tn(hidden_rows, grad_keys).astype(bf16), dot_tn(hidden_rows, grad_values).astype(bf16)], axis=1
    )
    summed_kv = lax.psum_scatter(grad_kv, "dp", scatter_dimension=0, tiled=True)
    summed_q = lax.psum_scatter(grad_q, "dp", scatter_dimension=0, tiled=True)

    merged = merge_hidden_grads(
        own_plan.transpose(0, 2, 1),
        grad_query_in.reshape(devices, att_capacity, D),
        grad_keys,
        grad_values,
        kv_blocks,
    ).reshape(devices // 2, 2, row_count, D)
    kept = lax.dynamic_index_in_dim(merged, core, 1, keepdims=False)
    passed = lax.ppermute(
        lax.dynamic_index_in_dim(merged, 1 - core, 1, keepdims=False), "expert", pair
    )
    chip_sum = (kept.astype(f32) + passed.astype(f32)).astype(bf16)
    same_core = [[2 * i + c for i in range(devices // 2)] for c in range(2)]
    arrived = lax.all_to_all(
        chip_sum, "expert", split_axis=0, concat_axis=0, axis_index_groups=same_core, tiled=True
    )
    arrived, summed_kv = lax.optimization_barrier((arrived, summed_kv))
    grad_att_router, hidden_one_extra = router_grads(
        hidden, att_router, att_gates, att_first, att_second, att_gate_grad
    )
    grad_hidden_one = jnp.sum(arrived.astype(f32), axis=0) + hidden_one_extra
    grad_gain_one = jnp.sum(grad_hidden_one * normed_one, axis=0)
    grad_input = grad_mid + norm_back(grad_hidden_one * gain_one, normed_one, inverse_one)

    everyone = devices * replicas
    smalls = [grad_gain_one, grad_gain_two, grad_att_router, grad_ffn_router]
    packed = jnp.concatenate([small.reshape(everyone, -1) for small in smalls], axis=1)
    own_smalls = jnp.sum(
        lax.all_to_all(packed, ("dp", "expert"), split_axis=0, concat_axis=0, tiled=True), axis=0
    )
    share = D // everyone
    shared_gain_one = own_smalls[:share]
    shared_gain_two = own_smalls[share : 2 * share]
    shared_att_router = own_smalls[2 * share : (2 + ATT_EXPERTS) * share].reshape(share, ATT_EXPERTS)
    shared_ffn_router = own_smalls[(2 + ATT_EXPERTS) * share :].reshape(share, FFN_EXPERTS)

    kv_rows = exchange(summed_kv.reshape(devices, -1, 2 * half))
    kv_sum = jnp.sum(kv_rows.astype(f32).reshape(devices // 2, 2, -1, 2, half), axis=0)
    shared_kv = kv_sum.transpose(1, 2, 0, 3).reshape(-1, 4 * half)

    return (
        result.astype(bf16),
        grad_input.astype(bf16),
        shared_gain_one,
        shared_kv,
        shared_att_router,
        summed_q.astype(f32),
        summed_o.astype(f32),
        shared_gain_two,
        shared_ffn_router,
        summed_gate.astype(f32),
        summed_up.astype(f32),
        summed_down.astype(f32),
    )


def solution(mesh):
    in_specs = (
        P(("dp", "expert"), None),
        P(("dp", "expert"), None),
        P(("dp", "expert"), None),
        P(("dp", "expert"), None),
        P("dp", None),
        P(),
        P(),
        P("expert", None),
        P(),
        P(None, "expert"),
        P(None, "expert"),
        P(),
        P(),
        P(None, "expert"),
        P(None, "expert"),
        P(None, "expert"),
    )
    out_specs = (
        P(("dp", "expert"), None),
        P(("dp", "expert"), None),
        P(("dp", "expert")),
        P(("dp", "expert"), None),
        P(("dp", "expert"), None),
        P("dp", "expert"),
        P("dp", "expert"),
        P(("dp", "expert")),
        P(("dp", "expert"), None),
        P("dp", "expert"),
        P("dp", "expert"),
        P("dp", "expert"),
    )
    return jax.shard_map(body, mesh=mesh, in_specs=in_specs, out_specs=out_specs, check_vma=False)
```

```python
import functools
import jax
import jax.numpy as jnp
from jax import lax
from jax.experimental import pallas as pl
from jax.experimental.pallas import tpu as pltpu
from jax.sharding import PartitionSpec as P

HEAD = 128
GROUPS = 4
LOG2E = 1.4426950408889634
VMEM_BYTES = 60 * 1024 * 1024


def dot_nt(left, right):
    return lax.dot_general(left, right, (((1,), (1,)), ((), ())), preferred_element_type=jnp.float32)


def dot_nn(left, right):
    return jnp.dot(left, right, preferred_element_type=jnp.float32)


def spin(values, cosine, sine):
    return values * cosine + pltpu.roll(values, HEAD // 2, 1) * sine


def fill_bias(bias_ref, key_ref, query_ref, keys):
    for group in range(GROUPS):
        place = query_ref[group, 0:1, :]
        own, parent, grand = (query_ref[group, 1 + n : 2 + n, :] for n in range(3))

        def one(block, carry, group=group, place=place, own=own, parent=parent, grand=grand):
            at = pl.multiple_of(block * keys, 16)
            key_place = key_ref[pl.ds(at, keys), 0:1]
            key_segment = key_ref[pl.ds(at, keys), 1:2]
            related = (key_segment == own) | (key_segment == parent) | (key_segment == grand)
            allowed = related & (key_place <= place)
            bias_ref[group * (group + 1) // 2 + block] = jnp.where(allowed, 0.0, -1e30)
            return carry

        lax.fori_loop(0, group + 1, one, 0)


def group_rows(refs, group, rows, lanes):
    parts = [ref[pl.ds(group * rows, rows), lanes] for ref in refs]
    return parts[0] if len(parts) == 1 else jnp.concatenate(parts, axis=0)


def attention_forward_body(sets, step_heads, rows, keys, scale, first_ref, *refs):
    query_refs = refs[:sets]
    key_ref, value_ref, key_info, query_info = refs[sets : sets + 4]
    out_refs = refs[sets + 4 : 2 * sets + 4]
    lse_ref, bias_ref, flipped_ref = refs[2 * sets + 4 :]
    wide = sets * rows

    @pl.when(pl.program_id(0) == 0)
    def _():
        fill_bias(bias_ref, key_info, query_info, keys)

    for head in range(step_heads):
        lanes = pl.ds(head * HEAD, HEAD)
        for block in range(GROUPS):
            values = value_ref[pl.ds(block * keys, keys), lanes].astype(jnp.float32)
            flipped_ref[head, block] = values.T.astype(jnp.bfloat16)
    for group in range(GROUPS):
        queries = [
            group_rows(query_refs, group, rows, pl.ds(head * HEAD, HEAD)) for head in range(step_heads)
        ]

        def one(block, carry, group=group, queries=queries):
            at = pl.multiple_of(block * keys, 16)
            bias = bias_ref[group * (group + 1) // 2 + block]
            result = []
            for head in range(step_heads):
                top, total, mixed = carry[3 * head : 3 * head + 3]
                scores = dot_nt(key_ref[pl.ds(at, keys), pl.ds(head * HEAD, HEAD)], queries[head])
                scores = scores * scale + bias
                new_top = jnp.maximum(top, jnp.max(scores, axis=0, keepdims=True))
                fade = jnp.exp2(top - new_top)
                parts = jnp.exp2(scores - new_top)
                total = total * fade + jnp.sum(parts, axis=0, keepdims=True)
                mixed = mixed * fade + dot_nn(flipped_ref[head, block], parts.astype(jnp.bfloat16))
                result += [new_top, total, mixed]
            return tuple(result)

        start = (
            jnp.full((1, wide), -1e30, jnp.float32),
            jnp.zeros((1, wide), jnp.float32),
            jnp.zeros((HEAD, wide), jnp.float32),
        ) * step_heads
        final = lax.fori_loop(0, group + 1, one, start)
        for head in range(step_heads):
            top, total, mixed = final[3 * head : 3 * head + 3]
            lse_ref[head, group : group + 1, :] = top + jnp.log2(total)
            rows_out = (mixed / total).T.astype(jnp.bfloat16)
            for n, ref in enumerate(out_refs):
                ref[pl.ds(group * rows, rows), pl.ds(head * HEAD, HEAD)] = rows_out[
                    n * rows : (n + 1) * rows
                ]


def attention_backward_body(sets, step_heads, rows, keys, scale, first_ref, *refs):
    query_refs, grad_refs, out_refs = (refs[n * sets : (n + 1) * sets] for n in range(3))
    key_ref, value_ref, lse_ref, key_info, query_info = refs[3 * sets : 3 * sets + 5]
    key_cos, key_sin = refs[3 * sets + 5 : 3 * sets + 7]
    table_refs = refs[3 * sets + 7 : 5 * sets + 7]
    rest = refs[5 * sets + 7 :]
    dq_refs = rest[:sets]
    dk_ref, dv_ref, bias_ref, flipped_ref, dk_acc, dv_acc = rest[sets:]
    softmax_scale = scale / LOG2E

    @pl.when(pl.program_id(0) == 0)
    def _():
        fill_bias(bias_ref, key_info, query_info, keys)

    dk_acc[...] = jnp.zeros_like(dk_acc)
    dv_acc[...] = jnp.zeros_like(dv_acc)
    for head in range(step_heads):
        lanes = pl.ds(head * HEAD, HEAD)
        for block in range(GROUPS):
            values = key_ref[pl.ds(block * keys, keys), lanes].astype(jnp.float32)
            flipped_ref[head, block] = values.T.astype(jnp.bfloat16)
    for group in range(GROUPS):
        queries, grads, centres, tops = [], [], [], []
        for head in range(step_heads):
            lanes = pl.ds(head * HEAD, HEAD)
            queries.append(group_rows(query_refs, group, rows, lanes))
            grad = group_rows(grad_refs, group, rows, lanes)
            out = group_rows(out_refs, group, rows, lanes)
            product = grad.astype(jnp.float32) * out.astype(jnp.float32)
            centres.append(jnp.sum(product.T, axis=0, keepdims=True))
            grads.append(grad)
            tops.append(lse_ref[head, group : group + 1, :])

        def one(block, carry, group=group, queries=queries, grads=grads, centres=centres, tops=tops):
            at = pl.multiple_of(block * keys, 16)
            bias = bias_ref[group * (group + 1) // 2 + block]
            result = []
            for head in range(step_heads):
                lanes = pl.ds(head * HEAD, HEAD)
                key_rows = key_ref[pl.ds(at, keys), lanes]
                scores = dot_nt(key_rows, queries[head])
                probs = jnp.exp2(scores * scale + (bias - tops[head]))
                grad_probs = dot_nt(value_ref[pl.ds(at, keys), lanes], grads[head])
                grad_scores = (probs * (grad_probs - centres[head])).astype(jnp.bfloat16)
                dv_acc[pl.ds(at, keys), lanes] += dot_nn(probs.astype(jnp.bfloat16), grads[head])
                dk_acc[pl.ds(at, keys), lanes] += dot_nn(grad_scores, queries[head])
                result.append(carry[head] + dot_nn(flipped_ref[head, block], grad_scores))
            return tuple(result)

        start = (jnp.zeros((HEAD, sets * rows), jnp.float32),) * step_heads
        final = lax.fori_loop(0, group + 1, one, start)
        for head in range(step_heads):
            dq = final[head].T * softmax_scale
            for n, ref in enumerate(dq_refs):
                span = pl.ds(group * rows, rows)
                turned = spin(
                    dq[n * rows : (n + 1) * rows], table_refs[2 * n][span, :], table_refs[2 * n + 1][span, :]
                )
                ref[span, pl.ds(head * HEAD, HEAD)] = turned.astype(jnp.bfloat16)
    for head in range(step_heads):
        lanes = pl.ds(head * HEAD, HEAD)
        for block in range(GROUPS):
            span = pl.ds(block * keys, keys)
            turned = spin(dk_acc[span, lanes] * softmax_scale, key_cos[span, :], key_sin[span, :])
            dk_ref[span, lanes] = turned.astype(jnp.bfloat16)
            dv_ref[span, lanes] = dv_acc[span, lanes].astype(jnp.bfloat16)


def whole_block(shape):
    return pl.BlockSpec(shape, lambda h, first: (0,) * len(shape))


def attention_forward(queries, starts, keys_all, values_all, key_info, query_info, heads):
    sets, total_rows, tokens = len(queries), queries[0].shape[0], keys_all.shape[0]
    rows, keys = total_rows // GROUPS, tokens // GROUPS
    step_heads = 2
    wide = step_heads * HEAD
    scale = HEAD ** (-0.5) * LOG2E
    query_specs = [
        pl.BlockSpec((total_rows, wide), lambda h, first, n=n: (0, first[n] + h)) for n in range(sets)
    ]
    plain = pl.BlockSpec((total_rows, wide), lambda h, first: (0, h))
    side = pl.BlockSpec((tokens, wide), lambda h, first: (0, h))
    return pl.pallas_call(
        functools.partial(attention_forward_body, sets, step_heads, rows, keys, scale),
        grid_spec=pltpu.PrefetchScalarGridSpec(
            num_scalar_prefetch=1,
            grid=(heads // step_heads,),
            in_specs=query_specs
            + [side, side, whole_block(key_info.shape), whole_block(query_info.shape)],
            out_specs=[plain] * sets
            + [pl.BlockSpec((step_heads, GROUPS, sets * rows), lambda h, first: (h, 0, 0))],
            scratch_shapes=[
                pltpu.VMEM((GROUPS * (GROUPS + 1) // 2, keys, sets * rows), jnp.float32),
                pltpu.VMEM((step_heads, GROUPS, HEAD, keys), jnp.bfloat16),
            ],
        ),
        out_shape=[jax.ShapeDtypeStruct((total_rows, heads * HEAD), jnp.bfloat16)] * sets
        + [jax.ShapeDtypeStruct((heads, GROUPS, sets * rows), jnp.float32)],
        compiler_params=pltpu.CompilerParams(vmem_limit_bytes=VMEM_BYTES),
        name="attention_forward",
    )(starts, *queries, keys_all, values_all, key_info, query_info)


def attention_backward(
    queries, starts, grads, outs, keys_all, values_all, lse, key_info, query_info, key_tables, row_tables, heads
):
    sets, total_rows, tokens = len(queries), queries[0].shape[0], keys_all.shape[0]
    rows, keys = total_rows // GROUPS, tokens // GROUPS
    step_heads = 1
    wide = step_heads * HEAD
    scale = HEAD ** (-0.5) * LOG2E
    shifted = [
        pl.BlockSpec((total_rows, wide), lambda h, first, n=n: (0, first[n] + h)) for n in range(sets)
    ]
    plain = pl.BlockSpec((total_rows, wide), lambda h, first: (0, h))
    side = pl.BlockSpec((tokens, wide), lambda h, first: (0, h))
    return pl.pallas_call(
        functools.partial(attention_backward_body, sets, step_heads, rows, keys, scale),
        grid_spec=pltpu.PrefetchScalarGridSpec(
            num_scalar_prefetch=1,
            grid=(heads // step_heads,),
            in_specs=shifted
            + shifted
            + [plain] * sets
            + [
                side,
                side,
                pl.BlockSpec((step_heads, GROUPS, sets * rows), lambda h, first: (h, 0, 0)),
                whole_block(key_info.shape),
                whole_block(query_info.shape),
                whole_block((tokens, HEAD)),
                whole_block((tokens, HEAD)),
            ]
            + [whole_block((total_rows, HEAD))] * (2 * sets),
            out_specs=[plain] * sets + [side, side],
            scratch_shapes=[
                pltpu.VMEM((GROUPS * (GROUPS + 1) // 2, keys, sets * rows), jnp.float32),
                pltpu.VMEM((step_heads, GROUPS, HEAD, keys), jnp.bfloat16),
                pltpu.VMEM((tokens, wide), jnp.float32),
                pltpu.VMEM((tokens, wide), jnp.float32),
            ],
        ),
        out_shape=[jax.ShapeDtypeStruct((total_rows, heads * HEAD), jnp.bfloat16)] * sets
        + [jax.ShapeDtypeStruct((tokens, heads * HEAD), jnp.bfloat16)] * 2,
        compiler_params=pltpu.CompilerParams(vmem_limit_bytes=VMEM_BYTES),
        name="attention_backward",
    )(
        starts,
        *queries,
        *grads,
        *outs,
        keys_all,
        values_all,
        lse,
        key_info,
        query_info,
        *key_tables,
        *[table for pair in row_tables for table in pair],
    )


def project_body(plan_ref, hidden_ref, weight_ref, cos_ref, sin_ref, out_ref, x_ref):
    sources, capacity = plan_ref.shape[0], plan_ref.shape[1]
    bundle = max(1, sources * capacity // GROUPS // capacity)
    tile = bundle * capacity

    @pl.when(pl.program_id(0) == 0)
    def _():
        for group in range(sources // bundle):
            parts = [
                dot_nn(plan_ref[group * bundle + n], hidden_ref[group * bundle + n]) for n in range(bundle)
            ]
            x_ref[pl.ds(group * tile, tile), :] = jnp.concatenate(parts, axis=0).astype(jnp.bfloat16)

    for at in range(0, x_ref.shape[0], tile):
        span = pl.ds(at, tile)
        product = dot_nn(x_ref[span, :], weight_ref[...])
        for lane in range(0, out_ref.shape[1], HEAD):
            turned = spin(product[:, lane : lane + HEAD], cos_ref[span, :], sin_ref[span, :])
            out_ref[span, lane : lane + HEAD] = turned.astype(jnp.bfloat16)


def project_queries(plan, hidden, weight, tables):
    sources, capacity, row_count = plan.shape
    depth, columns = weight.shape
    rows = sources * capacity
    block = 512
    return pl.pallas_call(
        project_body,
        grid=(columns // block,),
        in_specs=[
            pl.BlockSpec((sources, capacity, row_count), lambda j: (0, 0, 0)),
            pl.BlockSpec((sources, row_count, depth), lambda j: (0, 0, 0)),
            pl.BlockSpec((depth, block), lambda j: (0, j)),
            pl.BlockSpec((rows, HEAD), lambda j: (0, 0)),
            pl.BlockSpec((rows, HEAD), lambda j: (0, 0)),
        ],
        out_specs=[
            pl.BlockSpec((rows, block), lambda j: (0, j)),
            pl.BlockSpec((rows, depth), lambda j: (0, 0)),
        ],
        out_shape=[
            jax.ShapeDtypeStruct((rows, columns), jnp.bfloat16),
            jax.ShapeDtypeStruct((rows, depth), jnp.bfloat16),
        ],
        compiler_params=pltpu.CompilerParams(vmem_limit_bytes=VMEM_BYTES),
        name="project_queries",
    )(plan, hidden, weight, *tables)


def keys_values_body(half, order_ref, x_ref, weight_ref, cos_ref, sin_ref, key_ref, value_ref):
    rows = x_ref.shape[1]
    for source in range(x_ref.shape[0]):
        span = pl.ds(source * rows, rows)
        product = dot_nn(x_ref[source], weight_ref[0])
        for lane in range(0, half, HEAD):
            turned = spin(product[:, lane : lane + HEAD], cos_ref[span, :], sin_ref[span, :])
            key_ref[span, lane : lane + HEAD] = turned.astype(jnp.bfloat16)
        value_ref[span, :] = product[:, half:].astype(jnp.bfloat16)


def project_keys_values(hidden, weights, tables, order):
    sources, rows, unused = hidden.shape
    parts, depth, columns = weights.shape
    half, tokens = columns // 2, sources * rows
    return pl.pallas_call(
        functools.partial(keys_values_body, half),
        grid_spec=pltpu.PrefetchScalarGridSpec(
            num_scalar_prefetch=1,
            grid=(parts,),
            in_specs=[
                pl.BlockSpec((sources, rows, depth), lambda j, order: (0, 0, 0)),
                pl.BlockSpec((1, depth, columns), lambda j, order: (j, 0, 0)),
                pl.BlockSpec((tokens, HEAD), lambda j, order: (0, 0)),
                pl.BlockSpec((tokens, HEAD), lambda j, order: (0, 0)),
            ],
            out_specs=[pl.BlockSpec((tokens, half), lambda j, order: (0, order[j]))] * 2,
        ),
        out_shape=[jax.ShapeDtypeStruct((tokens, parts * half), jnp.bfloat16)] * 2,
        compiler_params=pltpu.CompilerParams(vmem_limit_bytes=VMEM_BYTES),
        name="project_keys_values",
    )(order, hidden, weights, *tables)


def merge_body(tile, order_ref, plan_ref, slots_ref, dk_ref, dv_ref, weight_ref, out_ref, acc_ref):
    part = pl.program_id(1)
    sources, rows = plan_ref.shape[0], plan_ref.shape[1]
    ck = dk_ref.shape[1]

    @pl.when(part == 0)
    def _():
        for source in range(sources):
            acc_ref[pl.ds(source * rows, rows), :] = dot_nn(plan_ref[source], slots_ref[source])

    last = part == pl.num_programs(1) - 1
    for at in range(0, acc_ref.shape[0], tile):
        span = pl.ds(at, tile)
        acc_ref[span, :] += dot_nt(dk_ref[span, :], weight_ref[0, :, :ck]) + dot_nt(
            dv_ref[span, :], weight_ref[0, :, ck:]
        )

    @pl.when(last)
    def _():
        out_ref[...] = acc_ref[...].astype(jnp.bfloat16)


def merge_hidden_grads(plan, slots, grad_keys, grad_values, weights, order):
    sources, rows, capacity = plan.shape
    parts, depth, columns = weights.shape
    ck, tokens = columns // 2, sources * rows
    wide = depth // 2
    return pl.pallas_call(
        functools.partial(merge_body, tokens // GROUPS),
        grid_spec=pltpu.PrefetchScalarGridSpec(
            num_scalar_prefetch=1,
            grid=(2, parts),
            in_specs=[
                pl.BlockSpec((sources, rows, capacity), lambda i, j, order: (0, 0, 0)),
                pl.BlockSpec((sources, capacity, wide), lambda i, j, order: (0, 0, i)),
                pl.BlockSpec((tokens, ck), lambda i, j, order: (0, order[j])),
                pl.BlockSpec((tokens, ck), lambda i, j, order: (0, order[j])),
                pl.BlockSpec((1, wide, columns), lambda i, j, order: (j, i, 0)),
            ],
            out_specs=pl.BlockSpec((tokens, wide), lambda i, j, order: (0, i)),
            scratch_shapes=[pltpu.VMEM((tokens, wide), jnp.float32)],
        ),
        out_shape=jax.ShapeDtypeStruct((tokens, depth), jnp.bfloat16),
        compiler_params=pltpu.CompilerParams(vmem_limit_bytes=VMEM_BYTES),
        name="merge_hidden_grads",
    )(order, plan, slots, grad_keys, grad_values, weights)


def mesh_device(index):
    return {"expert": index}


def chip_order(chip, step):
    flip = chip // 2
    near = chip + flip * (3 - 2 * chip)
    place = step + near * (1 - 2 * step) if step < 2 else step
    return place + flip * (3 - 2 * place)


def enter(devices, me):
    barrier = pltpu.get_barrier_semaphore()
    for step in range(1, devices):
        pl.semaphore_signal(
            barrier,
            inc=1,
            device_id=mesh_device(lax.rem(me + step, devices)),
            device_id_type=pl.DeviceIdType.MESH,
        )
    pl.semaphore_wait(barrier, devices - 1)


def remote(source, target, send, recv, device):
    return pltpu.make_async_remote_copy(
        src_ref=source,
        dst_ref=target,
        send_sem=send,
        recv_sem=recv,
        device_id=mesh_device(device),
        device_id_type=pl.DeviceIdType.MESH,
    )


class Dispatch:
    def __init__(self, me, slots, landing, local_sem, send, recv, pass_send, pass_recv):
        self.me, self.chip, self.core = me, me // 2, lax.rem(me, 2)
        self.slots, self.landing = slots, landing
        self.local_sem, self.send, self.recv = local_sem, send, recv
        self.pass_send, self.pass_recv = pass_send, pass_recv
        self.rows, self.half = slots.shape[1], slots.shape[2] // 2

    def columns(self, core):
        return pl.ds(pl.multiple_of(core * self.half, 128), self.half)

    def place(self, source, core):
        rows = pl.ds(pl.multiple_of(lax.rem(source, 2) * self.rows, 16), self.rows)
        return self.landing.at[source // 2, rows, self.columns(core)]

    def direct(self, step):
        target = lax.rem(self.me + step, 8)
        core = lax.rem(target, 2)
        return remote(
            self.slots.at[target // 2, :, self.columns(core)],
            self.place(self.me, core),
            self.send.at[step],
            self.recv.at[step],
            target,
        )

    def local(self):
        return pltpu.make_async_copy(
            self.slots.at[self.chip, :, self.columns(self.core)],
            self.place(self.me, self.core),
            self.local_sem,
        )

    def start(self):
        self.local().start()
        for step in range(1, 8):
            self.direct(step).start()

    def pass_on(self, source):
        place = self.place(source, self.core)
        return remote(
            place, place, self.pass_send.at[source], self.pass_recv.at[source], self.me + 1 - 2 * self.core
        )

    def arrive(self, step):
        chip = chip_order(self.chip, step)
        for source in (2 * chip, 2 * chip + 1):
            offset = lax.rem(self.me - source + 8, 8)

            @pl.when(offset == 0)
            def _():
                self.local().wait()

            @pl.when(offset != 0)
            def _(source=source, offset=offset):
                place = self.place(source, self.core)
                remote(place, place, self.send.at[offset], self.recv.at[offset], self.me).wait_recv()

            self.pass_on(source).start()

    def ready(self, step):
        chip = chip_order(self.chip, step)
        for source in (2 * chip, 2 * chip + 1):
            place = self.place(source, 1 - self.core)
            remote(
                place, place, self.pass_send.at[source], self.pass_recv.at[source], self.me
            ).wait_recv()
        return chip

    def finish(self):
        for step in range(1, 8):
            self.direct(step).wait_send()
        for source in range(8):
            self.pass_on(source).wait_send()


class Collect:
    def __init__(
        self, me, far_first, kept, passing, passed, total, back, local_sem, pass_send, pass_recv, send, recv
    ):
        self.me, self.chip, self.core, self.far_first = me, me // 2, lax.rem(me, 2), far_first
        self.kept, self.passing, self.passed, self.total, self.back = kept, passing, passed, total, back
        self.local_sem, self.pass_send, self.pass_recv = local_sem, pass_send, pass_recv
        self.send, self.recv = send, recv
        self.rows, self.half = back.shape[1], back.shape[2] // 2

    def swap(self, step):
        return remote(
            self.passing.at[step],
            self.passed.at[step],
            self.pass_send.at[step],
            self.pass_recv.at[step],
            self.me + 1 - 2 * self.core,
        )

    def place(self, chip, core):
        return self.back.at[chip, :, pl.ds(pl.multiple_of(core * self.half, 128), self.half)]

    def local(self, step, source_core):
        return pltpu.make_async_copy(
            self.total.at[step, pl.ds(pl.multiple_of(source_core * self.rows, 16), self.rows), :],
            self.place(self.chip, self.core),
            self.local_sem,
        )

    def outgoing(self, step, source):
        rows = pl.ds(pl.multiple_of(lax.rem(source, 2) * self.rows, 16), self.rows)
        offset = lax.rem(source - self.me + 8, 8)
        return remote(
            self.total.at[step, rows, :],
            self.place(self.chip, self.core),
            self.send.at[offset],
            self.recv.at[offset],
            source,
        )

    def block(self, step):
        return chip_order(self.chip, 3 - step if self.far_first else step)

    def each(self, step, own, other):
        chip = self.block(step)
        for source in (2 * chip, 2 * chip + 1):
            if step != (3 if self.far_first else 0):
                other(source)
                continue

            @pl.when(source == self.me)
            def _():
                own()

            @pl.when(source != self.me)
            def _(source=source):
                other(source)

    def settle(self, step):
        self.swap(step).wait_recv()
        tile = 2 * self.rows // 4
        for at in range(0, 2 * self.rows, tile):
            span = pl.ds(at, tile)
            summed = self.kept[step % 2, span, :] + self.passed[step, span, :].astype(jnp.float32)
            self.total[step, span, :] = summed.astype(jnp.bfloat16)
        self.each(
            step,
            lambda: self.local(step, self.core).start(),
            lambda source: self.outgoing(step, source).start(),
        )

    def finish(self):
        for step in range(4):
            self.swap(step).wait_send()
            self.each(
                step,
                lambda step=step: self.local(step, self.core).wait(),
                lambda source, step=step: self.outgoing(step, source).wait_send(),
            )
        for offset in range(1, 8):
            source = lax.rem(self.me + 8 - offset, 8)
            place = self.place(source // 2, lax.rem(source, 2))
            remote(place, place, self.send.at[offset], self.recv.at[offset], self.me).wait_recv()


def ffn_forward_body(
    chunk,
    slots,
    gate_hbm,
    up_hbm,
    down_hbm,
    rows_out,
    gate_out,
    up_out,
    act_out,
    back,
    gate,
    up,
    down,
    landing,
    pre_stage,
    act,
    kept,
    passing,
    passed,
    total,
    weight_sem,
    stage_sem,
    act_sem,
    rows_sem,
    local_sem,
    send,
    recv,
    pass_send,
    pass_recv,
    swap_send,
    swap_recv,
    out_send,
    out_recv,
):
    me = lax.axis_index("expert")
    enter(8, me)
    loads = [
        pltpu.make_async_copy(source, target, weight_sem.at[n])
        for n, (source, target) in enumerate(((gate_hbm, gate), (up_hbm, up), (down_hbm, down)))
    ]
    dispatch = Dispatch(me, slots, landing, local_sem.at[0], send, recv, pass_send, pass_recv)
    collect = Collect(
        me, False, kept, passing, passed, total, back, local_sem.at[1], swap_send, swap_recv, out_send, out_recv
    )
    dispatch.start()
    for load in loads:
        load.start()
    block = landing.shape[1]
    hidden_units = gate.shape[1]
    chunks = hidden_units // chunk
    half = back.shape[2] // 2

    def stage_copies(chip, part, slot):
        span = pl.ds(pl.multiple_of(chip * block, 16), block)
        columns = pl.ds(pl.multiple_of(part * chunk, 128), chunk)
        return [
            pltpu.make_async_copy(
                pre_stage.at[slot, n], out.at[span, columns], stage_sem.at[slot, n]
            )
            for n, out in enumerate((gate_out, up_out))
        ]

    def act_copy(chip, step):
        span = pl.ds(pl.multiple_of(chip * block, 16), block)
        return pltpu.make_async_copy(act.at[step % 2], act_out.at[span, :], act_sem.at[step % 2])

    def rows_copy(chip, step):
        span = pl.ds(pl.multiple_of(chip * block, 16), block)
        return pltpu.make_async_copy(landing.at[chip], rows_out.at[span, :], rows_sem.at[step])

    for step in range(4):
        if step == 0:
            dispatch.arrive(0)
        chip = dispatch.ready(step)
        rows_copy(chip, step).start()
        if step == 0:
            loads[0].wait()
            loads[1].wait()
        if step >= 2:
            act_copy(chip_order(me // 2, step - 2), step - 2).wait()

        def hidden_part(part, carry, chip=chip, step=step):
            slot = lax.rem(part + step * chunks, 2)
            columns = pl.ds(pl.multiple_of(part * chunk, 128), chunk)

            @pl.when(part + step * chunks >= 2)
            def _():
                for copy in stage_copies(chip, part, slot):
                    copy.wait()

            gated = dot_nn(landing[chip], gate[:, columns])
            raised = dot_nn(landing[chip], up[:, columns])
            pre_stage[slot, 0] = gated.astype(jnp.bfloat16)
            pre_stage[slot, 1] = raised.astype(jnp.bfloat16)
            act[step % 2, :, columns] = (gated * jax.nn.sigmoid(gated) * raised).astype(jnp.bfloat16)
            for copy in stage_copies(chip, part, slot):
                copy.start()
            return carry

        lax.fori_loop(0, chunks, hidden_part, 0)
        act_copy(chip, step).start()
        if step < 3:
            dispatch.arrive(step + 1)
        if step == 0:
            loads[2].wait()
        else:
            collect.settle(step - 1)
        core = collect.core
        width = min(256, half)

        def far_part(part, carry, step=step):
            at = pl.multiple_of((1 - core) * half + part * width, 128)
            product = dot_nt(act[step % 2], down[pl.ds(at, width), :])
            passing[step, :, pl.ds(pl.multiple_of(part * width, 128), width)] = product.astype(jnp.bfloat16)
            return carry

        def near_part(part, carry, step=step):
            at = pl.multiple_of(core * half + part * width, 128)
            product = dot_nt(act[step % 2], down[pl.ds(at, width), :])
            kept[step % 2, :, pl.ds(pl.multiple_of(part * width, 128), width)] = product
            return carry

        lax.fori_loop(0, half // width, far_part, 0)
        collect.swap(step).start()
        lax.fori_loop(0, half // width, near_part, 0)
    collect.settle(3)
    for step in (2, 3):
        act_copy(chip_order(me // 2, step), step).wait()
    for step in range(4):
        rows_copy(chip_order(me // 2, step), step).wait()
    for slot in range(2):
        for copy in stage_copies(0, 0, slot):
            copy.wait()
    dispatch.finish()
    collect.finish()


def ffn_forward(slots, gate_weight, up_weight, down_weight):
    chips, capacity, depth = slots.shape
    hidden_units = gate_weight.shape[1]
    block = 2 * capacity
    chunk = 256 if hidden_units % 256 == 0 else 128
    half = depth // 2
    rows = chips * block
    any_space = pl.BlockSpec(memory_space=pl.ANY)
    bf = jnp.bfloat16
    dma = pltpu.SemaphoreType.DMA
    return pl.pallas_call(
        functools.partial(ffn_forward_body, chunk),
        in_specs=[any_space] * 4,
        out_specs=[any_space] * 5,
        out_shape=[
            jax.ShapeDtypeStruct((rows, depth), bf),
            jax.ShapeDtypeStruct((rows, hidden_units), bf),
            jax.ShapeDtypeStruct((rows, hidden_units), bf),
            jax.ShapeDtypeStruct((rows, hidden_units), bf),
            jax.ShapeDtypeStruct((chips, capacity, depth), bf),
        ],
        scratch_shapes=[
            pltpu.VMEM((depth, hidden_units), bf),
            pltpu.VMEM((depth, hidden_units), bf),
            pltpu.VMEM((depth, hidden_units), bf),
            pltpu.VMEM((chips, block, depth), bf),
            pltpu.VMEM((2, 2, block, chunk), bf),
            pltpu.VMEM((2, block, hidden_units), bf),
            pltpu.VMEM((2, block, half), jnp.float32),
            pltpu.VMEM((chips, block, half), bf),
            pltpu.VMEM((chips, block, half), bf),
            pltpu.VMEM((chips, block, half), bf),
            dma((3,)),
            dma((2, 2)),
            dma((2,)),
            dma((4,)),
            dma((2,)),
            dma((8,)),
            dma((8,)),
            dma((8,)),
            dma((8,)),
            dma((4,)),
            dma((4,)),
            dma((8,)),
            dma((8,)),
        ],
        compiler_params=pltpu.CompilerParams(
            collective_id=1, has_side_effects=True, vmem_limit_bytes=VMEM_BYTES
        ),
        name="ffn_forward",
    )(slots, gate_weight, up_weight, down_weight)


def send_rows_body(slots, rows_out, local_sem, send, recv, pass_send, pass_recv):
    me = lax.axis_index("expert")
    enter(8, me)
    dispatch = Dispatch(me, slots, rows_out, local_sem.at[0], send, recv, pass_send, pass_recv)
    dispatch.start()
    for step in range(4):
        dispatch.arrive(step)
    for step in range(4):
        dispatch.ready(step)
    dispatch.finish()


def send_rows(slots, collective):
    chips, capacity, depth = slots.shape
    any_space = pl.BlockSpec(memory_space=pl.ANY)
    dma = pltpu.SemaphoreType.DMA
    return pl.pallas_call(
        send_rows_body,
        in_specs=[any_space],
        out_specs=any_space,
        out_shape=jax.ShapeDtypeStruct((chips, 2 * capacity, depth), jnp.bfloat16),
        scratch_shapes=[dma((1,)), dma((8,)), dma((8,)), dma((8,)), dma((8,))],
        compiler_params=pltpu.CompilerParams(collective_id=collective, has_side_effects=True),
        name="send_rows",
    )(slots)


def ffn_backward_body(
    chunk,
    grad_rows,
    gate_in,
    up_in,
    gate_hbm,
    up_hbm,
    down_hbm,
    dgate_out,
    dup_out,
    back,
    gate,
    up,
    down,
    grad,
    pre_stage,
    pair,
    kept,
    passing,
    passed,
    total,
    weight_sem,
    grad_sem,
    stage_sem,
    pair_sem,
    local_sem,
    swap_send,
    swap_recv,
    out_send,
    out_recv,
):
    me = lax.axis_index("expert")
    enter(8, me)
    collect = Collect(
        me, True, kept, passing, passed, total, back, local_sem.at[0], swap_send, swap_recv, out_send, out_recv
    )
    loads = [
        pltpu.make_async_copy(source, target, weight_sem.at[n])
        for n, (source, target) in enumerate(((down_hbm, down), (gate_hbm, gate), (up_hbm, up)))
    ]
    block = grad.shape[1]
    hidden_units = gate.shape[1]
    chunks = hidden_units // chunk
    half = back.shape[2] // 2
    width = min(256, half)

    def span_of(chip):
        return pl.ds(pl.multiple_of(chip * block, 16), block)

    def grad_copy(step):
        return pltpu.make_async_copy(
            grad_rows.at[span_of(collect.block(step)), :], grad.at[step % 2], grad_sem.at[step % 2]
        )

    def stage_copies(chip, part, slot):
        columns = pl.ds(pl.multiple_of(part * chunk, 128), chunk)
        return [
            pltpu.make_async_copy(
                source.at[span_of(chip), columns], pre_stage.at[slot, n], stage_sem.at[slot, n]
            )
            for n, source in enumerate((gate_in, up_in))
        ]

    def pair_copies(chip):
        return [
            pltpu.make_async_copy(pair.at[n], out.at[span_of(chip), :], pair_sem.at[n])
            for n, out in enumerate((dgate_out, dup_out))
        ]

    grad_copy(0).start()
    loads[0].start()
    for copy in stage_copies(collect.block(0), 0, 0):
        copy.start()
    loads[1].start()
    loads[2].start()
    loads[0].wait()
    for step in range(4):
        chip = collect.block(step)
        grad_copy(step).wait()
        if step < 3:
            grad_copy(step + 1).start()
        if step > 0:
            for copy in pair_copies(collect.block(step - 1)):
                copy.wait()

        def hidden_part(part, carry, chip=chip, step=step):
            slot = lax.rem(part, 2)
            columns = pl.ds(pl.multiple_of(part * chunk, 128), chunk)
            for copy in stage_copies(chip, part, slot):
                copy.wait()

            @pl.when(part + 1 < chunks)
            def _():
                for copy in stage_copies(chip, part + 1, 1 - slot):
                    copy.start()

            upstream = dot_nn(grad[step % 2], down[:, columns])
            gated = pre_stage[slot, 0].astype(jnp.float32)
            raised = pre_stage[slot, 1].astype(jnp.float32)
            sigmoid = jax.nn.sigmoid(gated)
            scaled = upstream * sigmoid
            pair[0, :, columns] = (scaled * raised * (1.0 + gated * (1.0 - sigmoid))).astype(jnp.bfloat16)
            pair[1, :, columns] = (scaled * gated).astype(jnp.bfloat16)
            return carry

        lax.fori_loop(0, chunks, hidden_part, 0)
        for copy in pair_copies(chip):
            copy.start()
        if step < 3:
            for copy in stage_copies(collect.block(step + 1), 0, 0):
                copy.start()
        if step == 0:
            loads[1].wait()
            loads[2].wait()
        else:
            collect.settle(step - 1)
        core = collect.core

        def product(at):
            return dot_nt(pair[0], gate[pl.ds(at, width), :]) + dot_nt(pair[1], up[pl.ds(at, width), :])

        def far_part(part, carry, step=step):
            at = pl.multiple_of((1 - core) * half + part * width, 128)
            columns = pl.ds(pl.multiple_of(part * width, 128), width)
            passing[step, :, columns] = product(at).astype(jnp.bfloat16)
            return carry

        def near_part(part, carry, step=step):
            at = pl.multiple_of(core * half + part * width, 128)
            kept[step % 2, :, pl.ds(pl.multiple_of(part * width, 128), width)] = product(at)
            return carry

        lax.fori_loop(0, half // width, far_part, 0)
        collect.swap(step).start()
        lax.fori_loop(0, half // width, near_part, 0)
    collect.settle(3)
    for copy in pair_copies(collect.block(3)):
        copy.wait()
    collect.finish()


def ffn_backward(grad_rows, gate_pre, up_pre, gate_weight, up_weight, down_weight, capacity):
    rows, depth = grad_rows.shape
    hidden_units = gate_weight.shape[1]
    block = 2 * capacity
    chips = rows // block
    chunk = 256 if hidden_units % 256 == 0 else 128
    half = depth // 2
    any_space = pl.BlockSpec(memory_space=pl.ANY)
    bf = jnp.bfloat16
    dma = pltpu.SemaphoreType.DMA
    return pl.pallas_call(
        functools.partial(ffn_backward_body, chunk),
        in_specs=[any_space] * 6,
        out_specs=[any_space] * 3,
        out_shape=[
            jax.ShapeDtypeStruct((rows, hidden_units), bf),
            jax.ShapeDtypeStruct((rows, hidden_units), bf),
            jax.ShapeDtypeStruct((chips, capacity, depth), bf),
        ],
        scratch_shapes=[
            pltpu.VMEM((depth, hidden_units), bf),
            pltpu.VMEM((depth, hidden_units), bf),
            pltpu.VMEM((depth, hidden_units), bf),
            pltpu.VMEM((2, block, depth), bf),
            pltpu.VMEM((2, 2, block, chunk), bf),
            pltpu.VMEM((2, block, hidden_units), bf),
            pltpu.VMEM((2, block, half), jnp.float32),
            pltpu.VMEM((chips, block, half), bf),
            pltpu.VMEM((chips, block, half), bf),
            pltpu.VMEM((chips, block, half), bf),
            dma((3,)),
            dma((2,)),
            dma((2, 2)),
            dma((2,)),
            dma((1,)),
            dma((4,)),
            dma((4,)),
            dma((8,)),
            dma((8,)),
        ],
        compiler_params=pltpu.CompilerParams(
            collective_id=3, has_side_effects=True, vmem_limit_bytes=VMEM_BYTES
        ),
        name="ffn_backward",
    )(grad_rows, gate_pre, up_pre, gate_weight, up_weight, down_weight)


D = 2048
HEADS = 16
ATT_EXPERTS = 8
FFN_EXPERTS = 4
TRUNK = 1024
SEG = 96
TREE_LEN = 2176
NODES = 13

epsilon = 1e-06
highest = lax.Precision.HIGHEST
bf16 = jnp.bfloat16
f32 = jnp.float32


def tree_layout(places):
    after_trunk = places - TRUNK
    after_branch = after_trunk - 4 * SEG
    segments = jnp.where(
        places < TRUNK,
        0,
        jnp.where(after_branch < 0, 1 + after_trunk // SEG, 5 + after_branch // SEG),
    )
    depths = jnp.where(
        places < TRUNK,
        places,
        jnp.where(after_branch < 0, TRUNK + after_trunk % SEG, TRUNK + SEG + after_branch % SEG),
    )
    return (segments.astype(jnp.int32), depths.astype(jnp.int32))


def rotation_tables(depths):
    half_size = HEAD // 2
    frequency = 10000.0 ** (-jnp.arange(half_size, dtype=f32) * 2.0 / HEAD)
    angles = depths.astype(f32)[:, None] * frequency[None, :]
    cosine, sine = jnp.cos(angles), jnp.sin(angles)
    cosines = jnp.concatenate([cosine, cosine], axis=1)
    forward = jnp.concatenate([-sine, sine], axis=1)
    return (cosines, forward), (cosines, -forward)


def lookup(table, indices):
    nodes = jnp.arange(NODES, dtype=jnp.int32)
    return jnp.sum(jnp.where(indices[:, None] == nodes[None, :], table[None, :], 0), axis=1)


def running_count(chosen):
    rows = chosen.shape[-1]
    index = jnp.arange(rows, dtype=jnp.int32)
    upto = (index[:, None] <= index[None, :]).astype(bf16)
    return jnp.dot(chosen.astype(bf16), upto, preferred_element_type=f32).astype(jnp.int32) - 1


def source_plan(routes, expert, capacity):
    chosen = jnp.any(routes == expert, axis=2)
    ranking = running_count(chosen)
    slots = jnp.arange(capacity, dtype=jnp.int32)
    return chosen[:, None, :] & (ranking[:, None, :] == slots[None, :, None])


def token_picks(routes, experts, capacity):
    labels = jnp.arange(experts, dtype=jnp.int32)
    hits = routes.T[:, None, :] == labels[None, :, None]
    ranking = running_count(hits[0] | hits[1])
    slots = jnp.arange(capacity, dtype=jnp.int32)
    picks = hits[:, :, None, :] & (ranking[None, :, None, :] == slots[None, None, :, None])
    return picks.astype(bf16), hits[0].T.astype(f32), hits[1].T.astype(f32)


def fill_slots(picks, pair):
    return jnp.einsum("kecr,krd->ecd", picks, pair, preferred_element_type=f32).astype(bf16)


def read_slots(picks, slots):
    return jnp.einsum("kecr,ecd->krd", picks, slots, preferred_element_type=f32)


def gate_values(hidden, router, first, second):
    logits = jnp.dot(hidden.astype(f32), router, precision=highest)
    picked = jnp.stack([jnp.sum(logits * first, axis=1), jnp.sum(logits * second, axis=1)], axis=1)
    return jax.nn.softmax(picked, axis=1)


def router_grads(hidden, router, gates, first, second, picked_grad):
    logit_pick = gates * (picked_grad - jnp.sum(gates * picked_grad, axis=1, keepdims=True))
    logit_grad = logit_pick[:, 0:1] * first + logit_pick[:, 1:2] * second
    router_grad = jnp.dot(hidden.astype(f32).T, logit_grad, precision=highest)
    hidden_grad = jnp.dot(logit_grad, router.T, precision=highest)
    return (router_grad, hidden_grad)


def rms_parts(values):
    inverse = lax.rsqrt(jnp.mean(values * values, axis=-1, keepdims=True) + epsilon)
    return (values * inverse, inverse)


def norm_back(grad_normed, normed, inverse):
    return inverse * (grad_normed - normed * jnp.mean(grad_normed * normed, axis=-1, keepdims=True))


def pair_grads(gates, branches, upstream):
    gate_grad = jnp.stack([jnp.sum(upstream * branches[k], axis=1) for k in range(2)], axis=1)
    scaled = jnp.stack([gates[:, k : k + 1] * upstream for k in range(2)]).astype(bf16)
    return gate_grad, scaled


def exchange(slots):
    return lax.all_to_all(slots, "expert", split_axis=0, concat_axis=0, tiled=True)


def shift(values, step, size, devices):
    moves = [(i, i // size * size + (i % size + step) % size) for i in range(devices)]
    return lax.ppermute(values, "expert", moves)


def group_gather(rows, size, devices):
    return jnp.concatenate([rows] + [shift(rows, step, size, devices) for step in range(1, size)])


def group_reduce(partial, size, devices):
    parts = partial.reshape(size, -1, partial.shape[1])
    total = parts[0].astype(f32)
    for step in range(1, size):
        total = total + shift(parts[step], -step, size, devices).astype(f32)
    return total.astype(bf16)


def spread_over_replicas(block, my_replica, replicas):
    if replicas != 4:
        return lax.all_gather(block, "dp", axis=0), jnp.arange(replicas, dtype=jnp.int32)
    across, along = ([(i, i ^ n) for i in range(4)] for n in (1, 2))
    first, second = lax.ppermute(block, "dp", across), lax.ppermute(block, "dp", along)
    cut = block.shape[0] // 2
    upper, lower = lax.ppermute(second[:cut], "dp", across), lax.ppermute(first[cut:], "dp", along)
    blocks = jnp.stack([block, first, second, jnp.concatenate([upper, lower])])
    return blocks, my_replica ^ jnp.arange(4, dtype=jnp.int32)


def dot_tn(left, right):
    return lax.dot_general(left, right, (((0,), (0,)), ((), ())), preferred_element_type=f32)


def body(
    tokens,
    teacher,
    att_routes,
    ffn_routes,
    parent,
    valid,
    gain_one,
    kv_weight,
    att_router,
    q_weight,
    o_weight,
    gain_two,
    ffn_router,
    gate_weight,
    up_weight,
    down_weight,
):
    row_count = tokens.shape[0]
    devices, replicas = lax.axis_size("expert"), lax.axis_size("dp")
    my_index, my_replica = lax.axis_index("expert"), lax.axis_index("dp")
    core = my_index % 2
    att_copies, ffn_copies = devices // ATT_EXPERTS, devices // FFN_EXPERTS
    att_capacity, ffn_capacity = row_count * 13 // 40, row_count * 13 // 20
    token_count = row_count * devices
    half = HEADS * HEAD // 2
    assert token_count == TREE_LEN * parent.shape[0] and parent.shape[0] == 1
    pair = [(i, i ^ 1) for i in range(devices)]
    own_places = my_index * row_count + jnp.arange(row_count, dtype=jnp.int32)

    x_in = tokens.astype(f32)
    normed_one, inverse_one = rms_parts(x_in)
    hidden = (normed_one * gain_one).astype(bf16)
    weight_rows = kv_weight.shape[0]
    piece = half // replicas
    kv_share = lax.dynamic_slice_in_dim(
        kv_weight.reshape(weight_rows, 4, replicas, piece), my_replica, 1, 2
    )
    kv_share = (
        kv_share.reshape(weight_rows, 2, 2, piece).transpose(0, 2, 1, 3).reshape(weight_rows, 4 * piece)
    )
    all_routes = lax.all_gather(att_routes, "expert", axis=0)
    kv_gathered = lax.all_gather(kv_share, "expert", axis=0)
    kv_gathered, hidden_sent = lax.optimization_barrier((kv_gathered, hidden))
    hidden_all = lax.all_gather(hidden_sent, "expert", axis=0)
    kv_half = lax.dynamic_slice_in_dim(kv_gathered, core * 2 * piece, 2 * piece, 2).reshape(D, 2 * piece)
    kv_blocks, block_order = spread_over_replicas(kv_half, my_replica, replicas)

    tree_places = jnp.arange(token_count, dtype=jnp.int32)
    tree_segments, tree_depths = tree_layout(tree_places)
    key_forward, key_backward = rotation_tables(tree_depths)
    key_info = jnp.pad(jnp.stack([tree_places, tree_segments], axis=1), ((0, 0), (0, 6)))
    experts_here = [my_index // att_copies]
    if att_copies == 1:
        experts_here.append(my_index ^ 1)
    plans = [source_plan(all_routes, expert, att_capacity) for expert in experts_here]
    slot_tables, query_parts = [], []
    for plan in plans:
        places = jnp.sum(
            jnp.where(plan, tree_places.reshape(devices, 1, row_count), 0), axis=2
        ).reshape(-1)
        segments, depths = tree_layout(places)
        parents = lookup(parent[0], segments)
        grands = lookup(parent[0], parents)
        query_parts.append(jnp.stack([places, segments, parents, grands]).reshape(4, GROUPS, -1))
        slot_tables.append(rotation_tables(depths))
    query_info = jnp.concatenate(query_parts, axis=2).transpose(1, 0, 2)
    own_plan = plans[0].astype(bf16)
    att_picks, att_first, att_second = token_picks(att_routes, ATT_EXPERTS, att_capacity)
    att_gates = gate_values(hidden, att_router, att_first, att_second)
    ffn_picks, ffn_first, ffn_second = token_picks(ffn_routes, FFN_EXPERTS, ffn_capacity)
    prepared = (key_forward, key_backward, key_info, slot_tables, query_info, own_plan, att_picks, att_gates, ffn_picks)
    hidden_all, prepared = lax.optimization_barrier((hidden_all, prepared))
    key_forward, key_backward, key_info, slot_tables, query_info, own_plan, att_picks, att_gates, ffn_picks = prepared

    queries, query_inputs = project_queries(own_plan, hidden_all, q_weight, slot_tables[0][0])
    keys_all, values_all = project_keys_values(hidden_all, kv_blocks, key_forward, block_order)

    def far_half(values):
        return lax.ppermute(
            lax.dynamic_slice_in_dim(values, (1 - core) * half, half, 1), "expert", pair
        )

    def join_halves(mine, sibling):
        other = lax.ppermute(sibling, "expert", pair)
        return jnp.where(
            core == 0,
            jnp.concatenate([mine, other], axis=1),
            jnp.concatenate([other, mine], axis=1),
        )

    heads = half // HEAD
    query_sets = [queries]
    starts = jnp.zeros((2,), jnp.int32)
    if att_copies == 1:
        query_sets.append(far_half(queries))
        starts = jnp.stack([core * heads, 0]).astype(jnp.int32)
    *att_outs, lse = attention_forward(
        query_sets, starts // 2, keys_all, values_all, key_info, query_info, heads
    )
    att_rows = join_halves(*att_outs) if att_copies == 1 else att_outs[0]
    att_partial = lax.dot_general(
        att_rows, o_weight, (((1,), (1,)), ((), ())), preferred_element_type=f32
    ).astype(bf16)
    att_back = exchange(att_partial.reshape(devices, att_capacity, D))
    if att_copies > 1:
        att_back = (
            att_back.astype(f32).reshape(ATT_EXPERTS, att_copies, att_capacity, D).sum(axis=1).astype(bf16)
        )
    att_branches = read_slots(att_picks, att_back)
    x_mid = x_in + att_gates[:, 0:1] * att_branches[0] + att_gates[:, 1:2] * att_branches[1]

    normed_two, inverse_two = rms_parts(x_mid)
    hidden_two = (normed_two * gain_two).astype(bf16)
    ffn_gates = gate_values(hidden_two, ffn_router, ffn_first, ffn_second)

    def to_experts(slots):
        rows = exchange(slots.reshape(devices, ffn_capacity // ffn_copies, D))
        return group_gather(rows.reshape(-1, D), ffn_copies, devices)

    def to_tokens(partial):
        rows = group_reduce(partial.astype(bf16), ffn_copies, devices)
        back = exchange(rows.reshape(devices, ffn_capacity // ffn_copies, D))
        return read_slots(ffn_picks, back.reshape(FFN_EXPERTS, ffn_capacity, D))

    ffn_slots = jnp.einsum(
        "ecr,rd->ecd", ffn_picks[0] + ffn_picks[1], hidden_two, preferred_element_type=f32
    ).astype(bf16)
    fused = devices == 8 and ffn_copies == 2 and ffn_capacity % 16 == 0
    if fused:
        ffn_inputs, gate_pre, up_pre, activated, ffn_back = ffn_forward(
            ffn_slots, gate_weight, up_weight, down_weight
        )
        ffn_branches = read_slots(ffn_picks, ffn_back)
    else:
        ffn_inputs = to_experts(ffn_slots)
        gate_pre = jnp.dot(ffn_inputs, gate_weight, preferred_element_type=f32)
        up_pre = jnp.dot(ffn_inputs, up_weight, preferred_element_type=f32)
        sigmoid_gate = jax.nn.sigmoid(gate_pre)
        silu_gate = gate_pre * sigmoid_gate
        activated = (silu_gate * up_pre).astype(bf16)
        ffn_branches = to_tokens(
            lax.dot_general(
                activated, down_weight, (((1,), (1,)), ((), ())), preferred_element_type=f32
            )
        )
    result = x_mid + ffn_gates[:, 0:1] * ffn_branches[0] + ffn_gates[:, 1:2] * ffn_branches[1]

    tree_global = my_replica * parent.shape[0] + own_places // TREE_LEN
    tree_labels = jnp.arange(valid.shape[0], dtype=jnp.int32)
    limits = jnp.sum(
        jnp.where(tree_global[:, None] == tree_labels[None, :], valid[None, :], 0), axis=1
    )
    counted = own_places % TREE_LEN < limits
    loss_factor = valid.shape[0] * TREE_LEN / jnp.sum(valid).astype(f32)
    grad_result = jnp.where(counted[:, None], (result - teacher.astype(f32)) * loss_factor, 0.0)

    ffn_gate_grad, ffn_scaled = pair_grads(ffn_gates, ffn_branches, grad_result)
    ffn_grad_slots = fill_slots(ffn_picks, ffn_scaled)
    if fused:
        grad_ffn_out = send_rows(ffn_grad_slots, 2).reshape(-1, D)
    else:
        grad_ffn_out = to_experts(ffn_grad_slots)
    grad_down = dot_tn(grad_ffn_out, activated).astype(bf16)
    grad_ffn_out, grad_down = lax.optimization_barrier((grad_ffn_out, grad_down))
    summed_down = lax.psum_scatter(grad_down, "dp", scatter_dimension=0, tiled=True)
    if fused:
        grad_gate_pre, grad_up_pre, ffn_grad_back = ffn_backward(
            grad_ffn_out, gate_pre, up_pre, gate_weight, up_weight, down_weight, ffn_capacity
        )
        grad_gate = dot_tn(ffn_inputs, grad_gate_pre).astype(bf16)
        ffn_grad_back, grad_gate = lax.optimization_barrier((ffn_grad_back, grad_gate))
        ffn_grad_pair = read_slots(ffn_picks, ffn_grad_back)
    else:
        grad_activated = jnp.dot(grad_ffn_out, down_weight, preferred_element_type=f32)
        grad_gate_pre = (
            grad_activated * up_pre * sigmoid_gate * (1.0 + gate_pre * (1.0 - sigmoid_gate))
        ).astype(bf16)
        grad_up_pre = (grad_activated * silu_gate).astype(bf16)
        grad_ffn_in = lax.dot_general(
            grad_gate_pre, gate_weight, (((1,), (1,)), ((), ())), preferred_element_type=f32
        ) + lax.dot_general(
            grad_up_pre, up_weight, (((1,), (1,)), ((), ())), preferred_element_type=f32
        )
        grad_gate = dot_tn(ffn_inputs, grad_gate_pre).astype(bf16)
        ffn_grad_pair = to_tokens(grad_ffn_in)
    grad_up = dot_tn(ffn_inputs, grad_up_pre).astype(bf16)
    summed_gate = lax.psum_scatter(grad_gate, "dp", scatter_dimension=0, tiled=True)
    summed_up = lax.psum_scatter(grad_up, "dp", scatter_dimension=0, tiled=True)
    grad_ffn_router, hidden_two_extra = router_grads(
        hidden_two, ffn_router, ffn_gates, ffn_first, ffn_second, ffn_gate_grad
    )
    grad_hidden_two = ffn_grad_pair[0] + ffn_grad_pair[1] + hidden_two_extra
    grad_gain_two = jnp.sum(grad_hidden_two * normed_two, axis=0)
    grad_mid = grad_result + norm_back(grad_hidden_two * gain_two, normed_two, inverse_two)

    att_gate_grad, att_scaled = pair_grads(att_gates, att_branches, grad_mid)
    att_slots = fill_slots(att_picks, att_scaled)
    att_slots, summed_down = lax.optimization_barrier((att_slots, summed_down))
    if att_copies > 1:
        att_slots = jnp.repeat(att_slots, att_copies, axis=0)
    grad_att_out = exchange(att_slots).reshape(-1, D)
    grad_o = dot_tn(grad_att_out, att_rows).astype(bf16)
    grad_att_out, grad_o = lax.optimization_barrier((grad_att_out, grad_o))
    summed_o = lax.psum_scatter(grad_o, "dp", scatter_dimension=0, tiled=True)
    grad_heads = jnp.dot(grad_att_out, o_weight, preferred_element_type=f32).astype(bf16)
    grad_sets = [grad_heads]
    if att_copies == 1:
        grad_sets.append(far_half(grad_heads))
    grad_sets[-1], summed_gate, grad_up = lax.optimization_barrier((grad_sets[-1], summed_gate, grad_up))
    *grad_queries, grad_keys, grad_values = attention_backward(
        query_sets,
        starts,
        grad_sets,
        att_outs,
        keys_all,
        values_all,
        lse,
        key_info,
        query_info,
        key_backward,
        [tables[1] for tables in slot_tables],
        heads,
    )
    grad_query_pre = join_halves(*grad_queries) if att_copies == 1 else grad_queries[0]
    grad_query_in = lax.dot_general(
        grad_query_pre, q_weight, (((1,), (1,)), ((), ())), preferred_element_type=f32
    ).astype(bf16)
    grad_q = dot_tn(query_inputs, grad_query_pre).astype(bf16)
    grad_query_in, summed_up, summed_o = lax.optimization_barrier((grad_query_in, summed_up, summed_o))
    hidden_rows = hidden_all.reshape(token_count, D)
    grad_kv = jnp.concatenate(
        [dot_tn(hidden_rows, grad_keys).astype(bf16), dot_tn(hidden_rows, grad_values).astype(bf16)], axis=1
    )
    summed_kv = lax.psum_scatter(grad_kv, "dp", scatter_dimension=0, tiled=True)
    summed_q = lax.psum_scatter(grad_q, "dp", scatter_dimension=0, tiled=True)

    merged = merge_hidden_grads(
        own_plan.transpose(0, 2, 1),
        grad_query_in.reshape(devices, att_capacity, D),
        grad_keys,
        grad_values,
        kv_blocks,
        block_order,
    ).reshape(devices // 2, 2, row_count, D)
    kept = lax.dynamic_index_in_dim(merged, core, 1, keepdims=False)
    passed = lax.ppermute(
        lax.dynamic_index_in_dim(merged, 1 - core, 1, keepdims=False), "expert", pair
    )
    chip_sum = (kept.astype(f32) + passed.astype(f32)).astype(bf16)
    same_core = [[2 * i + c for i in range(devices // 2)] for c in range(2)]
    arrived = lax.all_to_all(
        chip_sum, "expert", split_axis=0, concat_axis=0, axis_index_groups=same_core, tiled=True
    )
    arrived, summed_kv = lax.optimization_barrier((arrived, summed_kv))
    grad_att_router, hidden_one_extra = router_grads(
        hidden, att_router, att_gates, att_first, att_second, att_gate_grad
    )
    grad_hidden_one = jnp.sum(arrived.astype(f32), axis=0) + hidden_one_extra
    grad_gain_one = jnp.sum(grad_hidden_one * normed_one, axis=0)
    grad_input = grad_mid + norm_back(grad_hidden_one * gain_one, normed_one, inverse_one)

    everyone = devices * replicas
    smalls = [grad_gain_one, grad_gain_two, grad_att_router, grad_ffn_router]
    packed = jnp.concatenate([small.reshape(everyone, -1) for small in smalls], axis=1)
    own_smalls = jnp.sum(
        lax.all_to_all(packed, ("dp", "expert"), split_axis=0, concat_axis=0, tiled=True), axis=0
    )
    share = D // everyone
    shared_gain_one = own_smalls[:share]
    shared_gain_two = own_smalls[share : 2 * share]
    shared_att_router = own_smalls[2 * share : (2 + ATT_EXPERTS) * share].reshape(share, ATT_EXPERTS)
    shared_ffn_router = own_smalls[(2 + ATT_EXPERTS) * share :].reshape(share, FFN_EXPERTS)

    kv_rows = exchange(summed_kv.reshape(devices, -1, 2 * half))
    kv_sum = jnp.sum(kv_rows.astype(f32).reshape(devices // 2, 2, -1, 2, half), axis=0)
    shared_kv = kv_sum.transpose(1, 2, 0, 3).reshape(-1, 4 * half)

    return (
        result.astype(bf16),
        grad_input.astype(bf16),
        shared_gain_one,
        shared_kv,
        shared_att_router,
        summed_q.astype(f32),
        summed_o.astype(f32),
        shared_gain_two,
        shared_ffn_router,
        summed_gate.astype(f32),
        summed_up.astype(f32),
        summed_down.astype(f32),
    )


def solution(mesh):
    in_specs = (
        P(("dp", "expert"), None),
        P(("dp", "expert"), None),
        P(("dp", "expert"), None),
        P(("dp", "expert"), None),
        P("dp", None),
        P(),
        P(),
        P("expert", None),
        P(),
        P(None, "expert"),
        P(None, "expert"),
        P(),
        P(),
        P(None, "expert"),
        P(None, "expert"),
        P(None, "expert"),
    )
    out_specs = (
        P(("dp", "expert"), None),
        P(("dp", "expert"), None),
        P(("dp", "expert")),
        P(("dp", "expert"), None),
        P(("dp", "expert"), None),
        P("dp", "expert"),
        P("dp", "expert"),
        P(("dp", "expert")),
        P(("dp", "expert"), None),
        P("dp", "expert"),
        P("dp", "expert"),
        P("dp", "expert"),
    )
    return jax.shard_map(body, mesh=mesh, in_specs=in_specs, out_specs=out_specs, check_vma=False)
```

```python
import functools
import jax
import jax.numpy as jnp
from jax import lax
from jax.experimental import pallas as pl
from jax.experimental.pallas import tpu as pltpu
from jax.sharding import PartitionSpec as P

HEAD = 128
GROUPS = 4
LOG2E = 1.4426950408889634
VMEM_BYTES = 60 * 1024 * 1024


def dot_nt(left, right):
    return lax.dot_general(left, right, (((1,), (1,)), ((), ())), preferred_element_type=jnp.float32)


def dot_nn(left, right):
    return jnp.dot(left, right, preferred_element_type=jnp.float32)


def spin(values, cosine, sine):
    return values * cosine + pltpu.roll(values, HEAD // 2, 1) * sine


def fill_bias(bias_ref, key_ref, query_ref, keys):
    for group in range(GROUPS):
        place = query_ref[group, 0:1, :]
        own, parent, grand = (query_ref[group, 1 + n : 2 + n, :] for n in range(3))

        def one(block, carry, group=group, place=place, own=own, parent=parent, grand=grand):
            at = pl.multiple_of(block * keys, 16)
            key_place = key_ref[pl.ds(at, keys), 0:1]
            key_segment = key_ref[pl.ds(at, keys), 1:2]
            related = (key_segment == own) | (key_segment == parent) | (key_segment == grand)
            allowed = related & (key_place <= place)
            bias_ref[group * (group + 1) // 2 + block] = jnp.where(allowed, 0.0, -1e30)
            return carry

        lax.fori_loop(0, group + 1, one, 0)


def group_rows(refs, group, rows, lanes):
    parts = [ref[pl.ds(group * rows, rows), lanes] for ref in refs]
    return parts[0] if len(parts) == 1 else jnp.concatenate(parts, axis=0)


def attention_forward_body(sets, step_heads, rows, keys, scale, first_ref, *refs):
    query_refs = refs[:sets]
    key_ref, value_ref, key_info, query_info = refs[sets : sets + 4]
    out_refs = refs[sets + 4 : 2 * sets + 4]
    lse_ref, bias_ref, flipped_ref = refs[2 * sets + 4 :]
    wide = sets * rows

    @pl.when(pl.program_id(0) == 0)
    def _():
        fill_bias(bias_ref, key_info, query_info, keys)

    for head in range(step_heads):
        lanes = pl.ds(head * HEAD, HEAD)
        for block in range(GROUPS):
            values = value_ref[pl.ds(block * keys, keys), lanes].astype(jnp.float32)
            flipped_ref[head, block] = values.T.astype(jnp.bfloat16)
    for group in range(GROUPS):
        queries = [
            group_rows(query_refs, group, rows, pl.ds(head * HEAD, HEAD)) for head in range(step_heads)
        ]

        def one(block, carry, group=group, queries=queries):
            at = pl.multiple_of(block * keys, 16)
            bias = bias_ref[group * (group + 1) // 2 + block]
            result = []
            for head in range(step_heads):
                top, total, mixed = carry[3 * head : 3 * head + 3]
                scores = dot_nt(key_ref[pl.ds(at, keys), pl.ds(head * HEAD, HEAD)], queries[head])
                scores = scores * scale + bias
                new_top = jnp.maximum(top, jnp.max(scores, axis=0, keepdims=True))
                fade = jnp.exp2(top - new_top)
                parts = jnp.exp2(scores - new_top)
                total = total * fade + jnp.sum(parts, axis=0, keepdims=True)
                mixed = mixed * fade + dot_nn(flipped_ref[head, block], parts.astype(jnp.bfloat16))
                result += [new_top, total, mixed]
            return tuple(result)

        start = (
            jnp.full((1, wide), -1e30, jnp.float32),
            jnp.zeros((1, wide), jnp.float32),
            jnp.zeros((HEAD, wide), jnp.float32),
        ) * step_heads
        final = lax.fori_loop(0, group + 1, one, start)
        for head in range(step_heads):
            top, total, mixed = final[3 * head : 3 * head + 3]
            lse_ref[head, group] = top + jnp.log2(total)
            rows_out = (mixed / total).T.astype(jnp.bfloat16)
            for n, ref in enumerate(out_refs):
                ref[pl.ds(group * rows, rows), pl.ds(head * HEAD, HEAD)] = rows_out[
                    n * rows : (n + 1) * rows
                ]


def attention_backward_body(sets, step_heads, rows, keys, scale, first_ref, *refs):
    query_refs, grad_refs, out_refs = (refs[n * sets : (n + 1) * sets] for n in range(3))
    key_ref, value_ref, lse_ref, key_info, query_info = refs[3 * sets : 3 * sets + 5]
    key_cos, key_sin = refs[3 * sets + 5 : 3 * sets + 7]
    table_refs = refs[3 * sets + 7 : 5 * sets + 7]
    rest = refs[5 * sets + 7 :]
    dq_refs = rest[:sets]
    dk_ref, dv_ref, bias_ref, flipped_ref, dk_acc, dv_acc = rest[sets:]
    softmax_scale = scale / LOG2E

    @pl.when(pl.program_id(0) == 0)
    def _():
        fill_bias(bias_ref, key_info, query_info, keys)

    dk_acc[...] = jnp.zeros_like(dk_acc)
    dv_acc[...] = jnp.zeros_like(dv_acc)
    for head in range(step_heads):
        lanes = pl.ds(head * HEAD, HEAD)
        for block in range(GROUPS):
            values = key_ref[pl.ds(block * keys, keys), lanes].astype(jnp.float32)
            flipped_ref[head, block] = values.T.astype(jnp.bfloat16)
    for group in range(GROUPS):
        queries, grads, centres, tops = [], [], [], []
        for head in range(step_heads):
            lanes = pl.ds(head * HEAD, HEAD)
            queries.append(group_rows(query_refs, group, rows, lanes))
            grad = group_rows(grad_refs, group, rows, lanes)
            out = group_rows(out_refs, group, rows, lanes)
            product = grad.astype(jnp.float32) * out.astype(jnp.float32)
            centres.append(jnp.sum(product.T, axis=0, keepdims=True))
            grads.append(grad)
            tops.append(lse_ref[head, group])

        def one(block, carry, group=group, queries=queries, grads=grads, centres=centres, tops=tops):
            at = pl.multiple_of(block * keys, 16)
            bias = bias_ref[group * (group + 1) // 2 + block]
            result = []
            for head in range(step_heads):
                lanes = pl.ds(head * HEAD, HEAD)
                key_rows = key_ref[pl.ds(at, keys), lanes]
                scores = dot_nt(key_rows, queries[head])
                probs = jnp.exp2(scores * scale + (bias - tops[head]))
                grad_probs = dot_nt(value_ref[pl.ds(at, keys), lanes], grads[head])
                grad_scores = (probs * (grad_probs - centres[head])).astype(jnp.bfloat16)
                dv_acc[pl.ds(at, keys), lanes] += dot_nn(probs.astype(jnp.bfloat16), grads[head])
                dk_acc[pl.ds(at, keys), lanes] += dot_nn(grad_scores, queries[head])
                result.append(carry[head] + dot_nn(flipped_ref[head, block], grad_scores))
            return tuple(result)

        start = (jnp.zeros((HEAD, sets * rows), jnp.float32),) * step_heads
        final = lax.fori_loop(0, group + 1, one, start)
        for head in range(step_heads):
            dq = final[head].T * softmax_scale
            for n, ref in enumerate(dq_refs):
                span = pl.ds(group * rows, rows)
                turned = spin(
                    dq[n * rows : (n + 1) * rows], table_refs[2 * n][span, :], table_refs[2 * n + 1][span, :]
                )
                ref[span, pl.ds(head * HEAD, HEAD)] = turned.astype(jnp.bfloat16)
    for head in range(step_heads):
        lanes = pl.ds(head * HEAD, HEAD)
        for block in range(GROUPS):
            span = pl.ds(block * keys, keys)
            turned = spin(dk_acc[span, lanes] * softmax_scale, key_cos[span, :], key_sin[span, :])
            dk_ref[span, lanes] = turned.astype(jnp.bfloat16)
            dv_ref[span, lanes] = dv_acc[span, lanes].astype(jnp.bfloat16)


def whole_block(shape):
    return pl.BlockSpec(shape, lambda h, first: (0,) * len(shape))


def attention_forward(queries, starts, keys_all, values_all, key_info, query_info, heads):
    sets, total_rows, tokens = len(queries), queries[0].shape[0], keys_all.shape[0]
    rows, keys = total_rows // GROUPS, tokens // GROUPS
    step_heads = 2
    wide = step_heads * HEAD
    scale = HEAD ** (-0.5) * LOG2E
    query_specs = [
        pl.BlockSpec((total_rows, wide), lambda h, first, n=n: (0, first[n] + h)) for n in range(sets)
    ]
    plain = pl.BlockSpec((total_rows, wide), lambda h, first: (0, h))
    side = pl.BlockSpec((tokens, wide), lambda h, first: (0, h))
    return pl.pallas_call(
        functools.partial(attention_forward_body, sets, step_heads, rows, keys, scale),
        grid_spec=pltpu.PrefetchScalarGridSpec(
            num_scalar_prefetch=1,
            grid=(heads // step_heads,),
            in_specs=query_specs
            + [side, side, whole_block(key_info.shape), whole_block(query_info.shape)],
            out_specs=[plain] * sets
            + [pl.BlockSpec((step_heads, GROUPS, 1, sets * rows), lambda h, first: (h, 0, 0, 0))],
            scratch_shapes=[
                pltpu.VMEM((GROUPS * (GROUPS + 1) // 2, keys, sets * rows), jnp.float32),
                pltpu.VMEM((step_heads, GROUPS, HEAD, keys), jnp.bfloat16),
            ],
        ),
        out_shape=[jax.ShapeDtypeStruct((total_rows, heads * HEAD), jnp.bfloat16)] * sets
        + [jax.ShapeDtypeStruct((heads, GROUPS, 1, sets * rows), jnp.float32)],
        compiler_params=pltpu.CompilerParams(vmem_limit_bytes=VMEM_BYTES),
        name="attention_forward",
    )(starts, *queries, keys_all, values_all, key_info, query_info)


def attention_backward(
    queries, starts, grads, outs, keys_all, values_all, lse, key_info, query_info, key_tables, row_tables, heads
):
    sets, total_rows, tokens = len(queries), queries[0].shape[0], keys_all.shape[0]
    rows, keys = total_rows // GROUPS, tokens // GROUPS
    step_heads = 1
    wide = step_heads * HEAD
    scale = HEAD ** (-0.5) * LOG2E
    shifted = [
        pl.BlockSpec((total_rows, wide), lambda h, first, n=n: (0, first[n] + h)) for n in range(sets)
    ]
    plain = pl.BlockSpec((total_rows, wide), lambda h, first: (0, h))
    side = pl.BlockSpec((tokens, wide), lambda h, first: (0, h))
    return pl.pallas_call(
        functools.partial(attention_backward_body, sets, step_heads, rows, keys, scale),
        grid_spec=pltpu.PrefetchScalarGridSpec(
            num_scalar_prefetch=1,
            grid=(heads // step_heads,),
            in_specs=shifted
            + shifted
            + [plain] * sets
            + [
                side,
                side,
                pl.BlockSpec((step_heads, GROUPS, 1, sets * rows), lambda h, first: (h, 0, 0, 0)),
                whole_block(key_info.shape),
                whole_block(query_info.shape),
                whole_block((tokens, HEAD)),
                whole_block((tokens, HEAD)),
            ]
            + [whole_block((total_rows, HEAD))] * (2 * sets),
            out_specs=[plain] * sets + [side, side],
            scratch_shapes=[
                pltpu.VMEM((GROUPS * (GROUPS + 1) // 2, keys, sets * rows), jnp.float32),
                pltpu.VMEM((step_heads, GROUPS, HEAD, keys), jnp.bfloat16),
                pltpu.VMEM((tokens, wide), jnp.float32),
                pltpu.VMEM((tokens, wide), jnp.float32),
            ],
        ),
        out_shape=[jax.ShapeDtypeStruct((total_rows, heads * HEAD), jnp.bfloat16)] * sets
        + [jax.ShapeDtypeStruct((tokens, heads * HEAD), jnp.bfloat16)] * 2,
        compiler_params=pltpu.CompilerParams(vmem_limit_bytes=VMEM_BYTES),
        name="attention_backward",
    )(
        starts,
        *queries,
        *grads,
        *outs,
        keys_all,
        values_all,
        lse,
        key_info,
        query_info,
        *key_tables,
        *[table for pair in row_tables for table in pair],
    )


def project_body(plan_ref, hidden_ref, weight_ref, cos_ref, sin_ref, out_ref, x_ref):
    sources, capacity = plan_ref.shape[0], plan_ref.shape[1]
    bundle = max(1, sources * capacity // GROUPS // capacity)
    tile = bundle * capacity

    @pl.when(pl.program_id(0) == 0)
    def _():
        for group in range(sources // bundle):
            parts = [
                dot_nn(plan_ref[group * bundle + n], hidden_ref[group * bundle + n]) for n in range(bundle)
            ]
            x_ref[pl.ds(group * tile, tile), :] = jnp.concatenate(parts, axis=0).astype(jnp.bfloat16)

    for at in range(0, x_ref.shape[0], tile):
        span = pl.ds(at, tile)
        product = dot_nn(x_ref[span, :], weight_ref[...])
        for lane in range(0, out_ref.shape[1], HEAD):
            turned = spin(product[:, lane : lane + HEAD], cos_ref[span, :], sin_ref[span, :])
            out_ref[span, lane : lane + HEAD] = turned.astype(jnp.bfloat16)


def project_queries(plan, hidden, weight, tables):
    sources, capacity, row_count = plan.shape
    depth, columns = weight.shape
    rows = sources * capacity
    block = 512
    return pl.pallas_call(
        project_body,
        grid=(columns // block,),
        in_specs=[
            pl.BlockSpec((sources, capacity, row_count), lambda j: (0, 0, 0)),
            pl.BlockSpec((sources, row_count, depth), lambda j: (0, 0, 0)),
            pl.BlockSpec((depth, block), lambda j: (0, j)),
            pl.BlockSpec((rows, HEAD), lambda j: (0, 0)),
            pl.BlockSpec((rows, HEAD), lambda j: (0, 0)),
        ],
        out_specs=[
            pl.BlockSpec((rows, block), lambda j: (0, j)),
            pl.BlockSpec((rows, depth), lambda j: (0, 0)),
        ],
        out_shape=[
            jax.ShapeDtypeStruct((rows, columns), jnp.bfloat16),
            jax.ShapeDtypeStruct((rows, depth), jnp.bfloat16),
        ],
        compiler_params=pltpu.CompilerParams(vmem_limit_bytes=VMEM_BYTES),
        name="project_queries",
    )(plan, hidden, weight, *tables)


def keys_values_body(half, order_ref, x_ref, weight_ref, cos_ref, sin_ref, key_ref, value_ref):
    rows = x_ref.shape[1]
    for source in range(x_ref.shape[0]):
        span = pl.ds(source * rows, rows)
        product = dot_nn(x_ref[source], weight_ref[0])
        for lane in range(0, half, HEAD):
            turned = spin(product[:, lane : lane + HEAD], cos_ref[span, :], sin_ref[span, :])
            key_ref[span, lane : lane + HEAD] = turned.astype(jnp.bfloat16)
        value_ref[span, :] = product[:, half:].astype(jnp.bfloat16)


def project_keys_values(hidden, weights, tables, order):
    sources, rows, unused = hidden.shape
    parts, depth, columns = weights.shape
    half, tokens = columns // 2, sources * rows
    return pl.pallas_call(
        functools.partial(keys_values_body, half),
        grid_spec=pltpu.PrefetchScalarGridSpec(
            num_scalar_prefetch=1,
            grid=(parts,),
            in_specs=[
                pl.BlockSpec((sources, rows, depth), lambda j, order: (0, 0, 0)),
                pl.BlockSpec((1, depth, columns), lambda j, order: (j, 0, 0)),
                pl.BlockSpec((tokens, HEAD), lambda j, order: (0, 0)),
                pl.BlockSpec((tokens, HEAD), lambda j, order: (0, 0)),
            ],
            out_specs=[pl.BlockSpec((tokens, half), lambda j, order: (0, order[j]))] * 2,
        ),
        out_shape=[jax.ShapeDtypeStruct((tokens, parts * half), jnp.bfloat16)] * 2,
        compiler_params=pltpu.CompilerParams(vmem_limit_bytes=VMEM_BYTES),
        name="project_keys_values",
    )(order, hidden, weights, *tables)


def merge_body(tile, order_ref, plan_ref, slots_ref, dk_ref, dv_ref, weight_ref, out_ref, acc_ref):
    part = pl.program_id(1)
    sources, rows = plan_ref.shape[0], plan_ref.shape[1]
    ck = dk_ref.shape[1]

    @pl.when(part == 0)
    def _():
        for source in range(sources):
            acc_ref[pl.ds(source * rows, rows), :] = dot_nn(plan_ref[source], slots_ref[source])

    last = part == pl.num_programs(1) - 1
    for at in range(0, acc_ref.shape[0], tile):
        span = pl.ds(at, tile)
        acc_ref[span, :] += dot_nt(dk_ref[span, :], weight_ref[0, :, :ck]) + dot_nt(
            dv_ref[span, :], weight_ref[0, :, ck:]
        )

    @pl.when(last)
    def _():
        out_ref[...] = acc_ref[...].astype(jnp.bfloat16)


def merge_hidden_grads(plan, slots, grad_keys, grad_values, weights, order):
    sources, rows, capacity = plan.shape
    parts, depth, columns = weights.shape
    ck, tokens = columns // 2, sources * rows
    wide = depth // 2
    return pl.pallas_call(
        functools.partial(merge_body, tokens // GROUPS),
        grid_spec=pltpu.PrefetchScalarGridSpec(
            num_scalar_prefetch=1,
            grid=(2, parts),
            in_specs=[
                pl.BlockSpec((sources, rows, capacity), lambda i, j, order: (0, 0, 0)),
                pl.BlockSpec((sources, capacity, wide), lambda i, j, order: (0, 0, i)),
                pl.BlockSpec((tokens, ck), lambda i, j, order: (0, order[j])),
                pl.BlockSpec((tokens, ck), lambda i, j, order: (0, order[j])),
                pl.BlockSpec((1, wide, columns), lambda i, j, order: (j, i, 0)),
            ],
            out_specs=pl.BlockSpec((tokens, wide), lambda i, j, order: (0, i)),
            scratch_shapes=[pltpu.VMEM((tokens, wide), jnp.float32)],
        ),
        out_shape=jax.ShapeDtypeStruct((tokens, depth), jnp.bfloat16),
        compiler_params=pltpu.CompilerParams(vmem_limit_bytes=VMEM_BYTES),
        name="merge_hidden_grads",
    )(order, plan, slots, grad_keys, grad_values, weights)


def mesh_device(index):
    return {"expert": index}


def chip_order(chip, step):
    flip = chip // 2
    near = chip + flip * (3 - 2 * chip)
    place = step + near * (1 - 2 * step) if step < 2 else step
    return place + flip * (3 - 2 * place)


def enter(devices, me):
    barrier = pltpu.get_barrier_semaphore()
    for step in range(1, devices):
        pl.semaphore_signal(
            barrier,
            inc=1,
            device_id=mesh_device(lax.rem(me + step, devices)),
            device_id_type=pl.DeviceIdType.MESH,
        )
    pl.semaphore_wait(barrier, devices - 1)


def remote(source, target, send, recv, device):
    return pltpu.make_async_remote_copy(
        src_ref=source,
        dst_ref=target,
        send_sem=send,
        recv_sem=recv,
        device_id=mesh_device(device),
        device_id_type=pl.DeviceIdType.MESH,
    )


class Dispatch:
    def __init__(self, me, slots, landing, local_sem, send, recv, pass_send, pass_recv):
        self.me, self.chip, self.core = me, me // 2, lax.rem(me, 2)
        self.slots, self.landing = slots, landing
        self.local_sem, self.send, self.recv = local_sem, send, recv
        self.pass_send, self.pass_recv = pass_send, pass_recv
        self.rows, self.half = slots.shape[1], slots.shape[2] // 2

    def columns(self, core):
        return pl.ds(pl.multiple_of(core * self.half, 128), self.half)

    def place(self, source, core):
        rows = pl.ds(pl.multiple_of(lax.rem(source, 2) * self.rows, 16), self.rows)
        return self.landing.at[source // 2, rows, self.columns(core)]

    def direct(self, target):
        core = lax.rem(target, 2)
        offset = lax.rem(target - self.me + 8, 8)
        return remote(
            self.slots.at[target // 2, :, self.columns(core)],
            self.place(self.me, core),
            self.send.at[offset],
            self.recv.at[offset],
            target,
        )

    def sends(self, step):
        chip = chip_order(self.chip, step)
        targets = [2 * chip, 2 * chip + 1] if step else [self.me + 1 - 2 * self.core]
        return [self.direct(target) for target in targets]

    def local(self):
        return pltpu.make_async_copy(
            self.slots.at[self.chip, :, self.columns(self.core)],
            self.place(self.me, self.core),
            self.local_sem,
        )

    def start(self, steps):
        for step in steps:
            if step == 0:
                self.local().start()
            for copy in self.sends(step):
                copy.start()

    def sent(self, steps):
        for step in steps:
            for copy in self.sends(step):
                copy.wait_send()

    def pass_on(self, source):
        place = self.place(source, self.core)
        return remote(
            place, place, self.pass_send.at[source], self.pass_recv.at[source], self.me + 1 - 2 * self.core
        )

    def arrive(self, step):
        chip = chip_order(self.chip, step)
        for source in (2 * chip, 2 * chip + 1):
            offset = lax.rem(self.me - source + 8, 8)

            @pl.when(offset == 0)
            def _():
                self.local().wait()

            @pl.when(offset != 0)
            def _(source=source, offset=offset):
                place = self.place(source, self.core)
                remote(place, place, self.send.at[offset], self.recv.at[offset], self.me).wait_recv()

            self.pass_on(source).start()

    def ready(self, step):
        chip = chip_order(self.chip, step)
        for source in (2 * chip, 2 * chip + 1):
            place = self.place(source, 1 - self.core)
            remote(
                place, place, self.pass_send.at[source], self.pass_recv.at[source], self.me
            ).wait_recv()
        return chip

    def passed_on(self):
        for source in range(8):
            self.pass_on(source).wait_send()


class Collect:
    def __init__(
        self, me, far_first, kept, passing, passed, total, back, local_sem, pass_send, pass_recv, send, recv
    ):
        self.me, self.chip, self.core, self.far_first = me, me // 2, lax.rem(me, 2), far_first
        self.kept, self.passing, self.passed, self.total, self.back = kept, passing, passed, total, back
        self.local_sem, self.pass_send, self.pass_recv = local_sem, pass_send, pass_recv
        self.send, self.recv = send, recv
        self.rows, self.half = back.shape[1], back.shape[2] // 2

    def swap(self, step):
        return remote(
            self.passing.at[step % 2],
            self.passed.at[step],
            self.pass_send.at[step],
            self.pass_recv.at[step],
            self.me + 1 - 2 * self.core,
        )

    def place(self, chip, core):
        return self.back.at[chip, :, pl.ds(pl.multiple_of(core * self.half, 128), self.half)]

    def local(self, step, source_core):
        return pltpu.make_async_copy(
            self.total.at[step, pl.ds(pl.multiple_of(source_core * self.rows, 16), self.rows), :],
            self.place(self.chip, self.core),
            self.local_sem,
        )

    def outgoing(self, step, source):
        rows = pl.ds(pl.multiple_of(lax.rem(source, 2) * self.rows, 16), self.rows)
        offset = lax.rem(source - self.me + 8, 8)
        return remote(
            self.total.at[step, rows, :],
            self.place(self.chip, self.core),
            self.send.at[offset],
            self.recv.at[offset],
            source,
        )

    def block(self, step):
        return chip_order(self.chip, 3 - step if self.far_first else step)

    def each(self, step, own, other):
        chip = self.block(step)
        for source in (2 * chip, 2 * chip + 1):
            if step != (3 if self.far_first else 0):
                other(source)
                continue

            @pl.when(source == self.me)
            def _():
                own()

            @pl.when(source != self.me)
            def _(source=source):
                other(source)

    def settle(self, step):
        self.swap(step).wait_recv()
        tile = 2 * self.rows // 4
        for at in range(0, 2 * self.rows, tile):
            span = pl.ds(at, tile)
            summed = self.kept[span, :] + self.passed[step, span, :].astype(jnp.float32)
            self.total[step, span, :] = summed.astype(jnp.bfloat16)
        self.each(
            step,
            lambda: self.local(step, self.core).start(),
            lambda source: self.outgoing(step, source).start(),
        )

    def finish(self):
        for step in range(4):
            if step >= 2:
                self.swap(step).wait_send()
            self.each(
                step,
                lambda step=step: self.local(step, self.core).wait(),
                lambda source, step=step: self.outgoing(step, source).wait_send(),
            )
        for offset in range(1, 8):
            source = lax.rem(self.me + 8 - offset, 8)
            place = self.place(source // 2, lax.rem(source, 2))
            remote(place, place, self.send.at[offset], self.recv.at[offset], self.me).wait_recv()


def ffn_forward_body(
    chunk,
    slots,
    gate_hbm,
    up_hbm,
    down_hbm,
    rows_out,
    gate_out,
    up_out,
    act_out,
    back,
    gate,
    up,
    down,
    landing,
    pre_stage,
    act,
    kept,
    passing,
    passed,
    total,
    weight_sem,
    stage_sem,
    act_sem,
    rows_sem,
    local_sem,
    send,
    recv,
    pass_send,
    pass_recv,
    swap_send,
    swap_recv,
    out_send,
    out_recv,
):
    me = lax.axis_index("expert")
    enter(8, me)
    loads = [
        pltpu.make_async_copy(source, target, weight_sem.at[n])
        for n, (source, target) in enumerate(((gate_hbm, gate), (up_hbm, up), (down_hbm, down)))
    ]
    dispatch = Dispatch(me, slots, landing, local_sem.at[0], send, recv, pass_send, pass_recv)
    collect = Collect(
        me, False, kept, passing, passed, total, back, local_sem.at[1], swap_send, swap_recv, out_send, out_recv
    )
    dispatch.start((0, 1, 2))
    for load in loads:
        load.start()
    block = landing.shape[1]
    hidden_units = gate.shape[1]
    chunks = hidden_units // chunk
    half = back.shape[2] // 2

    def stage_copies(chip, part, slot):
        span = pl.ds(pl.multiple_of(chip * block, 16), block)
        columns = pl.ds(pl.multiple_of(part * chunk, 128), chunk)
        return [
            pltpu.make_async_copy(
                pre_stage.at[slot, n], out.at[span, columns], stage_sem.at[slot, n]
            )
            for n, out in enumerate((gate_out, up_out))
        ]

    def act_copy(chip, step):
        span = pl.ds(pl.multiple_of(chip * block, 16), block)
        return pltpu.make_async_copy(act.at[step % 2], act_out.at[span, :], act_sem.at[step % 2])

    def rows_copy(chip, step):
        span = pl.ds(pl.multiple_of(chip * block, 16), block)
        return pltpu.make_async_copy(landing.at[chip], rows_out.at[span, :], rows_sem.at[step])

    for step in range(4):
        if step == 0:
            dispatch.arrive(0)
        chip = dispatch.ready(step)
        rows_copy(chip, step).start()
        if step == 0:
            loads[0].wait()
            loads[1].wait()
        if step >= 2:
            act_copy(chip_order(me // 2, step - 2), step - 2).wait()

        def hidden_part(part, carry, chip=chip, step=step):
            slot = lax.rem(part + step * chunks, 2)
            columns = pl.ds(pl.multiple_of(part * chunk, 128), chunk)

            @pl.when(part + step * chunks >= 2)
            def _():
                for copy in stage_copies(chip, part, slot):
                    copy.wait()

            gated = dot_nn(landing[chip], gate[:, columns])
            raised = dot_nn(landing[chip], up[:, columns])
            pre_stage[slot, 0] = gated.astype(jnp.bfloat16)
            pre_stage[slot, 1] = raised.astype(jnp.bfloat16)
            act[step % 2, :, columns] = (gated * jax.nn.sigmoid(gated) * raised).astype(jnp.bfloat16)
            for copy in stage_copies(chip, part, slot):
                copy.start()
            return carry

        lax.fori_loop(0, chunks, hidden_part, 0)
        act_copy(chip, step).start()
        if step == 0:
            loads[2].wait()
        else:
            collect.settle(step - 1)
        core = collect.core
        width = min(512, half)

        def far_part(part, carry, step=step):
            at = pl.multiple_of((1 - core) * half + part * width, 128)
            product = dot_nt(act[step % 2], down[pl.ds(at, width), :])
            passing[step % 2, :, pl.ds(pl.multiple_of(part * width, 128), width)] = product.astype(jnp.bfloat16)
            return carry

        def near_part(part, carry, step=step):
            at = pl.multiple_of(core * half + part * width, 128)
            product = dot_nt(act[step % 2], down[pl.ds(at, width), :])
            kept[:, pl.ds(pl.multiple_of(part * width, 128), width)] = product
            return carry

        if step >= 2:
            collect.swap(step - 2).wait_send()
        lax.fori_loop(0, half // width, far_part, 0)
        collect.swap(step).start()
        if step in (1, 2):
            dispatch.arrive(step + 1)
        lax.fori_loop(0, half // width, near_part, 0)
        if step == 0:
            dispatch.sent((1, 2))
            dispatch.start((3,))
            dispatch.arrive(1)
    collect.settle(3)
    for step in (2, 3):
        act_copy(chip_order(me // 2, step), step).wait()
    for step in range(4):
        rows_copy(chip_order(me // 2, step), step).wait()
    for slot in range(2):
        for copy in stage_copies(0, 0, slot):
            copy.wait()
    dispatch.sent((0, 3))
    dispatch.passed_on()
    collect.finish()


def ffn_forward(slots, gate_weight, up_weight, down_weight):
    chips, capacity, depth = slots.shape
    hidden_units = gate_weight.shape[1]
    block = 2 * capacity
    chunk = 256 if hidden_units % 256 == 0 else 128
    half = depth // 2
    rows = chips * block
    any_space = pl.BlockSpec(memory_space=pl.ANY)
    bf = jnp.bfloat16
    dma = pltpu.SemaphoreType.DMA
    return pl.pallas_call(
        functools.partial(ffn_forward_body, chunk),
        in_specs=[any_space] * 4,
        out_specs=[any_space] * 5,
        out_shape=[
            jax.ShapeDtypeStruct((rows, depth), bf),
            jax.ShapeDtypeStruct((rows, hidden_units), bf),
            jax.ShapeDtypeStruct((rows, hidden_units), bf),
            jax.ShapeDtypeStruct((rows, hidden_units), bf),
            jax.ShapeDtypeStruct((chips, capacity, depth), bf),
        ],
        scratch_shapes=[
            pltpu.VMEM((depth, hidden_units), bf),
            pltpu.VMEM((depth, hidden_units), bf),
            pltpu.VMEM((depth, hidden_units), bf),
            pltpu.VMEM((chips, block, depth), bf),
            pltpu.VMEM((2, 2, block, chunk), bf),
            pltpu.VMEM((2, block, hidden_units), bf),
            pltpu.VMEM((block, half), jnp.float32),
            pltpu.VMEM((2, block, half), bf),
            pltpu.VMEM((chips, block, half), bf),
            pltpu.VMEM((chips, block, half), bf),
            dma((3,)),
            dma((2, 2)),
            dma((2,)),
            dma((4,)),
            dma((2,)),
            dma((8,)),
            dma((8,)),
            dma((8,)),
            dma((8,)),
            dma((4,)),
            dma((4,)),
            dma((8,)),
            dma((8,)),
        ],
        compiler_params=pltpu.CompilerParams(
            collective_id=1, has_side_effects=True, vmem_limit_bytes=VMEM_BYTES
        ),
        name="ffn_forward",
    )(slots, gate_weight, up_weight, down_weight)


def send_rows_body(slots, rows_out, local_sem, send, recv, pass_send, pass_recv):
    me = lax.axis_index("expert")
    enter(8, me)
    dispatch = Dispatch(me, slots, rows_out, local_sem.at[0], send, recv, pass_send, pass_recv)
    dispatch.start((0, 1, 2, 3))
    for step in range(4):
        dispatch.arrive(step)
    for step in range(4):
        dispatch.ready(step)
    dispatch.sent((0, 1, 2, 3))
    dispatch.passed_on()


def send_rows(slots, collective):
    chips, capacity, depth = slots.shape
    any_space = pl.BlockSpec(memory_space=pl.ANY)
    dma = pltpu.SemaphoreType.DMA
    return pl.pallas_call(
        send_rows_body,
        in_specs=[any_space],
        out_specs=any_space,
        out_shape=jax.ShapeDtypeStruct((chips, 2 * capacity, depth), jnp.bfloat16),
        scratch_shapes=[dma((1,)), dma((8,)), dma((8,)), dma((8,)), dma((8,))],
        compiler_params=pltpu.CompilerParams(collective_id=collective, has_side_effects=True),
        name="send_rows",
    )(slots)


def ffn_backward_body(
    chunk,
    grad_rows,
    gate_in,
    up_in,
    gate_hbm,
    up_hbm,
    down_hbm,
    dgate_out,
    dup_out,
    back,
    gate,
    up,
    down,
    grad,
    pre_stage,
    pair,
    kept,
    passing,
    passed,
    total,
    weight_sem,
    grad_sem,
    stage_sem,
    pair_sem,
    local_sem,
    swap_send,
    swap_recv,
    out_send,
    out_recv,
):
    me = lax.axis_index("expert")
    enter(8, me)
    collect = Collect(
        me, True, kept, passing, passed, total, back, local_sem.at[0], swap_send, swap_recv, out_send, out_recv
    )
    loads = [
        pltpu.make_async_copy(source, target, weight_sem.at[n])
        for n, (source, target) in enumerate(((down_hbm, down), (gate_hbm, gate), (up_hbm, up)))
    ]
    block = grad.shape[1]
    hidden_units = gate.shape[1]
    chunks = hidden_units // chunk
    half = back.shape[2] // 2
    width = min(512, half)

    def span_of(chip):
        return pl.ds(pl.multiple_of(chip * block, 16), block)

    def grad_copy(step):
        return pltpu.make_async_copy(
            grad_rows.at[span_of(collect.block(step)), :], grad.at[step % 2], grad_sem.at[step % 2]
        )

    def stage_copies(chip, part, slot):
        columns = pl.ds(pl.multiple_of(part * chunk, 128), chunk)
        return [
            pltpu.make_async_copy(
                source.at[span_of(chip), columns], pre_stage.at[slot, n], stage_sem.at[slot, n]
            )
            for n, source in enumerate((gate_in, up_in))
        ]

    def pair_copies(chip):
        return [
            pltpu.make_async_copy(pair.at[n], out.at[span_of(chip), :], pair_sem.at[n])
            for n, out in enumerate((dgate_out, dup_out))
        ]

    grad_copy(0).start()
    loads[0].start()
    for copy in stage_copies(collect.block(0), 0, 0):
        copy.start()
    loads[1].start()
    loads[2].start()
    loads[0].wait()
    for step in range(4):
        chip = collect.block(step)
        grad_copy(step).wait()
        if step < 3:
            grad_copy(step + 1).start()
        if step > 0:
            for copy in pair_copies(collect.block(step - 1)):
                copy.wait()

        def hidden_part(part, carry, chip=chip, step=step):
            slot = lax.rem(part, 2)
            columns = pl.ds(pl.multiple_of(part * chunk, 128), chunk)
            for copy in stage_copies(chip, part, slot):
                copy.wait()

            @pl.when(part + 1 < chunks)
            def _():
                for copy in stage_copies(chip, part + 1, 1 - slot):
                    copy.start()

            upstream = dot_nn(grad[step % 2], down[:, columns])
            gated = pre_stage[slot, 0].astype(jnp.float32)
            raised = pre_stage[slot, 1].astype(jnp.float32)
            sigmoid = jax.nn.sigmoid(gated)
            scaled = upstream * sigmoid
            pair[0, :, columns] = (scaled * raised * (1.0 + gated * (1.0 - sigmoid))).astype(jnp.bfloat16)
            pair[1, :, columns] = (scaled * gated).astype(jnp.bfloat16)
            return carry

        lax.fori_loop(0, chunks, hidden_part, 0)
        for copy in pair_copies(chip):
            copy.start()
        if step < 3:
            for copy in stage_copies(collect.block(step + 1), 0, 0):
                copy.start()
        if step == 0:
            loads[1].wait()
            loads[2].wait()
        else:
            collect.settle(step - 1)
        core = collect.core

        def product(at):
            return dot_nt(pair[0], gate[pl.ds(at, width), :]) + dot_nt(pair[1], up[pl.ds(at, width), :])

        def far_part(part, carry, step=step):
            at = pl.multiple_of((1 - core) * half + part * width, 128)
            columns = pl.ds(pl.multiple_of(part * width, 128), width)
            passing[step % 2, :, columns] = product(at).astype(jnp.bfloat16)
            return carry

        def near_part(part, carry, step=step):
            at = pl.multiple_of(core * half + part * width, 128)
            kept[:, pl.ds(pl.multiple_of(part * width, 128), width)] = product(at)
            return carry

        if step >= 2:
            collect.swap(step - 2).wait_send()
        lax.fori_loop(0, half // width, far_part, 0)
        collect.swap(step).start()
        lax.fori_loop(0, half // width, near_part, 0)
    collect.settle(3)
    for copy in pair_copies(collect.block(3)):
        copy.wait()
    collect.finish()


def ffn_backward(grad_rows, gate_pre, up_pre, gate_weight, up_weight, down_weight, capacity):
    rows, depth = grad_rows.shape
    hidden_units = gate_weight.shape[1]
    block = 2 * capacity
    chips = rows // block
    chunk = hidden_units // 2 if hidden_units % 256 == 0 else 128
    half = depth // 2
    any_space = pl.BlockSpec(memory_space=pl.ANY)
    bf = jnp.bfloat16
    dma = pltpu.SemaphoreType.DMA
    return pl.pallas_call(
        functools.partial(ffn_backward_body, chunk),
        in_specs=[any_space] * 6,
        out_specs=[any_space] * 3,
        out_shape=[
            jax.ShapeDtypeStruct((rows, hidden_units), bf),
            jax.ShapeDtypeStruct((rows, hidden_units), bf),
            jax.ShapeDtypeStruct((chips, capacity, depth), bf),
        ],
        scratch_shapes=[
            pltpu.VMEM((depth, hidden_units), bf),
            pltpu.VMEM((depth, hidden_units), bf),
            pltpu.VMEM((depth, hidden_units), bf),
            pltpu.VMEM((2, block, depth), bf),
            pltpu.VMEM((2, 2, block, chunk), bf),
            pltpu.VMEM((2, block, hidden_units), bf),
            pltpu.VMEM((block, half), jnp.float32),
            pltpu.VMEM((2, block, half), bf),
            pltpu.VMEM((chips, block, half), bf),
            pltpu.VMEM((chips, block, half), bf),
            dma((3,)),
            dma((2,)),
            dma((2, 2)),
            dma((2,)),
            dma((1,)),
            dma((4,)),
            dma((4,)),
            dma((8,)),
            dma((8,)),
        ],
        compiler_params=pltpu.CompilerParams(
            collective_id=3, has_side_effects=True, vmem_limit_bytes=VMEM_BYTES
        ),
        name="ffn_backward",
    )(grad_rows, gate_pre, up_pre, gate_weight, up_weight, down_weight)


def attention_send_body(
    scale,
    query_hbm,
    sibling_hbm,
    key_hbm,
    value_hbm,
    out_weight_hbm,
    key_info,
    query_info,
    own_out,
    sibling_out,
    rows_out,
    back,
    lse_ref,
    queries,
    siblings,
    keys_v,
    values_v,
    out_weight,
    bias_ref,
    flipped,
    own_stage,
    sibling_stage,
    arrived,
    rows_stage,
    sending,
    load_sem,
    own_sem,
    sibling_sem,
    rows_sem,
    local_sem,
    swap_send,
    swap_recv,
    out_send,
    out_recv,
):
    me = lax.axis_index("expert")
    chip, core = me // 2, lax.rem(me, 2)
    enter(8, me)
    half = keys_v.shape[1]
    rows = own_stage.shape[1]
    keys = keys_v.shape[0] // GROUPS
    heads = half // HEAD
    capacity = back.shape[1]
    own_columns = pl.ds(pl.multiple_of(core * half, 128), half)
    far_columns = pl.ds(pl.multiple_of((1 - core) * half, 128), half)
    loads = [
        pltpu.make_async_copy(source, target, load_sem.at[n])
        for n, (source, target) in enumerate(
            (
                (value_hbm, values_v),
                (key_hbm, keys_v),
                (query_hbm.at[:, own_columns], queries),
                (sibling_hbm, siblings),
                (out_weight_hbm, out_weight),
            )
        )
    ]
    for load in loads:
        load.start()
    fill_bias(bias_ref, key_info, query_info, keys)
    loads[0].wait()

    def flip(head, carry):
        lanes = pl.ds(pl.multiple_of(head * HEAD, HEAD), HEAD)
        for block in range(GROUPS):
            values = values_v[pl.ds(block * keys, keys), lanes].astype(jnp.float32)
            flipped[head, block] = values.T.astype(jnp.bfloat16)
        return carry

    lax.fori_loop(0, heads, flip, 0)
    for load in loads[1:4]:
        load.wait()

    def group_of(step):
        return chip_order(chip, 3 - step)

    def span_of(step):
        return pl.ds(pl.multiple_of(group_of(step) * rows, 16), rows)

    def own_copy(step):
        return pltpu.make_async_copy(own_stage.at[step], own_out.at[span_of(step), :], own_sem.at[step])

    def sibling_copy(step):
        return pltpu.make_async_copy(
            sibling_stage.at[step], sibling_out.at[span_of(step), :], sibling_sem.at[step]
        )

    def rows_copy(step):
        return pltpu.make_async_copy(
            rows_stage.at[step], rows_out.at[span_of(step), :], rows_sem.at[step]
        )

    def swap(step):
        return remote(
            sibling_stage.at[step], arrived.at[step], swap_send.at[step], swap_recv.at[step], me + 1 - 2 * core
        )

    def outgoing(step, n):
        source = 2 * group_of(step) + n
        offset = lax.rem(source - me + 8, 8)
        return remote(sending.at[step, n], back.at[me], out_send.at[offset], out_recv.at[offset], source)

    def local(step, n):
        return pltpu.make_async_copy(sending.at[step, n], back.at[me], local_sem)

    def each(step, own, other):
        for n in range(2):
            if step < 3:
                other(n)
                continue

            @pl.when(core == n)
            def _(n=n):
                own(n)

            @pl.when(core != n)
            def _(n=n):
                other(n)

    def attend(step):
        group = group_of(step)
        first_block = group * (group + 1) // 2
        span = span_of(step)

        def head_pair(pair, carry):
            lanes = [pl.ds(pl.multiple_of((2 * pair + n) * HEAD, HEAD), HEAD) for n in range(2)]
            parts = [jnp.concatenate([queries[span, lane], siblings[span, lane]], axis=0) for lane in lanes]

            def one(block, state):
                at = pl.multiple_of(block * keys, 16)
                bias = bias_ref[first_block + block]
                result = []
                for n in range(2):
                    top, total, mixed = state[3 * n : 3 * n + 3]
                    scores = dot_nt(keys_v[pl.ds(at, keys), lanes[n]], parts[n]) * scale + bias
                    new_top = jnp.maximum(top, jnp.max(scores, axis=0, keepdims=True))
                    fade = jnp.exp2(top - new_top)
                    probs = jnp.exp2(scores - new_top)
                    total = total * fade + jnp.sum(probs, axis=0, keepdims=True)
                    mixed = mixed * fade + dot_nn(flipped[2 * pair + n, block], probs.astype(jnp.bfloat16))
                    result += [new_top, total, mixed]
                return tuple(result)

            start = (
                jnp.full((1, 2 * rows), -1e30, jnp.float32),
                jnp.zeros((1, 2 * rows), jnp.float32),
                jnp.zeros((HEAD, 2 * rows), jnp.float32),
            ) * 2
            final = lax.fori_loop(0, group + 1, one, start)
            for n in range(2):
                top, total, mixed = final[3 * n : 3 * n + 3]
                lse_ref[2 * pair + n, group] = top + jnp.log2(total)
                result = (mixed / total).T.astype(jnp.bfloat16)
                own_stage[step, :, lanes[n]] = result[:rows]
                sibling_stage[step, :, lanes[n]] = result[rows:]
            return carry

        lax.fori_loop(0, heads // 2, head_pair, 0)
        swap(step).start()
        own_copy(step).start()
        sibling_copy(step).start()

    def settle(step):
        swap(step).wait_recv()
        rows_stage[step, :, own_columns] = own_stage[step]
        rows_stage[step, :, far_columns] = arrived[step]
        rows_copy(step).start()
        width = 512
        for at in range(0, back.shape[2], min(width, back.shape[2])):
            columns = pl.ds(at, min(width, back.shape[2]))
            product = dot_nt(rows_stage[step], out_weight[columns, :])
            for n in range(2):
                part = product[n * capacity : (n + 1) * capacity]
                sending[step, n, :, columns] = part.astype(jnp.bfloat16)
        each(step, lambda n: local(step, n).start(), lambda n: outgoing(step, n).start())

    for step in range(4):
        attend(step)
        if step == 1:
            loads[4].wait()
        if step > 0:
            settle(step - 1)
    settle(3)
    for step in range(4):
        swap(step).wait_send()
        own_copy(step).wait()
        sibling_copy(step).wait()
        rows_copy(step).wait()
        each(step, lambda n, step=step: local(step, n).wait(), lambda n, step=step: outgoing(step, n).wait_send())
    for offset in range(1, 8):
        place = back.at[lax.rem(me + 8 - offset, 8)]
        remote(place, place, out_send.at[offset], out_recv.at[offset], me).wait_recv()


def attention_send(queries, siblings, keys_all, values_all, out_weight, key_info, query_info, capacity):
    total_rows, width = queries.shape
    tokens, half = keys_all.shape
    depth = out_weight.shape[0]
    rows, keys, heads = total_rows // GROUPS, tokens // GROUPS, half // HEAD
    any_space = pl.BlockSpec(memory_space=pl.ANY)
    here = pl.BlockSpec(memory_space=pltpu.VMEM)
    bf = jnp.bfloat16
    dma = pltpu.SemaphoreType.DMA
    return pl.pallas_call(
        functools.partial(attention_send_body, HEAD ** (-0.5) * LOG2E),
        in_specs=[any_space] * 5 + [here] * 2,
        out_specs=[any_space] * 4 + [here],
        out_shape=[
            jax.ShapeDtypeStruct((total_rows, half), bf),
            jax.ShapeDtypeStruct((total_rows, half), bf),
            jax.ShapeDtypeStruct((total_rows, width), bf),
            jax.ShapeDtypeStruct((8, capacity, depth), bf),
            jax.ShapeDtypeStruct((heads, GROUPS, 1, 2 * rows), jnp.float32),
        ],
        scratch_shapes=[
            pltpu.VMEM((total_rows, half), bf),
            pltpu.VMEM((total_rows, half), bf),
            pltpu.VMEM((tokens, half), bf),
            pltpu.VMEM((tokens, half), bf),
            pltpu.VMEM(out_weight.shape, bf),
            pltpu.VMEM((GROUPS * (GROUPS + 1) // 2, keys, 2 * rows), jnp.float32),
            pltpu.VMEM((heads, GROUPS, HEAD, keys), bf),
            pltpu.VMEM((GROUPS, rows, half), bf),
            pltpu.VMEM((GROUPS, rows, half), bf),
            pltpu.VMEM((GROUPS, rows, half), bf),
            pltpu.VMEM((GROUPS, rows, width), bf),
            pltpu.VMEM((GROUPS, 2, capacity, depth), bf),
            dma((5,)),
            dma((GROUPS,)),
            dma((GROUPS,)),
            dma((GROUPS,)),
            dma,
            dma((GROUPS,)),
            dma((GROUPS,)),
            dma((8,)),
            dma((8,)),
        ],
        compiler_params=pltpu.CompilerParams(
            collective_id=4, has_side_effects=True, vmem_limit_bytes=VMEM_BYTES
        ),
        name="attention_send",
    )(queries, siblings, keys_all, values_all, out_weight, key_info, query_info)


D = 2048
HEADS = 16
ATT_EXPERTS = 8
FFN_EXPERTS = 4
TRUNK = 1024
SEG = 96
TREE_LEN = 2176
NODES = 13

epsilon = 1e-06
highest = lax.Precision.HIGHEST
bf16 = jnp.bfloat16
f32 = jnp.float32


def tree_layout(places):
    after_trunk = places - TRUNK
    after_branch = after_trunk - 4 * SEG
    segments = jnp.where(
        places < TRUNK,
        0,
        jnp.where(after_branch < 0, 1 + after_trunk // SEG, 5 + after_branch // SEG),
    )
    depths = jnp.where(
        places < TRUNK,
        places,
        jnp.where(after_branch < 0, TRUNK + after_trunk % SEG, TRUNK + SEG + after_branch % SEG),
    )
    return (segments.astype(jnp.int32), depths.astype(jnp.int32))


def rotation_tables(depths):
    half_size = HEAD // 2
    frequency = 10000.0 ** (-jnp.arange(half_size, dtype=f32) * 2.0 / HEAD)
    angles = depths.astype(f32)[:, None] * frequency[None, :]
    cosine, sine = jnp.cos(angles), jnp.sin(angles)
    cosines = jnp.concatenate([cosine, cosine], axis=1)
    forward = jnp.concatenate([-sine, sine], axis=1)
    return (cosines, forward), (cosines, -forward)


def lookup(table, indices):
    nodes = jnp.arange(NODES, dtype=jnp.int32)
    return jnp.sum(jnp.where(indices[:, None] == nodes[None, :], table[None, :], 0), axis=1)


def running_count(chosen):
    rows = chosen.shape[-1]
    index = jnp.arange(rows, dtype=jnp.int32)
    upto = (index[:, None] <= index[None, :]).astype(bf16)
    return jnp.dot(chosen.astype(bf16), upto, preferred_element_type=f32).astype(jnp.int32) - 1


def source_plan(routes, expert, capacity):
    chosen = jnp.any(routes == expert, axis=2)
    ranking = running_count(chosen)
    slots = jnp.arange(capacity, dtype=jnp.int32)
    return chosen[:, None, :] & (ranking[:, None, :] == slots[None, :, None])


def token_picks(routes, experts, capacity):
    labels = jnp.arange(experts, dtype=jnp.int32)
    hits = routes.T[:, None, :] == labels[None, :, None]
    ranking = running_count(hits[0] | hits[1])
    slots = jnp.arange(capacity, dtype=jnp.int32)
    picks = hits[:, :, None, :] & (ranking[None, :, None, :] == slots[None, None, :, None])
    return picks.astype(bf16), hits[0].T.astype(f32), hits[1].T.astype(f32)


def fill_slots(picks, pair):
    return jnp.einsum("kecr,krd->ecd", picks, pair, preferred_element_type=f32).astype(bf16)


def read_slots(picks, slots):
    return jnp.einsum("kecr,ecd->krd", picks, slots, preferred_element_type=f32)


def gate_values(hidden, router, first, second):
    logits = jnp.dot(hidden.astype(f32), router, precision=highest)
    picked = jnp.stack([jnp.sum(logits * first, axis=1), jnp.sum(logits * second, axis=1)], axis=1)
    return jax.nn.softmax(picked, axis=1)


def router_grads(hidden, router, gates, first, second, picked_grad):
    logit_pick = gates * (picked_grad - jnp.sum(gates * picked_grad, axis=1, keepdims=True))
    logit_grad = logit_pick[:, 0:1] * first + logit_pick[:, 1:2] * second
    router_grad = jnp.dot(hidden.astype(f32).T, logit_grad, precision=highest)
    hidden_grad = jnp.dot(logit_grad, router.T, precision=highest)
    return (router_grad, hidden_grad)


def rms_parts(values):
    inverse = lax.rsqrt(jnp.mean(values * values, axis=-1, keepdims=True) + epsilon)
    return (values * inverse, inverse)


def norm_back(grad_normed, normed, inverse):
    return inverse * (grad_normed - normed * jnp.mean(grad_normed * normed, axis=-1, keepdims=True))


def pair_grads(gates, branches, upstream):
    gate_grad = jnp.stack([jnp.sum(upstream * branches[k], axis=1) for k in range(2)], axis=1)
    scaled = jnp.stack([gates[:, k : k + 1] * upstream for k in range(2)]).astype(bf16)
    return gate_grad, scaled


def exchange(slots):
    return lax.all_to_all(slots, "expert", split_axis=0, concat_axis=0, tiled=True)


def shift(values, step, size, devices):
    moves = [(i, i // size * size + (i % size + step) % size) for i in range(devices)]
    return lax.ppermute(values, "expert", moves)


def group_gather(rows, size, devices):
    return jnp.concatenate([rows] + [shift(rows, step, size, devices) for step in range(1, size)])


def group_reduce(partial, size, devices):
    parts = partial.reshape(size, -1, partial.shape[1])
    total = parts[0].astype(f32)
    for step in range(1, size):
        total = total + shift(parts[step], -step, size, devices).astype(f32)
    return total.astype(bf16)


def spread_over_replicas(block, my_replica, replicas):
    if replicas != 4:
        return lax.all_gather(block, "dp", axis=0), jnp.arange(replicas, dtype=jnp.int32)
    across, along = ([(i, i ^ n) for i in range(4)] for n in (1, 2))
    first, second = lax.ppermute(block, "dp", across), lax.ppermute(block, "dp", along)
    cut = block.shape[0] // 2
    upper, lower = lax.ppermute(second[:cut], "dp", across), lax.ppermute(first[cut:], "dp", along)
    blocks = jnp.stack([block, first, second, jnp.concatenate([upper, lower])])
    return blocks, my_replica ^ jnp.arange(4, dtype=jnp.int32)


def dot_tn(left, right):
    return lax.dot_general(left, right, (((0,), (0,)), ((), ())), preferred_element_type=f32)


def body(
    tokens,
    teacher,
    att_routes,
    ffn_routes,
    parent,
    valid,
    gain_one,
    kv_weight,
    att_router,
    q_weight,
    o_weight,
    gain_two,
    ffn_router,
    gate_weight,
    up_weight,
    down_weight,
):
    row_count = tokens.shape[0]
    devices, replicas = lax.axis_size("expert"), lax.axis_size("dp")
    my_index, my_replica = lax.axis_index("expert"), lax.axis_index("dp")
    core = my_index % 2
    att_copies, ffn_copies = devices // ATT_EXPERTS, devices // FFN_EXPERTS
    att_capacity, ffn_capacity = row_count * 13 // 40, row_count * 13 // 20
    token_count = row_count * devices
    half = HEADS * HEAD // 2
    assert token_count == TREE_LEN * parent.shape[0] and parent.shape[0] == 1
    pair = [(i, i ^ 1) for i in range(devices)]
    own_places = my_index * row_count + jnp.arange(row_count, dtype=jnp.int32)

    x_in = tokens.astype(f32)
    normed_one, inverse_one = rms_parts(x_in)
    hidden = (normed_one * gain_one).astype(bf16)
    weight_rows = kv_weight.shape[0]
    piece = half // replicas
    kv_share = lax.dynamic_slice_in_dim(
        kv_weight.reshape(weight_rows, 4, replicas, piece), my_replica, 1, 2
    )
    kv_share = (
        kv_share.reshape(weight_rows, 2, 2, piece).transpose(0, 2, 1, 3).reshape(weight_rows, 4 * piece)
    )
    kv_gathered = lax.all_gather(kv_share, "expert", axis=0)
    kv_gathered, hidden_sent = lax.optimization_barrier((kv_gathered, hidden))
    hidden_all = lax.all_gather(hidden_sent, "expert", axis=0)
    kv_half = lax.dynamic_slice_in_dim(kv_gathered, core * 2 * piece, 2 * piece, 2).reshape(D, 2 * piece)
    kv_half, routes_sent = lax.optimization_barrier((kv_half, att_routes))
    kv_blocks, block_order = spread_over_replicas(kv_half, my_replica, replicas)
    all_routes = lax.all_gather(routes_sent, "expert", axis=0)

    tree_places = jnp.arange(token_count, dtype=jnp.int32)
    tree_segments, tree_depths = tree_layout(tree_places)
    key_forward, key_backward = rotation_tables(tree_depths)
    key_info = jnp.pad(jnp.stack([tree_places, tree_segments], axis=1), ((0, 0), (0, 6)))
    experts_here = [my_index // att_copies]
    if att_copies == 1:
        experts_here.append(my_index ^ 1)
    plans = [source_plan(all_routes, expert, att_capacity) for expert in experts_here]
    slot_tables, query_parts = [], []
    for plan in plans:
        places = jnp.sum(
            jnp.where(plan, tree_places.reshape(devices, 1, row_count), 0), axis=2
        ).reshape(-1)
        segments, depths = tree_layout(places)
        parents = lookup(parent[0], segments)
        grands = lookup(parent[0], parents)
        query_parts.append(jnp.stack([places, segments, parents, grands]).reshape(4, GROUPS, -1))
        slot_tables.append(rotation_tables(depths))
    query_info = jnp.concatenate(query_parts, axis=2).transpose(1, 0, 2)
    own_plan = plans[0].astype(bf16)
    att_picks, att_first, att_second = token_picks(att_routes, ATT_EXPERTS, att_capacity)
    att_gates = gate_values(hidden, att_router, att_first, att_second)
    ffn_picks, ffn_first, ffn_second = token_picks(ffn_routes, FFN_EXPERTS, ffn_capacity)
    prepared = (key_forward, key_backward, key_info, slot_tables, query_info, own_plan, att_picks, att_gates, ffn_picks)
    hidden_all, prepared = lax.optimization_barrier((hidden_all, prepared))
    key_forward, key_backward, key_info, slot_tables, query_info, own_plan, att_picks, att_gates, ffn_picks = prepared

    queries, query_inputs = project_queries(own_plan, hidden_all, q_weight, slot_tables[0][0])
    keys_all, values_all = project_keys_values(hidden_all, kv_blocks, key_forward, block_order)

    def far_half(values):
        return lax.ppermute(
            lax.dynamic_slice_in_dim(values, (1 - core) * half, half, 1), "expert", pair
        )

    def join_halves(mine, sibling):
        other = lax.ppermute(sibling, "expert", pair)
        return jnp.where(
            core == 0,
            jnp.concatenate([mine, other], axis=1),
            jnp.concatenate([other, mine], axis=1),
        )

    heads = half // HEAD
    query_sets = [queries]
    starts = jnp.zeros((2,), jnp.int32)
    if att_copies == 1:
        query_sets.append(far_half(queries))
        starts = jnp.stack([core * heads, 0]).astype(jnp.int32)
    fused = devices == 8 and att_copies == 1 and ffn_copies == 2 and ffn_capacity % 16 == 0
    if fused:
        *att_outs, att_rows, att_back, lse = attention_send(
            *query_sets, keys_all, values_all, o_weight, key_info, query_info, att_capacity
        )
    else:
        *att_outs, lse = attention_forward(
            query_sets, starts // 2, keys_all, values_all, key_info, query_info, heads
        )
        att_rows = join_halves(*att_outs) if att_copies == 1 else att_outs[0]
        att_partial = lax.dot_general(
            att_rows, o_weight, (((1,), (1,)), ((), ())), preferred_element_type=f32
        ).astype(bf16)
        att_back = exchange(att_partial.reshape(devices, att_capacity, D))
    if att_copies > 1:
        att_back = (
            att_back.astype(f32).reshape(ATT_EXPERTS, att_copies, att_capacity, D).sum(axis=1).astype(bf16)
        )
    att_branches = read_slots(att_picks, att_back)
    x_mid = x_in + att_gates[:, 0:1] * att_branches[0] + att_gates[:, 1:2] * att_branches[1]

    normed_two, inverse_two = rms_parts(x_mid)
    hidden_two = (normed_two * gain_two).astype(bf16)
    ffn_gates = gate_values(hidden_two, ffn_router, ffn_first, ffn_second)

    def to_experts(slots):
        rows = exchange(slots.reshape(devices, ffn_capacity // ffn_copies, D))
        return group_gather(rows.reshape(-1, D), ffn_copies, devices)

    def to_tokens(partial):
        rows = group_reduce(partial.astype(bf16), ffn_copies, devices)
        back = exchange(rows.reshape(devices, ffn_capacity // ffn_copies, D))
        return read_slots(ffn_picks, back.reshape(FFN_EXPERTS, ffn_capacity, D))

    ffn_slots = jnp.einsum(
        "ecr,rd->ecd", ffn_picks[0] + ffn_picks[1], hidden_two, preferred_element_type=f32
    ).astype(bf16)
    if fused:
        ffn_inputs, gate_pre, up_pre, activated, ffn_back = ffn_forward(
            ffn_slots, gate_weight, up_weight, down_weight
        )
        ffn_branches = read_slots(ffn_picks, ffn_back)
    else:
        ffn_inputs = to_experts(ffn_slots)
        gate_pre = jnp.dot(ffn_inputs, gate_weight, preferred_element_type=f32)
        up_pre = jnp.dot(ffn_inputs, up_weight, preferred_element_type=f32)
        sigmoid_gate = jax.nn.sigmoid(gate_pre)
        silu_gate = gate_pre * sigmoid_gate
        activated = (silu_gate * up_pre).astype(bf16)
        ffn_branches = to_tokens(
            lax.dot_general(
                activated, down_weight, (((1,), (1,)), ((), ())), preferred_element_type=f32
            )
        )
    result = x_mid + ffn_gates[:, 0:1] * ffn_branches[0] + ffn_gates[:, 1:2] * ffn_branches[1]

    tree_global = my_replica * parent.shape[0] + own_places // TREE_LEN
    tree_labels = jnp.arange(valid.shape[0], dtype=jnp.int32)
    limits = jnp.sum(
        jnp.where(tree_global[:, None] == tree_labels[None, :], valid[None, :], 0), axis=1
    )
    counted = own_places % TREE_LEN < limits
    loss_factor = valid.shape[0] * TREE_LEN / jnp.sum(valid).astype(f32)
    grad_result = jnp.where(counted[:, None], (result - teacher.astype(f32)) * loss_factor, 0.0)

    ffn_gate_grad, ffn_scaled = pair_grads(ffn_gates, ffn_branches, grad_result)
    ffn_grad_slots = fill_slots(ffn_picks, ffn_scaled)
    if fused:
        grad_ffn_out = send_rows(ffn_grad_slots, 2).reshape(-1, D)
    else:
        grad_ffn_out = to_experts(ffn_grad_slots)
    grad_down = dot_tn(grad_ffn_out, activated).astype(bf16)
    grad_ffn_out, grad_down = lax.optimization_barrier((grad_ffn_out, grad_down))
    summed_down = lax.psum_scatter(grad_down, "dp", scatter_dimension=0, tiled=True)
    if fused:
        grad_gate_pre, grad_up_pre, ffn_grad_back = ffn_backward(
            grad_ffn_out, gate_pre, up_pre, gate_weight, up_weight, down_weight, ffn_capacity
        )
        grad_gate = dot_tn(ffn_inputs, grad_gate_pre).astype(bf16)
        ffn_grad_back, grad_gate = lax.optimization_barrier((ffn_grad_back, grad_gate))
        ffn_grad_pair = read_slots(ffn_picks, ffn_grad_back)
    else:
        grad_activated = jnp.dot(grad_ffn_out, down_weight, preferred_element_type=f32)
        grad_gate_pre = (
            grad_activated * up_pre * sigmoid_gate * (1.0 + gate_pre * (1.0 - sigmoid_gate))
        ).astype(bf16)
        grad_up_pre = (grad_activated * silu_gate).astype(bf16)
        grad_ffn_in = lax.dot_general(
            grad_gate_pre, gate_weight, (((1,), (1,)), ((), ())), preferred_element_type=f32
        ) + lax.dot_general(
            grad_up_pre, up_weight, (((1,), (1,)), ((), ())), preferred_element_type=f32
        )
        grad_gate = dot_tn(ffn_inputs, grad_gate_pre).astype(bf16)
        ffn_grad_pair = to_tokens(grad_ffn_in)
    summed_gate = lax.psum_scatter(grad_gate, "dp", scatter_dimension=0, tiled=True)
    grad_ffn_router, hidden_two_extra = router_grads(
        hidden_two, ffn_router, ffn_gates, ffn_first, ffn_second, ffn_gate_grad
    )
    grad_hidden_two = ffn_grad_pair[0] + ffn_grad_pair[1] + hidden_two_extra
    grad_gain_two = jnp.sum(grad_hidden_two * normed_two, axis=0)
    grad_mid = grad_result + norm_back(grad_hidden_two * gain_two, normed_two, inverse_two)

    att_gate_grad, att_scaled = pair_grads(att_gates, att_branches, grad_mid)
    att_slots = fill_slots(att_picks, att_scaled)
    if att_copies > 1:
        att_slots = jnp.repeat(att_slots, att_copies, axis=0)
    att_slots, summed_down, ffn_inputs = lax.optimization_barrier((att_slots, summed_down, ffn_inputs))
    grad_up = dot_tn(ffn_inputs, grad_up_pre).astype(bf16)
    summed_up = lax.psum_scatter(grad_up, "dp", scatter_dimension=0, tiled=True)
    grad_att_out = exchange(att_slots).reshape(-1, D)
    grad_att_out, grad_up = lax.optimization_barrier((grad_att_out, grad_up))
    grad_heads = jnp.dot(grad_att_out, o_weight, preferred_element_type=f32).astype(bf16)
    grad_heads, grad_att_out = lax.optimization_barrier((grad_heads, grad_att_out))
    grad_sets = [grad_heads]
    if att_copies == 1:
        grad_sets.append(far_half(grad_heads))
    grad_o = dot_tn(grad_att_out, att_rows).astype(bf16)
    summed_o = lax.psum_scatter(grad_o, "dp", scatter_dimension=0, tiled=True)
    grad_sets[-1], summed_gate, grad_o = lax.optimization_barrier((grad_sets[-1], summed_gate, grad_o))
    *grad_queries, grad_keys, grad_values = attention_backward(
        query_sets,
        starts,
        grad_sets,
        att_outs,
        keys_all,
        values_all,
        lse,
        key_info,
        query_info,
        key_backward,
        [tables[1] for tables in slot_tables],
        heads,
    )
    grad_query_pre = join_halves(*grad_queries) if att_copies == 1 else grad_queries[0]
    grad_query_in = lax.dot_general(
        grad_query_pre, q_weight, (((1,), (1,)), ((), ())), preferred_element_type=f32
    ).astype(bf16)
    merged = merge_hidden_grads(
        own_plan.transpose(0, 2, 1),
        grad_query_in.reshape(devices, att_capacity, D),
        grad_keys,
        grad_values,
        kv_blocks,
        block_order,
    ).reshape(devices // 2, 2, row_count, D)
    kept = lax.dynamic_index_in_dim(merged, core, 1, keepdims=False)
    passed = lax.ppermute(
        lax.dynamic_index_in_dim(merged, 1 - core, 1, keepdims=False), "expert", pair
    )
    chip_sum = (kept.astype(f32) + passed.astype(f32)).astype(bf16)
    chip_sum, hidden_rows, query_inputs, summed_up = lax.optimization_barrier(
        (chip_sum, hidden_all.reshape(token_count, D), query_inputs, summed_up)
    )
    grad_kv = jnp.concatenate(
        [dot_tn(hidden_rows, grad_keys).astype(bf16), dot_tn(hidden_rows, grad_values).astype(bf16)], axis=1
    )
    summed_kv = lax.psum_scatter(grad_kv, "dp", scatter_dimension=0, tiled=True)
    grad_q = dot_tn(query_inputs, grad_query_pre).astype(bf16)
    summed_q = lax.psum_scatter(grad_q, "dp", scatter_dimension=0, tiled=True)
    same_core = [[2 * i + c for i in range(devices // 2)] for c in range(2)]
    arrived = lax.all_to_all(
        chip_sum, "expert", split_axis=0, concat_axis=0, axis_index_groups=same_core, tiled=True
    )
    arrived, grad_kv, grad_q, summed_o = lax.optimization_barrier((arrived, grad_kv, grad_q, summed_o))
    grad_att_router, hidden_one_extra = router_grads(
        hidden, att_router, att_gates, att_first, att_second, att_gate_grad
    )
    grad_hidden_one = jnp.sum(arrived.astype(f32), axis=0) + hidden_one_extra
    grad_gain_one = jnp.sum(grad_hidden_one * normed_one, axis=0)
    grad_input = grad_mid + norm_back(grad_hidden_one * gain_one, normed_one, inverse_one)

    everyone = devices * replicas
    smalls = [grad_gain_one, grad_gain_two, grad_att_router, grad_ffn_router]
    packed = jnp.concatenate([small.reshape(everyone, -1) for small in smalls], axis=1)
    own_smalls = jnp.sum(
        lax.all_to_all(packed, ("dp", "expert"), split_axis=0, concat_axis=0, tiled=True), axis=0
    )
    share = D // everyone
    shared_gain_one = own_smalls[:share]
    shared_gain_two = own_smalls[share : 2 * share]
    shared_att_router = own_smalls[2 * share : (2 + ATT_EXPERTS) * share].reshape(share, ATT_EXPERTS)
    shared_ffn_router = own_smalls[(2 + ATT_EXPERTS) * share :].reshape(share, FFN_EXPERTS)

    kv_rows = exchange(summed_kv.reshape(devices, -1, 2 * half))
    kv_sum = jnp.sum(kv_rows.astype(f32).reshape(devices // 2, 2, -1, 2 * half), axis=0)
    shared_kv = jnp.concatenate(
        [kv_sum[n, :, m * half : (m + 1) * half] for m in range(2) for n in range(2)], axis=1
    )

    return (
        result.astype(bf16),
        grad_input.astype(bf16),
        shared_gain_one,
        shared_kv,
        shared_att_router,
        summed_q.astype(f32),
        summed_o.astype(f32),
        shared_gain_two,
        shared_ffn_router,
        summed_gate.astype(f32),
        summed_up.astype(f32),
        summed_down.astype(f32),
    )


def solution(mesh):
    in_specs = (
        P(("dp", "expert"), None),
        P(("dp", "expert"), None),
        P(("dp", "expert"), None),
        P(("dp", "expert"), None),
        P("dp", None),
        P(),
        P(),
        P("expert", None),
        P(),
        P(None, "expert"),
        P(None, "expert"),
        P(),
        P(),
        P(None, "expert"),
        P(None, "expert"),
        P(None, "expert"),
    )
    out_specs = (
        P(("dp", "expert"), None),
        P(("dp", "expert"), None),
        P(("dp", "expert")),
        P(("dp", "expert"), None),
        P(("dp", "expert"), None),
        P("dp", "expert"),
        P("dp", "expert"),
        P(("dp", "expert")),
        P(("dp", "expert"), None),
        P("dp", "expert"),
        P("dp", "expert"),
        P("dp", "expert"),
    )
    return jax.shard_map(body, mesh=mesh, in_specs=in_specs, out_specs=out_specs, check_vma=False)
```

```python
import functools
import jax
import jax.numpy as jnp
from jax import lax
from jax.experimental import pallas as pl
from jax.experimental.pallas import tpu as pltpu
from jax.sharding import PartitionSpec as P

HEAD = 128
GROUPS = 4
LOG2E = 1.4426950408889634
VMEM_BYTES = 60 * 1024 * 1024


def dot_nt(left, right):
    return lax.dot_general(left, right, (((1,), (1,)), ((), ())), preferred_element_type=jnp.float32)


def dot_nn(left, right):
    return jnp.dot(left, right, preferred_element_type=jnp.float32)


def spin(values, cosine, sine):
    return values * cosine + pltpu.roll(values, HEAD // 2, 1) * sine


def fill_bias(bias_ref, key_ref, query_ref, keys):
    for group in range(GROUPS):
        place = query_ref[group, 0:1, :]
        own, parent, grand = (query_ref[group, 1 + n : 2 + n, :] for n in range(3))

        def one(block, carry, group=group, place=place, own=own, parent=parent, grand=grand):
            at = pl.multiple_of(block * keys, 16)
            key_place = key_ref[pl.ds(at, keys), 0:1]
            key_segment = key_ref[pl.ds(at, keys), 1:2]
            related = (key_segment == own) | (key_segment == parent) | (key_segment == grand)
            allowed = related & (key_place <= place)
            bias_ref[group * (group + 1) // 2 + block] = jnp.where(allowed, 0.0, -1e30)
            return carry

        lax.fori_loop(0, group + 1, one, 0)


def group_rows(refs, group, rows, lanes):
    parts = [ref[pl.ds(group * rows, rows), lanes] for ref in refs]
    return parts[0] if len(parts) == 1 else jnp.concatenate(parts, axis=0)


def attention_forward_body(sets, step_heads, rows, keys, scale, first_ref, *refs):
    query_refs = refs[:sets]
    key_ref, value_ref, key_info, query_info = refs[sets : sets + 4]
    out_refs = refs[sets + 4 : 2 * sets + 4]
    lse_ref, bias_ref, flipped_ref = refs[2 * sets + 4 :]
    wide = sets * rows

    @pl.when(pl.program_id(0) == 0)
    def _():
        fill_bias(bias_ref, key_info, query_info, keys)

    for head in range(step_heads):
        lanes = pl.ds(head * HEAD, HEAD)
        for block in range(GROUPS):
            values = value_ref[pl.ds(block * keys, keys), lanes].astype(jnp.float32)
            flipped_ref[head, block] = values.T.astype(jnp.bfloat16)
    for group in range(GROUPS):
        queries = [
            group_rows(query_refs, group, rows, pl.ds(head * HEAD, HEAD)) for head in range(step_heads)
        ]

        def one(block, carry, group=group, queries=queries):
            at = pl.multiple_of(block * keys, 16)
            bias = bias_ref[group * (group + 1) // 2 + block]
            result = []
            for head in range(step_heads):
                top, total, mixed = carry[3 * head : 3 * head + 3]
                scores = dot_nt(key_ref[pl.ds(at, keys), pl.ds(head * HEAD, HEAD)], queries[head])
                scores = scores * scale + bias
                new_top = jnp.maximum(top, jnp.max(scores, axis=0, keepdims=True))
                fade = jnp.exp2(top - new_top)
                parts = jnp.exp2(scores - new_top)
                total = total * fade + jnp.sum(parts, axis=0, keepdims=True)
                mixed = mixed * fade + dot_nn(flipped_ref[head, block], parts.astype(jnp.bfloat16))
                result += [new_top, total, mixed]
            return tuple(result)

        start = (
            jnp.full((1, wide), -1e30, jnp.float32),
            jnp.zeros((1, wide), jnp.float32),
            jnp.zeros((HEAD, wide), jnp.float32),
        ) * step_heads
        final = lax.fori_loop(0, group + 1, one, start)
        for head in range(step_heads):
            top, total, mixed = final[3 * head : 3 * head + 3]
            lse_ref[head, group] = top + jnp.log2(total)
            rows_out = (mixed / total).T.astype(jnp.bfloat16)
            for n, ref in enumerate(out_refs):
                ref[pl.ds(group * rows, rows), pl.ds(head * HEAD, HEAD)] = rows_out[
                    n * rows : (n + 1) * rows
                ]


def attention_backward_body(sets, step_heads, rows, keys, scale, first_ref, *refs):
    query_refs, grad_refs, out_refs = (refs[n * sets : (n + 1) * sets] for n in range(3))
    key_ref, value_ref, lse_ref, key_info, query_info = refs[3 * sets : 3 * sets + 5]
    key_cos, key_sin = refs[3 * sets + 5 : 3 * sets + 7]
    table_refs = refs[3 * sets + 7 : 5 * sets + 7]
    rest = refs[5 * sets + 7 :]
    dq_refs = rest[:sets]
    dkv_ref, bias_ref, flipped_ref, dk_acc, dv_acc = rest[sets:]
    half = dkv_ref.shape[1] // 2
    softmax_scale = scale / LOG2E

    @pl.when(pl.program_id(0) == 0)
    def _():
        fill_bias(bias_ref, key_info, query_info, keys)

    dk_acc[...] = jnp.zeros_like(dk_acc)
    dv_acc[...] = jnp.zeros_like(dv_acc)
    for head in range(step_heads):
        lanes = pl.ds(head * HEAD, HEAD)
        for block in range(GROUPS):
            values = key_ref[pl.ds(block * keys, keys), lanes].astype(jnp.float32)
            flipped_ref[head, block] = values.T.astype(jnp.bfloat16)
    for group in range(GROUPS):
        queries, grads, centres, tops = [], [], [], []
        for head in range(step_heads):
            lanes = pl.ds(head * HEAD, HEAD)
            queries.append(group_rows(query_refs, group, rows, lanes))
            grad = group_rows(grad_refs, group, rows, lanes)
            out = group_rows(out_refs, group, rows, lanes)
            product = grad.astype(jnp.float32) * out.astype(jnp.float32)
            centres.append(jnp.sum(product.T, axis=0, keepdims=True))
            grads.append(grad)
            tops.append(lse_ref[head, group])

        def one(block, carry, group=group, queries=queries, grads=grads, centres=centres, tops=tops):
            at = pl.multiple_of(block * keys, 16)
            bias = bias_ref[group * (group + 1) // 2 + block]
            result = []
            for head in range(step_heads):
                lanes = pl.ds(head * HEAD, HEAD)
                key_rows = key_ref[pl.ds(at, keys), lanes]
                scores = dot_nt(key_rows, queries[head])
                probs = jnp.exp2(scores * scale + (bias - tops[head]))
                grad_probs = dot_nt(value_ref[pl.ds(at, keys), lanes], grads[head])
                grad_scores = (probs * (grad_probs - centres[head])).astype(jnp.bfloat16)
                dv_acc[pl.ds(at, keys), lanes] += dot_nn(probs.astype(jnp.bfloat16), grads[head])
                dk_acc[pl.ds(at, keys), lanes] += dot_nn(grad_scores, queries[head])
                result.append(carry[head] + dot_nn(flipped_ref[head, block], grad_scores))
            return tuple(result)

        start = (jnp.zeros((HEAD, sets * rows), jnp.float32),) * step_heads
        final = lax.fori_loop(0, group + 1, one, start)
        for head in range(step_heads):
            dq = final[head].T * softmax_scale
            for n, ref in enumerate(dq_refs):
                span = pl.ds(group * rows, rows)
                turned = spin(
                    dq[n * rows : (n + 1) * rows], table_refs[2 * n][span, :], table_refs[2 * n + 1][span, :]
                )
                ref[span, pl.ds(head * HEAD, HEAD)] = turned.astype(jnp.bfloat16)
    for head in range(step_heads):
        lanes = pl.ds(head * HEAD, HEAD)
        first_lane = pl.multiple_of((pl.program_id(0) * step_heads + head) * HEAD, HEAD)
        for block in range(GROUPS):
            span = pl.ds(block * keys, keys)
            turned = spin(dk_acc[span, lanes] * softmax_scale, key_cos[span, :], key_sin[span, :])
            dkv_ref[span, pl.ds(first_lane, HEAD)] = turned.astype(jnp.bfloat16)
            dkv_ref[span, pl.ds(half + first_lane, HEAD)] = dv_acc[span, lanes].astype(jnp.bfloat16)


def whole_block(shape):
    return pl.BlockSpec(shape, lambda h, first: (0,) * len(shape))


def attention_forward(queries, starts, keys_all, values_all, key_info, query_info, heads):
    sets, total_rows, tokens = len(queries), queries[0].shape[0], keys_all.shape[0]
    rows, keys = total_rows // GROUPS, tokens // GROUPS
    step_heads = 2
    wide = step_heads * HEAD
    scale = HEAD ** (-0.5) * LOG2E
    query_specs = [
        pl.BlockSpec((total_rows, wide), lambda h, first, n=n: (0, first[n] + h)) for n in range(sets)
    ]
    plain = pl.BlockSpec((total_rows, wide), lambda h, first: (0, h))
    side = pl.BlockSpec((tokens, wide), lambda h, first: (0, h))
    return pl.pallas_call(
        functools.partial(attention_forward_body, sets, step_heads, rows, keys, scale),
        grid_spec=pltpu.PrefetchScalarGridSpec(
            num_scalar_prefetch=1,
            grid=(heads // step_heads,),
            in_specs=query_specs
            + [side, side, whole_block(key_info.shape), whole_block(query_info.shape)],
            out_specs=[plain] * sets
            + [pl.BlockSpec((step_heads, GROUPS, 1, sets * rows), lambda h, first: (h, 0, 0, 0))],
            scratch_shapes=[
                pltpu.VMEM((GROUPS * (GROUPS + 1) // 2, keys, sets * rows), jnp.float32),
                pltpu.VMEM((step_heads, GROUPS, HEAD, keys), jnp.bfloat16),
            ],
        ),
        out_shape=[jax.ShapeDtypeStruct((total_rows, heads * HEAD), jnp.bfloat16)] * sets
        + [jax.ShapeDtypeStruct((heads, GROUPS, 1, sets * rows), jnp.float32)],
        compiler_params=pltpu.CompilerParams(vmem_limit_bytes=VMEM_BYTES),
        name="attention_forward",
    )(starts, *queries, keys_all, values_all, key_info, query_info)


def attention_backward(
    queries, starts, grads, outs, keys_all, values_all, lse, key_info, query_info, key_tables, row_tables, heads
):
    sets, total_rows, tokens = len(queries), queries[0].shape[0], keys_all.shape[0]
    rows, keys = total_rows // GROUPS, tokens // GROUPS
    step_heads = 1
    wide = step_heads * HEAD
    scale = HEAD ** (-0.5) * LOG2E
    shifted = [
        pl.BlockSpec((total_rows, wide), lambda h, first, n=n: (0, first[n] + h)) for n in range(sets)
    ]
    plain = pl.BlockSpec((total_rows, wide), lambda h, first: (0, h))
    side = pl.BlockSpec((tokens, wide), lambda h, first: (0, h))
    return pl.pallas_call(
        functools.partial(attention_backward_body, sets, step_heads, rows, keys, scale),
        grid_spec=pltpu.PrefetchScalarGridSpec(
            num_scalar_prefetch=1,
            grid=(heads // step_heads,),
            in_specs=shifted
            + shifted
            + [plain] * sets
            + [
                side,
                side,
                pl.BlockSpec((step_heads, GROUPS, 1, sets * rows), lambda h, first: (h, 0, 0, 0)),
                whole_block(key_info.shape),
                whole_block(query_info.shape),
                whole_block((tokens, HEAD)),
                whole_block((tokens, HEAD)),
            ]
            + [whole_block((total_rows, HEAD))] * (2 * sets),
            out_specs=[plain] * sets + [whole_block((tokens, 2 * heads * HEAD))],
            scratch_shapes=[
                pltpu.VMEM((GROUPS * (GROUPS + 1) // 2, keys, sets * rows), jnp.float32),
                pltpu.VMEM((step_heads, GROUPS, HEAD, keys), jnp.bfloat16),
                pltpu.VMEM((tokens, wide), jnp.float32),
                pltpu.VMEM((tokens, wide), jnp.float32),
            ],
        ),
        out_shape=[jax.ShapeDtypeStruct((total_rows, heads * HEAD), jnp.bfloat16)] * sets
        + [jax.ShapeDtypeStruct((tokens, 2 * heads * HEAD), jnp.bfloat16)],
        compiler_params=pltpu.CompilerParams(vmem_limit_bytes=VMEM_BYTES),
        name="attention_backward",
    )(
        starts,
        *queries,
        *grads,
        *outs,
        keys_all,
        values_all,
        lse,
        key_info,
        query_info,
        *key_tables,
        *[table for pair in row_tables for table in pair],
    )


def project_body(plan_ref, hidden_ref, weight_ref, cos_ref, sin_ref, out_ref, x_ref):
    sources, capacity = plan_ref.shape[0], plan_ref.shape[1]
    bundle = max(1, sources * capacity // GROUPS // capacity)
    tile = bundle * capacity

    @pl.when(pl.program_id(0) == 0)
    def _():
        for group in range(sources // bundle):
            parts = [
                dot_nn(plan_ref[group * bundle + n], hidden_ref[group * bundle + n]) for n in range(bundle)
            ]
            x_ref[pl.ds(group * tile, tile), :] = jnp.concatenate(parts, axis=0).astype(jnp.bfloat16)

    for at in range(0, x_ref.shape[0], tile):
        span = pl.ds(at, tile)
        product = dot_nn(x_ref[span, :], weight_ref[...])
        for lane in range(0, out_ref.shape[1], HEAD):
            turned = spin(product[:, lane : lane + HEAD], cos_ref[span, :], sin_ref[span, :])
            out_ref[span, lane : lane + HEAD] = turned.astype(jnp.bfloat16)


def project_queries(plan, hidden, weight, tables):
    sources, capacity, row_count = plan.shape
    depth, columns = weight.shape
    rows = sources * capacity
    block = 512
    return pl.pallas_call(
        project_body,
        grid=(columns // block,),
        in_specs=[
            pl.BlockSpec((sources, capacity, row_count), lambda j: (0, 0, 0)),
            pl.BlockSpec((sources, row_count, depth), lambda j: (0, 0, 0)),
            pl.BlockSpec((depth, block), lambda j: (0, j)),
            pl.BlockSpec((rows, HEAD), lambda j: (0, 0)),
            pl.BlockSpec((rows, HEAD), lambda j: (0, 0)),
        ],
        out_specs=[
            pl.BlockSpec((rows, block), lambda j: (0, j)),
            pl.BlockSpec((rows, depth), lambda j: (0, 0)),
        ],
        out_shape=[
            jax.ShapeDtypeStruct((rows, columns), jnp.bfloat16),
            jax.ShapeDtypeStruct((rows, depth), jnp.bfloat16),
        ],
        compiler_params=pltpu.CompilerParams(vmem_limit_bytes=VMEM_BYTES),
        name="project_queries",
    )(plan, hidden, weight, *tables)


def keys_values_body(half, order_ref, x_ref, weight_ref, cos_ref, sin_ref, key_ref, value_ref):
    rows = x_ref.shape[1]
    for source in range(x_ref.shape[0]):
        span = pl.ds(source * rows, rows)
        product = dot_nn(x_ref[source], weight_ref[0])
        for lane in range(0, half, HEAD):
            turned = spin(product[:, lane : lane + HEAD], cos_ref[span, :], sin_ref[span, :])
            key_ref[span, lane : lane + HEAD] = turned.astype(jnp.bfloat16)
        value_ref[span, :] = product[:, half:].astype(jnp.bfloat16)


def project_keys_values(hidden, weights, tables, order):
    sources, rows, unused = hidden.shape
    parts, depth, columns = weights.shape
    half, tokens = columns // 2, sources * rows
    return pl.pallas_call(
        functools.partial(keys_values_body, half),
        grid_spec=pltpu.PrefetchScalarGridSpec(
            num_scalar_prefetch=1,
            grid=(parts,),
            in_specs=[
                pl.BlockSpec((sources, rows, depth), lambda j, order: (0, 0, 0)),
                pl.BlockSpec((1, depth, columns), lambda j, order: (j, 0, 0)),
                pl.BlockSpec((tokens, HEAD), lambda j, order: (0, 0)),
                pl.BlockSpec((tokens, HEAD), lambda j, order: (0, 0)),
            ],
            out_specs=[pl.BlockSpec((tokens, half), lambda j, order: (0, order[j]))] * 2,
        ),
        out_shape=[jax.ShapeDtypeStruct((tokens, parts * half), jnp.bfloat16)] * 2,
        compiler_params=pltpu.CompilerParams(vmem_limit_bytes=VMEM_BYTES),
        name="project_keys_values",
    )(order, hidden, weights, *tables)


def merge_body(tile, order_ref, plan_ref, slots_ref, dk_ref, dv_ref, weight_ref, out_ref, acc_ref):
    part = pl.program_id(1)
    sources, rows = plan_ref.shape[0], plan_ref.shape[1]
    ck = dk_ref.shape[1]

    @pl.when(part == 0)
    def _():
        for source in range(sources):
            acc_ref[pl.ds(source * rows, rows), :] = dot_nn(plan_ref[source], slots_ref[source])

    last = part == pl.num_programs(1) - 1
    for at in range(0, acc_ref.shape[0], tile):
        span = pl.ds(at, tile)
        acc_ref[span, :] += dot_nt(dk_ref[span, :], weight_ref[0, :, :ck]) + dot_nt(
            dv_ref[span, :], weight_ref[0, :, ck:]
        )

    @pl.when(last)
    def _():
        out_ref[...] = acc_ref[...].astype(jnp.bfloat16)


def merge_hidden_grads(plan, slots, grads, weights, order):
    sources, rows, capacity = plan.shape
    parts, depth, columns = weights.shape
    ck, tokens = columns // 2, sources * rows
    wide = depth // 2
    return pl.pallas_call(
        functools.partial(merge_body, tokens // GROUPS),
        grid_spec=pltpu.PrefetchScalarGridSpec(
            num_scalar_prefetch=1,
            grid=(2, parts),
            in_specs=[
                pl.BlockSpec((sources, rows, capacity), lambda i, j, order: (0, 0, 0)),
                pl.BlockSpec((sources, capacity, wide), lambda i, j, order: (0, 0, i)),
                pl.BlockSpec((tokens, ck), lambda i, j, order: (0, order[j])),
                pl.BlockSpec((tokens, ck), lambda i, j, order: (0, parts + order[j])),
                pl.BlockSpec((1, wide, columns), lambda i, j, order: (j, i, 0)),
            ],
            out_specs=pl.BlockSpec((tokens, wide), lambda i, j, order: (0, i)),
            scratch_shapes=[pltpu.VMEM((tokens, wide), jnp.float32)],
        ),
        out_shape=jax.ShapeDtypeStruct((tokens, depth), jnp.bfloat16),
        compiler_params=pltpu.CompilerParams(vmem_limit_bytes=VMEM_BYTES),
        name="merge_hidden_grads",
    )(order, plan, slots, grads, grads, weights)


def mesh_device(index):
    return {"expert": index}


def chip_order(chip, step):
    flip = chip // 2
    near = chip + flip * (3 - 2 * chip)
    place = step + near * (1 - 2 * step) if step < 2 else step
    return place + flip * (3 - 2 * place)


def far_order(chip, step):
    return chip_order(chip, 3 - step)


def is_middle(chip):
    flip = chip // 2
    return chip + flip * (3 - 2 * chip)


def crossing_order(chip, step):
    end, middle = chip_order(chip, step), chip_order(chip, (2, 3, 1, 0)[step])
    return end + is_middle(chip) * (middle - end)


def enter(devices, me):
    barrier = pltpu.get_barrier_semaphore()
    for step in range(1, devices):
        pl.semaphore_signal(
            barrier,
            inc=1,
            device_id=mesh_device(lax.rem(me + step, devices)),
            device_id_type=pl.DeviceIdType.MESH,
        )
    pl.semaphore_wait(barrier, devices - 1)


def remote(source, target, send, recv, device):
    return pltpu.make_async_remote_copy(
        src_ref=source,
        dst_ref=target,
        send_sem=send,
        recv_sem=recv,
        device_id=mesh_device(device),
        device_id_type=pl.DeviceIdType.MESH,
    )


class Dispatch:
    def __init__(self, me, order, slots, landing, local_sem, send, recv, pass_send, pass_recv):
        self.me, self.chip, self.core, self.order = me, me // 2, lax.rem(me, 2), order
        self.slots, self.landing = slots, landing
        self.local_sem, self.send, self.recv = local_sem, send, recv
        self.pass_send, self.pass_recv = pass_send, pass_recv
        self.rows, self.half = slots.shape[1], slots.shape[2] // 2

    def columns(self, core):
        return pl.ds(pl.multiple_of(core * self.half, 128), self.half)

    def place(self, source, core):
        rows = pl.ds(pl.multiple_of(lax.rem(source, 2) * self.rows, 16), self.rows)
        return self.landing.at[source // 2, rows, self.columns(core)]

    def direct(self, target):
        core = lax.rem(target, 2)
        offset = lax.rem(target - self.me + 8, 8)
        return remote(
            self.slots.at[target // 2, :, self.columns(core)],
            self.place(self.me, core),
            self.send.at[offset],
            self.recv.at[offset],
            target,
        )

    def sends(self, step):
        chip = chip_order(self.chip, step)
        targets = [2 * chip, 2 * chip + 1] if step else [self.me + 1 - 2 * self.core]
        return [self.direct(target) for target in targets]

    def local(self):
        return pltpu.make_async_copy(
            self.slots.at[self.chip, :, self.columns(self.core)],
            self.place(self.me, self.core),
            self.local_sem,
        )

    def start_local(self):
        self.local().start()

    def start(self, steps):
        for step in steps:
            for copy in self.sends(step):
                copy.start()

    def sent(self, steps):
        for step in steps:
            for copy in self.sends(step):
                copy.wait_send()

    def pass_on(self, source):
        place = self.place(source, self.core)
        return remote(
            place, place, self.pass_send.at[source], self.pass_recv.at[source], self.me + 1 - 2 * self.core
        )

    def arrive(self, step):
        chip = self.order(self.chip, step)
        for source in (2 * chip, 2 * chip + 1):
            offset = lax.rem(self.me - source + 8, 8)

            @pl.when(offset == 0)
            def _():
                self.local().wait()

            @pl.when(offset != 0)
            def _(source=source, offset=offset):
                place = self.place(source, self.core)
                remote(place, place, self.send.at[offset], self.recv.at[offset], self.me).wait_recv()

            self.pass_on(source).start()

    def ready(self, step):
        chip = self.order(self.chip, step)
        for source in (2 * chip, 2 * chip + 1):
            place = self.place(source, 1 - self.core)
            remote(
                place, place, self.pass_send.at[source], self.pass_recv.at[source], self.me
            ).wait_recv()
        return chip

    def passed_on(self):
        for source in range(8):
            self.pass_on(source).wait_send()


class Collect:
    def __init__(
        self, me, order, own_steps, kept, passing, passed, total, back, local_sem, pass_send, pass_recv, send, recv
    ):
        self.me, self.chip, self.core = me, me // 2, lax.rem(me, 2)
        self.order, self.own_steps = order, own_steps
        self.kept, self.passing, self.passed, self.total, self.back = kept, passing, passed, total, back
        self.local_sem, self.pass_send, self.pass_recv = local_sem, pass_send, pass_recv
        self.send, self.recv = send, recv
        self.rows, self.half = back.shape[1], back.shape[2] // 2

    def swap(self, step):
        return remote(
            self.passing.at[step % 2],
            self.passed.at[step],
            self.pass_send.at[step],
            self.pass_recv.at[step],
            self.me + 1 - 2 * self.core,
        )

    def place(self, chip, core):
        return self.back.at[chip, :, pl.ds(pl.multiple_of(core * self.half, 128), self.half)]

    def local(self, step, source_core):
        return pltpu.make_async_copy(
            self.total.at[step, pl.ds(pl.multiple_of(source_core * self.rows, 16), self.rows), :],
            self.place(self.chip, self.core),
            self.local_sem,
        )

    def outgoing(self, step, source):
        rows = pl.ds(pl.multiple_of(lax.rem(source, 2) * self.rows, 16), self.rows)
        offset = lax.rem(source - self.me + 8, 8)
        return remote(
            self.total.at[step, rows, :],
            self.place(self.chip, self.core),
            self.send.at[offset],
            self.recv.at[offset],
            source,
        )

    def block(self, step):
        return self.order(self.chip, step)

    def each(self, step, own, other):
        chip = self.block(step)
        for source in (2 * chip, 2 * chip + 1):
            if step not in self.own_steps:
                other(source)
                continue

            @pl.when(source == self.me)
            def _():
                own()

            @pl.when(source != self.me)
            def _(source=source):
                other(source)

    def settle(self, step):
        self.swap(step).wait_recv()
        tile = 2 * self.rows // 4
        for at in range(0, 2 * self.rows, tile):
            span = pl.ds(at, tile)
            summed = self.kept[span, :] + self.passed[step, span, :].astype(jnp.float32)
            self.total[step, span, :] = summed.astype(jnp.bfloat16)
        self.each(
            step,
            lambda: self.local(step, self.core).start(),
            lambda source: self.outgoing(step, source).start(),
        )

    def finish(self):
        for step in range(4):
            if step >= 2:
                self.swap(step).wait_send()
            self.each(
                step,
                lambda step=step: self.local(step, self.core).wait(),
                lambda source, step=step: self.outgoing(step, source).wait_send(),
            )
        for offset in range(1, 8):
            source = lax.rem(self.me + 8 - offset, 8)
            place = self.place(source // 2, lax.rem(source, 2))
            remote(place, place, self.send.at[offset], self.recv.at[offset], self.me).wait_recv()


def ffn_forward_body(
    chunk,
    slots,
    gate_hbm,
    up_hbm,
    down_hbm,
    rows_out,
    gate_out,
    up_out,
    act_out,
    back,
    gate,
    up,
    down,
    landing,
    pre_stage,
    act,
    kept,
    passing,
    passed,
    total,
    weight_sem,
    stage_sem,
    act_sem,
    rows_sem,
    local_sem,
    send,
    recv,
    pass_send,
    pass_recv,
    swap_send,
    swap_recv,
    out_send,
    out_recv,
):
    me = lax.axis_index("expert")
    enter(8, me)
    loads = [
        pltpu.make_async_copy(source, target, weight_sem.at[n])
        for n, (source, target) in enumerate(((gate_hbm, gate), (up_hbm, up), (down_hbm, down)))
    ]
    dispatch = Dispatch(me, crossing_order, slots, landing, local_sem.at[0], send, recv, pass_send, pass_recv)
    collect = Collect(
        me, crossing_order, (0, 3), kept, passing, passed, total, back, local_sem.at[1], swap_send, swap_recv, out_send, out_recv
    )
    middle = is_middle(me // 2)
    dispatch.start_local()
    dispatch.start((0, 1))

    @pl.when(middle == 1)
    def _():
        dispatch.start((2,))

    for load in loads:
        load.start()
    block = landing.shape[1]
    hidden_units = gate.shape[1]
    chunks = hidden_units // chunk
    half = back.shape[2] // 2

    def stage_copies(chip, part, slot):
        span = pl.ds(pl.multiple_of(chip * block, 16), block)
        columns = pl.ds(pl.multiple_of(part * chunk, 128), chunk)
        return [
            pltpu.make_async_copy(
                pre_stage.at[slot, n], out.at[span, columns], stage_sem.at[slot, n]
            )
            for n, out in enumerate((gate_out, up_out))
        ]

    def act_copy(chip, step):
        span = pl.ds(pl.multiple_of(chip * block, 16), block)
        return pltpu.make_async_copy(act.at[step % 2], act_out.at[span, :], act_sem.at[step % 2])

    def rows_copy(chip, step):
        span = pl.ds(pl.multiple_of(chip * block, 16), block)
        return pltpu.make_async_copy(landing.at[chip], rows_out.at[span, :], rows_sem.at[step])

    for step in range(4):
        if step == 0:
            dispatch.arrive(0)
        chip = dispatch.ready(step)
        rows_copy(chip, step).start()
        if step == 0:
            loads[0].wait()
            loads[1].wait()
        if step >= 2:
            act_copy(crossing_order(me // 2, step - 2), step - 2).wait()

        def hidden_part(part, carry, chip=chip, step=step):
            slot = lax.rem(part + step * chunks, 2)
            columns = pl.ds(pl.multiple_of(part * chunk, 128), chunk)

            @pl.when(part + step * chunks >= 2)
            def _():
                for copy in stage_copies(chip, part, slot):
                    copy.wait()

            gated = dot_nn(landing[chip], gate[:, columns])
            raised = dot_nn(landing[chip], up[:, columns])
            pre_stage[slot, 0] = gated.astype(jnp.bfloat16)
            pre_stage[slot, 1] = raised.astype(jnp.bfloat16)
            act[step % 2, :, columns] = (gated * jax.nn.sigmoid(gated) * raised).astype(jnp.bfloat16)
            for copy in stage_copies(chip, part, slot):
                copy.start()
            if step == 0:
                @pl.when((part == chunks // 3) & (middle == 0))
                def _():
                    dispatch.sent((1,))
                    dispatch.start((2,))

                @pl.when((part == chunks // 2) & (middle == 1))
                def _():
                    dispatch.sent((1, 2))
                    dispatch.start((3,))

            return carry

        lax.fori_loop(0, chunks, hidden_part, 0)
        act_copy(chip, step).start()
        if step == 0:
            loads[2].wait()
        else:
            collect.settle(step - 1)
        core = collect.core
        width = min(512, half)

        def far_part(part, carry, step=step):
            at = pl.multiple_of((1 - core) * half + part * width, 128)
            product = dot_nt(act[step % 2], down[pl.ds(at, width), :])
            passing[step % 2, :, pl.ds(pl.multiple_of(part * width, 128), width)] = product.astype(jnp.bfloat16)
            return carry

        def near_part(part, carry, step=step):
            at = pl.multiple_of(core * half + part * width, 128)
            product = dot_nt(act[step % 2], down[pl.ds(at, width), :])
            kept[:, pl.ds(pl.multiple_of(part * width, 128), width)] = product
            return carry

        if step >= 2:
            collect.swap(step - 2).wait_send()
        lax.fori_loop(0, half // width, far_part, 0)
        collect.swap(step).start()
        if step == 0:

            @pl.when(middle == 0)
            def _():
                dispatch.sent((2,))
                dispatch.start((3,))

        if step < 3:
            dispatch.arrive(step + 1)
        lax.fori_loop(0, half // width, near_part, 0)
    collect.settle(3)
    for step in (2, 3):
        act_copy(crossing_order(me // 2, step), step).wait()
    for step in range(4):
        rows_copy(crossing_order(me // 2, step), step).wait()
    for slot in range(2):
        for copy in stage_copies(0, 0, slot):
            copy.wait()
    dispatch.sent((0, 3))
    dispatch.passed_on()
    collect.finish()


def ffn_forward(slots, gate_weight, up_weight, down_weight):
    chips, capacity, depth = slots.shape
    hidden_units = gate_weight.shape[1]
    block = 2 * capacity
    chunk = 256 if hidden_units % 256 == 0 else 128
    half = depth // 2
    rows = chips * block
    any_space = pl.BlockSpec(memory_space=pl.ANY)
    bf = jnp.bfloat16
    dma = pltpu.SemaphoreType.DMA
    return pl.pallas_call(
        functools.partial(ffn_forward_body, chunk),
        in_specs=[any_space] * 4,
        out_specs=[any_space] * 5,
        out_shape=[
            jax.ShapeDtypeStruct((rows, depth), bf),
            jax.ShapeDtypeStruct((rows, hidden_units), bf),
            jax.ShapeDtypeStruct((rows, hidden_units), bf),
            jax.ShapeDtypeStruct((rows, hidden_units), bf),
            jax.ShapeDtypeStruct((chips, capacity, depth), bf),
        ],
        scratch_shapes=[
            pltpu.VMEM((depth, hidden_units), bf),
            pltpu.VMEM((depth, hidden_units), bf),
            pltpu.VMEM((depth, hidden_units), bf),
            pltpu.VMEM((chips, block, depth), bf),
            pltpu.VMEM((2, 2, block, chunk), bf),
            pltpu.VMEM((2, block, hidden_units), bf),
            pltpu.VMEM((block, half), jnp.float32),
            pltpu.VMEM((2, block, half), bf),
            pltpu.VMEM((chips, block, half), bf),
            pltpu.VMEM((chips, block, half), bf),
            dma((3,)),
            dma((2, 2)),
            dma((2,)),
            dma((4,)),
            dma((2,)),
            dma((8,)),
            dma((8,)),
            dma((8,)),
            dma((8,)),
            dma((4,)),
            dma((4,)),
            dma((8,)),
            dma((8,)),
        ],
        compiler_params=pltpu.CompilerParams(
            collective_id=1, has_side_effects=True, vmem_limit_bytes=VMEM_BYTES
        ),
        name="ffn_forward",
    )(slots, gate_weight, up_weight, down_weight)


def send_rows_body(slots, rows_out, local_sem, send, recv, pass_send, pass_recv):
    me = lax.axis_index("expert")
    enter(8, me)
    dispatch = Dispatch(me, chip_order, slots, rows_out, local_sem.at[0], send, recv, pass_send, pass_recv)
    dispatch.start_local()
    dispatch.start((0, 1, 2, 3))
    for step in range(4):
        dispatch.arrive(step)
    for step in range(4):
        dispatch.ready(step)
    dispatch.sent((0, 1, 2, 3))
    dispatch.passed_on()


def send_rows(slots, collective):
    chips, capacity, depth = slots.shape
    any_space = pl.BlockSpec(memory_space=pl.ANY)
    dma = pltpu.SemaphoreType.DMA
    return pl.pallas_call(
        send_rows_body,
        in_specs=[any_space],
        out_specs=any_space,
        out_shape=jax.ShapeDtypeStruct((chips, 2 * capacity, depth), jnp.bfloat16),
        scratch_shapes=[dma((1,)), dma((8,)), dma((8,)), dma((8,)), dma((8,))],
        compiler_params=pltpu.CompilerParams(collective_id=collective, has_side_effects=True),
        name="send_rows",
    )(slots)


def ffn_backward_body(
    chunk,
    grad_rows,
    gate_in,
    up_in,
    gate_hbm,
    up_hbm,
    down_hbm,
    dgate_out,
    dup_out,
    back,
    gate,
    up,
    down,
    grad,
    pre_stage,
    pair,
    kept,
    passing,
    passed,
    total,
    weight_sem,
    grad_sem,
    stage_sem,
    pair_sem,
    local_sem,
    swap_send,
    swap_recv,
    out_send,
    out_recv,
):
    me = lax.axis_index("expert")
    enter(8, me)
    collect = Collect(
        me, far_order, (3,), kept, passing, passed, total, back, local_sem.at[0], swap_send, swap_recv, out_send, out_recv
    )
    loads = [
        pltpu.make_async_copy(source, target, weight_sem.at[n])
        for n, (source, target) in enumerate(((down_hbm, down), (gate_hbm, gate), (up_hbm, up)))
    ]
    block = grad.shape[1]
    hidden_units = gate.shape[1]
    chunks = hidden_units // chunk
    half = back.shape[2] // 2
    width = min(512, half)

    def span_of(chip):
        return pl.ds(pl.multiple_of(chip * block, 16), block)

    def grad_copy(step):
        return pltpu.make_async_copy(
            grad_rows.at[span_of(collect.block(step)), :], grad.at[step % 2], grad_sem.at[step % 2]
        )

    def stage_copies(chip, part, slot):
        columns = pl.ds(pl.multiple_of(part * chunk, 128), chunk)
        return [
            pltpu.make_async_copy(
                source.at[span_of(chip), columns], pre_stage.at[slot, n], stage_sem.at[slot, n]
            )
            for n, source in enumerate((gate_in, up_in))
        ]

    def pair_copies(chip):
        return [
            pltpu.make_async_copy(pair.at[n], out.at[span_of(chip), :], pair_sem.at[n])
            for n, out in enumerate((dgate_out, dup_out))
        ]

    grad_copy(0).start()
    loads[0].start()
    for copy in stage_copies(collect.block(0), 0, 0):
        copy.start()
    loads[1].start()
    loads[2].start()
    loads[0].wait()
    for step in range(4):
        chip = collect.block(step)
        grad_copy(step).wait()
        if step < 3:
            grad_copy(step + 1).start()
        if step > 0:
            for copy in pair_copies(collect.block(step - 1)):
                copy.wait()

        def hidden_part(part, carry, chip=chip, step=step):
            slot = lax.rem(part, 2)
            columns = pl.ds(pl.multiple_of(part * chunk, 128), chunk)
            for copy in stage_copies(chip, part, slot):
                copy.wait()

            @pl.when(part + 1 < chunks)
            def _():
                for copy in stage_copies(chip, part + 1, 1 - slot):
                    copy.start()

            upstream = dot_nn(grad[step % 2], down[:, columns])
            gated = pre_stage[slot, 0].astype(jnp.float32)
            raised = pre_stage[slot, 1].astype(jnp.float32)
            sigmoid = jax.nn.sigmoid(gated)
            scaled = upstream * sigmoid
            pair[0, :, columns] = (scaled * raised * (1.0 + gated * (1.0 - sigmoid))).astype(jnp.bfloat16)
            pair[1, :, columns] = (scaled * gated).astype(jnp.bfloat16)
            return carry

        lax.fori_loop(0, chunks, hidden_part, 0)
        for copy in pair_copies(chip):
            copy.start()
        if step < 3:
            for copy in stage_copies(collect.block(step + 1), 0, 0):
                copy.start()
        if step == 0:
            loads[1].wait()
            loads[2].wait()
        else:
            collect.settle(step - 1)
        core = collect.core

        def product(at):
            return dot_nt(pair[0], gate[pl.ds(at, width), :]) + dot_nt(pair[1], up[pl.ds(at, width), :])

        def far_part(part, carry, step=step):
            at = pl.multiple_of((1 - core) * half + part * width, 128)
            columns = pl.ds(pl.multiple_of(part * width, 128), width)
            passing[step % 2, :, columns] = product(at).astype(jnp.bfloat16)
            return carry

        def near_part(part, carry, step=step):
            at = pl.multiple_of(core * half + part * width, 128)
            kept[:, pl.ds(pl.multiple_of(part * width, 128), width)] = product(at)
            return carry

        if step >= 2:
            collect.swap(step - 2).wait_send()
        lax.fori_loop(0, half // width, far_part, 0)
        collect.swap(step).start()
        lax.fori_loop(0, half // width, near_part, 0)
    collect.settle(3)
    for copy in pair_copies(collect.block(3)):
        copy.wait()
    collect.finish()


def ffn_backward(grad_rows, gate_pre, up_pre, gate_weight, up_weight, down_weight, capacity):
    rows, depth = grad_rows.shape
    hidden_units = gate_weight.shape[1]
    block = 2 * capacity
    chips = rows // block
    chunk = hidden_units // 2 if hidden_units % 256 == 0 else 128
    half = depth // 2
    any_space = pl.BlockSpec(memory_space=pl.ANY)
    bf = jnp.bfloat16
    dma = pltpu.SemaphoreType.DMA
    return pl.pallas_call(
        functools.partial(ffn_backward_body, chunk),
        in_specs=[any_space] * 6,
        out_specs=[any_space] * 3,
        out_shape=[
            jax.ShapeDtypeStruct((rows, hidden_units), bf),
            jax.ShapeDtypeStruct((rows, hidden_units), bf),
            jax.ShapeDtypeStruct((chips, capacity, depth), bf),
        ],
        scratch_shapes=[
            pltpu.VMEM((depth, hidden_units), bf),
            pltpu.VMEM((depth, hidden_units), bf),
            pltpu.VMEM((depth, hidden_units), bf),
            pltpu.VMEM((2, block, depth), bf),
            pltpu.VMEM((2, 2, block, chunk), bf),
            pltpu.VMEM((2, block, hidden_units), bf),
            pltpu.VMEM((block, half), jnp.float32),
            pltpu.VMEM((2, block, half), bf),
            pltpu.VMEM((chips, block, half), bf),
            pltpu.VMEM((chips, block, half), bf),
            dma((3,)),
            dma((2,)),
            dma((2, 2)),
            dma((2,)),
            dma((1,)),
            dma((4,)),
            dma((4,)),
            dma((8,)),
            dma((8,)),
        ],
        compiler_params=pltpu.CompilerParams(
            collective_id=3, has_side_effects=True, vmem_limit_bytes=VMEM_BYTES
        ),
        name="ffn_backward",
    )(grad_rows, gate_pre, up_pre, gate_weight, up_weight, down_weight)


def send_slots_body(
    slots, rows_hbm, grads_hbm, landing, grad_out, rows_v, grads_v, stage, load_sem, stage_sem, local_sem, send, recv
):
    me = lax.axis_index("expert")
    enter(8, me)

    def outgoing(offset):
        target = lax.rem(me + offset, 8)
        return remote(slots.at[target], landing.at[me], send.at[offset], recv.at[offset], target)

    local = pltpu.make_async_copy(slots.at[me], landing.at[me], local_sem)
    for offset in range(1, 8):
        outgoing(offset).start()
    local.start()
    loads = [
        pltpu.make_async_copy(source, target, load_sem.at[n])
        for n, (source, target) in enumerate(((rows_hbm, rows_v), (grads_hbm, grads_v)))
    ]
    for load in loads:
        load.start()
    for load in loads:
        load.wait()
    width = stage.shape[1]
    blocks = rows_v.shape[1] // width

    def stage_copy(block):
        slot = lax.rem(block, 2)
        span = pl.ds(pl.multiple_of(block * width, 16), width)
        return pltpu.make_async_copy(stage.at[slot], grad_out.at[span, :], stage_sem.at[slot])

    def one(block, carry):
        @pl.when(block >= 2)
        def _():
            stage_copy(block - 2).wait()

        columns = pl.ds(pl.multiple_of(block * width, 128), width)
        turned = rows_v[:, columns].astype(jnp.float32).T.astype(jnp.bfloat16)
        stage[lax.rem(block, 2)] = dot_nn(turned, grads_v[...]).astype(jnp.bfloat16)
        stage_copy(block).start()
        return carry

    lax.fori_loop(0, blocks, one, 0)
    for block in (blocks - 2, blocks - 1):
        stage_copy(block).wait()
    local.wait()
    for offset in range(1, 8):
        outgoing(offset).wait_send()
        place = landing.at[lax.rem(me + 8 - offset, 8)]
        remote(place, place, send.at[offset], recv.at[offset], me).wait_recv()


def send_slots(slots, rows, grads):
    total, depth = rows.shape
    hidden_units = grads.shape[1]
    width = min(256, depth // 2)
    any_space = pl.BlockSpec(memory_space=pl.ANY)
    bf = jnp.bfloat16
    dma = pltpu.SemaphoreType.DMA
    return pl.pallas_call(
        send_slots_body,
        in_specs=[any_space] * 3,
        out_specs=[any_space] * 2,
        out_shape=[
            jax.ShapeDtypeStruct(slots.shape, bf),
            jax.ShapeDtypeStruct((depth, hidden_units), bf),
        ],
        scratch_shapes=[
            pltpu.VMEM((total, depth), bf),
            pltpu.VMEM((total, hidden_units), bf),
            pltpu.VMEM((2, width, hidden_units), bf),
            dma((2,)),
            dma((2,)),
            dma,
            dma((8,)),
            dma((8,)),
        ],
        compiler_params=pltpu.CompilerParams(
            collective_id=5, has_side_effects=True, vmem_limit_bytes=VMEM_BYTES
        ),
        name="send_slots",
    )(slots, rows, grads)


def merge_return_body(
    dp_axis,
    plan_hbm,
    slots_hbm,
    grads_hbm,
    weight_hbm,
    back,
    plan,
    slots,
    grads,
    weight,
    kept,
    passing,
    passed,
    total,
    load_sem,
    local_sem,
    swap_send,
    swap_recv,
    out_send,
    out_recv,
):
    me = lax.axis_index("expert")
    replica = lax.axis_index(dp_axis)
    enter(8, me)
    loads = [
        pltpu.make_async_copy(source, target, load_sem.at[n])
        for n, (source, target) in enumerate(
            ((plan_hbm, plan), (slots_hbm, slots), (grads_hbm, grads), (weight_hbm, weight))
        )
    ]
    for load in loads:
        load.start()
    collect = Collect(
        me, far_order, (3,), kept, passing, passed, total, back, local_sem.at[0], swap_send, swap_recv, out_send, out_recv
    )
    rows, half = collect.rows, collect.half
    parts, ck = weight.shape[0], weight.shape[2] // 2
    values_at = grads.shape[1] // 2
    width = min(512, half)
    for load in loads:
        load.wait()
    for step in range(4):
        chip = collect.block(step)
        span = pl.ds(pl.multiple_of(chip * 2 * rows, 16), 2 * rows)

        def product(at, chip=chip, span=span):
            columns = pl.ds(at, width)
            result = jnp.concatenate(
                [dot_nn(plan[2 * chip + n], slots[2 * chip + n, :, columns]) for n in range(2)], axis=0
            )
            for part in range(parts):
                low = lax.rem(replica, 2) + (part % 2) * (1 - 2 * lax.rem(replica, 2))
                high = replica // 2 + (part // 2) * (1 - 2 * (replica // 2))
                at_keys = pl.multiple_of((2 * high + low) * ck, 128)
                result += dot_nt(grads[span, pl.ds(at_keys, ck)], weight[part, columns, :ck])
                result += dot_nt(grads[span, pl.ds(values_at + at_keys, ck)], weight[part, columns, ck:])
            return result

        def far_part(part, carry, step=step, product=product):
            at = pl.multiple_of((1 - collect.core) * half + part * width, 128)
            columns = pl.ds(pl.multiple_of(part * width, 128), width)
            passing[step % 2, :, columns] = product(at).astype(jnp.bfloat16)
            return carry

        def near_part(part, carry, product=product):
            at = pl.multiple_of(collect.core * half + part * width, 128)
            kept[:, pl.ds(pl.multiple_of(part * width, 128), width)] = product(at)
            return carry

        if step >= 2:
            collect.swap(step - 2).wait_send()
        lax.fori_loop(0, half // width, far_part, 0)
        collect.swap(step).start()
        if step > 0:
            collect.settle(step - 1)
        lax.fori_loop(0, half // width, near_part, 0)
    collect.settle(3)
    collect.finish()


def merge_return(plan, slots, grads, weights):
    sources, rows, capacity = plan.shape
    parts, depth, columns = weights.shape
    tokens = sources * rows
    half = depth // 2
    any_space = pl.BlockSpec(memory_space=pl.ANY)
    bf = jnp.bfloat16
    dma = pltpu.SemaphoreType.DMA
    return pl.pallas_call(
        functools.partial(merge_return_body, "dp"),
        in_specs=[any_space] * 4,
        out_specs=any_space,
        out_shape=jax.ShapeDtypeStruct((sources // 2, rows, depth), bf),
        scratch_shapes=[
            pltpu.VMEM(plan.shape, bf),
            pltpu.VMEM(slots.shape, bf),
            pltpu.VMEM(grads.shape, bf),
            pltpu.VMEM(weights.shape, bf),
            pltpu.VMEM((2 * rows, half), jnp.float32),
            pltpu.VMEM((2, 2 * rows, half), bf),
            pltpu.VMEM((sources // 2, 2 * rows, half), bf),
            pltpu.VMEM((sources // 2, 2 * rows, half), bf),
            dma((4,)),
            dma((1,)),
            dma((4,)),
            dma((4,)),
            dma((8,)),
            dma((8,)),
        ],
        compiler_params=pltpu.CompilerParams(
            collective_id=6, has_side_effects=True, vmem_limit_bytes=VMEM_BYTES
        ),
        name="merge_return",
    )(plan, slots, grads, weights)


def attention_send_body(
    scale,
    query_hbm,
    sibling_hbm,
    key_hbm,
    value_hbm,
    out_weight_hbm,
    key_info,
    query_info,
    own_out,
    sibling_out,
    rows_out,
    back,
    lse_ref,
    queries,
    siblings,
    keys_v,
    values_v,
    out_weight,
    bias_ref,
    flipped,
    own_stage,
    sibling_stage,
    arrived,
    rows_stage,
    sending,
    load_sem,
    own_sem,
    sibling_sem,
    rows_sem,
    local_sem,
    swap_send,
    swap_recv,
    out_send,
    out_recv,
):
    me = lax.axis_index("expert")
    chip, core = me // 2, lax.rem(me, 2)
    enter(8, me)
    half = keys_v.shape[1]
    rows = own_stage.shape[1]
    keys = keys_v.shape[0] // GROUPS
    heads = half // HEAD
    capacity = back.shape[1]
    own_columns = pl.ds(pl.multiple_of(core * half, 128), half)
    far_columns = pl.ds(pl.multiple_of((1 - core) * half, 128), half)
    loads = [
        pltpu.make_async_copy(source, target, load_sem.at[n])
        for n, (source, target) in enumerate(
            (
                (value_hbm, values_v),
                (key_hbm, keys_v),
                (query_hbm.at[:, own_columns], queries),
                (sibling_hbm, siblings),
                (out_weight_hbm, out_weight),
            )
        )
    ]
    for load in loads:
        load.start()
    fill_bias(bias_ref, key_info, query_info, keys)
    loads[0].wait()

    def flip(head, carry):
        lanes = pl.ds(pl.multiple_of(head * HEAD, HEAD), HEAD)
        for block in range(GROUPS):
            values = values_v[pl.ds(block * keys, keys), lanes].astype(jnp.float32)
            flipped[head, block] = values.T.astype(jnp.bfloat16)
        return carry

    lax.fori_loop(0, heads, flip, 0)
    for load in loads[1:4]:
        load.wait()

    def group_of(step):
        return chip_order(chip, 3 - step)

    def span_of(step):
        return pl.ds(pl.multiple_of(group_of(step) * rows, 16), rows)

    def own_copy(step):
        return pltpu.make_async_copy(own_stage.at[step], own_out.at[span_of(step), :], own_sem.at[step])

    def sibling_copy(step):
        return pltpu.make_async_copy(
            sibling_stage.at[step], sibling_out.at[span_of(step), :], sibling_sem.at[step]
        )

    def rows_copy(step):
        return pltpu.make_async_copy(
            rows_stage.at[step], rows_out.at[span_of(step), :], rows_sem.at[step]
        )

    def swap(step):
        return remote(
            sibling_stage.at[step], arrived.at[step], swap_send.at[step], swap_recv.at[step], me + 1 - 2 * core
        )

    def outgoing(step, n):
        source = 2 * group_of(step) + n
        offset = lax.rem(source - me + 8, 8)
        return remote(sending.at[step, n], back.at[me], out_send.at[offset], out_recv.at[offset], source)

    def local(step, n):
        return pltpu.make_async_copy(sending.at[step, n], back.at[me], local_sem)

    def each(step, own, other):
        for n in range(2):
            if step < 3:
                other(n)
                continue

            @pl.when(core == n)
            def _(n=n):
                own(n)

            @pl.when(core != n)
            def _(n=n):
                other(n)

    def attend(step):
        group = group_of(step)
        first_block = group * (group + 1) // 2
        span = span_of(step)

        def head_pair(pair, carry):
            lanes = [pl.ds(pl.multiple_of((2 * pair + n) * HEAD, HEAD), HEAD) for n in range(2)]
            parts = [jnp.concatenate([queries[span, lane], siblings[span, lane]], axis=0) for lane in lanes]

            def one(block, state):
                at = pl.multiple_of(block * keys, 16)
                bias = bias_ref[first_block + block]
                result = []
                for n in range(2):
                    top, total, mixed = state[3 * n : 3 * n + 3]
                    scores = dot_nt(keys_v[pl.ds(at, keys), lanes[n]], parts[n]) * scale + bias
                    new_top = jnp.maximum(top, jnp.max(scores, axis=0, keepdims=True))
                    fade = jnp.exp2(top - new_top)
                    probs = jnp.exp2(scores - new_top)
                    total = total * fade + jnp.sum(probs, axis=0, keepdims=True)
                    mixed = mixed * fade + dot_nn(flipped[2 * pair + n, block], probs.astype(jnp.bfloat16))
                    result += [new_top, total, mixed]
                return tuple(result)

            start = (
                jnp.full((1, 2 * rows), -1e30, jnp.float32),
                jnp.zeros((1, 2 * rows), jnp.float32),
                jnp.zeros((HEAD, 2 * rows), jnp.float32),
            ) * 2
            final = lax.fori_loop(0, group + 1, one, start)
            for n in range(2):
                top, total, mixed = final[3 * n : 3 * n + 3]
                lse_ref[2 * pair + n, group] = top + jnp.log2(total)
                result = (mixed / total).T.astype(jnp.bfloat16)
                own_stage[step, :, lanes[n]] = result[:rows]
                sibling_stage[step, :, lanes[n]] = result[rows:]
            return carry

        lax.fori_loop(0, heads // 2, head_pair, 0)
        swap(step).start()
        own_copy(step).start()
        sibling_copy(step).start()

    def settle(step):
        swap(step).wait_recv()
        rows_stage[step, :, own_columns] = own_stage[step]
        rows_stage[step, :, far_columns] = arrived[step]
        rows_copy(step).start()
        width = 512
        for at in range(0, back.shape[2], min(width, back.shape[2])):
            columns = pl.ds(at, min(width, back.shape[2]))
            product = dot_nt(rows_stage[step], out_weight[columns, :])
            for n in range(2):
                part = product[n * capacity : (n + 1) * capacity]
                sending[step, n, :, columns] = part.astype(jnp.bfloat16)
        each(step, lambda n: local(step, n).start(), lambda n: outgoing(step, n).start())

    for step in range(4):
        attend(step)
        if step == 1:
            loads[4].wait()
        if step > 0:
            settle(step - 1)
    settle(3)
    for step in range(4):
        swap(step).wait_send()
        own_copy(step).wait()
        sibling_copy(step).wait()
        rows_copy(step).wait()
        each(step, lambda n, step=step: local(step, n).wait(), lambda n, step=step: outgoing(step, n).wait_send())
    for offset in range(1, 8):
        place = back.at[lax.rem(me + 8 - offset, 8)]
        remote(place, place, out_send.at[offset], out_recv.at[offset], me).wait_recv()


def attention_send(queries, siblings, keys_all, values_all, out_weight, key_info, query_info, capacity):
    total_rows, width = queries.shape
    tokens, half = keys_all.shape
    depth = out_weight.shape[0]
    rows, keys, heads = total_rows // GROUPS, tokens // GROUPS, half // HEAD
    any_space = pl.BlockSpec(memory_space=pl.ANY)
    here = pl.BlockSpec(memory_space=pltpu.VMEM)
    bf = jnp.bfloat16
    dma = pltpu.SemaphoreType.DMA
    return pl.pallas_call(
        functools.partial(attention_send_body, HEAD ** (-0.5) * LOG2E),
        in_specs=[any_space] * 5 + [here] * 2,
        out_specs=[any_space] * 4 + [here],
        out_shape=[
            jax.ShapeDtypeStruct((total_rows, half), bf),
            jax.ShapeDtypeStruct((total_rows, half), bf),
            jax.ShapeDtypeStruct((total_rows, width), bf),
            jax.ShapeDtypeStruct((8, capacity, depth), bf),
            jax.ShapeDtypeStruct((heads, GROUPS, 1, 2 * rows), jnp.float32),
        ],
        scratch_shapes=[
            pltpu.VMEM((total_rows, half), bf),
            pltpu.VMEM((total_rows, half), bf),
            pltpu.VMEM((tokens, half), bf),
            pltpu.VMEM((tokens, half), bf),
            pltpu.VMEM(out_weight.shape, bf),
            pltpu.VMEM((GROUPS * (GROUPS + 1) // 2, keys, 2 * rows), jnp.float32),
            pltpu.VMEM((heads, GROUPS, HEAD, keys), bf),
            pltpu.VMEM((GROUPS, rows, half), bf),
            pltpu.VMEM((GROUPS, rows, half), bf),
            pltpu.VMEM((GROUPS, rows, half), bf),
            pltpu.VMEM((GROUPS, rows, width), bf),
            pltpu.VMEM((GROUPS, 2, capacity, depth), bf),
            dma((5,)),
            dma((GROUPS,)),
            dma((GROUPS,)),
            dma((GROUPS,)),
            dma,
            dma((GROUPS,)),
            dma((GROUPS,)),
            dma((8,)),
            dma((8,)),
        ],
        compiler_params=pltpu.CompilerParams(
            collective_id=4, has_side_effects=True, vmem_limit_bytes=VMEM_BYTES
        ),
        name="attention_send",
    )(queries, siblings, keys_all, values_all, out_weight, key_info, query_info)


D = 2048
HEADS = 16
ATT_EXPERTS = 8
FFN_EXPERTS = 4
TRUNK = 1024
SEG = 96
TREE_LEN = 2176
NODES = 13

epsilon = 1e-06
highest = lax.Precision.HIGHEST
bf16 = jnp.bfloat16
f32 = jnp.float32


def tree_layout(places):
    after_trunk = places - TRUNK
    after_branch = after_trunk - 4 * SEG
    segments = jnp.where(
        places < TRUNK,
        0,
        jnp.where(after_branch < 0, 1 + after_trunk // SEG, 5 + after_branch // SEG),
    )
    depths = jnp.where(
        places < TRUNK,
        places,
        jnp.where(after_branch < 0, TRUNK + after_trunk % SEG, TRUNK + SEG + after_branch % SEG),
    )
    return (segments.astype(jnp.int32), depths.astype(jnp.int32))


def rotation_tables(depths):
    half_size = HEAD // 2
    frequency = 10000.0 ** (-jnp.arange(half_size, dtype=f32) * 2.0 / HEAD)
    angles = depths.astype(f32)[:, None] * frequency[None, :]
    cosine, sine = jnp.cos(angles), jnp.sin(angles)
    cosines = jnp.concatenate([cosine, cosine], axis=1)
    forward = jnp.concatenate([-sine, sine], axis=1)
    return (cosines, forward), (cosines, -forward)


def lookup(table, indices):
    nodes = jnp.arange(NODES, dtype=jnp.int32)
    return jnp.sum(jnp.where(indices[:, None] == nodes[None, :], table[None, :], 0), axis=1)


def running_count(chosen):
    rows = chosen.shape[-1]
    index = jnp.arange(rows, dtype=jnp.int32)
    upto = (index[:, None] <= index[None, :]).astype(bf16)
    return jnp.dot(chosen.astype(bf16), upto, preferred_element_type=f32).astype(jnp.int32) - 1


def source_plan(routes, expert, capacity):
    chosen = jnp.any(routes == expert, axis=2)
    ranking = running_count(chosen)
    slots = jnp.arange(capacity, dtype=jnp.int32)
    return chosen[:, None, :] & (ranking[:, None, :] == slots[None, :, None])


def token_picks(routes, experts, capacity):
    labels = jnp.arange(experts, dtype=jnp.int32)
    hits = routes.T[:, None, :] == labels[None, :, None]
    ranking = running_count(hits[0] | hits[1])
    slots = jnp.arange(capacity, dtype=jnp.int32)
    picks = hits[:, :, None, :] & (ranking[None, :, None, :] == slots[None, None, :, None])
    return picks.astype(bf16), hits[0].T.astype(f32), hits[1].T.astype(f32)


def fill_slots(picks, pair):
    return jnp.einsum("kecr,krd->ecd", picks, pair, preferred_element_type=f32).astype(bf16)


def read_slots(picks, slots):
    return jnp.einsum("kecr,ecd->krd", picks, slots, preferred_element_type=f32)


def gate_values(hidden, router, first, second):
    logits = jnp.dot(hidden.astype(f32), router, precision=highest)
    picked = jnp.stack([jnp.sum(logits * first, axis=1), jnp.sum(logits * second, axis=1)], axis=1)
    return jax.nn.softmax(picked, axis=1)


def router_grads(hidden, router, gates, first, second, picked_grad):
    logit_pick = gates * (picked_grad - jnp.sum(gates * picked_grad, axis=1, keepdims=True))
    logit_grad = logit_pick[:, 0:1] * first + logit_pick[:, 1:2] * second
    router_grad = jnp.dot(hidden.astype(f32).T, logit_grad, precision=highest)
    hidden_grad = jnp.dot(logit_grad, router.T, precision=highest)
    return (router_grad, hidden_grad)


def rms_parts(values):
    inverse = lax.rsqrt(jnp.mean(values * values, axis=-1, keepdims=True) + epsilon)
    return (values * inverse, inverse)


def norm_back(grad_normed, normed, inverse):
    return inverse * (grad_normed - normed * jnp.mean(grad_normed * normed, axis=-1, keepdims=True))


def pair_grads(gates, branches, upstream):
    gate_grad = jnp.stack([jnp.sum(upstream * branches[k], axis=1) for k in range(2)], axis=1)
    scaled = jnp.stack([gates[:, k : k + 1] * upstream for k in range(2)]).astype(bf16)
    return gate_grad, scaled


def exchange(slots):
    return lax.all_to_all(slots, "expert", split_axis=0, concat_axis=0, tiled=True)


def shift(values, step, size, devices):
    moves = [(i, i // size * size + (i % size + step) % size) for i in range(devices)]
    return lax.ppermute(values, "expert", moves)


def group_gather(rows, size, devices):
    return jnp.concatenate([rows] + [shift(rows, step, size, devices) for step in range(1, size)])


def group_reduce(partial, size, devices):
    parts = partial.reshape(size, -1, partial.shape[1])
    total = parts[0].astype(f32)
    for step in range(1, size):
        total = total + shift(parts[step], -step, size, devices).astype(f32)
    return total.astype(bf16)


def spread_over_replicas(block, my_replica, replicas):
    if replicas != 4:
        return lax.all_gather(block, "dp", axis=0), jnp.arange(replicas, dtype=jnp.int32)
    across, along = ([(i, i ^ n) for i in range(4)] for n in (1, 2))
    first, second = lax.ppermute(block, "dp", across), lax.ppermute(block, "dp", along)
    cut = block.shape[0] // 2
    upper, lower = lax.ppermute(second[:cut], "dp", across), lax.ppermute(first[cut:], "dp", along)
    blocks = jnp.stack([block, first, second, jnp.concatenate([upper, lower])])
    return blocks, my_replica ^ jnp.arange(4, dtype=jnp.int32)


def dot_tn(left, right):
    return lax.dot_general(left, right, (((0,), (0,)), ((), ())), preferred_element_type=f32)


def body(
    tokens,
    teacher,
    att_routes,
    ffn_routes,
    parent,
    valid,
    gain_one,
    kv_weight,
    att_router,
    q_weight,
    o_weight,
    gain_two,
    ffn_router,
    gate_weight,
    up_weight,
    down_weight,
):
    row_count = tokens.shape[0]
    devices, replicas = lax.axis_size("expert"), lax.axis_size("dp")
    my_index, my_replica = lax.axis_index("expert"), lax.axis_index("dp")
    core = my_index % 2
    att_copies, ffn_copies = devices // ATT_EXPERTS, devices // FFN_EXPERTS
    att_capacity, ffn_capacity = row_count * 13 // 40, row_count * 13 // 20
    token_count = row_count * devices
    half = HEADS * HEAD // 2
    assert token_count == TREE_LEN * parent.shape[0] and parent.shape[0] == 1
    pair = [(i, i ^ 1) for i in range(devices)]
    own_places = my_index * row_count + jnp.arange(row_count, dtype=jnp.int32)

    x_in = tokens.astype(f32)
    normed_one, inverse_one = rms_parts(x_in)
    hidden = (normed_one * gain_one).astype(bf16)
    weight_rows = kv_weight.shape[0]
    piece = half // replicas
    kv_share = lax.dynamic_slice_in_dim(
        kv_weight.reshape(weight_rows, 4, replicas, piece), my_replica, 1, 2
    )
    kv_share = (
        kv_share.reshape(weight_rows, 2, 2, piece).transpose(0, 2, 1, 3).reshape(weight_rows, 4 * piece)
    )
    kv_gathered = lax.all_gather(kv_share, "expert", axis=0)
    kv_gathered, hidden_sent = lax.optimization_barrier((kv_gathered, hidden))
    hidden_all = lax.all_gather(hidden_sent, "expert", axis=0)
    kv_half = lax.dynamic_slice_in_dim(kv_gathered, core * 2 * piece, 2 * piece, 2).reshape(D, 2 * piece)
    kv_half, routes_sent = lax.optimization_barrier((kv_half, att_routes))
    kv_blocks, block_order = spread_over_replicas(kv_half, my_replica, replicas)
    all_routes = lax.all_gather(routes_sent, "expert", axis=0)

    tree_places = jnp.arange(token_count, dtype=jnp.int32)
    tree_segments, tree_depths = tree_layout(tree_places)
    key_forward, key_backward = rotation_tables(tree_depths)
    key_info = jnp.pad(jnp.stack([tree_places, tree_segments], axis=1), ((0, 0), (0, 6)))
    experts_here = [my_index // att_copies]
    if att_copies == 1:
        experts_here.append(my_index ^ 1)
    plans = [source_plan(all_routes, expert, att_capacity) for expert in experts_here]
    slot_tables, query_parts = [], []
    for plan in plans:
        places = jnp.sum(
            jnp.where(plan, tree_places.reshape(devices, 1, row_count), 0), axis=2
        ).reshape(-1)
        segments, depths = tree_layout(places)
        parents = lookup(parent[0], segments)
        grands = lookup(parent[0], parents)
        query_parts.append(jnp.stack([places, segments, parents, grands]).reshape(4, GROUPS, -1))
        slot_tables.append(rotation_tables(depths))
    query_info = jnp.concatenate(query_parts, axis=2).transpose(1, 0, 2)
    own_plan = plans[0].astype(bf16)
    att_picks, att_first, att_second = token_picks(att_routes, ATT_EXPERTS, att_capacity)
    att_gates = gate_values(hidden, att_router, att_first, att_second)
    ffn_picks, ffn_first, ffn_second = token_picks(ffn_routes, FFN_EXPERTS, ffn_capacity)
    prepared = (key_forward, key_backward, key_info, slot_tables, query_info, own_plan, att_picks, att_gates, ffn_picks)
    hidden_all, kv_blocks, prepared = lax.optimization_barrier((hidden_all, kv_blocks, prepared))
    key_forward, key_backward, key_info, slot_tables, query_info, own_plan, att_picks, att_gates, ffn_picks = prepared

    queries, query_inputs = project_queries(own_plan, hidden_all, q_weight, slot_tables[0][0])
    keys_all, values_all = project_keys_values(hidden_all, kv_blocks, key_forward, block_order)

    def far_half(values):
        return lax.ppermute(
            lax.dynamic_slice_in_dim(values, (1 - core) * half, half, 1), "expert", pair
        )

    def join_halves(mine, sibling):
        other = lax.ppermute(sibling, "expert", pair)
        return jnp.where(
            core == 0,
            jnp.concatenate([mine, other], axis=1),
            jnp.concatenate([other, mine], axis=1),
        )

    heads = half // HEAD
    query_sets = [queries]
    starts = jnp.zeros((2,), jnp.int32)
    if att_copies == 1:
        query_sets.append(far_half(queries))
        starts = jnp.stack([core * heads, 0]).astype(jnp.int32)
    fused = devices == 8 and replicas == 4 and att_copies == 1 and ffn_copies == 2 and ffn_capacity % 16 == 0
    if fused:
        *att_outs, att_rows, att_back, lse = attention_send(
            *query_sets, keys_all, values_all, o_weight, key_info, query_info, att_capacity
        )
        att_elsewhere = [
            lax.ppermute(att_rows, "dp", [(i, i ^ n) for i in range(replicas)]) for n in range(1, replicas)
        ]
    else:
        *att_outs, lse = attention_forward(
            query_sets, starts // 2, keys_all, values_all, key_info, query_info, heads
        )
        att_rows = join_halves(*att_outs) if att_copies == 1 else att_outs[0]
        att_partial = lax.dot_general(
            att_rows, o_weight, (((1,), (1,)), ((), ())), preferred_element_type=f32
        ).astype(bf16)
        att_back = exchange(att_partial.reshape(devices, att_capacity, D))
    if att_copies > 1:
        att_back = (
            att_back.astype(f32).reshape(ATT_EXPERTS, att_copies, att_capacity, D).sum(axis=1).astype(bf16)
        )
    att_branches = read_slots(att_picks, att_back)
    x_mid = x_in + att_gates[:, 0:1] * att_branches[0] + att_gates[:, 1:2] * att_branches[1]

    normed_two, inverse_two = rms_parts(x_mid)
    hidden_two = (normed_two * gain_two).astype(bf16)
    ffn_gates = gate_values(hidden_two, ffn_router, ffn_first, ffn_second)

    def to_experts(slots):
        rows = exchange(slots.reshape(devices, ffn_capacity // ffn_copies, D))
        return group_gather(rows.reshape(-1, D), ffn_copies, devices)

    def to_tokens(partial):
        rows = group_reduce(partial.astype(bf16), ffn_copies, devices)
        back = exchange(rows.reshape(devices, ffn_capacity // ffn_copies, D))
        return read_slots(ffn_picks, back.reshape(FFN_EXPERTS, ffn_capacity, D))

    ffn_slots = jnp.einsum(
        "ecr,rd->ecd", ffn_picks[0] + ffn_picks[1], hidden_two, preferred_element_type=f32
    ).astype(bf16)
    if fused:
        ffn_inputs, gate_pre, up_pre, activated, ffn_back = ffn_forward(
            ffn_slots, gate_weight, up_weight, down_weight
        )
        ffn_branches = read_slots(ffn_picks, ffn_back)
    else:
        ffn_inputs = to_experts(ffn_slots)
        gate_pre = jnp.dot(ffn_inputs, gate_weight, preferred_element_type=f32)
        up_pre = jnp.dot(ffn_inputs, up_weight, preferred_element_type=f32)
        sigmoid_gate = jax.nn.sigmoid(gate_pre)
        silu_gate = gate_pre * sigmoid_gate
        activated = (silu_gate * up_pre).astype(bf16)
        ffn_branches = to_tokens(
            lax.dot_general(
                activated, down_weight, (((1,), (1,)), ((), ())), preferred_element_type=f32
            )
        )
    result = x_mid + ffn_gates[:, 0:1] * ffn_branches[0] + ffn_gates[:, 1:2] * ffn_branches[1]

    tree_global = my_replica * parent.shape[0] + own_places // TREE_LEN
    tree_labels = jnp.arange(valid.shape[0], dtype=jnp.int32)
    limits = jnp.sum(
        jnp.where(tree_global[:, None] == tree_labels[None, :], valid[None, :], 0), axis=1
    )
    counted = own_places % TREE_LEN < limits
    loss_factor = valid.shape[0] * TREE_LEN / jnp.sum(valid).astype(f32)
    grad_result = jnp.where(counted[:, None], (result - teacher.astype(f32)) * loss_factor, 0.0)

    ffn_gate_grad, ffn_scaled = pair_grads(ffn_gates, ffn_branches, grad_result)
    ffn_grad_slots = fill_slots(ffn_picks, ffn_scaled)
    if fused:
        ffn_grad_slots, att_elsewhere = lax.optimization_barrier((ffn_grad_slots, att_elsewhere))
        grad_ffn_out = send_rows(ffn_grad_slots, 2).reshape(-1, D)
    else:
        grad_ffn_out = to_experts(ffn_grad_slots)
    grad_down = dot_tn(grad_ffn_out, activated).astype(bf16)
    grad_ffn_out, grad_down = lax.optimization_barrier((grad_ffn_out, grad_down))
    summed_down = lax.psum_scatter(grad_down, "dp", scatter_dimension=0, tiled=True)
    if fused:
        grad_gate_pre, grad_up_pre, ffn_grad_back = ffn_backward(
            grad_ffn_out, gate_pre, up_pre, gate_weight, up_weight, down_weight, ffn_capacity
        )
        grad_gate = dot_tn(ffn_inputs, grad_gate_pre).astype(bf16)
        ffn_grad_back, grad_gate = lax.optimization_barrier((ffn_grad_back, grad_gate))
        ffn_grad_pair = read_slots(ffn_picks, ffn_grad_back)
    else:
        grad_activated = jnp.dot(grad_ffn_out, down_weight, preferred_element_type=f32)
        grad_gate_pre = (
            grad_activated * up_pre * sigmoid_gate * (1.0 + gate_pre * (1.0 - sigmoid_gate))
        ).astype(bf16)
        grad_up_pre = (grad_activated * silu_gate).astype(bf16)
        grad_ffn_in = lax.dot_general(
            grad_gate_pre, gate_weight, (((1,), (1,)), ((), ())), preferred_element_type=f32
        ) + lax.dot_general(
            grad_up_pre, up_weight, (((1,), (1,)), ((), ())), preferred_element_type=f32
        )
        grad_gate = dot_tn(ffn_inputs, grad_gate_pre).astype(bf16)
        ffn_grad_pair = to_tokens(grad_ffn_in)
    summed_gate = lax.psum_scatter(grad_gate, "dp", scatter_dimension=0, tiled=True)
    grad_ffn_router, hidden_two_extra = router_grads(
        hidden_two, ffn_router, ffn_gates, ffn_first, ffn_second, ffn_gate_grad
    )
    grad_hidden_two = ffn_grad_pair[0] + ffn_grad_pair[1] + hidden_two_extra
    grad_gain_two = jnp.sum(grad_hidden_two * normed_two, axis=0)
    grad_mid = grad_result + norm_back(grad_hidden_two * gain_two, normed_two, inverse_two)

    att_gate_grad, att_scaled = pair_grads(att_gates, att_branches, grad_mid)
    att_slots = fill_slots(att_picks, att_scaled)
    if att_copies > 1:
        att_slots = jnp.repeat(att_slots, att_copies, axis=0)
    att_slots, summed_down = lax.optimization_barrier((att_slots, summed_down))
    if fused:
        grad_att_out, grad_up = send_slots(att_slots, ffn_inputs, grad_up_pre)
        grad_att_out = grad_att_out.reshape(-1, D)
    else:
        grad_att_out = exchange(att_slots).reshape(-1, D)
        grad_up = dot_tn(ffn_inputs, grad_up_pre).astype(bf16)
        grad_att_out, grad_up = lax.optimization_barrier((grad_att_out, grad_up))
    summed_up = lax.psum_scatter(grad_up, "dp", scatter_dimension=0, tiled=True)
    grad_heads = jnp.dot(grad_att_out, o_weight, preferred_element_type=f32).astype(bf16)
    grad_heads, grad_att_out = lax.optimization_barrier((grad_heads, grad_att_out))
    grad_sets = [grad_heads]
    if att_copies == 1:
        grad_sets.append(far_half(grad_heads))
    if fused:
        share = D // replicas

        def columns_of(replica):
            return lax.dynamic_slice_in_dim(grad_att_out, replica * share, share, 1)

        grad_columns = [columns_of(my_replica)] + [
            lax.ppermute(columns_of(my_replica ^ n), "dp", [(i, i ^ n) for i in range(replicas)])
            for n in range(1, replicas)
        ]
    else:
        grad_o = dot_tn(grad_att_out, att_rows).astype(bf16)
        summed_o = lax.psum_scatter(grad_o, "dp", scatter_dimension=0, tiled=True).astype(f32)
    grad_sets[-1], summed_gate = lax.optimization_barrier((grad_sets[-1], summed_gate))
    *grad_queries, grad_keys_values = attention_backward(
        query_sets,
        starts,
        grad_sets,
        att_outs,
        keys_all,
        values_all,
        lse,
        key_info,
        query_info,
        key_backward,
        [tables[1] for tables in slot_tables],
        heads,
    )
    grad_query_pre = join_halves(*grad_queries) if att_copies == 1 else grad_queries[0]
    grad_kv = dot_tn(hidden_all.reshape(token_count, D), grad_keys_values).astype(bf16)
    grad_q = dot_tn(query_inputs, grad_query_pre).astype(bf16)
    summed_kv = lax.psum_scatter(grad_kv, "dp", scatter_dimension=0, tiled=True)
    summed_q = lax.psum_scatter(grad_q, "dp", scatter_dimension=0, tiled=True)
    grad_query_in = lax.dot_general(
        grad_query_pre, q_weight, (((1,), (1,)), ((), ())), preferred_element_type=f32
    ).astype(bf16)
    grad_query_in, grad_kv, grad_q, summed_up = lax.optimization_barrier(
        (grad_query_in, grad_kv, grad_q, summed_up)
    )

    merge_args = (
        own_plan.transpose(0, 2, 1),
        grad_query_in.reshape(devices, att_capacity, D),
        grad_keys_values,
        kv_blocks,
    )
    if fused:
        arrived = merge_return(*merge_args)
        arrived, grad_columns, summed_kv = lax.optimization_barrier((arrived, grad_columns, summed_kv))
        summed_o = sum(
            dot_tn(grad, rows) for grad, rows in zip(grad_columns, [att_rows] + att_elsewhere)
        )
    else:
        merged = merge_hidden_grads(*merge_args, block_order).reshape(devices // 2, 2, row_count, D)
        kept = lax.dynamic_index_in_dim(merged, core, 1, keepdims=False)
        passed = lax.ppermute(
            lax.dynamic_index_in_dim(merged, 1 - core, 1, keepdims=False), "expert", pair
        )
        chip_sum = (kept.astype(f32) + passed.astype(f32)).astype(bf16)
        same_core = [[2 * i + c for i in range(devices // 2)] for c in range(2)]
        arrived = lax.all_to_all(
            chip_sum, "expert", split_axis=0, concat_axis=0, axis_index_groups=same_core, tiled=True
        )
    grad_att_router, hidden_one_extra = router_grads(
        hidden, att_router, att_gates, att_first, att_second, att_gate_grad
    )
    grad_hidden_one = jnp.sum(arrived.astype(f32), axis=0) + hidden_one_extra
    grad_gain_one = jnp.sum(grad_hidden_one * normed_one, axis=0)
    grad_input = grad_mid + norm_back(grad_hidden_one * gain_one, normed_one, inverse_one)

    everyone = devices * replicas
    smalls = [grad_gain_one, grad_gain_two, grad_att_router, grad_ffn_router]
    packed = jnp.concatenate([small.reshape(everyone, -1) for small in smalls], axis=1)
    own_smalls = jnp.sum(
        lax.all_to_all(packed, ("dp", "expert"), split_axis=0, concat_axis=0, tiled=True), axis=0
    )
    share = D // everyone
    shared_gain_one = own_smalls[:share]
    shared_gain_two = own_smalls[share : 2 * share]
    shared_att_router = own_smalls[2 * share : (2 + ATT_EXPERTS) * share].reshape(share, ATT_EXPERTS)
    shared_ffn_router = own_smalls[(2 + ATT_EXPERTS) * share :].reshape(share, FFN_EXPERTS)

    kv_rows = exchange(summed_kv.reshape(devices, -1, 2 * half))
    kv_sum = jnp.sum(kv_rows.astype(f32).reshape(devices // 2, 2, -1, 2 * half), axis=0)
    shared_kv = jnp.concatenate(
        [kv_sum[n, :, m * half : (m + 1) * half] for m in range(2) for n in range(2)], axis=1
    )

    return (
        result.astype(bf16),
        grad_input.astype(bf16),
        shared_gain_one,
        shared_kv,
        shared_att_router,
        summed_q.astype(f32),
        summed_o,
        shared_gain_two,
        shared_ffn_router,
        summed_gate.astype(f32),
        summed_up.astype(f32),
        summed_down.astype(f32),
    )


def solution(mesh):
    in_specs = (
        P(("dp", "expert"), None),
        P(("dp", "expert"), None),
        P(("dp", "expert"), None),
        P(("dp", "expert"), None),
        P("dp", None),
        P(),
        P(),
        P("expert", None),
        P(),
        P(None, "expert"),
        P(None, "expert"),
        P(),
        P(),
        P(None, "expert"),
        P(None, "expert"),
        P(None, "expert"),
    )
    out_specs = (
        P(("dp", "expert"), None),
        P(("dp", "expert"), None),
        P(("dp", "expert")),
        P(("dp", "expert"), None),
        P(("dp", "expert"), None),
        P("dp", "expert"),
        P("dp", "expert"),
        P(("dp", "expert")),
        P(("dp", "expert"), None),
        P("dp", "expert"),
        P("dp", "expert"),
        P("dp", "expert"),
    )
    return jax.shard_map(body, mesh=mesh, in_specs=in_specs, out_specs=out_specs, check_vma=False)
```

```python
import functools
import jax
import jax.numpy as jnp
from jax import lax
from jax.experimental import pallas as pl
from jax.experimental.pallas import tpu as pltpu
from jax.sharding import PartitionSpec as P

HEAD = 128
GROUPS = 4
LOG2E = 1.4426950408889634
VMEM_BYTES = 60 * 1024 * 1024


def dot_nt(left, right):
    return lax.dot_general(left, right, (((1,), (1,)), ((), ())), preferred_element_type=jnp.float32)


def dot_nn(left, right):
    return jnp.dot(left, right, preferred_element_type=jnp.float32)


def spin(values, cosine, sine):
    return values * cosine + pltpu.roll(values, HEAD // 2, 1) * sine


def fill_bias(bias_ref, key_ref, query_ref, keys):
    for group in range(GROUPS):
        place = query_ref[group, 0:1, :]
        own, parent, grand = (query_ref[group, 1 + n : 2 + n, :] for n in range(3))

        def one(block, carry, group=group, place=place, own=own, parent=parent, grand=grand):
            at = pl.multiple_of(block * keys, 16)
            key_place = key_ref[pl.ds(at, keys), 0:1]
            key_segment = key_ref[pl.ds(at, keys), 1:2]
            related = (key_segment == own) | (key_segment == parent) | (key_segment == grand)
            allowed = related & (key_place <= place)
            bias_ref[group * (group + 1) // 2 + block] = jnp.where(allowed, 0.0, -1e30)
            return carry

        lax.fori_loop(0, group + 1, one, 0)


def group_rows(refs, group, rows, lanes):
    parts = [ref[pl.ds(group * rows, rows), lanes] for ref in refs]
    return parts[0] if len(parts) == 1 else jnp.concatenate(parts, axis=0)


def attention_forward_body(sets, step_heads, rows, keys, scale, first_ref, *refs):
    query_refs = refs[:sets]
    key_ref, value_ref, key_info, query_info = refs[sets : sets + 4]
    out_refs = refs[sets + 4 : 2 * sets + 4]
    lse_ref, bias_ref, flipped_ref = refs[2 * sets + 4 :]
    wide = sets * rows

    @pl.when(pl.program_id(0) == 0)
    def _():
        fill_bias(bias_ref, key_info, query_info, keys)

    for head in range(step_heads):
        lanes = pl.ds(head * HEAD, HEAD)
        for block in range(GROUPS):
            values = value_ref[pl.ds(block * keys, keys), lanes].astype(jnp.float32)
            flipped_ref[head, block] = values.T.astype(jnp.bfloat16)
    for group in range(GROUPS):
        queries = [
            group_rows(query_refs, group, rows, pl.ds(head * HEAD, HEAD)) for head in range(step_heads)
        ]

        def one(block, carry, group=group, queries=queries):
            at = pl.multiple_of(block * keys, 16)
            bias = bias_ref[group * (group + 1) // 2 + block]
            result = []
            for head in range(step_heads):
                top, total, mixed = carry[3 * head : 3 * head + 3]
                scores = dot_nt(key_ref[pl.ds(at, keys), pl.ds(head * HEAD, HEAD)], queries[head])
                scores = scores * scale + bias
                new_top = jnp.maximum(top, jnp.max(scores, axis=0, keepdims=True))
                fade = jnp.exp2(top - new_top)
                parts = jnp.exp2(scores - new_top)
                total = total * fade + jnp.sum(parts, axis=0, keepdims=True)
                mixed = mixed * fade + dot_nn(flipped_ref[head, block], parts.astype(jnp.bfloat16))
                result += [new_top, total, mixed]
            return tuple(result)

        start = (
            jnp.full((1, wide), -1e30, jnp.float32),
            jnp.zeros((1, wide), jnp.float32),
            jnp.zeros((HEAD, wide), jnp.float32),
        ) * step_heads
        final = lax.fori_loop(0, group + 1, one, start)
        for head in range(step_heads):
            top, total, mixed = final[3 * head : 3 * head + 3]
            lse_ref[head, group] = top + jnp.log2(total)
            rows_out = (mixed / total).T.astype(jnp.bfloat16)
            for n, ref in enumerate(out_refs):
                ref[pl.ds(group * rows, rows), pl.ds(head * HEAD, HEAD)] = rows_out[
                    n * rows : (n + 1) * rows
                ]


def attention_backward_body(sets, step_heads, rows, keys, scale, first_ref, *refs):
    query_refs, grad_refs, out_refs = (refs[n * sets : (n + 1) * sets] for n in range(3))
    key_ref, value_ref, lse_ref, key_info, query_info = refs[3 * sets : 3 * sets + 5]
    key_cos, key_sin = refs[3 * sets + 5 : 3 * sets + 7]
    table_refs = refs[3 * sets + 7 : 5 * sets + 7]
    rest = refs[5 * sets + 7 :]
    dq_refs = rest[:sets]
    dkv_ref, bias_ref, flipped_ref, dk_acc, dv_acc = rest[sets:]
    half = dkv_ref.shape[1] // 2
    softmax_scale = scale / LOG2E

    @pl.when(pl.program_id(0) == 0)
    def _():
        fill_bias(bias_ref, key_info, query_info, keys)

    dk_acc[...] = jnp.zeros_like(dk_acc)
    dv_acc[...] = jnp.zeros_like(dv_acc)
    for head in range(step_heads):
        lanes = pl.ds(head * HEAD, HEAD)
        for block in range(GROUPS):
            values = key_ref[pl.ds(block * keys, keys), lanes].astype(jnp.float32)
            flipped_ref[head, block] = values.T.astype(jnp.bfloat16)
    for group in range(GROUPS):
        queries, grads, centres, tops = [], [], [], []
        for head in range(step_heads):
            lanes = pl.ds(head * HEAD, HEAD)
            queries.append(group_rows(query_refs, group, rows, lanes))
            grad = group_rows(grad_refs, group, rows, lanes)
            out = group_rows(out_refs, group, rows, lanes)
            product = grad.astype(jnp.float32) * out.astype(jnp.float32)
            centres.append(jnp.sum(product.T, axis=0, keepdims=True))
            grads.append(grad)
            tops.append(lse_ref[head, group])

        def one(block, carry, group=group, queries=queries, grads=grads, centres=centres, tops=tops):
            at = pl.multiple_of(block * keys, 16)
            bias = bias_ref[group * (group + 1) // 2 + block]
            result = []
            for head in range(step_heads):
                lanes = pl.ds(head * HEAD, HEAD)
                key_rows = key_ref[pl.ds(at, keys), lanes]
                scores = dot_nt(key_rows, queries[head])
                probs = jnp.exp2(scores * scale + (bias - tops[head]))
                grad_probs = dot_nt(value_ref[pl.ds(at, keys), lanes], grads[head])
                grad_scores = (probs * (grad_probs - centres[head])).astype(jnp.bfloat16)
                dv_acc[pl.ds(at, keys), lanes] += dot_nn(probs.astype(jnp.bfloat16), grads[head])
                dk_acc[pl.ds(at, keys), lanes] += dot_nn(grad_scores, queries[head])
                result.append(carry[head] + dot_nn(flipped_ref[head, block], grad_scores))
            return tuple(result)

        start = (jnp.zeros((HEAD, sets * rows), jnp.float32),) * step_heads
        final = lax.fori_loop(0, group + 1, one, start)
        for head in range(step_heads):
            dq = final[head].T * softmax_scale
            for n, ref in enumerate(dq_refs):
                span = pl.ds(group * rows, rows)
                turned = spin(
                    dq[n * rows : (n + 1) * rows], table_refs[2 * n][span, :], table_refs[2 * n + 1][span, :]
                )
                ref[span, pl.ds(head * HEAD, HEAD)] = turned.astype(jnp.bfloat16)
    for head in range(step_heads):
        lanes = pl.ds(head * HEAD, HEAD)
        first_lane = pl.multiple_of((pl.program_id(0) * step_heads + head) * HEAD, HEAD)
        for block in range(GROUPS):
            span = pl.ds(block * keys, keys)
            turned = spin(dk_acc[span, lanes] * softmax_scale, key_cos[span, :], key_sin[span, :])
            dkv_ref[span, pl.ds(first_lane, HEAD)] = turned.astype(jnp.bfloat16)
            dkv_ref[span, pl.ds(half + first_lane, HEAD)] = dv_acc[span, lanes].astype(jnp.bfloat16)


def whole_block(shape):
    return pl.BlockSpec(shape, lambda h, first: (0,) * len(shape))


def attention_forward(queries, starts, keys_all, values_all, key_info, query_info, heads):
    sets, total_rows, tokens = len(queries), queries[0].shape[0], keys_all.shape[0]
    rows, keys = total_rows // GROUPS, tokens // GROUPS
    step_heads = 2
    wide = step_heads * HEAD
    scale = HEAD ** (-0.5) * LOG2E
    query_specs = [
        pl.BlockSpec((total_rows, wide), lambda h, first, n=n: (0, first[n] + h)) for n in range(sets)
    ]
    plain = pl.BlockSpec((total_rows, wide), lambda h, first: (0, h))
    side = pl.BlockSpec((tokens, wide), lambda h, first: (0, h))
    return pl.pallas_call(
        functools.partial(attention_forward_body, sets, step_heads, rows, keys, scale),
        grid_spec=pltpu.PrefetchScalarGridSpec(
            num_scalar_prefetch=1,
            grid=(heads // step_heads,),
            in_specs=query_specs
            + [side, side, whole_block(key_info.shape), whole_block(query_info.shape)],
            out_specs=[plain] * sets
            + [pl.BlockSpec((step_heads, GROUPS, 1, sets * rows), lambda h, first: (h, 0, 0, 0))],
            scratch_shapes=[
                pltpu.VMEM((GROUPS * (GROUPS + 1) // 2, keys, sets * rows), jnp.float32),
                pltpu.VMEM((step_heads, GROUPS, HEAD, keys), jnp.bfloat16),
            ],
        ),
        out_shape=[jax.ShapeDtypeStruct((total_rows, heads * HEAD), jnp.bfloat16)] * sets
        + [jax.ShapeDtypeStruct((heads, GROUPS, 1, sets * rows), jnp.float32)],
        compiler_params=pltpu.CompilerParams(vmem_limit_bytes=VMEM_BYTES),
        name="attention_forward",
    )(starts, *queries, keys_all, values_all, key_info, query_info)


def attention_backward(
    queries, starts, grads, outs, keys_all, values_all, lse, key_info, query_info, key_tables, row_tables, heads
):
    sets, total_rows, tokens = len(queries), queries[0].shape[0], keys_all.shape[0]
    rows, keys = total_rows // GROUPS, tokens // GROUPS
    step_heads = 1
    wide = step_heads * HEAD
    scale = HEAD ** (-0.5) * LOG2E
    shifted = [
        pl.BlockSpec((total_rows, wide), lambda h, first, n=n: (0, first[n] + h)) for n in range(sets)
    ]
    plain = pl.BlockSpec((total_rows, wide), lambda h, first: (0, h))
    side = pl.BlockSpec((tokens, wide), lambda h, first: (0, h))
    return pl.pallas_call(
        functools.partial(attention_backward_body, sets, step_heads, rows, keys, scale),
        grid_spec=pltpu.PrefetchScalarGridSpec(
            num_scalar_prefetch=1,
            grid=(heads // step_heads,),
            in_specs=shifted
            + shifted
            + [plain] * sets
            + [
                side,
                side,
                pl.BlockSpec((step_heads, GROUPS, 1, sets * rows), lambda h, first: (h, 0, 0, 0)),
                whole_block(key_info.shape),
                whole_block(query_info.shape),
                whole_block((tokens, HEAD)),
                whole_block((tokens, HEAD)),
            ]
            + [whole_block((total_rows, HEAD))] * (2 * sets),
            out_specs=[plain] * sets + [whole_block((tokens, 2 * heads * HEAD))],
            scratch_shapes=[
                pltpu.VMEM((GROUPS * (GROUPS + 1) // 2, keys, sets * rows), jnp.float32),
                pltpu.VMEM((step_heads, GROUPS, HEAD, keys), jnp.bfloat16),
                pltpu.VMEM((tokens, wide), jnp.float32),
                pltpu.VMEM((tokens, wide), jnp.float32),
            ],
        ),
        out_shape=[jax.ShapeDtypeStruct((total_rows, heads * HEAD), jnp.bfloat16)] * sets
        + [jax.ShapeDtypeStruct((tokens, 2 * heads * HEAD), jnp.bfloat16)],
        compiler_params=pltpu.CompilerParams(vmem_limit_bytes=VMEM_BYTES),
        name="attention_backward",
    )(
        starts,
        *queries,
        *grads,
        *outs,
        keys_all,
        values_all,
        lse,
        key_info,
        query_info,
        *key_tables,
        *[table for pair in row_tables for table in pair],
    )


def project_body(plan_ref, hidden_ref, weight_ref, cos_ref, sin_ref, out_ref, x_ref):
    sources, capacity = plan_ref.shape[0], plan_ref.shape[1]
    bundle = max(1, sources * capacity // GROUPS // capacity)
    tile = bundle * capacity

    @pl.when(pl.program_id(0) == 0)
    def _():
        for group in range(sources // bundle):
            parts = [
                dot_nn(plan_ref[group * bundle + n], hidden_ref[group * bundle + n]) for n in range(bundle)
            ]
            x_ref[pl.ds(group * tile, tile), :] = jnp.concatenate(parts, axis=0).astype(jnp.bfloat16)

    for at in range(0, x_ref.shape[0], tile):
        span = pl.ds(at, tile)
        product = dot_nn(x_ref[span, :], weight_ref[...])
        for lane in range(0, out_ref.shape[1], HEAD):
            turned = spin(product[:, lane : lane + HEAD], cos_ref[span, :], sin_ref[span, :])
            out_ref[span, lane : lane + HEAD] = turned.astype(jnp.bfloat16)


def project_queries(plan, hidden, weight, tables):
    sources, capacity, row_count = plan.shape
    depth, columns = weight.shape
    rows = sources * capacity
    block = 512
    return pl.pallas_call(
        project_body,
        grid=(columns // block,),
        in_specs=[
            pl.BlockSpec((sources, capacity, row_count), lambda j: (0, 0, 0)),
            pl.BlockSpec((sources, row_count, depth), lambda j: (0, 0, 0)),
            pl.BlockSpec((depth, block), lambda j: (0, j)),
            pl.BlockSpec((rows, HEAD), lambda j: (0, 0)),
            pl.BlockSpec((rows, HEAD), lambda j: (0, 0)),
        ],
        out_specs=[
            pl.BlockSpec((rows, block), lambda j: (0, j)),
            pl.BlockSpec((rows, depth), lambda j: (0, 0)),
        ],
        out_shape=[
            jax.ShapeDtypeStruct((rows, columns), jnp.bfloat16),
            jax.ShapeDtypeStruct((rows, depth), jnp.bfloat16),
        ],
        compiler_params=pltpu.CompilerParams(vmem_limit_bytes=VMEM_BYTES),
        name="project_queries",
    )(plan, hidden, weight, *tables)


def keys_values_body(half, order_ref, x_ref, weight_ref, cos_ref, sin_ref, key_ref, value_ref):
    rows = x_ref.shape[1]
    for source in range(x_ref.shape[0]):
        span = pl.ds(source * rows, rows)
        product = dot_nn(x_ref[source], weight_ref[0])
        for lane in range(0, half, HEAD):
            turned = spin(product[:, lane : lane + HEAD], cos_ref[span, :], sin_ref[span, :])
            key_ref[span, lane : lane + HEAD] = turned.astype(jnp.bfloat16)
        value_ref[span, :] = product[:, half:].astype(jnp.bfloat16)


def project_keys_values(hidden, weights, tables, order):
    sources, rows, unused = hidden.shape
    parts, depth, columns = weights.shape
    half, tokens = columns // 2, sources * rows
    return pl.pallas_call(
        functools.partial(keys_values_body, half),
        grid_spec=pltpu.PrefetchScalarGridSpec(
            num_scalar_prefetch=1,
            grid=(parts,),
            in_specs=[
                pl.BlockSpec((sources, rows, depth), lambda j, order: (0, 0, 0)),
                pl.BlockSpec((1, depth, columns), lambda j, order: (j, 0, 0)),
                pl.BlockSpec((tokens, HEAD), lambda j, order: (0, 0)),
                pl.BlockSpec((tokens, HEAD), lambda j, order: (0, 0)),
            ],
            out_specs=[pl.BlockSpec((tokens, half), lambda j, order: (0, order[j]))] * 2,
        ),
        out_shape=[jax.ShapeDtypeStruct((tokens, parts * half), jnp.bfloat16)] * 2,
        compiler_params=pltpu.CompilerParams(vmem_limit_bytes=VMEM_BYTES),
        name="project_keys_values",
    )(order, hidden, weights, *tables)


def merge_body(tile, order_ref, plan_ref, slots_ref, dk_ref, dv_ref, weight_ref, out_ref, acc_ref):
    part = pl.program_id(1)
    sources, rows = plan_ref.shape[0], plan_ref.shape[1]
    ck = dk_ref.shape[1]

    @pl.when(part == 0)
    def _():
        for source in range(sources):
            acc_ref[pl.ds(source * rows, rows), :] = dot_nn(plan_ref[source], slots_ref[source])

    last = part == pl.num_programs(1) - 1
    for at in range(0, acc_ref.shape[0], tile):
        span = pl.ds(at, tile)
        acc_ref[span, :] += dot_nt(dk_ref[span, :], weight_ref[0, :, :ck]) + dot_nt(
            dv_ref[span, :], weight_ref[0, :, ck:]
        )

    @pl.when(last)
    def _():
        out_ref[...] = acc_ref[...].astype(jnp.bfloat16)


def merge_hidden_grads(plan, slots, grads, weights, order):
    sources, rows, capacity = plan.shape
    parts, depth, columns = weights.shape
    ck, tokens = columns // 2, sources * rows
    wide = depth // 2
    return pl.pallas_call(
        functools.partial(merge_body, tokens // GROUPS),
        grid_spec=pltpu.PrefetchScalarGridSpec(
            num_scalar_prefetch=1,
            grid=(2, parts),
            in_specs=[
                pl.BlockSpec((sources, rows, capacity), lambda i, j, order: (0, 0, 0)),
                pl.BlockSpec((sources, capacity, wide), lambda i, j, order: (0, 0, i)),
                pl.BlockSpec((tokens, ck), lambda i, j, order: (0, order[j])),
                pl.BlockSpec((tokens, ck), lambda i, j, order: (0, parts + order[j])),
                pl.BlockSpec((1, wide, columns), lambda i, j, order: (j, i, 0)),
            ],
            out_specs=pl.BlockSpec((tokens, wide), lambda i, j, order: (0, i)),
            scratch_shapes=[pltpu.VMEM((tokens, wide), jnp.float32)],
        ),
        out_shape=jax.ShapeDtypeStruct((tokens, depth), jnp.bfloat16),
        compiler_params=pltpu.CompilerParams(vmem_limit_bytes=VMEM_BYTES),
        name="merge_hidden_grads",
    )(order, plan, slots, grads, grads, weights)


def mesh_device(index):
    return {"expert": index}


def chip_order(chip, step):
    flip = chip // 2
    near = chip + flip * (3 - 2 * chip)
    place = step + near * (1 - 2 * step) if step < 2 else step
    return place + flip * (3 - 2 * place)


def far_order(chip, step):
    return chip_order(chip, 3 - step)


def is_middle(chip):
    flip = chip // 2
    return chip + flip * (3 - 2 * chip)


def crossing_order(chip, step):
    end, middle = chip_order(chip, step), chip_order(chip, (2, 3, 1, 0)[step])
    return end + is_middle(chip) * (middle - end)


def enter(devices, me):
    barrier = pltpu.get_barrier_semaphore()
    for step in range(1, devices):
        pl.semaphore_signal(
            barrier,
            inc=1,
            device_id=mesh_device(lax.rem(me + step, devices)),
            device_id_type=pl.DeviceIdType.MESH,
        )
    pl.semaphore_wait(barrier, devices - 1)


def remote(source, target, send, recv, device):
    return pltpu.make_async_remote_copy(
        src_ref=source,
        dst_ref=target,
        send_sem=send,
        recv_sem=recv,
        device_id=mesh_device(device),
        device_id_type=pl.DeviceIdType.MESH,
    )


class Dispatch:
    def __init__(self, me, order, slots, landing, local_sem, send, recv, pass_send, pass_recv):
        self.me, self.chip, self.core, self.order = me, me // 2, lax.rem(me, 2), order
        self.slots, self.landing = slots, landing
        self.local_sem, self.send, self.recv = local_sem, send, recv
        self.pass_send, self.pass_recv = pass_send, pass_recv
        self.rows, self.half = slots.shape[1], slots.shape[2] // 2

    def columns(self, core):
        return pl.ds(pl.multiple_of(core * self.half, 128), self.half)

    def place(self, source, core):
        rows = pl.ds(pl.multiple_of(lax.rem(source, 2) * self.rows, 16), self.rows)
        return self.landing.at[source // 2, rows, self.columns(core)]

    def direct(self, target):
        core = lax.rem(target, 2)
        offset = lax.rem(target - self.me + 8, 8)
        return remote(
            self.slots.at[target // 2, :, self.columns(core)],
            self.place(self.me, core),
            self.send.at[offset],
            self.recv.at[offset],
            target,
        )

    def sends(self, step):
        chip = chip_order(self.chip, step)
        targets = [2 * chip, 2 * chip + 1] if step else [self.me + 1 - 2 * self.core]
        return [self.direct(target) for target in targets]

    def local(self):
        return pltpu.make_async_copy(
            self.slots.at[self.chip, :, self.columns(self.core)],
            self.place(self.me, self.core),
            self.local_sem,
        )

    def start_local(self):
        self.local().start()

    def start(self, steps):
        for step in steps:
            for copy in self.sends(step):
                copy.start()

    def sent(self, steps):
        for step in steps:
            for copy in self.sends(step):
                copy.wait_send()

    def pass_on(self, source):
        place = self.place(source, self.core)
        return remote(
            place, place, self.pass_send.at[source], self.pass_recv.at[source], self.me + 1 - 2 * self.core
        )

    def arrive(self, step):
        chip = self.order(self.chip, step)
        for source in (2 * chip, 2 * chip + 1):
            offset = lax.rem(self.me - source + 8, 8)

            @pl.when(offset == 0)
            def _():
                self.local().wait()

            @pl.when(offset != 0)
            def _(source=source, offset=offset):
                place = self.place(source, self.core)
                remote(place, place, self.send.at[offset], self.recv.at[offset], self.me).wait_recv()

            self.pass_on(source).start()

    def ready(self, step):
        chip = self.order(self.chip, step)
        for source in (2 * chip, 2 * chip + 1):
            place = self.place(source, 1 - self.core)
            remote(
                place, place, self.pass_send.at[source], self.pass_recv.at[source], self.me
            ).wait_recv()
        return chip

    def passed_on(self):
        for source in range(8):
            self.pass_on(source).wait_send()


class Collect:
    def __init__(
        self, me, order, own_steps, kept, passing, passed, total, back, local_sem, pass_send, pass_recv, send, recv
    ):
        self.me, self.chip, self.core = me, me // 2, lax.rem(me, 2)
        self.order, self.own_steps = order, own_steps
        self.kept, self.passing, self.passed, self.total, self.back = kept, passing, passed, total, back
        self.local_sem, self.pass_send, self.pass_recv = local_sem, pass_send, pass_recv
        self.send, self.recv = send, recv
        self.rows, self.half = back.shape[1], back.shape[2] // 2

    def swap(self, step):
        return remote(
            self.passing.at[step % 2],
            self.passed.at[step],
            self.pass_send.at[step],
            self.pass_recv.at[step],
            self.me + 1 - 2 * self.core,
        )

    def place(self, chip, core):
        return self.back.at[chip, :, pl.ds(pl.multiple_of(core * self.half, 128), self.half)]

    def local(self, step, source_core):
        return pltpu.make_async_copy(
            self.total.at[step, pl.ds(pl.multiple_of(source_core * self.rows, 16), self.rows), :],
            self.place(self.chip, self.core),
            self.local_sem,
        )

    def outgoing(self, step, source):
        rows = pl.ds(pl.multiple_of(lax.rem(source, 2) * self.rows, 16), self.rows)
        offset = lax.rem(source - self.me + 8, 8)
        return remote(
            self.total.at[step, rows, :],
            self.place(self.chip, self.core),
            self.send.at[offset],
            self.recv.at[offset],
            source,
        )

    def block(self, step):
        return self.order(self.chip, step)

    def each(self, step, own, other):
        chip = self.block(step)
        for source in (2 * chip, 2 * chip + 1):
            if step not in self.own_steps:
                other(source)
                continue

            @pl.when(source == self.me)
            def _():
                own()

            @pl.when(source != self.me)
            def _(source=source):
                other(source)

    def settle(self, step):
        self.swap(step).wait_recv()
        tile = 2 * self.rows // 4
        for at in range(0, 2 * self.rows, tile):
            span = pl.ds(at, tile)
            summed = self.kept[span, :] + self.passed[step, span, :].astype(jnp.float32)
            self.total[step, span, :] = summed.astype(jnp.bfloat16)
        self.each(
            step,
            lambda: self.local(step, self.core).start(),
            lambda source: self.outgoing(step, source).start(),
        )

    def finish(self):
        for step in range(4):
            if step >= 2:
                self.swap(step).wait_send()
            self.each(
                step,
                lambda step=step: self.local(step, self.core).wait(),
                lambda source, step=step: self.outgoing(step, source).wait_send(),
            )
        for offset in range(1, 8):
            source = lax.rem(self.me + 8 - offset, 8)
            place = self.place(source // 2, lax.rem(source, 2))
            remote(place, place, self.send.at[offset], self.recv.at[offset], self.me).wait_recv()


def ffn_forward_body(
    chunk,
    slots,
    gate_hbm,
    up_hbm,
    down_hbm,
    rows_out,
    gate_out,
    up_out,
    act_out,
    back,
    gate,
    up,
    down,
    landing,
    pre_stage,
    act,
    kept,
    passing,
    passed,
    total,
    weight_sem,
    stage_sem,
    act_sem,
    rows_sem,
    local_sem,
    send,
    recv,
    pass_send,
    pass_recv,
    swap_send,
    swap_recv,
    out_send,
    out_recv,
):
    me = lax.axis_index("expert")
    enter(8, me)
    loads = [
        pltpu.make_async_copy(source, target, weight_sem.at[n])
        for n, (source, target) in enumerate(((gate_hbm, gate), (up_hbm, up), (down_hbm, down)))
    ]
    dispatch = Dispatch(me, crossing_order, slots, landing, local_sem.at[0], send, recv, pass_send, pass_recv)
    collect = Collect(
        me, crossing_order, (0, 3), kept, passing, passed, total, back, local_sem.at[1], swap_send, swap_recv, out_send, out_recv
    )
    middle = is_middle(me // 2)
    dispatch.start_local()
    dispatch.start((0, 1))

    @pl.when(middle == 1)
    def _():
        dispatch.start((2,))

    for load in loads:
        load.start()
    block = landing.shape[1]
    hidden_units = gate.shape[1]
    chunks = hidden_units // chunk
    half = back.shape[2] // 2

    def stage_copies(chip, part, slot):
        span = pl.ds(pl.multiple_of(chip * block, 16), block)
        columns = pl.ds(pl.multiple_of(part * chunk, 128), chunk)
        return [
            pltpu.make_async_copy(
                pre_stage.at[slot, n], out.at[span, columns], stage_sem.at[slot, n]
            )
            for n, out in enumerate((gate_out, up_out))
        ]

    def act_copy(chip, step):
        span = pl.ds(pl.multiple_of(chip * block, 16), block)
        return pltpu.make_async_copy(act.at[step % 2], act_out.at[span, :], act_sem.at[step % 2])

    def rows_copy(chip, step):
        span = pl.ds(pl.multiple_of(chip * block, 16), block)
        return pltpu.make_async_copy(landing.at[chip], rows_out.at[span, :], rows_sem.at[step])

    for step in range(4):
        if step == 0:
            dispatch.arrive(0)
        chip = dispatch.ready(step)
        rows_copy(chip, step).start()
        if step == 0:
            loads[0].wait()
            loads[1].wait()
        if step >= 2:
            act_copy(crossing_order(me // 2, step - 2), step - 2).wait()

        def hidden_part(part, carry, chip=chip, step=step):
            slot = lax.rem(part + step * chunks, 2)
            columns = pl.ds(pl.multiple_of(part * chunk, 128), chunk)

            @pl.when(part + step * chunks >= 2)
            def _():
                for copy in stage_copies(chip, part, slot):
                    copy.wait()

            gated = dot_nn(landing[chip], gate[:, columns])
            raised = dot_nn(landing[chip], up[:, columns])
            pre_stage[slot, 0] = gated.astype(jnp.bfloat16)
            pre_stage[slot, 1] = raised.astype(jnp.bfloat16)
            act[step % 2, :, columns] = (gated * jax.nn.sigmoid(gated) * raised).astype(jnp.bfloat16)
            for copy in stage_copies(chip, part, slot):
                copy.start()
            if step == 0:
                @pl.when((part == chunks // 3) & (middle == 0))
                def _():
                    dispatch.sent((1,))
                    dispatch.start((2,))

                @pl.when((part == chunks // 2) & (middle == 1))
                def _():
                    dispatch.sent((1, 2))
                    dispatch.start((3,))

            return carry

        lax.fori_loop(0, chunks, hidden_part, 0)
        act_copy(chip, step).start()
        if step == 0:
            loads[2].wait()
        else:
            collect.settle(step - 1)
        core = collect.core
        width = min(512, half)

        def far_part(part, carry, step=step):
            at = pl.multiple_of((1 - core) * half + part * width, 128)
            product = dot_nt(act[step % 2], down[pl.ds(at, width), :])
            passing[step % 2, :, pl.ds(pl.multiple_of(part * width, 128), width)] = product.astype(jnp.bfloat16)
            return carry

        def near_part(part, carry, step=step):
            at = pl.multiple_of(core * half + part * width, 128)
            product = dot_nt(act[step % 2], down[pl.ds(at, width), :])
            kept[:, pl.ds(pl.multiple_of(part * width, 128), width)] = product
            return carry

        if step >= 2:
            collect.swap(step - 2).wait_send()
        lax.fori_loop(0, half // width, far_part, 0)
        collect.swap(step).start()
        if step == 0:

            @pl.when(middle == 0)
            def _():
                dispatch.sent((2,))
                dispatch.start((3,))

        if step < 3:
            dispatch.arrive(step + 1)
        lax.fori_loop(0, half // width, near_part, 0)
    collect.settle(3)
    for step in (2, 3):
        act_copy(crossing_order(me // 2, step), step).wait()
    for step in range(4):
        rows_copy(crossing_order(me // 2, step), step).wait()
    for slot in range(2):
        for copy in stage_copies(0, 0, slot):
            copy.wait()
    dispatch.sent((0, 3))
    dispatch.passed_on()
    collect.finish()


def ffn_forward(slots, gate_weight, up_weight, down_weight):
    chips, capacity, depth = slots.shape
    hidden_units = gate_weight.shape[1]
    block = 2 * capacity
    chunk = 256 if hidden_units % 256 == 0 else 128
    half = depth // 2
    rows = chips * block
    any_space = pl.BlockSpec(memory_space=pl.ANY)
    bf = jnp.bfloat16
    dma = pltpu.SemaphoreType.DMA
    return pl.pallas_call(
        functools.partial(ffn_forward_body, chunk),
        in_specs=[any_space] * 4,
        out_specs=[any_space] * 5,
        out_shape=[
            jax.ShapeDtypeStruct((rows, depth), bf),
            jax.ShapeDtypeStruct((rows, hidden_units), bf),
            jax.ShapeDtypeStruct((rows, hidden_units), bf),
            jax.ShapeDtypeStruct((rows, hidden_units), bf),
            jax.ShapeDtypeStruct((chips, capacity, depth), bf),
        ],
        scratch_shapes=[
            pltpu.VMEM((depth, hidden_units), bf),
            pltpu.VMEM((depth, hidden_units), bf),
            pltpu.VMEM((depth, hidden_units), bf),
            pltpu.VMEM((chips, block, depth), bf),
            pltpu.VMEM((2, 2, block, chunk), bf),
            pltpu.VMEM((2, block, hidden_units), bf),
            pltpu.VMEM((block, half), jnp.float32),
            pltpu.VMEM((2, block, half), bf),
            pltpu.VMEM((chips, block, half), bf),
            pltpu.VMEM((chips, block, half), bf),
            dma((3,)),
            dma((2, 2)),
            dma((2,)),
            dma((4,)),
            dma((2,)),
            dma((8,)),
            dma((8,)),
            dma((8,)),
            dma((8,)),
            dma((4,)),
            dma((4,)),
            dma((8,)),
            dma((8,)),
        ],
        compiler_params=pltpu.CompilerParams(
            collective_id=1, has_side_effects=True, vmem_limit_bytes=VMEM_BYTES
        ),
        name="ffn_forward",
    )(slots, gate_weight, up_weight, down_weight)


def send_rows_body(
    slots,
    act_hbm,
    rows_out,
    grad_out,
    landing,
    act,
    total,
    stage,
    act_sem,
    rows_sem,
    stage_sem,
    local_sem,
    send,
    recv,
    pass_send,
    pass_recv,
):
    me = lax.axis_index("expert")
    enter(8, me)
    dispatch = Dispatch(me, chip_order, slots, landing, local_sem.at[0], send, recv, pass_send, pass_recv)
    dispatch.start_local()
    dispatch.start((0, 1, 2, 3))
    block = landing.shape[1]
    width = stage.shape[1]
    parts = landing.shape[2] // width

    def span_of(step):
        return pl.ds(pl.multiple_of(chip_order(me // 2, step) * block, 16), block)

    def act_copy(step):
        return pltpu.make_async_copy(
            act_hbm.at[span_of(step), :],
            act.at[step // 2, pl.ds(step % 2 * block, block), :],
            act_sem.at[step],
        )

    def rows_copy(step):
        chip = chip_order(me // 2, step)
        return pltpu.make_async_copy(landing.at[chip], rows_out.at[chip], rows_sem.at[step])

    def stage_copy(part):
        slot = lax.rem(part, 2)
        span = pl.ds(pl.multiple_of(part * width, 16), width)
        return pltpu.make_async_copy(stage.at[slot], grad_out.at[span, :], stage_sem.at[slot])

    for step in range(4):
        act_copy(step).start()
    for pair in range(2):
        steps = (2 * pair, 2 * pair + 1)
        for step in steps:
            dispatch.arrive(step)
        chips = [dispatch.ready(step) for step in steps]
        for step in steps:
            rows_copy(step).start()
            act_copy(step).wait()

        def one(part, carry, pair=pair, chips=chips):
            columns = pl.ds(pl.multiple_of(part * width, 128), width)
            rows = jnp.concatenate([landing[chip, :, columns] for chip in chips], axis=0)
            turned = rows.astype(jnp.float32).T.astype(jnp.bfloat16)
            product = dot_nn(turned, act[pair])
            span = pl.ds(pl.multiple_of(part * width, 16), width)
            if pair == 0:
                total[span, :] = product
                return carry

            @pl.when(part >= 2)
            def _():
                stage_copy(part - 2).wait()

            stage[lax.rem(part, 2)] = (total[span, :] + product).astype(jnp.bfloat16)
            stage_copy(part).start()
            return carry

        lax.fori_loop(0, parts, one, 0)
    for part in (parts - 2, parts - 1):
        stage_copy(part).wait()
    for step in range(4):
        rows_copy(step).wait()
    dispatch.sent((0, 1, 2, 3))
    dispatch.passed_on()


def send_rows(slots, act):
    chips, capacity, depth = slots.shape
    rows, hidden_units = act.shape
    block = 2 * capacity
    width = min(256, depth // 2)
    any_space = pl.BlockSpec(memory_space=pl.ANY)
    bf = jnp.bfloat16
    dma = pltpu.SemaphoreType.DMA
    return pl.pallas_call(
        send_rows_body,
        in_specs=[any_space] * 2,
        out_specs=[any_space] * 2,
        out_shape=[
            jax.ShapeDtypeStruct((chips, block, depth), bf),
            jax.ShapeDtypeStruct((depth, hidden_units), bf),
        ],
        scratch_shapes=[
            pltpu.VMEM((chips, block, depth), bf),
            pltpu.VMEM((2, 2 * block, hidden_units), bf),
            pltpu.VMEM((depth, hidden_units), jnp.float32),
            pltpu.VMEM((2, width, hidden_units), bf),
            dma((4,)),
            dma((4,)),
            dma((2,)),
            dma((1,)),
            dma((8,)),
            dma((8,)),
            dma((8,)),
            dma((8,)),
        ],
        compiler_params=pltpu.CompilerParams(
            collective_id=2, has_side_effects=True, vmem_limit_bytes=VMEM_BYTES
        ),
        name="send_rows",
    )(slots, act)


def ffn_backward_body(
    chunk,
    grad_rows,
    gate_in,
    up_in,
    gate_hbm,
    up_hbm,
    down_hbm,
    dgate_out,
    dup_out,
    back,
    gate,
    up,
    down,
    grad,
    pre_stage,
    pair,
    kept,
    passing,
    passed,
    total,
    weight_sem,
    grad_sem,
    stage_sem,
    pair_sem,
    local_sem,
    swap_send,
    swap_recv,
    out_send,
    out_recv,
):
    me = lax.axis_index("expert")
    enter(8, me)
    collect = Collect(
        me, far_order, (3,), kept, passing, passed, total, back, local_sem.at[0], swap_send, swap_recv, out_send, out_recv
    )
    loads = [
        pltpu.make_async_copy(source, target, weight_sem.at[n])
        for n, (source, target) in enumerate(((down_hbm, down), (gate_hbm, gate), (up_hbm, up)))
    ]
    block = grad.shape[1]
    hidden_units = gate.shape[1]
    chunks = hidden_units // chunk
    half = back.shape[2] // 2
    width = min(512, half)

    def span_of(chip):
        return pl.ds(pl.multiple_of(chip * block, 16), block)

    def grad_copy(step):
        return pltpu.make_async_copy(
            grad_rows.at[span_of(collect.block(step)), :], grad.at[step % 2], grad_sem.at[step % 2]
        )

    def stage_copies(chip, part, slot):
        columns = pl.ds(pl.multiple_of(part * chunk, 128), chunk)
        return [
            pltpu.make_async_copy(
                source.at[span_of(chip), columns], pre_stage.at[slot, n], stage_sem.at[slot, n]
            )
            for n, source in enumerate((gate_in, up_in))
        ]

    def pair_copies(chip):
        return [
            pltpu.make_async_copy(pair.at[n], out.at[span_of(chip), :], pair_sem.at[n])
            for n, out in enumerate((dgate_out, dup_out))
        ]

    grad_copy(0).start()
    loads[0].start()
    for copy in stage_copies(collect.block(0), 0, 0):
        copy.start()
    loads[1].start()
    loads[2].start()
    loads[0].wait()
    for step in range(4):
        chip = collect.block(step)
        grad_copy(step).wait()
        if step < 3:
            grad_copy(step + 1).start()
        if step > 0:
            for copy in pair_copies(collect.block(step - 1)):
                copy.wait()

        def hidden_part(part, carry, chip=chip, step=step):
            slot = lax.rem(part, 2)
            columns = pl.ds(pl.multiple_of(part * chunk, 128), chunk)
            for copy in stage_copies(chip, part, slot):
                copy.wait()

            @pl.when(part + 1 < chunks)
            def _():
                for copy in stage_copies(chip, part + 1, 1 - slot):
                    copy.start()

            upstream = dot_nn(grad[step % 2], down[:, columns])
            gated = pre_stage[slot, 0].astype(jnp.float32)
            raised = pre_stage[slot, 1].astype(jnp.float32)
            sigmoid = jax.nn.sigmoid(gated)
            scaled = upstream * sigmoid
            pair[0, :, columns] = (scaled * raised * (1.0 + gated * (1.0 - sigmoid))).astype(jnp.bfloat16)
            pair[1, :, columns] = (scaled * gated).astype(jnp.bfloat16)
            return carry

        lax.fori_loop(0, chunks, hidden_part, 0)
        for copy in pair_copies(chip):
            copy.start()
        if step < 3:
            for copy in stage_copies(collect.block(step + 1), 0, 0):
                copy.start()
        if step == 0:
            loads[1].wait()
            loads[2].wait()
        else:
            collect.settle(step - 1)
        core = collect.core

        def product(at):
            return dot_nt(pair[0], gate[pl.ds(at, width), :]) + dot_nt(pair[1], up[pl.ds(at, width), :])

        def far_part(part, carry, step=step):
            at = pl.multiple_of((1 - core) * half + part * width, 128)
            columns = pl.ds(pl.multiple_of(part * width, 128), width)
            passing[step % 2, :, columns] = product(at).astype(jnp.bfloat16)
            return carry

        def near_part(part, carry, step=step):
            at = pl.multiple_of(core * half + part * width, 128)
            kept[:, pl.ds(pl.multiple_of(part * width, 128), width)] = product(at)
            return carry

        if step >= 2:
            collect.swap(step - 2).wait_send()
        lax.fori_loop(0, half // width, far_part, 0)
        collect.swap(step).start()
        lax.fori_loop(0, half // width, near_part, 0)
    collect.settle(3)
    for copy in pair_copies(collect.block(3)):
        copy.wait()
    collect.finish()


def ffn_backward(grad_rows, gate_pre, up_pre, gate_weight, up_weight, down_weight, capacity):
    rows, depth = grad_rows.shape
    hidden_units = gate_weight.shape[1]
    block = 2 * capacity
    chips = rows // block
    chunk = hidden_units // 2 if hidden_units % 256 == 0 else 128
    half = depth // 2
    any_space = pl.BlockSpec(memory_space=pl.ANY)
    bf = jnp.bfloat16
    dma = pltpu.SemaphoreType.DMA
    return pl.pallas_call(
        functools.partial(ffn_backward_body, chunk),
        in_specs=[any_space] * 6,
        out_specs=[any_space] * 3,
        out_shape=[
            jax.ShapeDtypeStruct((rows, hidden_units), bf),
            jax.ShapeDtypeStruct((rows, hidden_units), bf),
            jax.ShapeDtypeStruct((chips, capacity, depth), bf),
        ],
        scratch_shapes=[
            pltpu.VMEM((depth, hidden_units), bf),
            pltpu.VMEM((depth, hidden_units), bf),
            pltpu.VMEM((depth, hidden_units), bf),
            pltpu.VMEM((2, block, depth), bf),
            pltpu.VMEM((2, 2, block, chunk), bf),
            pltpu.VMEM((2, block, hidden_units), bf),
            pltpu.VMEM((block, half), jnp.float32),
            pltpu.VMEM((2, block, half), bf),
            pltpu.VMEM((chips, block, half), bf),
            pltpu.VMEM((chips, block, half), bf),
            dma((3,)),
            dma((2,)),
            dma((2, 2)),
            dma((2,)),
            dma((1,)),
            dma((4,)),
            dma((4,)),
            dma((8,)),
            dma((8,)),
        ],
        compiler_params=pltpu.CompilerParams(
            collective_id=3, has_side_effects=True, vmem_limit_bytes=VMEM_BYTES
        ),
        name="ffn_backward",
    )(grad_rows, gate_pre, up_pre, gate_weight, up_weight, down_weight)


def send_slots_body(
    slots, rows_hbm, grads_hbm, landing, grad_out, rows_v, grads_v, stage, load_sem, stage_sem, local_sem, send, recv
):
    me = lax.axis_index("expert")
    enter(8, me)

    def outgoing(offset):
        target = lax.rem(me + offset, 8)
        return remote(slots.at[target], landing.at[me], send.at[offset], recv.at[offset], target)

    local = pltpu.make_async_copy(slots.at[me], landing.at[me], local_sem)
    for offset in range(1, 8):
        outgoing(offset).start()
    local.start()
    loads = [
        pltpu.make_async_copy(source, target, load_sem.at[n])
        for n, (source, target) in enumerate(((rows_hbm, rows_v), (grads_hbm, grads_v)))
    ]
    for load in loads:
        load.start()
    for load in loads:
        load.wait()
    width = stage.shape[1]
    blocks = rows_v.shape[1] // width

    def stage_copy(block):
        slot = lax.rem(block, 2)
        span = pl.ds(pl.multiple_of(block * width, 16), width)
        return pltpu.make_async_copy(stage.at[slot], grad_out.at[span, :], stage_sem.at[slot])

    def one(block, carry):
        @pl.when(block >= 2)
        def _():
            stage_copy(block - 2).wait()

        columns = pl.ds(pl.multiple_of(block * width, 128), width)
        turned = rows_v[:, columns].astype(jnp.float32).T.astype(jnp.bfloat16)
        stage[lax.rem(block, 2)] = dot_nn(turned, grads_v[...]).astype(jnp.bfloat16)
        stage_copy(block).start()
        return carry

    lax.fori_loop(0, blocks, one, 0)
    for block in (blocks - 2, blocks - 1):
        stage_copy(block).wait()
    local.wait()
    for offset in range(1, 8):
        outgoing(offset).wait_send()
        place = landing.at[lax.rem(me + 8 - offset, 8)]
        remote(place, place, send.at[offset], recv.at[offset], me).wait_recv()


def send_slots(slots, rows, grads):
    total, depth = rows.shape
    hidden_units = grads.shape[1]
    width = min(256, depth // 2)
    any_space = pl.BlockSpec(memory_space=pl.ANY)
    bf = jnp.bfloat16
    dma = pltpu.SemaphoreType.DMA
    return pl.pallas_call(
        send_slots_body,
        in_specs=[any_space] * 3,
        out_specs=[any_space] * 2,
        out_shape=[
            jax.ShapeDtypeStruct(slots.shape, bf),
            jax.ShapeDtypeStruct((depth, hidden_units), bf),
        ],
        scratch_shapes=[
            pltpu.VMEM((total, depth), bf),
            pltpu.VMEM((total, hidden_units), bf),
            pltpu.VMEM((2, width, hidden_units), bf),
            dma((2,)),
            dma((2,)),
            dma,
            dma((8,)),
            dma((8,)),
        ],
        compiler_params=pltpu.CompilerParams(
            collective_id=5, has_side_effects=True, vmem_limit_bytes=VMEM_BYTES
        ),
        name="send_slots",
    )(slots, rows, grads)


def merge_return_body(
    dp_axis,
    plan_hbm,
    slots_hbm,
    grads_hbm,
    weight_hbm,
    back,
    plan,
    slots,
    grads,
    weight,
    kept,
    passing,
    passed,
    total,
    load_sem,
    local_sem,
    swap_send,
    swap_recv,
    out_send,
    out_recv,
):
    me = lax.axis_index("expert")
    replica = lax.axis_index(dp_axis)
    enter(8, me)
    loads = [
        pltpu.make_async_copy(source, target, load_sem.at[n])
        for n, (source, target) in enumerate(
            ((plan_hbm, plan), (slots_hbm, slots), (grads_hbm, grads), (weight_hbm, weight))
        )
    ]
    for load in loads:
        load.start()
    collect = Collect(
        me, far_order, (3,), kept, passing, passed, total, back, local_sem.at[0], swap_send, swap_recv, out_send, out_recv
    )
    rows, half = collect.rows, collect.half
    parts, ck = weight.shape[0], weight.shape[2] // 2
    values_at = grads.shape[1] // 2
    width = min(512, half)
    for load in loads:
        load.wait()
    for step in range(4):
        chip = collect.block(step)
        span = pl.ds(pl.multiple_of(chip * 2 * rows, 16), 2 * rows)

        def product(at, chip=chip, span=span):
            columns = pl.ds(at, width)
            result = jnp.concatenate(
                [dot_nn(plan[2 * chip + n], slots[2 * chip + n, :, columns]) for n in range(2)], axis=0
            )
            for part in range(parts):
                low = lax.rem(replica, 2) + (part % 2) * (1 - 2 * lax.rem(replica, 2))
                high = replica // 2 + (part // 2) * (1 - 2 * (replica // 2))
                at_keys = pl.multiple_of((2 * high + low) * ck, 128)
                result += dot_nt(grads[span, pl.ds(at_keys, ck)], weight[part, columns, :ck])
                result += dot_nt(grads[span, pl.ds(values_at + at_keys, ck)], weight[part, columns, ck:])
            return result

        def far_part(part, carry, step=step, product=product):
            at = pl.multiple_of((1 - collect.core) * half + part * width, 128)
            columns = pl.ds(pl.multiple_of(part * width, 128), width)
            passing[step % 2, :, columns] = product(at).astype(jnp.bfloat16)
            return carry

        def near_part(part, carry, product=product):
            at = pl.multiple_of(collect.core * half + part * width, 128)
            kept[:, pl.ds(pl.multiple_of(part * width, 128), width)] = product(at)
            return carry

        if step >= 2:
            collect.swap(step - 2).wait_send()
        lax.fori_loop(0, half // width, far_part, 0)
        collect.swap(step).start()
        if step > 0:
            collect.settle(step - 1)
        lax.fori_loop(0, half // width, near_part, 0)
    collect.settle(3)
    collect.finish()


def merge_return(plan, slots, grads, weights):
    sources, rows, capacity = plan.shape
    parts, depth, columns = weights.shape
    tokens = sources * rows
    half = depth // 2
    any_space = pl.BlockSpec(memory_space=pl.ANY)
    bf = jnp.bfloat16
    dma = pltpu.SemaphoreType.DMA
    return pl.pallas_call(
        functools.partial(merge_return_body, "dp"),
        in_specs=[any_space] * 4,
        out_specs=any_space,
        out_shape=jax.ShapeDtypeStruct((sources // 2, rows, depth), bf),
        scratch_shapes=[
            pltpu.VMEM(plan.shape, bf),
            pltpu.VMEM(slots.shape, bf),
            pltpu.VMEM(grads.shape, bf),
            pltpu.VMEM(weights.shape, bf),
            pltpu.VMEM((2 * rows, half), jnp.float32),
            pltpu.VMEM((2, 2 * rows, half), bf),
            pltpu.VMEM((sources // 2, 2 * rows, half), bf),
            pltpu.VMEM((sources // 2, 2 * rows, half), bf),
            dma((4,)),
            dma((1,)),
            dma((4,)),
            dma((4,)),
            dma((8,)),
            dma((8,)),
        ],
        compiler_params=pltpu.CompilerParams(
            collective_id=6, has_side_effects=True, vmem_limit_bytes=VMEM_BYTES
        ),
        name="merge_return",
    )(plan, slots, grads, weights)


def attention_send_body(
    scale,
    query_hbm,
    sibling_hbm,
    key_hbm,
    value_hbm,
    out_weight_hbm,
    key_info,
    query_info,
    own_out,
    sibling_out,
    rows_out,
    back,
    lse_ref,
    queries,
    siblings,
    keys_v,
    values_v,
    out_weight,
    bias_ref,
    flipped,
    own_stage,
    sibling_stage,
    arrived,
    rows_stage,
    sending,
    load_sem,
    own_sem,
    sibling_sem,
    rows_sem,
    local_sem,
    swap_send,
    swap_recv,
    out_send,
    out_recv,
):
    me = lax.axis_index("expert")
    chip, core = me // 2, lax.rem(me, 2)
    enter(8, me)
    half = keys_v.shape[1]
    rows = own_stage.shape[1]
    keys = keys_v.shape[0] // GROUPS
    heads = half // HEAD
    capacity = back.shape[1]
    own_columns = pl.ds(pl.multiple_of(core * half, 128), half)
    far_columns = pl.ds(pl.multiple_of((1 - core) * half, 128), half)
    loads = [
        pltpu.make_async_copy(source, target, load_sem.at[n])
        for n, (source, target) in enumerate(
            (
                (value_hbm, values_v),
                (key_hbm, keys_v),
                (query_hbm.at[:, own_columns], queries),
                (sibling_hbm, siblings),
                (out_weight_hbm, out_weight),
            )
        )
    ]
    for load in loads:
        load.start()
    fill_bias(bias_ref, key_info, query_info, keys)
    loads[0].wait()

    def flip(head, carry):
        lanes = pl.ds(pl.multiple_of(head * HEAD, HEAD), HEAD)
        for block in range(GROUPS):
            values = values_v[pl.ds(block * keys, keys), lanes].astype(jnp.float32)
            flipped[head, block] = values.T.astype(jnp.bfloat16)
        return carry

    lax.fori_loop(0, heads, flip, 0)
    for load in loads[1:4]:
        load.wait()

    def group_of(step):
        return chip_order(chip, 3 - step)

    def span_of(step):
        return pl.ds(pl.multiple_of(group_of(step) * rows, 16), rows)

    def own_copy(step):
        return pltpu.make_async_copy(own_stage.at[step], own_out.at[span_of(step), :], own_sem.at[step])

    def sibling_copy(step):
        return pltpu.make_async_copy(
            sibling_stage.at[step], sibling_out.at[span_of(step), :], sibling_sem.at[step]
        )

    def rows_copy(step):
        return pltpu.make_async_copy(
            rows_stage.at[step], rows_out.at[span_of(step), :], rows_sem.at[step]
        )

    def swap(step):
        return remote(
            sibling_stage.at[step], arrived.at[step], swap_send.at[step], swap_recv.at[step], me + 1 - 2 * core
        )

    def outgoing(step, n):
        source = 2 * group_of(step) + n
        offset = lax.rem(source - me + 8, 8)
        return remote(sending.at[step, n], back.at[me], out_send.at[offset], out_recv.at[offset], source)

    def local(step, n):
        return pltpu.make_async_copy(sending.at[step, n], back.at[me], local_sem)

    def each(step, own, other):
        for n in range(2):
            if step < 3:
                other(n)
                continue

            @pl.when(core == n)
            def _(n=n):
                own(n)

            @pl.when(core != n)
            def _(n=n):
                other(n)

    def attend(step):
        group = group_of(step)
        first_block = group * (group + 1) // 2
        span = span_of(step)

        def head_pair(pair, carry):
            lanes = [pl.ds(pl.multiple_of((2 * pair + n) * HEAD, HEAD), HEAD) for n in range(2)]
            parts = [jnp.concatenate([queries[span, lane], siblings[span, lane]], axis=0) for lane in lanes]

            def one(block, state):
                at = pl.multiple_of(block * keys, 16)
                bias = bias_ref[first_block + block]
                result = []
                for n in range(2):
                    top, total, mixed = state[3 * n : 3 * n + 3]
                    scores = dot_nt(keys_v[pl.ds(at, keys), lanes[n]], parts[n]) * scale + bias
                    new_top = jnp.maximum(top, jnp.max(scores, axis=0, keepdims=True))
                    fade = jnp.exp2(top - new_top)
                    probs = jnp.exp2(scores - new_top)
                    total = total * fade + jnp.sum(probs, axis=0, keepdims=True)
                    mixed = mixed * fade + dot_nn(flipped[2 * pair + n, block], probs.astype(jnp.bfloat16))
                    result += [new_top, total, mixed]
                return tuple(result)

            start = (
                jnp.full((1, 2 * rows), -1e30, jnp.float32),
                jnp.zeros((1, 2 * rows), jnp.float32),
                jnp.zeros((HEAD, 2 * rows), jnp.float32),
            ) * 2
            final = lax.fori_loop(0, group + 1, one, start)
            for n in range(2):
                top, total, mixed = final[3 * n : 3 * n + 3]
                lse_ref[2 * pair + n, group] = top + jnp.log2(total)
                result = (mixed / total).T.astype(jnp.bfloat16)
                own_stage[step, :, lanes[n]] = result[:rows]
                sibling_stage[step, :, lanes[n]] = result[rows:]
            return carry

        lax.fori_loop(0, heads // 2, head_pair, 0)
        swap(step).start()
        own_copy(step).start()
        sibling_copy(step).start()

    def settle(step):
        swap(step).wait_recv()
        rows_stage[step, :, own_columns] = own_stage[step]
        rows_stage[step, :, far_columns] = arrived[step]
        rows_copy(step).start()
        width = 512
        for at in range(0, back.shape[2], min(width, back.shape[2])):
            columns = pl.ds(at, min(width, back.shape[2]))
            product = dot_nt(rows_stage[step], out_weight[columns, :])
            for n in range(2):
                part = product[n * capacity : (n + 1) * capacity]
                sending[step, n, :, columns] = part.astype(jnp.bfloat16)
        each(step, lambda n: local(step, n).start(), lambda n: outgoing(step, n).start())

    for step in range(4):
        attend(step)
        if step == 1:
            loads[4].wait()
        if step > 0:
            settle(step - 1)
    settle(3)
    for step in range(4):
        swap(step).wait_send()
        own_copy(step).wait()
        sibling_copy(step).wait()
        rows_copy(step).wait()
        each(step, lambda n, step=step: local(step, n).wait(), lambda n, step=step: outgoing(step, n).wait_send())
    for offset in range(1, 8):
        place = back.at[lax.rem(me + 8 - offset, 8)]
        remote(place, place, out_send.at[offset], out_recv.at[offset], me).wait_recv()


def attention_send(queries, siblings, keys_all, values_all, out_weight, key_info, query_info, capacity):
    total_rows, width = queries.shape
    tokens, half = keys_all.shape
    depth = out_weight.shape[0]
    rows, keys, heads = total_rows // GROUPS, tokens // GROUPS, half // HEAD
    any_space = pl.BlockSpec(memory_space=pl.ANY)
    here = pl.BlockSpec(memory_space=pltpu.VMEM)
    bf = jnp.bfloat16
    dma = pltpu.SemaphoreType.DMA
    return pl.pallas_call(
        functools.partial(attention_send_body, HEAD ** (-0.5) * LOG2E),
        in_specs=[any_space] * 5 + [here] * 2,
        out_specs=[any_space] * 4 + [here],
        out_shape=[
            jax.ShapeDtypeStruct((total_rows, half), bf),
            jax.ShapeDtypeStruct((total_rows, half), bf),
            jax.ShapeDtypeStruct((total_rows, width), bf),
            jax.ShapeDtypeStruct((8, capacity, depth), bf),
            jax.ShapeDtypeStruct((heads, GROUPS, 1, 2 * rows), jnp.float32),
        ],
        scratch_shapes=[
            pltpu.VMEM((total_rows, half), bf),
            pltpu.VMEM((total_rows, half), bf),
            pltpu.VMEM((tokens, half), bf),
            pltpu.VMEM((tokens, half), bf),
            pltpu.VMEM(out_weight.shape, bf),
            pltpu.VMEM((GROUPS * (GROUPS + 1) // 2, keys, 2 * rows), jnp.float32),
            pltpu.VMEM((heads, GROUPS, HEAD, keys), bf),
            pltpu.VMEM((GROUPS, rows, half), bf),
            pltpu.VMEM((GROUPS, rows, half), bf),
            pltpu.VMEM((GROUPS, rows, half), bf),
            pltpu.VMEM((GROUPS, rows, width), bf),
            pltpu.VMEM((GROUPS, 2, capacity, depth), bf),
            dma((5,)),
            dma((GROUPS,)),
            dma((GROUPS,)),
            dma((GROUPS,)),
            dma,
            dma((GROUPS,)),
            dma((GROUPS,)),
            dma((8,)),
            dma((8,)),
        ],
        compiler_params=pltpu.CompilerParams(
            collective_id=4, has_side_effects=True, vmem_limit_bytes=VMEM_BYTES
        ),
        name="attention_send",
    )(queries, siblings, keys_all, values_all, out_weight, key_info, query_info)


D = 2048
HEADS = 16
ATT_EXPERTS = 8
FFN_EXPERTS = 4
TRUNK = 1024
SEG = 96
TREE_LEN = 2176
NODES = 13

epsilon = 1e-06
highest = lax.Precision.HIGHEST
bf16 = jnp.bfloat16
f32 = jnp.float32


def tree_layout(places):
    after_trunk = places - TRUNK
    after_branch = after_trunk - 4 * SEG
    segments = jnp.where(
        places < TRUNK,
        0,
        jnp.where(after_branch < 0, 1 + after_trunk // SEG, 5 + after_branch // SEG),
    )
    depths = jnp.where(
        places < TRUNK,
        places,
        jnp.where(after_branch < 0, TRUNK + after_trunk % SEG, TRUNK + SEG + after_branch % SEG),
    )
    return (segments.astype(jnp.int32), depths.astype(jnp.int32))


def rotation_tables(depths):
    half_size = HEAD // 2
    frequency = 10000.0 ** (-jnp.arange(half_size, dtype=f32) * 2.0 / HEAD)
    angles = depths.astype(f32)[:, None] * frequency[None, :]
    cosine, sine = jnp.cos(angles), jnp.sin(angles)
    cosines = jnp.concatenate([cosine, cosine], axis=1)
    forward = jnp.concatenate([-sine, sine], axis=1)
    return (cosines, forward), (cosines, -forward)


def lookup(table, indices):
    nodes = jnp.arange(NODES, dtype=jnp.int32)
    return jnp.sum(jnp.where(indices[:, None] == nodes[None, :], table[None, :], 0), axis=1)


def running_count(chosen):
    rows = chosen.shape[-1]
    index = jnp.arange(rows, dtype=jnp.int32)
    upto = (index[:, None] <= index[None, :]).astype(bf16)
    return jnp.dot(chosen.astype(bf16), upto, preferred_element_type=f32).astype(jnp.int32) - 1


def source_plan(routes, expert, capacity):
    chosen = jnp.any(routes == expert, axis=2)
    ranking = running_count(chosen)
    slots = jnp.arange(capacity, dtype=jnp.int32)
    return chosen[:, None, :] & (ranking[:, None, :] == slots[None, :, None])


def token_picks(routes, experts, capacity):
    labels = jnp.arange(experts, dtype=jnp.int32)
    hits = routes.T[:, None, :] == labels[None, :, None]
    ranking = running_count(hits[0] | hits[1])
    slots = jnp.arange(capacity, dtype=jnp.int32)
    picks = hits[:, :, None, :] & (ranking[None, :, None, :] == slots[None, None, :, None])
    return picks.astype(bf16), hits[0].T.astype(f32), hits[1].T.astype(f32)


def fill_slots(picks, pair):
    return jnp.einsum("kecr,krd->ecd", picks, pair, preferred_element_type=f32).astype(bf16)


def read_slots(picks, slots):
    return jnp.einsum("kecr,ecd->krd", picks, slots, preferred_element_type=f32)


def gate_values(hidden, router, first, second):
    logits = jnp.dot(hidden.astype(f32), router, precision=highest)
    picked = jnp.stack([jnp.sum(logits * first, axis=1), jnp.sum(logits * second, axis=1)], axis=1)
    return jax.nn.softmax(picked, axis=1)


def router_grads(hidden, router, gates, first, second, picked_grad):
    logit_pick = gates * (picked_grad - jnp.sum(gates * picked_grad, axis=1, keepdims=True))
    logit_grad = logit_pick[:, 0:1] * first + logit_pick[:, 1:2] * second
    router_grad = jnp.dot(hidden.astype(f32).T, logit_grad, precision=highest)
    hidden_grad = jnp.dot(logit_grad, router.T, precision=highest)
    return (router_grad, hidden_grad)


def rms_parts(values):
    inverse = lax.rsqrt(jnp.mean(values * values, axis=-1, keepdims=True) + epsilon)
    return (values * inverse, inverse)


def norm_back(grad_normed, normed, inverse):
    return inverse * (grad_normed - normed * jnp.mean(grad_normed * normed, axis=-1, keepdims=True))


def pair_grads(gates, branches, upstream):
    gate_grad = jnp.stack([jnp.sum(upstream * branches[k], axis=1) for k in range(2)], axis=1)
    scaled = jnp.stack([gates[:, k : k + 1] * upstream for k in range(2)]).astype(bf16)
    return gate_grad, scaled


def exchange(slots):
    return lax.all_to_all(slots, "expert", split_axis=0, concat_axis=0, tiled=True)


def shift(values, step, size, devices):
    moves = [(i, i // size * size + (i % size + step) % size) for i in range(devices)]
    return lax.ppermute(values, "expert", moves)


def group_gather(rows, size, devices):
    return jnp.concatenate([rows] + [shift(rows, step, size, devices) for step in range(1, size)])


def group_reduce(partial, size, devices):
    parts = partial.reshape(size, -1, partial.shape[1])
    total = parts[0].astype(f32)
    for step in range(1, size):
        total = total + shift(parts[step], -step, size, devices).astype(f32)
    return total.astype(bf16)


def spread_over_replicas(block, my_replica, replicas):
    if replicas != 4:
        return lax.all_gather(block, "dp", axis=0), jnp.arange(replicas, dtype=jnp.int32)
    across, along = ([(i, i ^ n) for i in range(4)] for n in (1, 2))
    first, second = lax.ppermute(block, "dp", across), lax.ppermute(block, "dp", along)
    cut = block.shape[0] // 2
    upper, lower = lax.ppermute(second[:cut], "dp", across), lax.ppermute(first[cut:], "dp", along)
    blocks = jnp.stack([block, first, second, jnp.concatenate([upper, lower])])
    return blocks, my_replica ^ jnp.arange(4, dtype=jnp.int32)


def dot_tn(left, right):
    return lax.dot_general(left, right, (((0,), (0,)), ((), ())), preferred_element_type=f32)


def body(
    tokens,
    teacher,
    att_routes,
    ffn_routes,
    parent,
    valid,
    gain_one,
    kv_weight,
    att_router,
    q_weight,
    o_weight,
    gain_two,
    ffn_router,
    gate_weight,
    up_weight,
    down_weight,
):
    row_count = tokens.shape[0]
    devices, replicas = lax.axis_size("expert"), lax.axis_size("dp")
    my_index, my_replica = lax.axis_index("expert"), lax.axis_index("dp")
    core = my_index % 2
    att_copies, ffn_copies = devices // ATT_EXPERTS, devices // FFN_EXPERTS
    att_capacity, ffn_capacity = row_count * 13 // 40, row_count * 13 // 20
    token_count = row_count * devices
    half = HEADS * HEAD // 2
    assert token_count == TREE_LEN * parent.shape[0] and parent.shape[0] == 1
    pair = [(i, i ^ 1) for i in range(devices)]
    own_places = my_index * row_count + jnp.arange(row_count, dtype=jnp.int32)

    x_in = tokens.astype(f32)
    normed_one, inverse_one = rms_parts(x_in)
    hidden = (normed_one * gain_one).astype(bf16)
    weight_rows = kv_weight.shape[0]
    piece = half // replicas
    kv_share = lax.dynamic_slice_in_dim(
        kv_weight.reshape(weight_rows, 4, replicas, piece), my_replica, 1, 2
    )
    kv_share = (
        kv_share.reshape(weight_rows, 2, 2, piece).transpose(0, 2, 1, 3).reshape(weight_rows, 4 * piece)
    )
    kv_gathered = lax.all_gather(kv_share, "expert", axis=0)
    kv_gathered, hidden_sent = lax.optimization_barrier((kv_gathered, hidden))
    hidden_all = lax.all_gather(hidden_sent, "expert", axis=0)
    kv_half = lax.dynamic_slice_in_dim(kv_gathered, core * 2 * piece, 2 * piece, 2).reshape(D, 2 * piece)
    kv_half, routes_sent = lax.optimization_barrier((kv_half, att_routes))
    kv_blocks, block_order = spread_over_replicas(kv_half, my_replica, replicas)
    all_routes = lax.all_gather(routes_sent, "expert", axis=0)

    tree_places = jnp.arange(token_count, dtype=jnp.int32)
    tree_segments, tree_depths = tree_layout(tree_places)
    key_forward, key_backward = rotation_tables(tree_depths)
    key_info = jnp.pad(jnp.stack([tree_places, tree_segments], axis=1), ((0, 0), (0, 6)))
    experts_here = [my_index // att_copies]
    if att_copies == 1:
        experts_here.append(my_index ^ 1)
    plans = [source_plan(all_routes, expert, att_capacity) for expert in experts_here]
    slot_tables, query_parts = [], []
    for plan in plans:
        places = jnp.sum(
            jnp.where(plan, tree_places.reshape(devices, 1, row_count), 0), axis=2
        ).reshape(-1)
        segments, depths = tree_layout(places)
        parents = lookup(parent[0], segments)
        grands = lookup(parent[0], parents)
        query_parts.append(jnp.stack([places, segments, parents, grands]).reshape(4, GROUPS, -1))
        slot_tables.append(rotation_tables(depths))
    query_info = jnp.concatenate(query_parts, axis=2).transpose(1, 0, 2)
    own_plan = plans[0].astype(bf16)
    att_picks, att_first, att_second = token_picks(att_routes, ATT_EXPERTS, att_capacity)
    att_gates = gate_values(hidden, att_router, att_first, att_second)
    ffn_picks, ffn_first, ffn_second = token_picks(ffn_routes, FFN_EXPERTS, ffn_capacity)
    prepared = (key_forward, key_backward, key_info, slot_tables, query_info, own_plan, att_picks, att_gates, ffn_picks)
    hidden_all, kv_blocks, prepared = lax.optimization_barrier((hidden_all, kv_blocks, prepared))
    key_forward, key_backward, key_info, slot_tables, query_info, own_plan, att_picks, att_gates, ffn_picks = prepared

    queries, query_inputs = project_queries(own_plan, hidden_all, q_weight, slot_tables[0][0])
    keys_all, values_all = project_keys_values(hidden_all, kv_blocks, key_forward, block_order)

    def far_half(values):
        return lax.ppermute(
            lax.dynamic_slice_in_dim(values, (1 - core) * half, half, 1), "expert", pair
        )

    def join_halves(mine, sibling):
        other = lax.ppermute(sibling, "expert", pair)
        return jnp.where(
            core == 0,
            jnp.concatenate([mine, other], axis=1),
            jnp.concatenate([other, mine], axis=1),
        )

    heads = half // HEAD
    query_sets = [queries]
    starts = jnp.zeros((2,), jnp.int32)
    if att_copies == 1:
        query_sets.append(far_half(queries))
        starts = jnp.stack([core * heads, 0]).astype(jnp.int32)
    fused = devices == 8 and replicas == 4 and att_copies == 1 and ffn_copies == 2 and ffn_capacity % 16 == 0
    if fused:
        *att_outs, att_rows, att_back, lse = attention_send(
            *query_sets, keys_all, values_all, o_weight, key_info, query_info, att_capacity
        )
        att_everywhere = lax.all_gather(att_rows, "dp", axis=0, tiled=True)
    else:
        *att_outs, lse = attention_forward(
            query_sets, starts // 2, keys_all, values_all, key_info, query_info, heads
        )
        att_rows = join_halves(*att_outs) if att_copies == 1 else att_outs[0]
        att_partial = lax.dot_general(
            att_rows, o_weight, (((1,), (1,)), ((), ())), preferred_element_type=f32
        ).astype(bf16)
        att_back = exchange(att_partial.reshape(devices, att_capacity, D))
    if att_copies > 1:
        att_back = (
            att_back.astype(f32).reshape(ATT_EXPERTS, att_copies, att_capacity, D).sum(axis=1).astype(bf16)
        )
    att_branches = read_slots(att_picks, att_back)
    x_mid = x_in + att_gates[:, 0:1] * att_branches[0] + att_gates[:, 1:2] * att_branches[1]

    normed_two, inverse_two = rms_parts(x_mid)
    hidden_two = (normed_two * gain_two).astype(bf16)
    ffn_gates = gate_values(hidden_two, ffn_router, ffn_first, ffn_second)

    def to_experts(slots):
        rows = exchange(slots.reshape(devices, ffn_capacity // ffn_copies, D))
        return group_gather(rows.reshape(-1, D), ffn_copies, devices)

    def to_tokens(partial):
        rows = group_reduce(partial.astype(bf16), ffn_copies, devices)
        back = exchange(rows.reshape(devices, ffn_capacity // ffn_copies, D))
        return read_slots(ffn_picks, back.reshape(FFN_EXPERTS, ffn_capacity, D))

    ffn_slots = jnp.einsum(
        "ecr,rd->ecd", ffn_picks[0] + ffn_picks[1], hidden_two, preferred_element_type=f32
    ).astype(bf16)
    if fused:
        ffn_inputs, gate_pre, up_pre, activated, ffn_back = ffn_forward(
            ffn_slots, gate_weight, up_weight, down_weight
        )
        ffn_branches = read_slots(ffn_picks, ffn_back)
    else:
        ffn_inputs = to_experts(ffn_slots)
        gate_pre = jnp.dot(ffn_inputs, gate_weight, preferred_element_type=f32)
        up_pre = jnp.dot(ffn_inputs, up_weight, preferred_element_type=f32)
        sigmoid_gate = jax.nn.sigmoid(gate_pre)
        silu_gate = gate_pre * sigmoid_gate
        activated = (silu_gate * up_pre).astype(bf16)
        ffn_branches = to_tokens(
            lax.dot_general(
                activated, down_weight, (((1,), (1,)), ((), ())), preferred_element_type=f32
            )
        )
    result = x_mid + ffn_gates[:, 0:1] * ffn_branches[0] + ffn_gates[:, 1:2] * ffn_branches[1]

    tree_global = my_replica * parent.shape[0] + own_places // TREE_LEN
    tree_labels = jnp.arange(valid.shape[0], dtype=jnp.int32)
    limits = jnp.sum(
        jnp.where(tree_global[:, None] == tree_labels[None, :], valid[None, :], 0), axis=1
    )
    counted = own_places % TREE_LEN < limits
    loss_factor = valid.shape[0] * TREE_LEN / jnp.sum(valid).astype(f32)
    grad_result = jnp.where(counted[:, None], (result - teacher.astype(f32)) * loss_factor, 0.0)

    ffn_gate_grad, ffn_scaled = pair_grads(ffn_gates, ffn_branches, grad_result)
    ffn_grad_slots = fill_slots(ffn_picks, ffn_scaled)
    if fused:
        ffn_grad_slots, att_everywhere = lax.optimization_barrier((ffn_grad_slots, att_everywhere))
        grad_ffn_out, grad_down = send_rows(ffn_grad_slots, activated)
        grad_ffn_out = grad_ffn_out.reshape(-1, D)
    else:
        grad_ffn_out = to_experts(ffn_grad_slots)
        grad_down = dot_tn(grad_ffn_out, activated).astype(bf16)
    grad_ffn_out, grad_down = lax.optimization_barrier((grad_ffn_out, grad_down))
    summed_down = lax.psum_scatter(grad_down, "dp", scatter_dimension=0, tiled=True)
    if fused:
        grad_gate_pre, grad_up_pre, ffn_grad_back = ffn_backward(
            grad_ffn_out, gate_pre, up_pre, gate_weight, up_weight, down_weight, ffn_capacity
        )
        grad_gate = dot_tn(ffn_inputs, grad_gate_pre).astype(bf16)
        ffn_grad_back, grad_gate = lax.optimization_barrier((ffn_grad_back, grad_gate))
        ffn_grad_pair = read_slots(ffn_picks, ffn_grad_back)
    else:
        grad_activated = jnp.dot(grad_ffn_out, down_weight, preferred_element_type=f32)
        grad_gate_pre = (
            grad_activated * up_pre * sigmoid_gate * (1.0 + gate_pre * (1.0 - sigmoid_gate))
        ).astype(bf16)
        grad_up_pre = (grad_activated * silu_gate).astype(bf16)
        grad_ffn_in = lax.dot_general(
            grad_gate_pre, gate_weight, (((1,), (1,)), ((), ())), preferred_element_type=f32
        ) + lax.dot_general(
            grad_up_pre, up_weight, (((1,), (1,)), ((), ())), preferred_element_type=f32
        )
        grad_gate = dot_tn(ffn_inputs, grad_gate_pre).astype(bf16)
        ffn_grad_pair = to_tokens(grad_ffn_in)
    summed_gate = lax.psum_scatter(grad_gate, "dp", scatter_dimension=0, tiled=True)
    grad_ffn_router, hidden_two_extra = router_grads(
        hidden_two, ffn_router, ffn_gates, ffn_first, ffn_second, ffn_gate_grad
    )
    grad_hidden_two = ffn_grad_pair[0] + ffn_grad_pair[1] + hidden_two_extra
    grad_gain_two = jnp.sum(grad_hidden_two * normed_two, axis=0)
    grad_mid = grad_result + norm_back(grad_hidden_two * gain_two, normed_two, inverse_two)

    att_gate_grad, att_scaled = pair_grads(att_gates, att_branches, grad_mid)
    att_slots = fill_slots(att_picks, att_scaled)
    if att_copies > 1:
        att_slots = jnp.repeat(att_slots, att_copies, axis=0)
    att_slots, summed_down = lax.optimization_barrier((att_slots, summed_down))
    if fused:
        grad_att_out, grad_up = send_slots(att_slots, ffn_inputs, grad_up_pre)
        grad_att_out = grad_att_out.reshape(-1, D)
    else:
        grad_att_out = exchange(att_slots).reshape(-1, D)
        grad_up = dot_tn(ffn_inputs, grad_up_pre).astype(bf16)
        grad_att_out, grad_up = lax.optimization_barrier((grad_att_out, grad_up))
    summed_up = lax.psum_scatter(grad_up, "dp", scatter_dimension=0, tiled=True)
    grad_heads = jnp.dot(grad_att_out, o_weight, preferred_element_type=f32).astype(bf16)
    grad_heads, grad_att_out = lax.optimization_barrier((grad_heads, grad_att_out))
    grad_sets = [grad_heads]
    if att_copies == 1:
        grad_sets.append(far_half(grad_heads))
    if fused:
        share = D // replicas

        def columns_of(replica):
            return lax.dynamic_slice_in_dim(grad_att_out, replica * share, share, 1)

        grad_columns = [columns_of(my_replica)] + [
            lax.ppermute(columns_of(my_replica ^ n), "dp", [(i, i ^ n) for i in range(replicas)])
            for n in range(1, replicas)
        ]
    else:
        grad_o = dot_tn(grad_att_out, att_rows).astype(bf16)
        summed_o = lax.psum_scatter(grad_o, "dp", scatter_dimension=0, tiled=True).astype(f32)
    *grad_queries, grad_keys_values = attention_backward(
        query_sets,
        starts,
        grad_sets,
        att_outs,
        keys_all,
        values_all,
        lse,
        key_info,
        query_info,
        key_backward,
        [tables[1] for tables in slot_tables],
        heads,
    )
    grad_keys_values, summed_gate = lax.optimization_barrier((grad_keys_values, summed_gate))
    grad_query_pre = join_halves(*grad_queries) if att_copies == 1 else grad_queries[0]
    grad_kv = dot_tn(hidden_all.reshape(token_count, D), grad_keys_values).astype(bf16)
    grad_q = dot_tn(query_inputs, grad_query_pre).astype(bf16)
    summed_kv = lax.psum_scatter(grad_kv, "dp", scatter_dimension=0, tiled=True)
    summed_q = lax.psum_scatter(grad_q, "dp", scatter_dimension=0, tiled=True)
    grad_query_in = lax.dot_general(
        grad_query_pre, q_weight, (((1,), (1,)), ((), ())), preferred_element_type=f32
    ).astype(bf16)
    grad_query_in, grad_kv, grad_q, summed_up = lax.optimization_barrier(
        (grad_query_in, grad_kv, grad_q, summed_up)
    )

    merge_args = (
        own_plan.transpose(0, 2, 1),
        grad_query_in.reshape(devices, att_capacity, D),
        grad_keys_values,
        kv_blocks,
    )
    if fused:
        arrived = merge_return(*merge_args)
        arrived, grad_columns, summed_kv = lax.optimization_barrier((arrived, grad_columns, summed_kv))
        column_stack = jnp.stack(grad_columns)
        summed_o = dot_tn(
            jnp.concatenate(
                [lax.dynamic_index_in_dim(column_stack, my_replica ^ n, 0, False) for n in range(replicas)]
            ),
            att_everywhere,
        )
    else:
        merged = merge_hidden_grads(*merge_args, block_order).reshape(devices // 2, 2, row_count, D)
        kept = lax.dynamic_index_in_dim(merged, core, 1, keepdims=False)
        passed = lax.ppermute(
            lax.dynamic_index_in_dim(merged, 1 - core, 1, keepdims=False), "expert", pair
        )
        chip_sum = (kept.astype(f32) + passed.astype(f32)).astype(bf16)
        same_core = [[2 * i + c for i in range(devices // 2)] for c in range(2)]
        arrived = lax.all_to_all(
            chip_sum, "expert", split_axis=0, concat_axis=0, axis_index_groups=same_core, tiled=True
        )
    grad_att_router, hidden_one_extra = router_grads(
        hidden, att_router, att_gates, att_first, att_second, att_gate_grad
    )
    grad_hidden_one = jnp.sum(arrived.astype(f32), axis=0) + hidden_one_extra
    grad_gain_one = jnp.sum(grad_hidden_one * normed_one, axis=0)
    grad_input = grad_mid + norm_back(grad_hidden_one * gain_one, normed_one, inverse_one)

    everyone = devices * replicas
    smalls = [grad_gain_one, grad_gain_two, grad_att_router, grad_ffn_router]
    packed = jnp.concatenate([small.reshape(everyone, -1) for small in smalls], axis=1)
    packed, summed_o = lax.optimization_barrier((packed, summed_o))
    own_smalls = jnp.sum(
        lax.all_to_all(packed, ("dp", "expert"), split_axis=0, concat_axis=0, tiled=True), axis=0
    )
    share = D // everyone
    shared_gain_one = own_smalls[:share]
    shared_gain_two = own_smalls[share : 2 * share]
    shared_att_router = own_smalls[2 * share : (2 + ATT_EXPERTS) * share].reshape(share, ATT_EXPERTS)
    shared_ffn_router = own_smalls[(2 + ATT_EXPERTS) * share :].reshape(share, FFN_EXPERTS)

    kv_rows = exchange(summed_kv.reshape(devices, -1, 2 * half))
    kv_sum = jnp.sum(kv_rows.astype(f32).reshape(devices // 2, 2, -1, 2 * half), axis=0)
    shared_kv = jnp.concatenate(
        [kv_sum[n, :, m * half : (m + 1) * half] for m in range(2) for n in range(2)], axis=1
    )

    return (
        result.astype(bf16),
        grad_input.astype(bf16),
        shared_gain_one,
        shared_kv,
        shared_att_router,
        summed_q.astype(f32),
        summed_o,
        shared_gain_two,
        shared_ffn_router,
        summed_gate.astype(f32),
        summed_up.astype(f32),
        summed_down.astype(f32),
    )


def solution(mesh):
    in_specs = (
        P(("dp", "expert"), None),
        P(("dp", "expert"), None),
        P(("dp", "expert"), None),
        P(("dp", "expert"), None),
        P("dp", None),
        P(),
        P(),
        P("expert", None),
        P(),
        P(None, "expert"),
        P(None, "expert"),
        P(),
        P(),
        P(None, "expert"),
        P(None, "expert"),
        P(None, "expert"),
    )
    out_specs = (
        P(("dp", "expert"), None),
        P(("dp", "expert"), None),
        P(("dp", "expert")),
        P(("dp", "expert"), None),
        P(("dp", "expert"), None),
        P("dp", "expert"),
        P("dp", "expert"),
        P(("dp", "expert")),
        P(("dp", "expert"), None),
        P("dp", "expert"),
        P("dp", "expert"),
        P("dp", "expert"),
    )
    return jax.shard_map(body, mesh=mesh, in_specs=in_specs, out_specs=out_specs, check_vma=False)
```

```python
import functools
import jax
import jax.numpy as jnp
from jax import lax
from jax.experimental import pallas as pl
from jax.experimental.pallas import tpu as pltpu
from jax.sharding import PartitionSpec as P

HEAD = 128
GROUPS = 4
LOG2E = 1.4426950408889634
VMEM_BYTES = 60 * 1024 * 1024


def dot_nt(left, right):
    return lax.dot_general(left, right, (((1,), (1,)), ((), ())), preferred_element_type=jnp.float32)


def dot_nn(left, right):
    return jnp.dot(left, right, preferred_element_type=jnp.float32)


def spin(values, cosine, sine):
    return values * cosine + pltpu.roll(values, HEAD // 2, 1) * sine


def fill_bias(bias_ref, key_ref, query_ref, keys):
    for group in range(GROUPS):
        place = query_ref[group, 0:1, :]
        own, parent, grand = (query_ref[group, 1 + n : 2 + n, :] for n in range(3))

        def one(block, carry, group=group, place=place, own=own, parent=parent, grand=grand):
            at = pl.multiple_of(block * keys, 16)
            key_place = key_ref[pl.ds(at, keys), 0:1]
            key_segment = key_ref[pl.ds(at, keys), 1:2]
            related = (key_segment == own) | (key_segment == parent) | (key_segment == grand)
            allowed = related & (key_place <= place)
            bias_ref[group * (group + 1) // 2 + block] = jnp.where(allowed, 0.0, -1e30)
            return carry

        lax.fori_loop(0, group + 1, one, 0)


def group_rows(refs, group, rows, lanes):
    parts = [ref[pl.ds(group * rows, rows), lanes] for ref in refs]
    return parts[0] if len(parts) == 1 else jnp.concatenate(parts, axis=0)


def attention_forward_body(sets, step_heads, rows, keys, scale, first_ref, *refs):
    query_refs = refs[:sets]
    key_ref, value_ref, key_info, query_info = refs[sets : sets + 4]
    out_refs = refs[sets + 4 : 2 * sets + 4]
    lse_ref, bias_ref, flipped_ref = refs[2 * sets + 4 :]
    wide = sets * rows

    @pl.when(pl.program_id(0) == 0)
    def _():
        fill_bias(bias_ref, key_info, query_info, keys)

    for head in range(step_heads):
        lanes = pl.ds(head * HEAD, HEAD)
        for block in range(GROUPS):
            values = value_ref[pl.ds(block * keys, keys), lanes].astype(jnp.float32)
            flipped_ref[head, block] = values.T.astype(jnp.bfloat16)
    for group in range(GROUPS):
        queries = [
            group_rows(query_refs, group, rows, pl.ds(head * HEAD, HEAD)) for head in range(step_heads)
        ]

        def one(block, carry, group=group, queries=queries):
            at = pl.multiple_of(block * keys, 16)
            bias = bias_ref[group * (group + 1) // 2 + block]
            result = []
            for head in range(step_heads):
                top, total, mixed = carry[3 * head : 3 * head + 3]
                scores = dot_nt(key_ref[pl.ds(at, keys), pl.ds(head * HEAD, HEAD)], queries[head])
                scores = scores * scale + bias
                new_top = jnp.maximum(top, jnp.max(scores, axis=0, keepdims=True))
                fade = jnp.exp2(top - new_top)
                parts = jnp.exp2(scores - new_top)
                total = total * fade + jnp.sum(parts, axis=0, keepdims=True)
                mixed = mixed * fade + dot_nn(flipped_ref[head, block], parts.astype(jnp.bfloat16))
                result += [new_top, total, mixed]
            return tuple(result)

        start = (
            jnp.full((1, wide), -1e30, jnp.float32),
            jnp.zeros((1, wide), jnp.float32),
            jnp.zeros((HEAD, wide), jnp.float32),
        ) * step_heads
        final = lax.fori_loop(0, group + 1, one, start)
        for head in range(step_heads):
            top, total, mixed = final[3 * head : 3 * head + 3]
            lse_ref[head, group] = top + jnp.log2(total)
            rows_out = (mixed / total).T.astype(jnp.bfloat16)
            for n, ref in enumerate(out_refs):
                ref[pl.ds(group * rows, rows), pl.ds(head * HEAD, HEAD)] = rows_out[
                    n * rows : (n + 1) * rows
                ]


def attention_backward_body(sets, step_heads, rows, keys, scale, first_ref, *refs):
    query_refs, grad_refs, out_refs = (refs[n * sets : (n + 1) * sets] for n in range(3))
    key_ref, value_ref, lse_ref, key_info, query_info = refs[3 * sets : 3 * sets + 5]
    key_cos, key_sin = refs[3 * sets + 5 : 3 * sets + 7]
    table_refs = refs[3 * sets + 7 : 5 * sets + 7]
    rest = refs[5 * sets + 7 :]
    dq_refs = rest[:sets]
    dkv_ref, bias_ref, flipped_ref, dk_acc, dv_acc = rest[sets:]
    half = dkv_ref.shape[1] // 2
    softmax_scale = scale / LOG2E

    @pl.when(pl.program_id(0) == 0)
    def _():
        fill_bias(bias_ref, key_info, query_info, keys)

    dk_acc[...] = jnp.zeros_like(dk_acc)
    dv_acc[...] = jnp.zeros_like(dv_acc)
    for head in range(step_heads):
        lanes = pl.ds(head * HEAD, HEAD)
        for block in range(GROUPS):
            values = key_ref[pl.ds(block * keys, keys), lanes].astype(jnp.float32)
            flipped_ref[head, block] = values.T.astype(jnp.bfloat16)
    for group in range(GROUPS):
        queries, grads, centres, tops = [], [], [], []
        for head in range(step_heads):
            lanes = pl.ds(head * HEAD, HEAD)
            queries.append(group_rows(query_refs, group, rows, lanes))
            grad = group_rows(grad_refs, group, rows, lanes)
            out = group_rows(out_refs, group, rows, lanes)
            product = grad.astype(jnp.float32) * out.astype(jnp.float32)
            centres.append(jnp.sum(product.T, axis=0, keepdims=True))
            grads.append(grad)
            tops.append(lse_ref[head, group])

        def one(block, carry, group=group, queries=queries, grads=grads, centres=centres, tops=tops):
            at = pl.multiple_of(block * keys, 16)
            bias = bias_ref[group * (group + 1) // 2 + block]
            result = []
            for head in range(step_heads):
                lanes = pl.ds(head * HEAD, HEAD)
                key_rows = key_ref[pl.ds(at, keys), lanes]
                scores = dot_nt(key_rows, queries[head])
                probs = jnp.exp2(scores * scale + (bias - tops[head]))
                grad_probs = dot_nt(value_ref[pl.ds(at, keys), lanes], grads[head])
                grad_scores = (probs * (grad_probs - centres[head])).astype(jnp.bfloat16)
                dv_acc[pl.ds(at, keys), lanes] += dot_nn(probs.astype(jnp.bfloat16), grads[head])
                dk_acc[pl.ds(at, keys), lanes] += dot_nn(grad_scores, queries[head])
                result.append(carry[head] + dot_nn(flipped_ref[head, block], grad_scores))
            return tuple(result)

        start = (jnp.zeros((HEAD, sets * rows), jnp.float32),) * step_heads
        final = lax.fori_loop(0, group + 1, one, start)
        for head in range(step_heads):
            dq = final[head].T * softmax_scale
            for n, ref in enumerate(dq_refs):
                span = pl.ds(group * rows, rows)
                turned = spin(
                    dq[n * rows : (n + 1) * rows], table_refs[2 * n][span, :], table_refs[2 * n + 1][span, :]
                )
                ref[span, pl.ds(head * HEAD, HEAD)] = turned.astype(jnp.bfloat16)
    for head in range(step_heads):
        lanes = pl.ds(head * HEAD, HEAD)
        first_lane = pl.multiple_of((pl.program_id(0) * step_heads + head) * HEAD, HEAD)
        for block in range(GROUPS):
            span = pl.ds(block * keys, keys)
            turned = spin(dk_acc[span, lanes] * softmax_scale, key_cos[span, :], key_sin[span, :])
            dkv_ref[span, pl.ds(first_lane, HEAD)] = turned.astype(jnp.bfloat16)
            dkv_ref[span, pl.ds(half + first_lane, HEAD)] = dv_acc[span, lanes].astype(jnp.bfloat16)


def whole_block(shape):
    return pl.BlockSpec(shape, lambda h, first: (0,) * len(shape))


def attention_forward(queries, starts, keys_all, values_all, key_info, query_info, heads):
    sets, total_rows, tokens = len(queries), queries[0].shape[0], keys_all.shape[0]
    rows, keys = total_rows // GROUPS, tokens // GROUPS
    step_heads = 2
    wide = step_heads * HEAD
    scale = HEAD ** (-0.5) * LOG2E
    query_specs = [
        pl.BlockSpec((total_rows, wide), lambda h, first, n=n: (0, first[n] + h)) for n in range(sets)
    ]
    plain = pl.BlockSpec((total_rows, wide), lambda h, first: (0, h))
    side = pl.BlockSpec((tokens, wide), lambda h, first: (0, h))
    return pl.pallas_call(
        functools.partial(attention_forward_body, sets, step_heads, rows, keys, scale),
        grid_spec=pltpu.PrefetchScalarGridSpec(
            num_scalar_prefetch=1,
            grid=(heads // step_heads,),
            in_specs=query_specs
            + [side, side, whole_block(key_info.shape), whole_block(query_info.shape)],
            out_specs=[plain] * sets
            + [pl.BlockSpec((step_heads, GROUPS, 1, sets * rows), lambda h, first: (h, 0, 0, 0))],
            scratch_shapes=[
                pltpu.VMEM((GROUPS * (GROUPS + 1) // 2, keys, sets * rows), jnp.float32),
                pltpu.VMEM((step_heads, GROUPS, HEAD, keys), jnp.bfloat16),
            ],
        ),
        out_shape=[jax.ShapeDtypeStruct((total_rows, heads * HEAD), jnp.bfloat16)] * sets
        + [jax.ShapeDtypeStruct((heads, GROUPS, 1, sets * rows), jnp.float32)],
        compiler_params=pltpu.CompilerParams(vmem_limit_bytes=VMEM_BYTES),
        name="attention_forward",
    )(starts, *queries, keys_all, values_all, key_info, query_info)


def attention_backward(
    queries, starts, grads, outs, keys_all, values_all, lse, key_info, query_info, key_tables, row_tables, heads
):
    sets, total_rows, tokens = len(queries), queries[0].shape[0], keys_all.shape[0]
    rows, keys = total_rows // GROUPS, tokens // GROUPS
    step_heads = 1
    wide = step_heads * HEAD
    scale = HEAD ** (-0.5) * LOG2E
    shifted = [
        pl.BlockSpec((total_rows, wide), lambda h, first, n=n: (0, first[n] + h)) for n in range(sets)
    ]
    plain = pl.BlockSpec((total_rows, wide), lambda h, first: (0, h))
    side = pl.BlockSpec((tokens, wide), lambda h, first: (0, h))
    return pl.pallas_call(
        functools.partial(attention_backward_body, sets, step_heads, rows, keys, scale),
        grid_spec=pltpu.PrefetchScalarGridSpec(
            num_scalar_prefetch=1,
            grid=(heads // step_heads,),
            in_specs=shifted
            + shifted
            + [plain] * sets
            + [
                side,
                side,
                pl.BlockSpec((step_heads, GROUPS, 1, sets * rows), lambda h, first: (h, 0, 0, 0)),
                whole_block(key_info.shape),
                whole_block(query_info.shape),
                whole_block((tokens, HEAD)),
                whole_block((tokens, HEAD)),
            ]
            + [whole_block((total_rows, HEAD))] * (2 * sets),
            out_specs=[plain] * sets + [whole_block((tokens, 2 * heads * HEAD))],
            scratch_shapes=[
                pltpu.VMEM((GROUPS * (GROUPS + 1) // 2, keys, sets * rows), jnp.float32),
                pltpu.VMEM((step_heads, GROUPS, HEAD, keys), jnp.bfloat16),
                pltpu.VMEM((tokens, wide), jnp.float32),
                pltpu.VMEM((tokens, wide), jnp.float32),
            ],
        ),
        out_shape=[jax.ShapeDtypeStruct((total_rows, heads * HEAD), jnp.bfloat16)] * sets
        + [jax.ShapeDtypeStruct((tokens, 2 * heads * HEAD), jnp.bfloat16)],
        compiler_params=pltpu.CompilerParams(vmem_limit_bytes=VMEM_BYTES),
        name="attention_backward",
    )(
        starts,
        *queries,
        *grads,
        *outs,
        keys_all,
        values_all,
        lse,
        key_info,
        query_info,
        *key_tables,
        *[table for pair in row_tables for table in pair],
    )


def project_body(plan_ref, hidden_ref, weight_ref, cos_ref, sin_ref, out_ref, x_ref):
    sources, capacity = plan_ref.shape[0], plan_ref.shape[1]
    bundle = max(1, sources * capacity // GROUPS // capacity)
    tile = bundle * capacity

    @pl.when(pl.program_id(0) == 0)
    def _():
        for group in range(sources // bundle):
            parts = [
                dot_nn(plan_ref[group * bundle + n], hidden_ref[group * bundle + n]) for n in range(bundle)
            ]
            x_ref[pl.ds(group * tile, tile), :] = jnp.concatenate(parts, axis=0).astype(jnp.bfloat16)

    for at in range(0, x_ref.shape[0], tile):
        span = pl.ds(at, tile)
        product = dot_nn(x_ref[span, :], weight_ref[...])
        for lane in range(0, out_ref.shape[1], HEAD):
            turned = spin(product[:, lane : lane + HEAD], cos_ref[span, :], sin_ref[span, :])
            out_ref[span, lane : lane + HEAD] = turned.astype(jnp.bfloat16)


def project_queries(plan, hidden, weight, tables):
    sources, capacity, row_count = plan.shape
    depth, columns = weight.shape
    rows = sources * capacity
    block = 512
    return pl.pallas_call(
        project_body,
        grid=(columns // block,),
        in_specs=[
            pl.BlockSpec((sources, capacity, row_count), lambda j: (0, 0, 0)),
            pl.BlockSpec((sources, row_count, depth), lambda j: (0, 0, 0)),
            pl.BlockSpec((depth, block), lambda j: (0, j)),
            pl.BlockSpec((rows, HEAD), lambda j: (0, 0)),
            pl.BlockSpec((rows, HEAD), lambda j: (0, 0)),
        ],
        out_specs=[
            pl.BlockSpec((rows, block), lambda j: (0, j)),
            pl.BlockSpec((rows, depth), lambda j: (0, 0)),
        ],
        out_shape=[
            jax.ShapeDtypeStruct((rows, columns), jnp.bfloat16),
            jax.ShapeDtypeStruct((rows, depth), jnp.bfloat16),
        ],
        compiler_params=pltpu.CompilerParams(vmem_limit_bytes=VMEM_BYTES),
        name="project_queries",
    )(plan, hidden, weight, *tables)


def keys_values_body(half, order_ref, x_ref, weight_ref, cos_ref, sin_ref, key_ref, value_ref):
    rows = x_ref.shape[1]
    for source in range(x_ref.shape[0]):
        span = pl.ds(source * rows, rows)
        product = dot_nn(x_ref[source], weight_ref[0])
        for lane in range(0, half, HEAD):
            turned = spin(product[:, lane : lane + HEAD], cos_ref[span, :], sin_ref[span, :])
            key_ref[span, lane : lane + HEAD] = turned.astype(jnp.bfloat16)
        value_ref[span, :] = product[:, half:].astype(jnp.bfloat16)


def project_keys_values(hidden, weights, tables, order):
    sources, rows, unused = hidden.shape
    parts, depth, columns = weights.shape
    half, tokens = columns // 2, sources * rows
    return pl.pallas_call(
        functools.partial(keys_values_body, half),
        grid_spec=pltpu.PrefetchScalarGridSpec(
            num_scalar_prefetch=1,
            grid=(parts,),
            in_specs=[
                pl.BlockSpec((sources, rows, depth), lambda j, order: (0, 0, 0)),
                pl.BlockSpec((1, depth, columns), lambda j, order: (j, 0, 0)),
                pl.BlockSpec((tokens, HEAD), lambda j, order: (0, 0)),
                pl.BlockSpec((tokens, HEAD), lambda j, order: (0, 0)),
            ],
            out_specs=[pl.BlockSpec((tokens, half), lambda j, order: (0, order[j]))] * 2,
        ),
        out_shape=[jax.ShapeDtypeStruct((tokens, parts * half), jnp.bfloat16)] * 2,
        compiler_params=pltpu.CompilerParams(vmem_limit_bytes=VMEM_BYTES),
        name="project_keys_values",
    )(order, hidden, weights, *tables)


def merge_body(tile, order_ref, plan_ref, slots_ref, dk_ref, dv_ref, weight_ref, out_ref, acc_ref):
    part = pl.program_id(1)
    sources, rows = plan_ref.shape[0], plan_ref.shape[1]
    ck = dk_ref.shape[1]

    @pl.when(part == 0)
    def _():
        for source in range(sources):
            acc_ref[pl.ds(source * rows, rows), :] = dot_nn(plan_ref[source], slots_ref[source])

    last = part == pl.num_programs(1) - 1
    for at in range(0, acc_ref.shape[0], tile):
        span = pl.ds(at, tile)
        acc_ref[span, :] += dot_nt(dk_ref[span, :], weight_ref[0, :, :ck]) + dot_nt(
            dv_ref[span, :], weight_ref[0, :, ck:]
        )

    @pl.when(last)
    def _():
        out_ref[...] = acc_ref[...].astype(jnp.bfloat16)


def merge_hidden_grads(plan, slots, grads, weights, order):
    sources, rows, capacity = plan.shape
    parts, depth, columns = weights.shape
    ck, tokens = columns // 2, sources * rows
    wide = depth // 2
    return pl.pallas_call(
        functools.partial(merge_body, tokens // GROUPS),
        grid_spec=pltpu.PrefetchScalarGridSpec(
            num_scalar_prefetch=1,
            grid=(2, parts),
            in_specs=[
                pl.BlockSpec((sources, rows, capacity), lambda i, j, order: (0, 0, 0)),
                pl.BlockSpec((sources, capacity, wide), lambda i, j, order: (0, 0, i)),
                pl.BlockSpec((tokens, ck), lambda i, j, order: (0, order[j])),
                pl.BlockSpec((tokens, ck), lambda i, j, order: (0, parts + order[j])),
                pl.BlockSpec((1, wide, columns), lambda i, j, order: (j, i, 0)),
            ],
            out_specs=pl.BlockSpec((tokens, wide), lambda i, j, order: (0, i)),
            scratch_shapes=[pltpu.VMEM((tokens, wide), jnp.float32)],
        ),
        out_shape=jax.ShapeDtypeStruct((tokens, depth), jnp.bfloat16),
        compiler_params=pltpu.CompilerParams(vmem_limit_bytes=VMEM_BYTES),
        name="merge_hidden_grads",
    )(order, plan, slots, grads, grads, weights)


def mesh_device(index):
    return {"expert": index}


def chip_order(chip, step):
    flip = chip // 2
    near = chip + flip * (3 - 2 * chip)
    place = step + near * (1 - 2 * step) if step < 2 else step
    return place + flip * (3 - 2 * place)


def far_order(chip, step):
    return chip_order(chip, 3 - step)


def is_middle(chip):
    flip = chip // 2
    return chip + flip * (3 - 2 * chip)


def crossing_order(chip, step):
    end, middle = chip_order(chip, step), chip_order(chip, (2, 3, 1, 0)[step])
    return end + is_middle(chip) * (middle - end)


def enter(devices, me):
    barrier = pltpu.get_barrier_semaphore()
    for step in range(1, devices):
        pl.semaphore_signal(
            barrier,
            inc=1,
            device_id=mesh_device(lax.rem(me + step, devices)),
            device_id_type=pl.DeviceIdType.MESH,
        )
    pl.semaphore_wait(barrier, devices - 1)


def remote(source, target, send, recv, device):
    return pltpu.make_async_remote_copy(
        src_ref=source,
        dst_ref=target,
        send_sem=send,
        recv_sem=recv,
        device_id=mesh_device(device),
        device_id_type=pl.DeviceIdType.MESH,
    )


class Dispatch:
    def __init__(self, me, order, slots, landing, local_sem, send, recv, pass_send, pass_recv):
        self.me, self.chip, self.core, self.order = me, me // 2, lax.rem(me, 2), order
        self.sending = stagger_order if order is stagger_order else chip_order
        self.slots, self.landing = slots, landing
        self.local_sem, self.send, self.recv = local_sem, send, recv
        self.pass_send, self.pass_recv = pass_send, pass_recv
        self.rows, self.half = slots.shape[1], slots.shape[2] // 2

    def columns(self, core):
        return pl.ds(pl.multiple_of(core * self.half, 128), self.half)

    def place(self, source, core):
        rows = pl.ds(pl.multiple_of(lax.rem(source, 2) * self.rows, 16), self.rows)
        return self.landing.at[source // 2, rows, self.columns(core)]

    def direct(self, target):
        core = lax.rem(target, 2)
        offset = lax.rem(target - self.me + 8, 8)
        return remote(
            self.slots.at[target // 2, :, self.columns(core)],
            self.place(self.me, core),
            self.send.at[offset],
            self.recv.at[offset],
            target,
        )

    def sends(self, step):
        chip = self.sending(self.chip, step)
        targets = [2 * chip, 2 * chip + 1] if step else [self.me + 1 - 2 * self.core]
        return [self.direct(target) for target in targets]

    def local(self):
        return pltpu.make_async_copy(
            self.slots.at[self.chip, :, self.columns(self.core)],
            self.place(self.me, self.core),
            self.local_sem,
        )

    def start_local(self):
        self.local().start()

    def start(self, steps):
        for step in steps:
            for copy in self.sends(step):
                copy.start()

    def sent(self, steps):
        for step in steps:
            for copy in self.sends(step):
                copy.wait_send()

    def pass_on(self, source):
        place = self.place(source, self.core)
        return remote(
            place, place, self.pass_send.at[source], self.pass_recv.at[source], self.me + 1 - 2 * self.core
        )

    def arrive(self, step):
        chip = self.order(self.chip, step)
        for source in (2 * chip, 2 * chip + 1):
            offset = lax.rem(self.me - source + 8, 8)

            @pl.when(offset == 0)
            def _():
                self.local().wait()

            @pl.when(offset != 0)
            def _(source=source, offset=offset):
                place = self.place(source, self.core)
                remote(place, place, self.send.at[offset], self.recv.at[offset], self.me).wait_recv()

            self.pass_on(source).start()

    def ready(self, step):
        chip = self.order(self.chip, step)
        for source in (2 * chip, 2 * chip + 1):
            place = self.place(source, 1 - self.core)
            remote(
                place, place, self.pass_send.at[source], self.pass_recv.at[source], self.me
            ).wait_recv()
        return chip

    def passed_on(self):
        for source in range(8):
            self.pass_on(source).wait_send()


class Collect:
    def __init__(
        self, me, order, own_steps, kept, passing, passed, total, back, local_sem, pass_send, pass_recv, send, recv
    ):
        self.me, self.chip, self.core = me, me // 2, lax.rem(me, 2)
        self.order, self.own_steps = order, own_steps
        self.kept, self.passing, self.passed, self.total, self.back = kept, passing, passed, total, back
        self.local_sem, self.pass_send, self.pass_recv = local_sem, pass_send, pass_recv
        self.send, self.recv = send, recv
        self.rows, self.half = back.shape[1], back.shape[2] // 2

    def swap(self, step):
        return remote(
            self.passing.at[step % 2],
            self.passed.at[step],
            self.pass_send.at[step],
            self.pass_recv.at[step],
            self.me + 1 - 2 * self.core,
        )

    def place(self, chip, core):
        return self.back.at[chip, :, pl.ds(pl.multiple_of(core * self.half, 128), self.half)]

    def local(self, step, source_core):
        return pltpu.make_async_copy(
            self.total.at[step, pl.ds(pl.multiple_of(source_core * self.rows, 16), self.rows), :],
            self.place(self.chip, self.core),
            self.local_sem,
        )

    def outgoing(self, step, source):
        rows = pl.ds(pl.multiple_of(lax.rem(source, 2) * self.rows, 16), self.rows)
        offset = lax.rem(source - self.me + 8, 8)
        return remote(
            self.total.at[step, rows, :],
            self.place(self.chip, self.core),
            self.send.at[offset],
            self.recv.at[offset],
            source,
        )

    def block(self, step):
        return self.order(self.chip, step)

    def each(self, step, own, other):
        chip = self.block(step)
        for source in (2 * chip, 2 * chip + 1):
            if step not in self.own_steps:
                other(source)
                continue

            @pl.when(source == self.me)
            def _():
                own()

            @pl.when(source != self.me)
            def _(source=source):
                other(source)

    def settle(self, step):
        self.swap(step).wait_recv()
        tile = 2 * self.rows // 4
        for at in range(0, 2 * self.rows, tile):
            span = pl.ds(at, tile)
            summed = self.kept[span, :] + self.passed[step, span, :].astype(jnp.float32)
            self.total[step, span, :] = summed.astype(jnp.bfloat16)
        self.each(
            step,
            lambda: self.local(step, self.core).start(),
            lambda source: self.outgoing(step, source).start(),
        )

    def finish(self):
        for step in range(4):
            if step >= 2:
                self.swap(step).wait_send()
            self.each(
                step,
                lambda step=step: self.local(step, self.core).wait(),
                lambda source, step=step: self.outgoing(step, source).wait_send(),
            )
        for offset in range(1, 8):
            source = lax.rem(self.me + 8 - offset, 8)
            place = self.place(source // 2, lax.rem(source, 2))
            remote(place, place, self.send.at[offset], self.recv.at[offset], self.me).wait_recv()


def ffn_forward_body(
    chunk,
    slots,
    gate_hbm,
    up_hbm,
    down_hbm,
    rows_out,
    gate_out,
    up_out,
    act_out,
    back,
    gate,
    up,
    down,
    landing,
    pre_stage,
    act,
    kept,
    passing,
    passed,
    total,
    weight_sem,
    stage_sem,
    act_sem,
    rows_sem,
    local_sem,
    send,
    recv,
    pass_send,
    pass_recv,
    swap_send,
    swap_recv,
    out_send,
    out_recv,
):
    me = lax.axis_index("expert")
    enter(8, me)
    loads = [
        pltpu.make_async_copy(source, target, weight_sem.at[n])
        for n, (source, target) in enumerate(((gate_hbm, gate), (up_hbm, up), (down_hbm, down)))
    ]
    dispatch = Dispatch(me, crossing_order, slots, landing, local_sem.at[0], send, recv, pass_send, pass_recv)
    collect = Collect(
        me, crossing_order, (0, 3), kept, passing, passed, total, back, local_sem.at[1], swap_send, swap_recv, out_send, out_recv
    )
    middle = is_middle(me // 2)
    dispatch.start_local()
    dispatch.start((0, 1))

    @pl.when(middle == 1)
    def _():
        dispatch.start((2,))

    for load in loads:
        load.start()
    block = landing.shape[1]
    hidden_units = gate.shape[1]
    chunks = hidden_units // chunk
    half = back.shape[2] // 2

    def stage_copies(chip, part, slot):
        span = pl.ds(pl.multiple_of(chip * block, 16), block)
        columns = pl.ds(pl.multiple_of(part * chunk, 128), chunk)
        return [
            pltpu.make_async_copy(
                pre_stage.at[slot, n], out.at[span, columns], stage_sem.at[slot, n]
            )
            for n, out in enumerate((gate_out, up_out))
        ]

    def act_copy(chip, step):
        span = pl.ds(pl.multiple_of(chip * block, 16), block)
        return pltpu.make_async_copy(act.at[step % 2], act_out.at[span, :], act_sem.at[step % 2])

    def rows_copy(chip, step):
        span = pl.ds(pl.multiple_of(chip * block, 16), block)
        return pltpu.make_async_copy(landing.at[chip], rows_out.at[span, :], rows_sem.at[step])

    for step in range(4):
        if step == 0:
            dispatch.arrive(0)
        chip = dispatch.ready(step)
        rows_copy(chip, step).start()
        if step == 0:
            loads[0].wait()
            loads[1].wait()
        if step >= 2:
            act_copy(crossing_order(me // 2, step - 2), step - 2).wait()

        def hidden_part(part, carry, chip=chip, step=step):
            slot = lax.rem(part + step * chunks, 2)
            columns = pl.ds(pl.multiple_of(part * chunk, 128), chunk)

            @pl.when(part + step * chunks >= 2)
            def _():
                for copy in stage_copies(chip, part, slot):
                    copy.wait()

            gated = dot_nn(landing[chip], gate[:, columns])
            raised = dot_nn(landing[chip], up[:, columns])
            pre_stage[slot, 0] = gated.astype(jnp.bfloat16)
            pre_stage[slot, 1] = raised.astype(jnp.bfloat16)
            act[step % 2, :, columns] = (gated * jax.nn.sigmoid(gated) * raised).astype(jnp.bfloat16)
            for copy in stage_copies(chip, part, slot):
                copy.start()
            if step == 0:
                @pl.when((part == chunks // 3) & (middle == 0))
                def _():
                    dispatch.sent((1,))
                    dispatch.start((2,))

                @pl.when((part == chunks // 2) & (middle == 1))
                def _():
                    dispatch.sent((1, 2))
                    dispatch.start((3,))

            return carry

        lax.fori_loop(0, chunks, hidden_part, 0)
        act_copy(chip, step).start()
        if step == 0:
            loads[2].wait()
        else:
            collect.settle(step - 1)
        core = collect.core
        width = min(512, half)

        def far_part(part, carry, step=step):
            at = pl.multiple_of((1 - core) * half + part * width, 128)
            product = dot_nt(act[step % 2], down[pl.ds(at, width), :])
            passing[step % 2, :, pl.ds(pl.multiple_of(part * width, 128), width)] = product.astype(jnp.bfloat16)
            return carry

        def near_part(part, carry, step=step):
            at = pl.multiple_of(core * half + part * width, 128)
            product = dot_nt(act[step % 2], down[pl.ds(at, width), :])
            kept[:, pl.ds(pl.multiple_of(part * width, 128), width)] = product
            return carry

        if step >= 2:
            collect.swap(step - 2).wait_send()
        lax.fori_loop(0, half // width, far_part, 0)
        collect.swap(step).start()
        if step == 0:

            @pl.when(middle == 0)
            def _():
                dispatch.sent((2,))
                dispatch.start((3,))

        if step < 3:
            dispatch.arrive(step + 1)
        lax.fori_loop(0, half // width, near_part, 0)
    collect.settle(3)
    for step in (2, 3):
        act_copy(crossing_order(me // 2, step), step).wait()
    for step in range(4):
        rows_copy(crossing_order(me // 2, step), step).wait()
    for slot in range(2):
        for copy in stage_copies(0, 0, slot):
            copy.wait()
    dispatch.sent((0, 3))
    dispatch.passed_on()
    collect.finish()


def ffn_forward(slots, gate_weight, up_weight, down_weight):
    chips, capacity, depth = slots.shape
    hidden_units = gate_weight.shape[1]
    block = 2 * capacity
    chunk = 256 if hidden_units % 256 == 0 else 128
    half = depth // 2
    rows = chips * block
    any_space = pl.BlockSpec(memory_space=pl.ANY)
    bf = jnp.bfloat16
    dma = pltpu.SemaphoreType.DMA
    return pl.pallas_call(
        functools.partial(ffn_forward_body, chunk),
        in_specs=[any_space] * 4,
        out_specs=[any_space] * 5,
        out_shape=[
            jax.ShapeDtypeStruct((rows, depth), bf),
            jax.ShapeDtypeStruct((rows, hidden_units), bf),
            jax.ShapeDtypeStruct((rows, hidden_units), bf),
            jax.ShapeDtypeStruct((rows, hidden_units), bf),
            jax.ShapeDtypeStruct((chips, capacity, depth), bf),
        ],
        scratch_shapes=[
            pltpu.VMEM((depth, hidden_units), bf),
            pltpu.VMEM((depth, hidden_units), bf),
            pltpu.VMEM((depth, hidden_units), bf),
            pltpu.VMEM((chips, block, depth), bf),
            pltpu.VMEM((2, 2, block, chunk), bf),
            pltpu.VMEM((2, block, hidden_units), bf),
            pltpu.VMEM((block, half), jnp.float32),
            pltpu.VMEM((2, block, half), bf),
            pltpu.VMEM((chips, block, half), bf),
            pltpu.VMEM((chips, block, half), bf),
            dma((3,)),
            dma((2, 2)),
            dma((2,)),
            dma((4,)),
            dma((2,)),
            dma((8,)),
            dma((8,)),
            dma((8,)),
            dma((8,)),
            dma((4,)),
            dma((4,)),
            dma((8,)),
            dma((8,)),
        ],
        compiler_params=pltpu.CompilerParams(
            collective_id=1, has_side_effects=True, vmem_limit_bytes=VMEM_BYTES
        ),
        name="ffn_forward",
    )(slots, gate_weight, up_weight, down_weight)


def stagger_order(chip, step):
    if step < 2:
        return chip_order(chip, step)
    end, middle = chip_order(chip, 5 - step), chip_order(chip, step)
    return end + is_middle(chip) * (middle - end)


def send_rows_body(
    slots,
    act_hbm,
    rows_out,
    grad_out,
    landing,
    act,
    total,
    stage,
    act_sem,
    rows_sem,
    stage_sem,
    local_sem,
    send,
    recv,
    pass_send,
    pass_recv,
):
    me = lax.axis_index("expert")
    enter(8, me)
    dispatch = Dispatch(me, stagger_order, slots, landing, local_sem.at[0], send, recv, pass_send, pass_recv)
    dispatch.start_local()
    dispatch.start((0, 1, 2))
    block = landing.shape[1]
    width = stage.shape[1]
    parts = landing.shape[2] // width

    def span_of(step):
        return pl.ds(pl.multiple_of(stagger_order(me // 2, step) * block, 16), block)

    def act_copy(step):
        return pltpu.make_async_copy(
            act_hbm.at[span_of(step), :], act.at[pl.ds(step * block, block), :], act_sem.at[step]
        )

    def rows_copy(step):
        chip = stagger_order(me // 2, step)
        return pltpu.make_async_copy(landing.at[chip], rows_out.at[chip], rows_sem.at[step])

    def stage_copy(part):
        slot = lax.rem(part, 2)
        span = pl.ds(pl.multiple_of(part * width, 16), width)
        return pltpu.make_async_copy(stage.at[slot], grad_out.at[span, :], stage_sem.at[slot])

    for step in range(4):
        act_copy(step).start()
    for steps in ((0, 1), (2,), (3,)):
        for step in steps:
            dispatch.arrive(step)
        chips = [dispatch.ready(step) for step in steps]
        for step in steps:
            rows_copy(step).start()
            act_copy(step).wait()

        def one(part, carry, steps=steps, chips=chips):
            columns = pl.ds(pl.multiple_of(part * width, 128), width)
            rows = [landing[chip, :, columns] for chip in chips]
            rows = rows[0] if len(rows) == 1 else jnp.concatenate(rows, axis=0)
            turned = rows.astype(jnp.float32).T.astype(jnp.bfloat16)
            product = dot_nn(turned, act[pl.ds(steps[0] * block, len(steps) * block), :])
            span = pl.ds(pl.multiple_of(part * width, 16), width)
            if steps[0] == 0:
                total[span, :] = product

                @pl.when(part == 0)
                def _():
                    dispatch.sent((2,))
                    dispatch.start((3,))

                return carry
            if steps[0] == 2:
                total[span, :] += product
                return carry

            @pl.when(part >= 2)
            def _():
                stage_copy(part - 2).wait()

            stage[lax.rem(part, 2)] = (total[span, :] + product).astype(jnp.bfloat16)
            stage_copy(part).start()
            return carry

        lax.fori_loop(0, parts, one, 0)
    for part in (parts - 2, parts - 1):
        stage_copy(part).wait()
    for step in range(4):
        rows_copy(step).wait()
    dispatch.sent((0, 1, 3))
    dispatch.passed_on()


def send_rows(slots, act):
    chips, capacity, depth = slots.shape
    rows, hidden_units = act.shape
    block = 2 * capacity
    width = min(256, depth // 2)
    any_space = pl.BlockSpec(memory_space=pl.ANY)
    bf = jnp.bfloat16
    dma = pltpu.SemaphoreType.DMA
    return pl.pallas_call(
        send_rows_body,
        in_specs=[any_space] * 2,
        out_specs=[any_space] * 2,
        out_shape=[
            jax.ShapeDtypeStruct((chips, block, depth), bf),
            jax.ShapeDtypeStruct((depth, hidden_units), bf),
        ],
        scratch_shapes=[
            pltpu.VMEM((chips, block, depth), bf),
            pltpu.VMEM((rows, hidden_units), bf),
            pltpu.VMEM((depth, hidden_units), jnp.float32),
            pltpu.VMEM((2, width, hidden_units), bf),
            dma((4,)),
            dma((4,)),
            dma((2,)),
            dma((1,)),
            dma((8,)),
            dma((8,)),
            dma((8,)),
            dma((8,)),
        ],
        compiler_params=pltpu.CompilerParams(
            collective_id=2, has_side_effects=True, vmem_limit_bytes=VMEM_BYTES
        ),
        name="send_rows",
    )(slots, act)


def ffn_backward_body(
    chunk,
    grad_rows,
    gate_in,
    up_in,
    gate_hbm,
    up_hbm,
    down_hbm,
    dgate_out,
    dup_out,
    back,
    gate,
    up,
    down,
    grad,
    pre_stage,
    pair,
    kept,
    passing,
    passed,
    total,
    weight_sem,
    grad_sem,
    stage_sem,
    pair_sem,
    local_sem,
    swap_send,
    swap_recv,
    out_send,
    out_recv,
):
    me = lax.axis_index("expert")
    enter(8, me)
    collect = Collect(
        me, far_order, (3,), kept, passing, passed, total, back, local_sem.at[0], swap_send, swap_recv, out_send, out_recv
    )
    loads = [
        pltpu.make_async_copy(source, target, weight_sem.at[n])
        for n, (source, target) in enumerate(((down_hbm, down), (gate_hbm, gate), (up_hbm, up)))
    ]
    block = grad.shape[1]
    hidden_units = gate.shape[1]
    chunks = hidden_units // chunk
    half = back.shape[2] // 2
    width = min(512, half)

    def span_of(chip):
        return pl.ds(pl.multiple_of(chip * block, 16), block)

    def grad_copy(step):
        return pltpu.make_async_copy(
            grad_rows.at[span_of(collect.block(step)), :], grad.at[step % 2], grad_sem.at[step % 2]
        )

    def stage_copies(chip, part, slot):
        columns = pl.ds(pl.multiple_of(part * chunk, 128), chunk)
        return [
            pltpu.make_async_copy(
                source.at[span_of(chip), columns], pre_stage.at[slot, n], stage_sem.at[slot, n]
            )
            for n, source in enumerate((gate_in, up_in))
        ]

    def pair_copies(chip):
        return [
            pltpu.make_async_copy(pair.at[n], out.at[span_of(chip), :], pair_sem.at[n])
            for n, out in enumerate((dgate_out, dup_out))
        ]

    grad_copy(0).start()
    loads[0].start()
    for copy in stage_copies(collect.block(0), 0, 0):
        copy.start()
    loads[1].start()
    loads[2].start()
    loads[0].wait()
    for step in range(4):
        chip = collect.block(step)
        grad_copy(step).wait()
        if step < 3:
            grad_copy(step + 1).start()
        if step > 0:
            for copy in pair_copies(collect.block(step - 1)):
                copy.wait()

        def hidden_part(part, carry, chip=chip, step=step):
            slot = lax.rem(part, 2)
            columns = pl.ds(pl.multiple_of(part * chunk, 128), chunk)
            for copy in stage_copies(chip, part, slot):
                copy.wait()

            @pl.when(part + 1 < chunks)
            def _():
                for copy in stage_copies(chip, part + 1, 1 - slot):
                    copy.start()

            upstream = dot_nn(grad[step % 2], down[:, columns])
            gated = pre_stage[slot, 0].astype(jnp.float32)
            raised = pre_stage[slot, 1].astype(jnp.float32)
            sigmoid = jax.nn.sigmoid(gated)
            scaled = upstream * sigmoid
            pair[0, :, columns] = (scaled * raised * (1.0 + gated * (1.0 - sigmoid))).astype(jnp.bfloat16)
            pair[1, :, columns] = (scaled * gated).astype(jnp.bfloat16)
            return carry

        lax.fori_loop(0, chunks, hidden_part, 0)
        for copy in pair_copies(chip):
            copy.start()
        if step < 3:
            for copy in stage_copies(collect.block(step + 1), 0, 0):
                copy.start()
        if step == 0:
            loads[1].wait()
            loads[2].wait()
        else:
            collect.settle(step - 1)
        core = collect.core

        def product(at):
            return dot_nt(pair[0], gate[pl.ds(at, width), :]) + dot_nt(pair[1], up[pl.ds(at, width), :])

        def far_part(part, carry, step=step):
            at = pl.multiple_of((1 - core) * half + part * width, 128)
            columns = pl.ds(pl.multiple_of(part * width, 128), width)
            passing[step % 2, :, columns] = product(at).astype(jnp.bfloat16)
            return carry

        def near_part(part, carry, step=step):
            at = pl.multiple_of(core * half + part * width, 128)
            kept[:, pl.ds(pl.multiple_of(part * width, 128), width)] = product(at)
            return carry

        if step >= 2:
            collect.swap(step - 2).wait_send()
        lax.fori_loop(0, half // width, far_part, 0)
        collect.swap(step).start()
        lax.fori_loop(0, half // width, near_part, 0)
    collect.settle(3)
    for copy in pair_copies(collect.block(3)):
        copy.wait()
    collect.finish()


def ffn_backward(grad_rows, gate_pre, up_pre, gate_weight, up_weight, down_weight, capacity):
    rows, depth = grad_rows.shape
    hidden_units = gate_weight.shape[1]
    block = 2 * capacity
    chips = rows // block
    chunk = hidden_units // 2 if hidden_units % 256 == 0 else 128
    half = depth // 2
    any_space = pl.BlockSpec(memory_space=pl.ANY)
    bf = jnp.bfloat16
    dma = pltpu.SemaphoreType.DMA
    return pl.pallas_call(
        functools.partial(ffn_backward_body, chunk),
        in_specs=[any_space] * 6,
        out_specs=[any_space] * 3,
        out_shape=[
            jax.ShapeDtypeStruct((rows, hidden_units), bf),
            jax.ShapeDtypeStruct((rows, hidden_units), bf),
            jax.ShapeDtypeStruct((chips, capacity, depth), bf),
        ],
        scratch_shapes=[
            pltpu.VMEM((depth, hidden_units), bf),
            pltpu.VMEM((depth, hidden_units), bf),
            pltpu.VMEM((depth, hidden_units), bf),
            pltpu.VMEM((2, block, depth), bf),
            pltpu.VMEM((2, 2, block, chunk), bf),
            pltpu.VMEM((2, block, hidden_units), bf),
            pltpu.VMEM((block, half), jnp.float32),
            pltpu.VMEM((2, block, half), bf),
            pltpu.VMEM((chips, block, half), bf),
            pltpu.VMEM((chips, block, half), bf),
            dma((3,)),
            dma((2,)),
            dma((2, 2)),
            dma((2,)),
            dma((1,)),
            dma((4,)),
            dma((4,)),
            dma((8,)),
            dma((8,)),
        ],
        compiler_params=pltpu.CompilerParams(
            collective_id=3, has_side_effects=True, vmem_limit_bytes=VMEM_BYTES
        ),
        name="ffn_backward",
    )(grad_rows, gate_pre, up_pre, gate_weight, up_weight, down_weight)


def send_slots_body(
    slots, rows_hbm, grads_hbm, landing, grad_out, rows_v, grads_v, stage, load_sem, stage_sem, local_sem, send, recv
):
    me = lax.axis_index("expert")
    enter(8, me)

    def outgoing(offset):
        target = lax.rem(me + offset, 8)
        return remote(slots.at[target], landing.at[me], send.at[offset], recv.at[offset], target)

    local = pltpu.make_async_copy(slots.at[me], landing.at[me], local_sem)
    for offset in range(1, 8):
        outgoing(offset).start()
    local.start()
    loads = [
        pltpu.make_async_copy(source, target, load_sem.at[n])
        for n, (source, target) in enumerate(((rows_hbm, rows_v), (grads_hbm, grads_v)))
    ]
    for load in loads:
        load.start()
    for load in loads:
        load.wait()
    width = stage.shape[1]
    blocks = rows_v.shape[1] // width

    def stage_copy(block):
        slot = lax.rem(block, 2)
        span = pl.ds(pl.multiple_of(block * width, 16), width)
        return pltpu.make_async_copy(stage.at[slot], grad_out.at[span, :], stage_sem.at[slot])

    def one(block, carry):
        @pl.when(block >= 2)
        def _():
            stage_copy(block - 2).wait()

        columns = pl.ds(pl.multiple_of(block * width, 128), width)
        turned = rows_v[:, columns].astype(jnp.float32).T.astype(jnp.bfloat16)
        stage[lax.rem(block, 2)] = dot_nn(turned, grads_v[...]).astype(jnp.bfloat16)
        stage_copy(block).start()
        return carry

    lax.fori_loop(0, blocks, one, 0)
    for block in (blocks - 2, blocks - 1):
        stage_copy(block).wait()
    local.wait()
    for offset in range(1, 8):
        outgoing(offset).wait_send()
        place = landing.at[lax.rem(me + 8 - offset, 8)]
        remote(place, place, send.at[offset], recv.at[offset], me).wait_recv()


def send_slots(slots, rows, grads):
    total, depth = rows.shape
    hidden_units = grads.shape[1]
    width = min(256, depth // 2)
    any_space = pl.BlockSpec(memory_space=pl.ANY)
    bf = jnp.bfloat16
    dma = pltpu.SemaphoreType.DMA
    return pl.pallas_call(
        send_slots_body,
        in_specs=[any_space] * 3,
        out_specs=[any_space] * 2,
        out_shape=[
            jax.ShapeDtypeStruct(slots.shape, bf),
            jax.ShapeDtypeStruct((depth, hidden_units), bf),
        ],
        scratch_shapes=[
            pltpu.VMEM((total, depth), bf),
            pltpu.VMEM((total, hidden_units), bf),
            pltpu.VMEM((2, width, hidden_units), bf),
            dma((2,)),
            dma((2,)),
            dma,
            dma((8,)),
            dma((8,)),
        ],
        compiler_params=pltpu.CompilerParams(
            collective_id=5, has_side_effects=True, vmem_limit_bytes=VMEM_BYTES
        ),
        name="send_slots",
    )(slots, rows, grads)


def merge_return_body(
    dp_axis,
    plan_hbm,
    slots_hbm,
    grads_hbm,
    weight_hbm,
    back,
    plan,
    slots,
    grads,
    weight,
    kept,
    passing,
    passed,
    total,
    load_sem,
    local_sem,
    swap_send,
    swap_recv,
    out_send,
    out_recv,
):
    me = lax.axis_index("expert")
    replica = lax.axis_index(dp_axis)
    enter(8, me)
    loads = [
        pltpu.make_async_copy(source, target, load_sem.at[n])
        for n, (source, target) in enumerate(
            ((plan_hbm, plan), (slots_hbm, slots), (grads_hbm, grads), (weight_hbm, weight))
        )
    ]
    for load in loads:
        load.start()
    collect = Collect(
        me, far_order, (3,), kept, passing, passed, total, back, local_sem.at[0], swap_send, swap_recv, out_send, out_recv
    )
    rows, half = collect.rows, collect.half
    parts, ck = weight.shape[0], weight.shape[2] // 2
    values_at = grads.shape[1] // 2
    width = min(512, half)
    for load in loads:
        load.wait()
    for step in range(4):
        chip = collect.block(step)
        span = pl.ds(pl.multiple_of(chip * 2 * rows, 16), 2 * rows)

        def product(at, chip=chip, span=span):
            columns = pl.ds(at, width)
            result = jnp.concatenate(
                [dot_nn(plan[2 * chip + n], slots[2 * chip + n, :, columns]) for n in range(2)], axis=0
            )
            for part in range(parts):
                low = lax.rem(replica, 2) + (part % 2) * (1 - 2 * lax.rem(replica, 2))
                high = replica // 2 + (part // 2) * (1 - 2 * (replica // 2))
                at_keys = pl.multiple_of((2 * high + low) * ck, 128)
                result += dot_nt(grads[span, pl.ds(at_keys, ck)], weight[part, columns, :ck])
                result += dot_nt(grads[span, pl.ds(values_at + at_keys, ck)], weight[part, columns, ck:])
            return result

        def far_part(part, carry, step=step, product=product):
            at = pl.multiple_of((1 - collect.core) * half + part * width, 128)
            columns = pl.ds(pl.multiple_of(part * width, 128), width)
            passing[step % 2, :, columns] = product(at).astype(jnp.bfloat16)
            return carry

        def near_part(part, carry, product=product):
            at = pl.multiple_of(collect.core * half + part * width, 128)
            kept[:, pl.ds(pl.multiple_of(part * width, 128), width)] = product(at)
            return carry

        if step >= 2:
            collect.swap(step - 2).wait_send()
        lax.fori_loop(0, half // width, far_part, 0)
        collect.swap(step).start()
        if step > 0:
            collect.settle(step - 1)
        lax.fori_loop(0, half // width, near_part, 0)
    collect.settle(3)
    collect.finish()


def merge_return(plan, slots, grads, weights):
    sources, rows, capacity = plan.shape
    parts, depth, columns = weights.shape
    tokens = sources * rows
    half = depth // 2
    any_space = pl.BlockSpec(memory_space=pl.ANY)
    bf = jnp.bfloat16
    dma = pltpu.SemaphoreType.DMA
    return pl.pallas_call(
        functools.partial(merge_return_body, "dp"),
        in_specs=[any_space] * 4,
        out_specs=any_space,
        out_shape=jax.ShapeDtypeStruct((sources // 2, rows, depth), bf),
        scratch_shapes=[
            pltpu.VMEM(plan.shape, bf),
            pltpu.VMEM(slots.shape, bf),
            pltpu.VMEM(grads.shape, bf),
            pltpu.VMEM(weights.shape, bf),
            pltpu.VMEM((2 * rows, half), jnp.float32),
            pltpu.VMEM((2, 2 * rows, half), bf),
            pltpu.VMEM((sources // 2, 2 * rows, half), bf),
            pltpu.VMEM((sources // 2, 2 * rows, half), bf),
            dma((4,)),
            dma((1,)),
            dma((4,)),
            dma((4,)),
            dma((8,)),
            dma((8,)),
        ],
        compiler_params=pltpu.CompilerParams(
            collective_id=6, has_side_effects=True, vmem_limit_bytes=VMEM_BYTES
        ),
        name="merge_return",
    )(plan, slots, grads, weights)


def return_order(chip, step):
    lower, upper = chip_order(chip, (2, 3, 1, 0)[step]), chip_order(chip, 3 - step)
    return lower + chip // 2 * (upper - lower)


def attention_send_body(
    scale,
    query_hbm,
    sibling_hbm,
    key_hbm,
    value_hbm,
    out_weight_hbm,
    key_info,
    query_info,
    own_out,
    sibling_out,
    rows_out,
    back,
    lse_ref,
    queries,
    siblings,
    keys_v,
    values_v,
    out_weight,
    bias_ref,
    flipped,
    own_stage,
    sibling_stage,
    arrived,
    rows_stage,
    sending,
    load_sem,
    own_sem,
    sibling_sem,
    rows_sem,
    local_sem,
    swap_send,
    swap_recv,
    out_send,
    out_recv,
):
    me = lax.axis_index("expert")
    chip, core = me // 2, lax.rem(me, 2)
    enter(8, me)
    half = keys_v.shape[1]
    rows = own_stage.shape[1]
    keys = keys_v.shape[0] // GROUPS
    heads = half // HEAD
    capacity = back.shape[1]
    own_columns = pl.ds(pl.multiple_of(core * half, 128), half)
    far_columns = pl.ds(pl.multiple_of((1 - core) * half, 128), half)
    loads = [
        pltpu.make_async_copy(source, target, load_sem.at[n])
        for n, (source, target) in enumerate(
            (
                (value_hbm, values_v),
                (key_hbm, keys_v),
                (query_hbm.at[:, own_columns], queries),
                (sibling_hbm, siblings),
                (out_weight_hbm, out_weight),
            )
        )
    ]
    for load in loads:
        load.start()
    fill_bias(bias_ref, key_info, query_info, keys)
    loads[0].wait()

    def flip(head, carry):
        lanes = pl.ds(pl.multiple_of(head * HEAD, HEAD), HEAD)
        for block in range(GROUPS):
            values = values_v[pl.ds(block * keys, keys), lanes].astype(jnp.float32)
            flipped[head, block] = values.T.astype(jnp.bfloat16)
        return carry

    lax.fori_loop(0, heads, flip, 0)
    for load in loads[1:4]:
        load.wait()

    def group_of(step):
        return return_order(chip, step)

    def span_of(step):
        return pl.ds(pl.multiple_of(group_of(step) * rows, 16), rows)

    def own_copy(step):
        return pltpu.make_async_copy(own_stage.at[step], own_out.at[span_of(step), :], own_sem.at[step])

    def sibling_copy(step):
        return pltpu.make_async_copy(
            sibling_stage.at[step], sibling_out.at[span_of(step), :], sibling_sem.at[step]
        )

    def rows_copy(step):
        return pltpu.make_async_copy(
            rows_stage.at[step], rows_out.at[span_of(step), :], rows_sem.at[step]
        )

    def swap(step):
        return remote(
            sibling_stage.at[step], arrived.at[step], swap_send.at[step], swap_recv.at[step], me + 1 - 2 * core
        )

    def outgoing(step, n):
        source = 2 * group_of(step) + n
        offset = lax.rem(source - me + 8, 8)
        return remote(sending.at[step, n], back.at[me], out_send.at[offset], out_recv.at[offset], source)

    def local(step, n):
        return pltpu.make_async_copy(sending.at[step, n], back.at[me], local_sem)

    def each(step, own, other):
        for n in range(2):
            if step < 3:
                other(n)
                continue

            @pl.when(core == n)
            def _(n=n):
                own(n)

            @pl.when(core != n)
            def _(n=n):
                other(n)

    def attend(step):
        group = group_of(step)
        first_block = group * (group + 1) // 2
        span = span_of(step)

        def head_pair(pair, carry):
            lanes = [pl.ds(pl.multiple_of((2 * pair + n) * HEAD, HEAD), HEAD) for n in range(2)]
            parts = [jnp.concatenate([queries[span, lane], siblings[span, lane]], axis=0) for lane in lanes]

            def one(block, state):
                at = pl.multiple_of(block * keys, 16)
                bias = bias_ref[first_block + block]
                result = []
                for n in range(2):
                    top, total, mixed = state[3 * n : 3 * n + 3]
                    scores = dot_nt(keys_v[pl.ds(at, keys), lanes[n]], parts[n]) * scale + bias
                    new_top = jnp.maximum(top, jnp.max(scores, axis=0, keepdims=True))
                    fade = jnp.exp2(top - new_top)
                    probs = jnp.exp2(scores - new_top)
                    total = total * fade + jnp.sum(probs, axis=0, keepdims=True)
                    mixed = mixed * fade + dot_nn(flipped[2 * pair + n, block], probs.astype(jnp.bfloat16))
                    result += [new_top, total, mixed]
                return tuple(result)

            start = (
                jnp.full((1, 2 * rows), -1e30, jnp.float32),
                jnp.zeros((1, 2 * rows), jnp.float32),
                jnp.zeros((HEAD, 2 * rows), jnp.float32),
            ) * 2
            final = lax.fori_loop(0, group + 1, one, start)
            for n in range(2):
                top, total, mixed = final[3 * n : 3 * n + 3]
                lse_ref[2 * pair + n, group] = top + jnp.log2(total)
                result = (mixed / total).T.astype(jnp.bfloat16)
                own_stage[step, :, lanes[n]] = result[:rows]
                sibling_stage[step, :, lanes[n]] = result[rows:]
            return carry

        lax.fori_loop(0, heads // 2, head_pair, 0)
        swap(step).start()
        own_copy(step).start()
        sibling_copy(step).start()

    def settle(step):
        swap(step).wait_recv()
        rows_stage[step, :, own_columns] = own_stage[step]
        rows_stage[step, :, far_columns] = arrived[step]
        rows_copy(step).start()
        width = 512
        for at in range(0, back.shape[2], min(width, back.shape[2])):
            columns = pl.ds(at, min(width, back.shape[2]))
            product = dot_nt(rows_stage[step], out_weight[columns, :])
            for n in range(2):
                part = product[n * capacity : (n + 1) * capacity]
                sending[step, n, :, columns] = part.astype(jnp.bfloat16)
        each(step, lambda n: local(step, n).start(), lambda n: outgoing(step, n).start())

    for step in range(4):
        attend(step)
        if step == 0:
            loads[4].wait()
        if step < 2:
            settle(step)
        elif step == 3:
            settle(2)
            settle(3)
    for step in range(4):
        swap(step).wait_send()
        own_copy(step).wait()
        sibling_copy(step).wait()
        rows_copy(step).wait()
        each(step, lambda n, step=step: local(step, n).wait(), lambda n, step=step: outgoing(step, n).wait_send())
    for offset in range(1, 8):
        place = back.at[lax.rem(me + 8 - offset, 8)]
        remote(place, place, out_send.at[offset], out_recv.at[offset], me).wait_recv()


def attention_send(queries, siblings, keys_all, values_all, out_weight, key_info, query_info, capacity):
    total_rows, width = queries.shape
    tokens, half = keys_all.shape
    depth = out_weight.shape[0]
    rows, keys, heads = total_rows // GROUPS, tokens // GROUPS, half // HEAD
    any_space = pl.BlockSpec(memory_space=pl.ANY)
    here = pl.BlockSpec(memory_space=pltpu.VMEM)
    bf = jnp.bfloat16
    dma = pltpu.SemaphoreType.DMA
    return pl.pallas_call(
        functools.partial(attention_send_body, HEAD ** (-0.5) * LOG2E),
        in_specs=[any_space] * 5 + [here] * 2,
        out_specs=[any_space] * 4 + [here],
        out_shape=[
            jax.ShapeDtypeStruct((total_rows, half), bf),
            jax.ShapeDtypeStruct((total_rows, half), bf),
            jax.ShapeDtypeStruct((total_rows, width), bf),
            jax.ShapeDtypeStruct((8, capacity, depth), bf),
            jax.ShapeDtypeStruct((heads, GROUPS, 1, 2 * rows), jnp.float32),
        ],
        scratch_shapes=[
            pltpu.VMEM((total_rows, half), bf),
            pltpu.VMEM((total_rows, half), bf),
            pltpu.VMEM((tokens, half), bf),
            pltpu.VMEM((tokens, half), bf),
            pltpu.VMEM(out_weight.shape, bf),
            pltpu.VMEM((GROUPS * (GROUPS + 1) // 2, keys, 2 * rows), jnp.float32),
            pltpu.VMEM((heads, GROUPS, HEAD, keys), bf),
            pltpu.VMEM((GROUPS, rows, half), bf),
            pltpu.VMEM((GROUPS, rows, half), bf),
            pltpu.VMEM((GROUPS, rows, half), bf),
            pltpu.VMEM((GROUPS, rows, width), bf),
            pltpu.VMEM((GROUPS, 2, capacity, depth), bf),
            dma((5,)),
            dma((GROUPS,)),
            dma((GROUPS,)),
            dma((GROUPS,)),
            dma,
            dma((GROUPS,)),
            dma((GROUPS,)),
            dma((8,)),
            dma((8,)),
        ],
        compiler_params=pltpu.CompilerParams(
            collective_id=4, has_side_effects=True, vmem_limit_bytes=VMEM_BYTES
        ),
        name="attention_send",
    )(queries, siblings, keys_all, values_all, out_weight, key_info, query_info)


D = 2048
HEADS = 16
ATT_EXPERTS = 8
FFN_EXPERTS = 4
TRUNK = 1024
SEG = 96
TREE_LEN = 2176
NODES = 13

epsilon = 1e-06
highest = lax.Precision.HIGHEST
bf16 = jnp.bfloat16
f32 = jnp.float32


def tree_layout(places):
    after_trunk = places - TRUNK
    after_branch = after_trunk - 4 * SEG
    segments = jnp.where(
        places < TRUNK,
        0,
        jnp.where(after_branch < 0, 1 + after_trunk // SEG, 5 + after_branch // SEG),
    )
    depths = jnp.where(
        places < TRUNK,
        places,
        jnp.where(after_branch < 0, TRUNK + after_trunk % SEG, TRUNK + SEG + after_branch % SEG),
    )
    return (segments.astype(jnp.int32), depths.astype(jnp.int32))


def rotation_tables(depths):
    half_size = HEAD // 2
    frequency = 10000.0 ** (-jnp.arange(half_size, dtype=f32) * 2.0 / HEAD)
    angles = depths.astype(f32)[:, None] * frequency[None, :]
    cosine, sine = jnp.cos(angles), jnp.sin(angles)
    cosines = jnp.concatenate([cosine, cosine], axis=1)
    forward = jnp.concatenate([-sine, sine], axis=1)
    return (cosines, forward), (cosines, -forward)


def lookup(table, indices):
    nodes = jnp.arange(NODES, dtype=jnp.int32)
    return jnp.sum(jnp.where(indices[:, None] == nodes[None, :], table[None, :], 0), axis=1)


def running_count(chosen):
    rows = chosen.shape[-1]
    index = jnp.arange(rows, dtype=jnp.int32)
    upto = (index[:, None] <= index[None, :]).astype(bf16)
    return jnp.dot(chosen.astype(bf16), upto, preferred_element_type=f32).astype(jnp.int32) - 1


def source_plan(routes, expert, capacity):
    chosen = jnp.any(routes == expert, axis=2)
    ranking = running_count(chosen)
    slots = jnp.arange(capacity, dtype=jnp.int32)
    return chosen[:, None, :] & (ranking[:, None, :] == slots[None, :, None])


def token_picks(routes, experts, capacity):
    labels = jnp.arange(experts, dtype=jnp.int32)
    hits = routes.T[:, None, :] == labels[None, :, None]
    ranking = running_count(hits[0] | hits[1])
    slots = jnp.arange(capacity, dtype=jnp.int32)
    picks = hits[:, :, None, :] & (ranking[None, :, None, :] == slots[None, None, :, None])
    return picks.astype(bf16), hits[0].T.astype(f32), hits[1].T.astype(f32)


def fill_slots(picks, pair):
    return jnp.einsum("kecr,krd->ecd", picks, pair, preferred_element_type=f32).astype(bf16)


def read_slots(picks, slots):
    return jnp.einsum("kecr,ecd->krd", picks, slots, preferred_element_type=f32)


def gate_values(hidden, router, first, second):
    logits = jnp.dot(hidden.astype(f32), router, precision=highest)
    picked = jnp.stack([jnp.sum(logits * first, axis=1), jnp.sum(logits * second, axis=1)], axis=1)
    return jax.nn.softmax(picked, axis=1)


def router_grads(hidden, router, gates, first, second, picked_grad):
    logit_pick = gates * (picked_grad - jnp.sum(gates * picked_grad, axis=1, keepdims=True))
    logit_grad = logit_pick[:, 0:1] * first + logit_pick[:, 1:2] * second
    router_grad = jnp.dot(hidden.astype(f32).T, logit_grad, precision=highest)
    hidden_grad = jnp.dot(logit_grad, router.T, precision=highest)
    return (router_grad, hidden_grad)


def rms_parts(values):
    inverse = lax.rsqrt(jnp.mean(values * values, axis=-1, keepdims=True) + epsilon)
    return (values * inverse, inverse)


def norm_back(grad_normed, normed, inverse):
    return inverse * (grad_normed - normed * jnp.mean(grad_normed * normed, axis=-1, keepdims=True))


def pair_grads(gates, branches, upstream):
    gate_grad = jnp.stack([jnp.sum(upstream * branches[k], axis=1) for k in range(2)], axis=1)
    scaled = jnp.stack([gates[:, k : k + 1] * upstream for k in range(2)]).astype(bf16)
    return gate_grad, scaled


def exchange(slots):
    return lax.all_to_all(slots, "expert", split_axis=0, concat_axis=0, tiled=True)


def shift(values, step, size, devices):
    moves = [(i, i // size * size + (i % size + step) % size) for i in range(devices)]
    return lax.ppermute(values, "expert", moves)


def group_gather(rows, size, devices):
    return jnp.concatenate([rows] + [shift(rows, step, size, devices) for step in range(1, size)])


def group_reduce(partial, size, devices):
    parts = partial.reshape(size, -1, partial.shape[1])
    total = parts[0].astype(f32)
    for step in range(1, size):
        total = total + shift(parts[step], -step, size, devices).astype(f32)
    return total.astype(bf16)


def spread_over_replicas(block, my_replica, replicas):
    if replicas != 4:
        return lax.all_gather(block, "dp", axis=0), jnp.arange(replicas, dtype=jnp.int32)
    across, along = ([(i, i ^ n) for i in range(4)] for n in (1, 2))
    first, second = lax.ppermute(block, "dp", across), lax.ppermute(block, "dp", along)
    cut = block.shape[0] // 2
    upper, lower = lax.ppermute(second[:cut], "dp", across), lax.ppermute(first[cut:], "dp", along)
    blocks = jnp.stack([block, first, second, jnp.concatenate([upper, lower])])
    return blocks, my_replica ^ jnp.arange(4, dtype=jnp.int32)


def dot_tn(left, right):
    return lax.dot_general(left, right, (((0,), (0,)), ((), ())), preferred_element_type=f32)


def body(
    tokens,
    teacher,
    att_routes,
    ffn_routes,
    parent,
    valid,
    gain_one,
    kv_weight,
    att_router,
    q_weight,
    o_weight,
    gain_two,
    ffn_router,
    gate_weight,
    up_weight,
    down_weight,
):
    row_count = tokens.shape[0]
    devices, replicas = lax.axis_size("expert"), lax.axis_size("dp")
    my_index, my_replica = lax.axis_index("expert"), lax.axis_index("dp")
    core = my_index % 2
    att_copies, ffn_copies = devices // ATT_EXPERTS, devices // FFN_EXPERTS
    att_capacity, ffn_capacity = row_count * 13 // 40, row_count * 13 // 20
    token_count = row_count * devices
    half = HEADS * HEAD // 2
    assert token_count == TREE_LEN * parent.shape[0] and parent.shape[0] == 1
    pair = [(i, i ^ 1) for i in range(devices)]
    own_places = my_index * row_count + jnp.arange(row_count, dtype=jnp.int32)

    x_in = tokens.astype(f32)
    normed_one, inverse_one = rms_parts(x_in)
    hidden = (normed_one * gain_one).astype(bf16)
    weight_rows = kv_weight.shape[0]
    piece = half // replicas
    kv_share = lax.dynamic_slice_in_dim(
        kv_weight.reshape(weight_rows, 4, replicas, piece), my_replica, 1, 2
    )
    kv_share = (
        kv_share.reshape(weight_rows, 2, 2, piece).transpose(0, 2, 1, 3).reshape(weight_rows, 4 * piece)
    )
    kv_gathered = lax.all_gather(kv_share, "expert", axis=0)
    hidden_all = lax.all_gather(hidden, "expert", axis=0)
    all_routes = lax.all_gather(att_routes, "expert", axis=0)

    tree_places = jnp.arange(token_count, dtype=jnp.int32)
    tree_segments, tree_depths = tree_layout(tree_places)
    key_forward, key_backward = rotation_tables(tree_depths)
    key_info = jnp.pad(jnp.stack([tree_places, tree_segments], axis=1), ((0, 0), (0, 6)))
    experts_here = [my_index // att_copies]
    if att_copies == 1:
        experts_here.append(my_index ^ 1)
    plans = [source_plan(all_routes, expert, att_capacity) for expert in experts_here]
    slot_tables, query_parts = [], []
    for plan in plans:
        places = jnp.sum(
            jnp.where(plan, tree_places.reshape(devices, 1, row_count), 0), axis=2
        ).reshape(-1)
        segments, depths = tree_layout(places)
        parents = lookup(parent[0], segments)
        grands = lookup(parent[0], parents)
        query_parts.append(jnp.stack([places, segments, parents, grands]).reshape(4, GROUPS, -1))
        slot_tables.append(rotation_tables(depths))
    query_info = jnp.concatenate(query_parts, axis=2).transpose(1, 0, 2)
    own_plan = plans[0].astype(bf16)
    att_picks, att_first, att_second = token_picks(att_routes, ATT_EXPERTS, att_capacity)
    att_gates = gate_values(hidden, att_router, att_first, att_second)
    ffn_picks, ffn_first, ffn_second = token_picks(ffn_routes, FFN_EXPERTS, ffn_capacity)
    prepared = (key_forward, key_backward, key_info, slot_tables, query_info, own_plan, att_picks, att_gates, ffn_picks)
    kv_gathered, prepared = lax.optimization_barrier((kv_gathered, prepared))
    kv_half = lax.dynamic_slice_in_dim(kv_gathered, core * 2 * piece, 2 * piece, 2).reshape(D, 2 * piece)
    kv_blocks, block_order = spread_over_replicas(kv_half, my_replica, replicas)
    hidden_all, kv_blocks = lax.optimization_barrier((hidden_all, kv_blocks))
    key_forward, key_backward, key_info, slot_tables, query_info, own_plan, att_picks, att_gates, ffn_picks = prepared

    queries, query_inputs = project_queries(own_plan, hidden_all, q_weight, slot_tables[0][0])
    keys_all, values_all = project_keys_values(hidden_all, kv_blocks, key_forward, block_order)

    def far_half(values):
        return lax.ppermute(
            lax.dynamic_slice_in_dim(values, (1 - core) * half, half, 1), "expert", pair
        )

    def join_halves(mine, sibling):
        other = lax.ppermute(sibling, "expert", pair)
        return jnp.where(
            core == 0,
            jnp.concatenate([mine, other], axis=1),
            jnp.concatenate([other, mine], axis=1),
        )

    heads = half // HEAD
    query_sets = [queries]
    starts = jnp.zeros((2,), jnp.int32)
    if att_copies == 1:
        query_sets.append(far_half(queries))
        starts = jnp.stack([core * heads, 0]).astype(jnp.int32)
    fused = devices == 8 and replicas == 4 and att_copies == 1 and ffn_copies == 2 and ffn_capacity % 16 == 0
    if fused:
        *att_outs, att_rows, att_back, lse = attention_send(
            *query_sets, keys_all, values_all, o_weight, key_info, query_info, att_capacity
        )
        att_everywhere = lax.all_gather(att_rows, "dp", axis=0, tiled=True)
    else:
        *att_outs, lse = attention_forward(
            query_sets, starts // 2, keys_all, values_all, key_info, query_info, heads
        )
        att_rows = join_halves(*att_outs) if att_copies == 1 else att_outs[0]
        att_partial = lax.dot_general(
            att_rows, o_weight, (((1,), (1,)), ((), ())), preferred_element_type=f32
        ).astype(bf16)
        att_back = exchange(att_partial.reshape(devices, att_capacity, D))
    if att_copies > 1:
        att_back = (
            att_back.astype(f32).reshape(ATT_EXPERTS, att_copies, att_capacity, D).sum(axis=1).astype(bf16)
        )
    att_branches = read_slots(att_picks, att_back)
    x_mid = x_in + att_gates[:, 0:1] * att_branches[0] + att_gates[:, 1:2] * att_branches[1]

    normed_two, inverse_two = rms_parts(x_mid)
    hidden_two = (normed_two * gain_two).astype(bf16)
    ffn_gates = gate_values(hidden_two, ffn_router, ffn_first, ffn_second)

    def to_experts(slots):
        rows = exchange(slots.reshape(devices, ffn_capacity // ffn_copies, D))
        return group_gather(rows.reshape(-1, D), ffn_copies, devices)

    def to_tokens(partial):
        rows = group_reduce(partial.astype(bf16), ffn_copies, devices)
        back = exchange(rows.reshape(devices, ffn_capacity // ffn_copies, D))
        return read_slots(ffn_picks, back.reshape(FFN_EXPERTS, ffn_capacity, D))

    ffn_slots = jnp.einsum(
        "ecr,rd->ecd", ffn_picks[0] + ffn_picks[1], hidden_two, preferred_element_type=f32
    ).astype(bf16)
    if fused:
        ffn_inputs, gate_pre, up_pre, activated, ffn_back = ffn_forward(
            ffn_slots, gate_weight, up_weight, down_weight
        )
        ffn_branches = read_slots(ffn_picks, ffn_back)
    else:
        ffn_inputs = to_experts(ffn_slots)
        gate_pre = jnp.dot(ffn_inputs, gate_weight, preferred_element_type=f32)
        up_pre = jnp.dot(ffn_inputs, up_weight, preferred_element_type=f32)
        sigmoid_gate = jax.nn.sigmoid(gate_pre)
        silu_gate = gate_pre * sigmoid_gate
        activated = (silu_gate * up_pre).astype(bf16)
        ffn_branches = to_tokens(
            lax.dot_general(
                activated, down_weight, (((1,), (1,)), ((), ())), preferred_element_type=f32
            )
        )
    result = x_mid + ffn_gates[:, 0:1] * ffn_branches[0] + ffn_gates[:, 1:2] * ffn_branches[1]

    tree_global = my_replica * parent.shape[0] + own_places // TREE_LEN
    tree_labels = jnp.arange(valid.shape[0], dtype=jnp.int32)
    limits = jnp.sum(
        jnp.where(tree_global[:, None] == tree_labels[None, :], valid[None, :], 0), axis=1
    )
    counted = own_places % TREE_LEN < limits
    loss_factor = valid.shape[0] * TREE_LEN / jnp.sum(valid).astype(f32)
    grad_result = jnp.where(counted[:, None], (result - teacher.astype(f32)) * loss_factor, 0.0)

    ffn_gate_grad, ffn_scaled = pair_grads(ffn_gates, ffn_branches, grad_result)
    ffn_grad_slots = fill_slots(ffn_picks, ffn_scaled)
    if fused:
        ffn_grad_slots, att_everywhere = lax.optimization_barrier((ffn_grad_slots, att_everywhere))
        grad_ffn_out, grad_down = send_rows(ffn_grad_slots, activated)
        grad_ffn_out = grad_ffn_out.reshape(-1, D)
    else:
        grad_ffn_out = to_experts(ffn_grad_slots)
        grad_down = dot_tn(grad_ffn_out, activated).astype(bf16)
    grad_ffn_out, grad_down = lax.optimization_barrier((grad_ffn_out, grad_down))
    summed_down = lax.psum_scatter(grad_down, "dp", scatter_dimension=0, tiled=True)
    if fused:
        grad_gate_pre, grad_up_pre, ffn_grad_back = ffn_backward(
            grad_ffn_out, gate_pre, up_pre, gate_weight, up_weight, down_weight, ffn_capacity
        )
        grad_gate = dot_tn(ffn_inputs, grad_gate_pre).astype(bf16)
        ffn_grad_back, grad_gate = lax.optimization_barrier((ffn_grad_back, grad_gate))
        ffn_grad_pair = read_slots(ffn_picks, ffn_grad_back)
    else:
        grad_activated = jnp.dot(grad_ffn_out, down_weight, preferred_element_type=f32)
        grad_gate_pre = (
            grad_activated * up_pre * sigmoid_gate * (1.0 + gate_pre * (1.0 - sigmoid_gate))
        ).astype(bf16)
        grad_up_pre = (grad_activated * silu_gate).astype(bf16)
        grad_ffn_in = lax.dot_general(
            grad_gate_pre, gate_weight, (((1,), (1,)), ((), ())), preferred_element_type=f32
        ) + lax.dot_general(
            grad_up_pre, up_weight, (((1,), (1,)), ((), ())), preferred_element_type=f32
        )
        grad_gate = dot_tn(ffn_inputs, grad_gate_pre).astype(bf16)
        ffn_grad_pair = to_tokens(grad_ffn_in)
    summed_gate = lax.psum_scatter(grad_gate, "dp", scatter_dimension=0, tiled=True)
    grad_ffn_router, hidden_two_extra = router_grads(
        hidden_two, ffn_router, ffn_gates, ffn_first, ffn_second, ffn_gate_grad
    )
    grad_hidden_two = ffn_grad_pair[0] + ffn_grad_pair[1] + hidden_two_extra
    grad_gain_two = jnp.sum(grad_hidden_two * normed_two, axis=0)
    grad_mid = grad_result + norm_back(grad_hidden_two * gain_two, normed_two, inverse_two)

    att_gate_grad, att_scaled = pair_grads(att_gates, att_branches, grad_mid)
    att_slots = fill_slots(att_picks, att_scaled)
    if att_copies > 1:
        att_slots = jnp.repeat(att_slots, att_copies, axis=0)
    att_slots, summed_down = lax.optimization_barrier((att_slots, summed_down))
    if fused:
        grad_att_out, grad_up = send_slots(att_slots, ffn_inputs, grad_up_pre)
        grad_att_out = grad_att_out.reshape(-1, D)
    else:
        grad_att_out = exchange(att_slots).reshape(-1, D)
        grad_up = dot_tn(ffn_inputs, grad_up_pre).astype(bf16)
        grad_att_out, grad_up = lax.optimization_barrier((grad_att_out, grad_up))
    summed_up = lax.psum_scatter(grad_up, "dp", scatter_dimension=0, tiled=True)
    grad_heads = jnp.dot(grad_att_out, o_weight, preferred_element_type=f32).astype(bf16)
    grad_heads, grad_att_out = lax.optimization_barrier((grad_heads, grad_att_out))
    grad_sets = [grad_heads]
    if att_copies == 1:
        grad_sets.append(far_half(grad_heads))
    if fused:
        share = D // replicas

        def columns_of(replica):
            return lax.dynamic_slice_in_dim(grad_att_out, replica * share, share, 1)

        grad_columns = [columns_of(my_replica)] + [
            lax.ppermute(columns_of(my_replica ^ n), "dp", [(i, i ^ n) for i in range(replicas)])
            for n in range(1, replicas)
        ]
    else:
        grad_o = dot_tn(grad_att_out, att_rows).astype(bf16)
        summed_o = lax.psum_scatter(grad_o, "dp", scatter_dimension=0, tiled=True).astype(f32)
    *grad_queries, grad_keys_values = attention_backward(
        query_sets,
        starts,
        grad_sets,
        att_outs,
        keys_all,
        values_all,
        lse,
        key_info,
        query_info,
        key_backward,
        [tables[1] for tables in slot_tables],
        heads,
    )
    grad_keys_values, summed_gate = lax.optimization_barrier((grad_keys_values, summed_gate))
    grad_query_pre = join_halves(*grad_queries) if att_copies == 1 else grad_queries[0]
    grad_kv = dot_tn(hidden_all.reshape(token_count, D), grad_keys_values).astype(bf16)
    grad_q = dot_tn(query_inputs, grad_query_pre).astype(bf16)
    summed_kv = lax.psum_scatter(grad_kv, "dp", scatter_dimension=0, tiled=True)
    summed_q = lax.psum_scatter(grad_q, "dp", scatter_dimension=0, tiled=True)
    grad_query_in = lax.dot_general(
        grad_query_pre, q_weight, (((1,), (1,)), ((), ())), preferred_element_type=f32
    ).astype(bf16)
    grad_query_in, grad_kv, grad_q, summed_up = lax.optimization_barrier(
        (grad_query_in, grad_kv, grad_q, summed_up)
    )

    merge_args = (
        own_plan.transpose(0, 2, 1),
        grad_query_in.reshape(devices, att_capacity, D),
        grad_keys_values,
        kv_blocks,
    )
    if fused:
        arrived = merge_return(*merge_args)
        arrived, grad_columns, summed_kv = lax.optimization_barrier((arrived, grad_columns, summed_kv))
        column_stack = jnp.stack(grad_columns)
        summed_o = dot_tn(
            jnp.concatenate(
                [lax.dynamic_index_in_dim(column_stack, my_replica ^ n, 0, False) for n in range(replicas)]
            ),
            att_everywhere,
        )
    else:
        merged = merge_hidden_grads(*merge_args, block_order).reshape(devices // 2, 2, row_count, D)
        kept = lax.dynamic_index_in_dim(merged, core, 1, keepdims=False)
        passed = lax.ppermute(
            lax.dynamic_index_in_dim(merged, 1 - core, 1, keepdims=False), "expert", pair
        )
        chip_sum = (kept.astype(f32) + passed.astype(f32)).astype(bf16)
        same_core = [[2 * i + c for i in range(devices // 2)] for c in range(2)]
        arrived = lax.all_to_all(
            chip_sum, "expert", split_axis=0, concat_axis=0, axis_index_groups=same_core, tiled=True
        )
    grad_att_router, hidden_one_extra = router_grads(
        hidden, att_router, att_gates, att_first, att_second, att_gate_grad
    )
    grad_hidden_one = jnp.sum(arrived.astype(f32), axis=0) + hidden_one_extra
    grad_gain_one = jnp.sum(grad_hidden_one * normed_one, axis=0)
    grad_input = grad_mid + norm_back(grad_hidden_one * gain_one, normed_one, inverse_one)

    everyone = devices * replicas
    smalls = [grad_gain_one, grad_gain_two, grad_att_router, grad_ffn_router]
    packed = jnp.concatenate([small.reshape(everyone, -1) for small in smalls], axis=1)
    packed, summed_o = lax.optimization_barrier((packed, summed_o))
    own_smalls = jnp.sum(
        lax.all_to_all(packed, ("dp", "expert"), split_axis=0, concat_axis=0, tiled=True), axis=0
    )
    share = D // everyone
    shared_gain_one = own_smalls[:share]
    shared_gain_two = own_smalls[share : 2 * share]
    shared_att_router = own_smalls[2 * share : (2 + ATT_EXPERTS) * share].reshape(share, ATT_EXPERTS)
    shared_ffn_router = own_smalls[(2 + ATT_EXPERTS) * share :].reshape(share, FFN_EXPERTS)

    kv_rows = exchange(summed_kv.reshape(devices, -1, 2 * half))
    kv_sum = jnp.sum(kv_rows.astype(f32).reshape(devices // 2, 2, -1, 2 * half), axis=0)
    shared_kv = jnp.concatenate(
        [kv_sum[n, :, m * half : (m + 1) * half] for m in range(2) for n in range(2)], axis=1
    )

    return (
        result.astype(bf16),
        grad_input.astype(bf16),
        shared_gain_one,
        shared_kv,
        shared_att_router,
        summed_q.astype(f32),
        summed_o,
        shared_gain_two,
        shared_ffn_router,
        summed_gate.astype(f32),
        summed_up.astype(f32),
        summed_down.astype(f32),
    )


def solution(mesh):
    in_specs = (
        P(("dp", "expert"), None),
        P(("dp", "expert"), None),
        P(("dp", "expert"), None),
        P(("dp", "expert"), None),
        P("dp", None),
        P(),
        P(),
        P("expert", None),
        P(),
        P(None, "expert"),
        P(None, "expert"),
        P(),
        P(),
        P(None, "expert"),
        P(None, "expert"),
        P(None, "expert"),
    )
    out_specs = (
        P(("dp", "expert"), None),
        P(("dp", "expert"), None),
        P(("dp", "expert")),
        P(("dp", "expert"), None),
        P(("dp", "expert"), None),
        P("dp", "expert"),
        P("dp", "expert"),
        P(("dp", "expert")),
        P(("dp", "expert"), None),
        P("dp", "expert"),
        P("dp", "expert"),
        P("dp", "expert"),
    )
    return jax.shard_map(body, mesh=mesh, in_specs=in_specs, out_specs=out_specs, check_vma=False)
```

```python
import functools
import jax
import jax.numpy as jnp
from jax import lax
from jax.experimental import pallas as pl
from jax.experimental.pallas import tpu as pltpu
from jax.sharding import PartitionSpec as P

HEAD = 128
GROUPS = 4
LOG2E = 1.4426950408889634
VMEM_BYTES = 60 * 1024 * 1024


def dot_nt(left, right):
    return lax.dot_general(left, right, (((1,), (1,)), ((), ())), preferred_element_type=jnp.float32)


def dot_nn(left, right):
    return jnp.dot(left, right, preferred_element_type=jnp.float32)


def spin(values, cosine, sine):
    return values * cosine + pltpu.roll(values, HEAD // 2, 1) * sine


def fill_bias(bias_ref, key_ref, query_ref, keys):
    for group in range(GROUPS):
        place = query_ref[group, 0:1, :]
        own, parent, grand = (query_ref[group, 1 + n : 2 + n, :] for n in range(3))

        def one(block, carry, group=group, place=place, own=own, parent=parent, grand=grand):
            at = pl.multiple_of(block * keys, 16)
            key_place = key_ref[pl.ds(at, keys), 0:1]
            key_segment = key_ref[pl.ds(at, keys), 1:2]
            related = (key_segment == own) | (key_segment == parent) | (key_segment == grand)
            allowed = related & (key_place <= place)
            bias_ref[group * (group + 1) // 2 + block] = jnp.where(allowed, 0.0, -1e30)
            return carry

        lax.fori_loop(0, group + 1, one, 0)


def fill_group_bias(bias_ref, key_ref, query_ref, keys, group):
    place, own, parent, grand = (query_ref[group, n : n + 1, :] for n in range(4))

    def one(block, carry):
        at = pl.multiple_of(block * keys, 16)
        key_place = key_ref[pl.ds(at, keys), 0:1]
        key_segment = key_ref[pl.ds(at, keys), 1:2]
        related = (key_segment == own) | (key_segment == parent) | (key_segment == grand)
        bias_ref[block] = jnp.where(related & (key_place <= place), 0.0, -1e30)
        return carry

    lax.fori_loop(0, group + 1, one, 0)


def group_rows(refs, group, rows, lanes):
    parts = [ref[pl.ds(group * rows, rows), lanes] for ref in refs]
    return parts[0] if len(parts) == 1 else jnp.concatenate(parts, axis=0)


def attention_forward_body(sets, step_heads, rows, keys, scale, first_ref, *refs):
    query_refs = refs[:sets]
    key_ref, value_ref, key_info, query_info = refs[sets : sets + 4]
    out_refs = refs[sets + 4 : 2 * sets + 4]
    lse_ref, bias_ref, flipped_ref = refs[2 * sets + 4 :]
    wide = sets * rows

    @pl.when(pl.program_id(0) == 0)
    def _():
        fill_bias(bias_ref, key_info, query_info, keys)

    for head in range(step_heads):
        lanes = pl.ds(head * HEAD, HEAD)
        for block in range(GROUPS):
            values = value_ref[pl.ds(block * keys, keys), lanes].astype(jnp.float32)
            flipped_ref[head, block] = values.T.astype(jnp.bfloat16)
    for group in range(GROUPS):
        queries = [
            group_rows(query_refs, group, rows, pl.ds(head * HEAD, HEAD)) for head in range(step_heads)
        ]

        def one(block, carry, group=group, queries=queries):
            at = pl.multiple_of(block * keys, 16)
            bias = bias_ref[group * (group + 1) // 2 + block]
            result = []
            for head in range(step_heads):
                top, total, mixed = carry[3 * head : 3 * head + 3]
                scores = dot_nt(key_ref[pl.ds(at, keys), pl.ds(head * HEAD, HEAD)], queries[head])
                scores = scores + bias
                new_top = jnp.maximum(top, jnp.max(scores, axis=0, keepdims=True))
                fade = jnp.exp2(top - new_top)
                parts = jnp.exp2(scores - new_top)
                total = total * fade + jnp.sum(parts, axis=0, keepdims=True)
                mixed = mixed * fade + dot_nn(flipped_ref[head, block], parts.astype(jnp.bfloat16))
                result += [new_top, total, mixed]
            return tuple(result)

        start = (
            jnp.full((1, wide), -1e30, jnp.float32),
            jnp.zeros((1, wide), jnp.float32),
            jnp.zeros((HEAD, wide), jnp.float32),
        ) * step_heads
        final = lax.fori_loop(0, group + 1, one, start)
        for head in range(step_heads):
            top, total, mixed = final[3 * head : 3 * head + 3]
            lse_ref[head, group] = top + jnp.log2(total)
            rows_out = (mixed / total).T.astype(jnp.bfloat16)
            for n, ref in enumerate(out_refs):
                ref[pl.ds(group * rows, rows), pl.ds(head * HEAD, HEAD)] = rows_out[
                    n * rows : (n + 1) * rows
                ]


def attention_backward_body(sets, step_heads, rows, keys, scale, first_ref, *refs):
    query_refs, grad_refs, out_refs = (refs[n * sets : (n + 1) * sets] for n in range(3))
    key_ref, value_ref, lse_ref, key_info, query_info = refs[3 * sets : 3 * sets + 5]
    key_cos, key_sin = refs[3 * sets + 5 : 3 * sets + 7]
    table_refs = refs[3 * sets + 7 : 5 * sets + 7]
    rest = refs[5 * sets + 7 :]
    dq_refs = rest[:sets]
    dkv_ref, bias_ref, flipped_ref, dk_acc, dv_acc = rest[sets:]
    half = dkv_ref.shape[1] // 2
    softmax_scale = scale / LOG2E
    key_scale = 1.0 / LOG2E

    @pl.when(pl.program_id(0) == 0)
    def _():
        fill_bias(bias_ref, key_info, query_info, keys)

    dk_acc[...] = jnp.zeros_like(dk_acc)
    dv_acc[...] = jnp.zeros_like(dv_acc)
    for head in range(step_heads):
        lanes = pl.ds(head * HEAD, HEAD)
        for block in range(GROUPS):
            values = key_ref[pl.ds(block * keys, keys), lanes].astype(jnp.float32)
            flipped_ref[head, block] = values.T.astype(jnp.bfloat16)
    for group in range(GROUPS):
        queries, grads, centres, tops = [], [], [], []
        for head in range(step_heads):
            lanes = pl.ds(head * HEAD, HEAD)
            queries.append(group_rows(query_refs, group, rows, lanes))
            grad = group_rows(grad_refs, group, rows, lanes)
            out = group_rows(out_refs, group, rows, lanes)
            product = grad.astype(jnp.float32) * out.astype(jnp.float32)
            centres.append(jnp.sum(product.T, axis=0, keepdims=True))
            grads.append(grad)
            tops.append(lse_ref[head, group])

        def one(block, carry, group=group, queries=queries, grads=grads, centres=centres, tops=tops):
            at = pl.multiple_of(block * keys, 16)
            bias = bias_ref[group * (group + 1) // 2 + block]
            result = []
            for head in range(step_heads):
                lanes = pl.ds(head * HEAD, HEAD)
                key_rows = key_ref[pl.ds(at, keys), lanes]
                scores = dot_nt(key_rows, queries[head])
                probs = jnp.exp2(scores + (bias - tops[head]))
                grad_probs = dot_nt(value_ref[pl.ds(at, keys), lanes], grads[head])
                grad_scores = (probs * (grad_probs - centres[head])).astype(jnp.bfloat16)
                dv_acc[pl.ds(at, keys), lanes] += dot_nn(probs.astype(jnp.bfloat16), grads[head])
                dk_acc[pl.ds(at, keys), lanes] += dot_nn(grad_scores, queries[head])
                result.append(carry[head] + dot_nn(flipped_ref[head, block], grad_scores))
            return tuple(result)

        start = (jnp.zeros((HEAD, sets * rows), jnp.float32),) * step_heads
        final = lax.fori_loop(0, group + 1, one, start)
        for head in range(step_heads):
            dq = final[head].T * softmax_scale
            for n, ref in enumerate(dq_refs):
                span = pl.ds(group * rows, rows)
                turned = spin(
                    dq[n * rows : (n + 1) * rows], table_refs[2 * n][span, :], table_refs[2 * n + 1][span, :]
                )
                ref[span, pl.ds(head * HEAD, HEAD)] = turned.astype(jnp.bfloat16)
    for head in range(step_heads):
        lanes = pl.ds(head * HEAD, HEAD)
        first_lane = pl.multiple_of((pl.program_id(0) * step_heads + head) * HEAD, HEAD)
        for block in range(GROUPS):
            span = pl.ds(block * keys, keys)
            turned = spin(dk_acc[span, lanes] * key_scale, key_cos[span, :], key_sin[span, :])
            dkv_ref[span, pl.ds(first_lane, HEAD)] = turned.astype(jnp.bfloat16)
            dkv_ref[span, pl.ds(half + first_lane, HEAD)] = dv_acc[span, lanes].astype(jnp.bfloat16)


def whole_block(shape):
    return pl.BlockSpec(shape, lambda h, first: (0,) * len(shape))


def attention_forward(queries, starts, keys_all, values_all, key_info, query_info, heads):
    sets, total_rows, tokens = len(queries), queries[0].shape[0], keys_all.shape[0]
    rows, keys = total_rows // GROUPS, tokens // GROUPS
    step_heads = 2
    wide = step_heads * HEAD
    scale = HEAD ** (-0.5) * LOG2E
    query_specs = [
        pl.BlockSpec((total_rows, wide), lambda h, first, n=n: (0, first[n] + h)) for n in range(sets)
    ]
    plain = pl.BlockSpec((total_rows, wide), lambda h, first: (0, h))
    side = pl.BlockSpec((tokens, wide), lambda h, first: (0, h))
    return pl.pallas_call(
        functools.partial(attention_forward_body, sets, step_heads, rows, keys, scale),
        grid_spec=pltpu.PrefetchScalarGridSpec(
            num_scalar_prefetch=1,
            grid=(heads // step_heads,),
            in_specs=query_specs
            + [side, side, whole_block(key_info.shape), whole_block(query_info.shape)],
            out_specs=[plain] * sets
            + [pl.BlockSpec((step_heads, GROUPS, 1, sets * rows), lambda h, first: (h, 0, 0, 0))],
            scratch_shapes=[
                pltpu.VMEM((GROUPS * (GROUPS + 1) // 2, keys, sets * rows), jnp.float32),
                pltpu.VMEM((step_heads, GROUPS, HEAD, keys), jnp.bfloat16),
            ],
        ),
        out_shape=[jax.ShapeDtypeStruct((total_rows, heads * HEAD), jnp.bfloat16)] * sets
        + [jax.ShapeDtypeStruct((heads, GROUPS, 1, sets * rows), jnp.float32)],
        compiler_params=pltpu.CompilerParams(vmem_limit_bytes=VMEM_BYTES),
        name="attention_forward",
    )(starts, *queries, keys_all, values_all, key_info, query_info)


def attention_backward(
    queries, starts, grads, outs, keys_all, values_all, lse, key_info, query_info, key_tables, row_tables, heads
):
    sets, total_rows, tokens = len(queries), queries[0].shape[0], keys_all.shape[0]
    rows, keys = total_rows // GROUPS, tokens // GROUPS
    step_heads = 1
    wide = step_heads * HEAD
    scale = HEAD ** (-0.5) * LOG2E
    shifted = [
        pl.BlockSpec((total_rows, wide), lambda h, first, n=n: (0, first[n] + h)) for n in range(sets)
    ]
    plain = pl.BlockSpec((total_rows, wide), lambda h, first: (0, h))
    side = pl.BlockSpec((tokens, wide), lambda h, first: (0, h))
    return pl.pallas_call(
        functools.partial(attention_backward_body, sets, step_heads, rows, keys, scale),
        grid_spec=pltpu.PrefetchScalarGridSpec(
            num_scalar_prefetch=1,
            grid=(heads // step_heads,),
            in_specs=shifted
            + shifted
            + [plain] * sets
            + [
                side,
                side,
                pl.BlockSpec((step_heads, GROUPS, 1, sets * rows), lambda h, first: (h, 0, 0, 0)),
                whole_block(key_info.shape),
                whole_block(query_info.shape),
                whole_block((tokens, HEAD)),
                whole_block((tokens, HEAD)),
            ]
            + [whole_block((total_rows, HEAD))] * (2 * sets),
            out_specs=[plain] * sets + [whole_block((tokens, 2 * heads * HEAD))],
            scratch_shapes=[
                pltpu.VMEM((GROUPS * (GROUPS + 1) // 2, keys, sets * rows), jnp.float32),
                pltpu.VMEM((step_heads, GROUPS, HEAD, keys), jnp.bfloat16),
                pltpu.VMEM((tokens, wide), jnp.float32),
                pltpu.VMEM((tokens, wide), jnp.float32),
            ],
        ),
        out_shape=[jax.ShapeDtypeStruct((total_rows, heads * HEAD), jnp.bfloat16)] * sets
        + [jax.ShapeDtypeStruct((tokens, 2 * heads * HEAD), jnp.bfloat16)],
        compiler_params=pltpu.CompilerParams(vmem_limit_bytes=VMEM_BYTES),
        name="attention_backward",
    )(
        starts,
        *queries,
        *grads,
        *outs,
        keys_all,
        values_all,
        lse,
        key_info,
        query_info,
        *key_tables,
        *[table for pair in row_tables for table in pair],
    )


def project_body(scale, plan_ref, hidden_ref, weight_ref, cos_ref, sin_ref, out_ref, x_ref):
    sources, capacity = plan_ref.shape[0], plan_ref.shape[1]
    bundle = max(1, sources * capacity // GROUPS // capacity)
    tile = bundle * capacity

    @pl.when(pl.program_id(0) == 0)
    def _():
        for group in range(sources // bundle):
            parts = [
                dot_nn(plan_ref[group * bundle + n], hidden_ref[group * bundle + n]) for n in range(bundle)
            ]
            x_ref[pl.ds(group * tile, tile), :] = jnp.concatenate(parts, axis=0).astype(jnp.bfloat16)

    for at in range(0, x_ref.shape[0], tile):
        span = pl.ds(at, tile)
        product = dot_nn(x_ref[span, :], weight_ref[...])
        for lane in range(0, out_ref.shape[1], HEAD):
            turned = spin(product[:, lane : lane + HEAD], cos_ref[span, :], sin_ref[span, :])
            out_ref[span, lane : lane + HEAD] = (turned * scale).astype(jnp.bfloat16)


def project_queries(plan, hidden, weight, tables):
    sources, capacity, row_count = plan.shape
    depth, columns = weight.shape
    rows = sources * capacity
    block = 512
    return pl.pallas_call(
        functools.partial(project_body, HEAD ** (-0.5) * LOG2E),
        grid=(columns // block,),
        in_specs=[
            pl.BlockSpec((sources, capacity, row_count), lambda j: (0, 0, 0)),
            pl.BlockSpec((sources, row_count, depth), lambda j: (0, 0, 0)),
            pl.BlockSpec((depth, block), lambda j: (0, j)),
            pl.BlockSpec((rows, HEAD), lambda j: (0, 0)),
            pl.BlockSpec((rows, HEAD), lambda j: (0, 0)),
        ],
        out_specs=[
            pl.BlockSpec((rows, block), lambda j: (0, j)),
            pl.BlockSpec((rows, depth), lambda j: (0, 0)),
        ],
        out_shape=[
            jax.ShapeDtypeStruct((rows, columns), jnp.bfloat16),
            jax.ShapeDtypeStruct((rows, depth), jnp.bfloat16),
        ],
        compiler_params=pltpu.CompilerParams(vmem_limit_bytes=VMEM_BYTES),
        name="project_queries",
    )(plan, hidden, weight, *tables)


def keys_values_body(half, order_ref, x_ref, weight_ref, cos_ref, sin_ref, key_ref, value_ref):
    rows = x_ref.shape[1]
    for source in range(x_ref.shape[0]):
        span = pl.ds(source * rows, rows)
        product = dot_nn(x_ref[source], weight_ref[0])
        for lane in range(0, half, HEAD):
            turned = spin(product[:, lane : lane + HEAD], cos_ref[span, :], sin_ref[span, :])
            key_ref[span, lane : lane + HEAD] = turned.astype(jnp.bfloat16)
        value_ref[span, :] = product[:, half:].astype(jnp.bfloat16)


def project_keys_values(hidden, weights, tables, order):
    sources, rows, unused = hidden.shape
    parts, depth, columns = weights.shape
    half, tokens = columns // 2, sources * rows
    return pl.pallas_call(
        functools.partial(keys_values_body, half),
        grid_spec=pltpu.PrefetchScalarGridSpec(
            num_scalar_prefetch=1,
            grid=(parts,),
            in_specs=[
                pl.BlockSpec((sources, rows, depth), lambda j, order: (0, 0, 0)),
                pl.BlockSpec((1, depth, columns), lambda j, order: (j, 0, 0)),
                pl.BlockSpec((tokens, HEAD), lambda j, order: (0, 0)),
                pl.BlockSpec((tokens, HEAD), lambda j, order: (0, 0)),
            ],
            out_specs=[pl.BlockSpec((tokens, half), lambda j, order: (0, order[j]))] * 2,
        ),
        out_shape=[jax.ShapeDtypeStruct((tokens, parts * half), jnp.bfloat16)] * 2,
        compiler_params=pltpu.CompilerParams(vmem_limit_bytes=VMEM_BYTES),
        name="project_keys_values",
    )(order, hidden, weights, *tables)


def merge_body(tile, order_ref, plan_ref, slots_ref, dk_ref, dv_ref, weight_ref, out_ref, acc_ref):
    part = pl.program_id(1)
    sources, rows = plan_ref.shape[0], plan_ref.shape[1]
    ck = dk_ref.shape[1]

    @pl.when(part == 0)
    def _():
        for source in range(sources):
            acc_ref[pl.ds(source * rows, rows), :] = dot_nn(plan_ref[source], slots_ref[source])

    last = part == pl.num_programs(1) - 1
    for at in range(0, acc_ref.shape[0], tile):
        span = pl.ds(at, tile)
        acc_ref[span, :] += dot_nt(dk_ref[span, :], weight_ref[0, :, :ck]) + dot_nt(
            dv_ref[span, :], weight_ref[0, :, ck:]
        )

    @pl.when(last)
    def _():
        out_ref[...] = acc_ref[...].astype(jnp.bfloat16)


def merge_hidden_grads(plan, slots, grads, weights, order):
    sources, rows, capacity = plan.shape
    parts, depth, columns = weights.shape
    ck, tokens = columns // 2, sources * rows
    wide = depth // 2
    return pl.pallas_call(
        functools.partial(merge_body, tokens // GROUPS),
        grid_spec=pltpu.PrefetchScalarGridSpec(
            num_scalar_prefetch=1,
            grid=(2, parts),
            in_specs=[
                pl.BlockSpec((sources, rows, capacity), lambda i, j, order: (0, 0, 0)),
                pl.BlockSpec((sources, capacity, wide), lambda i, j, order: (0, 0, i)),
                pl.BlockSpec((tokens, ck), lambda i, j, order: (0, order[j])),
                pl.BlockSpec((tokens, ck), lambda i, j, order: (0, parts + order[j])),
                pl.BlockSpec((1, wide, columns), lambda i, j, order: (j, i, 0)),
            ],
            out_specs=pl.BlockSpec((tokens, wide), lambda i, j, order: (0, i)),
            scratch_shapes=[pltpu.VMEM((tokens, wide), jnp.float32)],
        ),
        out_shape=jax.ShapeDtypeStruct((tokens, depth), jnp.bfloat16),
        compiler_params=pltpu.CompilerParams(vmem_limit_bytes=VMEM_BYTES),
        name="merge_hidden_grads",
    )(order, plan, slots, grads, grads, weights)


def mesh_device(index):
    return {"expert": index}


def chip_order(chip, step):
    flip = chip // 2
    near = chip + flip * (3 - 2 * chip)
    place = step + near * (1 - 2 * step) if step < 2 else step
    return place + flip * (3 - 2 * place)


def far_order(chip, step):
    return chip_order(chip, 3 - step)


def is_middle(chip):
    flip = chip // 2
    return chip + flip * (3 - 2 * chip)


def crossing_order(chip, step):
    end, middle = chip_order(chip, step), chip_order(chip, (2, 3, 1, 0)[step])
    return end + is_middle(chip) * (middle - end)


def enter(devices, me):
    barrier = pltpu.get_barrier_semaphore()
    for step in range(1, devices):
        pl.semaphore_signal(
            barrier,
            inc=1,
            device_id=mesh_device(lax.rem(me + step, devices)),
            device_id_type=pl.DeviceIdType.MESH,
        )
    pl.semaphore_wait(barrier, devices - 1)


def remote(source, target, send, recv, device):
    return pltpu.make_async_remote_copy(
        src_ref=source,
        dst_ref=target,
        send_sem=send,
        recv_sem=recv,
        device_id=mesh_device(device),
        device_id_type=pl.DeviceIdType.MESH,
    )


class Dispatch:
    def __init__(self, me, order, slots, landing, local_sem, send, recv, pass_send, pass_recv):
        self.me, self.chip, self.core, self.order = me, me // 2, lax.rem(me, 2), order
        self.sending = stagger_order if order is stagger_order else chip_order
        self.slots, self.landing = slots, landing
        self.local_sem, self.send, self.recv = local_sem, send, recv
        self.pass_send, self.pass_recv = pass_send, pass_recv
        self.rows, self.half = slots.shape[1], slots.shape[2] // 2

    def columns(self, core):
        return pl.ds(pl.multiple_of(core * self.half, 128), self.half)

    def place(self, source, core):
        rows = pl.ds(pl.multiple_of(lax.rem(source, 2) * self.rows, 16), self.rows)
        return self.landing.at[source // 2, rows, self.columns(core)]

    def direct(self, target):
        core = lax.rem(target, 2)
        offset = lax.rem(target - self.me + 8, 8)
        return remote(
            self.slots.at[target // 2, :, self.columns(core)],
            self.place(self.me, core),
            self.send.at[offset],
            self.recv.at[offset],
            target,
        )

    def sends(self, step):
        chip = self.sending(self.chip, step)
        targets = [2 * chip, 2 * chip + 1] if step else [self.me + 1 - 2 * self.core]
        return [self.direct(target) for target in targets]

    def local(self):
        return pltpu.make_async_copy(
            self.slots.at[self.chip, :, self.columns(self.core)],
            self.place(self.me, self.core),
            self.local_sem,
        )

    def start_local(self):
        self.local().start()

    def start(self, steps):
        for step in steps:
            for copy in self.sends(step):
                copy.start()

    def sent(self, steps):
        for step in steps:
            for copy in self.sends(step):
                copy.wait_send()

    def pass_on(self, source):
        place = self.place(source, self.core)
        return remote(
            place, place, self.pass_send.at[source], self.pass_recv.at[source], self.me + 1 - 2 * self.core
        )

    def arrive(self, step):
        chip = self.order(self.chip, step)
        for source in (2 * chip, 2 * chip + 1):
            offset = lax.rem(self.me - source + 8, 8)

            @pl.when(offset == 0)
            def _():
                self.local().wait()

            @pl.when(offset != 0)
            def _(source=source, offset=offset):
                place = self.place(source, self.core)
                remote(place, place, self.send.at[offset], self.recv.at[offset], self.me).wait_recv()

            self.pass_on(source).start()

    def ready(self, step):
        chip = self.order(self.chip, step)
        for source in (2 * chip, 2 * chip + 1):
            place = self.place(source, 1 - self.core)
            remote(
                place, place, self.pass_send.at[source], self.pass_recv.at[source], self.me
            ).wait_recv()
        return chip

    def passed_on(self):
        for source in range(8):
            self.pass_on(source).wait_send()


class Collect:
    def __init__(
        self, me, order, own_steps, kept, passing, passed, total, back, local_sem, pass_send, pass_recv, send, recv
    ):
        self.me, self.chip, self.core = me, me // 2, lax.rem(me, 2)
        self.order, self.own_steps = order, own_steps
        self.kept, self.passing, self.passed, self.total, self.back = kept, passing, passed, total, back
        self.local_sem, self.pass_send, self.pass_recv = local_sem, pass_send, pass_recv
        self.send, self.recv = send, recv
        self.rows, self.half = back.shape[1], back.shape[2] // 2

    def swap(self, step):
        return remote(
            self.passing.at[step % 2],
            self.passed.at[step],
            self.pass_send.at[step],
            self.pass_recv.at[step],
            self.me + 1 - 2 * self.core,
        )

    def place(self, chip, core):
        return self.back.at[chip, :, pl.ds(pl.multiple_of(core * self.half, 128), self.half)]

    def local(self, step, source_core):
        return pltpu.make_async_copy(
            self.total.at[step, pl.ds(pl.multiple_of(source_core * self.rows, 16), self.rows), :],
            self.place(self.chip, self.core),
            self.local_sem,
        )

    def outgoing(self, step, source):
        rows = pl.ds(pl.multiple_of(lax.rem(source, 2) * self.rows, 16), self.rows)
        offset = lax.rem(source - self.me + 8, 8)
        return remote(
            self.total.at[step, rows, :],
            self.place(self.chip, self.core),
            self.send.at[offset],
            self.recv.at[offset],
            source,
        )

    def block(self, step):
        return self.order(self.chip, step)

    def each(self, step, own, other):
        chip = self.block(step)
        for source in (2 * chip, 2 * chip + 1):
            if step not in self.own_steps:
                other(source)
                continue

            @pl.when(source == self.me)
            def _():
                own()

            @pl.when(source != self.me)
            def _(source=source):
                other(source)

    def settle(self, step):
        self.swap(step).wait_recv()
        tile = 2 * self.rows // 4
        for at in range(0, 2 * self.rows, tile):
            span = pl.ds(at, tile)
            summed = self.kept[span, :] + self.passed[step, span, :].astype(jnp.float32)
            self.total[step, span, :] = summed.astype(jnp.bfloat16)
        self.each(
            step,
            lambda: self.local(step, self.core).start(),
            lambda source: self.outgoing(step, source).start(),
        )

    def finish(self):
        for step in range(4):
            if step >= 2:
                self.swap(step).wait_send()
            self.each(
                step,
                lambda step=step: self.local(step, self.core).wait(),
                lambda source, step=step: self.outgoing(step, source).wait_send(),
            )
        for offset in range(1, 8):
            source = lax.rem(self.me + 8 - offset, 8)
            place = self.place(source // 2, lax.rem(source, 2))
            remote(place, place, self.send.at[offset], self.recv.at[offset], self.me).wait_recv()


def ffn_forward_body(
    chunk,
    picks,
    hidden,
    gate_hbm,
    up_hbm,
    down_hbm,
    rows_out,
    gate_out,
    up_out,
    act_out,
    back,
    gate,
    up,
    down,
    slots,
    landing,
    pre_stage,
    act,
    kept,
    passing,
    passed,
    total,
    weight_sem,
    stage_sem,
    act_sem,
    rows_sem,
    local_sem,
    send,
    recv,
    pass_send,
    pass_recv,
    swap_send,
    swap_recv,
    out_send,
    out_recv,
):
    me = lax.axis_index("expert")
    enter(8, me)
    loads = [
        pltpu.make_async_copy(source, target, weight_sem.at[n])
        for n, (source, target) in enumerate(((gate_hbm, gate), (up_hbm, up), (down_hbm, down)))
    ]
    dispatch = Dispatch(me, crossing_order, slots, landing, local_sem.at[0], send, recv, pass_send, pass_recv)
    collect = Collect(
        me, crossing_order, (0, 3), kept, passing, passed, total, back, local_sem.at[1], swap_send, swap_recv, out_send, out_recv
    )
    middle = is_middle(me // 2)
    for load in loads:
        load.start()

    def pack(step):
        chip = chip_order(me // 2, step)
        slots[chip] = dot_nn(picks[chip], hidden[...]).astype(jnp.bfloat16)

    pack(1)
    dispatch.start((1,))
    pack(2)

    @pl.when(middle == 1)
    def _():
        dispatch.start((2,))

    pack(0)
    dispatch.start_local()
    dispatch.start((0,))
    pack(3)
    block = landing.shape[1]
    hidden_units = gate.shape[1]
    chunks = hidden_units // chunk
    half = back.shape[2] // 2

    def stage_copies(chip, part, slot):
        span = pl.ds(pl.multiple_of(chip * block, 16), block)
        columns = pl.ds(pl.multiple_of(part * chunk, 128), chunk)
        return [
            pltpu.make_async_copy(
                pre_stage.at[slot, n], out.at[span, columns], stage_sem.at[slot, n]
            )
            for n, out in enumerate((gate_out, up_out))
        ]

    def act_copy(chip, step):
        span = pl.ds(pl.multiple_of(chip * block, 16), block)
        return pltpu.make_async_copy(act, act_out.at[span, :], act_sem.at[0])

    def rows_copy(chip, step):
        span = pl.ds(pl.multiple_of(chip * block, 16), block)
        return pltpu.make_async_copy(landing.at[chip], rows_out.at[span, :], rows_sem.at[step])

    for step in range(4):
        if step == 0:
            dispatch.arrive(0)
        chip = dispatch.ready(step)
        rows_copy(chip, step).start()
        if step == 0:
            loads[0].wait()
            loads[1].wait()
        if step >= 1:
            act_copy(crossing_order(me // 2, step - 1), step - 1).wait()

        def hidden_part(part, carry, chip=chip, step=step):
            slot = lax.rem(part + step * chunks, 2)
            columns = pl.ds(pl.multiple_of(part * chunk, 128), chunk)

            @pl.when(part + step * chunks >= 2)
            def _():
                for copy in stage_copies(chip, part, slot):
                    copy.wait()

            gated = dot_nn(landing[chip], gate[:, columns])
            raised = dot_nn(landing[chip], up[:, columns])
            pre_stage[slot, 0] = gated.astype(jnp.bfloat16)
            pre_stage[slot, 1] = raised.astype(jnp.bfloat16)
            act[:, columns] = (gated * jax.nn.sigmoid(gated) * raised).astype(jnp.bfloat16)
            for copy in stage_copies(chip, part, slot):
                copy.start()
            if step == 0:
                @pl.when((part == chunks // 3) & (middle == 0))
                def _():
                    dispatch.sent((1,))
                    dispatch.start((2,))

                @pl.when((part == chunks // 2) & (middle == 1))
                def _():
                    dispatch.sent((1, 2))
                    dispatch.start((3,))

            return carry

        lax.fori_loop(0, chunks, hidden_part, 0)
        act_copy(chip, step).start()
        if step == 0:
            loads[2].wait()
        else:
            collect.settle(step - 1)
        core = collect.core
        width = min(512, half)

        def far_part(part, carry, step=step):
            at = pl.multiple_of((1 - core) * half + part * width, 128)
            product = dot_nt(act[...], down[pl.ds(at, width), :])
            passing[step % 2, :, pl.ds(pl.multiple_of(part * width, 128), width)] = product.astype(jnp.bfloat16)
            return carry

        def near_part(part, carry, step=step):
            at = pl.multiple_of(core * half + part * width, 128)
            product = dot_nt(act[...], down[pl.ds(at, width), :])
            kept[:, pl.ds(pl.multiple_of(part * width, 128), width)] = product
            return carry

        if step >= 2:
            collect.swap(step - 2).wait_send()
        lax.fori_loop(0, half // width, far_part, 0)
        collect.swap(step).start()
        if step == 0:

            @pl.when(middle == 0)
            def _():
                dispatch.sent((2,))
                dispatch.start((3,))

        if step < 3:
            dispatch.arrive(step + 1)
        lax.fori_loop(0, half // width, near_part, 0)
    collect.settle(3)
    act_copy(crossing_order(me // 2, 3), 3).wait()
    for step in range(4):
        rows_copy(crossing_order(me // 2, step), step).wait()
    for slot in range(2):
        for copy in stage_copies(0, 0, slot):
            copy.wait()
    dispatch.sent((0, 3))
    dispatch.passed_on()
    collect.finish()


def ffn_forward(picks, hidden, gate_weight, up_weight, down_weight):
    chips, capacity, row_count = picks.shape
    depth = hidden.shape[1]
    here = pl.BlockSpec(memory_space=pltpu.VMEM)
    hidden_units = gate_weight.shape[1]
    block = 2 * capacity
    chunk = 256 if hidden_units % 256 == 0 else 128
    half = depth // 2
    rows = chips * block
    any_space = pl.BlockSpec(memory_space=pl.ANY)
    bf = jnp.bfloat16
    dma = pltpu.SemaphoreType.DMA
    return pl.pallas_call(
        functools.partial(ffn_forward_body, chunk),
        in_specs=[here] * 2 + [any_space] * 3,
        out_specs=[any_space] * 5,
        out_shape=[
            jax.ShapeDtypeStruct((rows, depth), bf),
            jax.ShapeDtypeStruct((rows, hidden_units), bf),
            jax.ShapeDtypeStruct((rows, hidden_units), bf),
            jax.ShapeDtypeStruct((rows, hidden_units), bf),
            jax.ShapeDtypeStruct((chips, capacity, depth), bf),
        ],
        scratch_shapes=[
            pltpu.VMEM((depth, hidden_units), bf),
            pltpu.VMEM((depth, hidden_units), bf),
            pltpu.VMEM((depth, hidden_units), bf),
            pltpu.VMEM((chips, capacity, depth), bf),
            pltpu.VMEM((chips, block, depth), bf),
            pltpu.VMEM((2, 2, block, chunk), bf),
            pltpu.VMEM((block, hidden_units), bf),
            pltpu.VMEM((block, half), jnp.float32),
            pltpu.VMEM((2, block, half), bf),
            pltpu.VMEM((chips, block, half), bf),
            pltpu.VMEM((chips, block, half), bf),
            dma((3,)),
            dma((2, 2)),
            dma((2,)),
            dma((4,)),
            dma((2,)),
            dma((8,)),
            dma((8,)),
            dma((8,)),
            dma((8,)),
            dma((4,)),
            dma((4,)),
            dma((8,)),
            dma((8,)),
        ],
        compiler_params=pltpu.CompilerParams(
            collective_id=1, has_side_effects=True, vmem_limit_bytes=VMEM_BYTES
        ),
        name="ffn_forward",
    )(picks, hidden, gate_weight, up_weight, down_weight)


def stagger_order(chip, step):
    if step < 2:
        return chip_order(chip, step)
    end, middle = chip_order(chip, 5 - step), chip_order(chip, step)
    return end + is_middle(chip) * (middle - end)


def send_rows_body(
    picks,
    pair,
    act_hbm,
    rows_out,
    grad_out,
    slots,
    landing,
    act,
    total,
    stage,
    act_sem,
    rows_sem,
    stage_sem,
    local_sem,
    send,
    recv,
    pass_send,
    pass_recv,
):
    me = lax.axis_index("expert")
    enter(8, me)
    dispatch = Dispatch(me, stagger_order, slots, landing, local_sem.at[0], send, recv, pass_send, pass_recv)

    def pack(step):
        chip = stagger_order(me // 2, step)
        filled = dot_nn(picks[0, chip], pair[0]) + dot_nn(picks[1, chip], pair[1])
        slots[chip] = filled.astype(jnp.bfloat16)

    for step in (2, 1, 0):
        pack(step)
        if step == 0:
            dispatch.start_local()
        dispatch.start((step,))
    pack(3)
    block = landing.shape[1]
    width = stage.shape[1]
    parts = landing.shape[2] // width

    def span_of(step):
        return pl.ds(pl.multiple_of(stagger_order(me // 2, step) * block, 16), block)

    def act_copy(step):
        return pltpu.make_async_copy(
            act_hbm.at[span_of(step), :], act.at[pl.ds(step * block, block), :], act_sem.at[step]
        )

    def rows_copy(step):
        chip = stagger_order(me // 2, step)
        return pltpu.make_async_copy(landing.at[chip], rows_out.at[chip], rows_sem.at[step])

    def stage_copy(part):
        slot = lax.rem(part, 2)
        span = pl.ds(pl.multiple_of(part * width, 16), width)
        return pltpu.make_async_copy(stage.at[slot], grad_out.at[span, :], stage_sem.at[slot])

    for step in range(4):
        act_copy(step).start()
    for steps in ((0, 1), (2,), (3,)):
        for step in steps:
            dispatch.arrive(step)
        chips = [dispatch.ready(step) for step in steps]
        for step in steps:
            rows_copy(step).start()
            act_copy(step).wait()

        def one(part, carry, steps=steps, chips=chips):
            columns = pl.ds(pl.multiple_of(part * width, 128), width)
            rows = [landing[chip, :, columns] for chip in chips]
            rows = rows[0] if len(rows) == 1 else jnp.concatenate(rows, axis=0)
            turned = rows.astype(jnp.float32).T.astype(jnp.bfloat16)
            product = dot_nn(turned, act[pl.ds(steps[0] * block, len(steps) * block), :])
            span = pl.ds(pl.multiple_of(part * width, 16), width)
            if steps[0] == 0:
                total[span, :] = product

                @pl.when(part == 0)
                def _():
                    dispatch.sent((2,))
                    dispatch.start((3,))

                return carry
            if steps[0] == 2:
                total[span, :] += product
                return carry

            @pl.when(part >= 2)
            def _():
                stage_copy(part - 2).wait()

            stage[lax.rem(part, 2)] = (total[span, :] + product).astype(jnp.bfloat16)
            stage_copy(part).start()
            return carry

        lax.fori_loop(0, parts, one, 0)
    for part in (parts - 2, parts - 1):
        stage_copy(part).wait()
    for step in range(4):
        rows_copy(step).wait()
    dispatch.sent((0, 1, 3))
    dispatch.passed_on()


def send_rows(picks, pair, act):
    unused, chips, capacity, row_count = picks.shape
    depth = pair.shape[2]
    here = pl.BlockSpec(memory_space=pltpu.VMEM)
    rows, hidden_units = act.shape
    block = 2 * capacity
    width = min(256, depth // 2)
    any_space = pl.BlockSpec(memory_space=pl.ANY)
    bf = jnp.bfloat16
    dma = pltpu.SemaphoreType.DMA
    return pl.pallas_call(
        send_rows_body,
        in_specs=[here] * 2 + [any_space],
        out_specs=[any_space] * 2,
        out_shape=[
            jax.ShapeDtypeStruct((chips, block, depth), bf),
            jax.ShapeDtypeStruct((depth, hidden_units), bf),
        ],
        scratch_shapes=[
            pltpu.VMEM((chips, capacity, depth), bf),
            pltpu.VMEM((chips, block, depth), bf),
            pltpu.VMEM((rows, hidden_units), bf),
            pltpu.VMEM((depth, hidden_units), jnp.float32),
            pltpu.VMEM((2, width, hidden_units), bf),
            dma((4,)),
            dma((4,)),
            dma((2,)),
            dma((1,)),
            dma((8,)),
            dma((8,)),
            dma((8,)),
            dma((8,)),
        ],
        compiler_params=pltpu.CompilerParams(
            collective_id=2, has_side_effects=True, vmem_limit_bytes=VMEM_BYTES
        ),
        name="send_rows",
    )(picks, pair, act)


def ffn_backward_body(
    chunk,
    grad_rows,
    gate_in,
    up_in,
    gate_hbm,
    up_hbm,
    down_hbm,
    dgate_out,
    dup_out,
    back,
    gate,
    up,
    down,
    grad,
    pre_stage,
    pair,
    kept,
    passing,
    passed,
    total,
    weight_sem,
    grad_sem,
    stage_sem,
    pair_sem,
    local_sem,
    swap_send,
    swap_recv,
    out_send,
    out_recv,
):
    me = lax.axis_index("expert")
    enter(8, me)
    collect = Collect(
        me, far_order, (3,), kept, passing, passed, total, back, local_sem.at[0], swap_send, swap_recv, out_send, out_recv
    )
    loads = [
        pltpu.make_async_copy(source, target, weight_sem.at[n])
        for n, (source, target) in enumerate(((down_hbm, down), (gate_hbm, gate), (up_hbm, up)))
    ]
    block = grad.shape[1]
    hidden_units = gate.shape[1]
    chunks = hidden_units // chunk
    half = back.shape[2] // 2
    width = min(512, half)

    def span_of(chip):
        return pl.ds(pl.multiple_of(chip * block, 16), block)

    def grad_copy(step):
        return pltpu.make_async_copy(
            grad_rows.at[span_of(collect.block(step)), :], grad.at[step % 2], grad_sem.at[step % 2]
        )

    def stage_copies(chip, part, slot):
        columns = pl.ds(pl.multiple_of(part * chunk, 128), chunk)
        return [
            pltpu.make_async_copy(
                source.at[span_of(chip), columns], pre_stage.at[slot, n], stage_sem.at[slot, n]
            )
            for n, source in enumerate((gate_in, up_in))
        ]

    def pair_copies(chip):
        return [
            pltpu.make_async_copy(pair.at[n], out.at[span_of(chip), :], pair_sem.at[n])
            for n, out in enumerate((dgate_out, dup_out))
        ]

    grad_copy(0).start()
    loads[0].start()
    for copy in stage_copies(collect.block(0), 0, 0):
        copy.start()
    loads[1].start()
    loads[2].start()
    loads[0].wait()
    for step in range(4):
        chip = collect.block(step)
        grad_copy(step).wait()
        if step < 3:
            grad_copy(step + 1).start()
        if step > 0:
            for copy in pair_copies(collect.block(step - 1)):
                copy.wait()

        def hidden_part(part, carry, chip=chip, step=step):
            slot = lax.rem(part, 2)
            columns = pl.ds(pl.multiple_of(part * chunk, 128), chunk)
            for copy in stage_copies(chip, part, slot):
                copy.wait()

            @pl.when(part + 1 < chunks)
            def _():
                for copy in stage_copies(chip, part + 1, 1 - slot):
                    copy.start()

            upstream = dot_nn(grad[step % 2], down[:, columns])
            gated = pre_stage[slot, 0].astype(jnp.float32)
            raised = pre_stage[slot, 1].astype(jnp.float32)
            sigmoid = jax.nn.sigmoid(gated)
            scaled = upstream * sigmoid
            pair[0, :, columns] = (scaled * raised * (1.0 + gated * (1.0 - sigmoid))).astype(jnp.bfloat16)
            pair[1, :, columns] = (scaled * gated).astype(jnp.bfloat16)
            return carry

        lax.fori_loop(0, chunks, hidden_part, 0)
        for copy in pair_copies(chip):
            copy.start()
        if step < 3:
            for copy in stage_copies(collect.block(step + 1), 0, 0):
                copy.start()
        if step == 0:
            loads[1].wait()
            loads[2].wait()
        else:
            collect.settle(step - 1)
        core = collect.core

        def product(at):
            return dot_nt(pair[0], gate[pl.ds(at, width), :]) + dot_nt(pair[1], up[pl.ds(at, width), :])

        def far_part(part, carry, step=step):
            at = pl.multiple_of((1 - core) * half + part * width, 128)
            columns = pl.ds(pl.multiple_of(part * width, 128), width)
            passing[step % 2, :, columns] = product(at).astype(jnp.bfloat16)
            return carry

        def near_part(part, carry, step=step):
            at = pl.multiple_of(core * half + part * width, 128)
            kept[:, pl.ds(pl.multiple_of(part * width, 128), width)] = product(at)
            return carry

        if step >= 2:
            collect.swap(step - 2).wait_send()
        lax.fori_loop(0, half // width, far_part, 0)
        collect.swap(step).start()
        lax.fori_loop(0, half // width, near_part, 0)
    collect.settle(3)
    for copy in pair_copies(collect.block(3)):
        copy.wait()
    collect.finish()


def ffn_backward(grad_rows, gate_pre, up_pre, gate_weight, up_weight, down_weight, capacity):
    rows, depth = grad_rows.shape
    hidden_units = gate_weight.shape[1]
    block = 2 * capacity
    chips = rows // block
    chunk = hidden_units // 2 if hidden_units % 256 == 0 else 128
    half = depth // 2
    any_space = pl.BlockSpec(memory_space=pl.ANY)
    bf = jnp.bfloat16
    dma = pltpu.SemaphoreType.DMA
    return pl.pallas_call(
        functools.partial(ffn_backward_body, chunk),
        in_specs=[any_space] * 6,
        out_specs=[any_space] * 3,
        out_shape=[
            jax.ShapeDtypeStruct((rows, hidden_units), bf),
            jax.ShapeDtypeStruct((rows, hidden_units), bf),
            jax.ShapeDtypeStruct((chips, capacity, depth), bf),
        ],
        scratch_shapes=[
            pltpu.VMEM((depth, hidden_units), bf),
            pltpu.VMEM((depth, hidden_units), bf),
            pltpu.VMEM((depth, hidden_units), bf),
            pltpu.VMEM((2, block, depth), bf),
            pltpu.VMEM((2, 2, block, chunk), bf),
            pltpu.VMEM((2, block, hidden_units), bf),
            pltpu.VMEM((block, half), jnp.float32),
            pltpu.VMEM((2, block, half), bf),
            pltpu.VMEM((chips, block, half), bf),
            pltpu.VMEM((chips, block, half), bf),
            dma((3,)),
            dma((2,)),
            dma((2, 2)),
            dma((2,)),
            dma((1,)),
            dma((4,)),
            dma((4,)),
            dma((8,)),
            dma((8,)),
        ],
        compiler_params=pltpu.CompilerParams(
            collective_id=3, has_side_effects=True, vmem_limit_bytes=VMEM_BYTES
        ),
        name="ffn_backward",
    )(grad_rows, gate_pre, up_pre, gate_weight, up_weight, down_weight)


def send_slots_body(
    slots, rows_hbm, grads_hbm, landing, grad_out, rows_v, grads_v, stage, load_sem, stage_sem, local_sem, send, recv
):
    me = lax.axis_index("expert")
    enter(8, me)

    def outgoing(offset):
        target = lax.rem(me + offset, 8)
        return remote(slots.at[target], landing.at[me], send.at[offset], recv.at[offset], target)

    local = pltpu.make_async_copy(slots.at[me], landing.at[me], local_sem)
    for offset in range(1, 8):
        outgoing(offset).start()
    local.start()
    loads = [
        pltpu.make_async_copy(source, target, load_sem.at[n])
        for n, (source, target) in enumerate(((rows_hbm, rows_v), (grads_hbm, grads_v)))
    ]
    for load in loads:
        load.start()
    for load in loads:
        load.wait()
    width = stage.shape[1]
    blocks = rows_v.shape[1] // width

    def stage_copy(block):
        slot = lax.rem(block, 2)
        span = pl.ds(pl.multiple_of(block * width, 16), width)
        return pltpu.make_async_copy(stage.at[slot], grad_out.at[span, :], stage_sem.at[slot])

    def one(block, carry):
        @pl.when(block >= 2)
        def _():
            stage_copy(block - 2).wait()

        columns = pl.ds(pl.multiple_of(block * width, 128), width)
        turned = rows_v[:, columns].astype(jnp.float32).T.astype(jnp.bfloat16)
        stage[lax.rem(block, 2)] = dot_nn(turned, grads_v[...]).astype(jnp.bfloat16)
        stage_copy(block).start()
        return carry

    lax.fori_loop(0, blocks, one, 0)
    for block in (blocks - 2, blocks - 1):
        stage_copy(block).wait()
    local.wait()
    for offset in range(1, 8):
        outgoing(offset).wait_send()
        place = landing.at[lax.rem(me + 8 - offset, 8)]
        remote(place, place, send.at[offset], recv.at[offset], me).wait_recv()


def send_slots(slots, rows, grads):
    total, depth = rows.shape
    hidden_units = grads.shape[1]
    width = min(256, depth // 2)
    any_space = pl.BlockSpec(memory_space=pl.ANY)
    bf = jnp.bfloat16
    dma = pltpu.SemaphoreType.DMA
    return pl.pallas_call(
        send_slots_body,
        in_specs=[any_space] * 3,
        out_specs=[any_space] * 2,
        out_shape=[
            jax.ShapeDtypeStruct(slots.shape, bf),
            jax.ShapeDtypeStruct((depth, hidden_units), bf),
        ],
        scratch_shapes=[
            pltpu.VMEM((total, depth), bf),
            pltpu.VMEM((total, hidden_units), bf),
            pltpu.VMEM((2, width, hidden_units), bf),
            dma((2,)),
            dma((2,)),
            dma,
            dma((8,)),
            dma((8,)),
        ],
        compiler_params=pltpu.CompilerParams(
            collective_id=5, has_side_effects=True, vmem_limit_bytes=VMEM_BYTES
        ),
        name="send_slots",
    )(slots, rows, grads)


def merge_return_body(
    dp_axis,
    plan_hbm,
    slots_hbm,
    grads_hbm,
    weight_hbm,
    back,
    plan,
    slots,
    grads,
    weight,
    kept,
    passing,
    passed,
    total,
    load_sem,
    local_sem,
    swap_send,
    swap_recv,
    out_send,
    out_recv,
):
    me = lax.axis_index("expert")
    replica = lax.axis_index(dp_axis)
    enter(8, me)
    loads = [
        pltpu.make_async_copy(source, target, load_sem.at[n])
        for n, (source, target) in enumerate(
            ((plan_hbm, plan), (slots_hbm, slots), (grads_hbm, grads), (weight_hbm, weight))
        )
    ]
    for load in loads:
        load.start()
    collect = Collect(
        me, far_order, (3,), kept, passing, passed, total, back, local_sem.at[0], swap_send, swap_recv, out_send, out_recv
    )
    rows, half = collect.rows, collect.half
    parts, ck = weight.shape[0], weight.shape[2] // 2
    values_at = grads.shape[1] // 2
    width = min(512, half)
    for load in loads:
        load.wait()
    for step in range(4):
        chip = collect.block(step)
        span = pl.ds(pl.multiple_of(chip * 2 * rows, 16), 2 * rows)

        def product(at, chip=chip, span=span):
            columns = pl.ds(at, width)
            result = jnp.concatenate(
                [dot_nn(plan[2 * chip + n], slots[2 * chip + n, :, columns]) for n in range(2)], axis=0
            )
            for part in range(parts):
                low = lax.rem(replica, 2) + (part % 2) * (1 - 2 * lax.rem(replica, 2))
                high = replica // 2 + (part // 2) * (1 - 2 * (replica // 2))
                at_keys = pl.multiple_of((2 * high + low) * ck, 128)
                result += dot_nt(grads[span, pl.ds(at_keys, ck)], weight[part, columns, :ck])
                result += dot_nt(grads[span, pl.ds(values_at + at_keys, ck)], weight[part, columns, ck:])
            return result

        def far_part(part, carry, step=step, product=product):
            at = pl.multiple_of((1 - collect.core) * half + part * width, 128)
            columns = pl.ds(pl.multiple_of(part * width, 128), width)
            passing[step % 2, :, columns] = product(at).astype(jnp.bfloat16)
            return carry

        def near_part(part, carry, product=product):
            at = pl.multiple_of(collect.core * half + part * width, 128)
            kept[:, pl.ds(pl.multiple_of(part * width, 128), width)] = product(at)
            return carry

        if step >= 2:
            collect.swap(step - 2).wait_send()
        lax.fori_loop(0, half // width, far_part, 0)
        collect.swap(step).start()
        if step > 0:
            collect.settle(step - 1)
        lax.fori_loop(0, half // width, near_part, 0)
    collect.settle(3)
    collect.finish()


def merge_return(plan, slots, grads, weights):
    sources, rows, capacity = plan.shape
    parts, depth, columns = weights.shape
    tokens = sources * rows
    half = depth // 2
    any_space = pl.BlockSpec(memory_space=pl.ANY)
    bf = jnp.bfloat16
    dma = pltpu.SemaphoreType.DMA
    return pl.pallas_call(
        functools.partial(merge_return_body, "dp"),
        in_specs=[any_space] * 4,
        out_specs=any_space,
        out_shape=jax.ShapeDtypeStruct((sources // 2, rows, depth), bf),
        scratch_shapes=[
            pltpu.VMEM(plan.shape, bf),
            pltpu.VMEM(slots.shape, bf),
            pltpu.VMEM(grads.shape, bf),
            pltpu.VMEM(weights.shape, bf),
            pltpu.VMEM((2 * rows, half), jnp.float32),
            pltpu.VMEM((2, 2 * rows, half), bf),
            pltpu.VMEM((sources // 2, 2 * rows, half), bf),
            pltpu.VMEM((sources // 2, 2 * rows, half), bf),
            dma((4,)),
            dma((1,)),
            dma((4,)),
            dma((4,)),
            dma((8,)),
            dma((8,)),
        ],
        compiler_params=pltpu.CompilerParams(
            collective_id=6, has_side_effects=True, vmem_limit_bytes=VMEM_BYTES
        ),
        name="merge_return",
    )(plan, slots, grads, weights)


def return_order(chip, step):
    lower, upper = chip_order(chip, (2, 3, 1, 0)[step]), chip_order(chip, 3 - step)
    return lower + chip // 2 * (upper - lower)


def attention_send_body(
    query_hbm,
    sibling_hbm,
    key_hbm,
    value_hbm,
    out_weight_hbm,
    key_info,
    query_info,
    own_out,
    sibling_out,
    rows_out,
    back,
    lse_ref,
    queries,
    siblings,
    keys_v,
    values_v,
    out_weight,
    bias_ref,
    flipped,
    own_stage,
    sibling_stage,
    arrived,
    rows_stage,
    sending,
    load_sem,
    own_sem,
    sibling_sem,
    rows_sem,
    local_sem,
    swap_send,
    swap_recv,
    out_send,
    out_recv,
):
    me = lax.axis_index("expert")
    chip, core = me // 2, lax.rem(me, 2)
    enter(8, me)
    half = keys_v.shape[1]
    rows = own_stage.shape[1]
    keys = keys_v.shape[0] // GROUPS
    heads = half // HEAD
    capacity = back.shape[1]
    own_columns = pl.ds(pl.multiple_of(core * half, 128), half)
    far_columns = pl.ds(pl.multiple_of((1 - core) * half, 128), half)
    loads = [
        pltpu.make_async_copy(source, target, load_sem.at[n])
        for n, (source, target) in enumerate(
            (
                (value_hbm, values_v),
                (key_hbm, keys_v),
                (query_hbm.at[:, own_columns], queries),
                (sibling_hbm, siblings),
                (out_weight_hbm, out_weight),
            )
        )
    ]
    for load in loads:
        load.start()
    loads[0].wait()

    def flip(head, carry):
        lanes = pl.ds(pl.multiple_of(head * HEAD, HEAD), HEAD)
        for block in range(GROUPS):
            values = values_v[pl.ds(block * keys, keys), lanes].astype(jnp.float32)
            flipped[head, block] = values.T.astype(jnp.bfloat16)
        return carry

    lax.fori_loop(0, heads, flip, 0)
    for load in loads[1:4]:
        load.wait()

    def group_of(step):
        return return_order(chip, step)

    def span_of(step):
        return pl.ds(pl.multiple_of(group_of(step) * rows, 16), rows)

    def own_copy(step):
        return pltpu.make_async_copy(own_stage.at[step], own_out.at[span_of(step), :], own_sem.at[step])

    def sibling_copy(step):
        return pltpu.make_async_copy(
            sibling_stage.at[step], sibling_out.at[span_of(step), :], sibling_sem.at[step]
        )

    def rows_copy(step):
        return pltpu.make_async_copy(
            rows_stage.at[step], rows_out.at[span_of(step), :], rows_sem.at[step]
        )

    def swap(step):
        return remote(
            sibling_stage.at[step], arrived.at[step], swap_send.at[step], swap_recv.at[step], me + 1 - 2 * core
        )

    def outgoing(step, n):
        source = 2 * group_of(step) + n
        offset = lax.rem(source - me + 8, 8)
        return remote(sending.at[step, n], back.at[me], out_send.at[offset], out_recv.at[offset], source)

    def local(step, n):
        return pltpu.make_async_copy(sending.at[step, n], back.at[me], local_sem)

    def each(step, own, other):
        for n in range(2):
            if step < 3:
                other(n)
                continue

            @pl.when(core == n)
            def _(n=n):
                own(n)

            @pl.when(core != n)
            def _(n=n):
                other(n)

    def attend(step):
        group = group_of(step)
        span = span_of(step)
        fill_group_bias(bias_ref, key_info, query_info, keys, group)

        def head_pair(pair, carry):
            lanes = [pl.ds(pl.multiple_of((2 * pair + n) * HEAD, HEAD), HEAD) for n in range(2)]
            parts = [jnp.concatenate([queries[span, lane], siblings[span, lane]], axis=0) for lane in lanes]

            def one(block, state):
                at = pl.multiple_of(block * keys, 16)
                bias = bias_ref[block]
                result = []
                for n in range(2):
                    top, total, mixed = state[3 * n : 3 * n + 3]
                    scores = dot_nt(keys_v[pl.ds(at, keys), lanes[n]], parts[n]) + bias
                    new_top = jnp.maximum(top, jnp.max(scores, axis=0, keepdims=True))
                    fade = jnp.exp2(top - new_top)
                    probs = jnp.exp2(scores - new_top)
                    total = total * fade + jnp.sum(probs, axis=0, keepdims=True)
                    mixed = mixed * fade + dot_nn(flipped[2 * pair + n, block], probs.astype(jnp.bfloat16))
                    result += [new_top, total, mixed]
                return tuple(result)

            start = (
                jnp.full((1, 2 * rows), -1e30, jnp.float32),
                jnp.zeros((1, 2 * rows), jnp.float32),
                jnp.zeros((HEAD, 2 * rows), jnp.float32),
            ) * 2
            final = lax.fori_loop(0, group + 1, one, start)
            for n in range(2):
                top, total, mixed = final[3 * n : 3 * n + 3]
                lse_ref[2 * pair + n, group] = top + jnp.log2(total)
                result = (mixed / total).T.astype(jnp.bfloat16)
                own_stage[step, :, lanes[n]] = result[:rows]
                sibling_stage[step, :, lanes[n]] = result[rows:]
            return carry

        lax.fori_loop(0, heads // 2, head_pair, 0)
        swap(step).start()
        own_copy(step).start()
        sibling_copy(step).start()

    def settle(step):
        swap(step).wait_recv()
        rows_stage[step, :, own_columns] = own_stage[step]
        rows_stage[step, :, far_columns] = arrived[step]
        rows_copy(step).start()
        width = 512
        for at in range(0, back.shape[2], min(width, back.shape[2])):
            columns = pl.ds(at, min(width, back.shape[2]))
            product = dot_nt(rows_stage[step], out_weight[columns, :])
            for n in range(2):
                part = product[n * capacity : (n + 1) * capacity]
                sending[step, n, :, columns] = part.astype(jnp.bfloat16)
        each(step, lambda n: local(step, n).start(), lambda n: outgoing(step, n).start())

    for step in range(4):
        attend(step)
        if step == 0:
            loads[4].wait()
        if step < 2:
            settle(step)
        elif step == 3:
            settle(2)
            settle(3)
    for step in range(4):
        swap(step).wait_send()
        own_copy(step).wait()
        sibling_copy(step).wait()
        rows_copy(step).wait()
        each(step, lambda n, step=step: local(step, n).wait(), lambda n, step=step: outgoing(step, n).wait_send())
    for offset in range(1, 8):
        place = back.at[lax.rem(me + 8 - offset, 8)]
        remote(place, place, out_send.at[offset], out_recv.at[offset], me).wait_recv()


def attention_send(queries, siblings, keys_all, values_all, out_weight, key_info, query_info, capacity):
    total_rows, width = queries.shape
    tokens, half = keys_all.shape
    depth = out_weight.shape[0]
    rows, keys, heads = total_rows // GROUPS, tokens // GROUPS, half // HEAD
    any_space = pl.BlockSpec(memory_space=pl.ANY)
    here = pl.BlockSpec(memory_space=pltpu.VMEM)
    bf = jnp.bfloat16
    dma = pltpu.SemaphoreType.DMA
    return pl.pallas_call(
        attention_send_body,
        in_specs=[any_space] * 5 + [here] * 2,
        out_specs=[any_space] * 4 + [here],
        out_shape=[
            jax.ShapeDtypeStruct((total_rows, half), bf),
            jax.ShapeDtypeStruct((total_rows, half), bf),
            jax.ShapeDtypeStruct((total_rows, width), bf),
            jax.ShapeDtypeStruct((8, capacity, depth), bf),
            jax.ShapeDtypeStruct((heads, GROUPS, 1, 2 * rows), jnp.float32),
        ],
        scratch_shapes=[
            pltpu.VMEM((total_rows, half), bf),
            pltpu.VMEM((total_rows, half), bf),
            pltpu.VMEM((tokens, half), bf),
            pltpu.VMEM((tokens, half), bf),
            pltpu.VMEM(out_weight.shape, bf),
            pltpu.VMEM((GROUPS, keys, 2 * rows), jnp.float32),
            pltpu.VMEM((heads, GROUPS, HEAD, keys), bf),
            pltpu.VMEM((GROUPS, rows, half), bf),
            pltpu.VMEM((GROUPS, rows, half), bf),
            pltpu.VMEM((GROUPS, rows, half), bf),
            pltpu.VMEM((GROUPS, rows, width), bf),
            pltpu.VMEM((GROUPS, 2, capacity, depth), bf),
            dma((5,)),
            dma((GROUPS,)),
            dma((GROUPS,)),
            dma((GROUPS,)),
            dma,
            dma((GROUPS,)),
            dma((GROUPS,)),
            dma((8,)),
            dma((8,)),
        ],
        compiler_params=pltpu.CompilerParams(
            collective_id=4, has_side_effects=True, vmem_limit_bytes=VMEM_BYTES
        ),
        name="attention_send",
    )(queries, siblings, keys_all, values_all, out_weight, key_info, query_info)


def swap_blocks_body(blocks, landing, local_sem, send, recv):
    me = lax.axis_index("expert")
    enter(8, me)

    def outgoing(offset):
        target = lax.rem(me + offset, 8)
        return remote(blocks.at[target], landing.at[me], send.at[offset], recv.at[offset], target)

    local = pltpu.make_async_copy(blocks.at[me], landing.at[me], local_sem)
    for offset in range(1, 8):
        outgoing(offset).start()
    local.start()
    local.wait()
    for offset in range(1, 8):
        outgoing(offset).wait_send()
        place = landing.at[lax.rem(me + 8 - offset, 8)]
        remote(place, place, send.at[offset], recv.at[offset], me).wait_recv()


def swap_blocks(blocks):
    any_space = pl.BlockSpec(memory_space=pl.ANY)
    dma = pltpu.SemaphoreType.DMA
    return pl.pallas_call(
        swap_blocks_body,
        in_specs=[any_space],
        out_specs=any_space,
        out_shape=jax.ShapeDtypeStruct(blocks.shape, blocks.dtype),
        scratch_shapes=[dma, dma((8,)), dma((8,))],
        compiler_params=pltpu.CompilerParams(collective_id=7, has_side_effects=True),
        name="swap_blocks",
    )(blocks)


D = 2048
HEADS = 16
ATT_EXPERTS = 8
FFN_EXPERTS = 4
TRUNK = 1024
SEG = 96
TREE_LEN = 2176
NODES = 13

epsilon = 1e-06
highest = lax.Precision.HIGHEST
bf16 = jnp.bfloat16
f32 = jnp.float32


def tree_layout(places):
    after_trunk = places - TRUNK
    after_branch = after_trunk - 4 * SEG
    segments = jnp.where(
        places < TRUNK,
        0,
        jnp.where(after_branch < 0, 1 + after_trunk // SEG, 5 + after_branch // SEG),
    )
    depths = jnp.where(
        places < TRUNK,
        places,
        jnp.where(after_branch < 0, TRUNK + after_trunk % SEG, TRUNK + SEG + after_branch % SEG),
    )
    return (segments.astype(jnp.int32), depths.astype(jnp.int32))


def rotation_tables(depths):
    half_size = HEAD // 2
    frequency = 10000.0 ** (-jnp.arange(half_size, dtype=f32) * 2.0 / HEAD)
    angles = depths.astype(f32)[:, None] * frequency[None, :]
    cosine, sine = jnp.cos(angles), jnp.sin(angles)
    cosines = jnp.concatenate([cosine, cosine], axis=1)
    forward = jnp.concatenate([-sine, sine], axis=1)
    return (cosines, forward), (cosines, -forward)


def lookup(table, indices):
    nodes = jnp.arange(NODES, dtype=jnp.int32)
    return jnp.sum(jnp.where(indices[:, None] == nodes[None, :], table[None, :], 0), axis=1)


def running_count(chosen):
    rows = chosen.shape[-1]
    index = jnp.arange(rows, dtype=jnp.int32)
    upto = (index[:, None] <= index[None, :]).astype(bf16)
    return jnp.dot(chosen.astype(bf16), upto, preferred_element_type=f32).astype(jnp.int32) - 1


def source_plan(routes, expert, capacity):
    chosen = jnp.any(routes == expert, axis=2)
    ranking = running_count(chosen)
    slots = jnp.arange(capacity, dtype=jnp.int32)
    return chosen[:, None, :] & (ranking[:, None, :] == slots[None, :, None])


def token_picks(routes, experts, capacity):
    labels = jnp.arange(experts, dtype=jnp.int32)
    hits = routes.T[:, None, :] == labels[None, :, None]
    ranking = running_count(hits[0] | hits[1])
    slots = jnp.arange(capacity, dtype=jnp.int32)
    picks = hits[:, :, None, :] & (ranking[None, :, None, :] == slots[None, None, :, None])
    return picks.astype(bf16), hits[0].T.astype(f32), hits[1].T.astype(f32)


def fill_slots(picks, pair):
    return jnp.einsum("kecr,krd->ecd", picks, pair, preferred_element_type=f32).astype(bf16)


def read_slots(picks, slots):
    return jnp.einsum("kecr,ecd->krd", picks, slots, preferred_element_type=f32)


def gate_values(hidden, router, first, second):
    logits = jnp.dot(hidden.astype(f32), router, precision=highest)
    picked = jnp.stack([jnp.sum(logits * first, axis=1), jnp.sum(logits * second, axis=1)], axis=1)
    return jax.nn.softmax(picked, axis=1)


def router_grads(hidden, router, gates, first, second, picked_grad):
    logit_pick = gates * (picked_grad - jnp.sum(gates * picked_grad, axis=1, keepdims=True))
    logit_grad = logit_pick[:, 0:1] * first + logit_pick[:, 1:2] * second
    router_grad = jnp.dot(hidden.astype(f32).T, logit_grad, precision=highest)
    hidden_grad = jnp.dot(logit_grad, router.T, precision=highest)
    return (router_grad, hidden_grad)


def rms_parts(values):
    inverse = lax.rsqrt(jnp.mean(values * values, axis=-1, keepdims=True) + epsilon)
    return (values * inverse, inverse)


def norm_back(grad_normed, normed, inverse):
    return inverse * (grad_normed - normed * jnp.mean(grad_normed * normed, axis=-1, keepdims=True))


def pair_grads(gates, branches, upstream):
    gate_grad = jnp.stack([jnp.sum(upstream * branches[k], axis=1) for k in range(2)], axis=1)
    scaled = jnp.stack([gates[:, k : k + 1] * upstream for k in range(2)]).astype(bf16)
    return gate_grad, scaled


def exchange(slots):
    return lax.all_to_all(slots, "expert", split_axis=0, concat_axis=0, tiled=True)


def shift(values, step, size, devices):
    moves = [(i, i // size * size + (i % size + step) % size) for i in range(devices)]
    return lax.ppermute(values, "expert", moves)


def group_gather(rows, size, devices):
    return jnp.concatenate([rows] + [shift(rows, step, size, devices) for step in range(1, size)])


def group_reduce(partial, size, devices):
    parts = partial.reshape(size, -1, partial.shape[1])
    total = parts[0].astype(f32)
    for step in range(1, size):
        total = total + shift(parts[step], -step, size, devices).astype(f32)
    return total.astype(bf16)


def spread_over_replicas(block, my_replica, replicas):
    if replicas != 4:
        return lax.all_gather(block, "dp", axis=0), jnp.arange(replicas, dtype=jnp.int32)
    across, along = ([(i, i ^ n) for i in range(4)] for n in (1, 2))
    first, second = lax.ppermute(block, "dp", across), lax.ppermute(block, "dp", along)
    cut = block.shape[0] // 2
    upper, lower = lax.ppermute(second[:cut], "dp", across), lax.ppermute(first[cut:], "dp", along)
    blocks = jnp.stack([block, first, second, jnp.concatenate([upper, lower])])
    return blocks, my_replica ^ jnp.arange(4, dtype=jnp.int32)


def dot_tn(left, right):
    return lax.dot_general(left, right, (((0,), (0,)), ((), ())), preferred_element_type=f32)


def body(
    tokens,
    teacher,
    att_routes,
    ffn_routes,
    parent,
    valid,
    gain_one,
    kv_weight,
    att_router,
    q_weight,
    o_weight,
    gain_two,
    ffn_router,
    gate_weight,
    up_weight,
    down_weight,
):
    row_count = tokens.shape[0]
    devices, replicas = lax.axis_size("expert"), lax.axis_size("dp")
    my_index, my_replica = lax.axis_index("expert"), lax.axis_index("dp")
    core = my_index % 2
    att_copies, ffn_copies = devices // ATT_EXPERTS, devices // FFN_EXPERTS
    att_capacity, ffn_capacity = row_count * 13 // 40, row_count * 13 // 20
    token_count = row_count * devices
    half = HEADS * HEAD // 2
    assert token_count == TREE_LEN * parent.shape[0] and parent.shape[0] == 1
    pair = [(i, i ^ 1) for i in range(devices)]
    own_places = my_index * row_count + jnp.arange(row_count, dtype=jnp.int32)

    x_in = tokens.astype(f32)
    normed_one, inverse_one = rms_parts(x_in)
    hidden = (normed_one * gain_one).astype(bf16)
    weight_rows = kv_weight.shape[0]
    piece = half // replicas
    kv_share = lax.dynamic_slice_in_dim(
        kv_weight.reshape(weight_rows, 4, replicas, piece), my_replica, 1, 2
    )
    kv_share = (
        kv_share.reshape(weight_rows, 2, 2, piece).transpose(0, 2, 1, 3).reshape(weight_rows, 4 * piece)
    )
    kv_gathered = lax.all_gather(kv_share, "expert", axis=0)
    hidden_all = lax.all_gather(hidden, "expert", axis=0)
    all_routes = lax.all_gather(att_routes, "expert", axis=0)

    tree_places = jnp.arange(token_count, dtype=jnp.int32)
    tree_segments, tree_depths = tree_layout(tree_places)
    key_forward, key_backward = rotation_tables(tree_depths)
    key_info = jnp.pad(jnp.stack([tree_places, tree_segments], axis=1), ((0, 0), (0, 6)))
    experts_here = [my_index // att_copies]
    if att_copies == 1:
        experts_here.append(my_index ^ 1)
    plans = [source_plan(all_routes, expert, att_capacity) for expert in experts_here]
    slot_tables, query_parts = [], []
    for plan in plans:
        places = jnp.sum(
            jnp.where(plan, tree_places.reshape(devices, 1, row_count), 0), axis=2
        ).reshape(-1)
        segments, depths = tree_layout(places)
        parents = lookup(parent[0], segments)
        grands = lookup(parent[0], parents)
        query_parts.append(jnp.stack([places, segments, parents, grands]).reshape(4, GROUPS, -1))
        slot_tables.append(rotation_tables(depths))
    query_info = jnp.concatenate(query_parts, axis=2).transpose(1, 0, 2)
    own_plan = plans[0].astype(bf16)
    att_picks, att_first, att_second = token_picks(att_routes, ATT_EXPERTS, att_capacity)
    att_gates = gate_values(hidden, att_router, att_first, att_second)
    ffn_picks, ffn_first, ffn_second = token_picks(ffn_routes, FFN_EXPERTS, ffn_capacity)
    ffn_any = ffn_picks[0] + ffn_picks[1]
    prepared = (key_forward, key_backward, key_info, slot_tables, query_info, own_plan, att_picks, att_gates, ffn_picks, ffn_any)
    kv_gathered, prepared = lax.optimization_barrier((kv_gathered, prepared))
    kv_half = lax.dynamic_slice_in_dim(kv_gathered, core * 2 * piece, 2 * piece, 2).reshape(D, 2 * piece)
    kv_blocks, block_order = spread_over_replicas(kv_half, my_replica, replicas)
    hidden_all, kv_blocks = lax.optimization_barrier((hidden_all, kv_blocks))
    key_forward, key_backward, key_info, slot_tables, query_info, own_plan, att_picks, att_gates, ffn_picks, ffn_any = prepared

    queries, query_inputs = project_queries(own_plan, hidden_all, q_weight, slot_tables[0][0])
    keys_all, values_all = project_keys_values(hidden_all, kv_blocks, key_forward, block_order)

    def far_half(values):
        return lax.ppermute(
            lax.dynamic_slice_in_dim(values, (1 - core) * half, half, 1), "expert", pair
        )

    def join_halves(mine, sibling):
        other = lax.ppermute(sibling, "expert", pair)
        return jnp.where(
            core == 0,
            jnp.concatenate([mine, other], axis=1),
            jnp.concatenate([other, mine], axis=1),
        )

    heads = half // HEAD
    query_sets = [queries]
    starts = jnp.zeros((2,), jnp.int32)
    if att_copies == 1:
        query_sets.append(far_half(queries))
        starts = jnp.stack([core * heads, 0]).astype(jnp.int32)
    fused = devices == 8 and replicas == 4 and att_copies == 1 and ffn_copies == 2 and ffn_capacity % 16 == 0
    if fused:
        *att_outs, att_rows, att_back, lse = attention_send(
            *query_sets, keys_all, values_all, o_weight, key_info, query_info, att_capacity
        )
        att_everywhere = lax.all_gather(att_rows, "dp", axis=0, tiled=True)
    else:
        *att_outs, lse = attention_forward(
            query_sets, starts // 2, keys_all, values_all, key_info, query_info, heads
        )
        att_rows = join_halves(*att_outs) if att_copies == 1 else att_outs[0]
        att_partial = lax.dot_general(
            att_rows, o_weight, (((1,), (1,)), ((), ())), preferred_element_type=f32
        ).astype(bf16)
        att_back = exchange(att_partial.reshape(devices, att_capacity, D))
    if att_copies > 1:
        att_back = (
            att_back.astype(f32).reshape(ATT_EXPERTS, att_copies, att_capacity, D).sum(axis=1).astype(bf16)
        )
    att_branches = read_slots(att_picks, att_back)
    x_mid = x_in + att_gates[:, 0:1] * att_branches[0] + att_gates[:, 1:2] * att_branches[1]

    normed_two, inverse_two = rms_parts(x_mid)
    hidden_two = (normed_two * gain_two).astype(bf16)
    ffn_gates = gate_values(hidden_two, ffn_router, ffn_first, ffn_second)

    def to_experts(slots):
        rows = exchange(slots.reshape(devices, ffn_capacity // ffn_copies, D))
        return group_gather(rows.reshape(-1, D), ffn_copies, devices)

    def to_tokens(partial):
        rows = group_reduce(partial.astype(bf16), ffn_copies, devices)
        back = exchange(rows.reshape(devices, ffn_capacity // ffn_copies, D))
        return read_slots(ffn_picks, back.reshape(FFN_EXPERTS, ffn_capacity, D))

    if fused:
        ffn_inputs, gate_pre, up_pre, activated, ffn_back = ffn_forward(
            ffn_any, hidden_two, gate_weight, up_weight, down_weight
        )
        ffn_branches = read_slots(ffn_picks, ffn_back)
    else:
        ffn_inputs = to_experts(
            jnp.einsum(
                "ecr,rd->ecd", ffn_picks[0] + ffn_picks[1], hidden_two, preferred_element_type=f32
            ).astype(bf16)
        )
        gate_pre = jnp.dot(ffn_inputs, gate_weight, preferred_element_type=f32)
        up_pre = jnp.dot(ffn_inputs, up_weight, preferred_element_type=f32)
        sigmoid_gate = jax.nn.sigmoid(gate_pre)
        silu_gate = gate_pre * sigmoid_gate
        activated = (silu_gate * up_pre).astype(bf16)
        ffn_branches = to_tokens(
            lax.dot_general(
                activated, down_weight, (((1,), (1,)), ((), ())), preferred_element_type=f32
            )
        )
    result = x_mid + ffn_gates[:, 0:1] * ffn_branches[0] + ffn_gates[:, 1:2] * ffn_branches[1]

    tree_global = my_replica * parent.shape[0] + own_places // TREE_LEN
    tree_labels = jnp.arange(valid.shape[0], dtype=jnp.int32)
    limits = jnp.sum(
        jnp.where(tree_global[:, None] == tree_labels[None, :], valid[None, :], 0), axis=1
    )
    counted = own_places % TREE_LEN < limits
    loss_factor = valid.shape[0] * TREE_LEN / jnp.sum(valid).astype(f32)
    grad_result = jnp.where(counted[:, None], (result - teacher.astype(f32)) * loss_factor, 0.0)

    ffn_gate_grad, ffn_scaled = pair_grads(ffn_gates, ffn_branches, grad_result)
    if fused:
        ffn_scaled, att_everywhere = lax.optimization_barrier((ffn_scaled, att_everywhere))
        grad_ffn_out, grad_down = send_rows(ffn_picks, ffn_scaled, activated)
        grad_ffn_out = grad_ffn_out.reshape(-1, D)
    else:
        grad_ffn_out = to_experts(fill_slots(ffn_picks, ffn_scaled))
        grad_down = dot_tn(grad_ffn_out, activated).astype(bf16)
    grad_ffn_out, grad_down = lax.optimization_barrier((grad_ffn_out, grad_down))
    summed_down = lax.psum_scatter(grad_down, "dp", scatter_dimension=0, tiled=True)
    if fused:
        grad_gate_pre, grad_up_pre, ffn_grad_back = ffn_backward(
            grad_ffn_out, gate_pre, up_pre, gate_weight, up_weight, down_weight, ffn_capacity
        )
        grad_gate = dot_tn(ffn_inputs, grad_gate_pre).astype(bf16)
        ffn_grad_back, grad_gate = lax.optimization_barrier((ffn_grad_back, grad_gate))
        ffn_grad_pair = read_slots(ffn_picks, ffn_grad_back)
    else:
        grad_activated = jnp.dot(grad_ffn_out, down_weight, preferred_element_type=f32)
        grad_gate_pre = (
            grad_activated * up_pre * sigmoid_gate * (1.0 + gate_pre * (1.0 - sigmoid_gate))
        ).astype(bf16)
        grad_up_pre = (grad_activated * silu_gate).astype(bf16)
        grad_ffn_in = lax.dot_general(
            grad_gate_pre, gate_weight, (((1,), (1,)), ((), ())), preferred_element_type=f32
        ) + lax.dot_general(
            grad_up_pre, up_weight, (((1,), (1,)), ((), ())), preferred_element_type=f32
        )
        grad_gate = dot_tn(ffn_inputs, grad_gate_pre).astype(bf16)
        ffn_grad_pair = to_tokens(grad_ffn_in)
    summed_gate = lax.psum_scatter(grad_gate, "dp", scatter_dimension=0, tiled=True)
    grad_ffn_router, hidden_two_extra = router_grads(
        hidden_two, ffn_router, ffn_gates, ffn_first, ffn_second, ffn_gate_grad
    )
    grad_hidden_two = ffn_grad_pair[0] + ffn_grad_pair[1] + hidden_two_extra
    grad_gain_two = jnp.sum(grad_hidden_two * normed_two, axis=0)
    grad_mid = grad_result + norm_back(grad_hidden_two * gain_two, normed_two, inverse_two)

    att_gate_grad, att_scaled = pair_grads(att_gates, att_branches, grad_mid)
    att_slots = fill_slots(att_picks, att_scaled)
    if att_copies > 1:
        att_slots = jnp.repeat(att_slots, att_copies, axis=0)
    att_slots, summed_down = lax.optimization_barrier((att_slots, summed_down))
    if fused:
        grad_att_out, grad_up = send_slots(att_slots, ffn_inputs, grad_up_pre)
        grad_att_out = grad_att_out.reshape(-1, D)
    else:
        grad_att_out = exchange(att_slots).reshape(-1, D)
        grad_up = dot_tn(ffn_inputs, grad_up_pre).astype(bf16)
        grad_att_out, grad_up = lax.optimization_barrier((grad_att_out, grad_up))
    summed_up = lax.psum_scatter(grad_up, "dp", scatter_dimension=0, tiled=True)
    grad_heads = jnp.dot(grad_att_out, o_weight, preferred_element_type=f32).astype(bf16)
    grad_heads, grad_att_out = lax.optimization_barrier((grad_heads, grad_att_out))
    grad_sets = [grad_heads]
    if att_copies == 1:
        grad_sets.append(far_half(grad_heads))
    if fused:
        share = D // replicas

        def columns_of(replica):
            return lax.dynamic_slice_in_dim(grad_att_out, replica * share, share, 1)

        grad_columns = [columns_of(my_replica)] + [
            lax.ppermute(columns_of(my_replica ^ n), "dp", [(i, i ^ n) for i in range(replicas)])
            for n in range(1, replicas)
        ]
    else:
        grad_o = dot_tn(grad_att_out, att_rows).astype(bf16)
        summed_o = lax.psum_scatter(grad_o, "dp", scatter_dimension=0, tiled=True).astype(f32)
    *grad_queries, grad_keys_values = attention_backward(
        query_sets,
        starts,
        grad_sets,
        att_outs,
        keys_all,
        values_all,
        lse,
        key_info,
        query_info,
        key_backward,
        [tables[1] for tables in slot_tables],
        heads,
    )
    grad_keys_values, summed_gate = lax.optimization_barrier((grad_keys_values, summed_gate))
    grad_query_pre = join_halves(*grad_queries) if att_copies == 1 else grad_queries[0]
    grad_kv = dot_tn(hidden_all.reshape(token_count, D), grad_keys_values).astype(bf16)
    grad_q = dot_tn(query_inputs, grad_query_pre).astype(bf16)
    summed_kv = lax.psum_scatter(grad_kv, "dp", scatter_dimension=0, tiled=True)
    summed_q = lax.psum_scatter(grad_q, "dp", scatter_dimension=0, tiled=True)
    grad_query_in = lax.dot_general(
        grad_query_pre, q_weight, (((1,), (1,)), ((), ())), preferred_element_type=f32
    ).astype(bf16)
    grad_query_in, grad_kv, grad_q, summed_up = lax.optimization_barrier(
        (grad_query_in, grad_kv, grad_q, summed_up)
    )

    merge_args = (
        own_plan.transpose(0, 2, 1),
        grad_query_in.reshape(devices, att_capacity, D),
        grad_keys_values,
        kv_blocks,
    )
    if fused:
        arrived = merge_return(*merge_args)
        arrived, grad_columns, summed_kv = lax.optimization_barrier((arrived, grad_columns, summed_kv))
        column_stack = jnp.stack(grad_columns)
        summed_o = dot_tn(
            jnp.concatenate(
                [lax.dynamic_index_in_dim(column_stack, my_replica ^ n, 0, False) for n in range(replicas)]
            ),
            att_everywhere,
        )
    else:
        merged = merge_hidden_grads(*merge_args, block_order).reshape(devices // 2, 2, row_count, D)
        kept = lax.dynamic_index_in_dim(merged, core, 1, keepdims=False)
        passed = lax.ppermute(
            lax.dynamic_index_in_dim(merged, 1 - core, 1, keepdims=False), "expert", pair
        )
        chip_sum = (kept.astype(f32) + passed.astype(f32)).astype(bf16)
        same_core = [[2 * i + c for i in range(devices // 2)] for c in range(2)]
        arrived = lax.all_to_all(
            chip_sum, "expert", split_axis=0, concat_axis=0, axis_index_groups=same_core, tiled=True
        )
    grad_att_router, hidden_one_extra = router_grads(
        hidden, att_router, att_gates, att_first, att_second, att_gate_grad
    )
    grad_hidden_one = jnp.sum(arrived.astype(f32), axis=0) + hidden_one_extra
    grad_gain_one = jnp.sum(grad_hidden_one * normed_one, axis=0)
    grad_input = grad_mid + norm_back(grad_hidden_one * gain_one, normed_one, inverse_one)

    everyone = devices * replicas
    smalls = [grad_gain_one, grad_gain_two, grad_att_router, grad_ffn_router]
    packed = jnp.concatenate([small.reshape(everyone, -1) for small in smalls], axis=1)
    kv_exchange = swap_blocks if fused else exchange
    kv_rows = kv_exchange(summed_kv.reshape(devices, -1, 2 * half))
    packed, summed_o = lax.optimization_barrier((packed, summed_o))
    own_smalls = jnp.sum(
        lax.all_to_all(packed, ("dp", "expert"), split_axis=0, concat_axis=0, tiled=True), axis=0
    )
    own_smalls, kv_rows, summed_q = lax.optimization_barrier((own_smalls, kv_rows, summed_q))
    share = D // everyone
    shared_gain_one = own_smalls[:share]
    shared_gain_two = own_smalls[share : 2 * share]
    shared_att_router = own_smalls[2 * share : (2 + ATT_EXPERTS) * share].reshape(share, ATT_EXPERTS)
    shared_ffn_router = own_smalls[(2 + ATT_EXPERTS) * share :].reshape(share, FFN_EXPERTS)

    kv_sum = jnp.sum(kv_rows.astype(f32).reshape(devices // 2, 2, -1, 2 * half), axis=0)
    shared_kv = jnp.concatenate(
        [kv_sum[n, :, m * half : (m + 1) * half] for m in range(2) for n in range(2)], axis=1
    )

    return (
        result.astype(bf16),
        grad_input.astype(bf16),
        shared_gain_one,
        shared_kv,
        shared_att_router,
        summed_q.astype(f32),
        summed_o,
        shared_gain_two,
        shared_ffn_router,
        summed_gate.astype(f32),
        summed_up.astype(f32),
        summed_down.astype(f32),
    )


def solution(mesh):
    in_specs = (
        P(("dp", "expert"), None),
        P(("dp", "expert"), None),
        P(("dp", "expert"), None),
        P(("dp", "expert"), None),
        P("dp", None),
        P(),
        P(),
        P("expert", None),
        P(),
        P(None, "expert"),
        P(None, "expert"),
        P(),
        P(),
        P(None, "expert"),
        P(None, "expert"),
        P(None, "expert"),
    )
    out_specs = (
        P(("dp", "expert"), None),
        P(("dp", "expert"), None),
        P(("dp", "expert")),
        P(("dp", "expert"), None),
        P(("dp", "expert"), None),
        P("dp", "expert"),
        P("dp", "expert"),
        P(("dp", "expert")),
        P(("dp", "expert"), None),
        P("dp", "expert"),
        P("dp", "expert"),
        P("dp", "expert"),
    )
    return jax.shard_map(body, mesh=mesh, in_specs=in_specs, out_specs=out_specs, check_vma=False)
```

```python
import functools
import jax
import jax.numpy as jnp
from jax import lax
from jax.experimental import pallas as pl
from jax.experimental.pallas import tpu as pltpu
from jax.sharding import PartitionSpec as P

HEAD = 128
GROUPS = 4
LOG2E = 1.4426950408889634
VMEM_BYTES = 60 * 1024 * 1024


def dot_nt(left, right):
    return lax.dot_general(left, right, (((1,), (1,)), ((), ())), preferred_element_type=jnp.float32)


def dot_nn(left, right):
    return jnp.dot(left, right, preferred_element_type=jnp.float32)


def spin(values, cosine, sine):
    return values * cosine + pltpu.roll(values, HEAD // 2, 1) * sine


def fill_bias(bias_ref, key_ref, query_ref, keys):
    for group in range(GROUPS):
        place = query_ref[group, 0:1, :]
        own, parent, grand = (query_ref[group, 1 + n : 2 + n, :] for n in range(3))

        def one(block, carry, group=group, place=place, own=own, parent=parent, grand=grand):
            at = pl.multiple_of(block * keys, 16)
            key_place = key_ref[pl.ds(at, keys), 0:1]
            key_segment = key_ref[pl.ds(at, keys), 1:2]
            related = (key_segment == own) | (key_segment == parent) | (key_segment == grand)
            allowed = related & (key_place <= place)
            bias_ref[group * (group + 1) // 2 + block] = jnp.where(allowed, 0.0, -1e30)
            return carry

        lax.fori_loop(0, group + 1, one, 0)


def group_rows(refs, group, rows, lanes):
    parts = [ref[pl.ds(group * rows, rows), lanes] for ref in refs]
    return parts[0] if len(parts) == 1 else jnp.concatenate(parts, axis=0)


def attention_forward_body(sets, step_heads, rows, keys, scale, first_ref, *refs):
    query_refs = refs[:sets]
    key_ref, value_ref, key_info, query_info = refs[sets : sets + 4]
    out_refs = refs[sets + 4 : 2 * sets + 4]
    lse_ref, bias_ref, flipped_ref = refs[2 * sets + 4 :]
    wide = sets * rows

    @pl.when(pl.program_id(0) == 0)
    def _():
        fill_bias(bias_ref, key_info, query_info, keys)

    for head in range(step_heads):
        lanes = pl.ds(head * HEAD, HEAD)
        for block in range(GROUPS):
            values = value_ref[pl.ds(block * keys, keys), lanes].astype(jnp.float32)
            flipped_ref[head, block] = values.T.astype(jnp.bfloat16)
    for group in range(GROUPS):
        queries = [
            group_rows(query_refs, group, rows, pl.ds(head * HEAD, HEAD)) for head in range(step_heads)
        ]

        def one(block, carry, group=group, queries=queries):
            at = pl.multiple_of(block * keys, 16)
            bias = bias_ref[group * (group + 1) // 2 + block]
            result = []
            for head in range(step_heads):
                top, total, mixed = carry[3 * head : 3 * head + 3]
                scores = dot_nt(key_ref[pl.ds(at, keys), pl.ds(head * HEAD, HEAD)], queries[head])
                scores = scores * scale + bias
                new_top = jnp.maximum(top, jnp.max(scores, axis=0, keepdims=True))
                fade = jnp.exp2(top - new_top)
                parts = jnp.exp2(scores - new_top)
                total = total * fade + jnp.sum(parts, axis=0, keepdims=True)
                mixed = mixed * fade + dot_nn(flipped_ref[head, block], parts.astype(jnp.bfloat16))
                result += [new_top, total, mixed]
            return tuple(result)

        start = (
            jnp.full((1, wide), -1e30, jnp.float32),
            jnp.zeros((1, wide), jnp.float32),
            jnp.zeros((HEAD, wide), jnp.float32),
        ) * step_heads
        final = lax.fori_loop(0, group + 1, one, start)
        for head in range(step_heads):
            top, total, mixed = final[3 * head : 3 * head + 3]
            lse_ref[head, group] = top + jnp.log2(total)
            rows_out = (mixed / total).T.astype(jnp.bfloat16)
            for n, ref in enumerate(out_refs):
                ref[pl.ds(group * rows, rows), pl.ds(head * HEAD, HEAD)] = rows_out[
                    n * rows : (n + 1) * rows
                ]


def attention_backward_body(sets, step_heads, rows, keys, scale, first_ref, *refs):
    query_refs, grad_refs, out_refs = (refs[n * sets : (n + 1) * sets] for n in range(3))
    key_ref, value_ref, lse_ref, key_info, query_info = refs[3 * sets : 3 * sets + 5]
    key_cos, key_sin = refs[3 * sets + 5 : 3 * sets + 7]
    table_refs = refs[3 * sets + 7 : 5 * sets + 7]
    rest = refs[5 * sets + 7 :]
    dq_refs = rest[:sets]
    dkv_ref, bias_ref, flipped_ref, dk_acc, dv_acc = rest[sets:]
    half = dkv_ref.shape[1] // 2
    softmax_scale = scale / LOG2E

    @pl.when(pl.program_id(0) == 0)
    def _():
        fill_bias(bias_ref, key_info, query_info, keys)

    dk_acc[...] = jnp.zeros_like(dk_acc)
    dv_acc[...] = jnp.zeros_like(dv_acc)
    for head in range(step_heads):
        lanes = pl.ds(head * HEAD, HEAD)
        for block in range(GROUPS):
            values = key_ref[pl.ds(block * keys, keys), lanes].astype(jnp.float32)
            flipped_ref[head, block] = values.T.astype(jnp.bfloat16)
    for group in range(GROUPS):
        queries, grads, centres, tops = [], [], [], []
        for head in range(step_heads):
            lanes = pl.ds(head * HEAD, HEAD)
            queries.append(group_rows(query_refs, group, rows, lanes))
            grad = group_rows(grad_refs, group, rows, lanes)
            out = group_rows(out_refs, group, rows, lanes)
            product = grad.astype(jnp.float32) * out.astype(jnp.float32)
            centres.append(jnp.sum(product.T, axis=0, keepdims=True))
            grads.append(grad)
            tops.append(lse_ref[head, group])

        def one(block, carry, group=group, queries=queries, grads=grads, centres=centres, tops=tops):
            at = pl.multiple_of(block * keys, 16)
            bias = bias_ref[group * (group + 1) // 2 + block]
            result = []
            for head in range(step_heads):
                lanes = pl.ds(head * HEAD, HEAD)
                key_rows = key_ref[pl.ds(at, keys), lanes]
                scores = dot_nt(key_rows, queries[head])
                probs = jnp.exp2(scores * scale + (bias - tops[head]))
                grad_probs = dot_nt(value_ref[pl.ds(at, keys), lanes], grads[head])
                grad_scores = (probs * (grad_probs - centres[head])).astype(jnp.bfloat16)
                dv_acc[pl.ds(at, keys), lanes] += dot_nn(probs.astype(jnp.bfloat16), grads[head])
                dk_acc[pl.ds(at, keys), lanes] += dot_nn(grad_scores, queries[head])
                result.append(carry[head] + dot_nn(flipped_ref[head, block], grad_scores))
            return tuple(result)

        start = (jnp.zeros((HEAD, sets * rows), jnp.float32),) * step_heads
        final = lax.fori_loop(0, group + 1, one, start)
        for head in range(step_heads):
            dq = final[head].T * softmax_scale
            for n, ref in enumerate(dq_refs):
                span = pl.ds(group * rows, rows)
                turned = spin(
                    dq[n * rows : (n + 1) * rows], table_refs[2 * n][span, :], table_refs[2 * n + 1][span, :]
                )
                ref[span, pl.ds(head * HEAD, HEAD)] = turned.astype(jnp.bfloat16)
    for head in range(step_heads):
        lanes = pl.ds(head * HEAD, HEAD)
        first_lane = pl.multiple_of((pl.program_id(0) * step_heads + head) * HEAD, HEAD)
        for block in range(GROUPS):
            span = pl.ds(block * keys, keys)
            turned = spin(dk_acc[span, lanes] * softmax_scale, key_cos[span, :], key_sin[span, :])
            dkv_ref[span, pl.ds(first_lane, HEAD)] = turned.astype(jnp.bfloat16)
            dkv_ref[span, pl.ds(half + first_lane, HEAD)] = dv_acc[span, lanes].astype(jnp.bfloat16)


def whole_block(shape):
    return pl.BlockSpec(shape, lambda h, first: (0,) * len(shape))


def attention_forward(queries, starts, keys_all, values_all, key_info, query_info, heads):
    sets, total_rows, tokens = len(queries), queries[0].shape[0], keys_all.shape[0]
    rows, keys = total_rows // GROUPS, tokens // GROUPS
    step_heads = 2
    wide = step_heads * HEAD
    scale = HEAD ** (-0.5) * LOG2E
    query_specs = [
        pl.BlockSpec((total_rows, wide), lambda h, first, n=n: (0, first[n] + h)) for n in range(sets)
    ]
    plain = pl.BlockSpec((total_rows, wide), lambda h, first: (0, h))
    side = pl.BlockSpec((tokens, wide), lambda h, first: (0, h))
    return pl.pallas_call(
        functools.partial(attention_forward_body, sets, step_heads, rows, keys, scale),
        grid_spec=pltpu.PrefetchScalarGridSpec(
            num_scalar_prefetch=1,
            grid=(heads // step_heads,),
            in_specs=query_specs
            + [side, side, whole_block(key_info.shape), whole_block(query_info.shape)],
            out_specs=[plain] * sets
            + [pl.BlockSpec((step_heads, GROUPS, 1, sets * rows), lambda h, first: (h, 0, 0, 0))],
            scratch_shapes=[
                pltpu.VMEM((GROUPS * (GROUPS + 1) // 2, keys, sets * rows), jnp.float32),
                pltpu.VMEM((step_heads, GROUPS, HEAD, keys), jnp.bfloat16),
            ],
        ),
        out_shape=[jax.ShapeDtypeStruct((total_rows, heads * HEAD), jnp.bfloat16)] * sets
        + [jax.ShapeDtypeStruct((heads, GROUPS, 1, sets * rows), jnp.float32)],
        compiler_params=pltpu.CompilerParams(vmem_limit_bytes=VMEM_BYTES),
        name="attention_forward",
    )(starts, *queries, keys_all, values_all, key_info, query_info)


def attention_backward(
    queries, starts, grads, outs, keys_all, values_all, lse, key_info, query_info, key_tables, row_tables, heads
):
    sets, total_rows, tokens = len(queries), queries[0].shape[0], keys_all.shape[0]
    rows, keys = total_rows // GROUPS, tokens // GROUPS
    step_heads = 1
    wide = step_heads * HEAD
    scale = HEAD ** (-0.5) * LOG2E
    shifted = [
        pl.BlockSpec((total_rows, wide), lambda h, first, n=n: (0, first[n] + h)) for n in range(sets)
    ]
    plain = pl.BlockSpec((total_rows, wide), lambda h, first: (0, h))
    side = pl.BlockSpec((tokens, wide), lambda h, first: (0, h))
    return pl.pallas_call(
        functools.partial(attention_backward_body, sets, step_heads, rows, keys, scale),
        grid_spec=pltpu.PrefetchScalarGridSpec(
            num_scalar_prefetch=1,
            grid=(heads // step_heads,),
            in_specs=shifted
            + shifted
            + [plain] * sets
            + [
                side,
                side,
                pl.BlockSpec((step_heads, GROUPS, 1, sets * rows), lambda h, first: (h, 0, 0, 0)),
                whole_block(key_info.shape),
                whole_block(query_info.shape),
                whole_block((tokens, HEAD)),
                whole_block((tokens, HEAD)),
            ]
            + [whole_block((total_rows, HEAD))] * (2 * sets),
            out_specs=[plain] * sets + [whole_block((tokens, 2 * heads * HEAD))],
            scratch_shapes=[
                pltpu.VMEM((GROUPS * (GROUPS + 1) // 2, keys, sets * rows), jnp.float32),
                pltpu.VMEM((step_heads, GROUPS, HEAD, keys), jnp.bfloat16),
                pltpu.VMEM((tokens, wide), jnp.float32),
                pltpu.VMEM((tokens, wide), jnp.float32),
            ],
        ),
        out_shape=[jax.ShapeDtypeStruct((total_rows, heads * HEAD), jnp.bfloat16)] * sets
        + [jax.ShapeDtypeStruct((tokens, 2 * heads * HEAD), jnp.bfloat16)],
        compiler_params=pltpu.CompilerParams(vmem_limit_bytes=VMEM_BYTES),
        name="attention_backward",
    )(
        starts,
        *queries,
        *grads,
        *outs,
        keys_all,
        values_all,
        lse,
        key_info,
        query_info,
        *key_tables,
        *[table for pair in row_tables for table in pair],
    )


def project_body(plan_ref, hidden_ref, weight_ref, cos_ref, sin_ref, out_ref, x_ref):
    sources, capacity = plan_ref.shape[0], plan_ref.shape[1]
    bundle = max(1, sources * capacity // GROUPS // capacity)
    tile = bundle * capacity

    @pl.when(pl.program_id(0) == 0)
    def _():
        for group in range(sources // bundle):
            parts = [
                dot_nn(plan_ref[group * bundle + n], hidden_ref[group * bundle + n]) for n in range(bundle)
            ]
            x_ref[pl.ds(group * tile, tile), :] = jnp.concatenate(parts, axis=0).astype(jnp.bfloat16)

    for at in range(0, x_ref.shape[0], tile):
        span = pl.ds(at, tile)
        product = dot_nn(x_ref[span, :], weight_ref[...])
        for lane in range(0, out_ref.shape[1], HEAD):
            turned = spin(product[:, lane : lane + HEAD], cos_ref[span, :], sin_ref[span, :])
            out_ref[span, lane : lane + HEAD] = turned.astype(jnp.bfloat16)


def project_queries(plan, hidden, weight, tables):
    sources, capacity, row_count = plan.shape
    depth, columns = weight.shape
    rows = sources * capacity
    block = 512
    return pl.pallas_call(
        project_body,
        grid=(columns // block,),
        in_specs=[
            pl.BlockSpec((sources, capacity, row_count), lambda j: (0, 0, 0)),
            pl.BlockSpec((sources, row_count, depth), lambda j: (0, 0, 0)),
            pl.BlockSpec((depth, block), lambda j: (0, j)),
            pl.BlockSpec((rows, HEAD), lambda j: (0, 0)),
            pl.BlockSpec((rows, HEAD), lambda j: (0, 0)),
        ],
        out_specs=[
            pl.BlockSpec((rows, block), lambda j: (0, j)),
            pl.BlockSpec((rows, depth), lambda j: (0, 0)),
        ],
        out_shape=[
            jax.ShapeDtypeStruct((rows, columns), jnp.bfloat16),
            jax.ShapeDtypeStruct((rows, depth), jnp.bfloat16),
        ],
        compiler_params=pltpu.CompilerParams(vmem_limit_bytes=VMEM_BYTES),
        name="project_queries",
    )(plan, hidden, weight, *tables)


def keys_values_body(half, order_ref, x_ref, weight_ref, cos_ref, sin_ref, key_ref, value_ref):
    rows = x_ref.shape[1]
    for source in range(x_ref.shape[0]):
        span = pl.ds(source * rows, rows)
        product = dot_nn(x_ref[source], weight_ref[0])
        for lane in range(0, half, HEAD):
            turned = spin(product[:, lane : lane + HEAD], cos_ref[span, :], sin_ref[span, :])
            key_ref[span, lane : lane + HEAD] = turned.astype(jnp.bfloat16)
        value_ref[span, :] = product[:, half:].astype(jnp.bfloat16)


def project_keys_values(hidden, weights, tables, order):
    sources, rows, unused = hidden.shape
    parts, depth, columns = weights.shape
    half, tokens = columns // 2, sources * rows
    return pl.pallas_call(
        functools.partial(keys_values_body, half),
        grid_spec=pltpu.PrefetchScalarGridSpec(
            num_scalar_prefetch=1,
            grid=(parts,),
            in_specs=[
                pl.BlockSpec((sources, rows, depth), lambda j, order: (0, 0, 0)),
                pl.BlockSpec((1, depth, columns), lambda j, order: (j, 0, 0)),
                pl.BlockSpec((tokens, HEAD), lambda j, order: (0, 0)),
                pl.BlockSpec((tokens, HEAD), lambda j, order: (0, 0)),
            ],
            out_specs=[pl.BlockSpec((tokens, half), lambda j, order: (0, order[j]))] * 2,
        ),
        out_shape=[jax.ShapeDtypeStruct((tokens, parts * half), jnp.bfloat16)] * 2,
        compiler_params=pltpu.CompilerParams(vmem_limit_bytes=VMEM_BYTES),
        name="project_keys_values",
    )(order, hidden, weights, *tables)


def merge_body(tile, order_ref, plan_ref, slots_ref, dk_ref, dv_ref, weight_ref, out_ref, acc_ref):
    part = pl.program_id(1)
    sources, rows = plan_ref.shape[0], plan_ref.shape[1]
    ck = dk_ref.shape[1]

    @pl.when(part == 0)
    def _():
        for source in range(sources):
            acc_ref[pl.ds(source * rows, rows), :] = dot_nn(plan_ref[source], slots_ref[source])

    last = part == pl.num_programs(1) - 1
    for at in range(0, acc_ref.shape[0], tile):
        span = pl.ds(at, tile)
        acc_ref[span, :] += dot_nt(dk_ref[span, :], weight_ref[0, :, :ck]) + dot_nt(
            dv_ref[span, :], weight_ref[0, :, ck:]
        )

    @pl.when(last)
    def _():
        out_ref[...] = acc_ref[...].astype(jnp.bfloat16)


def merge_hidden_grads(plan, slots, grads, weights, order):
    sources, rows, capacity = plan.shape
    parts, depth, columns = weights.shape
    ck, tokens = columns // 2, sources * rows
    wide = depth // 2
    return pl.pallas_call(
        functools.partial(merge_body, tokens // GROUPS),
        grid_spec=pltpu.PrefetchScalarGridSpec(
            num_scalar_prefetch=1,
            grid=(2, parts),
            in_specs=[
                pl.BlockSpec((sources, rows, capacity), lambda i, j, order: (0, 0, 0)),
                pl.BlockSpec((sources, capacity, wide), lambda i, j, order: (0, 0, i)),
                pl.BlockSpec((tokens, ck), lambda i, j, order: (0, order[j])),
                pl.BlockSpec((tokens, ck), lambda i, j, order: (0, parts + order[j])),
                pl.BlockSpec((1, wide, columns), lambda i, j, order: (j, i, 0)),
            ],
            out_specs=pl.BlockSpec((tokens, wide), lambda i, j, order: (0, i)),
            scratch_shapes=[pltpu.VMEM((tokens, wide), jnp.float32)],
        ),
        out_shape=jax.ShapeDtypeStruct((tokens, depth), jnp.bfloat16),
        compiler_params=pltpu.CompilerParams(vmem_limit_bytes=VMEM_BYTES),
        name="merge_hidden_grads",
    )(order, plan, slots, grads, grads, weights)


def mesh_device(index):
    return {"expert": index}


def chip_order(chip, step):
    flip = chip // 2
    near = chip + flip * (3 - 2 * chip)
    place = step + near * (1 - 2 * step) if step < 2 else step
    return place + flip * (3 - 2 * place)


def far_order(chip, step):
    return chip_order(chip, 3 - step)


def is_middle(chip):
    flip = chip // 2
    return chip + flip * (3 - 2 * chip)


def crossing_order(chip, step):
    end, middle = chip_order(chip, step), chip_order(chip, (2, 3, 1, 0)[step])
    return end + is_middle(chip) * (middle - end)


def enter(devices, me):
    barrier = pltpu.get_barrier_semaphore()
    for step in range(1, devices):
        pl.semaphore_signal(
            barrier,
            inc=1,
            device_id=mesh_device(lax.rem(me + step, devices)),
            device_id_type=pl.DeviceIdType.MESH,
        )
    pl.semaphore_wait(barrier, devices - 1)


def remote(source, target, send, recv, device):
    return pltpu.make_async_remote_copy(
        src_ref=source,
        dst_ref=target,
        send_sem=send,
        recv_sem=recv,
        device_id=mesh_device(device),
        device_id_type=pl.DeviceIdType.MESH,
    )


class Dispatch:
    def __init__(self, me, order, slots, landing, local_sem, send, recv, pass_send, pass_recv):
        self.me, self.chip, self.core, self.order = me, me // 2, lax.rem(me, 2), order
        self.sending = stagger_order if order is stagger_order else chip_order
        self.slots, self.landing = slots, landing
        self.local_sem, self.send, self.recv = local_sem, send, recv
        self.pass_send, self.pass_recv = pass_send, pass_recv
        self.rows, self.half = slots.shape[1], slots.shape[2] // 2

    def columns(self, core):
        return pl.ds(pl.multiple_of(core * self.half, 128), self.half)

    def place(self, source, core):
        rows = pl.ds(pl.multiple_of(lax.rem(source, 2) * self.rows, 16), self.rows)
        return self.landing.at[source // 2, rows, self.columns(core)]

    def direct(self, target):
        core = lax.rem(target, 2)
        offset = lax.rem(target - self.me + 8, 8)
        return remote(
            self.slots.at[target // 2, :, self.columns(core)],
            self.place(self.me, core),
            self.send.at[offset],
            self.recv.at[offset],
            target,
        )

    def sends(self, step):
        chip = self.sending(self.chip, step)
        targets = [2 * chip, 2 * chip + 1] if step else [self.me + 1 - 2 * self.core]
        return [self.direct(target) for target in targets]

    def local(self):
        return pltpu.make_async_copy(
            self.slots.at[self.chip, :, self.columns(self.core)],
            self.place(self.me, self.core),
            self.local_sem,
        )

    def start_local(self):
        self.local().start()

    def start(self, steps):
        for step in steps:
            for copy in self.sends(step):
                copy.start()

    def sent(self, steps):
        for step in steps:
            for copy in self.sends(step):
                copy.wait_send()

    def pass_on(self, source):
        place = self.place(source, self.core)
        return remote(
            place, place, self.pass_send.at[source], self.pass_recv.at[source], self.me + 1 - 2 * self.core
        )

    def arrive(self, step):
        chip = self.order(self.chip, step)
        for source in (2 * chip, 2 * chip + 1):
            offset = lax.rem(self.me - source + 8, 8)

            @pl.when(offset == 0)
            def _():
                self.local().wait()

            @pl.when(offset != 0)
            def _(source=source, offset=offset):
                place = self.place(source, self.core)
                remote(place, place, self.send.at[offset], self.recv.at[offset], self.me).wait_recv()

            self.pass_on(source).start()

    def ready(self, step):
        chip = self.order(self.chip, step)
        for source in (2 * chip, 2 * chip + 1):
            place = self.place(source, 1 - self.core)
            remote(
                place, place, self.pass_send.at[source], self.pass_recv.at[source], self.me
            ).wait_recv()
        return chip

    def passed_on(self):
        for source in range(8):
            self.pass_on(source).wait_send()


class Collect:
    def __init__(
        self, me, order, own_steps, kept, passing, passed, total, back, local_sem, pass_send, pass_recv, send, recv
    ):
        self.me, self.chip, self.core = me, me // 2, lax.rem(me, 2)
        self.order, self.own_steps = order, own_steps
        self.kept, self.passing, self.passed, self.total, self.back = kept, passing, passed, total, back
        self.local_sem, self.pass_send, self.pass_recv = local_sem, pass_send, pass_recv
        self.send, self.recv = send, recv
        self.rows, self.half = back.shape[1], back.shape[2] // 2

    def swap(self, step):
        return remote(
            self.passing.at[step % 2],
            self.passed.at[step],
            self.pass_send.at[step],
            self.pass_recv.at[step],
            self.me + 1 - 2 * self.core,
        )

    def place(self, chip, core):
        return self.back.at[chip, :, pl.ds(pl.multiple_of(core * self.half, 128), self.half)]

    def local(self, step, source_core):
        return pltpu.make_async_copy(
            self.total.at[step, pl.ds(pl.multiple_of(source_core * self.rows, 16), self.rows), :],
            self.place(self.chip, self.core),
            self.local_sem,
        )

    def outgoing(self, step, source):
        rows = pl.ds(pl.multiple_of(lax.rem(source, 2) * self.rows, 16), self.rows)
        offset = lax.rem(source - self.me + 8, 8)
        return remote(
            self.total.at[step, rows, :],
            self.place(self.chip, self.core),
            self.send.at[offset],
            self.recv.at[offset],
            source,
        )

    def block(self, step):
        return self.order(self.chip, step)

    def each(self, step, own, other):
        chip = self.block(step)
        for source in (2 * chip, 2 * chip + 1):
            if step not in self.own_steps:
                other(source)
                continue

            @pl.when(source == self.me)
            def _():
                own()

            @pl.when(source != self.me)
            def _(source=source):
                other(source)

    def settle(self, step):
        self.swap(step).wait_recv()
        tile = 2 * self.rows // 4
        for at in range(0, 2 * self.rows, tile):
            span = pl.ds(at, tile)
            summed = self.kept[span, :] + self.passed[step, span, :].astype(jnp.float32)
            self.total[step, span, :] = summed.astype(jnp.bfloat16)
        self.each(
            step,
            lambda: self.local(step, self.core).start(),
            lambda source: self.outgoing(step, source).start(),
        )

    def finish(self):
        for step in range(4):
            if step >= 2:
                self.swap(step).wait_send()
            self.each(
                step,
                lambda step=step: self.local(step, self.core).wait(),
                lambda source, step=step: self.outgoing(step, source).wait_send(),
            )
        for offset in range(1, 8):
            source = lax.rem(self.me + 8 - offset, 8)
            place = self.place(source // 2, lax.rem(source, 2))
            remote(place, place, self.send.at[offset], self.recv.at[offset], self.me).wait_recv()


def ffn_forward_body(
    chunk,
    slots,
    gate_hbm,
    up_hbm,
    down_hbm,
    rows_out,
    gate_out,
    up_out,
    act_out,
    back,
    gate,
    up,
    down,
    landing,
    pre_stage,
    act,
    kept,
    passing,
    passed,
    total,
    weight_sem,
    stage_sem,
    act_sem,
    rows_sem,
    local_sem,
    send,
    recv,
    pass_send,
    pass_recv,
    swap_send,
    swap_recv,
    out_send,
    out_recv,
):
    me = lax.axis_index("expert")
    enter(8, me)
    loads = [
        pltpu.make_async_copy(source, target, weight_sem.at[n])
        for n, (source, target) in enumerate(((gate_hbm, gate), (up_hbm, up), (down_hbm, down)))
    ]
    dispatch = Dispatch(me, crossing_order, slots, landing, local_sem.at[0], send, recv, pass_send, pass_recv)
    collect = Collect(
        me, crossing_order, (0, 3), kept, passing, passed, total, back, local_sem.at[1], swap_send, swap_recv, out_send, out_recv
    )
    middle = is_middle(me // 2)
    dispatch.start_local()
    dispatch.start((0, 1))

    @pl.when(middle == 1)
    def _():
        dispatch.start((2,))

    for load in loads:
        load.start()
    block = landing.shape[1]
    hidden_units = gate.shape[1]
    chunks = hidden_units // chunk
    half = back.shape[2] // 2

    def stage_copies(chip, part, slot):
        span = pl.ds(pl.multiple_of(chip * block, 16), block)
        columns = pl.ds(pl.multiple_of(part * chunk, 128), chunk)
        return [
            pltpu.make_async_copy(
                pre_stage.at[slot, n], out.at[span, columns], stage_sem.at[slot, n]
            )
            for n, out in enumerate((gate_out, up_out))
        ]

    def act_copy(chip, step):
        span = pl.ds(pl.multiple_of(chip * block, 16), block)
        return pltpu.make_async_copy(act.at[step % 2], act_out.at[span, :], act_sem.at[step % 2])

    def rows_copy(chip, step):
        span = pl.ds(pl.multiple_of(chip * block, 16), block)
        return pltpu.make_async_copy(landing.at[chip], rows_out.at[span, :], rows_sem.at[step])

    for step in range(4):
        if step == 0:
            dispatch.arrive(0)
        chip = dispatch.ready(step)
        rows_copy(chip, step).start()
        if step == 0:
            loads[0].wait()
            loads[1].wait()
        if step >= 2:
            act_copy(crossing_order(me // 2, step - 2), step - 2).wait()

        def hidden_part(part, carry, chip=chip, step=step):
            slot = lax.rem(part + step * chunks, 2)
            columns = pl.ds(pl.multiple_of(part * chunk, 128), chunk)

            @pl.when(part + step * chunks >= 2)
            def _():
                for copy in stage_copies(chip, part, slot):
                    copy.wait()

            gated = dot_nn(landing[chip], gate[:, columns])
            raised = dot_nn(landing[chip], up[:, columns])
            pre_stage[slot, 0] = gated.astype(jnp.bfloat16)
            pre_stage[slot, 1] = raised.astype(jnp.bfloat16)
            act[step % 2, :, columns] = (gated * jax.nn.sigmoid(gated) * raised).astype(jnp.bfloat16)
            for copy in stage_copies(chip, part, slot):
                copy.start()
            if step == 0:
                @pl.when((part == chunks // 3) & (middle == 0))
                def _():
                    dispatch.sent((1,))
                    dispatch.start((2,))

                @pl.when((part == chunks // 2) & (middle == 1))
                def _():
                    dispatch.sent((1, 2))
                    dispatch.start((3,))

            return carry

        lax.fori_loop(0, chunks, hidden_part, 0)
        act_copy(chip, step).start()
        if step == 0:
            loads[2].wait()
        else:
            collect.settle(step - 1)
        core = collect.core
        width = min(512, half)

        def far_part(part, carry, step=step):
            at = pl.multiple_of((1 - core) * half + part * width, 128)
            product = dot_nt(act[step % 2], down[pl.ds(at, width), :])
            passing[step % 2, :, pl.ds(pl.multiple_of(part * width, 128), width)] = product.astype(jnp.bfloat16)
            return carry

        def near_part(part, carry, step=step):
            at = pl.multiple_of(core * half + part * width, 128)
            product = dot_nt(act[step % 2], down[pl.ds(at, width), :])
            kept[:, pl.ds(pl.multiple_of(part * width, 128), width)] = product
            return carry

        if step >= 2:
            collect.swap(step - 2).wait_send()
        lax.fori_loop(0, half // width, far_part, 0)
        collect.swap(step).start()
        if step == 0:

            @pl.when(middle == 0)
            def _():
                dispatch.sent((2,))
                dispatch.start((3,))

        if step < 3:
            dispatch.arrive(step + 1)
        lax.fori_loop(0, half // width, near_part, 0)
    collect.settle(3)
    for step in (2, 3):
        act_copy(crossing_order(me // 2, step), step).wait()
    for step in range(4):
        rows_copy(crossing_order(me // 2, step), step).wait()
    for slot in range(2):
        for copy in stage_copies(0, 0, slot):
            copy.wait()
    dispatch.sent((0, 3))
    dispatch.passed_on()
    collect.finish()


def ffn_forward(slots, gate_weight, up_weight, down_weight):
    chips, capacity, depth = slots.shape
    hidden_units = gate_weight.shape[1]
    block = 2 * capacity
    chunk = 256 if hidden_units % 256 == 0 else 128
    half = depth // 2
    rows = chips * block
    any_space = pl.BlockSpec(memory_space=pl.ANY)
    bf = jnp.bfloat16
    dma = pltpu.SemaphoreType.DMA
    return pl.pallas_call(
        functools.partial(ffn_forward_body, chunk),
        in_specs=[any_space] * 4,
        out_specs=[any_space] * 5,
        out_shape=[
            jax.ShapeDtypeStruct((rows, depth), bf),
            jax.ShapeDtypeStruct((rows, hidden_units), bf),
            jax.ShapeDtypeStruct((rows, hidden_units), bf),
            jax.ShapeDtypeStruct((rows, hidden_units), bf),
            jax.ShapeDtypeStruct((chips, capacity, depth), bf),
        ],
        scratch_shapes=[
            pltpu.VMEM((depth, hidden_units), bf),
            pltpu.VMEM((depth, hidden_units), bf),
            pltpu.VMEM((depth, hidden_units), bf),
            pltpu.VMEM((chips, block, depth), bf),
            pltpu.VMEM((2, 2, block, chunk), bf),
            pltpu.VMEM((2, block, hidden_units), bf),
            pltpu.VMEM((block, half), jnp.float32),
            pltpu.VMEM((2, block, half), bf),
            pltpu.VMEM((chips, block, half), bf),
            pltpu.VMEM((chips, block, half), bf),
            dma((3,)),
            dma((2, 2)),
            dma((2,)),
            dma((4,)),
            dma((2,)),
            dma((8,)),
            dma((8,)),
            dma((8,)),
            dma((8,)),
            dma((4,)),
            dma((4,)),
            dma((8,)),
            dma((8,)),
        ],
        compiler_params=pltpu.CompilerParams(
            collective_id=1, has_side_effects=True, vmem_limit_bytes=VMEM_BYTES
        ),
        name="ffn_forward",
    )(slots, gate_weight, up_weight, down_weight)


def stagger_order(chip, step):
    if step < 2:
        return chip_order(chip, step)
    end, middle = chip_order(chip, 5 - step), chip_order(chip, step)
    return end + is_middle(chip) * (middle - end)


def send_rows_body(
    slots,
    act_hbm,
    rows_out,
    grad_out,
    landing,
    act,
    total,
    stage,
    act_sem,
    rows_sem,
    stage_sem,
    local_sem,
    send,
    recv,
    pass_send,
    pass_recv,
):
    me = lax.axis_index("expert")
    enter(8, me)
    dispatch = Dispatch(me, stagger_order, slots, landing, local_sem.at[0], send, recv, pass_send, pass_recv)
    dispatch.start_local()
    dispatch.start((0, 1, 2))
    block = landing.shape[1]
    width = stage.shape[1]
    parts = landing.shape[2] // width

    def span_of(step):
        return pl.ds(pl.multiple_of(stagger_order(me // 2, step) * block, 16), block)

    def act_copy(step):
        return pltpu.make_async_copy(
            act_hbm.at[span_of(step), :], act.at[pl.ds(step * block, block), :], act_sem.at[step]
        )

    def rows_copy(step):
        chip = stagger_order(me // 2, step)
        return pltpu.make_async_copy(landing.at[chip], rows_out.at[chip], rows_sem.at[step])

    def stage_copy(part):
        slot = lax.rem(part, 2)
        span = pl.ds(pl.multiple_of(part * width, 16), width)
        return pltpu.make_async_copy(stage.at[slot], grad_out.at[span, :], stage_sem.at[slot])

    for step in range(4):
        act_copy(step).start()
    for steps in ((0, 1), (2,), (3,)):
        for step in steps:
            dispatch.arrive(step)
        chips = [dispatch.ready(step) for step in steps]
        for step in steps:
            rows_copy(step).start()
            act_copy(step).wait()

        def one(part, carry, steps=steps, chips=chips):
            columns = pl.ds(pl.multiple_of(part * width, 128), width)
            rows = [landing[chip, :, columns] for chip in chips]
            rows = rows[0] if len(rows) == 1 else jnp.concatenate(rows, axis=0)
            turned = rows.astype(jnp.float32).T.astype(jnp.bfloat16)
            product = dot_nn(turned, act[pl.ds(steps[0] * block, len(steps) * block), :])
            span = pl.ds(pl.multiple_of(part * width, 16), width)
            if steps[0] == 0:
                total[span, :] = product

                @pl.when(part == 0)
                def _():
                    dispatch.sent((2,))
                    dispatch.start((3,))

                return carry
            if steps[0] == 2:
                total[span, :] += product
                return carry

            @pl.when(part >= 2)
            def _():
                stage_copy(part - 2).wait()

            stage[lax.rem(part, 2)] = (total[span, :] + product).astype(jnp.bfloat16)
            stage_copy(part).start()
            return carry

        lax.fori_loop(0, parts, one, 0)
    for part in (parts - 2, parts - 1):
        stage_copy(part).wait()
    for step in range(4):
        rows_copy(step).wait()
    dispatch.sent((0, 1, 3))
    dispatch.passed_on()


def send_rows(slots, act):
    chips, capacity, depth = slots.shape
    rows, hidden_units = act.shape
    block = 2 * capacity
    width = min(256, depth // 2)
    any_space = pl.BlockSpec(memory_space=pl.ANY)
    bf = jnp.bfloat16
    dma = pltpu.SemaphoreType.DMA
    return pl.pallas_call(
        send_rows_body,
        in_specs=[any_space] * 2,
        out_specs=[any_space] * 2,
        out_shape=[
            jax.ShapeDtypeStruct((chips, block, depth), bf),
            jax.ShapeDtypeStruct((depth, hidden_units), bf),
        ],
        scratch_shapes=[
            pltpu.VMEM((chips, block, depth), bf),
            pltpu.VMEM((rows, hidden_units), bf),
            pltpu.VMEM((depth, hidden_units), jnp.float32),
            pltpu.VMEM((2, width, hidden_units), bf),
            dma((4,)),
            dma((4,)),
            dma((2,)),
            dma((1,)),
            dma((8,)),
            dma((8,)),
            dma((8,)),
            dma((8,)),
        ],
        compiler_params=pltpu.CompilerParams(
            collective_id=2, has_side_effects=True, vmem_limit_bytes=VMEM_BYTES
        ),
        name="send_rows",
    )(slots, act)


def ffn_backward_body(
    chunk,
    grad_rows,
    gate_in,
    up_in,
    gate_hbm,
    up_hbm,
    down_hbm,
    dgate_out,
    dup_out,
    back,
    gate,
    up,
    down,
    grad,
    pre_stage,
    pair,
    kept,
    passing,
    passed,
    total,
    weight_sem,
    grad_sem,
    stage_sem,
    pair_sem,
    local_sem,
    swap_send,
    swap_recv,
    out_send,
    out_recv,
):
    me = lax.axis_index("expert")
    enter(8, me)
    collect = Collect(
        me, far_order, (3,), kept, passing, passed, total, back, local_sem.at[0], swap_send, swap_recv, out_send, out_recv
    )
    loads = [
        pltpu.make_async_copy(source, target, weight_sem.at[n])
        for n, (source, target) in enumerate(((down_hbm, down), (gate_hbm, gate), (up_hbm, up)))
    ]
    block = grad.shape[1]
    hidden_units = gate.shape[1]
    chunks = hidden_units // chunk
    half = back.shape[2] // 2
    width = min(512, half)

    def span_of(chip):
        return pl.ds(pl.multiple_of(chip * block, 16), block)

    def grad_copy(step):
        return pltpu.make_async_copy(
            grad_rows.at[span_of(collect.block(step)), :], grad.at[step % 2], grad_sem.at[step % 2]
        )

    def stage_copies(chip, part, slot):
        columns = pl.ds(pl.multiple_of(part * chunk, 128), chunk)
        return [
            pltpu.make_async_copy(
                source.at[span_of(chip), columns], pre_stage.at[slot, n], stage_sem.at[slot, n]
            )
            for n, source in enumerate((gate_in, up_in))
        ]

    def pair_copies(chip):
        return [
            pltpu.make_async_copy(pair.at[n], out.at[span_of(chip), :], pair_sem.at[n])
            for n, out in enumerate((dgate_out, dup_out))
        ]

    grad_copy(0).start()
    loads[0].start()
    for copy in stage_copies(collect.block(0), 0, 0):
        copy.start()
    loads[1].start()
    loads[2].start()
    loads[0].wait()
    for step in range(4):
        chip = collect.block(step)
        grad_copy(step).wait()
        if step < 3:
            grad_copy(step + 1).start()
        if step > 0:
            for copy in pair_copies(collect.block(step - 1)):
                copy.wait()

        def hidden_part(part, carry, chip=chip, step=step):
            slot = lax.rem(part, 2)
            columns = pl.ds(pl.multiple_of(part * chunk, 128), chunk)
            for copy in stage_copies(chip, part, slot):
                copy.wait()

            @pl.when(part + 1 < chunks)
            def _():
                for copy in stage_copies(chip, part + 1, 1 - slot):
                    copy.start()

            upstream = dot_nn(grad[step % 2], down[:, columns])
            gated = pre_stage[slot, 0].astype(jnp.float32)
            raised = pre_stage[slot, 1].astype(jnp.float32)
            sigmoid = jax.nn.sigmoid(gated)
            scaled = upstream * sigmoid
            pair[0, :, columns] = (scaled * raised * (1.0 + gated * (1.0 - sigmoid))).astype(jnp.bfloat16)
            pair[1, :, columns] = (scaled * gated).astype(jnp.bfloat16)
            return carry

        lax.fori_loop(0, chunks, hidden_part, 0)
        for copy in pair_copies(chip):
            copy.start()
        if step < 3:
            for copy in stage_copies(collect.block(step + 1), 0, 0):
                copy.start()
        if step == 0:
            loads[1].wait()
            loads[2].wait()
        else:
            collect.settle(step - 1)
        core = collect.core

        def product(at):
            return dot_nt(pair[0], gate[pl.ds(at, width), :]) + dot_nt(pair[1], up[pl.ds(at, width), :])

        def far_part(part, carry, step=step):
            at = pl.multiple_of((1 - core) * half + part * width, 128)
            columns = pl.ds(pl.multiple_of(part * width, 128), width)
            passing[step % 2, :, columns] = product(at).astype(jnp.bfloat16)
            return carry

        def near_part(part, carry, step=step):
            at = pl.multiple_of(core * half + part * width, 128)
            kept[:, pl.ds(pl.multiple_of(part * width, 128), width)] = product(at)
            return carry

        if step >= 2:
            collect.swap(step - 2).wait_send()
        lax.fori_loop(0, half // width, far_part, 0)
        collect.swap(step).start()
        lax.fori_loop(0, half // width, near_part, 0)
    collect.settle(3)
    for copy in pair_copies(collect.block(3)):
        copy.wait()
    collect.finish()


def ffn_backward(grad_rows, gate_pre, up_pre, gate_weight, up_weight, down_weight, capacity):
    rows, depth = grad_rows.shape
    hidden_units = gate_weight.shape[1]
    block = 2 * capacity
    chips = rows // block
    chunk = hidden_units // 2 if hidden_units % 256 == 0 else 128
    half = depth // 2
    any_space = pl.BlockSpec(memory_space=pl.ANY)
    bf = jnp.bfloat16
    dma = pltpu.SemaphoreType.DMA
    return pl.pallas_call(
        functools.partial(ffn_backward_body, chunk),
        in_specs=[any_space] * 6,
        out_specs=[any_space] * 3,
        out_shape=[
            jax.ShapeDtypeStruct((rows, hidden_units), bf),
            jax.ShapeDtypeStruct((rows, hidden_units), bf),
            jax.ShapeDtypeStruct((chips, capacity, depth), bf),
        ],
        scratch_shapes=[
            pltpu.VMEM((depth, hidden_units), bf),
            pltpu.VMEM((depth, hidden_units), bf),
            pltpu.VMEM((depth, hidden_units), bf),
            pltpu.VMEM((2, block, depth), bf),
            pltpu.VMEM((2, 2, block, chunk), bf),
            pltpu.VMEM((2, block, hidden_units), bf),
            pltpu.VMEM((block, half), jnp.float32),
            pltpu.VMEM((2, block, half), bf),
            pltpu.VMEM((chips, block, half), bf),
            pltpu.VMEM((chips, block, half), bf),
            dma((3,)),
            dma((2,)),
            dma((2, 2)),
            dma((2,)),
            dma((1,)),
            dma((4,)),
            dma((4,)),
            dma((8,)),
            dma((8,)),
        ],
        compiler_params=pltpu.CompilerParams(
            collective_id=3, has_side_effects=True, vmem_limit_bytes=VMEM_BYTES
        ),
        name="ffn_backward",
    )(grad_rows, gate_pre, up_pre, gate_weight, up_weight, down_weight)


def send_slots_body(
    slots, rows_hbm, grads_hbm, landing, grad_out, rows_v, grads_v, stage, load_sem, stage_sem, local_sem, send, recv
):
    me = lax.axis_index("expert")
    enter(8, me)

    def outgoing(offset):
        target = lax.rem(me + offset, 8)
        return remote(slots.at[target], landing.at[me], send.at[offset], recv.at[offset], target)

    local = pltpu.make_async_copy(slots.at[me], landing.at[me], local_sem)
    for offset in range(1, 8):
        outgoing(offset).start()
    local.start()
    loads = [
        pltpu.make_async_copy(source, target, load_sem.at[n])
        for n, (source, target) in enumerate(((rows_hbm, rows_v), (grads_hbm, grads_v)))
    ]
    for load in loads:
        load.start()
    for load in loads:
        load.wait()
    width = stage.shape[1]
    blocks = rows_v.shape[1] // width

    def stage_copy(block):
        slot = lax.rem(block, 2)
        span = pl.ds(pl.multiple_of(block * width, 16), width)
        return pltpu.make_async_copy(stage.at[slot], grad_out.at[span, :], stage_sem.at[slot])

    def one(block, carry):
        @pl.when(block >= 2)
        def _():
            stage_copy(block - 2).wait()

        columns = pl.ds(pl.multiple_of(block * width, 128), width)
        turned = rows_v[:, columns].astype(jnp.float32).T.astype(jnp.bfloat16)
        stage[lax.rem(block, 2)] = dot_nn(turned, grads_v[...]).astype(jnp.bfloat16)
        stage_copy(block).start()
        return carry

    lax.fori_loop(0, blocks, one, 0)
    for block in (blocks - 2, blocks - 1):
        stage_copy(block).wait()
    local.wait()
    for offset in range(1, 8):
        outgoing(offset).wait_send()
        place = landing.at[lax.rem(me + 8 - offset, 8)]
        remote(place, place, send.at[offset], recv.at[offset], me).wait_recv()


def send_slots(slots, rows, grads):
    total, depth = rows.shape
    hidden_units = grads.shape[1]
    width = min(256, depth // 2)
    any_space = pl.BlockSpec(memory_space=pl.ANY)
    bf = jnp.bfloat16
    dma = pltpu.SemaphoreType.DMA
    return pl.pallas_call(
        send_slots_body,
        in_specs=[any_space] * 3,
        out_specs=[any_space] * 2,
        out_shape=[
            jax.ShapeDtypeStruct(slots.shape, bf),
            jax.ShapeDtypeStruct((depth, hidden_units), bf),
        ],
        scratch_shapes=[
            pltpu.VMEM((total, depth), bf),
            pltpu.VMEM((total, hidden_units), bf),
            pltpu.VMEM((2, width, hidden_units), bf),
            dma((2,)),
            dma((2,)),
            dma,
            dma((8,)),
            dma((8,)),
        ],
        compiler_params=pltpu.CompilerParams(
            collective_id=5, has_side_effects=True, vmem_limit_bytes=VMEM_BYTES
        ),
        name="send_slots",
    )(slots, rows, grads)


def merge_return_body(
    dp_axis,
    plan_hbm,
    slots_hbm,
    grads_hbm,
    weight_hbm,
    back,
    plan,
    slots,
    grads,
    weight,
    kept,
    passing,
    passed,
    total,
    load_sem,
    local_sem,
    swap_send,
    swap_recv,
    out_send,
    out_recv,
):
    me = lax.axis_index("expert")
    replica = lax.axis_index(dp_axis)
    enter(8, me)
    loads = [
        pltpu.make_async_copy(source, target, load_sem.at[n])
        for n, (source, target) in enumerate(
            ((plan_hbm, plan), (slots_hbm, slots), (grads_hbm, grads), (weight_hbm, weight))
        )
    ]
    for load in loads:
        load.start()
    collect = Collect(
        me, far_order, (3,), kept, passing, passed, total, back, local_sem.at[0], swap_send, swap_recv, out_send, out_recv
    )
    rows, half = collect.rows, collect.half
    parts, ck = weight.shape[0], weight.shape[2] // 2
    values_at = grads.shape[1] // 2
    width = min(512, half)
    for load in loads:
        load.wait()
    for step in range(4):
        chip = collect.block(step)
        span = pl.ds(pl.multiple_of(chip * 2 * rows, 16), 2 * rows)

        def product(at, chip=chip, span=span):
            columns = pl.ds(at, width)
            result = jnp.concatenate(
                [dot_nn(plan[2 * chip + n], slots[2 * chip + n, :, columns]) for n in range(2)], axis=0
            )
            for part in range(parts):
                low = lax.rem(replica, 2) + (part % 2) * (1 - 2 * lax.rem(replica, 2))
                high = replica // 2 + (part // 2) * (1 - 2 * (replica // 2))
                at_keys = pl.multiple_of((2 * high + low) * ck, 128)
                result += dot_nt(grads[span, pl.ds(at_keys, ck)], weight[part, columns, :ck])
                result += dot_nt(grads[span, pl.ds(values_at + at_keys, ck)], weight[part, columns, ck:])
            return result

        def far_part(part, carry, step=step, product=product):
            at = pl.multiple_of((1 - collect.core) * half + part * width, 128)
            columns = pl.ds(pl.multiple_of(part * width, 128), width)
            passing[step % 2, :, columns] = product(at).astype(jnp.bfloat16)
            return carry

        def near_part(part, carry, product=product):
            at = pl.multiple_of(collect.core * half + part * width, 128)
            kept[:, pl.ds(pl.multiple_of(part * width, 128), width)] = product(at)
            return carry

        if step >= 2:
            collect.swap(step - 2).wait_send()
        lax.fori_loop(0, half // width, far_part, 0)
        collect.swap(step).start()
        if step > 0:
            collect.settle(step - 1)
        lax.fori_loop(0, half // width, near_part, 0)
    collect.settle(3)
    collect.finish()


def merge_return(plan, slots, grads, weights):
    sources, rows, capacity = plan.shape
    parts, depth, columns = weights.shape
    tokens = sources * rows
    half = depth // 2
    any_space = pl.BlockSpec(memory_space=pl.ANY)
    bf = jnp.bfloat16
    dma = pltpu.SemaphoreType.DMA
    return pl.pallas_call(
        functools.partial(merge_return_body, "dp"),
        in_specs=[any_space] * 4,
        out_specs=any_space,
        out_shape=jax.ShapeDtypeStruct((sources // 2, rows, depth), bf),
        scratch_shapes=[
            pltpu.VMEM(plan.shape, bf),
            pltpu.VMEM(slots.shape, bf),
            pltpu.VMEM(grads.shape, bf),
            pltpu.VMEM(weights.shape, bf),
            pltpu.VMEM((2 * rows, half), jnp.float32),
            pltpu.VMEM((2, 2 * rows, half), bf),
            pltpu.VMEM((sources // 2, 2 * rows, half), bf),
            pltpu.VMEM((sources // 2, 2 * rows, half), bf),
            dma((4,)),
            dma((1,)),
            dma((4,)),
            dma((4,)),
            dma((8,)),
            dma((8,)),
        ],
        compiler_params=pltpu.CompilerParams(
            collective_id=6, has_side_effects=True, vmem_limit_bytes=VMEM_BYTES
        ),
        name="merge_return",
    )(plan, slots, grads, weights)


def return_order(chip, step):
    lower, upper = chip_order(chip, (2, 3, 1, 0)[step]), chip_order(chip, 3 - step)
    return lower + chip // 2 * (upper - lower)


def attention_send_body(
    scale,
    query_hbm,
    sibling_hbm,
    key_hbm,
    value_hbm,
    out_weight_hbm,
    key_info,
    query_info,
    own_out,
    sibling_out,
    rows_out,
    back,
    lse_ref,
    queries,
    siblings,
    keys_v,
    values_v,
    out_weight,
    bias_ref,
    flipped,
    own_stage,
    sibling_stage,
    arrived,
    rows_stage,
    sending,
    load_sem,
    own_sem,
    sibling_sem,
    rows_sem,
    local_sem,
    swap_send,
    swap_recv,
    out_send,
    out_recv,
):
    me = lax.axis_index("expert")
    chip, core = me // 2, lax.rem(me, 2)
    enter(8, me)
    half = keys_v.shape[1]
    rows = own_stage.shape[1]
    keys = keys_v.shape[0] // GROUPS
    heads = half // HEAD
    capacity = back.shape[1]
    own_columns = pl.ds(pl.multiple_of(core * half, 128), half)
    far_columns = pl.ds(pl.multiple_of((1 - core) * half, 128), half)
    loads = [
        pltpu.make_async_copy(source, target, load_sem.at[n])
        for n, (source, target) in enumerate(
            (
                (value_hbm, values_v),
                (key_hbm, keys_v),
                (query_hbm.at[:, own_columns], queries),
                (sibling_hbm, siblings),
                (out_weight_hbm, out_weight),
            )
        )
    ]
    for load in loads:
        load.start()
    fill_bias(bias_ref, key_info, query_info, keys)
    loads[0].wait()

    def flip(head, carry):
        lanes = pl.ds(pl.multiple_of(head * HEAD, HEAD), HEAD)
        for block in range(GROUPS):
            values = values_v[pl.ds(block * keys, keys), lanes].astype(jnp.float32)
            flipped[head, block] = values.T.astype(jnp.bfloat16)
        return carry

    lax.fori_loop(0, heads, flip, 0)
    for load in loads[1:4]:
        load.wait()

    def group_of(step):
        return return_order(chip, step)

    def span_of(step):
        return pl.ds(pl.multiple_of(group_of(step) * rows, 16), rows)

    def own_copy(step):
        return pltpu.make_async_copy(own_stage.at[step], own_out.at[span_of(step), :], own_sem.at[step])

    def sibling_copy(step):
        return pltpu.make_async_copy(
            sibling_stage.at[step], sibling_out.at[span_of(step), :], sibling_sem.at[step]
        )

    def rows_copy(step):
        return pltpu.make_async_copy(
            rows_stage.at[step], rows_out.at[span_of(step), :], rows_sem.at[step]
        )

    def swap(step):
        return remote(
            sibling_stage.at[step], arrived.at[step], swap_send.at[step], swap_recv.at[step], me + 1 - 2 * core
        )

    def outgoing(step, n):
        source = 2 * group_of(step) + n
        offset = lax.rem(source - me + 8, 8)
        return remote(sending.at[step, n], back.at[me], out_send.at[offset], out_recv.at[offset], source)

    def local(step, n):
        return pltpu.make_async_copy(sending.at[step, n], back.at[me], local_sem)

    def each(step, own, other):
        for n in range(2):
            if step < 3:
                other(n)
                continue

            @pl.when(core == n)
            def _(n=n):
                own(n)

            @pl.when(core != n)
            def _(n=n):
                other(n)

    def attend(step):
        group = group_of(step)
        first_block = group * (group + 1) // 2
        span = span_of(step)

        def head_pair(pair, carry):
            lanes = [pl.ds(pl.multiple_of((2 * pair + n) * HEAD, HEAD), HEAD) for n in range(2)]
            parts = [jnp.concatenate([queries[span, lane], siblings[span, lane]], axis=0) for lane in lanes]

            def one(block, state):
                at = pl.multiple_of(block * keys, 16)
                bias = bias_ref[first_block + block]
                result = []
                for n in range(2):
                    top, total, mixed = state[3 * n : 3 * n + 3]
                    scores = dot_nt(keys_v[pl.ds(at, keys), lanes[n]], parts[n]) * scale + bias
                    new_top = jnp.maximum(top, jnp.max(scores, axis=0, keepdims=True))
                    fade = jnp.exp2(top - new_top)
                    probs = jnp.exp2(scores - new_top)
                    total = total * fade + jnp.sum(probs, axis=0, keepdims=True)
                    mixed = mixed * fade + dot_nn(flipped[2 * pair + n, block], probs.astype(jnp.bfloat16))
                    result += [new_top, total, mixed]
                return tuple(result)

            start = (
                jnp.full((1, 2 * rows), -1e30, jnp.float32),
                jnp.zeros((1, 2 * rows), jnp.float32),
                jnp.zeros((HEAD, 2 * rows), jnp.float32),
            ) * 2
            final = lax.fori_loop(0, group + 1, one, start)
            for n in range(2):
                top, total, mixed = final[3 * n : 3 * n + 3]
                lse_ref[2 * pair + n, group] = top + jnp.log2(total)
                result = (mixed / total).T.astype(jnp.bfloat16)
                own_stage[step, :, lanes[n]] = result[:rows]
                sibling_stage[step, :, lanes[n]] = result[rows:]
            return carry

        lax.fori_loop(0, heads // 2, head_pair, 0)
        swap(step).start()
        own_copy(step).start()
        sibling_copy(step).start()

    def settle(step):
        swap(step).wait_recv()
        rows_stage[step, :, own_columns] = own_stage[step]
        rows_stage[step, :, far_columns] = arrived[step]
        rows_copy(step).start()
        width = 512
        for at in range(0, back.shape[2], min(width, back.shape[2])):
            columns = pl.ds(at, min(width, back.shape[2]))
            product = dot_nt(rows_stage[step], out_weight[columns, :])
            for n in range(2):
                part = product[n * capacity : (n + 1) * capacity]
                sending[step, n, :, columns] = part.astype(jnp.bfloat16)
        each(step, lambda n: local(step, n).start(), lambda n: outgoing(step, n).start())

    for step in range(4):
        attend(step)
        if step == 0:
            loads[4].wait()
        settle(step)
    for step in range(4):
        swap(step).wait_send()
        own_copy(step).wait()
        sibling_copy(step).wait()
        rows_copy(step).wait()
        each(step, lambda n, step=step: local(step, n).wait(), lambda n, step=step: outgoing(step, n).wait_send())
    for offset in range(1, 8):
        place = back.at[lax.rem(me + 8 - offset, 8)]
        remote(place, place, out_send.at[offset], out_recv.at[offset], me).wait_recv()


def attention_send(queries, siblings, keys_all, values_all, out_weight, key_info, query_info, capacity):
    total_rows, width = queries.shape
    tokens, half = keys_all.shape
    depth = out_weight.shape[0]
    rows, keys, heads = total_rows // GROUPS, tokens // GROUPS, half // HEAD
    any_space = pl.BlockSpec(memory_space=pl.ANY)
    here = pl.BlockSpec(memory_space=pltpu.VMEM)
    bf = jnp.bfloat16
    dma = pltpu.SemaphoreType.DMA
    return pl.pallas_call(
        functools.partial(attention_send_body, HEAD ** (-0.5) * LOG2E),
        in_specs=[any_space] * 5 + [here] * 2,
        out_specs=[any_space] * 4 + [here],
        out_shape=[
            jax.ShapeDtypeStruct((total_rows, half), bf),
            jax.ShapeDtypeStruct((total_rows, half), bf),
            jax.ShapeDtypeStruct((total_rows, width), bf),
            jax.ShapeDtypeStruct((8, capacity, depth), bf),
            jax.ShapeDtypeStruct((heads, GROUPS, 1, 2 * rows), jnp.float32),
        ],
        scratch_shapes=[
            pltpu.VMEM((total_rows, half), bf),
            pltpu.VMEM((total_rows, half), bf),
            pltpu.VMEM((tokens, half), bf),
            pltpu.VMEM((tokens, half), bf),
            pltpu.VMEM(out_weight.shape, bf),
            pltpu.VMEM((GROUPS * (GROUPS + 1) // 2, keys, 2 * rows), jnp.float32),
            pltpu.VMEM((heads, GROUPS, HEAD, keys), bf),
            pltpu.VMEM((GROUPS, rows, half), bf),
            pltpu.VMEM((GROUPS, rows, half), bf),
            pltpu.VMEM((GROUPS, rows, half), bf),
            pltpu.VMEM((GROUPS, rows, width), bf),
            pltpu.VMEM((GROUPS, 2, capacity, depth), bf),
            dma((5,)),
            dma((GROUPS,)),
            dma((GROUPS,)),
            dma((GROUPS,)),
            dma,
            dma((GROUPS,)),
            dma((GROUPS,)),
            dma((8,)),
            dma((8,)),
        ],
        compiler_params=pltpu.CompilerParams(
            collective_id=4, has_side_effects=True, vmem_limit_bytes=VMEM_BYTES
        ),
        name="attention_send",
    )(queries, siblings, keys_all, values_all, out_weight, key_info, query_info)


def swap_blocks_body(blocks, landing, local_sem, send, recv):
    me = lax.axis_index("expert")
    enter(8, me)

    def outgoing(offset):
        target = lax.rem(me + offset, 8)
        return remote(blocks.at[target], landing.at[me], send.at[offset], recv.at[offset], target)

    local = pltpu.make_async_copy(blocks.at[me], landing.at[me], local_sem)
    for offset in range(1, 8):
        outgoing(offset).start()
    local.start()
    local.wait()
    for offset in range(1, 8):
        outgoing(offset).wait_send()
        place = landing.at[lax.rem(me + 8 - offset, 8)]
        remote(place, place, send.at[offset], recv.at[offset], me).wait_recv()


def swap_blocks(blocks):
    any_space = pl.BlockSpec(memory_space=pl.ANY)
    dma = pltpu.SemaphoreType.DMA
    return pl.pallas_call(
        swap_blocks_body,
        in_specs=[any_space],
        out_specs=any_space,
        out_shape=jax.ShapeDtypeStruct(blocks.shape, blocks.dtype),
        scratch_shapes=[dma, dma((8,)), dma((8,))],
        compiler_params=pltpu.CompilerParams(collective_id=7, has_side_effects=True),
        name="swap_blocks",
    )(blocks)


D = 2048
HEADS = 16
ATT_EXPERTS = 8
FFN_EXPERTS = 4
TRUNK = 1024
SEG = 96
TREE_LEN = 2176
NODES = 13

epsilon = 1e-06
highest = lax.Precision.HIGHEST
bf16 = jnp.bfloat16
f32 = jnp.float32


def tree_layout(places):
    after_trunk = places - TRUNK
    after_branch = after_trunk - 4 * SEG
    segments = jnp.where(
        places < TRUNK,
        0,
        jnp.where(after_branch < 0, 1 + after_trunk // SEG, 5 + after_branch // SEG),
    )
    depths = jnp.where(
        places < TRUNK,
        places,
        jnp.where(after_branch < 0, TRUNK + after_trunk % SEG, TRUNK + SEG + after_branch % SEG),
    )
    return (segments.astype(jnp.int32), depths.astype(jnp.int32))


def rotation_tables(depths):
    half_size = HEAD // 2
    frequency = 10000.0 ** (-jnp.arange(half_size, dtype=f32) * 2.0 / HEAD)
    angles = depths.astype(f32)[:, None] * frequency[None, :]
    cosine, sine = jnp.cos(angles), jnp.sin(angles)
    cosines = jnp.concatenate([cosine, cosine], axis=1)
    forward = jnp.concatenate([-sine, sine], axis=1)
    return (cosines, forward), (cosines, -forward)


def lookup(table, indices):
    nodes = jnp.arange(NODES, dtype=jnp.int32)
    return jnp.sum(jnp.where(indices[:, None] == nodes[None, :], table[None, :], 0), axis=1)


def running_count(chosen):
    rows = chosen.shape[-1]
    index = jnp.arange(rows, dtype=jnp.int32)
    upto = (index[:, None] <= index[None, :]).astype(bf16)
    return jnp.dot(chosen.astype(bf16), upto, preferred_element_type=f32).astype(jnp.int32) - 1


def source_plan(routes, expert, capacity):
    chosen = jnp.any(routes == expert, axis=2)
    ranking = running_count(chosen)
    slots = jnp.arange(capacity, dtype=jnp.int32)
    return chosen[:, None, :] & (ranking[:, None, :] == slots[None, :, None])


def token_picks(routes, experts, capacity):
    labels = jnp.arange(experts, dtype=jnp.int32)
    hits = routes.T[:, None, :] == labels[None, :, None]
    ranking = running_count(hits[0] | hits[1])
    slots = jnp.arange(capacity, dtype=jnp.int32)
    picks = hits[:, :, None, :] & (ranking[None, :, None, :] == slots[None, None, :, None])
    return picks.astype(bf16), hits[0].T.astype(f32), hits[1].T.astype(f32)


def fill_slots(picks, pair):
    return jnp.einsum("kecr,krd->ecd", picks, pair, preferred_element_type=f32).astype(bf16)


def read_slots(picks, slots):
    return jnp.einsum("kecr,ecd->krd", picks, slots, preferred_element_type=f32)


def gate_values(hidden, router, first, second):
    logits = jnp.dot(hidden.astype(f32), router, precision=highest)
    picked = jnp.stack([jnp.sum(logits * first, axis=1), jnp.sum(logits * second, axis=1)], axis=1)
    return jax.nn.softmax(picked, axis=1)


def router_grads(hidden, router, gates, first, second, picked_grad):
    logit_pick = gates * (picked_grad - jnp.sum(gates * picked_grad, axis=1, keepdims=True))
    logit_grad = logit_pick[:, 0:1] * first + logit_pick[:, 1:2] * second
    router_grad = jnp.dot(hidden.astype(f32).T, logit_grad, precision=highest)
    hidden_grad = jnp.dot(logit_grad, router.T, precision=highest)
    return (router_grad, hidden_grad)


def rms_parts(values):
    inverse = lax.rsqrt(jnp.mean(values * values, axis=-1, keepdims=True) + epsilon)
    return (values * inverse, inverse)


def norm_back(grad_normed, normed, inverse):
    return inverse * (grad_normed - normed * jnp.mean(grad_normed * normed, axis=-1, keepdims=True))


def pair_grads(gates, branches, upstream):
    gate_grad = jnp.stack([jnp.sum(upstream * branches[k], axis=1) for k in range(2)], axis=1)
    scaled = jnp.stack([gates[:, k : k + 1] * upstream for k in range(2)]).astype(bf16)
    return gate_grad, scaled


def exchange(slots):
    return lax.all_to_all(slots, "expert", split_axis=0, concat_axis=0, tiled=True)


def shift(values, step, size, devices):
    moves = [(i, i // size * size + (i % size + step) % size) for i in range(devices)]
    return lax.ppermute(values, "expert", moves)


def group_gather(rows, size, devices):
    return jnp.concatenate([rows] + [shift(rows, step, size, devices) for step in range(1, size)])


def group_reduce(partial, size, devices):
    parts = partial.reshape(size, -1, partial.shape[1])
    total = parts[0].astype(f32)
    for step in range(1, size):
        total = total + shift(parts[step], -step, size, devices).astype(f32)
    return total.astype(bf16)


def spread_over_replicas(block, my_replica, replicas):
    if replicas != 4:
        return lax.all_gather(block, "dp", axis=0), jnp.arange(replicas, dtype=jnp.int32)
    across, along = ([(i, i ^ n) for i in range(4)] for n in (1, 2))
    first, second = lax.ppermute(block, "dp", across), lax.ppermute(block, "dp", along)
    cut = block.shape[0] // 2
    upper, lower = lax.ppermute(second[:cut], "dp", across), lax.ppermute(first[cut:], "dp", along)
    blocks = jnp.stack([block, first, second, jnp.concatenate([upper, lower])])
    return blocks, my_replica ^ jnp.arange(4, dtype=jnp.int32)


def dot_tn(left, right):
    return lax.dot_general(left, right, (((0,), (0,)), ((), ())), preferred_element_type=f32)


def body(
    tokens,
    teacher,
    att_routes,
    ffn_routes,
    parent,
    valid,
    gain_one,
    kv_weight,
    att_router,
    q_weight,
    o_weight,
    gain_two,
    ffn_router,
    gate_weight,
    up_weight,
    down_weight,
):
    row_count = tokens.shape[0]
    devices, replicas = lax.axis_size("expert"), lax.axis_size("dp")
    my_index, my_replica = lax.axis_index("expert"), lax.axis_index("dp")
    core = my_index % 2
    att_copies, ffn_copies = devices // ATT_EXPERTS, devices // FFN_EXPERTS
    att_capacity, ffn_capacity = row_count * 13 // 40, row_count * 13 // 20
    token_count = row_count * devices
    half = HEADS * HEAD // 2
    assert token_count == TREE_LEN * parent.shape[0] and parent.shape[0] == 1
    pair = [(i, i ^ 1) for i in range(devices)]
    own_places = my_index * row_count + jnp.arange(row_count, dtype=jnp.int32)

    x_in = tokens.astype(f32)
    normed_one, inverse_one = rms_parts(x_in)
    hidden = (normed_one * gain_one).astype(bf16)
    weight_rows = kv_weight.shape[0]
    piece = half // replicas
    kv_share = lax.dynamic_slice_in_dim(
        kv_weight.reshape(weight_rows, 4, replicas, piece), my_replica, 1, 2
    )
    kv_share = (
        kv_share.reshape(weight_rows, 2, 2, piece).transpose(0, 2, 1, 3).reshape(weight_rows, 4 * piece)
    )
    kv_gathered = lax.all_gather(kv_share, "expert", axis=0)
    hidden_all = lax.all_gather(hidden, "expert", axis=0)
    all_routes = lax.all_gather(att_routes, "expert", axis=0)

    tree_places = jnp.arange(token_count, dtype=jnp.int32)
    tree_segments, tree_depths = tree_layout(tree_places)
    key_forward, key_backward = rotation_tables(tree_depths)
    key_info = jnp.pad(jnp.stack([tree_places, tree_segments], axis=1), ((0, 0), (0, 6)))
    experts_here = [my_index // att_copies]
    if att_copies == 1:
        experts_here.append(my_index ^ 1)
    plans = [source_plan(all_routes, expert, att_capacity) for expert in experts_here]
    slot_tables, query_parts = [], []
    for plan in plans:
        places = jnp.sum(
            jnp.where(plan, tree_places.reshape(devices, 1, row_count), 0), axis=2
        ).reshape(-1)
        segments, depths = tree_layout(places)
        parents = lookup(parent[0], segments)
        grands = lookup(parent[0], parents)
        query_parts.append(jnp.stack([places, segments, parents, grands]).reshape(4, GROUPS, -1))
        slot_tables.append(rotation_tables(depths))
    query_info = jnp.concatenate(query_parts, axis=2).transpose(1, 0, 2)
    own_plan = plans[0].astype(bf16)
    att_picks, att_first, att_second = token_picks(att_routes, ATT_EXPERTS, att_capacity)
    att_gates = gate_values(hidden, att_router, att_first, att_second)
    ffn_picks, ffn_first, ffn_second = token_picks(ffn_routes, FFN_EXPERTS, ffn_capacity)
    prepared = (key_forward, key_backward, key_info, slot_tables, query_info, own_plan, att_picks, att_gates, ffn_picks)
    kv_gathered, prepared = lax.optimization_barrier((kv_gathered, prepared))
    kv_half = lax.dynamic_slice_in_dim(kv_gathered, core * 2 * piece, 2 * piece, 2).reshape(D, 2 * piece)
    kv_blocks, block_order = spread_over_replicas(kv_half, my_replica, replicas)
    hidden_all, kv_blocks = lax.optimization_barrier((hidden_all, kv_blocks))
    key_forward, key_backward, key_info, slot_tables, query_info, own_plan, att_picks, att_gates, ffn_picks = prepared

    queries, query_inputs = project_queries(own_plan, hidden_all, q_weight, slot_tables[0][0])
    keys_all, values_all = project_keys_values(hidden_all, kv_blocks, key_forward, block_order)

    def far_half(values):
        return lax.ppermute(
            lax.dynamic_slice_in_dim(values, (1 - core) * half, half, 1), "expert", pair
        )

    def join_halves(mine, sibling):
        other = lax.ppermute(sibling, "expert", pair)
        return jnp.where(
            core == 0,
            jnp.concatenate([mine, other], axis=1),
            jnp.concatenate([other, mine], axis=1),
        )

    heads = half // HEAD
    query_sets = [queries]
    starts = jnp.zeros((2,), jnp.int32)
    if att_copies == 1:
        query_sets.append(far_half(queries))
        starts = jnp.stack([core * heads, 0]).astype(jnp.int32)
    fused = devices == 8 and replicas == 4 and att_copies == 1 and ffn_copies == 2 and ffn_capacity % 16 == 0
    if fused:
        *att_outs, att_rows, att_back, lse = attention_send(
            *query_sets, keys_all, values_all, o_weight, key_info, query_info, att_capacity
        )
        att_everywhere = lax.all_gather(att_rows, "dp", axis=0, tiled=True)
    else:
        *att_outs, lse = attention_forward(
            query_sets, starts // 2, keys_all, values_all, key_info, query_info, heads
        )
        att_rows = join_halves(*att_outs) if att_copies == 1 else att_outs[0]
        att_partial = lax.dot_general(
            att_rows, o_weight, (((1,), (1,)), ((), ())), preferred_element_type=f32
        ).astype(bf16)
        att_back = exchange(att_partial.reshape(devices, att_capacity, D))
    if att_copies > 1:
        att_back = (
            att_back.astype(f32).reshape(ATT_EXPERTS, att_copies, att_capacity, D).sum(axis=1).astype(bf16)
        )
    att_branches = read_slots(att_picks, att_back)
    x_mid = x_in + att_gates[:, 0:1] * att_branches[0] + att_gates[:, 1:2] * att_branches[1]

    normed_two, inverse_two = rms_parts(x_mid)
    hidden_two = (normed_two * gain_two).astype(bf16)
    ffn_gates = gate_values(hidden_two, ffn_router, ffn_first, ffn_second)

    def to_experts(slots):
        rows = exchange(slots.reshape(devices, ffn_capacity // ffn_copies, D))
        return group_gather(rows.reshape(-1, D), ffn_copies, devices)

    def to_tokens(partial):
        rows = group_reduce(partial.astype(bf16), ffn_copies, devices)
        back = exchange(rows.reshape(devices, ffn_capacity // ffn_copies, D))
        return read_slots(ffn_picks, back.reshape(FFN_EXPERTS, ffn_capacity, D))

    ffn_slots = jnp.einsum(
        "ecr,rd->ecd", ffn_picks[0] + ffn_picks[1], hidden_two, preferred_element_type=f32
    ).astype(bf16)
    if fused:
        ffn_inputs, gate_pre, up_pre, activated, ffn_back = ffn_forward(
            ffn_slots, gate_weight, up_weight, down_weight
        )
        ffn_branches = read_slots(ffn_picks, ffn_back)
    else:
        ffn_inputs = to_experts(ffn_slots)
        gate_pre = jnp.dot(ffn_inputs, gate_weight, preferred_element_type=f32)
        up_pre = jnp.dot(ffn_inputs, up_weight, preferred_element_type=f32)
        sigmoid_gate = jax.nn.sigmoid(gate_pre)
        silu_gate = gate_pre * sigmoid_gate
        activated = (silu_gate * up_pre).astype(bf16)
        ffn_branches = to_tokens(
            lax.dot_general(
                activated, down_weight, (((1,), (1,)), ((), ())), preferred_element_type=f32
            )
        )
    result = x_mid + ffn_gates[:, 0:1] * ffn_branches[0] + ffn_gates[:, 1:2] * ffn_branches[1]

    tree_global = my_replica * parent.shape[0] + own_places // TREE_LEN
    tree_labels = jnp.arange(valid.shape[0], dtype=jnp.int32)
    limits = jnp.sum(
        jnp.where(tree_global[:, None] == tree_labels[None, :], valid[None, :], 0), axis=1
    )
    counted = own_places % TREE_LEN < limits
    loss_factor = valid.shape[0] * TREE_LEN / jnp.sum(valid).astype(f32)
    grad_result = jnp.where(counted[:, None], (result - teacher.astype(f32)) * loss_factor, 0.0)

    ffn_gate_grad, ffn_scaled = pair_grads(ffn_gates, ffn_branches, grad_result)
    ffn_grad_slots = fill_slots(ffn_picks, ffn_scaled)
    if fused:
        ffn_grad_slots, att_everywhere = lax.optimization_barrier((ffn_grad_slots, att_everywhere))
        grad_ffn_out, grad_down = send_rows(ffn_grad_slots, activated)
        grad_ffn_out = grad_ffn_out.reshape(-1, D)
    else:
        grad_ffn_out = to_experts(ffn_grad_slots)
        grad_down = dot_tn(grad_ffn_out, activated).astype(bf16)
    grad_ffn_out, grad_down = lax.optimization_barrier((grad_ffn_out, grad_down))
    summed_down = lax.psum_scatter(grad_down, "dp", scatter_dimension=0, tiled=True)
    if fused:
        grad_gate_pre, grad_up_pre, ffn_grad_back = ffn_backward(
            grad_ffn_out, gate_pre, up_pre, gate_weight, up_weight, down_weight, ffn_capacity
        )
        grad_gate = dot_tn(ffn_inputs, grad_gate_pre).astype(bf16)
        ffn_grad_back, grad_gate = lax.optimization_barrier((ffn_grad_back, grad_gate))
        ffn_grad_pair = read_slots(ffn_picks, ffn_grad_back)
    else:
        grad_activated = jnp.dot(grad_ffn_out, down_weight, preferred_element_type=f32)
        grad_gate_pre = (
            grad_activated * up_pre * sigmoid_gate * (1.0 + gate_pre * (1.0 - sigmoid_gate))
        ).astype(bf16)
        grad_up_pre = (grad_activated * silu_gate).astype(bf16)
        grad_ffn_in = lax.dot_general(
            grad_gate_pre, gate_weight, (((1,), (1,)), ((), ())), preferred_element_type=f32
        ) + lax.dot_general(
            grad_up_pre, up_weight, (((1,), (1,)), ((), ())), preferred_element_type=f32
        )
        grad_gate = dot_tn(ffn_inputs, grad_gate_pre).astype(bf16)
        ffn_grad_pair = to_tokens(grad_ffn_in)
    summed_gate = lax.psum_scatter(grad_gate, "dp", scatter_dimension=0, tiled=True)
    grad_ffn_router, hidden_two_extra = router_grads(
        hidden_two, ffn_router, ffn_gates, ffn_first, ffn_second, ffn_gate_grad
    )
    grad_hidden_two = ffn_grad_pair[0] + ffn_grad_pair[1] + hidden_two_extra
    grad_gain_two = jnp.sum(grad_hidden_two * normed_two, axis=0)
    grad_mid = grad_result + norm_back(grad_hidden_two * gain_two, normed_two, inverse_two)

    att_gate_grad, att_scaled = pair_grads(att_gates, att_branches, grad_mid)
    att_slots = fill_slots(att_picks, att_scaled)
    if att_copies > 1:
        att_slots = jnp.repeat(att_slots, att_copies, axis=0)
    att_slots, summed_down = lax.optimization_barrier((att_slots, summed_down))
    if fused:
        grad_att_out, grad_up = send_slots(att_slots, ffn_inputs, grad_up_pre)
        grad_att_out = grad_att_out.reshape(-1, D)
    else:
        grad_att_out = exchange(att_slots).reshape(-1, D)
        grad_up = dot_tn(ffn_inputs, grad_up_pre).astype(bf16)
        grad_att_out, grad_up = lax.optimization_barrier((grad_att_out, grad_up))
    summed_up = lax.psum_scatter(grad_up, "dp", scatter_dimension=0, tiled=True)
    grad_heads = jnp.dot(grad_att_out, o_weight, preferred_element_type=f32).astype(bf16)
    grad_heads, grad_att_out = lax.optimization_barrier((grad_heads, grad_att_out))
    grad_sets = [grad_heads]
    if att_copies == 1:
        grad_sets.append(far_half(grad_heads))
    if fused:
        share = D // replicas

        def columns_of(replica):
            return lax.dynamic_slice_in_dim(grad_att_out, replica * share, share, 1)

        grad_columns = [columns_of(my_replica)] + [
            lax.ppermute(columns_of(my_replica ^ n), "dp", [(i, i ^ n) for i in range(replicas)])
            for n in range(1, replicas)
        ]
    else:
        grad_o = dot_tn(grad_att_out, att_rows).astype(bf16)
        summed_o = lax.psum_scatter(grad_o, "dp", scatter_dimension=0, tiled=True).astype(f32)
    *grad_queries, grad_keys_values = attention_backward(
        query_sets,
        starts,
        grad_sets,
        att_outs,
        keys_all,
        values_all,
        lse,
        key_info,
        query_info,
        key_backward,
        [tables[1] for tables in slot_tables],
        heads,
    )
    grad_keys_values, summed_gate = lax.optimization_barrier((grad_keys_values, summed_gate))
    grad_query_pre = join_halves(*grad_queries) if att_copies == 1 else grad_queries[0]
    grad_kv = dot_tn(hidden_all.reshape(token_count, D), grad_keys_values).astype(bf16)
    grad_q = dot_tn(query_inputs, grad_query_pre).astype(bf16)
    summed_kv = lax.psum_scatter(grad_kv, "dp", scatter_dimension=0, tiled=True)
    summed_q = lax.psum_scatter(grad_q, "dp", scatter_dimension=0, tiled=True)
    grad_query_in = lax.dot_general(
        grad_query_pre, q_weight, (((1,), (1,)), ((), ())), preferred_element_type=f32
    ).astype(bf16)
    grad_query_in, grad_kv, grad_q, summed_up = lax.optimization_barrier(
        (grad_query_in, grad_kv, grad_q, summed_up)
    )

    merge_args = (
        own_plan.transpose(0, 2, 1),
        grad_query_in.reshape(devices, att_capacity, D),
        grad_keys_values,
        kv_blocks,
    )
    if fused:
        arrived = merge_return(*merge_args)
        arrived, grad_columns, summed_kv = lax.optimization_barrier((arrived, grad_columns, summed_kv))
        column_stack = jnp.stack(grad_columns)
        summed_o = dot_tn(
            jnp.concatenate(
                [lax.dynamic_index_in_dim(column_stack, my_replica ^ n, 0, False) for n in range(replicas)]
            ),
            att_everywhere,
        )
    else:
        merged = merge_hidden_grads(*merge_args, block_order).reshape(devices // 2, 2, row_count, D)
        kept = lax.dynamic_index_in_dim(merged, core, 1, keepdims=False)
        passed = lax.ppermute(
            lax.dynamic_index_in_dim(merged, 1 - core, 1, keepdims=False), "expert", pair
        )
        chip_sum = (kept.astype(f32) + passed.astype(f32)).astype(bf16)
        same_core = [[2 * i + c for i in range(devices // 2)] for c in range(2)]
        arrived = lax.all_to_all(
            chip_sum, "expert", split_axis=0, concat_axis=0, axis_index_groups=same_core, tiled=True
        )
    grad_att_router, hidden_one_extra = router_grads(
        hidden, att_router, att_gates, att_first, att_second, att_gate_grad
    )
    grad_hidden_one = jnp.sum(arrived.astype(f32), axis=0) + hidden_one_extra
    grad_gain_one = jnp.sum(grad_hidden_one * normed_one, axis=0)
    grad_input = grad_mid + norm_back(grad_hidden_one * gain_one, normed_one, inverse_one)

    everyone = devices * replicas
    smalls = [grad_gain_one, grad_gain_two, grad_att_router, grad_ffn_router]
    packed = jnp.concatenate([small.reshape(everyone, -1) for small in smalls], axis=1)
    packed, summed_o = lax.optimization_barrier((packed, summed_o))
    kv_exchange = swap_blocks if fused else exchange
    kv_rows = kv_exchange(summed_kv.reshape(devices, -1, 2 * half))
    own_smalls = jnp.sum(
        lax.all_to_all(packed, ("dp", "expert"), split_axis=0, concat_axis=0, tiled=True), axis=0
    )
    own_smalls, kv_rows, summed_q = lax.optimization_barrier((own_smalls, kv_rows, summed_q))
    share = D // everyone
    shared_gain_one = own_smalls[:share]
    shared_gain_two = own_smalls[share : 2 * share]
    shared_att_router = own_smalls[2 * share : (2 + ATT_EXPERTS) * share].reshape(share, ATT_EXPERTS)
    shared_ffn_router = own_smalls[(2 + ATT_EXPERTS) * share :].reshape(share, FFN_EXPERTS)

    kv_sum = jnp.sum(kv_rows.astype(f32).reshape(devices // 2, 2, -1, 2 * half), axis=0)
    shared_kv = jnp.concatenate(
        [kv_sum[n, :, m * half : (m + 1) * half] for m in range(2) for n in range(2)], axis=1
    )

    return (
        result.astype(bf16),
        grad_input.astype(bf16),
        shared_gain_one,
        shared_kv,
        shared_att_router,
        summed_q.astype(f32),
        summed_o,
        shared_gain_two,
        shared_ffn_router,
        summed_gate.astype(f32),
        summed_up.astype(f32),
        summed_down.astype(f32),
    )


def solution(mesh):
    in_specs = (
        P(("dp", "expert"), None),
        P(("dp", "expert"), None),
        P(("dp", "expert"), None),
        P(("dp", "expert"), None),
        P("dp", None),
        P(),
        P(),
        P("expert", None),
        P(),
        P(None, "expert"),
        P(None, "expert"),
        P(),
        P(),
        P(None, "expert"),
        P(None, "expert"),
        P(None, "expert"),
    )
    out_specs = (
        P(("dp", "expert"), None),
        P(("dp", "expert"), None),
        P(("dp", "expert")),
        P(("dp", "expert"), None),
        P(("dp", "expert"), None),
        P("dp", "expert"),
        P("dp", "expert"),
        P(("dp", "expert")),
        P(("dp", "expert"), None),
        P("dp", "expert"),
        P("dp", "expert"),
        P("dp", "expert"),
    )
    return jax.shard_map(body, mesh=mesh, in_specs=in_specs, out_specs=out_specs, check_vma=False)
```

```python
import functools
import jax
import jax.numpy as jnp
from jax import lax
from jax.experimental import pallas as pl
from jax.experimental.pallas import tpu as pltpu
from jax.sharding import PartitionSpec as P

HEAD = 128
GROUPS = 4
LOG2E = 1.4426950408889634
VMEM_BYTES = 60 * 1024 * 1024


def dot_nt(left, right):
    return lax.dot_general(left, right, (((1,), (1,)), ((), ())), preferred_element_type=jnp.float32)


def dot_nn(left, right):
    return jnp.dot(left, right, preferred_element_type=jnp.float32)


def spin(values, cosine, sine):
    return values * cosine + pltpu.roll(values, HEAD // 2, 1) * sine


def fill_bias(bias_ref, key_ref, query_ref, keys):
    for group in range(GROUPS):
        place = query_ref[group, 0:1, :]
        own, parent, grand = (query_ref[group, 1 + n : 2 + n, :] for n in range(3))

        def one(block, carry, group=group, place=place, own=own, parent=parent, grand=grand):
            at = pl.multiple_of(block * keys, 16)
            key_place = key_ref[pl.ds(at, keys), 0:1]
            key_segment = key_ref[pl.ds(at, keys), 1:2]
            related = (key_segment == own) | (key_segment == parent) | (key_segment == grand)
            allowed = related & (key_place <= place)
            bias_ref[group * (group + 1) // 2 + block] = jnp.where(allowed, 0.0, -1e30)
            return carry

        lax.fori_loop(0, group + 1, one, 0)


def group_rows(refs, group, rows, lanes):
    parts = [ref[pl.ds(group * rows, rows), lanes] for ref in refs]
    return parts[0] if len(parts) == 1 else jnp.concatenate(parts, axis=0)


def attention_forward_body(sets, step_heads, rows, keys, scale, first_ref, *refs):
    query_refs = refs[:sets]
    key_ref, value_ref, key_info, query_info = refs[sets : sets + 4]
    out_refs = refs[sets + 4 : 2 * sets + 4]
    lse_ref, bias_ref, flipped_ref = refs[2 * sets + 4 :]
    wide = sets * rows

    @pl.when(pl.program_id(0) == 0)
    def _():
        fill_bias(bias_ref, key_info, query_info, keys)

    for head in range(step_heads):
        lanes = pl.ds(head * HEAD, HEAD)
        for block in range(GROUPS):
            values = value_ref[pl.ds(block * keys, keys), lanes].astype(jnp.float32)
            flipped_ref[head, block] = values.T.astype(jnp.bfloat16)
    for group in range(GROUPS):
        queries = [
            group_rows(query_refs, group, rows, pl.ds(head * HEAD, HEAD)) for head in range(step_heads)
        ]

        def one(block, carry, group=group, queries=queries):
            at = pl.multiple_of(block * keys, 16)
            bias = bias_ref[group * (group + 1) // 2 + block]
            result = []
            for head in range(step_heads):
                top, total, mixed = carry[3 * head : 3 * head + 3]
                scores = dot_nt(key_ref[pl.ds(at, keys), pl.ds(head * HEAD, HEAD)], queries[head])
                scores = scores * scale + bias
                new_top = jnp.maximum(top, jnp.max(scores, axis=0, keepdims=True))
                fade = jnp.exp2(top - new_top)
                parts = jnp.exp2(scores - new_top)
                total = total * fade + jnp.sum(parts, axis=0, keepdims=True)
                mixed = mixed * fade + dot_nn(flipped_ref[head, block], parts.astype(jnp.bfloat16))
                result += [new_top, total, mixed]
            return tuple(result)

        start = (
            jnp.full((1, wide), -1e30, jnp.float32),
            jnp.zeros((1, wide), jnp.float32),
            jnp.zeros((HEAD, wide), jnp.float32),
        ) * step_heads
        final = lax.fori_loop(0, group + 1, one, start)
        for head in range(step_heads):
            top, total, mixed = final[3 * head : 3 * head + 3]
            lse_ref[head, group] = top + jnp.log2(total)
            rows_out = (mixed / total).T.astype(jnp.bfloat16)
            for n, ref in enumerate(out_refs):
                ref[pl.ds(group * rows, rows), pl.ds(head * HEAD, HEAD)] = rows_out[
                    n * rows : (n + 1) * rows
                ]


def attention_backward_body(sets, step_heads, rows, keys, scale, first_ref, *refs):
    query_refs, grad_refs, out_refs = (refs[n * sets : (n + 1) * sets] for n in range(3))
    key_ref, value_ref, lse_ref, key_info, query_info = refs[3 * sets : 3 * sets + 5]
    key_cos, key_sin = refs[3 * sets + 5 : 3 * sets + 7]
    table_refs = refs[3 * sets + 7 : 5 * sets + 7]
    rest = refs[5 * sets + 7 :]
    dq_refs = rest[:sets]
    dkv_ref, bias_ref, flipped_ref, dk_acc, dv_acc = rest[sets:]
    half = dkv_ref.shape[1] // 2
    softmax_scale = scale / LOG2E

    @pl.when(pl.program_id(0) == 0)
    def _():
        fill_bias(bias_ref, key_info, query_info, keys)

    dk_acc[...] = jnp.zeros_like(dk_acc)
    dv_acc[...] = jnp.zeros_like(dv_acc)
    for head in range(step_heads):
        lanes = pl.ds(head * HEAD, HEAD)
        for block in range(GROUPS):
            values = key_ref[pl.ds(block * keys, keys), lanes].astype(jnp.float32)
            flipped_ref[head, block] = values.T.astype(jnp.bfloat16)
    for group in range(GROUPS):
        queries, grads, centres, tops = [], [], [], []
        for head in range(step_heads):
            lanes = pl.ds(head * HEAD, HEAD)
            queries.append(group_rows(query_refs, group, rows, lanes))
            grad = group_rows(grad_refs, group, rows, lanes)
            out = group_rows(out_refs, group, rows, lanes)
            product = grad.astype(jnp.float32) * out.astype(jnp.float32)
            centres.append(jnp.sum(product.T, axis=0, keepdims=True))
            grads.append(grad)
            tops.append(lse_ref[head, group])

        def one(block, carry, group=group, queries=queries, grads=grads, centres=centres, tops=tops):
            at = pl.multiple_of(block * keys, 16)
            bias = bias_ref[group * (group + 1) // 2 + block]
            result = []
            for head in range(step_heads):
                lanes = pl.ds(head * HEAD, HEAD)
                key_rows = key_ref[pl.ds(at, keys), lanes]
                scores = dot_nt(key_rows, queries[head])
                probs = jnp.exp2(scores * scale + (bias - tops[head]))
                grad_probs = dot_nt(value_ref[pl.ds(at, keys), lanes], grads[head])
                grad_scores = (probs * (grad_probs - centres[head])).astype(jnp.bfloat16)
                dv_acc[pl.ds(at, keys), lanes] += dot_nn(probs.astype(jnp.bfloat16), grads[head])
                dk_acc[pl.ds(at, keys), lanes] += dot_nn(grad_scores, queries[head])
                result.append(carry[head] + dot_nn(flipped_ref[head, block], grad_scores))
            return tuple(result)

        start = (jnp.zeros((HEAD, sets * rows), jnp.float32),) * step_heads
        final = lax.fori_loop(0, group + 1, one, start)
        for head in range(step_heads):
            dq = final[head].T * softmax_scale
            for n, ref in enumerate(dq_refs):
                span = pl.ds(group * rows, rows)
                turned = spin(
                    dq[n * rows : (n + 1) * rows], table_refs[2 * n][span, :], table_refs[2 * n + 1][span, :]
                )
                ref[span, pl.ds(head * HEAD, HEAD)] = turned.astype(jnp.bfloat16)
    for head in range(step_heads):
        lanes = pl.ds(head * HEAD, HEAD)
        first_lane = pl.multiple_of((pl.program_id(0) * step_heads + head) * HEAD, HEAD)
        for block in range(GROUPS):
            span = pl.ds(block * keys, keys)
            turned = spin(dk_acc[span, lanes] * softmax_scale, key_cos[span, :], key_sin[span, :])
            dkv_ref[span, pl.ds(first_lane, HEAD)] = turned.astype(jnp.bfloat16)
            dkv_ref[span, pl.ds(half + first_lane, HEAD)] = dv_acc[span, lanes].astype(jnp.bfloat16)


def whole_block(shape):
    return pl.BlockSpec(shape, lambda h, first: (0,) * len(shape))


def attention_forward(queries, starts, keys_all, values_all, key_info, query_info, heads):
    sets, total_rows, tokens = len(queries), queries[0].shape[0], keys_all.shape[0]
    rows, keys = total_rows // GROUPS, tokens // GROUPS
    step_heads = 2
    wide = step_heads * HEAD
    scale = HEAD ** (-0.5) * LOG2E
    query_specs = [
        pl.BlockSpec((total_rows, wide), lambda h, first, n=n: (0, first[n] + h)) for n in range(sets)
    ]
    plain = pl.BlockSpec((total_rows, wide), lambda h, first: (0, h))
    side = pl.BlockSpec((tokens, wide), lambda h, first: (0, h))
    return pl.pallas_call(
        functools.partial(attention_forward_body, sets, step_heads, rows, keys, scale),
        grid_spec=pltpu.PrefetchScalarGridSpec(
            num_scalar_prefetch=1,
            grid=(heads // step_heads,),
            in_specs=query_specs
            + [side, side, whole_block(key_info.shape), whole_block(query_info.shape)],
            out_specs=[plain] * sets
            + [pl.BlockSpec((step_heads, GROUPS, 1, sets * rows), lambda h, first: (h, 0, 0, 0))],
            scratch_shapes=[
                pltpu.VMEM((GROUPS * (GROUPS + 1) // 2, keys, sets * rows), jnp.float32),
                pltpu.VMEM((step_heads, GROUPS, HEAD, keys), jnp.bfloat16),
            ],
        ),
        out_shape=[jax.ShapeDtypeStruct((total_rows, heads * HEAD), jnp.bfloat16)] * sets
        + [jax.ShapeDtypeStruct((heads, GROUPS, 1, sets * rows), jnp.float32)],
        compiler_params=pltpu.CompilerParams(vmem_limit_bytes=VMEM_BYTES),
        name="attention_forward",
    )(starts, *queries, keys_all, values_all, key_info, query_info)


def attention_backward(
    queries, starts, grads, outs, keys_all, values_all, lse, key_info, query_info, key_tables, row_tables, heads
):
    sets, total_rows, tokens = len(queries), queries[0].shape[0], keys_all.shape[0]
    rows, keys = total_rows // GROUPS, tokens // GROUPS
    step_heads = 1
    wide = step_heads * HEAD
    scale = HEAD ** (-0.5) * LOG2E
    shifted = [
        pl.BlockSpec((total_rows, wide), lambda h, first, n=n: (0, first[n] + h)) for n in range(sets)
    ]
    plain = pl.BlockSpec((total_rows, wide), lambda h, first: (0, h))
    side = pl.BlockSpec((tokens, wide), lambda h, first: (0, h))
    return pl.pallas_call(
        functools.partial(attention_backward_body, sets, step_heads, rows, keys, scale),
        grid_spec=pltpu.PrefetchScalarGridSpec(
            num_scalar_prefetch=1,
            grid=(heads // step_heads,),
            in_specs=shifted
            + shifted
            + [plain] * sets
            + [
                side,
                side,
                pl.BlockSpec((step_heads, GROUPS, 1, sets * rows), lambda h, first: (h, 0, 0, 0)),
                whole_block(key_info.shape),
                whole_block(query_info.shape),
                whole_block((tokens, HEAD)),
                whole_block((tokens, HEAD)),
            ]
            + [whole_block((total_rows, HEAD))] * (2 * sets),
            out_specs=[plain] * sets + [whole_block((tokens, 2 * heads * HEAD))],
            scratch_shapes=[
                pltpu.VMEM((GROUPS * (GROUPS + 1) // 2, keys, sets * rows), jnp.float32),
                pltpu.VMEM((step_heads, GROUPS, HEAD, keys), jnp.bfloat16),
                pltpu.VMEM((tokens, wide), jnp.float32),
                pltpu.VMEM((tokens, wide), jnp.float32),
            ],
        ),
        out_shape=[jax.ShapeDtypeStruct((total_rows, heads * HEAD), jnp.bfloat16)] * sets
        + [jax.ShapeDtypeStruct((tokens, 2 * heads * HEAD), jnp.bfloat16)],
        compiler_params=pltpu.CompilerParams(vmem_limit_bytes=VMEM_BYTES),
        name="attention_backward",
    )(
        starts,
        *queries,
        *grads,
        *outs,
        keys_all,
        values_all,
        lse,
        key_info,
        query_info,
        *key_tables,
        *[table for pair in row_tables for table in pair],
    )


def project_body(plan_ref, hidden_ref, weight_ref, cos_ref, sin_ref, out_ref, x_ref):
    sources, capacity = plan_ref.shape[0], plan_ref.shape[1]
    bundle = max(1, sources * capacity // GROUPS // capacity)
    tile = bundle * capacity

    @pl.when(pl.program_id(0) == 0)
    def _():
        for group in range(sources // bundle):
            parts = [
                dot_nn(plan_ref[group * bundle + n], hidden_ref[group * bundle + n]) for n in range(bundle)
            ]
            x_ref[pl.ds(group * tile, tile), :] = jnp.concatenate(parts, axis=0).astype(jnp.bfloat16)

    for at in range(0, x_ref.shape[0], tile):
        span = pl.ds(at, tile)
        product = dot_nn(x_ref[span, :], weight_ref[...])
        for lane in range(0, out_ref.shape[1], HEAD):
            turned = spin(product[:, lane : lane + HEAD], cos_ref[span, :], sin_ref[span, :])
            out_ref[span, lane : lane + HEAD] = turned.astype(jnp.bfloat16)


def project_queries(plan, hidden, weight, tables):
    sources, capacity, row_count = plan.shape
    depth, columns = weight.shape
    rows = sources * capacity
    block = 512
    return pl.pallas_call(
        project_body,
        grid=(columns // block,),
        in_specs=[
            pl.BlockSpec((sources, capacity, row_count), lambda j: (0, 0, 0)),
            pl.BlockSpec((sources, row_count, depth), lambda j: (0, 0, 0)),
            pl.BlockSpec((depth, block), lambda j: (0, j)),
            pl.BlockSpec((rows, HEAD), lambda j: (0, 0)),
            pl.BlockSpec((rows, HEAD), lambda j: (0, 0)),
        ],
        out_specs=[
            pl.BlockSpec((rows, block), lambda j: (0, j)),
            pl.BlockSpec((rows, depth), lambda j: (0, 0)),
        ],
        out_shape=[
            jax.ShapeDtypeStruct((rows, columns), jnp.bfloat16),
            jax.ShapeDtypeStruct((rows, depth), jnp.bfloat16),
        ],
        compiler_params=pltpu.CompilerParams(vmem_limit_bytes=VMEM_BYTES),
        name="project_queries",
    )(plan, hidden, weight, *tables)


def keys_values_body(half, order_ref, x_ref, weight_ref, cos_ref, sin_ref, key_ref, value_ref):
    rows = x_ref.shape[1]
    for source in range(x_ref.shape[0]):
        span = pl.ds(source * rows, rows)
        product = dot_nn(x_ref[source], weight_ref[0])
        for lane in range(0, half, HEAD):
            turned = spin(product[:, lane : lane + HEAD], cos_ref[span, :], sin_ref[span, :])
            key_ref[span, lane : lane + HEAD] = turned.astype(jnp.bfloat16)
        value_ref[span, :] = product[:, half:].astype(jnp.bfloat16)


def project_keys_values(hidden, weights, tables, order):
    sources, rows, unused = hidden.shape
    parts, depth, columns = weights.shape
    half, tokens = columns // 2, sources * rows
    return pl.pallas_call(
        functools.partial(keys_values_body, half),
        grid_spec=pltpu.PrefetchScalarGridSpec(
            num_scalar_prefetch=1,
            grid=(parts,),
            in_specs=[
                pl.BlockSpec((sources, rows, depth), lambda j, order: (0, 0, 0)),
                pl.BlockSpec((1, depth, columns), lambda j, order: (j, 0, 0)),
                pl.BlockSpec((tokens, HEAD), lambda j, order: (0, 0)),
                pl.BlockSpec((tokens, HEAD), lambda j, order: (0, 0)),
            ],
            out_specs=[pl.BlockSpec((tokens, half), lambda j, order: (0, order[j]))] * 2,
        ),
        out_shape=[jax.ShapeDtypeStruct((tokens, parts * half), jnp.bfloat16)] * 2,
        compiler_params=pltpu.CompilerParams(vmem_limit_bytes=VMEM_BYTES),
        name="project_keys_values",
    )(order, hidden, weights, *tables)


def merge_body(tile, order_ref, plan_ref, slots_ref, dk_ref, dv_ref, weight_ref, out_ref, acc_ref):
    part = pl.program_id(1)
    sources, rows = plan_ref.shape[0], plan_ref.shape[1]
    ck = dk_ref.shape[1]

    @pl.when(part == 0)
    def _():
        for source in range(sources):
            acc_ref[pl.ds(source * rows, rows), :] = dot_nn(plan_ref[source], slots_ref[source])

    last = part == pl.num_programs(1) - 1
    for at in range(0, acc_ref.shape[0], tile):
        span = pl.ds(at, tile)
        acc_ref[span, :] += dot_nt(dk_ref[span, :], weight_ref[0, :, :ck]) + dot_nt(
            dv_ref[span, :], weight_ref[0, :, ck:]
        )

    @pl.when(last)
    def _():
        out_ref[...] = acc_ref[...].astype(jnp.bfloat16)


def merge_hidden_grads(plan, slots, grads, weights, order):
    sources, rows, capacity = plan.shape
    parts, depth, columns = weights.shape
    ck, tokens = columns // 2, sources * rows
    wide = depth // 2
    return pl.pallas_call(
        functools.partial(merge_body, tokens // GROUPS),
        grid_spec=pltpu.PrefetchScalarGridSpec(
            num_scalar_prefetch=1,
            grid=(2, parts),
            in_specs=[
                pl.BlockSpec((sources, rows, capacity), lambda i, j, order: (0, 0, 0)),
                pl.BlockSpec((sources, capacity, wide), lambda i, j, order: (0, 0, i)),
                pl.BlockSpec((tokens, ck), lambda i, j, order: (0, order[j])),
                pl.BlockSpec((tokens, ck), lambda i, j, order: (0, parts + order[j])),
                pl.BlockSpec((1, wide, columns), lambda i, j, order: (j, i, 0)),
            ],
            out_specs=pl.BlockSpec((tokens, wide), lambda i, j, order: (0, i)),
            scratch_shapes=[pltpu.VMEM((tokens, wide), jnp.float32)],
        ),
        out_shape=jax.ShapeDtypeStruct((tokens, depth), jnp.bfloat16),
        compiler_params=pltpu.CompilerParams(vmem_limit_bytes=VMEM_BYTES),
        name="merge_hidden_grads",
    )(order, plan, slots, grads, grads, weights)


def mesh_device(index):
    return {"expert": index}


def chip_order(chip, step):
    flip = chip // 2
    near = chip + flip * (3 - 2 * chip)
    place = step + near * (1 - 2 * step) if step < 2 else step
    return place + flip * (3 - 2 * place)


def far_order(chip, step):
    return chip_order(chip, 3 - step)


def is_middle(chip):
    flip = chip // 2
    return chip + flip * (3 - 2 * chip)


def crossing_order(chip, step):
    end, middle = chip_order(chip, step), chip_order(chip, (2, 3, 1, 0)[step])
    return end + is_middle(chip) * (middle - end)


def enter(devices, me):
    barrier = pltpu.get_barrier_semaphore()
    for step in range(1, devices):
        pl.semaphore_signal(
            barrier,
            inc=1,
            device_id=mesh_device(lax.rem(me + step, devices)),
            device_id_type=pl.DeviceIdType.MESH,
        )
    pl.semaphore_wait(barrier, devices - 1)


def remote(source, target, send, recv, device):
    return pltpu.make_async_remote_copy(
        src_ref=source,
        dst_ref=target,
        send_sem=send,
        recv_sem=recv,
        device_id=mesh_device(device),
        device_id_type=pl.DeviceIdType.MESH,
    )


class Dispatch:
    def __init__(self, me, order, slots, landing, local_sem, send, recv, pass_send, pass_recv):
        self.me, self.chip, self.core, self.order = me, me // 2, lax.rem(me, 2), order
        self.sending = stagger_order if order is stagger_order else chip_order
        self.slots, self.landing = slots, landing
        self.local_sem, self.send, self.recv = local_sem, send, recv
        self.pass_send, self.pass_recv = pass_send, pass_recv
        self.rows, self.half = slots.shape[1], slots.shape[2] // 2

    def columns(self, core):
        return pl.ds(pl.multiple_of(core * self.half, 128), self.half)

    def place(self, source, core):
        rows = pl.ds(pl.multiple_of(lax.rem(source, 2) * self.rows, 16), self.rows)
        return self.landing.at[source // 2, rows, self.columns(core)]

    def direct(self, target):
        core = lax.rem(target, 2)
        offset = lax.rem(target - self.me + 8, 8)
        return remote(
            self.slots.at[target // 2, :, self.columns(core)],
            self.place(self.me, core),
            self.send.at[offset],
            self.recv.at[offset],
            target,
        )

    def sends(self, step):
        chip = self.sending(self.chip, step)
        targets = [2 * chip + self.core, 2 * chip + 1 - self.core] if step else [self.me + 1 - 2 * self.core]
        return [self.direct(target) for target in targets]

    def local(self):
        return pltpu.make_async_copy(
            self.slots.at[self.chip, :, self.columns(self.core)],
            self.place(self.me, self.core),
            self.local_sem,
        )

    def start_local(self):
        self.local().start()

    def start(self, steps):
        for step in steps:
            for copy in self.sends(step):
                copy.start()

    def sent(self, steps):
        for step in steps:
            for copy in self.sends(step):
                copy.wait_send()

    def pass_on(self, source):
        place = self.place(source, self.core)
        return remote(
            place, place, self.pass_send.at[source], self.pass_recv.at[source], self.me + 1 - 2 * self.core
        )

    def arrive(self, step):
        chip = self.order(self.chip, step)
        for source in (2 * chip, 2 * chip + 1):
            offset = lax.rem(self.me - source + 8, 8)

            @pl.when(offset == 0)
            def _():
                self.local().wait()

            @pl.when(offset != 0)
            def _(source=source, offset=offset):
                place = self.place(source, self.core)
                remote(place, place, self.send.at[offset], self.recv.at[offset], self.me).wait_recv()

            self.pass_on(source).start()

    def ready(self, step):
        chip = self.order(self.chip, step)
        for source in (2 * chip, 2 * chip + 1):
            place = self.place(source, 1 - self.core)
            remote(
                place, place, self.pass_send.at[source], self.pass_recv.at[source], self.me
            ).wait_recv()
        return chip

    def passed_on(self):
        for source in range(8):
            self.pass_on(source).wait_send()


class Collect:
    def __init__(
        self, me, order, own_steps, kept, passing, passed, total, back, local_sem, pass_send, pass_recv, send, recv
    ):
        self.me, self.chip, self.core = me, me // 2, lax.rem(me, 2)
        self.order, self.own_steps = order, own_steps
        self.kept, self.passing, self.passed, self.total, self.back = kept, passing, passed, total, back
        self.local_sem, self.pass_send, self.pass_recv = local_sem, pass_send, pass_recv
        self.send, self.recv = send, recv
        self.rows, self.half = back.shape[1], back.shape[2] // 2

    def swap(self, step):
        return remote(
            self.passing.at[step % 2],
            self.passed.at[step],
            self.pass_send.at[step],
            self.pass_recv.at[step],
            self.me + 1 - 2 * self.core,
        )

    def place(self, chip, core):
        return self.back.at[chip, :, pl.ds(pl.multiple_of(core * self.half, 128), self.half)]

    def local(self, step, source_core):
        return pltpu.make_async_copy(
            self.total.at[step, pl.ds(pl.multiple_of(source_core * self.rows, 16), self.rows), :],
            self.place(self.chip, self.core),
            self.local_sem,
        )

    def outgoing(self, step, source):
        rows = pl.ds(pl.multiple_of(lax.rem(source, 2) * self.rows, 16), self.rows)
        offset = lax.rem(source - self.me + 8, 8)
        return remote(
            self.total.at[step, rows, :],
            self.place(self.chip, self.core),
            self.send.at[offset],
            self.recv.at[offset],
            source,
        )

    def block(self, step):
        return self.order(self.chip, step)

    def each(self, step, own, other):
        chip = self.block(step)
        for source in (2 * chip + self.core, 2 * chip + 1 - self.core):
            if step not in self.own_steps:
                other(source)
                continue

            @pl.when(source == self.me)
            def _():
                own()

            @pl.when(source != self.me)
            def _(source=source):
                other(source)

    def settle(self, step):
        self.swap(step).wait_recv()
        tile = 2 * self.rows // 4
        for at in range(0, 2 * self.rows, tile):
            span = pl.ds(at, tile)
            summed = self.kept[span, :] + self.passed[step, span, :].astype(jnp.float32)
            self.total[step, span, :] = summed.astype(jnp.bfloat16)
        self.each(
            step,
            lambda: self.local(step, self.core).start(),
            lambda source: self.outgoing(step, source).start(),
        )

    def finish(self):
        for step in range(4):
            if step >= 2:
                self.swap(step).wait_send()
            self.each(
                step,
                lambda step=step: self.local(step, self.core).wait(),
                lambda source, step=step: self.outgoing(step, source).wait_send(),
            )
        for offset in range(1, 8):
            source = lax.rem(self.me + 8 - offset, 8)
            place = self.place(source // 2, lax.rem(source, 2))
            remote(place, place, self.send.at[offset], self.recv.at[offset], self.me).wait_recv()


def ffn_forward_body(
    chunk,
    slots,
    gate_hbm,
    up_hbm,
    down_hbm,
    rows_out,
    gate_out,
    up_out,
    act_out,
    back,
    gate,
    up,
    down,
    landing,
    pre_stage,
    act,
    kept,
    passing,
    passed,
    total,
    weight_sem,
    stage_sem,
    act_sem,
    rows_sem,
    local_sem,
    send,
    recv,
    pass_send,
    pass_recv,
    swap_send,
    swap_recv,
    out_send,
    out_recv,
):
    me = lax.axis_index("expert")
    enter(8, me)
    loads = [
        pltpu.make_async_copy(source, target, weight_sem.at[n])
        for n, (source, target) in enumerate(((gate_hbm, gate), (up_hbm, up), (down_hbm, down)))
    ]
    dispatch = Dispatch(me, crossing_order, slots, landing, local_sem.at[0], send, recv, pass_send, pass_recv)
    collect = Collect(
        me, crossing_order, (0, 3), kept, passing, passed, total, back, local_sem.at[1], swap_send, swap_recv, out_send, out_recv
    )
    middle = is_middle(me // 2)
    dispatch.start_local()
    dispatch.start((0, 1))

    @pl.when(middle == 1)
    def _():
        dispatch.start((2,))

    for load in loads:
        load.start()
    block = landing.shape[1]
    hidden_units = gate.shape[1]
    chunks = hidden_units // chunk
    half = back.shape[2] // 2

    def stage_copies(chip, part, slot):
        span = pl.ds(pl.multiple_of(chip * block, 16), block)
        columns = pl.ds(pl.multiple_of(part * chunk, 128), chunk)
        return [
            pltpu.make_async_copy(
                pre_stage.at[slot, n], out.at[span, columns], stage_sem.at[slot, n]
            )
            for n, out in enumerate((gate_out, up_out))
        ]

    def act_copy(chip, step):
        span = pl.ds(pl.multiple_of(chip * block, 16), block)
        return pltpu.make_async_copy(act.at[step % 2], act_out.at[span, :], act_sem.at[step % 2])

    def rows_copy(chip, step):
        span = pl.ds(pl.multiple_of(chip * block, 16), block)
        return pltpu.make_async_copy(landing.at[chip], rows_out.at[span, :], rows_sem.at[step])

    for step in range(4):
        if step == 0:
            dispatch.arrive(0)
        chip = dispatch.ready(step)
        rows_copy(chip, step).start()
        if step == 0:
            loads[0].wait()
            loads[1].wait()
        if step >= 2:
            act_copy(crossing_order(me // 2, step - 2), step - 2).wait()

        def hidden_part(part, carry, chip=chip, step=step):
            slot = lax.rem(part + step * chunks, 2)
            columns = pl.ds(pl.multiple_of(part * chunk, 128), chunk)

            @pl.when(part + step * chunks >= 2)
            def _():
                for copy in stage_copies(chip, part, slot):
                    copy.wait()

            gated = dot_nn(landing[chip], gate[:, columns])
            raised = dot_nn(landing[chip], up[:, columns])
            pre_stage[slot, 0] = gated.astype(jnp.bfloat16)
            pre_stage[slot, 1] = raised.astype(jnp.bfloat16)
            act[step % 2, :, columns] = (gated * jax.nn.sigmoid(gated) * raised).astype(jnp.bfloat16)
            for copy in stage_copies(chip, part, slot):
                copy.start()
            if step == 0:
                @pl.when((part == chunks // 3) & (middle == 0))
                def _():
                    dispatch.sent((1,))
                    dispatch.start((2,))

                @pl.when((part == chunks // 2) & (middle == 1))
                def _():
                    dispatch.sent((1, 2))
                    dispatch.start((3,))

            return carry

        lax.fori_loop(0, chunks, hidden_part, 0)
        act_copy(chip, step).start()
        if step == 0:
            loads[2].wait()
        else:
            collect.settle(step - 1)
        core = collect.core
        width = min(512, half)

        def far_part(part, carry, step=step):
            at = pl.multiple_of((1 - core) * half + part * width, 128)
            product = dot_nt(act[step % 2], down[pl.ds(at, width), :])
            passing[step % 2, :, pl.ds(pl.multiple_of(part * width, 128), width)] = product.astype(jnp.bfloat16)
            return carry

        def near_part(part, carry, step=step):
            at = pl.multiple_of(core * half + part * width, 128)
            product = dot_nt(act[step % 2], down[pl.ds(at, width), :])
            kept[:, pl.ds(pl.multiple_of(part * width, 128), width)] = product
            return carry

        if step >= 2:
            collect.swap(step - 2).wait_send()
        lax.fori_loop(0, half // width, far_part, 0)
        collect.swap(step).start()
        if step == 0:

            @pl.when(middle == 0)
            def _():
                dispatch.sent((2,))
                dispatch.start((3,))

        if step < 3:
            dispatch.arrive(step + 1)
        lax.fori_loop(0, half // width, near_part, 0)
    collect.settle(3)
    for step in (2, 3):
        act_copy(crossing_order(me // 2, step), step).wait()
    for step in range(4):
        rows_copy(crossing_order(me // 2, step), step).wait()
    for slot in range(2):
        for copy in stage_copies(0, 0, slot):
            copy.wait()
    dispatch.sent((0, 3))
    dispatch.passed_on()
    collect.finish()


def ffn_forward(slots, gate_weight, up_weight, down_weight):
    chips, capacity, depth = slots.shape
    hidden_units = gate_weight.shape[1]
    block = 2 * capacity
    chunk = 256 if hidden_units % 256 == 0 else 128
    half = depth // 2
    rows = chips * block
    any_space = pl.BlockSpec(memory_space=pl.ANY)
    bf = jnp.bfloat16
    dma = pltpu.SemaphoreType.DMA
    return pl.pallas_call(
        functools.partial(ffn_forward_body, chunk),
        in_specs=[any_space] * 4,
        out_specs=[any_space] * 5,
        out_shape=[
            jax.ShapeDtypeStruct((rows, depth), bf),
            jax.ShapeDtypeStruct((rows, hidden_units), bf),
            jax.ShapeDtypeStruct((rows, hidden_units), bf),
            jax.ShapeDtypeStruct((rows, hidden_units), bf),
            jax.ShapeDtypeStruct((chips, capacity, depth), bf),
        ],
        scratch_shapes=[
            pltpu.VMEM((depth, hidden_units), bf),
            pltpu.VMEM((depth, hidden_units), bf),
            pltpu.VMEM((depth, hidden_units), bf),
            pltpu.VMEM((chips, block, depth), bf),
            pltpu.VMEM((2, 2, block, chunk), bf),
            pltpu.VMEM((2, block, hidden_units), bf),
            pltpu.VMEM((block, half), jnp.float32),
            pltpu.VMEM((2, block, half), bf),
            pltpu.VMEM((chips, block, half), bf),
            pltpu.VMEM((chips, block, half), bf),
            dma((3,)),
            dma((2, 2)),
            dma((2,)),
            dma((4,)),
            dma((2,)),
            dma((8,)),
            dma((8,)),
            dma((8,)),
            dma((8,)),
            dma((4,)),
            dma((4,)),
            dma((8,)),
            dma((8,)),
        ],
        compiler_params=pltpu.CompilerParams(
            collective_id=1, has_side_effects=True, vmem_limit_bytes=VMEM_BYTES
        ),
        name="ffn_forward",
    )(slots, gate_weight, up_weight, down_weight)


def stagger_order(chip, step):
    if step < 2:
        return chip_order(chip, step)
    end, middle = chip_order(chip, 5 - step), chip_order(chip, step)
    return end + is_middle(chip) * (middle - end)


def send_rows_body(
    slots,
    act_hbm,
    rows_out,
    grad_out,
    landing,
    act,
    total,
    stage,
    act_sem,
    rows_sem,
    stage_sem,
    local_sem,
    send,
    recv,
    pass_send,
    pass_recv,
):
    me = lax.axis_index("expert")
    enter(8, me)
    dispatch = Dispatch(me, stagger_order, slots, landing, local_sem.at[0], send, recv, pass_send, pass_recv)
    dispatch.start_local()
    dispatch.start((0, 1, 2))
    block = landing.shape[1]
    width = stage.shape[1]
    parts = landing.shape[2] // width

    def span_of(step):
        return pl.ds(pl.multiple_of(stagger_order(me // 2, step) * block, 16), block)

    def act_copy(step):
        return pltpu.make_async_copy(
            act_hbm.at[span_of(step), :], act.at[pl.ds(step * block, block), :], act_sem.at[step]
        )

    def rows_copy(step):
        chip = stagger_order(me // 2, step)
        return pltpu.make_async_copy(landing.at[chip], rows_out.at[chip], rows_sem.at[step])

    def stage_copy(part):
        slot = lax.rem(part, 2)
        span = pl.ds(pl.multiple_of(part * width, 16), width)
        return pltpu.make_async_copy(stage.at[slot], grad_out.at[span, :], stage_sem.at[slot])

    for step in range(4):
        act_copy(step).start()
    for steps in ((0, 1), (2,), (3,)):
        for step in steps:
            dispatch.arrive(step)
        chips = [dispatch.ready(step) for step in steps]
        for step in steps:
            rows_copy(step).start()
            act_copy(step).wait()

        def one(part, carry, steps=steps, chips=chips):
            columns = pl.ds(pl.multiple_of(part * width, 128), width)
            rows = [landing[chip, :, columns] for chip in chips]
            rows = rows[0] if len(rows) == 1 else jnp.concatenate(rows, axis=0)
            turned = rows.astype(jnp.float32).T.astype(jnp.bfloat16)
            product = dot_nn(turned, act[pl.ds(steps[0] * block, len(steps) * block), :])
            span = pl.ds(pl.multiple_of(part * width, 16), width)
            if steps[0] == 0:
                total[span, :] = product

                @pl.when(part == 0)
                def _():
                    dispatch.sent((2,))
                    dispatch.start((3,))

                return carry
            if steps[0] == 2:
                total[span, :] += product
                return carry

            @pl.when(part >= 2)
            def _():
                stage_copy(part - 2).wait()

            stage[lax.rem(part, 2)] = (total[span, :] + product).astype(jnp.bfloat16)
            stage_copy(part).start()
            return carry

        lax.fori_loop(0, parts, one, 0)
    for part in (parts - 2, parts - 1):
        stage_copy(part).wait()
    for step in range(4):
        rows_copy(step).wait()
    dispatch.sent((0, 1, 3))
    dispatch.passed_on()


def send_rows(slots, act):
    chips, capacity, depth = slots.shape
    rows, hidden_units = act.shape
    block = 2 * capacity
    width = min(256, depth // 2)
    any_space = pl.BlockSpec(memory_space=pl.ANY)
    bf = jnp.bfloat16
    dma = pltpu.SemaphoreType.DMA
    return pl.pallas_call(
        send_rows_body,
        in_specs=[any_space] * 2,
        out_specs=[any_space] * 2,
        out_shape=[
            jax.ShapeDtypeStruct((chips, block, depth), bf),
            jax.ShapeDtypeStruct((depth, hidden_units), bf),
        ],
        scratch_shapes=[
            pltpu.VMEM((chips, block, depth), bf),
            pltpu.VMEM((rows, hidden_units), bf),
            pltpu.VMEM((depth, hidden_units), jnp.float32),
            pltpu.VMEM((2, width, hidden_units), bf),
            dma((4,)),
            dma((4,)),
            dma((2,)),
            dma((1,)),
            dma((8,)),
            dma((8,)),
            dma((8,)),
            dma((8,)),
        ],
        compiler_params=pltpu.CompilerParams(
            collective_id=2, has_side_effects=True, vmem_limit_bytes=VMEM_BYTES
        ),
        name="send_rows",
    )(slots, act)


def ffn_backward_body(
    chunk,
    grad_rows,
    gate_in,
    up_in,
    gate_hbm,
    up_hbm,
    down_hbm,
    dgate_out,
    dup_out,
    back,
    gate,
    up,
    down,
    grad,
    pre_stage,
    pair,
    kept,
    passing,
    passed,
    total,
    weight_sem,
    grad_sem,
    stage_sem,
    pair_sem,
    local_sem,
    swap_send,
    swap_recv,
    out_send,
    out_recv,
):
    me = lax.axis_index("expert")
    enter(8, me)
    collect = Collect(
        me, far_order, (3,), kept, passing, passed, total, back, local_sem.at[0], swap_send, swap_recv, out_send, out_recv
    )
    loads = [
        pltpu.make_async_copy(source, target, weight_sem.at[n])
        for n, (source, target) in enumerate(((down_hbm, down), (gate_hbm, gate), (up_hbm, up)))
    ]
    block = grad.shape[1]
    hidden_units = gate.shape[1]
    chunks = hidden_units // chunk
    half = back.shape[2] // 2
    width = min(512, half)

    def span_of(chip):
        return pl.ds(pl.multiple_of(chip * block, 16), block)

    def grad_copy(step):
        return pltpu.make_async_copy(
            grad_rows.at[span_of(collect.block(step)), :], grad.at[step % 2], grad_sem.at[step % 2]
        )

    def stage_copies(chip, part, slot):
        columns = pl.ds(pl.multiple_of(part * chunk, 128), chunk)
        return [
            pltpu.make_async_copy(
                source.at[span_of(chip), columns], pre_stage.at[slot, n], stage_sem.at[slot, n]
            )
            for n, source in enumerate((gate_in, up_in))
        ]

    def pair_copies(chip):
        return [
            pltpu.make_async_copy(pair.at[n], out.at[span_of(chip), :], pair_sem.at[n])
            for n, out in enumerate((dgate_out, dup_out))
        ]

    grad_copy(0).start()
    loads[0].start()
    for copy in stage_copies(collect.block(0), 0, 0):
        copy.start()
    loads[1].start()
    loads[2].start()
    loads[0].wait()
    for step in range(4):
        chip = collect.block(step)
        grad_copy(step).wait()
        if step < 3:
            grad_copy(step + 1).start()
        if step > 0:
            for copy in pair_copies(collect.block(step - 1)):
                copy.wait()

        def hidden_part(part, carry, chip=chip, step=step):
            slot = lax.rem(part, 2)
            columns = pl.ds(pl.multiple_of(part * chunk, 128), chunk)
            for copy in stage_copies(chip, part, slot):
                copy.wait()

            @pl.when(part + 1 < chunks)
            def _():
                for copy in stage_copies(chip, part + 1, 1 - slot):
                    copy.start()

            upstream = dot_nn(grad[step % 2], down[:, columns])
            gated = pre_stage[slot, 0].astype(jnp.float32)
            raised = pre_stage[slot, 1].astype(jnp.float32)
            sigmoid = jax.nn.sigmoid(gated)
            scaled = upstream * sigmoid
            pair[0, :, columns] = (scaled * raised * (1.0 + gated * (1.0 - sigmoid))).astype(jnp.bfloat16)
            pair[1, :, columns] = (scaled * gated).astype(jnp.bfloat16)
            return carry

        lax.fori_loop(0, chunks, hidden_part, 0)
        for copy in pair_copies(chip):
            copy.start()
        if step < 3:
            for copy in stage_copies(collect.block(step + 1), 0, 0):
                copy.start()
        if step == 0:
            loads[1].wait()
            loads[2].wait()
        else:
            collect.settle(step - 1)
        core = collect.core

        def product(at):
            return dot_nt(pair[0], gate[pl.ds(at, width), :]) + dot_nt(pair[1], up[pl.ds(at, width), :])

        def far_part(part, carry, step=step):
            at = pl.multiple_of((1 - core) * half + part * width, 128)
            columns = pl.ds(pl.multiple_of(part * width, 128), width)
            passing[step % 2, :, columns] = product(at).astype(jnp.bfloat16)
            return carry

        def near_part(part, carry, step=step):
            at = pl.multiple_of(core * half + part * width, 128)
            kept[:, pl.ds(pl.multiple_of(part * width, 128), width)] = product(at)
            return carry

        if step >= 2:
            collect.swap(step - 2).wait_send()
        lax.fori_loop(0, half // width, far_part, 0)
        collect.swap(step).start()
        lax.fori_loop(0, half // width, near_part, 0)
    collect.settle(3)
    for copy in pair_copies(collect.block(3)):
        copy.wait()
    collect.finish()


def ffn_backward(grad_rows, gate_pre, up_pre, gate_weight, up_weight, down_weight, capacity):
    rows, depth = grad_rows.shape
    hidden_units = gate_weight.shape[1]
    block = 2 * capacity
    chips = rows // block
    chunk = hidden_units // 2 if hidden_units % 256 == 0 else 128
    half = depth // 2
    any_space = pl.BlockSpec(memory_space=pl.ANY)
    bf = jnp.bfloat16
    dma = pltpu.SemaphoreType.DMA
    return pl.pallas_call(
        functools.partial(ffn_backward_body, chunk),
        in_specs=[any_space] * 6,
        out_specs=[any_space] * 3,
        out_shape=[
            jax.ShapeDtypeStruct((rows, hidden_units), bf),
            jax.ShapeDtypeStruct((rows, hidden_units), bf),
            jax.ShapeDtypeStruct((chips, capacity, depth), bf),
        ],
        scratch_shapes=[
            pltpu.VMEM((depth, hidden_units), bf),
            pltpu.VMEM((depth, hidden_units), bf),
            pltpu.VMEM((depth, hidden_units), bf),
            pltpu.VMEM((2, block, depth), bf),
            pltpu.VMEM((2, 2, block, chunk), bf),
            pltpu.VMEM((2, block, hidden_units), bf),
            pltpu.VMEM((block, half), jnp.float32),
            pltpu.VMEM((2, block, half), bf),
            pltpu.VMEM((chips, block, half), bf),
            pltpu.VMEM((chips, block, half), bf),
            dma((3,)),
            dma((2,)),
            dma((2, 2)),
            dma((2,)),
            dma((1,)),
            dma((4,)),
            dma((4,)),
            dma((8,)),
            dma((8,)),
        ],
        compiler_params=pltpu.CompilerParams(
            collective_id=3, has_side_effects=True, vmem_limit_bytes=VMEM_BYTES
        ),
        name="ffn_backward",
    )(grad_rows, gate_pre, up_pre, gate_weight, up_weight, down_weight)


def send_slots_body(
    slots, rows_hbm, grads_hbm, landing, grad_out, rows_v, grads_v, stage, load_sem, stage_sem, local_sem, send, recv
):
    me = lax.axis_index("expert")
    enter(8, me)

    def outgoing(offset):
        target = lax.rem(me + offset, 8)
        return remote(slots.at[target], landing.at[me], send.at[offset], recv.at[offset], target)

    local = pltpu.make_async_copy(slots.at[me], landing.at[me], local_sem)
    for offset in range(1, 8):
        outgoing(offset).start()
    local.start()
    loads = [
        pltpu.make_async_copy(source, target, load_sem.at[n])
        for n, (source, target) in enumerate(((rows_hbm, rows_v), (grads_hbm, grads_v)))
    ]
    for load in loads:
        load.start()
    for load in loads:
        load.wait()
    width = stage.shape[1]
    blocks = rows_v.shape[1] // width

    def stage_copy(block):
        slot = lax.rem(block, 2)
        span = pl.ds(pl.multiple_of(block * width, 16), width)
        return pltpu.make_async_copy(stage.at[slot], grad_out.at[span, :], stage_sem.at[slot])

    def one(block, carry):
        @pl.when(block >= 2)
        def _():
            stage_copy(block - 2).wait()

        columns = pl.ds(pl.multiple_of(block * width, 128), width)
        turned = rows_v[:, columns].astype(jnp.float32).T.astype(jnp.bfloat16)
        stage[lax.rem(block, 2)] = dot_nn(turned, grads_v[...]).astype(jnp.bfloat16)
        stage_copy(block).start()
        return carry

    lax.fori_loop(0, blocks, one, 0)
    for block in (blocks - 2, blocks - 1):
        stage_copy(block).wait()
    local.wait()
    for offset in range(1, 8):
        outgoing(offset).wait_send()
        place = landing.at[lax.rem(me + 8 - offset, 8)]
        remote(place, place, send.at[offset], recv.at[offset], me).wait_recv()


def send_slots(slots, rows, grads):
    total, depth = rows.shape
    hidden_units = grads.shape[1]
    width = min(256, depth // 2)
    any_space = pl.BlockSpec(memory_space=pl.ANY)
    bf = jnp.bfloat16
    dma = pltpu.SemaphoreType.DMA
    return pl.pallas_call(
        send_slots_body,
        in_specs=[any_space] * 3,
        out_specs=[any_space] * 2,
        out_shape=[
            jax.ShapeDtypeStruct(slots.shape, bf),
            jax.ShapeDtypeStruct((depth, hidden_units), bf),
        ],
        scratch_shapes=[
            pltpu.VMEM((total, depth), bf),
            pltpu.VMEM((total, hidden_units), bf),
            pltpu.VMEM((2, width, hidden_units), bf),
            dma((2,)),
            dma((2,)),
            dma,
            dma((8,)),
            dma((8,)),
        ],
        compiler_params=pltpu.CompilerParams(
            collective_id=5, has_side_effects=True, vmem_limit_bytes=VMEM_BYTES
        ),
        name="send_slots",
    )(slots, rows, grads)


def merge_return_body(
    dp_axis,
    plan_hbm,
    slots_hbm,
    grads_hbm,
    weight_hbm,
    back,
    plan,
    slots,
    grads,
    weight,
    kept,
    passing,
    passed,
    total,
    load_sem,
    local_sem,
    swap_send,
    swap_recv,
    out_send,
    out_recv,
):
    me = lax.axis_index("expert")
    replica = lax.axis_index(dp_axis)
    enter(8, me)
    loads = [
        pltpu.make_async_copy(source, target, load_sem.at[n])
        for n, (source, target) in enumerate(
            ((plan_hbm, plan), (slots_hbm, slots), (grads_hbm, grads), (weight_hbm, weight))
        )
    ]
    for load in loads:
        load.start()
    collect = Collect(
        me, far_order, (3,), kept, passing, passed, total, back, local_sem.at[0], swap_send, swap_recv, out_send, out_recv
    )
    rows, half = collect.rows, collect.half
    parts, ck = weight.shape[0], weight.shape[2] // 2
    values_at = grads.shape[1] // 2
    width = min(512, half)
    for load in loads:
        load.wait()
    for step in range(4):
        chip = collect.block(step)
        span = pl.ds(pl.multiple_of(chip * 2 * rows, 16), 2 * rows)

        def product(at, chip=chip, span=span):
            columns = pl.ds(at, width)
            result = jnp.concatenate(
                [dot_nn(plan[2 * chip + n], slots[2 * chip + n, :, columns]) for n in range(2)], axis=0
            )
            for part in range(parts):
                low = lax.rem(replica, 2) + (part % 2) * (1 - 2 * lax.rem(replica, 2))
                high = replica // 2 + (part // 2) * (1 - 2 * (replica // 2))
                at_keys = pl.multiple_of((2 * high + low) * ck, 128)
                result += dot_nt(grads[span, pl.ds(at_keys, ck)], weight[part, columns, :ck])
                result += dot_nt(grads[span, pl.ds(values_at + at_keys, ck)], weight[part, columns, ck:])
            return result

        def far_part(part, carry, step=step, product=product):
            at = pl.multiple_of((1 - collect.core) * half + part * width, 128)
            columns = pl.ds(pl.multiple_of(part * width, 128), width)
            passing[step % 2, :, columns] = product(at).astype(jnp.bfloat16)
            return carry

        def near_part(part, carry, product=product):
            at = pl.multiple_of(collect.core * half + part * width, 128)
            kept[:, pl.ds(pl.multiple_of(part * width, 128), width)] = product(at)
            return carry

        if step >= 2:
            collect.swap(step - 2).wait_send()
        lax.fori_loop(0, half // width, far_part, 0)
        collect.swap(step).start()
        if step > 0:
            collect.settle(step - 1)
        lax.fori_loop(0, half // width, near_part, 0)
    collect.settle(3)
    collect.finish()


def merge_return(plan, slots, grads, weights):
    sources, rows, capacity = plan.shape
    parts, depth, columns = weights.shape
    tokens = sources * rows
    half = depth // 2
    any_space = pl.BlockSpec(memory_space=pl.ANY)
    bf = jnp.bfloat16
    dma = pltpu.SemaphoreType.DMA
    return pl.pallas_call(
        functools.partial(merge_return_body, "dp"),
        in_specs=[any_space] * 4,
        out_specs=any_space,
        out_shape=jax.ShapeDtypeStruct((sources // 2, rows, depth), bf),
        scratch_shapes=[
            pltpu.VMEM(plan.shape, bf),
            pltpu.VMEM(slots.shape, bf),
            pltpu.VMEM(grads.shape, bf),
            pltpu.VMEM(weights.shape, bf),
            pltpu.VMEM((2 * rows, half), jnp.float32),
            pltpu.VMEM((2, 2 * rows, half), bf),
            pltpu.VMEM((sources // 2, 2 * rows, half), bf),
            pltpu.VMEM((sources // 2, 2 * rows, half), bf),
            dma((4,)),
            dma((1,)),
            dma((4,)),
            dma((4,)),
            dma((8,)),
            dma((8,)),
        ],
        compiler_params=pltpu.CompilerParams(
            collective_id=6, has_side_effects=True, vmem_limit_bytes=VMEM_BYTES
        ),
        name="merge_return",
    )(plan, slots, grads, weights)


def return_order(chip, step):
    lower, upper = chip_order(chip, (2, 3, 1, 0)[step]), chip_order(chip, 3 - step)
    return lower + chip // 2 * (upper - lower)


def attention_send_body(
    scale,
    query_hbm,
    sibling_hbm,
    key_hbm,
    value_hbm,
    out_weight_hbm,
    key_info,
    query_info,
    own_out,
    sibling_out,
    rows_out,
    back,
    lse_ref,
    queries,
    siblings,
    keys_v,
    values_v,
    out_weight,
    bias_ref,
    flipped,
    own_stage,
    sibling_stage,
    arrived,
    rows_stage,
    sending,
    load_sem,
    own_sem,
    sibling_sem,
    rows_sem,
    local_sem,
    swap_send,
    swap_recv,
    out_send,
    out_recv,
):
    me = lax.axis_index("expert")
    chip, core = me // 2, lax.rem(me, 2)
    enter(8, me)
    half = keys_v.shape[1]
    rows = own_stage.shape[1]
    keys = keys_v.shape[0] // GROUPS
    heads = half // HEAD
    capacity = back.shape[1]
    own_columns = pl.ds(pl.multiple_of(core * half, 128), half)
    far_columns = pl.ds(pl.multiple_of((1 - core) * half, 128), half)
    loads = [
        pltpu.make_async_copy(source, target, load_sem.at[n])
        for n, (source, target) in enumerate(
            (
                (value_hbm, values_v),
                (key_hbm, keys_v),
                (query_hbm.at[:, own_columns], queries),
                (sibling_hbm, siblings),
                (out_weight_hbm, out_weight),
            )
        )
    ]
    for load in loads:
        load.start()
    fill_bias(bias_ref, key_info, query_info, keys)
    loads[0].wait()

    def flip(head, carry):
        lanes = pl.ds(pl.multiple_of(head * HEAD, HEAD), HEAD)
        for block in range(GROUPS):
            values = values_v[pl.ds(block * keys, keys), lanes].astype(jnp.float32)
            flipped[head, block] = values.T.astype(jnp.bfloat16)
        return carry

    lax.fori_loop(0, heads, flip, 0)
    for load in loads[1:4]:
        load.wait()

    def group_of(step):
        return return_order(chip, step)

    def span_of(step):
        return pl.ds(pl.multiple_of(group_of(step) * rows, 16), rows)

    def own_copy(step):
        return pltpu.make_async_copy(own_stage.at[step], own_out.at[span_of(step), :], own_sem.at[step])

    def sibling_copy(step):
        return pltpu.make_async_copy(
            sibling_stage.at[step], sibling_out.at[span_of(step), :], sibling_sem.at[step]
        )

    def rows_copy(step):
        return pltpu.make_async_copy(
            rows_stage.at[step], rows_out.at[span_of(step), :], rows_sem.at[step]
        )

    def swap(step):
        return remote(
            sibling_stage.at[step], arrived.at[step], swap_send.at[step], swap_recv.at[step], me + 1 - 2 * core
        )

    def outgoing(step, n):
        source = 2 * group_of(step) + n
        offset = lax.rem(source - me + 8, 8)
        return remote(sending.at[step, n], back.at[me], out_send.at[offset], out_recv.at[offset], source)

    def local(step, n):
        return pltpu.make_async_copy(sending.at[step, n], back.at[me], local_sem)

    def each(step, own, other):
        (own if step == 3 else other)(core)
        other(1 - core)

    def attend(step):
        group = group_of(step)
        first_block = group * (group + 1) // 2
        span = span_of(step)

        def head_pair(pair, carry):
            lanes = [pl.ds(pl.multiple_of((2 * pair + n) * HEAD, HEAD), HEAD) for n in range(2)]
            parts = [jnp.concatenate([queries[span, lane], siblings[span, lane]], axis=0) for lane in lanes]

            def one(block, state):
                at = pl.multiple_of(block * keys, 16)
                bias = bias_ref[first_block + block]
                result = []
                for n in range(2):
                    top, total, mixed = state[3 * n : 3 * n + 3]
                    scores = dot_nt(keys_v[pl.ds(at, keys), lanes[n]], parts[n]) * scale + bias
                    new_top = jnp.maximum(top, jnp.max(scores, axis=0, keepdims=True))
                    fade = jnp.exp2(top - new_top)
                    probs = jnp.exp2(scores - new_top)
                    total = total * fade + jnp.sum(probs, axis=0, keepdims=True)
                    mixed = mixed * fade + dot_nn(flipped[2 * pair + n, block], probs.astype(jnp.bfloat16))
                    result += [new_top, total, mixed]
                return tuple(result)

            start = (
                jnp.full((1, 2 * rows), -1e30, jnp.float32),
                jnp.zeros((1, 2 * rows), jnp.float32),
                jnp.zeros((HEAD, 2 * rows), jnp.float32),
            ) * 2
            final = lax.fori_loop(0, group + 1, one, start)
            for n in range(2):
                top, total, mixed = final[3 * n : 3 * n + 3]
                lse_ref[2 * pair + n, group] = top + jnp.log2(total)
                result = (mixed / total).T.astype(jnp.bfloat16)
                own_stage[step, :, lanes[n]] = result[:rows]
                sibling_stage[step, :, lanes[n]] = result[rows:]
            return carry

        lax.fori_loop(0, heads // 2, head_pair, 0)
        swap(step).start()
        own_copy(step).start()
        sibling_copy(step).start()

    def settle(step):
        swap(step).wait_recv()
        rows_stage[step, :, own_columns] = own_stage[step]
        rows_stage[step, :, far_columns] = arrived[step]
        rows_copy(step).start()
        width = 512
        for at in range(0, back.shape[2], min(width, back.shape[2])):
            columns = pl.ds(at, min(width, back.shape[2]))
            product = dot_nt(rows_stage[step], out_weight[columns, :])
            for n in range(2):
                part = product[n * capacity : (n + 1) * capacity]
                sending[step, n, :, columns] = part.astype(jnp.bfloat16)
        each(step, lambda n: local(step, n).start(), lambda n: outgoing(step, n).start())

    for step in range(4):
        attend(step)
        if step == 0:
            loads[4].wait()
        settle(step)
    for step in range(4):
        swap(step).wait_send()
        own_copy(step).wait()
        sibling_copy(step).wait()
        rows_copy(step).wait()
        each(step, lambda n, step=step: local(step, n).wait(), lambda n, step=step: outgoing(step, n).wait_send())
    for offset in range(1, 8):
        place = back.at[lax.rem(me + 8 - offset, 8)]
        remote(place, place, out_send.at[offset], out_recv.at[offset], me).wait_recv()


def attention_send(queries, siblings, keys_all, values_all, out_weight, key_info, query_info, capacity):
    total_rows, width = queries.shape
    tokens, half = keys_all.shape
    depth = out_weight.shape[0]
    rows, keys, heads = total_rows // GROUPS, tokens // GROUPS, half // HEAD
    any_space = pl.BlockSpec(memory_space=pl.ANY)
    here = pl.BlockSpec(memory_space=pltpu.VMEM)
    bf = jnp.bfloat16
    dma = pltpu.SemaphoreType.DMA
    return pl.pallas_call(
        functools.partial(attention_send_body, HEAD ** (-0.5) * LOG2E),
        in_specs=[any_space] * 5 + [here] * 2,
        out_specs=[any_space] * 4 + [here],
        out_shape=[
            jax.ShapeDtypeStruct((total_rows, half), bf),
            jax.ShapeDtypeStruct((total_rows, half), bf),
            jax.ShapeDtypeStruct((total_rows, width), bf),
            jax.ShapeDtypeStruct((8, capacity, depth), bf),
            jax.ShapeDtypeStruct((heads, GROUPS, 1, 2 * rows), jnp.float32),
        ],
        scratch_shapes=[
            pltpu.VMEM((total_rows, half), bf),
            pltpu.VMEM((total_rows, half), bf),
            pltpu.VMEM((tokens, half), bf),
            pltpu.VMEM((tokens, half), bf),
            pltpu.VMEM(out_weight.shape, bf),
            pltpu.VMEM((GROUPS * (GROUPS + 1) // 2, keys, 2 * rows), jnp.float32),
            pltpu.VMEM((heads, GROUPS, HEAD, keys), bf),
            pltpu.VMEM((GROUPS, rows, half), bf),
            pltpu.VMEM((GROUPS, rows, half), bf),
            pltpu.VMEM((GROUPS, rows, half), bf),
            pltpu.VMEM((GROUPS, rows, width), bf),
            pltpu.VMEM((GROUPS, 2, capacity, depth), bf),
            dma((5,)),
            dma((GROUPS,)),
            dma((GROUPS,)),
            dma((GROUPS,)),
            dma,
            dma((GROUPS,)),
            dma((GROUPS,)),
            dma((8,)),
            dma((8,)),
        ],
        compiler_params=pltpu.CompilerParams(
            collective_id=4, has_side_effects=True, vmem_limit_bytes=VMEM_BYTES
        ),
        name="attention_send",
    )(queries, siblings, keys_all, values_all, out_weight, key_info, query_info)


def swap_blocks_body(blocks, landing, local_sem, send, recv):
    me = lax.axis_index("expert")
    enter(8, me)

    def outgoing(offset):
        target = lax.rem(me + offset, 8)
        return remote(blocks.at[target], landing.at[me], send.at[offset], recv.at[offset], target)

    local = pltpu.make_async_copy(blocks.at[me], landing.at[me], local_sem)
    for offset in range(1, 8):
        outgoing(offset).start()
    local.start()
    local.wait()
    for offset in range(1, 8):
        outgoing(offset).wait_send()
        place = landing.at[lax.rem(me + 8 - offset, 8)]
        remote(place, place, send.at[offset], recv.at[offset], me).wait_recv()


def swap_blocks(blocks):
    any_space = pl.BlockSpec(memory_space=pl.ANY)
    dma = pltpu.SemaphoreType.DMA
    return pl.pallas_call(
        swap_blocks_body,
        in_specs=[any_space],
        out_specs=any_space,
        out_shape=jax.ShapeDtypeStruct(blocks.shape, blocks.dtype),
        scratch_shapes=[dma, dma((8,)), dma((8,))],
        compiler_params=pltpu.CompilerParams(collective_id=7, has_side_effects=True),
        name="swap_blocks",
    )(blocks)


D = 2048
HEADS = 16
ATT_EXPERTS = 8
FFN_EXPERTS = 4
TRUNK = 1024
SEG = 96
TREE_LEN = 2176
NODES = 13

epsilon = 1e-06
highest = lax.Precision.HIGHEST
bf16 = jnp.bfloat16
f32 = jnp.float32


def tree_layout(places):
    after_trunk = places - TRUNK
    after_branch = after_trunk - 4 * SEG
    segments = jnp.where(
        places < TRUNK,
        0,
        jnp.where(after_branch < 0, 1 + after_trunk // SEG, 5 + after_branch // SEG),
    )
    depths = jnp.where(
        places < TRUNK,
        places,
        jnp.where(after_branch < 0, TRUNK + after_trunk % SEG, TRUNK + SEG + after_branch % SEG),
    )
    return (segments.astype(jnp.int32), depths.astype(jnp.int32))


def rotation_tables(depths):
    half_size = HEAD // 2
    frequency = 10000.0 ** (-jnp.arange(half_size, dtype=f32) * 2.0 / HEAD)
    angles = depths.astype(f32)[:, None] * frequency[None, :]
    cosine, sine = jnp.cos(angles), jnp.sin(angles)
    cosines = jnp.concatenate([cosine, cosine], axis=1)
    forward = jnp.concatenate([-sine, sine], axis=1)
    return (cosines, forward), (cosines, -forward)


def lookup(table, indices):
    nodes = jnp.arange(NODES, dtype=jnp.int32)
    return jnp.sum(jnp.where(indices[:, None] == nodes[None, :], table[None, :], 0), axis=1)


def running_count(chosen):
    rows = chosen.shape[-1]
    index = jnp.arange(rows, dtype=jnp.int32)
    upto = (index[:, None] <= index[None, :]).astype(bf16)
    return jnp.dot(chosen.astype(bf16), upto, preferred_element_type=f32).astype(jnp.int32) - 1


def source_plan(routes, expert, capacity):
    chosen = jnp.any(routes == expert, axis=2)
    ranking = running_count(chosen)
    slots = jnp.arange(capacity, dtype=jnp.int32)
    return chosen[:, None, :] & (ranking[:, None, :] == slots[None, :, None])


def token_picks(routes, experts, capacity):
    labels = jnp.arange(experts, dtype=jnp.int32)
    hits = routes.T[:, None, :] == labels[None, :, None]
    ranking = running_count(hits[0] | hits[1])
    slots = jnp.arange(capacity, dtype=jnp.int32)
    picks = hits[:, :, None, :] & (ranking[None, :, None, :] == slots[None, None, :, None])
    return picks.astype(bf16), hits[0].T.astype(f32), hits[1].T.astype(f32)


def fill_slots(picks, pair):
    return jnp.einsum("kecr,krd->ecd", picks, pair, preferred_element_type=f32).astype(bf16)


def read_slots(picks, slots):
    return jnp.einsum("kecr,ecd->krd", picks, slots, preferred_element_type=f32)


def gate_values(hidden, router, first, second):
    logits = jnp.dot(hidden.astype(f32), router, precision=highest)
    picked = jnp.stack([jnp.sum(logits * first, axis=1), jnp.sum(logits * second, axis=1)], axis=1)
    return jax.nn.softmax(picked, axis=1)


def router_grads(hidden, router, gates, first, second, picked_grad):
    logit_pick = gates * (picked_grad - jnp.sum(gates * picked_grad, axis=1, keepdims=True))
    logit_grad = logit_pick[:, 0:1] * first + logit_pick[:, 1:2] * second
    router_grad = jnp.dot(hidden.astype(f32).T, logit_grad, precision=highest)
    hidden_grad = jnp.dot(logit_grad, router.T, precision=highest)
    return (router_grad, hidden_grad)


def rms_parts(values):
    inverse = lax.rsqrt(jnp.mean(values * values, axis=-1, keepdims=True) + epsilon)
    return (values * inverse, inverse)


def norm_back(grad_normed, normed, inverse):
    return inverse * (grad_normed - normed * jnp.mean(grad_normed * normed, axis=-1, keepdims=True))


def pair_grads(gates, branches, upstream):
    gate_grad = jnp.stack([jnp.sum(upstream * branches[k], axis=1) for k in range(2)], axis=1)
    scaled = jnp.stack([gates[:, k : k + 1] * upstream for k in range(2)]).astype(bf16)
    return gate_grad, scaled


def exchange(slots):
    return lax.all_to_all(slots, "expert", split_axis=0, concat_axis=0, tiled=True)


def shift(values, step, size, devices):
    moves = [(i, i // size * size + (i % size + step) % size) for i in range(devices)]
    return lax.ppermute(values, "expert", moves)


def group_gather(rows, size, devices):
    return jnp.concatenate([rows] + [shift(rows, step, size, devices) for step in range(1, size)])


def group_reduce(partial, size, devices):
    parts = partial.reshape(size, -1, partial.shape[1])
    total = parts[0].astype(f32)
    for step in range(1, size):
        total = total + shift(parts[step], -step, size, devices).astype(f32)
    return total.astype(bf16)


def spread_over_replicas(block, my_replica, replicas):
    if replicas != 4:
        return lax.all_gather(block, "dp", axis=0), jnp.arange(replicas, dtype=jnp.int32)
    across, along = ([(i, i ^ n) for i in range(4)] for n in (1, 2))
    first, second = lax.ppermute(block, "dp", across), lax.ppermute(block, "dp", along)
    cut = block.shape[0] // 2
    upper, lower = lax.ppermute(second[:cut], "dp", across), lax.ppermute(first[cut:], "dp", along)
    blocks = jnp.stack([block, first, second, jnp.concatenate([upper, lower])])
    return blocks, my_replica ^ jnp.arange(4, dtype=jnp.int32)


def dot_tn(left, right):
    return lax.dot_general(left, right, (((0,), (0,)), ((), ())), preferred_element_type=f32)


def body(
    tokens,
    teacher,
    att_routes,
    ffn_routes,
    parent,
    valid,
    gain_one,
    kv_weight,
    att_router,
    q_weight,
    o_weight,
    gain_two,
    ffn_router,
    gate_weight,
    up_weight,
    down_weight,
):
    row_count = tokens.shape[0]
    devices, replicas = lax.axis_size("expert"), lax.axis_size("dp")
    my_index, my_replica = lax.axis_index("expert"), lax.axis_index("dp")
    core = my_index % 2
    att_copies, ffn_copies = devices // ATT_EXPERTS, devices // FFN_EXPERTS
    att_capacity, ffn_capacity = row_count * 13 // 40, row_count * 13 // 20
    token_count = row_count * devices
    half = HEADS * HEAD // 2
    assert token_count == TREE_LEN * parent.shape[0] and parent.shape[0] == 1
    pair = [(i, i ^ 1) for i in range(devices)]
    own_places = my_index * row_count + jnp.arange(row_count, dtype=jnp.int32)

    x_in = tokens.astype(f32)
    normed_one, inverse_one = rms_parts(x_in)
    hidden = (normed_one * gain_one).astype(bf16)
    weight_rows = kv_weight.shape[0]
    piece = half // replicas
    kv_share = lax.dynamic_slice_in_dim(
        kv_weight.reshape(weight_rows, 4, replicas, piece), my_replica, 1, 2
    )
    kv_share = (
        kv_share.reshape(weight_rows, 2, 2, piece).transpose(0, 2, 1, 3).reshape(weight_rows, 4 * piece)
    )
    kv_gathered = lax.all_gather(kv_share, "expert", axis=0)
    hidden_all = lax.all_gather(hidden, "expert", axis=0)
    all_routes = lax.all_gather(att_routes, "expert", axis=0)

    tree_places = jnp.arange(token_count, dtype=jnp.int32)
    tree_segments, tree_depths = tree_layout(tree_places)
    key_forward, key_backward = rotation_tables(tree_depths)
    key_info = jnp.pad(jnp.stack([tree_places, tree_segments], axis=1), ((0, 0), (0, 6)))
    experts_here = [my_index // att_copies]
    if att_copies == 1:
        experts_here.append(my_index ^ 1)
    plans = [source_plan(all_routes, expert, att_capacity) for expert in experts_here]
    slot_tables, query_parts = [], []
    for plan in plans:
        places = jnp.sum(
            jnp.where(plan, tree_places.reshape(devices, 1, row_count), 0), axis=2
        ).reshape(-1)
        segments, depths = tree_layout(places)
        parents = lookup(parent[0], segments)
        grands = lookup(parent[0], parents)
        query_parts.append(jnp.stack([places, segments, parents, grands]).reshape(4, GROUPS, -1))
        slot_tables.append(rotation_tables(depths))
    query_info = jnp.concatenate(query_parts, axis=2).transpose(1, 0, 2)
    own_plan = plans[0].astype(bf16)
    att_picks, att_first, att_second = token_picks(att_routes, ATT_EXPERTS, att_capacity)
    att_gates = gate_values(hidden, att_router, att_first, att_second)
    ffn_picks, ffn_first, ffn_second = token_picks(ffn_routes, FFN_EXPERTS, ffn_capacity)
    prepared = (key_forward, key_backward, key_info, slot_tables, query_info, own_plan, att_picks, att_gates, ffn_picks)
    kv_gathered, prepared = lax.optimization_barrier((kv_gathered, prepared))
    kv_half = lax.dynamic_slice_in_dim(kv_gathered, core * 2 * piece, 2 * piece, 2).reshape(D, 2 * piece)
    kv_blocks, block_order = spread_over_replicas(kv_half, my_replica, replicas)
    hidden_all, kv_blocks = lax.optimization_barrier((hidden_all, kv_blocks))
    key_forward, key_backward, key_info, slot_tables, query_info, own_plan, att_picks, att_gates, ffn_picks = prepared

    queries, query_inputs = project_queries(own_plan, hidden_all, q_weight, slot_tables[0][0])
    keys_all, values_all = project_keys_values(hidden_all, kv_blocks, key_forward, block_order)

    def far_half(values):
        return lax.ppermute(
            lax.dynamic_slice_in_dim(values, (1 - core) * half, half, 1), "expert", pair
        )

    def join_halves(mine, sibling):
        other = lax.ppermute(sibling, "expert", pair)
        return jnp.where(
            core == 0,
            jnp.concatenate([mine, other], axis=1),
            jnp.concatenate([other, mine], axis=1),
        )

    heads = half // HEAD
    query_sets = [queries]
    starts = jnp.zeros((2,), jnp.int32)
    if att_copies == 1:
        query_sets.append(far_half(queries))
        starts = jnp.stack([core * heads, 0]).astype(jnp.int32)
    fused = devices == 8 and replicas == 4 and att_copies == 1 and ffn_copies == 2 and ffn_capacity % 16 == 0
    if fused:
        *att_outs, att_rows, att_back, lse = attention_send(
            *query_sets, keys_all, values_all, o_weight, key_info, query_info, att_capacity
        )
        att_everywhere = lax.all_gather(att_rows, "dp", axis=0, tiled=True)
    else:
        *att_outs, lse = attention_forward(
            query_sets, starts // 2, keys_all, values_all, key_info, query_info, heads
        )
        att_rows = join_halves(*att_outs) if att_copies == 1 else att_outs[0]
        att_partial = lax.dot_general(
            att_rows, o_weight, (((1,), (1,)), ((), ())), preferred_element_type=f32
        ).astype(bf16)
        att_back = exchange(att_partial.reshape(devices, att_capacity, D))
    if att_copies > 1:
        att_back = (
            att_back.astype(f32).reshape(ATT_EXPERTS, att_copies, att_capacity, D).sum(axis=1).astype(bf16)
        )
    att_branches = read_slots(att_picks, att_back)
    x_mid = x_in + att_gates[:, 0:1] * att_branches[0] + att_gates[:, 1:2] * att_branches[1]

    normed_two, inverse_two = rms_parts(x_mid)
    hidden_two = (normed_two * gain_two).astype(bf16)
    ffn_gates = gate_values(hidden_two, ffn_router, ffn_first, ffn_second)

    def to_experts(slots):
        rows = exchange(slots.reshape(devices, ffn_capacity // ffn_copies, D))
        return group_gather(rows.reshape(-1, D), ffn_copies, devices)

    def to_tokens(partial):
        rows = group_reduce(partial.astype(bf16), ffn_copies, devices)
        back = exchange(rows.reshape(devices, ffn_capacity // ffn_copies, D))
        return read_slots(ffn_picks, back.reshape(FFN_EXPERTS, ffn_capacity, D))

    ffn_slots = jnp.einsum(
        "ecr,rd->ecd", ffn_picks[0] + ffn_picks[1], hidden_two, preferred_element_type=f32
    ).astype(bf16)
    if fused:
        ffn_inputs, gate_pre, up_pre, activated, ffn_back = ffn_forward(
            ffn_slots, gate_weight, up_weight, down_weight
        )
        ffn_branches = read_slots(ffn_picks, ffn_back)
    else:
        ffn_inputs = to_experts(ffn_slots)
        gate_pre = jnp.dot(ffn_inputs, gate_weight, preferred_element_type=f32)
        up_pre = jnp.dot(ffn_inputs, up_weight, preferred_element_type=f32)
        sigmoid_gate = jax.nn.sigmoid(gate_pre)
        silu_gate = gate_pre * sigmoid_gate
        activated = (silu_gate * up_pre).astype(bf16)
        ffn_branches = to_tokens(
            lax.dot_general(
                activated, down_weight, (((1,), (1,)), ((), ())), preferred_element_type=f32
            )
        )
    result = x_mid + ffn_gates[:, 0:1] * ffn_branches[0] + ffn_gates[:, 1:2] * ffn_branches[1]

    tree_global = my_replica * parent.shape[0] + own_places // TREE_LEN
    tree_labels = jnp.arange(valid.shape[0], dtype=jnp.int32)
    limits = jnp.sum(
        jnp.where(tree_global[:, None] == tree_labels[None, :], valid[None, :], 0), axis=1
    )
    counted = own_places % TREE_LEN < limits
    loss_factor = valid.shape[0] * TREE_LEN / jnp.sum(valid).astype(f32)
    grad_result = jnp.where(counted[:, None], (result - teacher.astype(f32)) * loss_factor, 0.0)

    ffn_gate_grad, ffn_scaled = pair_grads(ffn_gates, ffn_branches, grad_result)
    ffn_grad_slots = fill_slots(ffn_picks, ffn_scaled)
    if fused:
        ffn_grad_slots, att_everywhere = lax.optimization_barrier((ffn_grad_slots, att_everywhere))
        grad_ffn_out, grad_down = send_rows(ffn_grad_slots, activated)
        grad_ffn_out = grad_ffn_out.reshape(-1, D)
    else:
        grad_ffn_out = to_experts(ffn_grad_slots)
        grad_down = dot_tn(grad_ffn_out, activated).astype(bf16)
    grad_ffn_out, grad_down = lax.optimization_barrier((grad_ffn_out, grad_down))
    summed_down = lax.psum_scatter(grad_down, "dp", scatter_dimension=0, tiled=True)
    if fused:
        grad_gate_pre, grad_up_pre, ffn_grad_back = ffn_backward(
            grad_ffn_out, gate_pre, up_pre, gate_weight, up_weight, down_weight, ffn_capacity
        )
        grad_gate = dot_tn(ffn_inputs, grad_gate_pre).astype(bf16)
        ffn_grad_back, grad_gate = lax.optimization_barrier((ffn_grad_back, grad_gate))
        ffn_grad_pair = read_slots(ffn_picks, ffn_grad_back)
    else:
        grad_activated = jnp.dot(grad_ffn_out, down_weight, preferred_element_type=f32)
        grad_gate_pre = (
            grad_activated * up_pre * sigmoid_gate * (1.0 + gate_pre * (1.0 - sigmoid_gate))
        ).astype(bf16)
        grad_up_pre = (grad_activated * silu_gate).astype(bf16)
        grad_ffn_in = lax.dot_general(
            grad_gate_pre, gate_weight, (((1,), (1,)), ((), ())), preferred_element_type=f32
        ) + lax.dot_general(
            grad_up_pre, up_weight, (((1,), (1,)), ((), ())), preferred_element_type=f32
        )
        grad_gate = dot_tn(ffn_inputs, grad_gate_pre).astype(bf16)
        ffn_grad_pair = to_tokens(grad_ffn_in)
    summed_gate = lax.psum_scatter(grad_gate, "dp", scatter_dimension=0, tiled=True)
    grad_ffn_router, hidden_two_extra = router_grads(
        hidden_two, ffn_router, ffn_gates, ffn_first, ffn_second, ffn_gate_grad
    )
    grad_hidden_two = ffn_grad_pair[0] + ffn_grad_pair[1] + hidden_two_extra
    grad_gain_two = jnp.sum(grad_hidden_two * normed_two, axis=0)
    grad_mid = grad_result + norm_back(grad_hidden_two * gain_two, normed_two, inverse_two)

    att_gate_grad, att_scaled = pair_grads(att_gates, att_branches, grad_mid)
    att_slots = fill_slots(att_picks, att_scaled)
    if att_copies > 1:
        att_slots = jnp.repeat(att_slots, att_copies, axis=0)
    att_slots, summed_down = lax.optimization_barrier((att_slots, summed_down))
    if fused:
        grad_att_out, grad_up = send_slots(att_slots, ffn_inputs, grad_up_pre)
        grad_att_out = grad_att_out.reshape(-1, D)
    else:
        grad_att_out = exchange(att_slots).reshape(-1, D)
        grad_up = dot_tn(ffn_inputs, grad_up_pre).astype(bf16)
        grad_att_out, grad_up = lax.optimization_barrier((grad_att_out, grad_up))
    summed_up = lax.psum_scatter(grad_up, "dp", scatter_dimension=0, tiled=True)
    grad_heads = jnp.dot(grad_att_out, o_weight, preferred_element_type=f32).astype(bf16)
    grad_heads, grad_att_out = lax.optimization_barrier((grad_heads, grad_att_out))
    grad_sets = [grad_heads]
    if att_copies == 1:
        grad_sets.append(far_half(grad_heads))
    if fused:
        share = D // replicas

        def columns_of(replica):
            return lax.dynamic_slice_in_dim(grad_att_out, replica * share, share, 1)

        grad_columns = [columns_of(my_replica)] + [
            lax.ppermute(columns_of(my_replica ^ n), "dp", [(i, i ^ n) for i in range(replicas)])
            for n in range(1, replicas)
        ]
    else:
        grad_o = dot_tn(grad_att_out, att_rows).astype(bf16)
        summed_o = lax.psum_scatter(grad_o, "dp", scatter_dimension=0, tiled=True).astype(f32)
    *grad_queries, grad_keys_values = attention_backward(
        query_sets,
        starts,
        grad_sets,
        att_outs,
        keys_all,
        values_all,
        lse,
        key_info,
        query_info,
        key_backward,
        [tables[1] for tables in slot_tables],
        heads,
    )
    grad_keys_values, summed_gate = lax.optimization_barrier((grad_keys_values, summed_gate))
    grad_query_pre = join_halves(*grad_queries) if att_copies == 1 else grad_queries[0]
    grad_kv = dot_tn(hidden_all.reshape(token_count, D), grad_keys_values).astype(bf16)
    grad_q = dot_tn(query_inputs, grad_query_pre).astype(bf16)
    summed_kv = lax.psum_scatter(grad_kv, "dp", scatter_dimension=0, tiled=True)
    summed_q = lax.psum_scatter(grad_q, "dp", scatter_dimension=0, tiled=True)
    grad_query_in = lax.dot_general(
        grad_query_pre, q_weight, (((1,), (1,)), ((), ())), preferred_element_type=f32
    ).astype(bf16)
    grad_query_in, grad_kv, grad_q, summed_up = lax.optimization_barrier(
        (grad_query_in, grad_kv, grad_q, summed_up)
    )

    merge_args = (
        own_plan.transpose(0, 2, 1),
        grad_query_in.reshape(devices, att_capacity, D),
        grad_keys_values,
        kv_blocks,
    )
    if fused:
        arrived = merge_return(*merge_args)
        arrived, grad_columns, summed_kv = lax.optimization_barrier((arrived, grad_columns, summed_kv))
        column_stack = jnp.stack(grad_columns)
        summed_o = dot_tn(
            jnp.concatenate(
                [lax.dynamic_index_in_dim(column_stack, my_replica ^ n, 0, False) for n in range(replicas)]
            ),
            att_everywhere,
        )
    else:
        merged = merge_hidden_grads(*merge_args, block_order).reshape(devices // 2, 2, row_count, D)
        kept = lax.dynamic_index_in_dim(merged, core, 1, keepdims=False)
        passed = lax.ppermute(
            lax.dynamic_index_in_dim(merged, 1 - core, 1, keepdims=False), "expert", pair
        )
        chip_sum = (kept.astype(f32) + passed.astype(f32)).astype(bf16)
        same_core = [[2 * i + c for i in range(devices // 2)] for c in range(2)]
        arrived = lax.all_to_all(
            chip_sum, "expert", split_axis=0, concat_axis=0, axis_index_groups=same_core, tiled=True
        )
    grad_att_router, hidden_one_extra = router_grads(
        hidden, att_router, att_gates, att_first, att_second, att_gate_grad
    )
    grad_hidden_one = jnp.sum(arrived.astype(f32), axis=0) + hidden_one_extra
    grad_gain_one = jnp.sum(grad_hidden_one * normed_one, axis=0)
    grad_input = grad_mid + norm_back(grad_hidden_one * gain_one, normed_one, inverse_one)

    everyone = devices * replicas
    smalls = [grad_gain_one, grad_gain_two, grad_att_router, grad_ffn_router]
    packed = jnp.concatenate([small.reshape(everyone, -1) for small in smalls], axis=1)
    packed, summed_o = lax.optimization_barrier((packed, summed_o))
    kv_exchange = swap_blocks if fused else exchange
    kv_rows = kv_exchange(summed_kv.reshape(devices, -1, 2 * half))
    own_smalls = jnp.sum(
        lax.all_to_all(packed, ("dp", "expert"), split_axis=0, concat_axis=0, tiled=True), axis=0
    )
    own_smalls, kv_rows, summed_q = lax.optimization_barrier((own_smalls, kv_rows, summed_q))
    share = D // everyone
    shared_gain_one = own_smalls[:share]
    shared_gain_two = own_smalls[share : 2 * share]
    shared_att_router = own_smalls[2 * share : (2 + ATT_EXPERTS) * share].reshape(share, ATT_EXPERTS)
    shared_ffn_router = own_smalls[(2 + ATT_EXPERTS) * share :].reshape(share, FFN_EXPERTS)

    kv_sum = jnp.sum(kv_rows.astype(f32).reshape(devices // 2, 2, -1, 2 * half), axis=0)
    shared_kv = jnp.concatenate(
        [kv_sum[n, :, m * half : (m + 1) * half] for m in range(2) for n in range(2)], axis=1
    )

    return (
        result.astype(bf16),
        grad_input.astype(bf16),
        shared_gain_one,
        shared_kv,
        shared_att_router,
        summed_q.astype(f32),
        summed_o,
        shared_gain_two,
        shared_ffn_router,
        summed_gate.astype(f32),
        summed_up.astype(f32),
        summed_down.astype(f32),
    )


def solution(mesh):
    in_specs = (
        P(("dp", "expert"), None),
        P(("dp", "expert"), None),
        P(("dp", "expert"), None),
        P(("dp", "expert"), None),
        P("dp", None),
        P(),
        P(),
        P("expert", None),
        P(),
        P(None, "expert"),
        P(None, "expert"),
        P(),
        P(),
        P(None, "expert"),
        P(None, "expert"),
        P(None, "expert"),
    )
    out_specs = (
        P(("dp", "expert"), None),
        P(("dp", "expert"), None),
        P(("dp", "expert")),
        P(("dp", "expert"), None),
        P(("dp", "expert"), None),
        P("dp", "expert"),
        P("dp", "expert"),
        P(("dp", "expert")),
        P(("dp", "expert"), None),
        P("dp", "expert"),
        P("dp", "expert"),
        P("dp", "expert"),
    )
    return jax.shard_map(body, mesh=mesh, in_specs=in_specs, out_specs=out_specs, check_vma=False)
```

```python
import functools
import jax
import jax.numpy as jnp
from jax import lax
from jax.experimental import pallas as pl
from jax.experimental.pallas import tpu as pltpu
from jax.sharding import PartitionSpec as P

HEAD = 128
GROUPS = 4
LOG2E = 1.4426950408889634
VMEM_BYTES = 60 * 1024 * 1024


def dot_nt(left, right):
    return lax.dot_general(left, right, (((1,), (1,)), ((), ())), preferred_element_type=jnp.float32)


def dot_nn(left, right):
    return jnp.dot(left, right, preferred_element_type=jnp.float32)


def spin(values, cosine, sine):
    return values * cosine + pltpu.roll(values, HEAD // 2, 1) * sine


def fill_bias(bias_ref, key_ref, query_ref, keys):
    for group in range(GROUPS):
        place = query_ref[group, 0:1, :]
        own, parent, grand = (query_ref[group, 1 + n : 2 + n, :] for n in range(3))

        def one(block, carry, group=group, place=place, own=own, parent=parent, grand=grand):
            at = pl.multiple_of(block * keys, 16)
            key_place = key_ref[pl.ds(at, keys), 0:1]
            key_segment = key_ref[pl.ds(at, keys), 1:2]
            related = (key_segment == own) | (key_segment == parent) | (key_segment == grand)
            allowed = related & (key_place <= place)
            bias_ref[group * (group + 1) // 2 + block] = jnp.where(allowed, 0.0, -1e30)
            return carry

        lax.fori_loop(0, group + 1, one, 0)


def group_rows(refs, group, rows, lanes):
    parts = [ref[pl.ds(group * rows, rows), lanes] for ref in refs]
    return parts[0] if len(parts) == 1 else jnp.concatenate(parts, axis=0)


def attention_forward_body(sets, step_heads, rows, keys, scale, first_ref, *refs):
    query_refs = refs[:sets]
    key_ref, value_ref, key_info, query_info = refs[sets : sets + 4]
    out_refs = refs[sets + 4 : 2 * sets + 4]
    lse_ref, bias_ref, flipped_ref = refs[2 * sets + 4 :]
    wide = sets * rows

    @pl.when(pl.program_id(0) == 0)
    def _():
        fill_bias(bias_ref, key_info, query_info, keys)

    for head in range(step_heads):
        lanes = pl.ds(head * HEAD, HEAD)
        for block in range(GROUPS):
            values = value_ref[pl.ds(block * keys, keys), lanes].astype(jnp.float32)
            flipped_ref[head, block] = values.T.astype(jnp.bfloat16)
    for group in range(GROUPS):
        queries = [
            group_rows(query_refs, group, rows, pl.ds(head * HEAD, HEAD)) for head in range(step_heads)
        ]

        def one(block, carry, group=group, queries=queries):
            at = pl.multiple_of(block * keys, 16)
            bias = bias_ref[group * (group + 1) // 2 + block]
            result = []
            for head in range(step_heads):
                top, total, mixed = carry[3 * head : 3 * head + 3]
                scores = dot_nt(key_ref[pl.ds(at, keys), pl.ds(head * HEAD, HEAD)], queries[head])
                scores = scores * scale + bias
                new_top = jnp.maximum(top, jnp.max(scores, axis=0, keepdims=True))
                fade = jnp.exp2(top - new_top)
                parts = jnp.exp2(scores - new_top)
                total = total * fade + jnp.sum(parts, axis=0, keepdims=True)
                mixed = mixed * fade + dot_nn(flipped_ref[head, block], parts.astype(jnp.bfloat16))
                result += [new_top, total, mixed]
            return tuple(result)

        start = (
            jnp.full((1, wide), -1e30, jnp.float32),
            jnp.zeros((1, wide), jnp.float32),
            jnp.zeros((HEAD, wide), jnp.float32),
        ) * step_heads
        final = lax.fori_loop(0, group + 1, one, start)
        for head in range(step_heads):
            top, total, mixed = final[3 * head : 3 * head + 3]
            lse_ref[head, group] = top + jnp.log2(total)
            rows_out = (mixed / total).T.astype(jnp.bfloat16)
            for n, ref in enumerate(out_refs):
                ref[pl.ds(group * rows, rows), pl.ds(head * HEAD, HEAD)] = rows_out[
                    n * rows : (n + 1) * rows
                ]


def attention_backward_body(sets, step_heads, rows, keys, scale, first_ref, *refs):
    query_refs, grad_refs, out_refs = (refs[n * sets : (n + 1) * sets] for n in range(3))
    key_ref, value_ref, lse_ref, key_info, query_info = refs[3 * sets : 3 * sets + 5]
    key_cos, key_sin = refs[3 * sets + 5 : 3 * sets + 7]
    table_refs = refs[3 * sets + 7 : 5 * sets + 7]
    rest = refs[5 * sets + 7 :]
    dq_refs = rest[:sets]
    dkv_ref, bias_ref, flipped_ref, dk_acc, dv_acc = rest[sets:]
    half = dkv_ref.shape[1] // 2
    softmax_scale = scale / LOG2E

    @pl.when(pl.program_id(0) == 0)
    def _():
        fill_bias(bias_ref, key_info, query_info, keys)

    dk_acc[...] = jnp.zeros_like(dk_acc)
    dv_acc[...] = jnp.zeros_like(dv_acc)
    for head in range(step_heads):
        lanes = pl.ds(head * HEAD, HEAD)
        for block in range(GROUPS):
            values = key_ref[pl.ds(block * keys, keys), lanes].astype(jnp.float32)
            flipped_ref[head, block] = values.T.astype(jnp.bfloat16)
    for group in range(GROUPS):
        queries, grads, centres, tops = [], [], [], []
        for head in range(step_heads):
            lanes = pl.ds(head * HEAD, HEAD)
            queries.append(group_rows(query_refs, group, rows, lanes))
            grad = group_rows(grad_refs, group, rows, lanes)
            out = group_rows(out_refs, group, rows, lanes)
            product = grad.astype(jnp.float32) * out.astype(jnp.float32)
            centres.append(jnp.sum(product.T, axis=0, keepdims=True))
            grads.append(grad)
            tops.append(lse_ref[head, group])

        def one(block, carry, group=group, queries=queries, grads=grads, centres=centres, tops=tops):
            at = pl.multiple_of(block * keys, 16)
            bias = bias_ref[group * (group + 1) // 2 + block]
            result = []
            for head in range(step_heads):
                lanes = pl.ds(head * HEAD, HEAD)
                key_rows = key_ref[pl.ds(at, keys), lanes]
                scores = dot_nt(key_rows, queries[head])
                probs = jnp.exp2(scores * scale + (bias - tops[head]))
                grad_probs = dot_nt(value_ref[pl.ds(at, keys), lanes], grads[head])
                grad_scores = (probs * (grad_probs - centres[head])).astype(jnp.bfloat16)
                dv_acc[pl.ds(at, keys), lanes] += dot_nn(probs.astype(jnp.bfloat16), grads[head])
                dk_acc[pl.ds(at, keys), lanes] += dot_nn(grad_scores, queries[head])
                result.append(carry[head] + dot_nn(flipped_ref[head, block], grad_scores))
            return tuple(result)

        start = (jnp.zeros((HEAD, sets * rows), jnp.float32),) * step_heads
        final = lax.fori_loop(0, group + 1, one, start)
        for head in range(step_heads):
            dq = final[head].T * softmax_scale
            for n, ref in enumerate(dq_refs):
                span = pl.ds(group * rows, rows)
                turned = spin(
                    dq[n * rows : (n + 1) * rows], table_refs[2 * n][span, :], table_refs[2 * n + 1][span, :]
                )
                ref[span, pl.ds(head * HEAD, HEAD)] = turned.astype(jnp.bfloat16)
    for head in range(step_heads):
        lanes = pl.ds(head * HEAD, HEAD)
        first_lane = pl.multiple_of((pl.program_id(0) * step_heads + head) * HEAD, HEAD)
        for block in range(GROUPS):
            span = pl.ds(block * keys, keys)
            turned = spin(dk_acc[span, lanes] * softmax_scale, key_cos[span, :], key_sin[span, :])
            dkv_ref[span, pl.ds(first_lane, HEAD)] = turned.astype(jnp.bfloat16)
            dkv_ref[span, pl.ds(half + first_lane, HEAD)] = dv_acc[span, lanes].astype(jnp.bfloat16)


def whole_block(shape):
    return pl.BlockSpec(shape, lambda h, first: (0,) * len(shape))


def attention_forward(queries, starts, keys_all, values_all, key_info, query_info, heads):
    sets, total_rows, tokens = len(queries), queries[0].shape[0], keys_all.shape[0]
    rows, keys = total_rows // GROUPS, tokens // GROUPS
    step_heads = 2
    wide = step_heads * HEAD
    scale = HEAD ** (-0.5) * LOG2E
    query_specs = [
        pl.BlockSpec((total_rows, wide), lambda h, first, n=n: (0, first[n] + h)) for n in range(sets)
    ]
    plain = pl.BlockSpec((total_rows, wide), lambda h, first: (0, h))
    side = pl.BlockSpec((tokens, wide), lambda h, first: (0, h))
    return pl.pallas_call(
        functools.partial(attention_forward_body, sets, step_heads, rows, keys, scale),
        grid_spec=pltpu.PrefetchScalarGridSpec(
            num_scalar_prefetch=1,
            grid=(heads // step_heads,),
            in_specs=query_specs
            + [side, side, whole_block(key_info.shape), whole_block(query_info.shape)],
            out_specs=[plain] * sets
            + [pl.BlockSpec((step_heads, GROUPS, 1, sets * rows), lambda h, first: (h, 0, 0, 0))],
            scratch_shapes=[
                pltpu.VMEM((GROUPS * (GROUPS + 1) // 2, keys, sets * rows), jnp.float32),
                pltpu.VMEM((step_heads, GROUPS, HEAD, keys), jnp.bfloat16),
            ],
        ),
        out_shape=[jax.ShapeDtypeStruct((total_rows, heads * HEAD), jnp.bfloat16)] * sets
        + [jax.ShapeDtypeStruct((heads, GROUPS, 1, sets * rows), jnp.float32)],
        compiler_params=pltpu.CompilerParams(vmem_limit_bytes=VMEM_BYTES),
        name="attention_forward",
    )(starts, *queries, keys_all, values_all, key_info, query_info)


def attention_backward(
    queries, starts, grads, outs, keys_all, values_all, lse, key_info, query_info, key_tables, row_tables, heads
):
    sets, total_rows, tokens = len(queries), queries[0].shape[0], keys_all.shape[0]
    rows, keys = total_rows // GROUPS, tokens // GROUPS
    step_heads = 1
    wide = step_heads * HEAD
    scale = HEAD ** (-0.5) * LOG2E
    shifted = [
        pl.BlockSpec((total_rows, wide), lambda h, first, n=n: (0, first[n] + h)) for n in range(sets)
    ]
    plain = pl.BlockSpec((total_rows, wide), lambda h, first: (0, h))
    side = pl.BlockSpec((tokens, wide), lambda h, first: (0, h))
    return pl.pallas_call(
        functools.partial(attention_backward_body, sets, step_heads, rows, keys, scale),
        grid_spec=pltpu.PrefetchScalarGridSpec(
            num_scalar_prefetch=1,
            grid=(heads // step_heads,),
            in_specs=shifted
            + shifted
            + [plain] * sets
            + [
                side,
                side,
                pl.BlockSpec((step_heads, GROUPS, 1, sets * rows), lambda h, first: (h, 0, 0, 0)),
                whole_block(key_info.shape),
                whole_block(query_info.shape),
                whole_block((tokens, HEAD)),
                whole_block((tokens, HEAD)),
            ]
            + [whole_block((total_rows, HEAD))] * (2 * sets),
            out_specs=[plain] * sets + [whole_block((tokens, 2 * heads * HEAD))],
            scratch_shapes=[
                pltpu.VMEM((GROUPS * (GROUPS + 1) // 2, keys, sets * rows), jnp.float32),
                pltpu.VMEM((step_heads, GROUPS, HEAD, keys), jnp.bfloat16),
                pltpu.VMEM((tokens, wide), jnp.float32),
                pltpu.VMEM((tokens, wide), jnp.float32),
            ],
        ),
        out_shape=[jax.ShapeDtypeStruct((total_rows, heads * HEAD), jnp.bfloat16)] * sets
        + [jax.ShapeDtypeStruct((tokens, 2 * heads * HEAD), jnp.bfloat16)],
        compiler_params=pltpu.CompilerParams(vmem_limit_bytes=VMEM_BYTES),
        name="attention_backward",
    )(
        starts,
        *queries,
        *grads,
        *outs,
        keys_all,
        values_all,
        lse,
        key_info,
        query_info,
        *key_tables,
        *[table for pair in row_tables for table in pair],
    )


def project_body(plan_ref, hidden_ref, weight_ref, cos_ref, sin_ref, out_ref, x_ref):
    sources, capacity = plan_ref.shape[0], plan_ref.shape[1]
    bundle = max(1, sources * capacity // GROUPS // capacity)
    tile = bundle * capacity

    @pl.when(pl.program_id(0) == 0)
    def _():
        for group in range(sources // bundle):
            parts = [
                dot_nn(plan_ref[group * bundle + n], hidden_ref[group * bundle + n]) for n in range(bundle)
            ]
            x_ref[pl.ds(group * tile, tile), :] = jnp.concatenate(parts, axis=0).astype(jnp.bfloat16)

    for at in range(0, x_ref.shape[0], tile):
        span = pl.ds(at, tile)
        product = dot_nn(x_ref[span, :], weight_ref[...])
        for lane in range(0, out_ref.shape[1], HEAD):
            turned = spin(product[:, lane : lane + HEAD], cos_ref[span, :], sin_ref[span, :])
            out_ref[span, lane : lane + HEAD] = turned.astype(jnp.bfloat16)


def project_queries(plan, hidden, weight, tables):
    sources, capacity, row_count = plan.shape
    depth, columns = weight.shape
    rows = sources * capacity
    block = 512
    return pl.pallas_call(
        project_body,
        grid=(columns // block,),
        in_specs=[
            pl.BlockSpec((sources, capacity, row_count), lambda j: (0, 0, 0)),
            pl.BlockSpec((sources, row_count, depth), lambda j: (0, 0, 0)),
            pl.BlockSpec((depth, block), lambda j: (0, j)),
            pl.BlockSpec((rows, HEAD), lambda j: (0, 0)),
            pl.BlockSpec((rows, HEAD), lambda j: (0, 0)),
        ],
        out_specs=[
            pl.BlockSpec((rows, block), lambda j: (0, j)),
            pl.BlockSpec((rows, depth), lambda j: (0, 0)),
        ],
        out_shape=[
            jax.ShapeDtypeStruct((rows, columns), jnp.bfloat16),
            jax.ShapeDtypeStruct((rows, depth), jnp.bfloat16),
        ],
        compiler_params=pltpu.CompilerParams(vmem_limit_bytes=VMEM_BYTES),
        name="project_queries",
    )(plan, hidden, weight, *tables)


def keys_values_body(half, order_ref, x_ref, weight_ref, cos_ref, sin_ref, key_ref, value_ref):
    rows = x_ref.shape[1]
    for source in range(x_ref.shape[0]):
        span = pl.ds(source * rows, rows)
        product = dot_nn(x_ref[source], weight_ref[0])
        for lane in range(0, half, HEAD):
            turned = spin(product[:, lane : lane + HEAD], cos_ref[span, :], sin_ref[span, :])
            key_ref[span, lane : lane + HEAD] = turned.astype(jnp.bfloat16)
        value_ref[span, :] = product[:, half:].astype(jnp.bfloat16)


def project_keys_values(hidden, weights, tables, order):
    sources, rows, unused = hidden.shape
    parts, depth, columns = weights.shape
    half, tokens = columns // 2, sources * rows
    return pl.pallas_call(
        functools.partial(keys_values_body, half),
        grid_spec=pltpu.PrefetchScalarGridSpec(
            num_scalar_prefetch=1,
            grid=(parts,),
            in_specs=[
                pl.BlockSpec((sources, rows, depth), lambda j, order: (0, 0, 0)),
                pl.BlockSpec((1, depth, columns), lambda j, order: (j, 0, 0)),
                pl.BlockSpec((tokens, HEAD), lambda j, order: (0, 0)),
                pl.BlockSpec((tokens, HEAD), lambda j, order: (0, 0)),
            ],
            out_specs=[pl.BlockSpec((tokens, half), lambda j, order: (0, order[j]))] * 2,
        ),
        out_shape=[jax.ShapeDtypeStruct((tokens, parts * half), jnp.bfloat16)] * 2,
        compiler_params=pltpu.CompilerParams(vmem_limit_bytes=VMEM_BYTES),
        name="project_keys_values",
    )(order, hidden, weights, *tables)


def merge_body(tile, order_ref, plan_ref, slots_ref, dk_ref, dv_ref, weight_ref, out_ref, acc_ref):
    part = pl.program_id(1)
    sources, rows = plan_ref.shape[0], plan_ref.shape[1]
    ck = dk_ref.shape[1]

    @pl.when(part == 0)
    def _():
        for source in range(sources):
            acc_ref[pl.ds(source * rows, rows), :] = dot_nn(plan_ref[source], slots_ref[source])

    last = part == pl.num_programs(1) - 1
    for at in range(0, acc_ref.shape[0], tile):
        span = pl.ds(at, tile)
        acc_ref[span, :] += dot_nt(dk_ref[span, :], weight_ref[0, :, :ck]) + dot_nt(
            dv_ref[span, :], weight_ref[0, :, ck:]
        )

    @pl.when(last)
    def _():
        out_ref[...] = acc_ref[...].astype(jnp.bfloat16)


def merge_hidden_grads(plan, slots, grads, weights, order):
    sources, rows, capacity = plan.shape
    parts, depth, columns = weights.shape
    ck, tokens = columns // 2, sources * rows
    wide = depth // 2
    return pl.pallas_call(
        functools.partial(merge_body, tokens // GROUPS),
        grid_spec=pltpu.PrefetchScalarGridSpec(
            num_scalar_prefetch=1,
            grid=(2, parts),
            in_specs=[
                pl.BlockSpec((sources, rows, capacity), lambda i, j, order: (0, 0, 0)),
                pl.BlockSpec((sources, capacity, wide), lambda i, j, order: (0, 0, i)),
                pl.BlockSpec((tokens, ck), lambda i, j, order: (0, order[j])),
                pl.BlockSpec((tokens, ck), lambda i, j, order: (0, parts + order[j])),
                pl.BlockSpec((1, wide, columns), lambda i, j, order: (j, i, 0)),
            ],
            out_specs=pl.BlockSpec((tokens, wide), lambda i, j, order: (0, i)),
            scratch_shapes=[pltpu.VMEM((tokens, wide), jnp.float32)],
        ),
        out_shape=jax.ShapeDtypeStruct((tokens, depth), jnp.bfloat16),
        compiler_params=pltpu.CompilerParams(vmem_limit_bytes=VMEM_BYTES),
        name="merge_hidden_grads",
    )(order, plan, slots, grads, grads, weights)


def mesh_device(index):
    return {"expert": index}


def chip_order(chip, step):
    flip = chip // 2
    near = chip + flip * (3 - 2 * chip)
    place = step + near * (1 - 2 * step) if step < 2 else step
    return place + flip * (3 - 2 * place)


def far_order(chip, step):
    return chip_order(chip, 3 - step)


def is_middle(chip):
    flip = chip // 2
    return chip + flip * (3 - 2 * chip)


def crossing_order(chip, step):
    end, middle = chip_order(chip, step), chip_order(chip, (2, 3, 1, 0)[step])
    return end + is_middle(chip) * (middle - end)


def enter(devices, me):
    barrier = pltpu.get_barrier_semaphore()
    for step in range(1, devices):
        pl.semaphore_signal(
            barrier,
            inc=1,
            device_id=mesh_device(lax.rem(me + step, devices)),
            device_id_type=pl.DeviceIdType.MESH,
        )
    pl.semaphore_wait(barrier, devices - 1)


def remote(source, target, send, recv, device):
    return pltpu.make_async_remote_copy(
        src_ref=source,
        dst_ref=target,
        send_sem=send,
        recv_sem=recv,
        device_id=mesh_device(device),
        device_id_type=pl.DeviceIdType.MESH,
    )


class Dispatch:
    def __init__(self, me, order, slots, landing, local_sem, send, recv, pass_send, pass_recv):
        self.me, self.chip, self.core, self.order = me, me // 2, lax.rem(me, 2), order
        self.sending = stagger_order if order is stagger_order else chip_order
        self.slots, self.landing = slots, landing
        self.local_sem, self.send, self.recv = local_sem, send, recv
        self.pass_send, self.pass_recv = pass_send, pass_recv
        self.rows, self.half = slots.shape[1], slots.shape[2] // 2

    def columns(self, core):
        return pl.ds(pl.multiple_of(core * self.half, 128), self.half)

    def place(self, source, core):
        rows = pl.ds(pl.multiple_of(lax.rem(source, 2) * self.rows, 16), self.rows)
        return self.landing.at[source // 2, rows, self.columns(core)]

    def direct(self, target):
        core = lax.rem(target, 2)
        offset = lax.rem(target - self.me + 8, 8)
        return remote(
            self.slots.at[target // 2, :, self.columns(core)],
            self.place(self.me, core),
            self.send.at[offset],
            self.recv.at[offset],
            target,
        )

    def sends(self, step):
        chip = self.sending(self.chip, step)
        targets = [2 * chip + self.core, 2 * chip + 1 - self.core] if step else [self.me + 1 - 2 * self.core]
        return [self.direct(target) for target in targets]

    def local(self):
        return pltpu.make_async_copy(
            self.slots.at[self.chip, :, self.columns(self.core)],
            self.place(self.me, self.core),
            self.local_sem,
        )

    def start_local(self):
        self.local().start()

    def start(self, steps):
        for step in steps:
            for copy in self.sends(step):
                copy.start()

    def sent(self, steps):
        for step in steps:
            for copy in self.sends(step):
                copy.wait_send()

    def pass_on(self, source):
        place = self.place(source, self.core)
        return remote(
            place, place, self.pass_send.at[source], self.pass_recv.at[source], self.me + 1 - 2 * self.core
        )

    def arrive(self, step):
        chip = self.order(self.chip, step)
        for source in (2 * chip + self.core, 2 * chip + 1 - self.core):
            offset = lax.rem(self.me - source + 8, 8)

            @pl.when(offset == 0)
            def _():
                self.local().wait()

            @pl.when(offset != 0)
            def _(source=source, offset=offset):
                place = self.place(source, self.core)
                remote(place, place, self.send.at[offset], self.recv.at[offset], self.me).wait_recv()

            self.pass_on(source).start()

    def ready(self, step):
        chip = self.order(self.chip, step)
        for source in (2 * chip, 2 * chip + 1):
            place = self.place(source, 1 - self.core)
            remote(
                place, place, self.pass_send.at[source], self.pass_recv.at[source], self.me
            ).wait_recv()
        return chip

    def passed_on(self):
        for source in range(8):
            self.pass_on(source).wait_send()


class Collect:
    def __init__(
        self, me, order, own_steps, kept, passing, passed, total, back, local_sem, pass_send, pass_recv, send, recv
    ):
        self.me, self.chip, self.core = me, me // 2, lax.rem(me, 2)
        self.order, self.own_steps = order, own_steps
        self.kept, self.passing, self.passed, self.total, self.back = kept, passing, passed, total, back
        self.local_sem, self.pass_send, self.pass_recv = local_sem, pass_send, pass_recv
        self.send, self.recv = send, recv
        self.rows, self.half = back.shape[1], back.shape[2] // 2

    def swap(self, step):
        return remote(
            self.passing.at[step % 2],
            self.passed.at[step],
            self.pass_send.at[step],
            self.pass_recv.at[step],
            self.me + 1 - 2 * self.core,
        )

    def place(self, chip, core):
        return self.back.at[chip, :, pl.ds(pl.multiple_of(core * self.half, 128), self.half)]

    def local(self, step, source_core):
        return pltpu.make_async_copy(
            self.total.at[step, pl.ds(pl.multiple_of(source_core * self.rows, 16), self.rows), :],
            self.place(self.chip, self.core),
            self.local_sem,
        )

    def outgoing(self, step, source):
        rows = pl.ds(pl.multiple_of(lax.rem(source, 2) * self.rows, 16), self.rows)
        offset = lax.rem(source - self.me + 8, 8)
        return remote(
            self.total.at[step, rows, :],
            self.place(self.chip, self.core),
            self.send.at[offset],
            self.recv.at[offset],
            source,
        )

    def block(self, step):
        return self.order(self.chip, step)

    def each(self, step, own, other):
        chip = self.block(step)
        for source in (2 * chip + self.core, 2 * chip + 1 - self.core):
            if step not in self.own_steps:
                other(source)
                continue

            @pl.when(source == self.me)
            def _():
                own()

            @pl.when(source != self.me)
            def _(source=source):
                other(source)

    def settle(self, step):
        self.swap(step).wait_recv()
        tile = 2 * self.rows // 4
        for at in range(0, 2 * self.rows, tile):
            span = pl.ds(at, tile)
            summed = self.kept[span, :] + self.passed[step, span, :].astype(jnp.float32)
            self.total[step, span, :] = summed.astype(jnp.bfloat16)
        self.each(
            step,
            lambda: self.local(step, self.core).start(),
            lambda source: self.outgoing(step, source).start(),
        )

    def finish(self):
        for step in range(4):
            if step >= 2:
                self.swap(step).wait_send()
            self.each(
                step,
                lambda step=step: self.local(step, self.core).wait(),
                lambda source, step=step: self.outgoing(step, source).wait_send(),
            )
        for offset in range(1, 8):
            source = lax.rem(self.me + 8 - offset, 8)
            place = self.place(source // 2, lax.rem(source, 2))
            remote(place, place, self.send.at[offset], self.recv.at[offset], self.me).wait_recv()


def ffn_forward_body(
    chunk,
    slots,
    gate_hbm,
    up_hbm,
    down_hbm,
    rows_out,
    gate_out,
    up_out,
    act_out,
    back,
    gate,
    up,
    down,
    landing,
    pre_stage,
    act,
    kept,
    passing,
    passed,
    total,
    weight_sem,
    stage_sem,
    act_sem,
    rows_sem,
    local_sem,
    send,
    recv,
    pass_send,
    pass_recv,
    swap_send,
    swap_recv,
    out_send,
    out_recv,
):
    me = lax.axis_index("expert")
    enter(8, me)
    loads = [
        pltpu.make_async_copy(source, target, weight_sem.at[n])
        for n, (source, target) in enumerate(((gate_hbm, gate), (up_hbm, up), (down_hbm, down)))
    ]
    dispatch = Dispatch(me, crossing_order, slots, landing, local_sem.at[0], send, recv, pass_send, pass_recv)
    collect = Collect(
        me, crossing_order, (0, 3), kept, passing, passed, total, back, local_sem.at[1], swap_send, swap_recv, out_send, out_recv
    )
    middle = is_middle(me // 2)
    dispatch.start_local()
    dispatch.start((0, 1))

    @pl.when(middle == 1)
    def _():
        dispatch.start((2,))

    for load in loads:
        load.start()
    block = landing.shape[1]
    hidden_units = gate.shape[1]
    chunks = hidden_units // chunk
    half = back.shape[2] // 2

    def stage_copies(chip, part, slot):
        span = pl.ds(pl.multiple_of(chip * block, 16), block)
        columns = pl.ds(pl.multiple_of(part * chunk, 128), chunk)
        return [
            pltpu.make_async_copy(
                pre_stage.at[slot, n], out.at[span, columns], stage_sem.at[slot, n]
            )
            for n, out in enumerate((gate_out, up_out))
        ]

    def act_copy(chip, step):
        span = pl.ds(pl.multiple_of(chip * block, 16), block)
        return pltpu.make_async_copy(act.at[step % 2], act_out.at[span, :], act_sem.at[step % 2])

    def rows_copy(chip, step):
        span = pl.ds(pl.multiple_of(chip * block, 16), block)
        return pltpu.make_async_copy(landing.at[chip], rows_out.at[span, :], rows_sem.at[step])

    for step in range(4):
        if step == 0:
            dispatch.arrive(0)
        chip = dispatch.ready(step)
        rows_copy(chip, step).start()
        if step == 0:
            loads[0].wait()
            loads[1].wait()
        if step >= 2:
            act_copy(crossing_order(me // 2, step - 2), step - 2).wait()

        def hidden_part(part, carry, chip=chip, step=step):
            slot = lax.rem(part + step * chunks, 2)
            columns = pl.ds(pl.multiple_of(part * chunk, 128), chunk)

            @pl.when(part + step * chunks >= 2)
            def _():
                for copy in stage_copies(chip, part, slot):
                    copy.wait()

            gated = dot_nn(landing[chip], gate[:, columns])
            raised = dot_nn(landing[chip], up[:, columns])
            pre_stage[slot, 0] = gated.astype(jnp.bfloat16)
            pre_stage[slot, 1] = raised.astype(jnp.bfloat16)
            act[step % 2, :, columns] = (gated * jax.nn.sigmoid(gated) * raised).astype(jnp.bfloat16)
            for copy in stage_copies(chip, part, slot):
                copy.start()
            if step == 0:
                @pl.when((part == chunks // 3) & (middle == 0))
                def _():
                    dispatch.sent((1,))
                    dispatch.start((2,))

                @pl.when((part == chunks // 2) & (middle == 1))
                def _():
                    dispatch.sent((1, 2))
                    dispatch.start((3,))

            return carry

        lax.fori_loop(0, chunks, hidden_part, 0)
        act_copy(chip, step).start()
        if step == 0:
            loads[2].wait()
        else:
            collect.settle(step - 1)
        core = collect.core
        width = min(512, half)

        def far_part(part, carry, step=step):
            at = pl.multiple_of((1 - core) * half + part * width, 128)
            product = dot_nt(act[step % 2], down[pl.ds(at, width), :])
            passing[step % 2, :, pl.ds(pl.multiple_of(part * width, 128), width)] = product.astype(jnp.bfloat16)
            return carry

        def near_part(part, carry, step=step):
            at = pl.multiple_of(core * half + part * width, 128)
            product = dot_nt(act[step % 2], down[pl.ds(at, width), :])
            kept[:, pl.ds(pl.multiple_of(part * width, 128), width)] = product
            return carry

        if step >= 2:
            collect.swap(step - 2).wait_send()
        lax.fori_loop(0, half // width, far_part, 0)
        collect.swap(step).start()
        if step == 0:

            @pl.when(middle == 0)
            def _():
                dispatch.sent((2,))
                dispatch.start((3,))

        if step < 3:
            dispatch.arrive(step + 1)
        lax.fori_loop(0, half // width, near_part, 0)
    collect.settle(3)
    for step in (2, 3):
        act_copy(crossing_order(me // 2, step), step).wait()
    for step in range(4):
        rows_copy(crossing_order(me // 2, step), step).wait()
    for slot in range(2):
        for copy in stage_copies(0, 0, slot):
            copy.wait()
    dispatch.sent((0, 3))
    dispatch.passed_on()
    collect.finish()


def ffn_forward(slots, gate_weight, up_weight, down_weight):
    chips, capacity, depth = slots.shape
    hidden_units = gate_weight.shape[1]
    block = 2 * capacity
    chunk = 256 if hidden_units % 256 == 0 else 128
    half = depth // 2
    rows = chips * block
    any_space = pl.BlockSpec(memory_space=pl.ANY)
    bf = jnp.bfloat16
    dma = pltpu.SemaphoreType.DMA
    return pl.pallas_call(
        functools.partial(ffn_forward_body, chunk),
        in_specs=[any_space] * 4,
        out_specs=[any_space] * 5,
        out_shape=[
            jax.ShapeDtypeStruct((rows, depth), bf),
            jax.ShapeDtypeStruct((rows, hidden_units), bf),
            jax.ShapeDtypeStruct((rows, hidden_units), bf),
            jax.ShapeDtypeStruct((rows, hidden_units), bf),
            jax.ShapeDtypeStruct((chips, capacity, depth), bf),
        ],
        scratch_shapes=[
            pltpu.VMEM((depth, hidden_units), bf),
            pltpu.VMEM((depth, hidden_units), bf),
            pltpu.VMEM((depth, hidden_units), bf),
            pltpu.VMEM((chips, block, depth), bf),
            pltpu.VMEM((2, 2, block, chunk), bf),
            pltpu.VMEM((2, block, hidden_units), bf),
            pltpu.VMEM((block, half), jnp.float32),
            pltpu.VMEM((2, block, half), bf),
            pltpu.VMEM((chips, block, half), bf),
            pltpu.VMEM((chips, block, half), bf),
            dma((3,)),
            dma((2, 2)),
            dma((2,)),
            dma((4,)),
            dma((2,)),
            dma((8,)),
            dma((8,)),
            dma((8,)),
            dma((8,)),
            dma((4,)),
            dma((4,)),
            dma((8,)),
            dma((8,)),
        ],
        compiler_params=pltpu.CompilerParams(
            collective_id=1, has_side_effects=True, vmem_limit_bytes=VMEM_BYTES
        ),
        name="ffn_forward",
    )(slots, gate_weight, up_weight, down_weight)


def stagger_order(chip, step):
    if step < 2:
        return chip_order(chip, step)
    end, middle = chip_order(chip, 5 - step), chip_order(chip, step)
    return end + is_middle(chip) * (middle - end)


def send_rows_body(
    slots,
    act_hbm,
    rows_out,
    grad_out,
    landing,
    act,
    total,
    stage,
    act_sem,
    rows_sem,
    stage_sem,
    local_sem,
    send,
    recv,
    pass_send,
    pass_recv,
):
    me = lax.axis_index("expert")
    enter(8, me)
    dispatch = Dispatch(me, stagger_order, slots, landing, local_sem.at[0], send, recv, pass_send, pass_recv)
    dispatch.start_local()
    dispatch.start((0, 1, 2))
    block = landing.shape[1]
    width = stage.shape[1]
    parts = landing.shape[2] // width

    def span_of(step):
        return pl.ds(pl.multiple_of(stagger_order(me // 2, step) * block, 16), block)

    def act_copy(step):
        return pltpu.make_async_copy(
            act_hbm.at[span_of(step), :], act.at[pl.ds(step * block, block), :], act_sem.at[step]
        )

    def rows_copy(step):
        chip = stagger_order(me // 2, step)
        return pltpu.make_async_copy(landing.at[chip], rows_out.at[chip], rows_sem.at[step])

    def stage_copy(part):
        slot = lax.rem(part, 2)
        span = pl.ds(pl.multiple_of(part * width, 16), width)
        return pltpu.make_async_copy(stage.at[slot], grad_out.at[span, :], stage_sem.at[slot])

    for step in range(4):
        act_copy(step).start()
    for steps in ((0, 1), (2,), (3,)):
        for step in steps:
            dispatch.arrive(step)
        chips = [dispatch.ready(step) for step in steps]
        for step in steps:
            rows_copy(step).start()
            act_copy(step).wait()

        def one(part, carry, steps=steps, chips=chips):
            columns = pl.ds(pl.multiple_of(part * width, 128), width)
            rows = [landing[chip, :, columns] for chip in chips]
            rows = rows[0] if len(rows) == 1 else jnp.concatenate(rows, axis=0)
            turned = rows.astype(jnp.float32).T.astype(jnp.bfloat16)
            product = dot_nn(turned, act[pl.ds(steps[0] * block, len(steps) * block), :])
            span = pl.ds(pl.multiple_of(part * width, 16), width)
            if steps[0] == 0:
                total[span, :] = product

                @pl.when(part == 0)
                def _():
                    dispatch.sent((2,))
                    dispatch.start((3,))

                return carry
            if steps[0] == 2:
                total[span, :] += product
                return carry

            @pl.when(part >= 2)
            def _():
                stage_copy(part - 2).wait()

            stage[lax.rem(part, 2)] = (total[span, :] + product).astype(jnp.bfloat16)
            stage_copy(part).start()
            return carry

        lax.fori_loop(0, parts, one, 0)
    for part in (parts - 2, parts - 1):
        stage_copy(part).wait()
    for step in range(4):
        rows_copy(step).wait()
    dispatch.sent((0, 1, 3))
    dispatch.passed_on()


def send_rows(slots, act):
    chips, capacity, depth = slots.shape
    rows, hidden_units = act.shape
    block = 2 * capacity
    width = min(256, depth // 2)
    any_space = pl.BlockSpec(memory_space=pl.ANY)
    bf = jnp.bfloat16
    dma = pltpu.SemaphoreType.DMA
    return pl.pallas_call(
        send_rows_body,
        in_specs=[any_space] * 2,
        out_specs=[any_space] * 2,
        out_shape=[
            jax.ShapeDtypeStruct((chips, block, depth), bf),
            jax.ShapeDtypeStruct((depth, hidden_units), bf),
        ],
        scratch_shapes=[
            pltpu.VMEM((chips, block, depth), bf),
            pltpu.VMEM((rows, hidden_units), bf),
            pltpu.VMEM((depth, hidden_units), jnp.float32),
            pltpu.VMEM((2, width, hidden_units), bf),
            dma((4,)),
            dma((4,)),
            dma((2,)),
            dma((1,)),
            dma((8,)),
            dma((8,)),
            dma((8,)),
            dma((8,)),
        ],
        compiler_params=pltpu.CompilerParams(
            collective_id=2, has_side_effects=True, vmem_limit_bytes=VMEM_BYTES
        ),
        name="send_rows",
    )(slots, act)


def ffn_backward_body(
    chunk,
    grad_rows,
    gate_in,
    up_in,
    gate_hbm,
    up_hbm,
    down_hbm,
    dgate_out,
    dup_out,
    back,
    gate,
    up,
    down,
    grad,
    pre_stage,
    pair,
    kept,
    passing,
    passed,
    total,
    weight_sem,
    grad_sem,
    stage_sem,
    pair_sem,
    local_sem,
    swap_send,
    swap_recv,
    out_send,
    out_recv,
):
    me = lax.axis_index("expert")
    enter(8, me)
    collect = Collect(
        me, far_order, (3,), kept, passing, passed, total, back, local_sem.at[0], swap_send, swap_recv, out_send, out_recv
    )
    loads = [
        pltpu.make_async_copy(source, target, weight_sem.at[n])
        for n, (source, target) in enumerate(((down_hbm, down), (gate_hbm, gate), (up_hbm, up)))
    ]
    block = grad.shape[1]
    hidden_units = gate.shape[1]
    chunks = hidden_units // chunk
    half = back.shape[2] // 2
    width = min(512, half)

    def span_of(chip):
        return pl.ds(pl.multiple_of(chip * block, 16), block)

    def grad_copy(step):
        return pltpu.make_async_copy(
            grad_rows.at[span_of(collect.block(step)), :], grad.at[step % 2], grad_sem.at[step % 2]
        )

    def stage_copies(chip, part, slot):
        columns = pl.ds(pl.multiple_of(part * chunk, 128), chunk)
        return [
            pltpu.make_async_copy(
                source.at[span_of(chip), columns], pre_stage.at[slot, n], stage_sem.at[slot, n]
            )
            for n, source in enumerate((gate_in, up_in))
        ]

    def pair_copies(chip):
        return [
            pltpu.make_async_copy(pair.at[n], out.at[span_of(chip), :], pair_sem.at[n])
            for n, out in enumerate((dgate_out, dup_out))
        ]

    grad_copy(0).start()
    loads[0].start()
    for copy in stage_copies(collect.block(0), 0, 0):
        copy.start()
    loads[1].start()
    loads[2].start()
    loads[0].wait()
    for step in range(4):
        chip = collect.block(step)
        grad_copy(step).wait()
        if step < 3:
            grad_copy(step + 1).start()
        if step > 0:
            for copy in pair_copies(collect.block(step - 1)):
                copy.wait()

        def hidden_part(part, carry, chip=chip, step=step):
            slot = lax.rem(part, 2)
            columns = pl.ds(pl.multiple_of(part * chunk, 128), chunk)
            for copy in stage_copies(chip, part, slot):
                copy.wait()

            @pl.when(part + 1 < chunks)
            def _():
                for copy in stage_copies(chip, part + 1, 1 - slot):
                    copy.start()

            upstream = dot_nn(grad[step % 2], down[:, columns])
            gated = pre_stage[slot, 0].astype(jnp.float32)
            raised = pre_stage[slot, 1].astype(jnp.float32)
            sigmoid = jax.nn.sigmoid(gated)
            scaled = upstream * sigmoid
            pair[0, :, columns] = (scaled * raised * (1.0 + gated * (1.0 - sigmoid))).astype(jnp.bfloat16)
            pair[1, :, columns] = (scaled * gated).astype(jnp.bfloat16)
            return carry

        lax.fori_loop(0, chunks, hidden_part, 0)
        for copy in pair_copies(chip):
            copy.start()
        if step < 3:
            for copy in stage_copies(collect.block(step + 1), 0, 0):
                copy.start()
        if step == 0:
            loads[1].wait()
            loads[2].wait()
        else:
            collect.settle(step - 1)
        core = collect.core

        def product(at):
            return dot_nt(pair[0], gate[pl.ds(at, width), :]) + dot_nt(pair[1], up[pl.ds(at, width), :])

        def far_part(part, carry, step=step):
            at = pl.multiple_of((1 - core) * half + part * width, 128)
            columns = pl.ds(pl.multiple_of(part * width, 128), width)
            passing[step % 2, :, columns] = product(at).astype(jnp.bfloat16)
            return carry

        def near_part(part, carry, step=step):
            at = pl.multiple_of(core * half + part * width, 128)
            kept[:, pl.ds(pl.multiple_of(part * width, 128), width)] = product(at)
            return carry

        if step >= 2:
            collect.swap(step - 2).wait_send()
        lax.fori_loop(0, half // width, far_part, 0)
        collect.swap(step).start()
        lax.fori_loop(0, half // width, near_part, 0)
    collect.settle(3)
    for copy in pair_copies(collect.block(3)):
        copy.wait()
    collect.finish()


def ffn_backward(grad_rows, gate_pre, up_pre, gate_weight, up_weight, down_weight, capacity):
    rows, depth = grad_rows.shape
    hidden_units = gate_weight.shape[1]
    block = 2 * capacity
    chips = rows // block
    chunk = hidden_units // 2 if hidden_units % 256 == 0 else 128
    half = depth // 2
    any_space = pl.BlockSpec(memory_space=pl.ANY)
    bf = jnp.bfloat16
    dma = pltpu.SemaphoreType.DMA
    return pl.pallas_call(
        functools.partial(ffn_backward_body, chunk),
        in_specs=[any_space] * 6,
        out_specs=[any_space] * 3,
        out_shape=[
            jax.ShapeDtypeStruct((rows, hidden_units), bf),
            jax.ShapeDtypeStruct((rows, hidden_units), bf),
            jax.ShapeDtypeStruct((chips, capacity, depth), bf),
        ],
        scratch_shapes=[
            pltpu.VMEM((depth, hidden_units), bf),
            pltpu.VMEM((depth, hidden_units), bf),
            pltpu.VMEM((depth, hidden_units), bf),
            pltpu.VMEM((2, block, depth), bf),
            pltpu.VMEM((2, 2, block, chunk), bf),
            pltpu.VMEM((2, block, hidden_units), bf),
            pltpu.VMEM((block, half), jnp.float32),
            pltpu.VMEM((2, block, half), bf),
            pltpu.VMEM((chips, block, half), bf),
            pltpu.VMEM((chips, block, half), bf),
            dma((3,)),
            dma((2,)),
            dma((2, 2)),
            dma((2,)),
            dma((1,)),
            dma((4,)),
            dma((4,)),
            dma((8,)),
            dma((8,)),
        ],
        compiler_params=pltpu.CompilerParams(
            collective_id=3, has_side_effects=True, vmem_limit_bytes=VMEM_BYTES
        ),
        name="ffn_backward",
    )(grad_rows, gate_pre, up_pre, gate_weight, up_weight, down_weight)


def send_slots_body(
    slots, rows_hbm, grads_hbm, landing, grad_out, rows_v, grads_v, stage, load_sem, stage_sem, local_sem, send, recv
):
    me = lax.axis_index("expert")
    enter(8, me)

    def outgoing(offset):
        target = lax.rem(me + offset, 8)
        return remote(slots.at[target], landing.at[me], send.at[offset], recv.at[offset], target)

    local = pltpu.make_async_copy(slots.at[me], landing.at[me], local_sem)
    for offset in range(1, 8):
        outgoing(offset).start()
    local.start()
    loads = [
        pltpu.make_async_copy(source, target, load_sem.at[n])
        for n, (source, target) in enumerate(((rows_hbm, rows_v), (grads_hbm, grads_v)))
    ]
    for load in loads:
        load.start()
    for load in loads:
        load.wait()
    width = stage.shape[1]
    blocks = rows_v.shape[1] // width

    def stage_copy(block):
        slot = lax.rem(block, 2)
        span = pl.ds(pl.multiple_of(block * width, 16), width)
        return pltpu.make_async_copy(stage.at[slot], grad_out.at[span, :], stage_sem.at[slot])

    def one(block, carry):
        @pl.when(block >= 2)
        def _():
            stage_copy(block - 2).wait()

        columns = pl.ds(pl.multiple_of(block * width, 128), width)
        turned = rows_v[:, columns].astype(jnp.float32).T.astype(jnp.bfloat16)
        stage[lax.rem(block, 2)] = dot_nn(turned, grads_v[...]).astype(jnp.bfloat16)
        stage_copy(block).start()
        return carry

    lax.fori_loop(0, blocks, one, 0)
    for block in (blocks - 2, blocks - 1):
        stage_copy(block).wait()
    local.wait()
    for offset in range(1, 8):
        outgoing(offset).wait_send()
        place = landing.at[lax.rem(me + 8 - offset, 8)]
        remote(place, place, send.at[offset], recv.at[offset], me).wait_recv()


def send_slots(slots, rows, grads):
    total, depth = rows.shape
    hidden_units = grads.shape[1]
    width = min(256, depth // 2)
    any_space = pl.BlockSpec(memory_space=pl.ANY)
    bf = jnp.bfloat16
    dma = pltpu.SemaphoreType.DMA
    return pl.pallas_call(
        send_slots_body,
        in_specs=[any_space] * 3,
        out_specs=[any_space] * 2,
        out_shape=[
            jax.ShapeDtypeStruct(slots.shape, bf),
            jax.ShapeDtypeStruct((depth, hidden_units), bf),
        ],
        scratch_shapes=[
            pltpu.VMEM((total, depth), bf),
            pltpu.VMEM((total, hidden_units), bf),
            pltpu.VMEM((2, width, hidden_units), bf),
            dma((2,)),
            dma((2,)),
            dma,
            dma((8,)),
            dma((8,)),
        ],
        compiler_params=pltpu.CompilerParams(
            collective_id=5, has_side_effects=True, vmem_limit_bytes=VMEM_BYTES
        ),
        name="send_slots",
    )(slots, rows, grads)


def merge_return_body(
    dp_axis,
    plan_hbm,
    slots_hbm,
    grads_hbm,
    weight_hbm,
    back,
    plan,
    slots,
    grads,
    weight,
    kept,
    passing,
    passed,
    total,
    load_sem,
    local_sem,
    swap_send,
    swap_recv,
    out_send,
    out_recv,
):
    me = lax.axis_index("expert")
    replica = lax.axis_index(dp_axis)
    enter(8, me)
    loads = [
        pltpu.make_async_copy(source, target, load_sem.at[n])
        for n, (source, target) in enumerate(
            ((plan_hbm, plan), (slots_hbm, slots), (grads_hbm, grads), (weight_hbm, weight))
        )
    ]
    for load in loads:
        load.start()
    collect = Collect(
        me, far_order, (3,), kept, passing, passed, total, back, local_sem.at[0], swap_send, swap_recv, out_send, out_recv
    )
    rows, half = collect.rows, collect.half
    parts, ck = weight.shape[0], weight.shape[2] // 2
    values_at = grads.shape[1] // 2
    width = min(512, half)
    for load in loads:
        load.wait()
    for step in range(4):
        chip = collect.block(step)
        span = pl.ds(pl.multiple_of(chip * 2 * rows, 16), 2 * rows)

        def product(at, chip=chip, span=span):
            columns = pl.ds(at, width)
            result = jnp.concatenate(
                [dot_nn(plan[2 * chip + n], slots[2 * chip + n, :, columns]) for n in range(2)], axis=0
            )
            for part in range(parts):
                low = lax.rem(replica, 2) + (part % 2) * (1 - 2 * lax.rem(replica, 2))
                high = replica // 2 + (part // 2) * (1 - 2 * (replica // 2))
                at_keys = pl.multiple_of((2 * high + low) * ck, 128)
                result += dot_nt(grads[span, pl.ds(at_keys, ck)], weight[part, columns, :ck])
                result += dot_nt(grads[span, pl.ds(values_at + at_keys, ck)], weight[part, columns, ck:])
            return result

        def far_part(part, carry, step=step, product=product):
            at = pl.multiple_of((1 - collect.core) * half + part * width, 128)
            columns = pl.ds(pl.multiple_of(part * width, 128), width)
            passing[step % 2, :, columns] = product(at).astype(jnp.bfloat16)
            return carry

        def near_part(part, carry, product=product):
            at = pl.multiple_of(collect.core * half + part * width, 128)
            kept[:, pl.ds(pl.multiple_of(part * width, 128), width)] = product(at)
            return carry

        if step >= 2:
            collect.swap(step - 2).wait_send()
        lax.fori_loop(0, half // width, far_part, 0)
        collect.swap(step).start()
        if step > 0:
            collect.settle(step - 1)
        lax.fori_loop(0, half // width, near_part, 0)
    collect.settle(3)
    collect.finish()


def merge_return(plan, slots, grads, weights):
    sources, rows, capacity = plan.shape
    parts, depth, columns = weights.shape
    tokens = sources * rows
    half = depth // 2
    any_space = pl.BlockSpec(memory_space=pl.ANY)
    bf = jnp.bfloat16
    dma = pltpu.SemaphoreType.DMA
    return pl.pallas_call(
        functools.partial(merge_return_body, "dp"),
        in_specs=[any_space] * 4,
        out_specs=any_space,
        out_shape=jax.ShapeDtypeStruct((sources // 2, rows, depth), bf),
        scratch_shapes=[
            pltpu.VMEM(plan.shape, bf),
            pltpu.VMEM(slots.shape, bf),
            pltpu.VMEM(grads.shape, bf),
            pltpu.VMEM(weights.shape, bf),
            pltpu.VMEM((2 * rows, half), jnp.float32),
            pltpu.VMEM((2, 2 * rows, half), bf),
            pltpu.VMEM((sources // 2, 2 * rows, half), bf),
            pltpu.VMEM((sources // 2, 2 * rows, half), bf),
            dma((4,)),
            dma((1,)),
            dma((4,)),
            dma((4,)),
            dma((8,)),
            dma((8,)),
        ],
        compiler_params=pltpu.CompilerParams(
            collective_id=6, has_side_effects=True, vmem_limit_bytes=VMEM_BYTES
        ),
        name="merge_return",
    )(plan, slots, grads, weights)


def return_order(chip, step):
    lower, upper = chip_order(chip, (2, 3, 1, 0)[step]), chip_order(chip, 3 - step)
    return lower + chip // 2 * (upper - lower)


def attention_send_body(
    scale,
    query_hbm,
    sibling_hbm,
    key_hbm,
    value_hbm,
    out_weight_hbm,
    key_info,
    query_info,
    own_out,
    sibling_out,
    rows_out,
    back,
    lse_ref,
    queries,
    siblings,
    keys_v,
    values_v,
    out_weight,
    bias_ref,
    flipped,
    own_stage,
    sibling_stage,
    arrived,
    rows_stage,
    sending,
    load_sem,
    own_sem,
    sibling_sem,
    rows_sem,
    local_sem,
    swap_send,
    swap_recv,
    out_send,
    out_recv,
):
    me = lax.axis_index("expert")
    chip, core = me // 2, lax.rem(me, 2)
    enter(8, me)
    half = keys_v.shape[1]
    rows = own_stage.shape[1]
    keys = keys_v.shape[0] // GROUPS
    heads = half // HEAD
    capacity = back.shape[1]
    own_columns = pl.ds(pl.multiple_of(core * half, 128), half)
    far_columns = pl.ds(pl.multiple_of((1 - core) * half, 128), half)
    loads = [
        pltpu.make_async_copy(source, target, load_sem.at[n])
        for n, (source, target) in enumerate(
            (
                (value_hbm, values_v),
                (key_hbm, keys_v),
                (query_hbm.at[:, own_columns], queries),
                (sibling_hbm, siblings),
                (out_weight_hbm, out_weight),
            )
        )
    ]
    for load in loads:
        load.start()
    fill_bias(bias_ref, key_info, query_info, keys)
    loads[0].wait()

    def flip(head, carry):
        lanes = pl.ds(pl.multiple_of(head * HEAD, HEAD), HEAD)
        for block in range(GROUPS):
            values = values_v[pl.ds(block * keys, keys), lanes].astype(jnp.float32)
            flipped[head, block] = values.T.astype(jnp.bfloat16)
        return carry

    lax.fori_loop(0, heads, flip, 0)
    for load in loads[1:4]:
        load.wait()

    def group_of(step):
        return return_order(chip, step)

    def span_of(step):
        return pl.ds(pl.multiple_of(group_of(step) * rows, 16), rows)

    def own_copy(step):
        return pltpu.make_async_copy(own_stage.at[step], own_out.at[span_of(step), :], own_sem.at[step])

    def sibling_copy(step):
        return pltpu.make_async_copy(
            sibling_stage.at[step], sibling_out.at[span_of(step), :], sibling_sem.at[step]
        )

    def rows_copy(step):
        return pltpu.make_async_copy(
            rows_stage.at[step], rows_out.at[span_of(step), :], rows_sem.at[step]
        )

    def swap(step):
        return remote(
            sibling_stage.at[step], arrived.at[step], swap_send.at[step], swap_recv.at[step], me + 1 - 2 * core
        )

    def outgoing(step, n):
        source = 2 * group_of(step) + n
        offset = lax.rem(source - me + 8, 8)
        return remote(sending.at[step, n], back.at[me], out_send.at[offset], out_recv.at[offset], source)

    def local(step, n):
        return pltpu.make_async_copy(sending.at[step, n], back.at[me], local_sem)

    def each(step, own, other):
        (own if step == 3 else other)(core)
        other(1 - core)

    def attend(step):
        group = group_of(step)
        first_block = group * (group + 1) // 2
        span = span_of(step)

        def head_pair(pair, carry):
            lanes = [pl.ds(pl.multiple_of((2 * pair + n) * HEAD, HEAD), HEAD) for n in range(2)]
            parts = [jnp.concatenate([queries[span, lane], siblings[span, lane]], axis=0) for lane in lanes]

            def one(block, state):
                at = pl.multiple_of(block * keys, 16)
                bias = bias_ref[first_block + block]
                result = []
                for n in range(2):
                    top, total, mixed = state[3 * n : 3 * n + 3]
                    scores = dot_nt(keys_v[pl.ds(at, keys), lanes[n]], parts[n]) * scale + bias
                    new_top = jnp.maximum(top, jnp.max(scores, axis=0, keepdims=True))
                    fade = jnp.exp2(top - new_top)
                    probs = jnp.exp2(scores - new_top)
                    total = total * fade + jnp.sum(probs, axis=0, keepdims=True)
                    mixed = mixed * fade + dot_nn(flipped[2 * pair + n, block], probs.astype(jnp.bfloat16))
                    result += [new_top, total, mixed]
                return tuple(result)

            start = (
                jnp.full((1, 2 * rows), -1e30, jnp.float32),
                jnp.zeros((1, 2 * rows), jnp.float32),
                jnp.zeros((HEAD, 2 * rows), jnp.float32),
            ) * 2
            final = lax.fori_loop(0, group + 1, one, start)
            for n in range(2):
                top, total, mixed = final[3 * n : 3 * n + 3]
                lse_ref[2 * pair + n, group] = top + jnp.log2(total)
                result = (mixed / total).T.astype(jnp.bfloat16)
                own_stage[step, :, lanes[n]] = result[:rows]
                sibling_stage[step, :, lanes[n]] = result[rows:]
            return carry

        lax.fori_loop(0, heads // 2, head_pair, 0)
        swap(step).start()
        own_copy(step).start()
        sibling_copy(step).start()

    def settle(step):
        swap(step).wait_recv()
        rows_stage[step, :, own_columns] = own_stage[step]
        rows_stage[step, :, far_columns] = arrived[step]
        rows_copy(step).start()
        width = 512
        for at in range(0, back.shape[2], min(width, back.shape[2])):
            columns = pl.ds(at, min(width, back.shape[2]))
            product = dot_nt(rows_stage[step], out_weight[columns, :])
            for n in range(2):
                part = product[n * capacity : (n + 1) * capacity]
                sending[step, n, :, columns] = part.astype(jnp.bfloat16)
        each(step, lambda n: local(step, n).start(), lambda n: outgoing(step, n).start())

    for step in range(4):
        attend(step)
        if step == 0:
            loads[4].wait()
        settle(step)
    for step in range(4):
        swap(step).wait_send()
        own_copy(step).wait()
        sibling_copy(step).wait()
        rows_copy(step).wait()
        each(step, lambda n, step=step: local(step, n).wait(), lambda n, step=step: outgoing(step, n).wait_send())
    for offset in range(1, 8):
        place = back.at[lax.rem(me + 8 - offset, 8)]
        remote(place, place, out_send.at[offset], out_recv.at[offset], me).wait_recv()


def attention_send(queries, siblings, keys_all, values_all, out_weight, key_info, query_info, capacity):
    total_rows, width = queries.shape
    tokens, half = keys_all.shape
    depth = out_weight.shape[0]
    rows, keys, heads = total_rows // GROUPS, tokens // GROUPS, half // HEAD
    any_space = pl.BlockSpec(memory_space=pl.ANY)
    here = pl.BlockSpec(memory_space=pltpu.VMEM)
    bf = jnp.bfloat16
    dma = pltpu.SemaphoreType.DMA
    return pl.pallas_call(
        functools.partial(attention_send_body, HEAD ** (-0.5) * LOG2E),
        in_specs=[any_space] * 5 + [here] * 2,
        out_specs=[any_space] * 4 + [here],
        out_shape=[
            jax.ShapeDtypeStruct((total_rows, half), bf),
            jax.ShapeDtypeStruct((total_rows, half), bf),
            jax.ShapeDtypeStruct((total_rows, width), bf),
            jax.ShapeDtypeStruct((8, capacity, depth), bf),
            jax.ShapeDtypeStruct((heads, GROUPS, 1, 2 * rows), jnp.float32),
        ],
        scratch_shapes=[
            pltpu.VMEM((total_rows, half), bf),
            pltpu.VMEM((total_rows, half), bf),
            pltpu.VMEM((tokens, half), bf),
            pltpu.VMEM((tokens, half), bf),
            pltpu.VMEM(out_weight.shape, bf),
            pltpu.VMEM((GROUPS * (GROUPS + 1) // 2, keys, 2 * rows), jnp.float32),
            pltpu.VMEM((heads, GROUPS, HEAD, keys), bf),
            pltpu.VMEM((GROUPS, rows, half), bf),
            pltpu.VMEM((GROUPS, rows, half), bf),
            pltpu.VMEM((GROUPS, rows, half), bf),
            pltpu.VMEM((GROUPS, rows, width), bf),
            pltpu.VMEM((GROUPS, 2, capacity, depth), bf),
            dma((5,)),
            dma((GROUPS,)),
            dma((GROUPS,)),
            dma((GROUPS,)),
            dma,
            dma((GROUPS,)),
            dma((GROUPS,)),
            dma((8,)),
            dma((8,)),
        ],
        compiler_params=pltpu.CompilerParams(
            collective_id=4, has_side_effects=True, vmem_limit_bytes=VMEM_BYTES
        ),
        name="attention_send",
    )(queries, siblings, keys_all, values_all, out_weight, key_info, query_info)


def swap_blocks_body(blocks, landing, local_sem, send, recv):
    me = lax.axis_index("expert")
    enter(8, me)

    def outgoing(offset):
        target = lax.rem(me + offset, 8)
        return remote(blocks.at[target], landing.at[me], send.at[offset], recv.at[offset], target)

    local = pltpu.make_async_copy(blocks.at[me], landing.at[me], local_sem)
    for offset in range(1, 8):
        outgoing(offset).start()
    local.start()
    local.wait()
    for offset in range(1, 8):
        outgoing(offset).wait_send()
        place = landing.at[lax.rem(me + 8 - offset, 8)]
        remote(place, place, send.at[offset], recv.at[offset], me).wait_recv()


def swap_blocks(blocks):
    any_space = pl.BlockSpec(memory_space=pl.ANY)
    dma = pltpu.SemaphoreType.DMA
    return pl.pallas_call(
        swap_blocks_body,
        in_specs=[any_space],
        out_specs=any_space,
        out_shape=jax.ShapeDtypeStruct(blocks.shape, blocks.dtype),
        scratch_shapes=[dma, dma((8,)), dma((8,))],
        compiler_params=pltpu.CompilerParams(collective_id=7, has_side_effects=True),
        name="swap_blocks",
    )(blocks)


D = 2048
HEADS = 16
ATT_EXPERTS = 8
FFN_EXPERTS = 4
TRUNK = 1024
SEG = 96
TREE_LEN = 2176
NODES = 13

epsilon = 1e-06
highest = lax.Precision.HIGHEST
bf16 = jnp.bfloat16
f32 = jnp.float32


def tree_layout(places):
    after_trunk = places - TRUNK
    after_branch = after_trunk - 4 * SEG
    segments = jnp.where(
        places < TRUNK,
        0,
        jnp.where(after_branch < 0, 1 + after_trunk // SEG, 5 + after_branch // SEG),
    )
    depths = jnp.where(
        places < TRUNK,
        places,
        jnp.where(after_branch < 0, TRUNK + after_trunk % SEG, TRUNK + SEG + after_branch % SEG),
    )
    return (segments.astype(jnp.int32), depths.astype(jnp.int32))


def rotation_tables(depths):
    half_size = HEAD // 2
    frequency = 10000.0 ** (-jnp.arange(half_size, dtype=f32) * 2.0 / HEAD)
    angles = depths.astype(f32)[:, None] * frequency[None, :]
    cosine, sine = jnp.cos(angles), jnp.sin(angles)
    cosines = jnp.concatenate([cosine, cosine], axis=1)
    forward = jnp.concatenate([-sine, sine], axis=1)
    return (cosines, forward), (cosines, -forward)


def lookup(table, indices):
    nodes = jnp.arange(NODES, dtype=jnp.int32)
    return jnp.sum(jnp.where(indices[:, None] == nodes[None, :], table[None, :], 0), axis=1)


def running_count(chosen):
    rows = chosen.shape[-1]
    index = jnp.arange(rows, dtype=jnp.int32)
    upto = (index[:, None] <= index[None, :]).astype(bf16)
    return jnp.dot(chosen.astype(bf16), upto, preferred_element_type=f32).astype(jnp.int32) - 1


def source_plan(routes, expert, capacity):
    chosen = jnp.any(routes == expert, axis=2)
    ranking = running_count(chosen)
    slots = jnp.arange(capacity, dtype=jnp.int32)
    return chosen[:, None, :] & (ranking[:, None, :] == slots[None, :, None])


def token_picks(routes, experts, capacity):
    labels = jnp.arange(experts, dtype=jnp.int32)
    hits = routes.T[:, None, :] == labels[None, :, None]
    ranking = running_count(hits[0] | hits[1])
    slots = jnp.arange(capacity, dtype=jnp.int32)
    picks = hits[:, :, None, :] & (ranking[None, :, None, :] == slots[None, None, :, None])
    return picks.astype(bf16), hits[0].T.astype(f32), hits[1].T.astype(f32)


def fill_slots(picks, pair):
    return jnp.einsum("kecr,krd->ecd", picks, pair, preferred_element_type=f32).astype(bf16)


def read_slots(picks, slots):
    return jnp.einsum("kecr,ecd->krd", picks, slots, preferred_element_type=f32)


def gate_values(hidden, router, first, second):
    logits = jnp.dot(hidden.astype(f32), router, precision=highest)
    picked = jnp.stack([jnp.sum(logits * first, axis=1), jnp.sum(logits * second, axis=1)], axis=1)
    return jax.nn.softmax(picked, axis=1)


def router_grads(hidden, router, gates, first, second, picked_grad):
    logit_pick = gates * (picked_grad - jnp.sum(gates * picked_grad, axis=1, keepdims=True))
    logit_grad = logit_pick[:, 0:1] * first + logit_pick[:, 1:2] * second
    router_grad = jnp.dot(hidden.astype(f32).T, logit_grad, precision=highest)
    hidden_grad = jnp.dot(logit_grad, router.T, precision=highest)
    return (router_grad, hidden_grad)


def rms_parts(values):
    inverse = lax.rsqrt(jnp.mean(values * values, axis=-1, keepdims=True) + epsilon)
    return (values * inverse, inverse)


def norm_back(grad_normed, normed, inverse):
    return inverse * (grad_normed - normed * jnp.mean(grad_normed * normed, axis=-1, keepdims=True))


def pair_grads(gates, branches, upstream):
    gate_grad = jnp.stack([jnp.sum(upstream * branches[k], axis=1) for k in range(2)], axis=1)
    scaled = jnp.stack([gates[:, k : k + 1] * upstream for k in range(2)]).astype(bf16)
    return gate_grad, scaled


def exchange(slots):
    return lax.all_to_all(slots, "expert", split_axis=0, concat_axis=0, tiled=True)


def shift(values, step, size, devices):
    moves = [(i, i // size * size + (i % size + step) % size) for i in range(devices)]
    return lax.ppermute(values, "expert", moves)


def group_gather(rows, size, devices):
    return jnp.concatenate([rows] + [shift(rows, step, size, devices) for step in range(1, size)])


def group_reduce(partial, size, devices):
    parts = partial.reshape(size, -1, partial.shape[1])
    total = parts[0].astype(f32)
    for step in range(1, size):
        total = total + shift(parts[step], -step, size, devices).astype(f32)
    return total.astype(bf16)


def spread_over_replicas(block, my_replica, replicas):
    if replicas != 4:
        return lax.all_gather(block, "dp", axis=0), jnp.arange(replicas, dtype=jnp.int32)
    across, along = ([(i, i ^ n) for i in range(4)] for n in (1, 2))
    first, second = lax.ppermute(block, "dp", across), lax.ppermute(block, "dp", along)
    cut = block.shape[0] // 2
    upper, lower = lax.ppermute(second[:cut], "dp", across), lax.ppermute(first[cut:], "dp", along)
    blocks = jnp.stack([block, first, second, jnp.concatenate([upper, lower])])
    return blocks, my_replica ^ jnp.arange(4, dtype=jnp.int32)


def dot_tn(left, right):
    return lax.dot_general(left, right, (((0,), (0,)), ((), ())), preferred_element_type=f32)


def body(
    tokens,
    teacher,
    att_routes,
    ffn_routes,
    parent,
    valid,
    gain_one,
    kv_weight,
    att_router,
    q_weight,
    o_weight,
    gain_two,
    ffn_router,
    gate_weight,
    up_weight,
    down_weight,
):
    row_count = tokens.shape[0]
    devices, replicas = lax.axis_size("expert"), lax.axis_size("dp")
    my_index, my_replica = lax.axis_index("expert"), lax.axis_index("dp")
    core = my_index % 2
    att_copies, ffn_copies = devices // ATT_EXPERTS, devices // FFN_EXPERTS
    att_capacity, ffn_capacity = row_count * 13 // 40, row_count * 13 // 20
    token_count = row_count * devices
    half = HEADS * HEAD // 2
    assert token_count == TREE_LEN * parent.shape[0] and parent.shape[0] == 1
    pair = [(i, i ^ 1) for i in range(devices)]
    own_places = my_index * row_count + jnp.arange(row_count, dtype=jnp.int32)

    x_in = tokens.astype(f32)
    normed_one, inverse_one = rms_parts(x_in)
    hidden = (normed_one * gain_one).astype(bf16)
    weight_rows = kv_weight.shape[0]
    piece = half // replicas
    kv_share = lax.dynamic_slice_in_dim(
        kv_weight.reshape(weight_rows, 4, replicas, piece), my_replica, 1, 2
    )
    kv_share = (
        kv_share.reshape(weight_rows, 2, 2, piece).transpose(0, 2, 1, 3).reshape(weight_rows, 4 * piece)
    )
    kv_gathered = lax.all_gather(kv_share, "expert", axis=0)
    hidden_all = lax.all_gather(hidden, "expert", axis=0)
    all_routes = lax.all_gather(att_routes, "expert", axis=0)

    tree_places = jnp.arange(token_count, dtype=jnp.int32)
    tree_segments, tree_depths = tree_layout(tree_places)
    key_forward, key_backward = rotation_tables(tree_depths)
    key_info = jnp.pad(jnp.stack([tree_places, tree_segments], axis=1), ((0, 0), (0, 6)))
    experts_here = [my_index // att_copies]
    if att_copies == 1:
        experts_here.append(my_index ^ 1)
    plans = [source_plan(all_routes, expert, att_capacity) for expert in experts_here]
    slot_tables, query_parts = [], []
    for plan in plans:
        places = jnp.sum(
            jnp.where(plan, tree_places.reshape(devices, 1, row_count), 0), axis=2
        ).reshape(-1)
        segments, depths = tree_layout(places)
        parents = lookup(parent[0], segments)
        grands = lookup(parent[0], parents)
        query_parts.append(jnp.stack([places, segments, parents, grands]).reshape(4, GROUPS, -1))
        slot_tables.append(rotation_tables(depths))
    query_info = jnp.concatenate(query_parts, axis=2).transpose(1, 0, 2)
    own_plan = plans[0].astype(bf16)
    att_picks, att_first, att_second = token_picks(att_routes, ATT_EXPERTS, att_capacity)
    att_gates = gate_values(hidden, att_router, att_first, att_second)
    ffn_picks, ffn_first, ffn_second = token_picks(ffn_routes, FFN_EXPERTS, ffn_capacity)
    prepared = (key_forward, key_backward, key_info, slot_tables, query_info, own_plan, att_picks, att_gates, ffn_picks)
    kv_gathered, prepared = lax.optimization_barrier((kv_gathered, prepared))
    kv_half = lax.dynamic_slice_in_dim(kv_gathered, core * 2 * piece, 2 * piece, 2).reshape(D, 2 * piece)
    kv_blocks, block_order = spread_over_replicas(kv_half, my_replica, replicas)
    hidden_all, kv_blocks = lax.optimization_barrier((hidden_all, kv_blocks))
    key_forward, key_backward, key_info, slot_tables, query_info, own_plan, att_picks, att_gates, ffn_picks = prepared

    queries, query_inputs = project_queries(own_plan, hidden_all, q_weight, slot_tables[0][0])
    keys_all, values_all = project_keys_values(hidden_all, kv_blocks, key_forward, block_order)

    def far_half(values):
        return lax.ppermute(
            lax.dynamic_slice_in_dim(values, (1 - core) * half, half, 1), "expert", pair
        )

    def join_halves(mine, sibling):
        other = lax.ppermute(sibling, "expert", pair)
        return jnp.where(
            core == 0,
            jnp.concatenate([mine, other], axis=1),
            jnp.concatenate([other, mine], axis=1),
        )

    heads = half // HEAD
    query_sets = [queries]
    starts = jnp.zeros((2,), jnp.int32)
    if att_copies == 1:
        query_sets.append(far_half(queries))
        starts = jnp.stack([core * heads, 0]).astype(jnp.int32)
    fused = devices == 8 and replicas == 4 and att_copies == 1 and ffn_copies == 2 and ffn_capacity % 16 == 0
    if fused:
        *att_outs, att_rows, att_back, lse = attention_send(
            *query_sets, keys_all, values_all, o_weight, key_info, query_info, att_capacity
        )
        att_everywhere = lax.all_gather(att_rows, "dp", axis=0, tiled=True)
    else:
        *att_outs, lse = attention_forward(
            query_sets, starts // 2, keys_all, values_all, key_info, query_info, heads
        )
        att_rows = join_halves(*att_outs) if att_copies == 1 else att_outs[0]
        att_partial = lax.dot_general(
            att_rows, o_weight, (((1,), (1,)), ((), ())), preferred_element_type=f32
        ).astype(bf16)
        att_back = exchange(att_partial.reshape(devices, att_capacity, D))
    if att_copies > 1:
        att_back = (
            att_back.astype(f32).reshape(ATT_EXPERTS, att_copies, att_capacity, D).sum(axis=1).astype(bf16)
        )
    att_branches = read_slots(att_picks, att_back)
    x_mid = x_in + att_gates[:, 0:1] * att_branches[0] + att_gates[:, 1:2] * att_branches[1]

    normed_two, inverse_two = rms_parts(x_mid)
    hidden_two = (normed_two * gain_two).astype(bf16)
    ffn_gates = gate_values(hidden_two, ffn_router, ffn_first, ffn_second)

    def to_experts(slots):
        rows = exchange(slots.reshape(devices, ffn_capacity // ffn_copies, D))
        return group_gather(rows.reshape(-1, D), ffn_copies, devices)

    def to_tokens(partial):
        rows = group_reduce(partial.astype(bf16), ffn_copies, devices)
        back = exchange(rows.reshape(devices, ffn_capacity // ffn_copies, D))
        return read_slots(ffn_picks, back.reshape(FFN_EXPERTS, ffn_capacity, D))

    ffn_slots = jnp.einsum(
        "ecr,rd->ecd", ffn_picks[0] + ffn_picks[1], hidden_two, preferred_element_type=f32
    ).astype(bf16)
    if fused:
        ffn_inputs, gate_pre, up_pre, activated, ffn_back = ffn_forward(
            ffn_slots, gate_weight, up_weight, down_weight
        )
        ffn_branches = read_slots(ffn_picks, ffn_back)
    else:
        ffn_inputs = to_experts(ffn_slots)
        gate_pre = jnp.dot(ffn_inputs, gate_weight, preferred_element_type=f32)
        up_pre = jnp.dot(ffn_inputs, up_weight, preferred_element_type=f32)
        sigmoid_gate = jax.nn.sigmoid(gate_pre)
        silu_gate = gate_pre * sigmoid_gate
        activated = (silu_gate * up_pre).astype(bf16)
        ffn_branches = to_tokens(
            lax.dot_general(
                activated, down_weight, (((1,), (1,)), ((), ())), preferred_element_type=f32
            )
        )
    result = x_mid + ffn_gates[:, 0:1] * ffn_branches[0] + ffn_gates[:, 1:2] * ffn_branches[1]

    tree_global = my_replica * parent.shape[0] + own_places // TREE_LEN
    tree_labels = jnp.arange(valid.shape[0], dtype=jnp.int32)
    limits = jnp.sum(
        jnp.where(tree_global[:, None] == tree_labels[None, :], valid[None, :], 0), axis=1
    )
    counted = own_places % TREE_LEN < limits
    loss_factor = valid.shape[0] * TREE_LEN / jnp.sum(valid).astype(f32)
    grad_result = jnp.where(counted[:, None], (result - teacher.astype(f32)) * loss_factor, 0.0)

    ffn_gate_grad, ffn_scaled = pair_grads(ffn_gates, ffn_branches, grad_result)
    ffn_grad_slots = fill_slots(ffn_picks, ffn_scaled)
    if fused:
        ffn_grad_slots, att_everywhere = lax.optimization_barrier((ffn_grad_slots, att_everywhere))
        grad_ffn_out, grad_down = send_rows(ffn_grad_slots, activated)
        grad_ffn_out = grad_ffn_out.reshape(-1, D)
    else:
        grad_ffn_out = to_experts(ffn_grad_slots)
        grad_down = dot_tn(grad_ffn_out, activated).astype(bf16)
    grad_ffn_out, grad_down = lax.optimization_barrier((grad_ffn_out, grad_down))
    summed_down = lax.psum_scatter(grad_down, "dp", scatter_dimension=0, tiled=True)
    if fused:
        grad_gate_pre, grad_up_pre, ffn_grad_back = ffn_backward(
            grad_ffn_out, gate_pre, up_pre, gate_weight, up_weight, down_weight, ffn_capacity
        )
        grad_gate = dot_tn(ffn_inputs, grad_gate_pre).astype(bf16)
        ffn_grad_back, grad_gate = lax.optimization_barrier((ffn_grad_back, grad_gate))
        ffn_grad_pair = read_slots(ffn_picks, ffn_grad_back)
    else:
        grad_activated = jnp.dot(grad_ffn_out, down_weight, preferred_element_type=f32)
        grad_gate_pre = (
            grad_activated * up_pre * sigmoid_gate * (1.0 + gate_pre * (1.0 - sigmoid_gate))
        ).astype(bf16)
        grad_up_pre = (grad_activated * silu_gate).astype(bf16)
        grad_ffn_in = lax.dot_general(
            grad_gate_pre, gate_weight, (((1,), (1,)), ((), ())), preferred_element_type=f32
        ) + lax.dot_general(
            grad_up_pre, up_weight, (((1,), (1,)), ((), ())), preferred_element_type=f32
        )
        grad_gate = dot_tn(ffn_inputs, grad_gate_pre).astype(bf16)
        ffn_grad_pair = to_tokens(grad_ffn_in)
    summed_gate = lax.psum_scatter(grad_gate, "dp", scatter_dimension=0, tiled=True)
    grad_ffn_router, hidden_two_extra = router_grads(
        hidden_two, ffn_router, ffn_gates, ffn_first, ffn_second, ffn_gate_grad
    )
    grad_hidden_two = ffn_grad_pair[0] + ffn_grad_pair[1] + hidden_two_extra
    grad_gain_two = jnp.sum(grad_hidden_two * normed_two, axis=0)
    grad_mid = grad_result + norm_back(grad_hidden_two * gain_two, normed_two, inverse_two)

    att_gate_grad, att_scaled = pair_grads(att_gates, att_branches, grad_mid)
    att_slots = fill_slots(att_picks, att_scaled)
    if att_copies > 1:
        att_slots = jnp.repeat(att_slots, att_copies, axis=0)
    att_slots, summed_down = lax.optimization_barrier((att_slots, summed_down))
    if fused:
        grad_att_out, grad_up = send_slots(att_slots, ffn_inputs, grad_up_pre)
        grad_att_out = grad_att_out.reshape(-1, D)
    else:
        grad_att_out = exchange(att_slots).reshape(-1, D)
        grad_up = dot_tn(ffn_inputs, grad_up_pre).astype(bf16)
        grad_att_out, grad_up = lax.optimization_barrier((grad_att_out, grad_up))
    summed_up = lax.psum_scatter(grad_up, "dp", scatter_dimension=0, tiled=True)
    grad_heads = jnp.dot(grad_att_out, o_weight, preferred_element_type=f32).astype(bf16)
    grad_heads, grad_att_out = lax.optimization_barrier((grad_heads, grad_att_out))
    grad_sets = [grad_heads]
    if att_copies == 1:
        grad_sets.append(far_half(grad_heads))
    if fused:
        share = D // replicas

        def columns_of(replica):
            return lax.dynamic_slice_in_dim(grad_att_out, replica * share, share, 1)

        grad_columns = [columns_of(my_replica)] + [
            lax.ppermute(columns_of(my_replica ^ n), "dp", [(i, i ^ n) for i in range(replicas)])
            for n in range(1, replicas)
        ]
    else:
        grad_o = dot_tn(grad_att_out, att_rows).astype(bf16)
        summed_o = lax.psum_scatter(grad_o, "dp", scatter_dimension=0, tiled=True).astype(f32)
    *grad_queries, grad_keys_values = attention_backward(
        query_sets,
        starts,
        grad_sets,
        att_outs,
        keys_all,
        values_all,
        lse,
        key_info,
        query_info,
        key_backward,
        [tables[1] for tables in slot_tables],
        heads,
    )
    grad_keys_values, summed_gate = lax.optimization_barrier((grad_keys_values, summed_gate))
    grad_query_pre = join_halves(*grad_queries) if att_copies == 1 else grad_queries[0]
    grad_kv = dot_tn(hidden_all.reshape(token_count, D), grad_keys_values).astype(bf16)
    grad_q = dot_tn(query_inputs, grad_query_pre).astype(bf16)
    summed_kv = lax.psum_scatter(grad_kv, "dp", scatter_dimension=0, tiled=True)
    summed_q = lax.psum_scatter(grad_q, "dp", scatter_dimension=0, tiled=True)
    grad_query_in = lax.dot_general(
        grad_query_pre, q_weight, (((1,), (1,)), ((), ())), preferred_element_type=f32
    ).astype(bf16)
    grad_query_in, grad_kv, grad_q, summed_up = lax.optimization_barrier(
        (grad_query_in, grad_kv, grad_q, summed_up)
    )

    merge_args = (
        own_plan.transpose(0, 2, 1),
        grad_query_in.reshape(devices, att_capacity, D),
        grad_keys_values,
        kv_blocks,
    )
    if fused:
        arrived = merge_return(*merge_args)
        arrived, grad_columns, summed_kv = lax.optimization_barrier((arrived, grad_columns, summed_kv))
        column_stack = jnp.stack(grad_columns)
        summed_o = dot_tn(
            jnp.concatenate(
                [lax.dynamic_index_in_dim(column_stack, my_replica ^ n, 0, False) for n in range(replicas)]
            ),
            att_everywhere,
        )
    else:
        merged = merge_hidden_grads(*merge_args, block_order).reshape(devices // 2, 2, row_count, D)
        kept = lax.dynamic_index_in_dim(merged, core, 1, keepdims=False)
        passed = lax.ppermute(
            lax.dynamic_index_in_dim(merged, 1 - core, 1, keepdims=False), "expert", pair
        )
        chip_sum = (kept.astype(f32) + passed.astype(f32)).astype(bf16)
        same_core = [[2 * i + c for i in range(devices // 2)] for c in range(2)]
        arrived = lax.all_to_all(
            chip_sum, "expert", split_axis=0, concat_axis=0, axis_index_groups=same_core, tiled=True
        )
    grad_att_router, hidden_one_extra = router_grads(
        hidden, att_router, att_gates, att_first, att_second, att_gate_grad
    )
    grad_hidden_one = jnp.sum(arrived.astype(f32), axis=0) + hidden_one_extra
    grad_gain_one = jnp.sum(grad_hidden_one * normed_one, axis=0)
    grad_input = grad_mid + norm_back(grad_hidden_one * gain_one, normed_one, inverse_one)

    everyone = devices * replicas
    smalls = [grad_gain_one, grad_gain_two, grad_att_router, grad_ffn_router]
    packed = jnp.concatenate([small.reshape(everyone, -1) for small in smalls], axis=1)
    packed, summed_o = lax.optimization_barrier((packed, summed_o))
    kv_exchange = swap_blocks if fused else exchange
    kv_rows = kv_exchange(summed_kv.reshape(devices, -1, 2 * half))
    own_smalls = jnp.sum(
        lax.all_to_all(packed, ("dp", "expert"), split_axis=0, concat_axis=0, tiled=True), axis=0
    )
    own_smalls, kv_rows, summed_q = lax.optimization_barrier((own_smalls, kv_rows, summed_q))
    share = D // everyone
    shared_gain_one = own_smalls[:share]
    shared_gain_two = own_smalls[share : 2 * share]
    shared_att_router = own_smalls[2 * share : (2 + ATT_EXPERTS) * share].reshape(share, ATT_EXPERTS)
    shared_ffn_router = own_smalls[(2 + ATT_EXPERTS) * share :].reshape(share, FFN_EXPERTS)

    kv_sum = jnp.sum(kv_rows.astype(f32).reshape(devices // 2, 2, -1, 2 * half), axis=0)
    shared_kv = jnp.concatenate(
        [kv_sum[n, :, m * half : (m + 1) * half] for m in range(2) for n in range(2)], axis=1
    )

    return (
        result.astype(bf16),
        grad_input.astype(bf16),
        shared_gain_one,
        shared_kv,
        shared_att_router,
        summed_q.astype(f32),
        summed_o,
        shared_gain_two,
        shared_ffn_router,
        summed_gate.astype(f32),
        summed_up.astype(f32),
        summed_down.astype(f32),
    )


def solution(mesh):
    in_specs = (
        P(("dp", "expert"), None),
        P(("dp", "expert"), None),
        P(("dp", "expert"), None),
        P(("dp", "expert"), None),
        P("dp", None),
        P(),
        P(),
        P("expert", None),
        P(),
        P(None, "expert"),
        P(None, "expert"),
        P(),
        P(),
        P(None, "expert"),
        P(None, "expert"),
        P(None, "expert"),
    )
    out_specs = (
        P(("dp", "expert"), None),
        P(("dp", "expert"), None),
        P(("dp", "expert")),
        P(("dp", "expert"), None),
        P(("dp", "expert"), None),
        P("dp", "expert"),
        P("dp", "expert"),
        P(("dp", "expert")),
        P(("dp", "expert"), None),
        P("dp", "expert"),
        P("dp", "expert"),
        P("dp", "expert"),
    )
    return jax.shard_map(body, mesh=mesh, in_specs=in_specs, out_specs=out_specs, check_vma=False)
```
